32 devices in a mesh: dp: 8 (over z, x), seq: 4 (over y, core).
Axes of the slice: x: 2, y: 2, z: 4, core: 2. Of those that a mesh axis runs over, the one named last changes fastest.
Arguments:
- tokens: bfloat16 [16, 1024, 512], P('dp', 'seq'), may hold values from -6 to 6
- memory: bfloat16 [16, 256, 512], P('dp', 'seq'), may hold values from -6 to 6
- target_ids: int32 [16, 1024], P('dp', 'seq'), may hold values from 0 to 3, never falling along the last dimension, each value on 1 to 768 neighbouring positions
- source_ids: int32 [16, 256], P('dp', 'seq'), may hold values from 0 to 3, never falling along the last dimension, each value on 1 to 192 neighbouring positions
- cotangent: bfloat16 [16, 1024, 512], P('dp', 'seq'), may hold values from -6 to 6
- query_weight: bfloat16 [512, 512], P(('dp', 'seq')), may hold values from -0.25 to 0.25
- key_weight: bfloat16 [512, 512], P(('dp', 'seq')), may hold values from -0.25 to 0.25
- value_weight: bfloat16 [512, 512], P(('dp', 'seq')), may hold values from -0.25 to 0.25
- output_weight: bfloat16 [512, 512], P(('dp', 'seq')), may hold values from -1 to 1
- query_bias: bfloat16 [512], P(('dp', 'seq')), may hold values from -1.796875 to 1.796875
- value_bias: bfloat16 [512], P(('dp', 'seq')), may hold values from -1.796875 to 1.796875
- output_bias: bfloat16 [512], P(('dp', 'seq')), may hold values from -1.796875 to 1.796875
- attention_gain: bfloat16 [512], P(('dp', 'seq')), may hold values from 0.5 to 1.5
- attention_shift: bfloat16 [512], P(('dp', 'seq')), may hold values from -1.1953125 to 1.1953125
- source_query: bfloat16 [512, 512], P(('dp', 'seq')), may hold values from -0.25 to 0.25
- source_key: bfloat16 [512, 512], P(('dp', 'seq')), may hold values from -0.25 to 0.25
- source_value: bfloat16 [512, 512], P(('dp', 'seq')), may hold values from -0.25 to 0.25
- source_output: bfloat16 [512, 512], P(('dp', 'seq')), may hold values from -1 to 1
- source_query_bias: bfloat16 [512], P(('dp', 'seq')), may hold values from -1.796875 to 1.796875
- source_value_bias: bfloat16 [512], P(('dp', 'seq')), may hold values from -1.796875 to 1.796875
- source_output_bias: bfloat16 [512], P(('dp', 'seq')), may hold values from -1.796875 to 1.796875
- source_gain: bfloat16 [512], P(('dp', 'seq')), may hold values from 0.5 to 1.5
- source_shift: bfloat16 [512], P(('dp', 'seq')), may hold values from -1.1953125 to 1.1953125
- inner_weight: bfloat16 [512, 2048], P(('dp', 'seq')), may hold values from -0.25 to 0.25
- inner_bias: bfloat16 [2048], P(('dp', 'seq')), may hold values from -1.796875 to 1.796875
- outer_weight: bfloat16 [2048, 512], P(('dp', 'seq')), may hold values from -0.125 to 0.125
- outer_bias: bfloat16 [512], P(('dp', 'seq')), may hold values from -1.796875 to 1.796875
- final_gain: bfloat16 [512], P(('dp', 'seq')), may hold values from 0.5 to 1.5
- final_shift: bfloat16 [512], P(('dp', 'seq')), may hold values from -1.1953125 to 1.1953125
Outputs:
- output: float32 [16, 1024, 512], P('dp', 'seq')
- input_gradient: float32 [16, 1024, 512], P('dp', 'seq')
- memory_gradient: float32 [16, 256, 512], P('dp', 'seq')
- query_weight_gradient: float32 [512, 512], P(('dp', 'seq'))
- key_weight_gradient: float32 [512, 512], P(('dp', 'seq'))
- value_weight_gradient: float32 [512, 512], P(('dp', 'seq'))
- output_weight_gradient: float32 [512, 512], P(('dp', 'seq'))
- query_bias_gradient: float32 [512], P(('dp', 'seq'))
- value_bias_gradient: float32 [512], P(('dp', 'seq'))
- output_bias_gradient: float32 [512], P(('dp', 'seq'))
- attention_gain_gradient: float32 [512], P(('dp', 'seq'))
- attention_shift_gradient: float32 [512], P(('dp', 'seq'))
- source_query_gradient: float32 [512, 512], P(('dp', 'seq'))
- source_key_gradient: float32 [512, 512], P(('dp', 'seq'))
- source_value_gradient: float32 [512, 512], P(('dp', 'seq'))
- source_output_gradient: float32 [512, 512], P(('dp', 'seq'))
- source_query_bias_gradient: float32 [512], P(('dp', 'seq'))
- source_value_bias_gradient: float32 [512], P(('dp', 'seq'))
- source_output_bias_gradient: float32 [512], P(('dp', 'seq'))
- source_gain_gradient: float32 [512], P(('dp', 'seq'))
- source_shift_gradient: float32 [512], P(('dp', 'seq'))
- inner_weight_gradient: float32 [512, 2048], P(('dp', 'seq'))
- inner_bias_gradient: float32 [2048], P(('dp', 'seq'))
- outer_weight_gradient: float32 [2048, 512], P(('dp', 'seq'))
- outer_bias_gradient: float32 [512], P(('dp', 'seq'))
- final_gain_gradient: float32 [512], P(('dp', 'seq'))
- final_shift_gradient: float32 [512], P(('dp', 'seq'))
The draws below stay inside these ranges and needn't reach their ends.
Inputs may be any that keep to these rules, and one draw needn't show every extreme that they name: `target_ids`: along each row the ids never fall; every id of 0 to 3 covers at least one position of every row, none covers more than 768 positions of a row, and some row reaches that many. `source_ids`: along each row the ids never fall; every id of 0 to 3 covers at least one memory position of every row, none covers more than 192 positions of a row, and some row reaches that many.
All inputs are finite; a program needn't handle non-finite values.
Results may differ from the reference program's by a relative error of at most 0.018.
Values may be sent and summed in bfloat16 or wider, within the bound.
No kernel may reach another device: no remote copies, remote signals or barrier semaphores. Data moves between devices by JAX's collectives and lax.ppermute only.
A program may use at most 256 MiB of HBM per device.

```python
import math
import jax
import jax.numpy as jnp
import numpy as np
from jax import lax

D = 512
HEADS = 8
HEAD_DIM = 64
FF = 2048
SEGS = 4
ROWS = 16
LENGTH = 1024
MEM = 256


def activation_field(key, count, length, boosted):
    first_key, second_key = jax.random.split(jax.random.fold_in(key, 11), 2)
    values = jax.random.normal(first_key, (count, length, D), jnp.float32)
    if boosted:
        picked = jax.random.randint(second_key, (count,), 0, 16)
        blocks = jnp.arange(D, dtype=jnp.int32) // (D // 16)
        values = values * jnp.where(blocks[None, None, :] == picked[:, None, None], 2.0, 1.0)
    return jnp.clip(values, -6.0, 6.0)


def draw_tokens(key, part):
    return activation_field(key, ROWS, LENGTH, True).astype(jnp.bfloat16)


def draw_memory(key, part):
    return activation_field(jax.random.fold_in(key, 5), ROWS, MEM, False).astype(jnp.bfloat16)


def block_levels(stream_key, extent, shards, smallest, top_value):
    level = 1.0
    for axis_at, shards_of in shards:
        steps = jax.random.uniform(jax.random.fold_in(jax.random.fold_in(stream_key, 6), axis_at), (shards_of,), jnp.float32, smallest / len(shards), top_value / len(shards))
        level = level * jnp.repeat(jnp.exp(steps), extent[axis_at] // shards_of).reshape((-1,) + (1,) * (len(extent) - 1 - axis_at))
    return level


def length_profile(number_of, total, reach, skew):
    loads = [(1 << 20) // math.isqrt(rank ** skew) + 1 for rank in range(2, number_of + 1)]
    surplus, given = total - reach - (number_of - 1), [1] * (number_of - 1)
    while surplus > 0:
        movable = [i for i in range(number_of - 1) if given[i] < reach]
        pool, budget = sum([loads[i] for i in movable]), surplus
        for i in movable:
            more = min(reach - given[i], max(1, budget * loads[i] // pool), surplus)
            given[i] = given[i] + more
            surplus = surplus - more
    return np.array([reach] + given)


def ragged(stream_key, count, total, most, lean):
    if count == 2:
        one = jax.random.randint(stream_key, (), max(1, total - most), min(most, total - 1) + 1)
        return jnp.stack([one, total - one])
    lengths = jnp.asarray(length_profile(count, total, most, lean), jnp.int32)
    couples = (count - 1) // 2
    giver, sink = lengths[1:1 + 2 * couples:2], lengths[2:2 + 2 * couples:2]
    room = jnp.minimum(giver - 1, most - sink)
    moved = jax.random.randint(jax.random.fold_in(stream_key, 1), (couples,), 0, 1 << 20) % (room + 1)
    lengths = lengths.at[1:1 + 2 * couples:2].set(giver - moved).at[2:2 + 2 * couples:2].set(sink + moved)
    return lengths[jax.random.permutation(jax.random.fold_in(stream_key, 2), count)]


def noise(key, extent, width, bound, cuts=(), held_as=jnp.bfloat16):
    entries = jax.random.normal(key, extent, jnp.float32) * width
    if len(cuts) > 0:
        entries = block_levels(key, extent, cuts, -0.22, 0.18) * entries
    return jnp.clip(entries, min=-bound, max=bound).astype(held_as)


def setup_inputs(seed: int = 0) -> dict:
    streams_of = jax.random.split(jax.random.key(seed), 30)
    return {
        "tokens": draw_tokens(jax.random.fold_in(streams_of[29], 71), 0),
        "memory": draw_memory(jax.random.fold_in(streams_of[29], 71), 0),
        "target_ids": jax.vmap(lambda own: jnp.searchsorted(jnp.cumsum(ragged(own, SEGS, LENGTH, 3 * LENGTH // 4, 0)), jnp.arange(LENGTH), side="right"))(jax.random.split(streams_of[2], ROWS)).reshape((ROWS, LENGTH)).astype(jnp.int32),
        "source_ids": jax.vmap(lambda own: jnp.searchsorted(jnp.cumsum(ragged(own, SEGS, MEM, 3 * MEM // 4, 0)), jnp.arange(MEM), side="right"))(jax.random.split(streams_of[3], ROWS)).reshape((ROWS, MEM)).astype(jnp.int32),
        "cotangent": noise(streams_of[4], (ROWS, LENGTH, D), 1.0, 6.0, ((0, 8), (1, 4))),
        "query_weight": noise(streams_of[5], (D, D), D ** -0.5, 0.25, ((0, 32),)),
        "key_weight": noise(streams_of[6], (D, D), D ** -0.5, 0.25, ((0, 32),)),
        "value_weight": noise(streams_of[7], (D, D), D ** -0.5, 0.25, ((0, 32),)),
        "output_weight": noise(streams_of[8], (D, D), (D // 16) ** -0.5, 1.0, ((0, 32),)),
        "query_bias": noise(streams_of[9], (D,), 0.3, 1.796875, ((0, 32),)),
        "value_bias": noise(streams_of[10], (D,), 0.3, 1.796875, ((0, 32),)),
        "output_bias": noise(streams_of[11], (D,), 0.3, 1.796875, ((0, 32),)),
        "attention_gain": jnp.clip(1.0 + 0.1 * jax.random.normal(streams_of[12], (D,), jnp.float32), 0.5, 1.5).astype(jnp.bfloat16),
        "attention_shift": noise(streams_of[13], (D,), 0.2, 1.1953125, ((0, 32),)),
        "source_query": noise(streams_of[14], (D, D), D ** -0.5, 0.25, ((0, 32),)),
        "source_key": noise(streams_of[15], (D, D), D ** -0.5, 0.25, ((0, 32),)),
        "source_value": noise(streams_of[16], (D, D), D ** -0.5, 0.25, ((0, 32),)),
        "source_output": noise(streams_of[17], (D, D), (D // 16) ** -0.5, 1.0, ((0, 32),)),
        "source_query_bias": noise(streams_of[18], (D,), 0.3, 1.796875, ((0, 32),)),
        "source_value_bias": noise(streams_of[19], (D,), 0.3, 1.796875, ((0, 32),)),
        "source_output_bias": noise(streams_of[20], (D,), 0.3, 1.796875, ((0, 32),)),
        "source_gain": jnp.clip(1.0 + 0.1 * jax.random.normal(streams_of[21], (D,), jnp.float32), 0.5, 1.5).astype(jnp.bfloat16),
        "source_shift": noise(streams_of[22], (D,), 0.2, 1.1953125, ((0, 32),)),
        "inner_weight": noise(streams_of[23], (D, FF), D ** -0.5, 0.25, ((0, 32),)),
        "inner_bias": noise(streams_of[24], (FF,), 0.3, 1.796875, ((0, 32),)),
        "outer_weight": noise(streams_of[25], (FF, D), FF ** -0.5, 0.125, ((0, 32),)),
        "outer_bias": noise(streams_of[26], (D,), 0.3, 1.796875, ((0, 32),)),
        "final_gain": jnp.clip(1.0 + 0.1 * jax.random.normal(streams_of[27], (D,), jnp.float32), 0.5, 1.5).astype(jnp.bfloat16),
        "final_shift": noise(streams_of[28], (D,), 0.2, 1.1953125, ((0, 32),)),
    }


@jax.custom_vjp
def low(v):
    return lax.optimization_barrier(v.astype(jnp.bfloat16)).astype(jnp.float32)

@jax.custom_vjp
def low_back(v):
    return v

def low_keep(v):
    return (low(v), None)

def low_pass(kept, grad):
    return (grad,)

def back_keep(v):
    return (v, None)

def back_low(kept, grad):
    return (low(grad),)
low.defvjp(low_keep, low_pass)
low_back.defvjp(back_keep, back_low)

def matmul(former, latter):
    return jnp.dot(former, latter, precision=lax.Precision.HIGHEST, preferred_element_type=jnp.float32)

def layer_norm(total, gain, shift):
    average = lax.optimization_barrier(jnp.mean(total, axis=-1, keepdims=True))
    centered = total - average
    variance = lax.optimization_barrier(jnp.mean(centered * centered, axis=-1, keepdims=True))
    return centered * lax.rsqrt(variance + 1e-05) * gain + shift

def attention(queries, key_rows, values, matching):
    heads_q = queries.reshape(queries.shape[0], HEADS, HEAD_DIM)
    heads_k = key_rows.reshape(key_rows.shape[0], HEADS, HEAD_DIM)
    heads_v = values.reshape(values.shape[0], HEADS, HEAD_DIM)
    scores = jnp.einsum('qhd,khd->hqk', heads_q, heads_k, precision=lax.Precision.HIGHEST) * HEAD_DIM ** (-0.5)
    scores = low_back(jnp.where(matching[None], scores, -1000000000.0))
    highest = lax.optimization_barrier(jnp.max(scores, axis=-1, keepdims=True))
    weights = jnp.exp(scores - highest)
    chances = weights / lax.optimization_barrier(jnp.sum(weights, axis=-1, keepdims=True))
    mixture = jnp.einsum('hqk,khd->qhd', low(chances), heads_v, precision=lax.Precision.HIGHEST)
    return mixture.reshape(queries.shape[0], HEADS * HEAD_DIM)

def row_forward(params, tokens, memory, target_row, source_row):
    query_weight, key_weight, value_weight, output_weight, query_bias, value_bias, output_bias, attention_gain, attention_shift, source_query, source_key, source_value, source_output, source_query_bias, source_value_bias, source_output_bias, source_gain, source_shift, inner_weight, inner_bias, outer_weight, outer_bias, final_gain, final_shift = params
    same_target = target_row[:, None] == target_row[None, :]
    same_source = target_row[:, None] == source_row[None, :]
    queries = low(low_back(matmul(tokens, query_weight) + query_bias))
    key_rows = low(low_back(matmul(tokens, key_weight)))
    values = low(low_back(matmul(tokens, value_weight) + value_bias))
    mixture = low(low_back(attention(queries, key_rows, values, same_target)))
    branch = low_back(matmul(mixture, output_weight) + output_bias)
    first = layer_norm(tokens + branch, attention_gain, attention_shift)
    first_low = low(first)
    cross_queries = low(low_back(matmul(first_low, source_query) + source_query_bias))
    memory_keys = low(low_back(matmul(memory, source_key)))
    memory_values = low(low_back(matmul(memory, source_value) + source_value_bias))
    cross = low(low_back(attention(cross_queries, memory_keys, memory_values, same_source)))
    cross_branch = low_back(matmul(cross, source_output) + source_output_bias)
    second = layer_norm(first + cross_branch, source_gain, source_shift)
    second_low = low(second)
    inner = low_back(matmul(second_low, inner_weight) + inner_bias)
    active = low(jax.nn.gelu(inner, approximate=False))
    outer = low_back(matmul(active, outer_weight) + outer_bias)
    return layer_norm(second + outer, final_gain, final_shift)

def reference(tokens, memory, target_ids, source_ids, cotangent, query_weight, key_weight, value_weight, output_weight, query_bias, value_bias, output_bias, attention_gain, attention_shift, source_query, source_key, source_value, source_output, source_query_bias, source_value_bias, source_output_bias, source_gain, source_shift, inner_weight, inner_bias, outer_weight, outer_bias, final_gain, final_shift):
    params = (query_weight, key_weight, value_weight, output_weight, query_bias, value_bias, output_bias, attention_gain, attention_shift, source_query, source_key, source_value, source_output, source_query_bias, source_value_bias, source_output_bias, source_gain, source_shift, inner_weight, inner_bias, outer_weight, outer_bias, final_gain, final_shift)
    params = tuple((item.astype(jnp.float32) for item in params))

    def one_row(totals, row):
        row_tokens, row_memory, row_targets, row_sources, row_cotangent = row

        def forward(weights, inputs, context):
            return row_forward(weights, inputs, context, row_targets, row_sources)
        result, pullback = jax.vjp(forward, params, row_tokens, row_memory)
        param_grads, token_grad, memory_grad = pullback(row_cotangent)
        totals = jax.tree.map(lambda former, latter: former + latter, totals, param_grads)
        return (totals, (result, token_grad, memory_grad))
    start = jax.tree.map(jnp.zeros_like, params)
    totals, stacked = lax.scan(one_row, start, (tokens.astype(jnp.float32), memory.astype(jnp.float32), target_ids, source_ids, cotangent.astype(jnp.float32)))
    output, input_gradient, memory_gradient = stacked
    query_weight_gradient, key_weight_gradient, value_weight_gradient, output_weight_gradient, query_bias_gradient, value_bias_gradient, output_bias_gradient, attention_gain_gradient, attention_shift_gradient, source_query_gradient, source_key_gradient, source_value_gradient, source_output_gradient, source_query_bias_gradient, source_value_bias_gradient, source_output_bias_gradient, source_gain_gradient, source_shift_gradient, inner_weight_gradient, inner_bias_gradient, outer_weight_gradient, outer_bias_gradient, final_gain_gradient, final_shift_gradient = totals
    return (output, input_gradient, memory_gradient, query_weight_gradient, key_weight_gradient, value_weight_gradient, output_weight_gradient, query_bias_gradient, value_bias_gradient, output_bias_gradient, attention_gain_gradient, attention_shift_gradient, source_query_gradient, source_key_gradient, source_value_gradient, source_output_gradient, source_query_bias_gradient, source_value_bias_gradient, source_output_bias_gradient, source_gain_gradient, source_shift_gradient, inner_weight_gradient, inner_bias_gradient, outer_weight_gradient, outer_bias_gradient, final_gain_gradient, final_shift_gradient)
```

```python
import functools
import math

import jax
import jax.numpy as jnp
from jax import lax
from jax.experimental import pallas as pl
from jax.experimental.pallas import tpu as pltpu
from jax.sharding import PartitionSpec as P

HEADS = 8
HEAD_DIM = 64
PAIR = 128
EPSILON = 1e-05
MASKED = 1e9
AXES = ("dp", "seq")
F32 = jnp.float32
BF16 = jnp.bfloat16

(
    QUERY_BIAS,
    VALUE_BIAS,
    OUTPUT_BIAS,
    ATTENTION_GAIN,
    ATTENTION_SHIFT,
    SOURCE_QUERY_BIAS,
    SOURCE_VALUE_BIAS,
    SOURCE_OUTPUT_BIAS,
    SOURCE_GAIN,
    SOURCE_SHIFT,
    OUTER_BIAS,
    FINAL_GAIN,
    FINAL_SHIFT,
    INNER_BIAS,
) = range(14)


def dot(a, b):
    return lax.dot_general(a, b, (((1,), (0,)), ((), ())), preferred_element_type=F32)


def dot_nt(a, b):
    return lax.dot_general(a, b, (((1,), (1,)), ((), ())), preferred_element_type=F32)


def dot_tn(a, b):
    return lax.dot_general(a, b, (((0,), (0,)), ((), ())), preferred_element_type=F32)


def total(values):
    return jnp.sum(values.astype(F32), axis=0, keepdims=True)


def normalize(h):
    average = jnp.mean(h, axis=-1, keepdims=True)
    centered = h - average
    variance = jnp.mean(centered * centered, axis=-1, keepdims=True)
    inverse = lax.rsqrt(variance + EPSILON)
    return centered * inverse, inverse


def normalize_back(upstream, normed, inverse, gain):
    scaled = upstream * gain
    first_mean = jnp.mean(scaled, axis=-1, keepdims=True)
    second_mean = jnp.mean(scaled * normed, axis=-1, keepdims=True)
    return inverse * (scaled - first_mean - normed * second_mean)


def normal_parts(v):
    density = 0.3989422804014327 * jnp.exp(-0.5 * v * v)
    t = 1.0 / (1.0 + 0.2316419 * jnp.abs(v))
    series = t * (
        0.319381530
        + t * (-0.356563782 + t * (1.781477937 + t * (-1.821255978 + t * 1.330274429)))
    )
    tail = density * series
    return jnp.where(v >= 0.0, 1.0 - tail, tail), density


class Layout:
    def __init__(self, devices):
        self.devices = devices
        bits = devices.bit_length() - 1
        rest = list(range(1, bits))
        self.groups = [[0]] + [rest[i : i + 2] for i in range(0, len(rest), 2)]
        self.packed = devices == 32

    def masks(self, group):
        found = [0]
        for bit in group:
            found = found + [m | (1 << bit) for m in found]
        return found


def swap(array, mask, devices):
    return lax.ppermute(array, AXES, [(i, i ^ mask) for i in range(devices)])


def unpack(me, pieces, layout, stride, first, rows, put):
    low, mid, high = (layout.masks(g) for g in layout.groups)
    for a, outer in enumerate(mid):
        for b, core in enumerate(low):
            ref = pieces[a * len(low) + b]
            for c, inner in enumerate(high):
                device = me ^ (outer | core | inner)
                put(device, ref[c * stride + first : c * stride + first + rows, :])


def weight(me, pieces, layout, stride, first, rows, scratch):
    def put(device, values):
        scratch[pl.ds(pl.multiple_of(device * rows, rows), rows), :] = values

    unpack(me, pieces, layout, stride, first, rows, put)


def pack(me, layout, rows, get, keep, send, first):
    low, mid, high = (layout.masks(g) for g in layout.groups)
    for a, outer in enumerate(mid):
        for c, inner in enumerate(high):
            slot = a * len(high) + c
            for core, ref in zip(low, (keep, send)):
                device = me ^ (outer | inner | core)
                ref[slot, first : first + rows, :] = get(device).astype(ref.dtype)


def segment_masks(ids):
    place = lax.broadcasted_iota(jnp.int32, (PAIR, ids.shape[1]), 0)
    same = place == ids
    hot = jnp.where(same, 1.0, 0.0).astype(F32)
    penalty = jnp.where(same | (place >= 4), 0.0, -MASKED)
    return hot.T.astype(BF16), penalty


def penalties(ids):
    place = lax.broadcasted_iota(jnp.int32, (PAIR, ids.shape[1]), 0)
    return jnp.where((place == ids) | (place >= 4), 0.0, -MASKED).astype(BF16)


def one_hot(ids):
    place = lax.broadcasted_iota(jnp.int32, (PAIR, ids.shape[1]), 0)
    return jnp.where(place == ids, 1.0, 0.0).astype(F32).T.astype(BF16)


def spread(part, half):
    empty = jnp.zeros_like(part)
    return [part, empty] if half == 0 else [empty, part]


def attend(query_t, keys, value_t, hot, penalty, mixture_t, logs):
    length = keys.shape[0]

    def pair(p, carry):
        columns = pl.ds(pl.multiple_of(p * PAIR, PAIR), PAIR)
        left = jnp.concatenate([keys[:, columns], hot[...]], axis=1)
        for half in range(2):
            rows = pl.ds(pl.multiple_of(p * PAIR + half * HEAD_DIM, HEAD_DIM), HEAD_DIM)
            right = jnp.concatenate(spread(query_t[rows, :], half) + [penalty[...]], axis=0)
            scores = dot(left, right)
            highest = jnp.max(scores, axis=0, keepdims=True)
            weights = jnp.exp(scores - highest).astype(BF16)
            values = jnp.concatenate(
                [value_t[rows, :], jnp.ones((16, length), BF16)], axis=0
            )
            found = dot(values, weights)
            denominator = found[HEAD_DIM : HEAD_DIM + 1, :]
            mixture_t[rows, :] = (found[:HEAD_DIM, :] / denominator).astype(BF16)
            logs[2 * p + half] = highest + jnp.log(denominator)
        return carry

    lax.fori_loop(0, HEADS // 2, pair, 0)


def attend_back(
    query_t, query, keys, key_t, values, slope_t, slope, hot, penalty, logs, deltas,
    query_grad_t, key_grad, value_grad,
):
    tokens = query.shape[0]
    lane = lax.broadcasted_iota(jnp.int32, (tokens, PAIR), 1)

    def pair(p, carry):
        columns = pl.ds(pl.multiple_of(p * PAIR, PAIR), PAIR)
        left = jnp.concatenate([keys[:, columns], hot[...]], axis=1)
        value_pair = values[:, columns]
        key_sum, value_sum = None, None
        for half in range(2):
            rows = pl.ds(pl.multiple_of(p * PAIR + half * HEAD_DIM, HEAD_DIM), HEAD_DIM)
            right = jnp.concatenate(spread(query_t[rows, :], half) + [penalty[...]], axis=0)
            chances = jnp.exp(dot(left, right) - logs[2 * p + half])
            slopes = dot(value_pair, jnp.concatenate(spread(slope_t[rows, :], half), axis=0))
            grads = (chances * (slopes - deltas[2 * p + half])).astype(BF16)
            query_grad_t[rows, :] = dot(key_t[rows, :], grads) * HEAD_DIM**-0.5
            mine = (lane < HEAD_DIM) if half == 0 else (lane >= HEAD_DIM)
            none = jnp.zeros((tokens, PAIR), BF16)
            value_part = dot(chances.astype(BF16), jnp.where(mine, slope[:, columns], none))
            key_part = dot(grads, jnp.where(mine, query[:, columns], none))
            value_sum = value_part if value_sum is None else value_sum + value_part
            key_sum = key_part if key_sum is None else key_sum + key_part
        key_grad[:, columns] = key_sum
        value_grad[:, columns] = value_sum
        return carry

    lax.fori_loop(0, HEADS // 2, pair, 0)


def deltas_of(slope_t, mixture_t, deltas):
    for head in range(HEADS):
        rows = slice(head * HEAD_DIM, (head + 1) * HEAD_DIM)
        deltas[head] = jnp.sum(
            slope_t[rows, :].astype(F32) * mixture_t[rows, :].astype(F32), axis=0, keepdims=True
        )


VM = pl.BlockSpec(memory_space=pltpu.VMEM)
SM = pl.BlockSpec(memory_space=pltpu.SMEM)


def call(kernel, outs, args, scratch, flops, name):
    moved = sum(math.prod(a.shape) * a.dtype.itemsize for a in args[1:])
    moved += sum(math.prod(s) * jnp.dtype(d).itemsize for s, d in outs)
    return pl.pallas_call(
        kernel,
        out_shape=[jax.ShapeDtypeStruct(s, d) for s, d in outs],
        in_specs=[SM] + [VM] * (len(args) - 1),
        out_specs=[VM] * len(outs),
        scratch_shapes=[pltpu.VMEM(s, d) for s, d in scratch],
        compiler_params=pltpu.CompilerParams(vmem_limit_bytes=56 << 20),
        cost_estimate=pl.CostEstimate(flops=flops, bytes_accessed=moved, transcendentals=0),
        name=name,
    )(*args)


def weights_from(refs, me, layout, stride, plan, scratch):
    if not layout.packed:
        return list(refs)
    for (first, rows), ref in zip(plan, scratch):
        weight(me, refs, layout, stride, first, rows, ref)
    return list(scratch)


def self_forward(me, layout, pieces, stride, tokens, ids, vectors):
    count = len(tokens)
    share, width = tokens[0].shape[0] - 0, tokens[0].shape[1]
    return count, share, width


def make_self_forward(layout, parts, share, width, stride, n_pieces):
    length = parts * share

    def kernel(*refs):
        me_ref, refs = refs[0], list(refs[1:])
        pieces, refs = refs[:n_pieces], refs[n_pieces:]
        tokens, refs = refs[:parts], refs[parts:]
        ids, vectors, query, keys, values, mixture_t, logs = refs[:7]
        scratch = refs[7:]
        query_t, value_t, hot, penalty = scratch[:4]
        me = me_ref[0]
        rows = width // layout.devices
        plan = [(i * rows, rows) for i in range(3)]
        query_w, key_w, value_w = weights_from(pieces, me, layout, stride, plan, scratch[4:])
        scaled = (dot(tokens[0][:share, :], query_w[...]) + vectors[QUERY_BIAS : QUERY_BIAS + 1, :]).astype(BF16) * BF16(HEAD_DIM**-0.5)
        query[...] = scaled
        query_t[...] = scaled.T
        for i in range(parts):
            here = slice(i * share, (i + 1) * share)
            keys[here, :] = dot(tokens[i][:share, :], key_w[...]).astype(BF16)
            found = (dot(tokens[i][:share, :], value_w[...]) + vectors[VALUE_BIAS : VALUE_BIAS + 1, :]).astype(BF16)
            values[here, :] = found
            value_t[:, here] = found.T
        hot[...] = one_hot(ids[...])
        penalty[...] = penalties(ids[:, :share])
        attend(query_t, keys, value_t, hot, penalty, mixture_t, logs)

    outs = [
        ((share, width), BF16),
        ((length, width), BF16),
        ((length, width), BF16),
        ((width, share), BF16),
        ((HEADS, 1, share), F32),
    ]
    scratch = [((width, share), BF16), ((width, length), BF16), ((length, PAIR), BF16), ((PAIR, share), BF16)]
    if layout.packed:
        scratch += [((width, width), BF16)] * 3
    flops = 2 * share * width * width + 4 * length * width * width + 4 * share * length * width
    return kernel, outs, scratch, flops


def make_cross_forward(layout, parts, share, memory_share, width, stride, n_pieces):
    memory_length = parts * memory_share

    def kernel(*refs):
        me_ref, refs = refs[0], list(refs[1:])
        pieces, refs = refs[:n_pieces], refs[n_pieces:]
        tokens, refs = refs[:parts], refs[parts:]
        ids, memory_ids, vectors, mixture_t = refs[:4]
        first_sum, second_sum, query, memory_keys, memory_values, cross_t, logs = refs[4:11]
        scratch = refs[11:]
        query_t, value_t, hot, penalty = scratch[:4]
        me = me_ref[0]
        rows = width // layout.devices
        plan = [(i * rows, rows) for i in range(5)]
        output_w, query_w, key_w, value_w, source_w = weights_from(
            pieces, me, layout, stride, plan, scratch[4:]
        )

        def vector(i):
            return vectors[i : i + 1, :]

        h = tokens[0][:share, :].astype(F32) + dot_tn(mixture_t[...], output_w[...]) + vector(OUTPUT_BIAS)
        first_sum[...] = h
        first = normalize(h)[0] * vector(ATTENTION_GAIN) + vector(ATTENTION_SHIFT)
        scaled = (dot(first.astype(BF16), query_w[...]) + vector(SOURCE_QUERY_BIAS)).astype(BF16) * BF16(HEAD_DIM**-0.5)
        query[...] = scaled
        query_t[...] = scaled.T
        for i in range(parts):
            here = slice(i * memory_share, (i + 1) * memory_share)
            memory = tokens[i][share:, :]
            memory_keys[here, :] = dot(memory, key_w[...]).astype(BF16)
            memory_values[here, :] = (dot(memory, value_w[...]) + vector(SOURCE_VALUE_BIAS)).astype(BF16)
        value_t[...] = memory_values[...].T
        hot[...] = one_hot(memory_ids[...])
        penalty[...] = penalties(ids[:, :share])
        attend(query_t, memory_keys, value_t, hot, penalty, cross_t, logs)
        first = normalize(first_sum[...])[0] * vector(ATTENTION_GAIN) + vector(ATTENTION_SHIFT)
        second_sum[...] = first + dot_tn(cross_t[...], source_w[...]) + vector(SOURCE_OUTPUT_BIAS)

    outs = [
        ((share, width), F32),
        ((share, width), F32),
        ((share, width), BF16),
        ((memory_length, width), BF16),
        ((memory_length, width), BF16),
        ((width, share), BF16),
        ((HEADS, 1, share), F32),
    ]
    scratch = [((width, share), BF16), ((width, memory_length), BF16), ((memory_length, PAIR), BF16), ((PAIR, share), BF16)]
    if layout.packed:
        scratch += [((width, width), BF16)] * 5
    flops = 6 * share * width * width + 4 * memory_length * width * width + 4 * share * memory_length * width
    return kernel, outs, scratch, flops


def grad_outs(layout, rows, width, natural):
    if layout.packed:
        slots = layout.devices // 2
        return [((slots, rows, width), BF16)] * 2
    return [(s, F32) for s in natural]


def make_inner(layout, share, width, hidden, stride, n_pieces):
    blocks = hidden // width
    half = share // 2

    def kernel(*refs):
        me_ref, refs = refs[0], list(refs[1:])
        pieces, refs = refs[:n_pieces], refs[n_pieces:]
        second_sum, cotangent, vectors = refs[:3]
        out_own, out_send, back, sums = refs[3:7]
        grads, scratch = refs[7:9], refs[9:]
        low, active, gate, slope = scratch[:4]
        me = me_ref[0]
        rows = width // layout.devices
        if layout.packed:
            inner_w, outer_w, gathered = scratch[4:7]

            for block in range(blocks):
                def put(device, values, block=block):
                    inner_w[block, pl.ds(pl.multiple_of(device * rows, rows), rows), :] = values

                unpack(me, pieces, layout, stride, block * rows, rows, put)

            def put_outer(device, values):
                per = width // (blocks * rows)
                inner_w_row = pl.multiple_of((device % per) * blocks * rows, blocks * rows)
                outer_w[device // per, pl.ds(inner_w_row, blocks * rows), :] = values

            unpack(me, pieces, layout, stride, blocks * rows, blocks * rows, put_outer)
        else:
            inner_w, outer_w = pieces

        def vector(i):
            return vectors[i : i + 1, :]

        second = normalize(second_sum[...])[0] * vector(SOURCE_GAIN) + vector(SOURCE_SHIFT)
        low[...] = second.astype(BF16)
        back[...] = second + vector(OUTER_BIAS)

        def forward(block, carry):
            inner = dot(low[...], inner_w[block]) + vectors[pl.ds(INNER_BIAS + block, 1), :]
            chance, density = normal_parts(inner)
            found = (inner * chance).astype(BF16)
            active[block] = found
            gate[block] = chance + inner * density
            back[...] += dot(found, outer_w[block])
            return carry

        lax.fori_loop(0, blocks, forward, 0)
        normed, inverse = normalize(back[...])
        final = normed * vector(FINAL_GAIN) + vector(FINAL_SHIFT)
        out_own[...] = final[:half, :]
        out_send[...] = final[half:, :].astype(BF16)
        upstream = cotangent[...].astype(F32)
        sums[0:1, :] = total(upstream * normed)
        sums[1:2, :] = total(upstream)
        back3 = normalize_back(upstream, normed, inverse, vector(FINAL_GAIN))
        slope[...] = back3.astype(BF16)
        sums[2:3, :] = total(slope[...])
        sums[7:8, :] = jnp.zeros_like(sums[7:8, :])
        back[...] = back3

        def backward(block, carry):
            grad = dot_nt(slope[...], outer_w[block]) * gate[block]
            inner_low = grad.astype(BF16)
            sums[pl.ds(3 + block, 1), :] = total(inner_low)
            outer_grad = dot_tn(active[block], slope[...])
            inner_grad = dot_tn(low[...], inner_low)
            back[...] += dot_nt(inner_low, inner_w[block])
            if layout.packed:
                gathered[block] = inner_grad
                gathered[blocks + block] = outer_grad
            else:
                grads[0][block] = inner_grad
                grads[1][block] = outer_grad
            return carry

        lax.fori_loop(0, blocks, backward, 0)
        if layout.packed:
            keep, send = grads
            for block in range(blocks):
                def get(device, block=block):
                    return gathered[block, pl.ds(pl.multiple_of(device * rows, rows), rows), :]

                pack(me, layout, rows, get, keep, send, block * rows)

            def get_outer(device):
                per = width // (blocks * rows)
                row = pl.multiple_of((device % per) * blocks * rows, blocks * rows)
                return gathered[blocks + device // per, pl.ds(row, blocks * rows), :]

            pack(me, layout, blocks * rows, get_outer, keep, send, blocks * rows)

    outs = [((half, width), F32), ((half, width), BF16), ((share, width), F32), ((8, width), F32)]
    outs += grad_outs(layout, 2 * blocks * (width // layout.devices), width, [(blocks, width, width)] * 2)
    scratch = [((share, width), BF16), ((blocks, share, width), BF16), ((blocks, share, width), F32), ((share, width), BF16)]
    if layout.packed:
        scratch += [((blocks, width, width), BF16)] * 2 + [((2 * blocks, width, width), F32)]
    return kernel, outs, scratch, 12 * share * width * hidden


def make_cross_back(layout, parts, share, memory_share, width, stride, n_pieces):
    memory_length = parts * memory_share

    def kernel(*refs):
        me_ref, refs = refs[0], list(refs[1:])
        pieces, refs = refs[:n_pieces], refs[n_pieces:]
        (back2_in, first_sum, second_sum, query, memory_keys, memory_values, cross_t, logs, ids,
         memory_ids, mixture_t, vectors) = refs[:12]
        refs = refs[12:]
        back1, self_slope, self_slope_t, self_deltas, sums, key_own, value_own = refs[:7]
        sends, refs = refs[7 : 7 + parts - 1], refs[7 + parts - 1 :]
        n_grads = 2 if layout.packed else 3
        grads, scratch = refs[:n_grads], refs[n_grads:]
        (slope_t, slope, key_t, hot, penalty, query_t, deltas, query_grad_t, key_grad, value_grad) = scratch[:10]
        me = me_ref[0]
        rows = width // layout.devices
        if layout.packed:
            plan = [(0, rows), (rows, rows), (4 * rows, rows)]
            output_w, query_w, source_w = weights_from(pieces, me, layout, stride, plan, scratch[10:13])
            dense = scratch[13]
        else:
            output_w, query_w, source_w = pieces

        def vector(i):
            return vectors[i : i + 1, :]

        def give(index, grad):
            if layout.packed:
                dense[...] = grad

                def get(device):
                    return dense[pl.ds(pl.multiple_of(device * rows, rows), rows), :]

                pack(me, layout, rows, get, grads[0], grads[1], index * rows)
            else:
                grads[index][...] = grad

        upstream = back2_in[...]
        normed, inverse = normalize(second_sum[...])
        sums[0:1, :] = total(upstream * normed)
        sums[1:2, :] = total(upstream)
        back2 = normalize_back(upstream, normed, inverse, vector(SOURCE_GAIN))
        back1[...] = back2
        cross_low = back2.astype(BF16)
        sums[2:3, :] = total(cross_low)
        give(0, dot(cross_t[...], cross_low))
        found = dot_nt(cross_low, source_w[...]).astype(BF16)
        slope[...] = found
        slope_t[...] = found.T
        deltas_of(slope_t, cross_t, deltas)
        query_t[...] = query[...].T
        key_t[...] = memory_keys[...].T
        hot[...] = one_hot(memory_ids[...])
        penalty[...] = penalties(ids[:, :share])
        attend_back(query_t, query, memory_keys, key_t, memory_values, slope_t, slope, hot, penalty,
                    logs, deltas, query_grad_t, key_grad, value_grad)
        key_own[...] = key_grad[:memory_share, :]
        value_own[...] = value_grad[:memory_share, :]
        for i in range(1, parts):
            here = slice(i * memory_share, (i + 1) * memory_share)
            sends[i - 1][:memory_share, :] = key_grad[here, :].astype(BF16)
            sends[i - 1][memory_share:, :] = value_grad[here, :].astype(BF16)
        query_low = query_grad_t[...].T.astype(BF16)
        sums[3:4, :] = total(query_low)
        normed, inverse = normalize(first_sum[...])
        first_low = (normed * vector(ATTENTION_GAIN) + vector(ATTENTION_SHIFT)).astype(BF16)
        give(1, dot_tn(first_low, query_low))
        upstream = back1[...] + dot_nt(query_low, query_w[...])
        sums[4:5, :] = total(upstream * normed)
        sums[5:6, :] = total(upstream)
        grad = normalize_back(upstream, normed, inverse, vector(ATTENTION_GAIN))
        back1[...] = grad
        branch_low = grad.astype(BF16)
        sums[6:7, :] = total(branch_low)
        sums[7:8, :] = jnp.zeros_like(sums[7:8, :])
        give(2, dot(mixture_t[...], branch_low))
        found = dot_nt(branch_low, output_w[...]).astype(BF16)
        self_slope[...] = found
        self_slope_t[...] = found.T
        deltas_of(self_slope_t, mixture_t, self_deltas)

    outs = [
        ((share, width), F32),
        ((share, width), BF16),
        ((width, share), BF16),
        ((HEADS, 1, share), F32),
        ((8, width), F32),
        ((memory_share, width), F32),
        ((memory_share, width), F32),
    ]
    outs += [((2 * memory_share, width), BF16)] * (parts - 1)
    outs += grad_outs(layout, 3 * (width // layout.devices), width, [(width, width)] * 3)
    scratch = [
        ((width, share), BF16),
        ((share, width), BF16),
        ((width, memory_length), BF16),
        ((memory_length, PAIR), BF16),
        ((PAIR, share), BF16),
        ((width, share), BF16),
        ((HEADS, 1, share), F32),
        ((width, share), F32),
        ((memory_length, width), F32),
        ((memory_length, width), F32),
    ]
    if layout.packed:
        scratch += [((width, width), BF16)] * 3 + [((width, width), F32)]
    flops = 14 * share * width * width + 10 * share * memory_length * width
    return kernel, outs, scratch, flops


def make_self_back(layout, parts, share, width):
    length = parts * share

    def kernel(*refs):
        query, keys, values, slope, slope_t, logs, deltas, ids = refs[1:9]
        query_low, key_own, value_own = refs[9:12]
        sends, scratch = refs[12 : 12 + parts - 1], refs[12 + parts - 1 :]
        query_t, key_t, hot, penalty, query_grad_t, key_grad, value_grad = scratch
        query_t[...] = query[...].T
        key_t[...] = keys[...].T
        hot[...] = one_hot(ids[...])
        penalty[...] = penalties(ids[:, :share])
        attend_back(query_t, query, keys, key_t, values, slope_t, slope, hot, penalty, logs, deltas,
                    query_grad_t, key_grad, value_grad)
        query_low[...] = query_grad_t[...].T.astype(BF16)
        key_own[...] = key_grad[:share, :]
        value_own[...] = value_grad[:share, :]
        for i in range(1, parts):
            here = slice(i * share, (i + 1) * share)
            sends[i - 1][:share, :] = key_grad[here, :].astype(BF16)
            sends[i - 1][share:, :] = value_grad[here, :].astype(BF16)

    outs = [((share, width), BF16), ((share, width), F32), ((share, width), F32)]
    outs += [((2 * share, width), BF16)] * (parts - 1)
    scratch = [
        ((width, share), BF16),
        ((width, length), BF16),
        ((length, PAIR), BF16),
        ((PAIR, share), BF16),
        ((width, share), F32),
        ((length, width), F32),
        ((length, width), F32),
    ]
    return kernel, outs, scratch, 10 * share * length * width


def make_last(layout, parts, share, memory_share, width, strides, n_pieces):
    half, memory_half = share // 2, memory_share // 2

    def kernel(*refs):
        me_ref, refs = refs[0], list(refs[1:])
        pieces, refs = refs[:n_pieces], refs[n_pieces:]
        others, refs = refs[:n_pieces] if layout.packed else refs[:2], refs[n_pieces if layout.packed else 2 :]
        tokens, back1, query_low, key_own, value_own, memory_key_own, memory_value_own = refs[:7]
        refs = refs[7:]
        received, refs = refs[: parts - 1], refs[parts - 1 :]
        memory_received, refs = refs[: parts - 1], refs[parts - 1 :]
        in_own, in_send, memory_own, memory_send, sums = refs[:5]
        n_grads = 2 if layout.packed else 5
        grads, scratch = refs[5 : 5 + n_grads], refs[5 + n_grads :]
        me = me_ref[0]
        rows = width // layout.devices
        if layout.packed:
            query_w, key_w, value_w = weights_from(pieces, me, layout, strides[0], [(i * rows, rows) for i in range(3)], scratch[:3])
            source_key, source_value = weights_from(others, me, layout, strides[1], [(2 * rows, rows), (3 * rows, rows)], scratch[3:5])
            dense = scratch[5]
        else:
            query_w, key_w, value_w = pieces
            source_key, source_value = others

        def give(index, grad):
            if layout.packed:
                dense[...] = grad

                def get(device):
                    return dense[pl.ds(pl.multiple_of(device * rows, rows), rows), :]

                pack(me, layout, rows, get, grads[0], grads[1], index * rows)
            else:
                grads[index][...] = grad

        memory = tokens[share:, :]
        key_sum, value_sum = memory_key_own[...], memory_value_own[...]
        for ref in memory_received:
            key_sum = key_sum + ref[:memory_share, :].astype(F32)
            value_sum = value_sum + ref[memory_share:, :].astype(F32)
        key_low, value_low = key_sum.astype(BF16), value_sum.astype(BF16)
        sums[2:3, :] = total(value_low)
        give(3, dot_tn(memory, key_low))
        give(4, dot_tn(memory, value_low))
        grad = dot_nt(key_low, source_key[...]) + dot_nt(value_low, source_value[...])
        memory_own[...] = grad[:memory_half, :]
        memory_send[...] = grad[memory_half:, :].astype(BF16)
        own = tokens[:share, :]
        key_sum, value_sum = key_own[...], value_own[...]
        for ref in received:
            key_sum = key_sum + ref[:share, :].astype(F32)
            value_sum = value_sum + ref[share:, :].astype(F32)
        key_low, value_low = key_sum.astype(BF16), value_sum.astype(BF16)
        sums[0:1, :] = total(query_low[...])
        sums[1:2, :] = total(value_low)
        sums[3:8, :] = jnp.zeros_like(sums[3:8, :])
        give(0, dot_tn(own, query_low[...]))
        give(1, dot_tn(own, key_low))
        give(2, dot_tn(own, value_low))
        grad = back1[...] + dot_nt(query_low[...], query_w[...]) + dot_nt(key_low, key_w[...]) + dot_nt(value_low, value_w[...])
        in_own[...] = grad[:half, :]
        in_send[...] = grad[half:, :].astype(BF16)

    outs = [
        ((half, width), F32),
        ((half, width), BF16),
        ((memory_half, width), F32),
        ((memory_half, width), BF16),
        ((8, width), F32),
    ]
    outs += grad_outs(layout, 5 * (width // layout.devices), width, [(width, width)] * 5)
    scratch = []
    if layout.packed:
        scratch = [((width, width), BF16)] * 5 + [((width, width), F32)]
    flops = 12 * share * width * width + 8 * memory_share * width * width
    return kernel, outs, scratch, flops


def combine(arrays, splits, out_dtype):
    count = arrays[0].shape[0] // splits
    shape = (count,) + arrays[0].shape[1:]

    def kernel(*refs):
        given, outs = refs[: len(arrays)], refs[len(arrays) :]
        for i, out in enumerate(outs):
            here = slice(i * count, (i + 1) * count)
            found = given[0][here].astype(F32)
            for ref in given[1:]:
                found = found + ref[here].astype(F32)
            out[...] = found.astype(out.dtype)

    moved = 2 * sum(math.prod(a.shape) * a.dtype.itemsize for a in arrays)
    return pl.pallas_call(
        kernel,
        out_shape=[jax.ShapeDtypeStruct(shape, out_dtype)] * splits,
        in_specs=[VM] * len(arrays),
        out_specs=[VM] * splits,
        compiler_params=pltpu.CompilerParams(vmem_limit_bytes=32 << 20),
        cost_estimate=pl.CostEstimate(flops=0, bytes_accessed=moved, transcendentals=0),
        name="combine",
    )(*arrays)


def gather_tree(block, layout):
    devices = layout.devices
    arrays = [block]
    for group in reversed(layout.groups):
        if group != [0]:
            joined = arrays[0] if len(arrays) == 1 else jnp.concatenate(arrays, axis=0)
            arrays = [joined] + [swap(joined, m, devices) for m in layout.masks(group)[1:]]
        else:
            arrays = [a for array in arrays for a in (array, swap(array, 1, devices))]
    return arrays


def scatter_tree(keep, send, layout):
    devices = layout.devices
    given = [keep, swap(send, 1, devices)]
    for group in layout.groups[1:]:
        masks = layout.masks(group)
        parts = combine(given, len(masks), BF16)
        given = [parts[0]] + [swap(a, m, devices) for a, m in zip(parts[1:], masks[1:])]
    return combine(given, 1, F32)[0]


def reduce_all(array, layout):
    for group in layout.groups[::-1]:
        array = sum([swap(array, m, layout.devices) for m in layout.masks(group)[1:]], array)
    return array


def per_device(
    tokens, memory, target_ids, source_ids, cotangent,
    query_weight, key_weight, value_weight, output_weight, query_bias, value_bias, output_bias,
    attention_gain, attention_shift,
    source_query, source_key, source_value, source_output, source_query_bias, source_value_bias,
    source_output_bias, source_gain, source_shift,
    inner_weight, inner_bias, outer_weight, outer_bias, final_gain, final_shift,
    *, devices, sequence,
):
    layout = Layout(devices)
    row_count, block, width = tokens.shape
    memory_block = memory.shape[1]
    parts = sequence // row_count
    share, memory_share = row_count * block, row_count * memory_block
    hidden = inner_weight.shape[1]
    blocks = hidden // width
    me = lax.axis_index(AXES)
    me_array = me.reshape(1).astype(jnp.int32)
    turn = (me // parts) % row_count
    narrow, wide = width // devices, hidden // devices

    def packet(arrays):
        return gather_tree(jnp.concatenate(arrays, axis=0), layout)

    def whole(array):
        return lax.all_gather(array, AXES, axis=0, tiled=True)

    if layout.packed:
        inner_rows = inner_weight.reshape(narrow, blocks, width).transpose(1, 0, 2).reshape(blocks * narrow, width)
        packet_self = packet([query_weight, key_weight, value_weight])
        packet_cross = packet([output_weight, source_query, source_key, source_value, source_output])
        packet_inner = packet([inner_rows, outer_weight])
        set_self, set_cross, set_inner = packet_self, packet_cross, packet_inner
        set_back, set_last, set_memory = packet_cross, packet_self, packet_cross
        strides = (3 * narrow, 5 * narrow, 2 * blocks * narrow)
    else:
        full = [whole(w) for w in (query_weight, key_weight, value_weight, output_weight, source_query, source_key, source_value, source_output)]
        set_self, set_cross = full[:3], full[3:]
        set_inner = [
            whole(inner_weight).reshape(width, blocks, width).transpose(1, 0, 2),
            whole(outer_weight).reshape(blocks, width, width),
        ]
        set_back, set_last, set_memory = [full[3], full[4], full[7]], full[:3], full[5:7]
        strides = (0, 0, 0)

    short = jnp.stack([query_bias, value_bias, output_bias, attention_gain, attention_shift,
                       source_query_bias, source_value_bias, source_output_bias, source_gain,
                       source_shift, outer_bias, final_gain, final_shift])
    lane = lax.broadcasted_iota(jnp.int32, (1, width), 1)
    spread_short = jnp.where(lane // narrow == me, jnp.tile(short, (1, devices)), 0)
    place = lax.broadcasted_iota(jnp.int32, (blocks, width), 0) * width + lane
    spread_wide = jnp.where(place // wide == me, jnp.tile(inner_bias.reshape(1, wide), (blocks, width // wide)), 0)
    vectors = jnp.concatenate([spread_short, spread_wide, jnp.zeros((7, width), BF16)], axis=0)
    vectors = reduce_all(vectors, layout).astype(F32)

    def pick(array, index):
        return lax.dynamic_index_in_dim(array, index, axis=0, keepdims=False)

    other = row_count - 1 - turn
    sent = jnp.concatenate([pick(tokens, other), pick(memory, other)], axis=0)
    came = swap(sent, parts, devices)
    own = jnp.concatenate([pick(tokens, turn), came[:block], pick(memory, turn), came[block:]], axis=0)
    row_tokens = [own] + [swap(own, m, devices) for m in range(1, parts)]
    cot = jnp.concatenate([pick(cotangent, turn), swap(pick(cotangent, other), parts, devices)], axis=0)
    all_ids = jnp.concatenate([target_ids, source_ids], axis=1)
    own_ids = jnp.stack([pick(all_ids, turn), swap(pick(all_ids, other), parts, devices)])
    row_ids = [own_ids] + [swap(own_ids, m, devices) for m in range(1, parts)]
    ids = jnp.concatenate([i[:, :block].reshape(1, share) for i in row_ids], axis=1)
    memory_ids = jnp.concatenate([i[:, block:].reshape(1, memory_share) for i in row_ids], axis=1)

    def run(made, name, *args):
        kernel, outs, scratch, flops = made
        return call(kernel, outs, (me_array,) + args, scratch, flops, name)

    query, keys, values, mixture_t, logs = run(
        make_self_forward(layout, parts, share, width, strides[0], len(set_self)), "self_forward",
        *set_self, *row_tokens, ids, vectors,
    )
    first_sum, second_sum, cross_query, memory_keys, memory_values, cross_t, cross_logs = run(
        make_cross_forward(layout, parts, share, memory_share, width, strides[1], len(set_cross)),
        "cross_forward", *set_cross, *row_tokens, ids, memory_ids, vectors, mixture_t,
    )
    out_own, out_send, back2_in, sums_inner, *grads_inner = run(
        make_inner(layout, share, width, hidden, strides[2], len(set_inner)), "inner",
        *set_inner, second_sum, cot, vectors,
    )
    found = run(
        make_cross_back(layout, parts, share, memory_share, width, strides[1], len(set_back)),
        "cross_back", *set_back, back2_in, first_sum, second_sum, cross_query, memory_keys,
        memory_values, cross_t, cross_logs, ids, memory_ids, mixture_t, vectors,
    )
    back1, slope, slope_t, deltas, sums_cross, memory_key_own, memory_value_own = found[:7]
    memory_sends, grads_cross = found[7 : 7 + parts - 1], found[7 + parts - 1 :]
    memory_received = [swap(a, m + 1, devices) for m, a in enumerate(memory_sends)]
    found = run(
        make_self_back(layout, parts, share, width), "self_back",
        query, keys, values, slope, slope_t, logs, deltas, ids,
    )
    query_low, key_own, value_own = found[:3]
    received = [swap(a, m + 1, devices) for m, a in enumerate(found[3:])]
    in_own, in_send, memory_own, memory_send, sums_last, *grads_last = run(
        make_last(layout, parts, share, memory_share, width, strides[:2], len(set_last)), "last",
        *set_last, *set_memory, own, back1, query_low, key_own, value_own, memory_key_own,
        memory_value_own, *received, *memory_received,
    )

    def regroup(mine, theirs):
        came = swap(theirs, parts, devices).astype(F32)
        return jnp.where(turn == 0, jnp.stack([mine, came]), jnp.stack([came, mine]))

    output = regroup(out_own, out_send)
    input_gradient = regroup(in_own, in_send)
    memory_gradient = regroup(memory_own, memory_send)

    if layout.packed:
        got = scatter_tree(*grads_inner, layout)[0]
        inner_share = got[: blocks * narrow].reshape(blocks, narrow, width).transpose(1, 0, 2).reshape(narrow, hidden)
        outer_share = got[blocks * narrow :]
        got = scatter_tree(*grads_cross, layout)[0]
        source_output_share, source_query_share, output_share = (got[i * narrow : (i + 1) * narrow] for i in range(3))
        got = scatter_tree(*grads_last, layout)[0]
        query_share, key_share, value_share, source_key_share, source_value_share = (got[i * narrow : (i + 1) * narrow] for i in range(5))
    else:
        def scatter(array):
            return lax.psum_scatter(array, AXES, scatter_dimension=0, tiled=True)

        inner_share = scatter(grads_inner[0].transpose(1, 0, 2).reshape(width, hidden))
        outer_share = scatter(grads_inner[1].reshape(hidden, width))
        source_output_share, source_query_share, output_share = (scatter(g) for g in grads_cross)
        query_share, key_share, value_share, source_key_share, source_value_share = (scatter(g) for g in grads_last)
    sums = reduce_all(jnp.concatenate([sums_inner, sums_cross, sums_last], axis=0), layout)

    def narrow_part(row):
        return lax.dynamic_slice(sums[row], (me * narrow,), (narrow,))

    inner_bias_share = lax.dynamic_slice(sums[3 : 3 + blocks].reshape(hidden), (me * wide,), (wide,))
    return (
        output,
        input_gradient,
        memory_gradient,
        query_share,
        key_share,
        value_share,
        output_share,
        narrow_part(16),
        narrow_part(17),
        narrow_part(14),
        narrow_part(12),
        narrow_part(13),
        source_query_share,
        source_key_share,
        source_value_share,
        source_output_share,
        narrow_part(11),
        narrow_part(18),
        narrow_part(10),
        narrow_part(8),
        narrow_part(9),
        inner_share,
        inner_bias_share,
        outer_share,
        narrow_part(2),
        narrow_part(0),
        narrow_part(1),
    )


def solution(mesh):
    sequence, devices = mesh.shape["seq"], mesh.size
    tokens, ids = P("dp", "seq", None), P("dp", "seq")
    matrix, vector = P(AXES, None), P(AXES)
    attention = (matrix,) * 4 + (vector,) * 5
    inner = (matrix, vector, matrix, vector, vector, vector)
    return jax.shard_map(
        functools.partial(per_device, devices=devices, sequence=sequence),
        mesh=mesh,
        in_specs=(tokens, tokens, ids, ids, tokens) + attention + attention + inner,
        out_specs=(tokens, tokens, tokens) + attention + attention + inner,
        check_vma=False,
    )
```

```python
import functools
import math

import jax
import jax.numpy as jnp
from jax import lax
from jax.experimental import pallas as pl
from jax.experimental.pallas import tpu as pltpu
from jax.sharding import PartitionSpec as P

HEADS = 8
HEAD_DIM = 64
PAIR = 128
EPSILON = 1e-05
MASKED = 1e9
AXES = ("dp", "seq")
F32 = jnp.float32
BF16 = jnp.bfloat16

(
    OUTPUT_BIAS,
    ATTENTION_GAIN,
    ATTENTION_SHIFT,
    SOURCE_QUERY_BIAS,
    SOURCE_VALUE_BIAS,
    SOURCE_OUTPUT_BIAS,
    SOURCE_GAIN,
    SOURCE_SHIFT,
    OUTER_BIAS,
    FINAL_GAIN,
    FINAL_SHIFT,
    INNER_BIAS,
) = range(12)
Z_MASKS = (0, 8, 16, 24)
VM = pl.BlockSpec(memory_space=pltpu.VMEM)
SM = pl.BlockSpec(memory_space=pltpu.SMEM)


def dot(a, b):
    return lax.dot_general(a, b, (((1,), (0,)), ((), ())), preferred_element_type=F32)


def dot_nt(a, b):
    return lax.dot_general(a, b, (((1,), (1,)), ((), ())), preferred_element_type=F32)


def dot_tn(a, b):
    return lax.dot_general(a, b, (((0,), (0,)), ((), ())), preferred_element_type=F32)


def total(values):
    return jnp.sum(values.astype(F32), axis=0, keepdims=True)


def normalize(h):
    average = jnp.mean(h, axis=-1, keepdims=True)
    centered = h - average
    variance = jnp.mean(centered * centered, axis=-1, keepdims=True)
    inverse = lax.rsqrt(variance + EPSILON)
    return centered * inverse, inverse


def normalize_back(upstream, normed, inverse, gain):
    scaled = upstream * gain
    first_mean = jnp.mean(scaled, axis=-1, keepdims=True)
    second_mean = jnp.mean(scaled * normed, axis=-1, keepdims=True)
    return inverse * (scaled - first_mean - normed * second_mean)


def normal_parts(v):
    density = 0.3989422804014327 * jnp.exp(-0.5 * v * v)
    t = 1.0 / (1.0 + 0.2316419 * jnp.abs(v))
    series = t * (
        0.319381530
        + t * (-0.356563782 + t * (1.781477937 + t * (-1.821255978 + t * 1.330274429)))
    )
    tail = density * series
    return jnp.where(v >= 0.0, 1.0 - tail, tail), density


def penalties(ids):
    place = lax.broadcasted_iota(jnp.int32, (PAIR, ids.shape[1]), 0)
    return jnp.where((place == ids) | (place >= 4), 0.0, -MASKED).astype(BF16)


def one_hot(ids):
    place = lax.broadcasted_iota(jnp.int32, (PAIR, ids.shape[1]), 0)
    return jnp.where(place == ids, 1.0, 0.0).astype(F32).T.astype(BF16)


def spread(part, half):
    empty = jnp.zeros_like(part)
    return [part, empty] if half == 0 else [empty, part]


def attend(query_t, keys, value_t, hot, penalty, mixture_t, logs):
    length = keys.shape[0]

    def pair(p, carry):
        columns = pl.ds(pl.multiple_of(p * PAIR, PAIR), PAIR)
        left = jnp.concatenate([keys[:, columns], hot[...]], axis=1)
        for half in range(2):
            rows = pl.ds(pl.multiple_of(p * PAIR + half * HEAD_DIM, HEAD_DIM), HEAD_DIM)
            right = jnp.concatenate(spread(query_t[rows, :], half) + [penalty[...]], axis=0)
            scores = dot(left, right)
            highest = jnp.max(scores, axis=0, keepdims=True)
            weights = jnp.exp(scores - highest).astype(BF16)
            values = jnp.concatenate(
                [value_t[rows, :], jnp.ones((16, length), BF16)], axis=0
            )
            found = dot(values, weights)
            denominator = found[HEAD_DIM : HEAD_DIM + 1, :]
            mixture_t[rows, :] = (found[:HEAD_DIM, :] / denominator).astype(BF16)
            logs[2 * p + half] = highest + jnp.log(denominator)
        return carry

    lax.fori_loop(0, HEADS // 2, pair, 0)


def attend_back(
    query_t, query, keys, key_t, values, slope_t, slope, hot, penalty, logs, deltas,
    query_grad_t, key_grad, value_grad,
):
    tokens = query.shape[0]
    lane = lax.broadcasted_iota(jnp.int32, (tokens, PAIR), 1)

    def pair(p, carry):
        columns = pl.ds(pl.multiple_of(p * PAIR, PAIR), PAIR)
        left = jnp.concatenate([keys[:, columns], hot[...]], axis=1)
        value_pair = values[:, columns]
        key_sum, value_sum = None, None
        for half in range(2):
            rows = pl.ds(pl.multiple_of(p * PAIR + half * HEAD_DIM, HEAD_DIM), HEAD_DIM)
            right = jnp.concatenate(spread(query_t[rows, :], half) + [penalty[...]], axis=0)
            chances = jnp.exp(dot(left, right) - logs[2 * p + half])
            slopes = dot(value_pair, jnp.concatenate(spread(slope_t[rows, :], half), axis=0))
            grads = (chances * (slopes - deltas[2 * p + half])).astype(BF16)
            query_grad_t[rows, :] = dot(key_t[rows, :], grads) * HEAD_DIM**-0.5
            mine = (lane < HEAD_DIM) if half == 0 else (lane >= HEAD_DIM)
            none = jnp.zeros((tokens, PAIR), BF16)
            value_part = dot(chances.astype(BF16), jnp.where(mine, slope[:, columns], none))
            key_part = dot(grads, jnp.where(mine, query[:, columns], none))
            value_sum = value_part if value_sum is None else value_sum + value_part
            key_sum = key_part if key_sum is None else key_sum + key_part
        key_grad[:, columns] = key_sum
        value_grad[:, columns] = value_sum
        return carry

    lax.fori_loop(0, HEADS // 2, pair, 0)


def deltas_of(slope_t, mixture_t, deltas):
    for head in range(HEADS):
        rows = slice(head * HEAD_DIM, (head + 1) * HEAD_DIM)
        deltas[head] = jnp.sum(
            slope_t[rows, :].astype(F32) * mixture_t[rows, :].astype(F32), axis=0, keepdims=True
        )


def swap(array, mask, devices):
    return lax.ppermute(array, AXES, [(i, i ^ mask) for i in range(devices)])


def turned_swap(array, step):
    pairs = []
    for i in range(32):
        near = 2 if i % 2 == 0 else 4
        pairs.append((i, i ^ (near if step == 1 else 6 - near)))
    return lax.ppermute(array, AXES, pairs)


def after(value, *others):
    return lax.optimization_barrier((value, others))[0]


def places(me):
    found = []
    for core in range(2):
        near = jnp.where(((me & 1) ^ core) == 0, 2, 4)
        for far in range(2):
            for step in range(2):
                for at, mask in enumerate(Z_MASKS):
                    device = me ^ (core | mask)
                    if step:
                        device = device ^ near
                    if far:
                        device = device ^ (6 - near)
                    found.append((core, far, step * 4 + at, device))
    return found


def unpack(me, pieces, stride, first, rows, scratch):
    for core, far, slot, device in places(me):
        ref = pieces[2 * core + far]
        at = slot * stride + first
        scratch[pl.ds(pl.multiple_of(device * rows, rows), rows), :] = ref[at : at + rows, :]


def vector_sum(pieces, stride, first):
    found = None
    for ref in pieces:
        for slot in range(8):
            part = ref[slot * stride + first : (slot + 1) * stride, :].astype(F32)
            found = part if found is None else found + part
    return found


class Grads:
    def __init__(self, me, refs, dense, rows):
        self.me, self.refs, self.dense, self.rows = me, refs, dense, rows

    def put(self, index, grad):
        if self.dense is None:
            self.refs[index][...] = grad
            return
        self.dense[...] = grad
        rows = self.rows
        for core, far, slot, device in places(self.me):
            found = self.dense[pl.ds(pl.multiple_of(device * rows, rows), rows), :]
            self.refs[core][far * 8 + slot, index * rows : (index + 1) * rows, :] = found.astype(BF16)

    def put_sums(self, first, sums):
        if self.dense is None:
            self.refs[-1][...] = sums
            return
        low = sums.astype(BF16)
        for ref in self.refs:
            for slot in range(16):
                ref[slot, first : first + sums.shape[0], :] = low


def grad_outs(packed, count, rows, width, sums):
    if packed:
        return [((16, count * rows + sums, width), BF16)] * 2
    return [((width, width), F32)] * count + [((sums, width), F32)]


def call(kernel, outs, args, scratch, micros, name):
    moved = sum(math.prod(a.shape) * a.dtype.itemsize for a in args[1:])
    moved += sum(math.prod(s) * jnp.dtype(d).itemsize for s, d in outs)
    return pl.pallas_call(
        kernel,
        out_shape=[jax.ShapeDtypeStruct(s, d) for s, d in outs],
        in_specs=[SM] + [VM] * (len(args) - 1),
        out_specs=[VM] * len(outs),
        scratch_shapes=[pltpu.VMEM(s, d) for s, d in scratch],
        compiler_params=pltpu.CompilerParams(vmem_limit_bytes=56 << 20),
        cost_estimate=pl.CostEstimate(
            flops=int(micros * 1.15e9), bytes_accessed=moved, transcendentals=0
        ),
        name=name,
    )(*args)


def make_tokens_packet(block, memory_block, width):
    rows = block + memory_block + 8

    def kernel(turn, tokens, memory, target_ids, source_ids, cotangent, sent, kept, cot_sent, cot_kept):
        mine = turn[0]
        for row, out, cot in ((1 - mine, sent, cot_sent), (mine, kept, cot_kept)):
            out[:block, :] = tokens[row]
            out[block : block + memory_block, :] = memory[row]
            ids = target_ids[pl.ds(row, 1), :].astype(F32)
            ids = jnp.concatenate([ids, jnp.zeros((1, width - block), F32)], axis=1)
            others = source_ids[pl.ds(row, 1), :].astype(F32)
            others = jnp.concatenate([others, jnp.zeros((1, width - memory_block), F32)], axis=1)
            place = lax.broadcasted_iota(jnp.int32, (8, width), 0)
            found = jnp.where(place == 0, ids, jnp.where(place == 1, others, 0.0))
            out[block + memory_block :, :] = found.astype(BF16)
            cot[...] = cotangent[row]

    return kernel, [((rows, width), BF16)] * 2 + [((block, width), BF16)] * 2


def placed(me, parts, width):
    here = lax.broadcasted_iota(jnp.int32, (parts.shape[1], width), 0) + me * parts.shape[1]
    lane = lax.broadcasted_iota(jnp.int32, (parts.shape[1], width), 1)
    return dot(parts, jnp.where(lane == here, 1.0, 0.0).astype(BF16))


def make_self_packet(narrow, width):
    def kernel(me_ref, query_w, key_w, value_w, biases, out):
        for i, ref in enumerate((query_w, key_w, value_w)):
            out[i * narrow : (i + 1) * narrow, :] = ref[...]
        found = placed(me_ref[0], biases[...], width)
        out[3 * narrow :, :] = jnp.concatenate([found, jnp.zeros((6, width), F32)], axis=0).astype(BF16)

    return kernel, [((3 * narrow + 8, width), BF16)]


def make_cross_packet(narrow, width, blocks):
    def kernel(me_ref, *refs):
        weights, short, wide, out = refs[:5], refs[5], refs[6], refs[7]
        me = me_ref[0]
        for i, ref in enumerate(weights):
            out[i * narrow : (i + 1) * narrow, :] = ref[...]
        found = placed(me, short[...], width)
        per = width // wide.shape[1]
        row = placed(me % per, wide[...], width)
        place = lax.broadcasted_iota(jnp.int32, (blocks, width), 0)
        spread_row = jnp.where(place == me // per, row, 0.0)
        rest = jnp.zeros((16 - found.shape[0] - blocks, width), F32)
        out[5 * narrow :, :] = jnp.concatenate([found, spread_row, rest], axis=0).astype(BF16)

    return kernel, [((5 * narrow + 16, width), BF16)]


def join(arrays):
    def kernel(*refs):
        at = 0
        for ref in refs[:-1]:
            refs[-1][at : at + ref.shape[0], :] = ref[...]
            at += ref.shape[0]

    rows = sum(a.shape[0] for a in arrays)
    return pl.pallas_call(
        kernel,
        out_shape=jax.ShapeDtypeStruct((rows, arrays[0].shape[1]), arrays[0].dtype),
        in_specs=[VM] * len(arrays),
        out_specs=VM,
        compiler_params=pltpu.CompilerParams(vmem_limit_bytes=16 << 20),
        cost_estimate=pl.CostEstimate(flops=1 << 20, bytes_accessed=0, transcendentals=0),
        name="join",
    )(*arrays)


def make_project(packed, parts, rows, block, memory_block, width, narrow, n_pieces):
    share = rows * block
    length = parts * share
    memory_share = rows * memory_block
    stride = 3 * narrow + 8

    def kernel(*refs):
        me_ref, refs = refs[0], list(refs[1:])
        pieces, refs = refs[:n_pieces], refs[n_pieces:]
        tokens, refs = refs[: parts * rows], refs[parts * rows :]
        query, query_t, keys, values, value_t, memory, ids, memory_ids = refs[:8]
        scratch = refs[8:]
        me = me_ref[0]
        if packed:
            for i in range(3):
                unpack(me, pieces, stride, i * narrow, narrow, scratch[i])
            query_w, key_w, value_w = scratch
            biases = vector_sum(pieces, stride, 3 * narrow)
        else:
            query_w, key_w, value_w = pieces[:3]
            biases = pieces[3][...]
        own = jnp.concatenate([t[:block, :] for t in tokens[:rows]], axis=0)
        scaled = (dot(own, query_w[...]) + biases[0:1, :]).astype(BF16) * BF16(HEAD_DIM**-0.5)
        query[...] = scaled
        query_t[...] = scaled.T
        for i in range(parts):
            here = slice(i * share, (i + 1) * share)
            some = tokens[i * rows : (i + 1) * rows]
            own = jnp.concatenate([t[:block, :] for t in some], axis=0)
            keys[here, :] = dot(own, key_w[...]).astype(BF16)
            found = (dot(own, value_w[...]) + biases[1:2, :]).astype(BF16)
            values[here, :] = found
            value_t[:, here] = found.T
        for i, t in enumerate(tokens):
            memory[i * memory_block : (i + 1) * memory_block, :] = t[block : block + memory_block, :]
            found = t[block + memory_block :, :].astype(F32).astype(jnp.int32)
            ids[:, i * block : (i + 1) * block] = found[0:1, :block]
        found = [t[block + memory_block :, :].astype(F32).astype(jnp.int32)[1:2, :memory_block] for t in tokens]
        memory_ids[...] = jnp.concatenate(found, axis=1)

    outs = [
        ((share, width), BF16),
        ((width, share), BF16),
        ((length, width), BF16),
        ((length, width), BF16),
        ((width, length), BF16),
        ((parts * memory_share, width), BF16),
        ((1, length), jnp.int32),
        ((1, parts * memory_share), jnp.int32),
    ]
    return kernel, outs, [((width, width), BF16)] * 3 if packed else []


def make_self_attention(share, length, width):
    def kernel(me_ref, query_t, keys, value_t, ids, mixture_t, logs, hot, penalty):
        hot[...] = one_hot(ids[...])
        penalty[...] = penalties(ids[:, :share])
        attend(query_t, keys, value_t, hot, penalty, mixture_t, logs)

    outs = [((width, share), BF16), ((HEADS, 1, share), F32)]
    return kernel, outs, [((length, PAIR), BF16), ((PAIR, share), BF16)]


def make_cross_forward(packed, rows, block, memory_length, width, narrow, n_pieces):
    share = rows * block
    stride = 5 * narrow + 16

    def kernel(*refs):
        me_ref, refs = refs[0], list(refs[1:])
        pieces, refs = refs[:n_pieces], refs[n_pieces:]
        tokens, refs = refs[:rows], refs[rows:]
        memory, ids, memory_ids, mixture_t = refs[:4]
        first_sum, second_sum, query, memory_keys, memory_values, cross_t, logs, vectors = refs[4:12]
        scratch = refs[12:]
        query_t, value_t, hot, penalty = scratch[:4]
        if packed:
            for i in range(5):
                unpack(me_ref[0], pieces, stride, i * narrow, narrow, scratch[4 + i])
            output_w, query_w, key_w, value_w, source_w = scratch[4:]
            vectors[...] = vector_sum(pieces, stride, 5 * narrow)
        else:
            output_w, query_w, key_w, value_w, source_w = pieces[:5]
            vectors[...] = pieces[5][...]

        def vector(i):
            return vectors[i : i + 1, :]

        own = jnp.concatenate([t[:block, :] for t in tokens], axis=0)
        h = own.astype(F32) + dot_tn(mixture_t[...], output_w[...]) + vector(OUTPUT_BIAS)
        first_sum[...] = h
        first = normalize(h)[0] * vector(ATTENTION_GAIN) + vector(ATTENTION_SHIFT)
        scaled = (dot(first.astype(BF16), query_w[...]) + vector(SOURCE_QUERY_BIAS)).astype(BF16) * BF16(HEAD_DIM**-0.5)
        query[...] = scaled
        query_t[...] = scaled.T
        memory_keys[...] = dot(memory[...], key_w[...]).astype(BF16)
        memory_values[...] = (dot(memory[...], value_w[...]) + vector(SOURCE_VALUE_BIAS)).astype(BF16)
        value_t[...] = memory_values[...].T
        hot[...] = one_hot(memory_ids[...])
        penalty[...] = penalties(ids[:, :share])
        attend(query_t, memory_keys, value_t, hot, penalty, cross_t, logs)
        first = normalize(first_sum[...])[0] * vector(ATTENTION_GAIN) + vector(ATTENTION_SHIFT)
        second_sum[...] = first + dot_tn(cross_t[...], source_w[...]) + vector(SOURCE_OUTPUT_BIAS)

    outs = [
        ((share, width), F32),
        ((share, width), F32),
        ((share, width), BF16),
        ((memory_length, width), BF16),
        ((memory_length, width), BF16),
        ((width, share), BF16),
        ((HEADS, 1, share), F32),
        ((16, width), F32),
    ]
    scratch = [((width, share), BF16), ((width, memory_length), BF16), ((memory_length, PAIR), BF16), ((PAIR, share), BF16)]
    if packed:
        scratch += [((width, width), BF16)] * 5
    return kernel, outs, scratch


def make_inner(packed, rows, block, width, hidden, narrow, n_pieces):
    blocks = hidden // width
    share = rows * block
    per = width // (blocks * narrow)

    def kernel(*refs):
        me_ref, refs = refs[0], list(refs[1:])
        pieces, refs = refs[:n_pieces], refs[n_pieces:]
        second_sum, cot_own, cot_came, vectors = refs[:4]
        out_own, out_send, back, sums = refs[4:8]
        grads, scratch = refs[8:10], refs[10:]
        low, active, gate, slope = scratch[:4]
        if packed:
            inner_w, outer_w, gathered = scratch[4:7]
            whole = pieces[0]
            for device in range(32):
                at = device * 2 * blocks * narrow
                for i in range(blocks):
                    inner_w[i, device * narrow : (device + 1) * narrow, :] = whole[at + i * narrow : at + (i + 1) * narrow, :]
                row = (device % per) * blocks * narrow
                outer_w[device // per, row : row + blocks * narrow, :] = whole[at + blocks * narrow : at + 2 * blocks * narrow, :]
        else:
            inner_w, outer_w = pieces

        def vector(i):
            return vectors[i : i + 1, :]

        second = normalize(second_sum[...])[0] * vector(SOURCE_GAIN) + vector(SOURCE_SHIFT)
        low[...] = second.astype(BF16)
        back[...] = second + vector(OUTER_BIAS)

        def forward(i, carry):
            inner = dot(low[...], inner_w[i]) + vectors[pl.ds(INNER_BIAS + i, 1), :]
            chance, density = normal_parts(inner)
            found = (inner * chance).astype(BF16)
            active[i] = found
            gate[i] = chance + inner * density
            back[...] += dot(found, outer_w[i])
            return carry

        lax.fori_loop(0, blocks, forward, 0)
        normed, inverse = normalize(back[...])
        final = normed * vector(FINAL_GAIN) + vector(FINAL_SHIFT)
        out_own[...] = final[:block, :]
        out_send[...] = final[block:, :].astype(BF16)
        upstream = jnp.concatenate([cot_own[...], cot_came[...]], axis=0).astype(F32)
        sums[0:1, :] = total(upstream * normed)
        sums[1:2, :] = total(upstream)
        back3 = normalize_back(upstream, normed, inverse, vector(FINAL_GAIN))
        slope[...] = back3.astype(BF16)
        sums[2:3, :] = total(slope[...])
        sums[7:8, :] = jnp.zeros_like(sums[7:8, :])
        back[...] = back3

        def backward(i, carry):
            grad = dot_nt(slope[...], outer_w[i]) * gate[i]
            inner_low = grad.astype(BF16)
            sums[pl.ds(3 + i, 1), :] = total(inner_low)
            outer_grad = dot_tn(active[i], slope[...])
            inner_grad = dot_tn(low[...], inner_low)
            back[...] += dot_nt(inner_low, inner_w[i])
            if packed:
                gathered[i] = inner_grad
                gathered[blocks + i] = outer_grad
            else:
                grads[0][i] = inner_grad
                grads[1][i] = outer_grad
            return carry

        lax.fori_loop(0, blocks, backward, 0)
        if packed:
            tall = blocks * narrow
            for core, far, slot, device in places(me_ref[0]):
                ref, at = grads[core], far * 8 + slot
                row = pl.multiple_of(device * narrow, narrow)
                for i in range(blocks):
                    ref[at, i * narrow : (i + 1) * narrow, :] = gathered[i, pl.ds(row, narrow), :].astype(BF16)
                row = pl.multiple_of((device % per) * tall, tall)
                ref[at, tall:, :] = gathered[blocks + device // per, pl.ds(row, tall), :].astype(BF16)

    outs = [((block, width), F32), ((block, width), BF16), ((share, width), F32), ((8, width), F32)]
    if packed:
        outs += [((16, 2 * blocks * narrow, width), BF16)] * 2
    else:
        outs += [((blocks, width, width), F32)] * 2
    scratch = [((share, width), BF16), ((blocks, share, width), BF16), ((blocks, share, width), F32), ((share, width), BF16)]
    if packed:
        scratch += [((blocks, width, width), BF16)] * 2 + [((2 * blocks, width, width), F32)]
    return kernel, outs, scratch


def make_cross_back(packed, parts, share, memory_share, width, narrow, n_pieces):
    memory_length = parts * memory_share
    stride = 5 * narrow + 16

    def kernel(*refs):
        me_ref, refs = refs[0], list(refs[1:])
        pieces, refs = refs[:n_pieces], refs[n_pieces:]
        (back2_in, first_sum, second_sum, query, memory_keys, memory_values, cross_t, logs, ids,
         memory_ids, mixture_t, vectors, sums_inner) = refs[:13]
        refs = refs[13:]
        back1, self_slope, self_slope_t, self_deltas, key_own, value_own = refs[:6]
        sends, refs = refs[6 : 6 + parts - 1], refs[6 + parts - 1 :]
        n_grads = 2 if packed else 4
        grad_refs, scratch = refs[:n_grads], refs[n_grads:]
        (slope_t, slope, key_t, hot, penalty, query_t, deltas, query_grad_t, key_grad, value_grad, sums) = scratch[:11]
        if packed:
            for i, at in enumerate((0, 1, 4)):
                unpack(me_ref[0], pieces, stride, at * narrow, narrow, scratch[11 + i])
            output_w, query_w, source_w = scratch[11:14]
        else:
            output_w, query_w, source_w = pieces
        grads = Grads(me_ref[0], grad_refs, scratch[14] if packed else None, narrow)

        def vector(i):
            return vectors[i : i + 1, :]

        sums[0:7, :] = sums_inner[0:7, :]
        upstream = back2_in[...]
        normed, inverse = normalize(second_sum[...])
        sums[7:8, :] = total(upstream * normed)
        sums[8:9, :] = total(upstream)
        back2 = normalize_back(upstream, normed, inverse, vector(SOURCE_GAIN))
        back1[...] = back2
        cross_low = back2.astype(BF16)
        sums[9:10, :] = total(cross_low)
        grads.put(0, dot(cross_t[...], cross_low))
        found = dot_nt(cross_low, source_w[...]).astype(BF16)
        slope[...] = found
        slope_t[...] = found.T
        deltas_of(slope_t, cross_t, deltas)
        query_t[...] = query[...].T
        key_t[...] = memory_keys[...].T
        hot[...] = one_hot(memory_ids[...])
        penalty[...] = penalties(ids[:, :share])
        attend_back(query_t, query, memory_keys, key_t, memory_values, slope_t, slope, hot, penalty,
                    logs, deltas, query_grad_t, key_grad, value_grad)
        key_own[...] = key_grad[:memory_share, :]
        value_own[...] = value_grad[:memory_share, :]
        for i in range(1, parts):
            here = slice(i * memory_share, (i + 1) * memory_share)
            sends[i - 1][:memory_share, :] = key_grad[here, :].astype(BF16)
            sends[i - 1][memory_share:, :] = value_grad[here, :].astype(BF16)
        query_low = query_grad_t[...].T.astype(BF16)
        sums[10:11, :] = total(query_low)
        normed, inverse = normalize(first_sum[...])
        first_low = (normed * vector(ATTENTION_GAIN) + vector(ATTENTION_SHIFT)).astype(BF16)
        grads.put(1, dot_tn(first_low, query_low))
        upstream = back1[...] + dot_nt(query_low, query_w[...])
        sums[11:12, :] = total(upstream * normed)
        sums[12:13, :] = total(upstream)
        grad = normalize_back(upstream, normed, inverse, vector(ATTENTION_GAIN))
        back1[...] = grad
        branch_low = grad.astype(BF16)
        sums[13:14, :] = total(branch_low)
        sums[14:16, :] = jnp.zeros_like(sums[14:16, :])
        grads.put_sums(3 * narrow, sums[...])
        grads.put(2, dot(mixture_t[...], branch_low))
        found = dot_nt(branch_low, output_w[...]).astype(BF16)
        self_slope[...] = found
        self_slope_t[...] = found.T
        deltas_of(self_slope_t, mixture_t, self_deltas)

    outs = [
        ((share, width), F32),
        ((share, width), BF16),
        ((width, share), BF16),
        ((HEADS, 1, share), F32),
        ((memory_share, width), F32),
        ((memory_share, width), F32),
    ]
    outs += [((2 * memory_share, width), BF16)] * (parts - 1)
    outs += grad_outs(packed, 3, narrow, width, 16)
    scratch = [
        ((width, share), BF16),
        ((share, width), BF16),
        ((width, memory_length), BF16),
        ((memory_length, PAIR), BF16),
        ((PAIR, share), BF16),
        ((width, share), BF16),
        ((HEADS, 1, share), F32),
        ((width, share), F32),
        ((memory_length, width), F32),
        ((memory_length, width), F32),
        ((16, width), F32),
    ]
    if packed:
        scratch += [((width, width), BF16)] * 3 + [((width, width), F32)]
    return kernel, outs, scratch


def make_self_back(packed, parts, rows, block, memory_block, width, narrow, n_pieces, n_others):
    share, memory_share = rows * block, rows * memory_block
    length = parts * share

    def kernel(*refs):
        me_ref, refs = refs[0], list(refs[1:])
        pieces, refs = refs[:n_pieces], refs[n_pieces:]
        others, refs = refs[:n_others], refs[n_others:]
        tokens, refs = refs[:rows], refs[rows:]
        (query, keys, values, slope, slope_t, logs, deltas, ids, back1, memory_key_own,
         memory_value_own) = refs[:11]
        memory_received, refs = refs[11 : 11 + parts - 1], refs[11 + parts - 1 :]
        in_part, key_own, value_own, memory_own, memory_send = refs[:5]
        sends, refs = refs[5 : 5 + parts - 1], refs[5 + parts - 1 :]
        n_grads = 2 if packed else 4
        grad_refs, scratch = refs[:n_grads], refs[n_grads:]
        query_t, key_t, hot, penalty, query_grad_t, key_grad, value_grad, sums = scratch[:8]
        me = me_ref[0]
        if packed:
            unpack(me, pieces, 3 * narrow + 8, 0, narrow, scratch[8])
            for i in range(2):
                unpack(me, others, 5 * narrow + 16, (2 + i) * narrow, narrow, scratch[9 + i])
            query_w, source_key, source_value = scratch[8:11]
        else:
            (query_w,) = pieces
            source_key, source_value = others
        grads = Grads(me, grad_refs, scratch[11] if packed else None, narrow)
        query_t[...] = query[...].T
        key_t[...] = keys[...].T
        hot[...] = one_hot(ids[...])
        penalty[...] = penalties(ids[:, :share])
        attend_back(query_t, query, keys, key_t, values, slope_t, slope, hot, penalty, logs, deltas,
                    query_grad_t, key_grad, value_grad)
        key_own[...] = key_grad[:share, :]
        value_own[...] = value_grad[:share, :]
        for i in range(1, parts):
            here = slice(i * share, (i + 1) * share)
            sends[i - 1][:share, :] = key_grad[here, :].astype(BF16)
            sends[i - 1][share:, :] = value_grad[here, :].astype(BF16)
        query_low = query_grad_t[...].T.astype(BF16)
        own = jnp.concatenate([t[:block, :] for t in tokens], axis=0)
        in_part[...] = back1[...] + dot_nt(query_low, query_w[...])
        sums[0:1, :] = total(query_low)
        grads.put(0, dot_tn(own, query_low))
        memory = jnp.concatenate([t[block : block + memory_block, :] for t in tokens], axis=0)
        key_sum, value_sum = memory_key_own[...], memory_value_own[...]
        for ref in memory_received:
            key_sum = key_sum + ref[:memory_share, :].astype(F32)
            value_sum = value_sum + ref[memory_share:, :].astype(F32)
        key_low, value_low = key_sum.astype(BF16), value_sum.astype(BF16)
        sums[1:2, :] = total(value_low)
        sums[2:8, :] = jnp.zeros_like(sums[2:8, :])
        grads.put_sums(3 * narrow, sums[...])
        grads.put(1, dot_tn(memory, key_low))
        grads.put(2, dot_tn(memory, value_low))
        grad = dot_nt(key_low, source_key[...]) + dot_nt(value_low, source_value[...])
        memory_own[...] = grad[:memory_block, :]
        memory_send[...] = grad[memory_block:, :].astype(BF16)

    outs = [((share, width), F32)] * 3 + [((memory_block, width), F32), ((memory_block, width), BF16)]
    outs += [((2 * share, width), BF16)] * (parts - 1)
    outs += grad_outs(packed, 3, narrow, width, 8)
    scratch = [
        ((width, share), BF16),
        ((width, length), BF16),
        ((length, PAIR), BF16),
        ((PAIR, share), BF16),
        ((width, share), F32),
        ((length, width), F32),
        ((length, width), F32),
        ((8, width), F32),
    ]
    if packed:
        scratch += [((width, width), BF16)] * 3 + [((width, width), F32)]
    return kernel, outs, scratch


def make_last(packed, parts, rows, block, memory_block, width, narrow, n_pieces):
    share = rows * block

    def kernel(*refs):
        me_ref, refs = refs[0], list(refs[1:])
        pieces, refs = refs[:n_pieces], refs[n_pieces:]
        tokens, refs = refs[:rows], refs[rows:]
        in_part, key_own, value_own, memory_send = refs[:4]
        received, refs = refs[4 : 4 + parts - 1], refs[4 + parts - 1 :]
        in_own, in_send = refs[:2]
        n_grads = 2 if packed else 3
        grad_refs, scratch = refs[2 : 2 + n_grads], refs[2 + n_grads :]
        sums = scratch[0]
        me = me_ref[0]
        if packed:
            for i in range(2):
                unpack(me, pieces, 3 * narrow + 8, (1 + i) * narrow, narrow, scratch[1 + i])
            key_w, value_w = scratch[1:3]
        else:
            key_w, value_w = pieces
        grads = Grads(me, grad_refs, scratch[3] if packed else None, narrow)
        own = jnp.concatenate([t[:block, :] for t in tokens], axis=0)
        key_sum, value_sum = key_own[...], value_own[...]
        for ref in received:
            key_sum = key_sum + ref[:share, :].astype(F32)
            value_sum = value_sum + ref[share:, :].astype(F32)
        key_low, value_low = key_sum.astype(BF16), value_sum.astype(BF16)
        sums[0:1, :] = total(value_low)
        sums[1:8, :] = jnp.zeros_like(sums[1:8, :])
        grads.put_sums(2 * narrow, sums[...])
        grads.put(0, dot_tn(own, key_low))
        grads.put(1, dot_tn(own, value_low))
        grad = in_part[...] + dot_nt(key_low, key_w[...]) + dot_nt(value_low, value_w[...])
        in_own[...] = grad[:block, :]
        in_send[:block, :] = grad[block:, :].astype(BF16)
        in_send[block:, :] = memory_send[...]

    outs = [((block, width), F32), ((block + memory_block, width), BF16)]
    outs += grad_outs(packed, 2, narrow, width, 8)
    scratch = [((8, width), F32)]
    if packed:
        scratch += [((width, width), BF16)] * 2 + [((width, width), F32)]
    return kernel, outs, scratch


def combine(arrays, splits):
    count = arrays[0].shape[0] // splits
    shape = (count,) + arrays[0].shape[1:]

    def kernel(*refs):
        given, outs = refs[: len(arrays)], refs[len(arrays) :]
        for i, out in enumerate(outs):
            here = slice(i * count, (i + 1) * count)
            found = given[0][here].astype(F32)
            for ref in given[1:]:
                found = found + ref[here].astype(F32)
            out[...] = found.astype(out.dtype)

    return pl.pallas_call(
        kernel,
        out_shape=[jax.ShapeDtypeStruct(shape, BF16)] * splits,
        in_specs=[VM] * len(arrays),
        out_specs=[VM] * splits,
        compiler_params=pltpu.CompilerParams(vmem_limit_bytes=32 << 20),
        cost_estimate=pl.CostEstimate(flops=1 << 20, bytes_accessed=0, transcendentals=0),
        name="combine",
    )(*arrays)


def finish(me_array, arrays, plan, shapes, name):
    def kernel(me_ref, *refs):
        given, outs = refs[: len(arrays)], refs[len(arrays) :]
        found = given[0][0].astype(F32)
        for ref in given[1:]:
            found = found + ref[0].astype(F32)
        plan(me_ref[0], found, outs)

    return call(kernel, [(s, F32) for s in shapes], (me_array, *arrays), [], 0.5, name)


def chosen(me, rows, wide):
    width = rows.shape[1]
    line = lax.broadcasted_iota(jnp.int32, (width, wide), 0)
    here = lax.broadcasted_iota(jnp.int32, (width, wide), 1) + me * wide
    choice = jnp.where(line == here, 1.0, 0.0)
    return lax.dot_general(rows, choice, (((1,), (0,)), ((), ())), precision=lax.Precision.HIGHEST, preferred_element_type=F32)


def reduce_all(array, devices):
    mask = 1
    while mask < devices:
        array = array + swap(array, mask, devices)
        mask *= 2
    return array


def per_device(
    tokens, memory, target_ids, source_ids, cotangent,
    query_weight, key_weight, value_weight, output_weight, query_bias, value_bias, output_bias,
    attention_gain, attention_shift,
    source_query, source_key, source_value, source_output, source_query_bias, source_value_bias,
    source_output_bias, source_gain, source_shift,
    inner_weight, inner_bias, outer_weight, outer_bias, final_gain, final_shift,
    *, devices, sequence,
):
    packed = devices == 32
    rows, block, width = tokens.shape
    memory_block = memory.shape[1]
    parts = sequence // rows
    share, memory_share = rows * block, rows * memory_block
    hidden = inner_weight.shape[1]
    blocks = hidden // width
    me = lax.axis_index(AXES)
    me_array = me.reshape(1).astype(jnp.int32)
    turn = lax.rem(lax.div(me, parts), rows)
    narrow, wide = width // devices, hidden // devices

    def run(made, micros, name, *args):
        kernel, outs, scratch = made
        return call(kernel, outs, (me_array,) + args, scratch, micros, name)

    short_self = jnp.stack([query_bias, value_bias])
    short_cross = jnp.stack([output_bias, attention_gain, attention_shift, source_query_bias,
                             source_value_bias, source_output_bias, source_gain, source_shift,
                             outer_bias, final_gain, final_shift])
    inner_rows = inner_weight.reshape(narrow, blocks, width).transpose(1, 0, 2).reshape(blocks * narrow, width)

    def whole(array):
        return lax.all_gather(array, AXES, axis=0, tiled=True)

    kernel, outs = make_tokens_packet(block, memory_block, width)
    sent, kept, cot_sent, cot_own = call(
        kernel, outs, (turn.reshape(1).astype(jnp.int32), tokens, memory, target_ids, source_ids, cotangent),
        [], 2.0, "tokens_packet",
    )

    if packed:
        set_inner = [whole(jnp.concatenate([inner_rows, outer_weight], axis=0))]
        kernel, outs = make_self_packet(narrow, width)
        (first,) = call(kernel, outs, (me_array, query_weight, key_weight, value_weight, short_self), [], 1.0, "self_packet")
        kernel, outs = make_cross_packet(narrow, width, blocks)
        (second,) = call(kernel, outs, (me_array, output_weight, source_query, source_key, source_value,
                         source_output, short_cross, inner_bias.reshape(1, wide)), [], 1.0, "cross_packet")
        first_z = [swap(first, m, 32) for m in Z_MASKS[1:]]
        came = swap(sent, parts, devices)
        second = after(second, *first_z)
        second_z = [swap(second, m, 32) for m in Z_MASKS[1:]]
        first_a = join(after([first, *first_z], sent))
        first_b = turned_swap(first_a, 1)
        first_c = join([first_a, first_b])
        first_d = turned_swap(first_c, 2)
        set_self = [first_c, first_d, swap(first_c, 1, 32), swap(first_d, 1, 32)]
        second_a = after(join([second, *second_z]), first_b)
        second_b = turned_swap(second_a, 1)
    else:
        came = swap(sent, parts, devices)
        full = [whole(w) for w in (query_weight, key_weight, value_weight, output_weight, source_query, source_key, source_value, source_output)]
        lane = lax.broadcasted_iota(jnp.int32, (1, width), 1)
        place = lax.broadcasted_iota(jnp.int32, (blocks, width), 0) * width + lane
        spread_wide = jnp.where(place // wide == me, jnp.tile(inner_bias.reshape(1, wide), (blocks, width // wide)), 0)

        def natural(short):
            return jnp.where(lane // narrow == me, jnp.tile(short, (1, devices)), 0)

        vectors = jnp.concatenate([natural(short_self), jnp.zeros((6, width), BF16), natural(short_cross), spread_wide, jnp.zeros((1, width), BF16)])
        vectors = reduce_all(vectors, devices).astype(F32)
        set_self = full[:3] + [vectors[:8]]
        set_cross = full[3:] + [vectors[8:]]
        set_inner = [
            whole(inner_weight).reshape(width, blocks, width).transpose(1, 0, 2),
            whole(outer_weight).reshape(blocks, width, width),
        ]
    row_tokens = [kept, came]
    for m in range(1, parts):
        row_tokens += [swap(kept, m, devices), swap(came, m, devices)]
    own_tokens = row_tokens[:rows]
    if packed:
        set_self[0] = after(set_self[0], *second_z)
    query, query_t, keys, values, value_t, row_memory, ids, memory_ids = run(
        make_project(packed, parts, rows, block, memory_block, width, narrow, len(set_self)), 4.0,
        "project", *set_self, *row_tokens,
    )
    if packed:
        second_c = join([second_a, second_b])
        second_d = turned_swap(second_c, 2)
        query_t = after(query_t, second_c)
        cot_sent = after(cot_sent, second_c)
        set_cross = [second_c, second_d, swap(second_c, 1, 32), swap(second_d, 1, 32)]
        set_back, set_query, set_last, set_memory = set_cross, set_self, set_self, set_cross
    else:
        set_back, set_query, set_last, set_memory = [full[3], full[4], full[7]], full[:1], full[1:3], full[5:7]
    cot_came = swap(cot_sent, parts, devices)
    mixture_t, logs = run(
        make_self_attention(share, parts * share, width), 9.0, "self_attention",
        query_t, keys, value_t, ids,
    )
    first_sum, second_sum, cross_query, memory_keys, memory_values, cross_t, cross_logs, vectors = run(
        make_cross_forward(packed, rows, block, parts * memory_share, width, narrow, len(set_cross)),
        9.0, "cross_forward", *set_cross, *own_tokens, row_memory, ids, memory_ids, mixture_t,
    )
    out_own, out_send, back2_in, sums_inner, *grads_inner = run(
        make_inner(packed, rows, block, width, hidden, narrow, len(set_inner)), 18.0, "inner",
        *set_inner, second_sum, cot_own, cot_came, vectors,
    )
    found = run(
        make_cross_back(packed, parts, share, memory_share, width, narrow, len(set_back)), 14.0,
        "cross_back", *set_back, back2_in, first_sum, second_sum, cross_query, memory_keys,
        memory_values, cross_t, cross_logs, ids, memory_ids, mixture_t, vectors, sums_inner,
    )
    back1, slope, slope_t, deltas, memory_key_own, memory_value_own = found[:6]
    memory_sends, grads_cross = found[6 : 6 + parts - 1], found[6 + parts - 1 :]
    memory_received = [swap(a, m + 1, devices) for m, a in enumerate(memory_sends)]
    if packed:
        keep, send = combine([grads_inner[0], swap(grads_inner[1], 1, 32)], 2)
        query = after(query, keep)
        inner_step = [keep, turned_swap(send, 2)]
    found = run(
        make_self_back(packed, parts, rows, block, memory_block, width, narrow, len(set_query), len(set_memory)),
        17.0, "self_back", *set_query, *set_memory, *own_tokens, query, keys, values, slope, slope_t,
        logs, deltas, ids, back1, memory_key_own, memory_value_own, *memory_received,
    )
    in_part, key_own, value_own, memory_own, memory_send = found[:5]
    received = [swap(a, m + 1, devices) for m, a in enumerate(found[5 : 5 + parts - 1])]
    grads_query = found[5 + parts - 1 :]
    if packed:
        keep, send = combine([grads_cross[0], swap(grads_cross[1], 1, 32)], 2)
        cross_step = [keep, turned_swap(send, 2)]
        keep_inner, send_inner = combine(inner_step, 2)
        key_own = after(key_own, keep, keep_inner)
        inner_step = [keep_inner, turned_swap(send_inner, 1)]
    in_own, in_send, *grads_last = run(
        make_last(packed, parts, rows, block, memory_block, width, narrow, len(set_last)), 6.0,
        "last", *set_last, *own_tokens, in_part, key_own, value_own, memory_send, *received,
    )

    def regroup(mine, came):
        came = came.astype(F32)
        return jnp.where(turn == 0, jnp.stack([mine, came]), jnp.stack([came, mine]))

    output = regroup(out_own, swap(out_send, parts, devices))
    in_came = swap(in_send, parts, devices)
    input_gradient = regroup(in_own, in_came[:block])
    memory_gradient = regroup(memory_own, in_came[block:])

    if packed:
        def lower(arrays):
            found = combine(arrays, 4)
            return [found[0]] + [swap(a, m, 32) for a, m in zip(found[1:], Z_MASKS[1:])]

        def rest(grads):
            keep, send = combine([grads[0], swap(grads[1], 1, 32)], 2)
            keep, send = combine([keep, turned_swap(send, 2)], 2)
            return lower([keep, turned_swap(send, 1)])

        def inner_plan(me, found, outs):
            for i in range(blocks):
                outs[0][:, i * width : (i + 1) * width] = found[i * narrow : (i + 1) * narrow, :]
            outs[1][...] = found[blocks * narrow :, :]

        def cross_plan(me, found, outs):
            for i in range(3):
                outs[i][...] = found[i * narrow : (i + 1) * narrow, :]
            sums = found[3 * narrow :, :]
            outs[3][...] = chosen(me, sums, narrow)
            per = width // wide
            line = lax.broadcasted_iota(jnp.int32, (blocks, width), 0)
            row = jnp.sum(jnp.where(line == me // per, sums[3 : 3 + blocks, :], 0.0), axis=0, keepdims=True)
            outs[4][...] = chosen(me % per, row, wide)

        def query_plan(me, found, outs):
            for i in range(3):
                outs[i][...] = found[i * narrow : (i + 1) * narrow, :]
            outs[3][...] = chosen(me, found[3 * narrow :, :], narrow)

        def last_plan(me, found, outs):
            for i in range(2):
                outs[i][...] = found[i * narrow : (i + 1) * narrow, :]
            outs[2][...] = chosen(me, found[2 * narrow :, :], narrow)

        part = (narrow, width)
        inner_step = lower(inner_step)
        keep, send = combine(cross_step, 2)
        cross_step = lower([keep, turned_swap(send, 1)])
        inner_share, outer_share = finish(me_array, inner_step, inner_plan, [(narrow, hidden), (wide, width)], "finish_inner")
        source_output_share, source_query_share, output_share, sums, inner_bias_share = finish(
            me_array, cross_step, cross_plan, [part] * 3 + [(16, narrow), (1, wide)], "finish_cross"
        )
        query_share, source_key_share, source_value_share, sums_query = finish(
            me_array, rest(grads_query), query_plan, [part] * 3 + [(8, narrow)], "finish_query"
        )
        key_share, value_share, sums_last = finish(
            me_array, rest(grads_last), last_plan, [part] * 2 + [(8, narrow)], "finish_last"
        )
        inner_bias_share = inner_bias_share.reshape(wide)
    else:
        def scatter(array):
            return lax.psum_scatter(array, AXES, scatter_dimension=0, tiled=True)

        inner_share = scatter(grads_inner[0].transpose(1, 0, 2).reshape(width, hidden))
        outer_share = scatter(grads_inner[1].reshape(hidden, width))
        source_output_share, source_query_share, output_share = (scatter(g) for g in grads_cross[:3])
        query_share, source_key_share, source_value_share = (scatter(g) for g in grads_query[:3])
        key_share, value_share = (scatter(g) for g in grads_last[:2])
        sums = jnp.concatenate([grads_cross[3], grads_query[3], grads_last[2]], axis=0)
        sums = reduce_all(sums, devices)
        inner_bias_share = lax.dynamic_slice(sums[3 : 3 + blocks].reshape(hidden), (me * wide,), (wide,))
        sums = lax.dynamic_slice(sums, (0, me * narrow), (sums.shape[0], narrow))
        sums, sums_query, sums_last = sums[:16], sums[16:24], sums[24:]
    return (
        output,
        input_gradient,
        memory_gradient,
        query_share,
        key_share,
        value_share,
        output_share,
        sums_query[0],
        sums_last[0],
        sums[13],
        sums[11],
        sums[12],
        source_query_share,
        source_key_share,
        source_value_share,
        source_output_share,
        sums[10],
        sums_query[1],
        sums[9],
        sums[7],
        sums[8],
        inner_share,
        inner_bias_share,
        outer_share,
        sums[2],
        sums[0],
        sums[1],
    )


def solution(mesh):
    sequence, devices = mesh.shape["seq"], mesh.size
    tokens, ids = P("dp", "seq", None), P("dp", "seq")
    matrix, vector = P(AXES, None), P(AXES)
    attention = (matrix,) * 4 + (vector,) * 5
    inner = (matrix, vector, matrix, vector, vector, vector)
    return jax.shard_map(
        functools.partial(per_device, devices=devices, sequence=sequence),
        mesh=mesh,
        in_specs=(tokens, tokens, ids, ids, tokens) + attention + attention + inner,
        out_specs=(tokens, tokens, tokens) + attention + attention + inner,
        check_vma=False,
    )
```

```python
import functools
import math

import jax
import jax.numpy as jnp
from jax import lax
from jax.experimental import pallas as pl
from jax.experimental.pallas import tpu as pltpu
from jax.sharding import PartitionSpec as P

HEADS = 8
HEAD_DIM = 64
PAIR = 128
EPSILON = 1e-05
MASKED = 1e9
AXES = ("dp", "seq")
F32 = jnp.float32
BF16 = jnp.bfloat16

(
    OUTPUT_BIAS,
    ATTENTION_GAIN,
    ATTENTION_SHIFT,
    SOURCE_QUERY_BIAS,
    SOURCE_VALUE_BIAS,
    SOURCE_OUTPUT_BIAS,
    SOURCE_GAIN,
    SOURCE_SHIFT,
    OUTER_BIAS,
    FINAL_GAIN,
    FINAL_SHIFT,
    INNER_BIAS,
) = range(12)
Z_MASKS = (0, 8, 16, 24)
VM = pl.BlockSpec(memory_space=pltpu.VMEM)
SM = pl.BlockSpec(memory_space=pltpu.SMEM)


def dot(a, b):
    return lax.dot_general(a, b, (((1,), (0,)), ((), ())), preferred_element_type=F32)


def dot_nt(a, b):
    return lax.dot_general(a, b, (((1,), (1,)), ((), ())), preferred_element_type=F32)


def dot_tn(a, b):
    return lax.dot_general(a, b, (((0,), (0,)), ((), ())), preferred_element_type=F32)


def total(values):
    return jnp.sum(values.astype(F32), axis=0, keepdims=True)


def normalize(h):
    average = jnp.mean(h, axis=-1, keepdims=True)
    centered = h - average
    variance = jnp.mean(centered * centered, axis=-1, keepdims=True)
    inverse = lax.rsqrt(variance + EPSILON)
    return centered * inverse, inverse


def normalize_back(upstream, normed, inverse, gain):
    scaled = upstream * gain
    first_mean = jnp.mean(scaled, axis=-1, keepdims=True)
    second_mean = jnp.mean(scaled * normed, axis=-1, keepdims=True)
    return inverse * (scaled - first_mean - normed * second_mean)


def normal_parts(v):
    density = 0.3989422804014327 * jnp.exp(-0.5 * v * v)
    t = 1.0 / (1.0 + 0.2316419 * jnp.abs(v))
    series = t * (
        0.319381530
        + t * (-0.356563782 + t * (1.781477937 + t * (-1.821255978 + t * 1.330274429)))
    )
    tail = density * series
    return jnp.where(v >= 0.0, 1.0 - tail, tail), density


def penalties(ids):
    place = lax.broadcasted_iota(jnp.int32, (PAIR, ids.shape[1]), 0)
    return jnp.where((place == ids) | (place >= 4), 0.0, -MASKED).astype(BF16)


def one_hot(ids):
    place = lax.broadcasted_iota(jnp.int32, (PAIR, ids.shape[1]), 0)
    return jnp.where(place == ids, 1.0, 0.0).astype(F32).T.astype(BF16)


def spread(part, half):
    empty = jnp.zeros_like(part)
    return [part, empty] if half == 0 else [empty, part]


def attend(query_t, keys, value_t, hot, penalty, mixture_t, logs):
    length = keys.shape[0]

    def pair(p, carry):
        columns = pl.ds(pl.multiple_of(p * PAIR, PAIR), PAIR)
        left = jnp.concatenate([keys[:, columns], hot[...]], axis=1)
        for half in range(2):
            rows = pl.ds(pl.multiple_of(p * PAIR + half * HEAD_DIM, HEAD_DIM), HEAD_DIM)
            right = jnp.concatenate(spread(query_t[rows, :], half) + [penalty[...]], axis=0)
            scores = dot(left, right)
            highest = jnp.max(scores, axis=0, keepdims=True)
            weights = jnp.exp(scores - highest).astype(BF16)
            values = jnp.concatenate(
                [value_t[rows, :], jnp.ones((16, length), BF16)], axis=0
            )
            found = dot(values, weights)
            denominator = found[HEAD_DIM : HEAD_DIM + 1, :]
            mixture_t[rows, :] = (found[:HEAD_DIM, :] / denominator).astype(BF16)
            logs[2 * p + half] = highest + jnp.log(denominator)
        return carry

    lax.fori_loop(0, keys.shape[1] // PAIR, pair, 0)


def attend_back(
    query_t, query, keys, key_t, values, slope_t, slope, hot, penalty, logs, deltas,
    query_grad_t, key_grad, value_grad,
):
    tokens = query.shape[0]
    lane = lax.broadcasted_iota(jnp.int32, (tokens, PAIR), 1)

    def pair(p, carry):
        columns = pl.ds(pl.multiple_of(p * PAIR, PAIR), PAIR)
        left = jnp.concatenate([keys[:, columns], hot[...]], axis=1)
        value_pair = values[:, columns]
        key_sum, value_sum = None, None
        for half in range(2):
            rows = pl.ds(pl.multiple_of(p * PAIR + half * HEAD_DIM, HEAD_DIM), HEAD_DIM)
            right = jnp.concatenate(spread(query_t[rows, :], half) + [penalty[...]], axis=0)
            chances = jnp.exp(dot(left, right) - logs[2 * p + half])
            slopes = dot(value_pair, jnp.concatenate(spread(slope_t[rows, :], half), axis=0))
            grads = (chances * (slopes - deltas[2 * p + half])).astype(BF16)
            query_grad_t[rows, :] = dot(key_t[rows, :], grads) * HEAD_DIM**-0.5
            mine = (lane < HEAD_DIM) if half == 0 else (lane >= HEAD_DIM)
            none = jnp.zeros((tokens, PAIR), BF16)
            value_part = dot(chances.astype(BF16), jnp.where(mine, slope[:, columns], none))
            key_part = dot(grads, jnp.where(mine, query[:, columns], none))
            value_sum = value_part if value_sum is None else value_sum + value_part
            key_sum = key_part if key_sum is None else key_sum + key_part
        key_grad[:, columns] = key_sum
        value_grad[:, columns] = value_sum
        return carry

    lax.fori_loop(0, keys.shape[1] // PAIR, pair, 0)


def deltas_of(slope_t, mixture_t, deltas):
    for head in range(slope_t.shape[0] // HEAD_DIM):
        rows = slice(head * HEAD_DIM, (head + 1) * HEAD_DIM)
        deltas[head] = jnp.sum(
            slope_t[rows, :].astype(F32) * mixture_t[rows, :].astype(F32), axis=0, keepdims=True
        )


def swap(array, mask, devices):
    return lax.ppermute(array, AXES, [(i, i ^ mask) for i in range(devices)])


def turned_swap(array, step):
    pairs = []
    for i in range(32):
        near = 2 if i % 2 == 0 else 4
        pairs.append((i, i ^ (near if step == 1 else 6 - near)))
    return lax.ppermute(array, AXES, pairs)


def after(value, *others):
    return lax.optimization_barrier((value, others))[0]


def places(me):
    found = []
    for core in range(2):
        near = jnp.where(((me & 1) ^ core) == 0, 2, 4)
        for far in range(2):
            for step in range(2):
                for at, mask in enumerate(Z_MASKS):
                    device = me ^ (core | mask)
                    if step:
                        device = device ^ near
                    if far:
                        device = device ^ (6 - near)
                    found.append((core, far, step * 4 + at, device))
    return found


def unpack(me, pieces, stride, first, rows, scratch):
    for core, far, slot, device in places(me):
        ref = pieces[2 * core + far]
        at = slot * stride + first
        scratch[pl.ds(pl.multiple_of(device * rows, rows), rows), :] = ref[at : at + rows, :]


def vector_sum(pieces, stride, first):
    found = None
    for ref in pieces:
        for slot in range(8):
            part = ref[slot * stride + first : (slot + 1) * stride, :].astype(F32)
            found = part if found is None else found + part
    return found


class Grads:
    def __init__(self, me, refs, dense, rows):
        self.me, self.refs, self.dense, self.rows = me, refs, dense, rows

    def put(self, index, grad):
        if self.dense is None:
            self.refs[index][...] = grad
            return
        self.dense[...] = grad
        rows = self.rows
        for core, far, slot, device in places(self.me):
            found = self.dense[pl.ds(pl.multiple_of(device * rows, rows), rows), :]
            self.refs[core][far * 8 + slot, index * rows : (index + 1) * rows, :] = found.astype(BF16)

    def put_sums(self, first, sums):
        if self.dense is None:
            self.refs[-1][...] = sums
            return
        low = sums.astype(BF16)
        for ref in self.refs:
            for slot in range(16):
                ref[slot, first : first + sums.shape[0], :] = low


def grad_outs(packed, count, rows, width, sums):
    if packed:
        return [((16, count * rows + sums, width), BF16)] * 2
    return [((width, width), F32)] * count + [((sums, width), F32)]


def call(kernel, outs, args, scratch, micros, name):
    moved = sum(math.prod(a.shape) * a.dtype.itemsize for a in args[1:])
    moved += sum(math.prod(s) * jnp.dtype(d).itemsize for s, d in outs)
    return pl.pallas_call(
        kernel,
        out_shape=[jax.ShapeDtypeStruct(s, d) for s, d in outs],
        in_specs=[SM] + [VM] * (len(args) - 1),
        out_specs=[VM] * len(outs),
        scratch_shapes=[pltpu.VMEM(s, d) for s, d in scratch],
        compiler_params=pltpu.CompilerParams(vmem_limit_bytes=56 << 20),
        cost_estimate=pl.CostEstimate(
            flops=int(micros * 1.15e9), bytes_accessed=moved, transcendentals=0
        ),
        name=name,
    )(*args)


def make_tokens_packet(block, memory_block, width):
    rows = block + memory_block + 8

    def kernel(turn, tokens, memory, target_ids, source_ids, sent, kept):
        mine = turn[0]
        for row, out in ((1 - mine, sent), (mine, kept)):
            out[:block, :] = tokens[row]
            out[block : block + memory_block, :] = memory[row]
            ids = target_ids[pl.ds(row, 1), :].astype(F32)
            ids = jnp.concatenate([ids, jnp.zeros((1, width - block), F32)], axis=1)
            others = source_ids[pl.ds(row, 1), :].astype(F32)
            others = jnp.concatenate([others, jnp.zeros((1, width - memory_block), F32)], axis=1)
            place = lax.broadcasted_iota(jnp.int32, (8, width), 0)
            found = jnp.where(place == 0, ids, jnp.where(place == 1, others, 0.0))
            out[block + memory_block :, :] = found.astype(BF16)

    return kernel, [((rows, width), BF16)] * 2


def make_cot_packet(block, width):
    def kernel(turn, cotangent, sent, kept):
        sent[...] = cotangent[1 - turn[0]]
        kept[...] = cotangent[turn[0]]

    return kernel, [((block, width), BF16)] * 2


def make_inner_packet(narrow, width, blocks):
    def kernel(me_ref, inner, outer, out):
        for i in range(blocks):
            out[i * narrow : (i + 1) * narrow, :] = inner[:, i * width : (i + 1) * width]
        out[blocks * narrow :, :] = outer[...]

    return kernel, [((2 * blocks * narrow, width), BF16)]


def placed(me, parts, width):
    here = lax.broadcasted_iota(jnp.int32, (parts.shape[1], width), 0) + me * parts.shape[1]
    lane = lax.broadcasted_iota(jnp.int32, (parts.shape[1], width), 1)
    return dot(parts, jnp.where(lane == here, 1.0, 0.0).astype(BF16))


def make_self_packet(narrow, width):
    def kernel(me_ref, query_w, key_w, value_w, biases, out):
        for i, ref in enumerate((query_w, key_w, value_w)):
            out[i * narrow : (i + 1) * narrow, :] = ref[...]
        found = placed(me_ref[0], biases[0:2, :], width)
        out[3 * narrow :, :] = jnp.concatenate([found, jnp.zeros((6, width), F32)], axis=0).astype(BF16)

    return kernel, [((3 * narrow + 8, width), BF16)]


def make_cross_packet(narrow, width, blocks):
    def kernel(me_ref, *refs):
        weights, short, wide, out = refs[:5], refs[5], refs[6], refs[7]
        me = me_ref[0]
        for i, ref in enumerate(weights):
            out[i * narrow : (i + 1) * narrow, :] = ref[...]
        found = placed(me, short[2:, :], width)
        per = width // wide.shape[1]
        row = placed(lax.rem(me, per), wide[...], width)
        place = lax.broadcasted_iota(jnp.int32, (blocks, width), 0)
        spread_row = jnp.where(place == lax.div(me, per), row, 0.0)
        rest = jnp.zeros((16 - found.shape[0] - blocks, width), F32)
        out[5 * narrow :, :] = jnp.concatenate([found, spread_row, rest], axis=0).astype(BF16)

    return kernel, [((5 * narrow + 16, width), BF16)]


def join(arrays):
    def kernel(*refs):
        at = 0
        for ref in refs[:-1]:
            refs[-1][at : at + ref.shape[0], :] = ref[...]
            at += ref.shape[0]

    rows = sum(a.shape[0] for a in arrays)
    return pl.pallas_call(
        kernel,
        out_shape=jax.ShapeDtypeStruct((rows, arrays[0].shape[1]), arrays[0].dtype),
        in_specs=[VM] * len(arrays),
        out_specs=VM,
        compiler_params=pltpu.CompilerParams(vmem_limit_bytes=16 << 20),
        cost_estimate=pl.CostEstimate(flops=1 << 20, bytes_accessed=0, transcendentals=0),
        name="join",
    )(*arrays)


def make_project(packed, parts, rows, block, memory_block, width, narrow, n_pieces):
    share = rows * block
    length = parts * share
    memory_share = rows * memory_block
    stride = 3 * narrow + 8
    half = width // 2

    def kernel(*refs):
        me_ref, refs = refs[0], list(refs[1:])
        pieces, refs = refs[:n_pieces], refs[n_pieces:]
        tokens, refs = refs[: parts * rows], refs[parts * rows :]
        query, query_t, keys, values, value_t = (refs[2 * i : 2 * i + 2] for i in range(5))
        memory, ids, memory_ids = refs[10:13]
        scratch = refs[13:]
        me = me_ref[0]
        if packed:
            for i in range(3):
                unpack(me, pieces, stride, i * narrow, narrow, scratch[i])
            query_w, key_w, value_w = scratch
            biases = vector_sum(pieces, stride, 3 * narrow)
        else:
            query_w, key_w, value_w = pieces[:3]
            biases = pieces[3][...]
        for i in range(parts):
            here = slice(i * share, (i + 1) * share)
            some = tokens[i * rows : (i + 1) * rows]
            own = jnp.concatenate([t[:block, :] for t in some], axis=0)
            if i == 0:
                scaled = (dot(own, query_w[...]) + biases[0:1, :]).astype(BF16) * BF16(HEAD_DIM**-0.5)
            key = dot(own, key_w[...]).astype(BF16)
            found = (dot(own, value_w[...]) + biases[1:2, :]).astype(BF16)
            for side in range(2):
                columns = slice(side * half, (side + 1) * half)
                if i == 0:
                    query[side][...] = scaled[:, columns]
                    query_t[side][...] = scaled[:, columns].T
                keys[side][here, :] = key[:, columns]
                values[side][here, :] = found[:, columns]
                value_t[side][:, here] = found[:, columns].T
        for i, t in enumerate(tokens):
            memory[i * memory_block : (i + 1) * memory_block, :] = t[block : block + memory_block, :]
            found = t[block + memory_block :, :].astype(F32).astype(jnp.int32)
            ids[:, i * block : (i + 1) * block] = found[0:1, :block]
        found = [t[block + memory_block :, :].astype(F32).astype(jnp.int32)[1:2, :memory_block] for t in tokens]
        memory_ids[...] = jnp.concatenate(found, axis=1)

    outs = [((share, half), BF16)] * 2 + [((half, share), BF16)] * 2
    outs += [((length, half), BF16)] * 4 + [((half, length), BF16)] * 2
    outs += [
        ((parts * memory_share, width), BF16),
        ((1, length), jnp.int32),
        ((1, parts * memory_share), jnp.int32),
    ]
    return kernel, outs, [((width, width), BF16)] * 3 if packed else []


def make_self_attention(share, length, width):
    def kernel(me_ref, query_t, keys, value_t, ids, mixture_t, logs, hot, penalty):
        hot[...] = one_hot(ids[...])
        penalty[...] = penalties(ids[:, :share])
        attend(query_t, keys, value_t, hot, penalty, mixture_t, logs)

    outs = [((width // 2, share), BF16), ((HEADS // 2, 1, share), F32)]
    return kernel, outs, [((length, PAIR), BF16), ((PAIR, share), BF16)]


def make_cross_forward(packed, rows, block, memory_length, width, narrow, n_pieces):
    share = rows * block
    stride = 5 * narrow + 16

    def kernel(*refs):
        me_ref, refs = refs[0], list(refs[1:])
        pieces, refs = refs[:n_pieces], refs[n_pieces:]
        tokens, refs = refs[:rows], refs[rows:]
        memory, ids, memory_ids, upper, lower = refs[:5]
        first_sum, second_sum, query, memory_keys, memory_values, cross_t, logs, vectors = refs[5:13]
        scratch = refs[13:]
        query_t, value_t, hot, penalty = scratch[:4]
        if packed:
            for i in range(5):
                unpack(me_ref[0], pieces, stride, i * narrow, narrow, scratch[4 + i])
            output_w, query_w, key_w, value_w, source_w = scratch[4:]
            vectors[...] = vector_sum(pieces, stride, 5 * narrow)
        else:
            output_w, query_w, key_w, value_w, source_w = pieces[:5]
            vectors[...] = pieces[5][...]

        def vector(i):
            return vectors[i : i + 1, :]

        own = jnp.concatenate([t[:block, :] for t in tokens], axis=0)
        mixture_t = jnp.concatenate([upper[...], lower[...]], axis=0)
        h = own.astype(F32) + dot_tn(mixture_t, output_w[...]) + vector(OUTPUT_BIAS)
        first_sum[...] = h
        first = normalize(h)[0] * vector(ATTENTION_GAIN) + vector(ATTENTION_SHIFT)
        scaled = (dot(first.astype(BF16), query_w[...]) + vector(SOURCE_QUERY_BIAS)).astype(BF16) * BF16(HEAD_DIM**-0.5)
        query[...] = scaled
        query_t[...] = scaled.T
        memory_keys[...] = dot(memory[...], key_w[...]).astype(BF16)
        memory_values[...] = (dot(memory[...], value_w[...]) + vector(SOURCE_VALUE_BIAS)).astype(BF16)
        value_t[...] = memory_values[...].T
        hot[...] = one_hot(memory_ids[...])
        penalty[...] = penalties(ids[:, :share])
        attend(query_t, memory_keys, value_t, hot, penalty, cross_t, logs)
        first = normalize(first_sum[...])[0] * vector(ATTENTION_GAIN) + vector(ATTENTION_SHIFT)
        second_sum[...] = first + dot_tn(cross_t[...], source_w[...]) + vector(SOURCE_OUTPUT_BIAS)

    outs = [
        ((share, width), F32),
        ((share, width), F32),
        ((share, width), BF16),
        ((memory_length, width), BF16),
        ((memory_length, width), BF16),
        ((width, share), BF16),
        ((HEADS, 1, share), F32),
        ((16, width), F32),
    ]
    scratch = [((width, share), BF16), ((width, memory_length), BF16), ((memory_length, PAIR), BF16), ((PAIR, share), BF16)]
    if packed:
        scratch += [((width, width), BF16)] * 5
    return kernel, outs, scratch


def make_inner(packed, rows, block, width, hidden, narrow, n_pieces):
    blocks = hidden // width
    share = rows * block
    per = width // (blocks * narrow)

    def kernel(*refs):
        me_ref, refs = refs[0], list(refs[1:])
        pieces, refs = refs[:n_pieces], refs[n_pieces:]
        second_sum, cot_own, cot_came, vectors = refs[:4]
        out_own, out_send, back, sums = refs[4:8]
        grads, scratch = refs[8:10], refs[10:]
        low, active, gate, slope = scratch[:4]
        if packed:
            inner_w, outer_w, gathered = scratch[4:7]
            tall = blocks * narrow
            for core, far, slot, device in places(me_ref[0]):
                ref, at = pieces[2 * core + far], slot * 2 * tall
                row = pl.multiple_of(device * narrow, narrow)
                for i in range(blocks):
                    inner_w[i, pl.ds(row, narrow), :] = ref[at + i * narrow : at + (i + 1) * narrow, :]
                row = pl.multiple_of(lax.rem(device, per) * tall, tall)
                outer_w[lax.div(device, per), pl.ds(row, tall), :] = ref[at + tall : at + 2 * tall, :]
        else:
            inner_w, outer_w = pieces

        def vector(i):
            return vectors[i : i + 1, :]

        second = normalize(second_sum[...])[0] * vector(SOURCE_GAIN) + vector(SOURCE_SHIFT)
        low[...] = second.astype(BF16)
        back[...] = second + vector(OUTER_BIAS)

        def forward(i, carry):
            inner = dot(low[...], inner_w[i]) + vectors[pl.ds(INNER_BIAS + i, 1), :]
            chance, density = normal_parts(inner)
            found = (inner * chance).astype(BF16)
            active[i] = found
            gate[i] = chance + inner * density
            back[...] += dot(found, outer_w[i])
            return carry

        lax.fori_loop(0, blocks, forward, 0)
        normed, inverse = normalize(back[...])
        final = normed * vector(FINAL_GAIN) + vector(FINAL_SHIFT)
        out_own[...] = final[:block, :]
        out_send[...] = final[block:, :].astype(BF16)
        upstream = jnp.concatenate([cot_own[...], cot_came[...]], axis=0).astype(F32)
        sums[0:1, :] = total(upstream * normed)
        sums[1:2, :] = total(upstream)
        back3 = normalize_back(upstream, normed, inverse, vector(FINAL_GAIN))
        slope[...] = back3.astype(BF16)
        sums[2:3, :] = total(slope[...])
        sums[7:8, :] = jnp.zeros_like(sums[7:8, :])
        back[...] = back3

        def backward(i, carry):
            grad = dot_nt(slope[...], outer_w[i]) * gate[i]
            inner_low = grad.astype(BF16)
            sums[pl.ds(3 + i, 1), :] = total(inner_low)
            outer_grad = dot_tn(active[i], slope[...])
            inner_grad = dot_tn(low[...], inner_low)
            back[...] += dot_nt(inner_low, inner_w[i])
            if packed:
                gathered[i] = inner_grad
                gathered[blocks + i] = outer_grad
            else:
                grads[0][i] = inner_grad
                grads[1][i] = outer_grad
            return carry

        lax.fori_loop(0, blocks, backward, 0)
        if packed:
            tall = blocks * narrow
            for core, far, slot, device in places(me_ref[0]):
                ref, at = grads[core], far * 8 + slot
                row = pl.multiple_of(device * narrow, narrow)
                for i in range(blocks):
                    ref[at, i * narrow : (i + 1) * narrow, :] = gathered[i, pl.ds(row, narrow), :].astype(BF16)
                row = pl.multiple_of(lax.rem(device, per) * tall, tall)
                ref[at, tall:, :] = gathered[blocks + lax.div(device, per), pl.ds(row, tall), :].astype(BF16)

    outs = [((block, width), F32), ((block, width), BF16), ((share, width), F32), ((8, width), F32)]
    if packed:
        outs += [((16, 2 * blocks * narrow, width), BF16)] * 2
    else:
        outs += [((blocks, width, width), F32)] * 2
    scratch = [((share, width), BF16), ((blocks, share, width), BF16), ((blocks, share, width), F32), ((share, width), BF16)]
    if packed:
        scratch += [((blocks, width, width), BF16)] * 2 + [((2 * blocks, width, width), F32)]
    return kernel, outs, scratch


def make_cross_back(packed, parts, share, memory_share, width, narrow, n_pieces):
    memory_length = parts * memory_share
    stride = 5 * narrow + 16

    def kernel(*refs):
        me_ref, refs = refs[0], list(refs[1:])
        pieces, refs = refs[:n_pieces], refs[n_pieces:]
        (back2_in, first_sum, second_sum, query, memory_keys, memory_values, cross_t, logs, ids,
         memory_ids, vectors, sums_inner) = refs[:12]
        mixtures, refs = refs[12:14], refs[14:]
        back1, key_own, value_own, sums = refs[:4]
        self_slope, self_slope_t, self_deltas = (refs[4 + 2 * i : 6 + 2 * i] for i in range(3))
        sends, refs = refs[10 : 10 + parts - 1], refs[10 + parts - 1 :]
        grads, scratch = refs[:3], refs[3:]
        (slope_t, slope, key_t, hot, penalty, query_t, deltas, query_grad_t, key_grad, value_grad) = scratch[:10]
        upper, lower = mixtures
        if packed:
            for i, at in enumerate((0, 1, 4)):
                unpack(me_ref[0], pieces, stride, at * narrow, narrow, scratch[10 + i])
            output_w, query_w, source_w = scratch[10:13]
        else:
            output_w, query_w, source_w = pieces

        def vector(i):
            return vectors[i : i + 1, :]

        sums[0:7, :] = sums_inner[0:7, :]
        upstream = back2_in[...]
        normed, inverse = normalize(second_sum[...])
        sums[7:8, :] = total(upstream * normed)
        sums[8:9, :] = total(upstream)
        back2 = normalize_back(upstream, normed, inverse, vector(SOURCE_GAIN))
        back1[...] = back2
        cross_low = back2.astype(BF16)
        sums[9:10, :] = total(cross_low)
        grads[0][...] = dot(cross_t[...], cross_low).astype(BF16)
        found = dot_nt(cross_low, source_w[...]).astype(BF16)
        slope[...] = found
        slope_t[...] = found.T
        deltas_of(slope_t, cross_t, deltas)
        query_t[...] = query[...].T
        key_t[...] = memory_keys[...].T
        hot[...] = one_hot(memory_ids[...])
        penalty[...] = penalties(ids[:, :share])
        attend_back(query_t, query, memory_keys, key_t, memory_values, slope_t, slope, hot, penalty,
                    logs, deltas, query_grad_t, key_grad, value_grad)
        key_own[...] = key_grad[:memory_share, :]
        value_own[...] = value_grad[:memory_share, :]
        for i in range(1, parts):
            here = slice(i * memory_share, (i + 1) * memory_share)
            sends[i - 1][:memory_share, :] = key_grad[here, :].astype(BF16)
            sends[i - 1][memory_share:, :] = value_grad[here, :].astype(BF16)
        query_low = query_grad_t[...].T.astype(BF16)
        sums[10:11, :] = total(query_low)
        normed, inverse = normalize(first_sum[...])
        first_low = (normed * vector(ATTENTION_GAIN) + vector(ATTENTION_SHIFT)).astype(BF16)
        grads[1][...] = dot_tn(first_low, query_low).astype(BF16)
        upstream = back1[...] + dot_nt(query_low, query_w[...])
        sums[11:12, :] = total(upstream * normed)
        sums[12:13, :] = total(upstream)
        grad = normalize_back(upstream, normed, inverse, vector(ATTENTION_GAIN))
        back1[...] = grad
        branch_low = grad.astype(BF16)
        sums[13:14, :] = total(branch_low)
        sums[14:16, :] = jnp.zeros_like(sums[14:16, :])
        mixture_t = jnp.concatenate([upper[...], lower[...]], axis=0)
        grads[2][...] = dot(mixture_t, branch_low).astype(BF16)
        found = dot_nt(branch_low, output_w[...]).astype(BF16)
        for side in range(2):
            columns = slice(side * width // 2, (side + 1) * width // 2)
            self_slope[side][...] = found[:, columns]
            self_slope_t[side][...] = found[:, columns].T
            deltas_of(self_slope_t[side], mixtures[side], self_deltas[side])

    half = width // 2
    outs = [
        ((share, width), F32),
        ((memory_share, width), F32),
        ((memory_share, width), F32),
        ((16, width), F32),
    ]
    outs += [((share, half), BF16)] * 2 + [((half, share), BF16)] * 2
    outs += [((HEADS // 2, 1, share), F32)] * 2
    outs += [((2 * memory_share, width), BF16)] * (parts - 1)
    outs += [((width, width), BF16)] * 3
    scratch = [
        ((width, share), BF16),
        ((share, width), BF16),
        ((width, memory_length), BF16),
        ((memory_length, PAIR), BF16),
        ((PAIR, share), BF16),
        ((width, share), BF16),
        ((HEADS, 1, share), F32),
        ((width, share), F32),
        ((memory_length, width), F32),
        ((memory_length, width), F32),
    ]
    if packed:
        scratch += [((width, width), BF16)] * 3
    return kernel, outs, scratch


def attention_back_half(refs, share, scratch):
    query, keys, values, slope, slope_t, logs, deltas, ids = refs
    query_t, key_t, hot, penalty, query_grad_t, key_grad, value_grad = scratch
    query_t[...] = query[...].T
    key_t[...] = keys[...].T
    hot[...] = one_hot(ids[...])
    penalty[...] = penalties(ids[:, :share])
    attend_back(query_t, query, keys, key_t, values, slope_t, slope, hot, penalty, logs, deltas,
                query_grad_t, key_grad, value_grad)


def half_scratch(share, length, half):
    return [
        ((half, share), BF16),
        ((half, length), BF16),
        ((length, PAIR), BF16),
        ((PAIR, share), BF16),
        ((half, share), F32),
        ((length, half), F32),
        ((length, half), F32),
    ]


def give_half(share, scratch, own, sends):
    key_grad, value_grad = scratch[5:7]
    own[:share, :] = key_grad[:share, :]
    own[share:, :] = value_grad[:share, :]
    for i, send in enumerate(sends):
        here = slice((i + 1) * share, (i + 2) * share)
        send[:share, :] = key_grad[here, :].astype(BF16)
        send[share:, :] = value_grad[here, :].astype(BF16)


def make_self_back_upper(packed, parts, rows, block, memory_block, width, narrow, n_pieces):
    share, memory_share = rows * block, rows * memory_block
    length, half = parts * share, width // 2

    def kernel(*refs):
        me_ref, refs = refs[0], list(refs[1:])
        pieces, refs = refs[:n_pieces], refs[n_pieces:]
        tokens, refs = refs[:rows], refs[rows:]
        operands, refs = refs[:8], refs[8:]
        memory_key_own, memory_value_own, sums_in = refs[:3]
        early, refs = refs[3:6], refs[6:]
        memory_received, refs = refs[: parts - 1], refs[parts - 1 :]
        query_grad, own, memory_own, memory_send = refs[:4]
        sends, refs = refs[4 : 4 + parts - 1], refs[4 + parts - 1 :]
        n_grads = 2 if packed else 3
        grad_refs, scratch = refs[:n_grads], refs[n_grads:]
        sums = scratch[7]
        me = me_ref[0]
        if packed:
            for i in range(2):
                unpack(me, pieces, 5 * narrow + 16, (2 + i) * narrow, narrow, scratch[8 + i])
            source_key, source_value = scratch[8:10]
        else:
            source_key, source_value = pieces
        grads = Grads(me, grad_refs, scratch[10] if packed else None, narrow)
        memory = jnp.concatenate([t[block : block + memory_block, :] for t in tokens], axis=0)
        key_sum, value_sum = memory_key_own[...], memory_value_own[...]
        for ref in memory_received:
            key_sum = key_sum + ref[:memory_share, :].astype(F32)
            value_sum = value_sum + ref[memory_share:, :].astype(F32)
        key_low, value_low = key_sum.astype(BF16), value_sum.astype(BF16)
        sums[...] = sums_in[...]
        sums[14:15, :] = total(value_low)
        grads.put_sums(5 * narrow, sums[...])
        grads.put(0, dot_tn(memory, key_low))
        grads.put(1, dot_tn(memory, value_low))
        if packed:
            for i, ref in enumerate(early):
                grads.put(2 + i, ref[...].astype(F32))
        grad = dot_nt(key_low, source_key[...]) + dot_nt(value_low, source_value[...])
        memory_own[...] = grad[:memory_block, :]
        memory_send[...] = grad[memory_block:, :].astype(BF16)
        attention_back_half(operands, share, scratch[:7])
        query_grad[...] = scratch[4][...].T.astype(BF16)
        give_half(share, scratch, own, sends)

    outs = [
        ((share, half), BF16),
        ((2 * share, half), F32),
        ((memory_block, width), F32),
        ((memory_block, width), BF16),
    ]
    outs += [((2 * share, half), BF16)] * (parts - 1)
    if packed:
        outs += [((16, 5 * narrow + 16, width), BF16)] * 2
    else:
        outs += [((width, width), F32)] * 2 + [((16, width), F32)]
    scratch = half_scratch(share, length, half) + [((16, width), F32)]
    if packed:
        scratch += [((width, width), BF16)] * 2 + [((width, width), F32)]
    return kernel, outs, scratch


def make_self_back_lower(packed, parts, rows, block, width, narrow, n_pieces):
    share = rows * block
    length, half = parts * share, width // 2

    def kernel(*refs):
        me_ref, refs = refs[0], list(refs[1:])
        pieces, refs = refs[:n_pieces], refs[n_pieces:]
        tokens, refs = refs[:rows], refs[rows:]
        operands, refs = refs[:8], refs[8:]
        back1, query_upper = refs[:2]
        in_part, query_sum, query_w_grad, own = refs[2:6]
        sends, scratch = refs[6 : 6 + parts - 1], refs[6 + parts - 1 :]
        if packed:
            unpack(me_ref[0], pieces, 3 * narrow + 8, 0, narrow, scratch[7])
            query_w = scratch[7]
        else:
            (query_w,) = pieces
        attention_back_half(operands, share, scratch[:7])
        give_half(share, scratch, own, sends)
        query_low = jnp.concatenate([query_upper[...], scratch[4][...].T.astype(BF16)], axis=1)
        tokens_own = jnp.concatenate([t[:block, :] for t in tokens], axis=0)
        in_part[...] = back1[...] + dot_nt(query_low, query_w[...])
        query_sum[...] = jnp.concatenate([total(query_low), jnp.zeros((7, width), F32)], axis=0)
        query_w_grad[...] = dot_tn(tokens_own, query_low).astype(query_w_grad.dtype)

    outs = [
        ((share, width), F32),
        ((8, width), F32),
        ((width, width), BF16 if packed else F32),
        ((2 * share, half), F32),
    ]
    outs += [((2 * share, half), BF16)] * (parts - 1)
    scratch = half_scratch(share, length, half)
    if packed:
        scratch += [((width, width), BF16)]
    return kernel, outs, scratch


def make_last(packed, parts, rows, block, memory_block, width, narrow, n_pieces):
    share = rows * block

    def kernel(*refs):
        me_ref, refs = refs[0], list(refs[1:])
        pieces, refs = refs[:n_pieces], refs[n_pieces:]
        tokens, refs = refs[:rows], refs[rows:]
        in_part, query_sum, query_w_grad, memory_send = refs[:4]
        owns, refs = refs[4:6], refs[6:]
        received = [refs[: parts - 1], refs[parts - 1 : 2 * (parts - 1)]]
        refs = refs[2 * (parts - 1) :]
        in_own, in_send = refs[:2]
        n_grads = 2 if packed else 3
        grad_refs, scratch = refs[2 : 2 + n_grads], refs[2 + n_grads :]
        sums = scratch[0]
        me = me_ref[0]
        if packed:
            for i in range(2):
                unpack(me, pieces, 3 * narrow + 8, (1 + i) * narrow, narrow, scratch[1 + i])
            key_w, value_w = scratch[1:3]
        else:
            key_w, value_w = pieces
        grads = Grads(me, grad_refs, scratch[3] if packed else None, narrow)
        if packed:
            grads.put(2, query_w_grad[...].astype(F32))
        lows = []
        for own, others in zip(owns, received):
            found = own[...]
            for ref in others:
                found = found + ref[...].astype(F32)
            lows.append(found.astype(BF16))
        key_low = jnp.concatenate([low[:share, :] for low in lows], axis=1)
        value_low = jnp.concatenate([low[share:, :] for low in lows], axis=1)
        tokens_own = jnp.concatenate([t[:block, :] for t in tokens], axis=0)
        sums[...] = query_sum[...]
        sums[1:2, :] = total(value_low)
        grads.put_sums(3 * narrow, sums[...])
        grads.put(0, dot_tn(tokens_own, key_low))
        grads.put(1, dot_tn(tokens_own, value_low))
        grad = in_part[...] + dot_nt(key_low, key_w[...]) + dot_nt(value_low, value_w[...])
        in_own[...] = grad[:block, :]
        in_send[:block, :] = grad[block:, :].astype(BF16)
        in_send[block:, :] = memory_send[...]

    outs = [((block, width), F32), ((block + memory_block, width), BF16)]
    if packed:
        outs += [((16, 3 * narrow + 8, width), BF16)] * 2
    else:
        outs += [((width, width), F32)] * 2 + [((8, width), F32)]
    scratch = [((8, width), F32)]
    if packed:
        scratch += [((width, width), BF16)] * 2 + [((width, width), F32)]
    return kernel, outs, scratch


def combine(arrays, splits):
    count = arrays[0].shape[0] // splits
    shape = (count,) + arrays[0].shape[1:]

    def kernel(*refs):
        given, outs = refs[: len(arrays)], refs[len(arrays) :]
        for i, out in enumerate(outs):
            here = slice(i * count, (i + 1) * count)
            found = given[0][here].astype(F32)
            for ref in given[1:]:
                found = found + ref[here].astype(F32)
            out[...] = found.astype(out.dtype)

    return pl.pallas_call(
        kernel,
        out_shape=[jax.ShapeDtypeStruct(shape, BF16)] * splits,
        in_specs=[VM] * len(arrays),
        out_specs=[VM] * splits,
        compiler_params=pltpu.CompilerParams(vmem_limit_bytes=32 << 20),
        cost_estimate=pl.CostEstimate(flops=1 << 20, bytes_accessed=0, transcendentals=0),
        name="combine",
    )(*arrays)


def chosen(me, rows, wide):
    width = rows.shape[1]
    line = lax.broadcasted_iota(jnp.int32, (width, wide), 0)
    here = lax.broadcasted_iota(jnp.int32, (width, wide), 1) + me * wide
    choice = jnp.where(line == here, 1.0, 0.0)
    return lax.dot_general(rows, choice, (((1,), (0,)), ((), ())), precision=lax.Precision.HIGHEST, preferred_element_type=F32)


def reduce_all(array, devices):
    mask = 1
    while mask < devices:
        array = array + swap(array, mask, devices)
        mask *= 2
    return array


def per_device(
    tokens, memory, target_ids, source_ids, cotangent,
    query_weight, key_weight, value_weight, output_weight, query_bias, value_bias, output_bias,
    attention_gain, attention_shift,
    source_query, source_key, source_value, source_output, source_query_bias, source_value_bias,
    source_output_bias, source_gain, source_shift,
    inner_weight, inner_bias, outer_weight, outer_bias, final_gain, final_shift,
    *, devices, sequence,
):
    packed = devices == 32
    rows, block, width = tokens.shape
    memory_block = memory.shape[1]
    parts = sequence // rows
    share, memory_share = rows * block, rows * memory_block
    hidden = inner_weight.shape[1]
    blocks = hidden // width
    me = lax.axis_index(AXES)
    me_array = me.reshape(1).astype(jnp.int32)
    turn = lax.rem(lax.div(me, parts), rows)
    narrow, wide = width // devices, hidden // devices

    def run(made, micros, name, *args):
        kernel, outs, *scratch = made
        return call(kernel, outs, (me_array,) + args, scratch[0] if scratch else [], micros, name)

    turn_array = turn.reshape(1).astype(jnp.int32)

    def turned(made, name, *args):
        kernel, outs = made
        return call(kernel, outs, (turn_array,) + args, [], 1.0, name)

    short = jnp.stack([query_bias, value_bias, output_bias, attention_gain, attention_shift,
                       source_query_bias, source_value_bias, source_output_bias, source_gain,
                       source_shift, outer_bias, final_gain, final_shift])

    def whole(array):
        return lax.all_gather(array, AXES, axis=0, tiled=True)

    sent, kept = turned(
        make_tokens_packet(block, memory_block, width), "tokens_packet",
        tokens, memory, target_ids, source_ids,
    )
    came = swap(sent, parts, devices)
    row_tokens = [kept, came]
    kept_swaps = [swap(kept, m, devices) for m in range(1, parts)]
    came_swaps = [swap(came, m, devices) for m in range(1, parts)]
    for pair in zip(kept_swaps, came_swaps):
        row_tokens += pair
    own_tokens = row_tokens[:rows]

    if packed:
        (first,) = run(make_self_packet(narrow, width), 1.0, "self_packet",
                       query_weight, key_weight, value_weight, short)
        first = after(first, sent)
        first_z = [swap(first, m, 32) for m in Z_MASKS[1:]]
        (second,) = run(make_cross_packet(narrow, width, blocks), 1.0, "cross_packet", output_weight,
                        source_query, source_key, source_value, source_output, short,
                        inner_bias.reshape(1, wide))
        (third,) = run(make_inner_packet(narrow, width, blocks), 1.0, "inner_packet", inner_weight, outer_weight)
        first_a = join(after([first, *first_z], second, third))
        first_b = turned_swap(first_a, 1)
        second = after(second, first_a)
        second_z = [swap(second, m, 32) for m in Z_MASKS[1:]]
        first_c = join(after([first_a, first_b], came, *kept_swaps))
        first_d = turned_swap(first_c, 2)
        second_a = join([second, *second_z])
        first_d = after(first_d, second_a, *came_swaps)
        third = after(third, second_a)
        third_z = [swap(third, m, 32) for m in Z_MASKS[1:]]
        set_self = [first_c, first_d, swap(first_c, 1, 32), swap(first_d, 1, 32)]
        second_b = turned_swap(second_a, 1)
    else:
        full = [whole(w) for w in (query_weight, key_weight, value_weight, output_weight, source_query, source_key, source_value, source_output)]
        lane = lax.broadcasted_iota(jnp.int32, (1, width), 1)
        place = lax.broadcasted_iota(jnp.int32, (blocks, width), 0) * width + lane
        spread_wide = jnp.where(place // wide == me, jnp.tile(inner_bias.reshape(1, wide), (blocks, width // wide)), 0)

        def natural(rows):
            return jnp.where(lane // narrow == me, jnp.tile(rows, (1, devices)), 0)

        vectors = jnp.concatenate([natural(short[:2]), jnp.zeros((6, width), BF16), natural(short[2:]), spread_wide, jnp.zeros((1, width), BF16)])
        vectors = reduce_all(vectors, devices).astype(F32)
        set_self = full[:3] + [vectors[:8]]
        set_cross = full[3:] + [vectors[8:]]
        set_inner = [
            whole(inner_weight).reshape(width, blocks, width).transpose(1, 0, 2),
            whole(outer_weight).reshape(blocks, width, width),
        ]
    found = run(
        make_project(packed, parts, rows, block, memory_block, width, narrow, len(set_self)), 5.0,
        "project", *set_self, *row_tokens,
    )
    query, query_t, keys, values, value_t = (found[2 * i : 2 * i + 2] for i in range(5))
    row_memory, ids, memory_ids = found[10:]
    attention = make_self_attention(share, parts * share, width)
    if packed:
        second_c = join(after([second_a, second_b], query_t[1]))
        second_d = turned_swap(second_c, 2)
        third_a = join(after([third, *third_z], query_t[1]))
        third_b = turned_swap(third_a, 1)
        second_e = swap(second_c, 1, 32)
        query_t = [after(query_t[0], second_c, third_a), query_t[1]]
    upper = run(attention, 5.5, "self_upper", query_t[0], keys[0], value_t[0], ids)
    if packed:
        second_d = after(second_d, upper[0])
        set_cross = [second_c, second_d, second_e, swap(second_d, 1, 32)]
        third_c = join(after([third_a, third_b], upper[0]))
        third_d = turned_swap(third_c, 2)
        set_inner = [third_c, third_d, swap(third_c, 1, 32), swap(third_d, 1, 32)]
        query_t = [query_t[0], after(query_t[1], third_c, second_d)]
        set_back, set_query, set_last, set_memory = set_cross, set_self, set_self, set_cross
        cotangent = after(cotangent, third_c)
    else:
        set_back, set_query, set_last, set_memory = [full[3], full[4], full[7]], full[:1], full[1:3], full[5:7]
    cot_sent, cot_own = turned(make_cot_packet(block, width), "cot_packet", cotangent)
    cot_came = swap(cot_sent, parts, devices)
    lower = run(attention, 5.5, "self_lower", query_t[1], keys[1], value_t[1], ids)
    mixtures, logs = (upper[0], lower[0]), (upper[1], lower[1])
    first_sum, second_sum, cross_query, memory_keys, memory_values, cross_t, cross_logs, vectors = run(
        make_cross_forward(packed, rows, block, parts * memory_share, width, narrow, len(set_cross)),
        9.0, "cross_forward", *set_cross, *own_tokens, row_memory, ids, memory_ids, *mixtures,
    )
    out_own, out_send, back2_in, sums_inner, *grads_inner = run(
        make_inner(packed, rows, block, width, hidden, narrow, len(set_inner)), 18.0, "inner",
        *set_inner, second_sum, cot_own, cot_came, vectors,
    )
    out_came = swap(out_send, parts, devices)
    found = run(
        make_cross_back(packed, parts, share, memory_share, width, narrow, len(set_back)), 14.0,
        "cross_back", *set_back, back2_in, first_sum, second_sum, cross_query, memory_keys,
        memory_values, cross_t, cross_logs, ids, memory_ids, vectors, sums_inner, *mixtures,
    )
    back1, memory_key_own, memory_value_own, sums_cross = found[:4]
    slope, slope_t, deltas = (found[4 + 2 * i : 6 + 2 * i] for i in range(3))
    memory_received = [swap(a, m + 1, devices) for m, a in enumerate(found[10 : 10 + parts - 1])]
    grads_early = found[10 + parts - 1 :]
    query = list(query)
    if packed:
        keep, send = combine([grads_inner[0], swap(grads_inner[1], 1, 32)], 2)
        query[0] = after(query[0], keep, out_came)
        inner_step = [keep, turned_swap(send, 2)]
    found = run(
        make_self_back_upper(packed, parts, rows, block, memory_block, width, narrow, len(set_memory)),
        12.0, "self_back_upper", *set_memory, *own_tokens, query[0], keys[0], values[0], slope[0],
        slope_t[0], logs[0], deltas[0], ids, memory_key_own, memory_value_own, sums_cross,
        *grads_early, *memory_received,
    )
    query_upper, own_upper, memory_own, memory_send = found[:4]
    received_upper = [swap(a, m + 1, devices) for m, a in enumerate(found[4 : 4 + parts - 1])]
    grads_cross = found[4 + parts - 1 :]
    if packed:
        keep, send = combine(inner_step, 2)
        inner_step = [keep, turned_swap(send, 1)]
        query[1] = after(query[1], keep)
    in_part, query_sum, query_w_grad, own_lower, *sends = run(
        make_self_back_lower(packed, parts, rows, block, width, narrow, len(set_query)), 11.0,
        "self_back_lower", *set_query, *own_tokens, query[1], keys[1], values[1], slope[1],
        slope_t[1], logs[1], deltas[1], ids, back1, query_upper,
    )
    received_lower = [swap(a, m + 1, devices) for m, a in enumerate(sends)]
    if packed:
        def lowest(arrays):
            found = combine(arrays, 4)
            return [found[0]] + [swap(a, m, 32) for a, m in zip(found[1:], Z_MASKS[1:])]

        keep_cross, send = combine([grads_cross[0], swap(grads_cross[1], 1, 32)], 2)
        cross_step = [keep_cross, turned_swap(send, 2)]
        inner_step = lowest(inner_step)
        in_part = after(in_part, keep_cross, inner_step[0])
    in_own, in_send, *grads_last = run(
        make_last(packed, parts, rows, block, memory_block, width, narrow, len(set_last)), 6.0,
        "last", *set_last, *own_tokens, in_part, query_sum, query_w_grad, memory_send, own_upper,
        own_lower, *received_upper, *received_lower,
    )

    def regroup(mine, came):
        came = came.astype(F32)
        return jnp.where(turn == 0, jnp.stack([mine, came]), jnp.stack([came, mine]))

    output = regroup(out_own, out_came)
    in_came = swap(in_send, parts, devices)
    input_gradient = regroup(in_own, in_came[:block])
    memory_gradient = regroup(memory_own, in_came[block:])

    if packed:
        keep, send = combine(cross_step, 2)
        cross_step = lowest([keep, turned_swap(send, 1)])
        keep, send = combine([grads_last[0], swap(grads_last[1], 1, 32)], 2)
        keep, send = combine(after([keep, turned_swap(send, 2)], *inner_step), 2)
        last_step = lowest([keep, turned_swap(send, 1)])

        def plan(me_ref, *refs):
            me = me_ref[0]
            steps, outs = [refs[:4], refs[4:8], refs[8:12]], refs[12:]
            inner, cross, last = (sum(r[0].astype(F32) for r in given) for given in steps)
            for i in range(blocks):
                outs[0][:, i * width : (i + 1) * width] = inner[i * narrow : (i + 1) * narrow, :]
            outs[1][...] = inner[blocks * narrow :, :]
            for i in range(5):
                outs[2 + i][...] = cross[i * narrow : (i + 1) * narrow, :]
            for i in range(3):
                outs[7 + i][...] = last[i * narrow : (i + 1) * narrow, :]
            rows_in = jnp.concatenate([cross[5 * narrow :, :], last[3 * narrow :, :]], axis=0)
            outs[10][...] = chosen(me, rows_in, narrow)
            per = width // wide
            line = lax.broadcasted_iota(jnp.int32, (blocks, width), 0)
            row = jnp.sum(jnp.where(line == lax.div(me, per), rows_in[3 : 3 + blocks, :], 0.0), axis=0, keepdims=True)
            outs[11][...] = chosen(lax.rem(me, per), row, wide)

        part = (narrow, width)
        shapes = [(narrow, hidden), (wide, width)] + [part] * 8 + [(24, narrow), (1, wide)]
        (inner_share, outer_share, source_key_share, source_value_share, source_output_share,
         source_query_share, output_share, key_share, value_share, query_share, sums,
         inner_bias_share) = call(
            plan, [(s, F32) for s in shapes], (me_array, *inner_step, *cross_step, *last_step), [], 2.0,
            "finish",
        )
        inner_bias_share = inner_bias_share.reshape(wide)
    else:
        def scatter(array):
            return lax.psum_scatter(array, AXES, scatter_dimension=0, tiled=True)

        inner_share = scatter(grads_inner[0].transpose(1, 0, 2).reshape(width, hidden))
        outer_share = scatter(grads_inner[1].reshape(hidden, width))
        source_output_share, source_query_share, output_share = (scatter(g.astype(F32)) for g in grads_early)
        source_key_share, source_value_share = (scatter(g) for g in grads_cross[:2])
        key_share, value_share = (scatter(g) for g in grads_last[:2])
        query_share = scatter(query_w_grad)
        sums = reduce_all(jnp.concatenate([grads_cross[2], grads_last[2]], axis=0), devices)
        inner_bias_share = lax.dynamic_slice(sums[3 : 3 + blocks].reshape(hidden), (me * wide,), (wide,))
        sums = lax.dynamic_slice(sums, (0, me * narrow), (sums.shape[0], narrow))
    return (
        output,
        input_gradient,
        memory_gradient,
        query_share,
        key_share,
        value_share,
        output_share,
        sums[16],
        sums[17],
        sums[13],
        sums[11],
        sums[12],
        source_query_share,
        source_key_share,
        source_value_share,
        source_output_share,
        sums[10],
        sums[14],
        sums[9],
        sums[7],
        sums[8],
        inner_share,
        inner_bias_share,
        outer_share,
        sums[2],
        sums[0],
        sums[1],
    )


def solution(mesh):
    sequence, devices = mesh.shape["seq"], mesh.size
    tokens, ids = P("dp", "seq", None), P("dp", "seq")
    matrix, vector = P(AXES, None), P(AXES)
    attention = (matrix,) * 4 + (vector,) * 5
    inner = (matrix, vector, matrix, vector, vector, vector)
    return jax.shard_map(
        functools.partial(per_device, devices=devices, sequence=sequence),
        mesh=mesh,
        in_specs=(tokens, tokens, ids, ids, tokens) + attention + attention + inner,
        out_specs=(tokens, tokens, tokens) + attention + attention + inner,
        check_vma=False,
    )
```

```python
import functools
import math

import jax
import jax.numpy as jnp
from jax import lax
from jax.experimental import pallas as pl
from jax.experimental.pallas import tpu as pltpu
from jax.sharding import PartitionSpec as P

HEADS = 8
HEAD_DIM = 64
PAIR = 128
EPSILON = 1e-05
MASKED = 1e9
AXES = ("dp", "seq")
F32 = jnp.float32
BF16 = jnp.bfloat16

(
    OUTPUT_BIAS,
    ATTENTION_GAIN,
    ATTENTION_SHIFT,
    SOURCE_QUERY_BIAS,
    SOURCE_VALUE_BIAS,
    SOURCE_OUTPUT_BIAS,
    SOURCE_GAIN,
    SOURCE_SHIFT,
    OUTER_BIAS,
    FINAL_GAIN,
    FINAL_SHIFT,
    INNER_BIAS,
) = range(12)
Z_MASKS = (0, 8, 16, 24)
VM = pl.BlockSpec(memory_space=pltpu.VMEM)
SM = pl.BlockSpec(memory_space=pltpu.SMEM)


def dot(a, b):
    return lax.dot_general(a, b, (((1,), (0,)), ((), ())), preferred_element_type=F32)


def dot_nt(a, b):
    return lax.dot_general(a, b, (((1,), (1,)), ((), ())), preferred_element_type=F32)


def dot_tn(a, b):
    return lax.dot_general(a, b, (((0,), (0,)), ((), ())), preferred_element_type=F32)


def total(values):
    return jnp.sum(values.astype(F32), axis=0, keepdims=True)


def normalize(h):
    average = jnp.mean(h, axis=-1, keepdims=True)
    centered = h - average
    variance = jnp.mean(centered * centered, axis=-1, keepdims=True)
    inverse = lax.rsqrt(variance + EPSILON)
    return centered * inverse, inverse


def normalize_back(upstream, normed, inverse, gain):
    scaled = upstream * gain
    first_mean = jnp.mean(scaled, axis=-1, keepdims=True)
    second_mean = jnp.mean(scaled * normed, axis=-1, keepdims=True)
    return inverse * (scaled - first_mean - normed * second_mean)


def normal_parts(v):
    density = 0.3989422804014327 * jnp.exp(-0.5 * v * v)
    t = 1.0 / (1.0 + 0.2316419 * jnp.abs(v))
    series = t * (
        0.319381530
        + t * (-0.356563782 + t * (1.781477937 + t * (-1.821255978 + t * 1.330274429)))
    )
    tail = density * series
    return jnp.where(v >= 0.0, 1.0 - tail, tail), density


def penalties(ids):
    place = lax.broadcasted_iota(jnp.int32, (PAIR, ids.shape[1]), 0)
    return jnp.where((place == ids) | (place >= 4), 0.0, -MASKED).astype(BF16)


def one_hot(ids):
    place = lax.broadcasted_iota(jnp.int32, (PAIR, ids.shape[1]), 0)
    return jnp.where(place == ids, 1.0, 0.0).astype(F32).T.astype(BF16)


def spread(part, half):
    empty = jnp.zeros_like(part)
    return [part, empty] if half == 0 else [empty, part]


def attend(query_t, keys, value_t, hot, penalty, mixture_t, logs):
    length = keys.shape[0]

    def pair(p, carry):
        columns = pl.ds(pl.multiple_of(p * PAIR, PAIR), PAIR)
        left = jnp.concatenate([keys[:, columns], hot[...]], axis=1)
        for half in range(2):
            rows = pl.ds(pl.multiple_of(p * PAIR + half * HEAD_DIM, HEAD_DIM), HEAD_DIM)
            right = jnp.concatenate(spread(query_t[rows, :], half) + [penalty[...]], axis=0)
            scores = dot(left, right)
            highest = jnp.max(scores, axis=0, keepdims=True)
            weights = jnp.exp(scores - highest).astype(BF16)
            values = jnp.concatenate(
                [value_t[rows, :], jnp.ones((16, length), BF16)], axis=0
            )
            found = dot(values, weights)
            denominator = found[HEAD_DIM : HEAD_DIM + 1, :]
            mixture_t[rows, :] = (found[:HEAD_DIM, :] / denominator).astype(BF16)
            logs[2 * p + half] = highest + jnp.log(denominator)
        return carry

    lax.fori_loop(0, keys.shape[1] // PAIR, pair, 0)


def attend_back(
    query_t, query, keys, key_t, values, slope_t, slope, hot, penalty, logs, deltas,
    query_grad_t, key_grad, value_grad,
):
    tokens = query.shape[0]
    lane = lax.broadcasted_iota(jnp.int32, (tokens, PAIR), 1)

    def pair(p, carry):
        columns = pl.ds(pl.multiple_of(p * PAIR, PAIR), PAIR)
        left = jnp.concatenate([keys[:, columns], hot[...]], axis=1)
        value_pair = values[:, columns]
        key_sum, value_sum = None, None
        for half in range(2):
            rows = pl.ds(pl.multiple_of(p * PAIR + half * HEAD_DIM, HEAD_DIM), HEAD_DIM)
            right = jnp.concatenate(spread(query_t[rows, :], half) + [penalty[...]], axis=0)
            chances = jnp.exp(dot(left, right) - logs[2 * p + half])
            slopes = dot(value_pair, jnp.concatenate(spread(slope_t[rows, :], half), axis=0))
            grads = (chances * (slopes - deltas[2 * p + half])).astype(BF16)
            query_grad_t[rows, :] = dot(key_t[rows, :], grads) * HEAD_DIM**-0.5
            mine = (lane < HEAD_DIM) if half == 0 else (lane >= HEAD_DIM)
            none = jnp.zeros((tokens, PAIR), BF16)
            value_part = dot(chances.astype(BF16), jnp.where(mine, slope[:, columns], none))
            key_part = dot(grads, jnp.where(mine, query[:, columns], none))
            value_sum = value_part if value_sum is None else value_sum + value_part
            key_sum = key_part if key_sum is None else key_sum + key_part
        key_grad[:, columns] = key_sum
        value_grad[:, columns] = value_sum
        return carry

    lax.fori_loop(0, keys.shape[1] // PAIR, pair, 0)


def deltas_of(slope_t, mixture_t, deltas):
    for head in range(slope_t.shape[0] // HEAD_DIM):
        rows = slice(head * HEAD_DIM, (head + 1) * HEAD_DIM)
        deltas[head] = jnp.sum(
            slope_t[rows, :].astype(F32) * mixture_t[rows, :].astype(F32), axis=0, keepdims=True
        )


def swap(array, mask, devices):
    return lax.ppermute(array, AXES, [(i, i ^ mask) for i in range(devices)])


def turned_swap(array, step):
    pairs = []
    for i in range(32):
        near = 2 if i % 2 == 0 else 4
        pairs.append((i, i ^ (near if step == 1 else 6 - near)))
    return lax.ppermute(array, AXES, pairs)


def after(value, *others):
    return lax.optimization_barrier((value, others))[0]


def places(me):
    found = []
    for core in range(2):
        near = jnp.where(((me & 1) ^ core) == 0, 2, 4)
        for far in range(2):
            for step in range(2):
                for at, mask in enumerate(Z_MASKS):
                    device = me ^ (core | mask)
                    if step:
                        device = device ^ near
                    if far:
                        device = device ^ (6 - near)
                    found.append((core, far, step * 4 + at, device))
    return found


def unpack(me, pieces, stride, first, rows, scratch):
    for core, far, slot, device in places(me):
        ref = pieces[2 * core + far]
        at = slot * stride + first
        scratch[pl.ds(pl.multiple_of(device * rows, rows), rows), :] = ref[at : at + rows, :]


def vector_sum(pieces, stride, first):
    found = None
    for ref in pieces:
        for slot in range(8):
            part = ref[slot * stride + first : (slot + 1) * stride, :].astype(F32)
            found = part if found is None else found + part
    return found


class Grads:
    def __init__(self, me, refs, dense, rows):
        self.me, self.refs, self.dense, self.rows = me, refs, dense, rows

    def put(self, index, grad):
        if self.dense is None:
            self.refs[index][...] = grad
            return
        self.dense[...] = grad
        rows = self.rows
        for core, far, slot, device in places(self.me):
            found = self.dense[pl.ds(pl.multiple_of(device * rows, rows), rows), :]
            self.refs[core][far * 8 + slot, index * rows : (index + 1) * rows, :] = found.astype(BF16)

    def put_sums(self, first, sums):
        if self.dense is None:
            self.refs[-1][...] = sums
            return
        low = sums.astype(BF16)
        for ref in self.refs:
            for slot in range(16):
                ref[slot, first : first + sums.shape[0], :] = low


def grad_outs(packed, count, rows, width, sums):
    if packed:
        return [((16, count * rows + sums, width), BF16)] * 2
    return [((width, width), F32)] * count + [((sums, width), F32)]


def padded(shape, dtype):
    last = -(-shape[-1] // 128) * 128
    tall = -(-shape[-2] // 16) * 16 if len(shape) > 1 else 16
    return math.prod(shape[:-2]) * tall * last * jnp.dtype(dtype).itemsize


def call(kernel, outs, args, scratch, micros, name, room=14):
    moved = sum(math.prod(a.shape) * a.dtype.itemsize for a in args[1:])
    moved += sum(math.prod(s) * jnp.dtype(d).itemsize for s, d in outs)
    need = sum(padded(a.shape, a.dtype) for a in args[1:])
    need += sum(padded(s, d) for s, d in list(outs) + list(scratch))
    return pl.pallas_call(
        kernel,
        out_shape=[jax.ShapeDtypeStruct(s, d) for s, d in outs],
        in_specs=[SM] + [VM] * (len(args) - 1),
        out_specs=[VM] * len(outs),
        scratch_shapes=[pltpu.VMEM(s, d) for s, d in scratch],
        compiler_params=pltpu.CompilerParams(vmem_limit_bytes=min(need + (room << 20), 58 << 20)),
        cost_estimate=pl.CostEstimate(
            flops=int(micros * 1.15e9), bytes_accessed=moved, transcendentals=0
        ),
        name=name,
    )(*args)


def make_tokens_packet(block, memory_block, width):
    rows = block + memory_block + 8

    def kernel(turn, tokens, memory, target_ids, source_ids, sent, kept):
        mine = turn[0]
        for row, out in ((1 - mine, sent), (mine, kept)):
            out[:block, :] = tokens[row]
            out[block : block + memory_block, :] = memory[row]
            ids = target_ids[pl.ds(row, 1), :].astype(F32)
            ids = jnp.concatenate([ids, jnp.zeros((1, width - block), F32)], axis=1)
            others = source_ids[pl.ds(row, 1), :].astype(F32)
            others = jnp.concatenate([others, jnp.zeros((1, width - memory_block), F32)], axis=1)
            place = lax.broadcasted_iota(jnp.int32, (8, width), 0)
            found = jnp.where(place == 0, ids, jnp.where(place == 1, others, 0.0))
            out[block + memory_block :, :] = found.astype(BF16)

    return kernel, [((rows, width), BF16)] * 2


def placed(me, parts, width):
    here = lax.broadcasted_iota(jnp.int32, (parts.shape[1], width), 0) + me * parts.shape[1]
    lane = lax.broadcasted_iota(jnp.int32, (parts.shape[1], width), 1)
    return dot(parts, jnp.where(lane == here, 1.0, 0.0).astype(BF16))


def make_weights_packet(narrow, width, blocks):
    tall = blocks * narrow
    starts = (0, 3 * narrow + 8, 8 * narrow + 24)

    def kernel(me_ref, *refs):
        weights, inner, outer, short, wide, out = refs[:8], refs[8], refs[9], refs[10], refs[11], refs[12]
        me = me_ref[0]
        for i, ref in enumerate(weights):
            at = i * narrow if i < 3 else starts[1] + (i - 3) * narrow
            out[at : at + narrow, :] = ref[...]
        found = placed(me, short[...], width)
        out[3 * narrow : starts[1], :] = jnp.concatenate([found[:2, :], jnp.zeros((6, width), F32)], axis=0).astype(BF16)
        per = width // wide.shape[1]
        row = placed(lax.rem(me, per), wide[...], width)
        place = lax.broadcasted_iota(jnp.int32, (blocks, width), 0)
        spread_row = jnp.where(place == lax.div(me, per), row, 0.0)
        rest = jnp.zeros((16 - (found.shape[0] - 2) - blocks, width), F32)
        out[starts[2] - 16 : starts[2], :] = jnp.concatenate([found[2:, :], spread_row, rest], axis=0).astype(BF16)
        for i in range(blocks):
            out[starts[2] + i * narrow : starts[2] + (i + 1) * narrow, :] = inner[:, i * width : (i + 1) * width]
        out[starts[2] + tall :, :] = outer[...]

    return kernel, [((starts[2] + 2 * tall, width), BF16)]


def make_sort(rows, width):
    def kernel(me_ref, *refs):
        given, outs = refs[:4], refs[4:]
        at = 0
        for count, out in zip(rows, outs):
            for i, ref in enumerate(given):
                out[i * count : (i + 1) * count, :] = ref[at : at + count, :]
            at += count

    return kernel, [((4 * count, width), BF16) for count in rows]


def join(arrays):
    def kernel(*refs):
        at = 0
        for ref in refs[:-1]:
            refs[-1][at : at + ref.shape[0], :] = ref[...]
            at += ref.shape[0]

    rows = sum(a.shape[0] for a in arrays)
    return pl.pallas_call(
        kernel,
        out_shape=jax.ShapeDtypeStruct((rows, arrays[0].shape[1]), arrays[0].dtype),
        in_specs=[VM] * len(arrays),
        out_specs=VM,
        compiler_params=pltpu.CompilerParams(vmem_limit_bytes=16 << 20),
        cost_estimate=pl.CostEstimate(flops=1 << 20, bytes_accessed=0, transcendentals=0),
        name="join",
    )(*arrays)


def make_project(packed, parts, rows, block, memory_block, width, narrow, n_pieces):
    share = rows * block
    length = parts * share
    memory_share = rows * memory_block
    stride = 3 * narrow + 8
    half = width // 2

    def kernel(*refs):
        me_ref, refs = refs[0], list(refs[1:])
        pieces, refs = refs[:n_pieces], refs[n_pieces:]
        tokens, refs = refs[: parts * rows], refs[parts * rows :]
        query, query_t, keys, values, value_t = (refs[2 * i : 2 * i + 2] for i in range(5))
        memory, ids, memory_ids = refs[10:13]
        scratch = refs[13:]
        me = me_ref[0]
        if packed:
            for i in range(3):
                unpack(me, pieces, stride, i * narrow, narrow, scratch[i])
            query_w, key_w, value_w = scratch
            biases = vector_sum(pieces, stride, 3 * narrow)
        else:
            query_w, key_w, value_w = pieces[:3]
            biases = pieces[3][...]
        for i in range(parts):
            here = slice(i * share, (i + 1) * share)
            some = tokens[i * rows : (i + 1) * rows]
            own = jnp.concatenate([t[:block, :] for t in some], axis=0)
            if i == 0:
                scaled = (dot(own, query_w[...]) + biases[0:1, :]).astype(BF16) * BF16(HEAD_DIM**-0.5)
            key = dot(own, key_w[...]).astype(BF16)
            found = (dot(own, value_w[...]) + biases[1:2, :]).astype(BF16)
            for side in range(2):
                columns = slice(side * half, (side + 1) * half)
                if i == 0:
                    query[side][...] = scaled[:, columns]
                    query_t[side][...] = scaled[:, columns].T
                keys[side][here, :] = key[:, columns]
                values[side][here, :] = found[:, columns]
                value_t[side][:, here] = found[:, columns].T
        for i, t in enumerate(tokens):
            memory[i * memory_block : (i + 1) * memory_block, :] = t[block : block + memory_block, :]
            found = t[block + memory_block :, :].astype(F32).astype(jnp.int32)
            ids[:, i * block : (i + 1) * block] = found[0:1, :block]
        found = [t[block + memory_block :, :].astype(F32).astype(jnp.int32)[1:2, :memory_block] for t in tokens]
        memory_ids[...] = jnp.concatenate(found, axis=1)

    outs = [((share, half), BF16)] * 2 + [((half, share), BF16)] * 2
    outs += [((length, half), BF16)] * 4 + [((half, length), BF16)] * 2
    outs += [
        ((parts * memory_share, width), BF16),
        ((1, length), jnp.int32),
        ((1, parts * memory_share), jnp.int32),
    ]
    return kernel, outs, [((width, width), BF16)] * 3 if packed else []


def make_self_attention(share, length, width):
    def kernel(me_ref, *refs):
        query_t, keys, value_t, ids = refs[:2], refs[2:4], refs[4:6], refs[6]
        mixture_t, logs, hot, penalty = refs[7:9], refs[9:11], refs[11], refs[12]
        hot[...] = one_hot(ids[...])
        penalty[...] = penalties(ids[:, :share])
        for side in range(2):
            attend(query_t[side], keys[side], value_t[side], hot, penalty, mixture_t[side], logs[side])

    outs = [((width // 2, share), BF16)] * 2 + [((HEADS // 2, 1, share), F32)] * 2
    return kernel, outs, [((length, PAIR), BF16), ((PAIR, share), BF16)]


def make_cross_forward(packed, rows, block, memory_length, width, narrow, n_pieces):
    share = rows * block
    stride = 5 * narrow + 16

    def kernel(*refs):
        me_ref, refs = refs[0], list(refs[1:])
        pieces, refs = refs[:n_pieces], refs[n_pieces:]
        tokens, refs = refs[:rows], refs[rows:]
        memory, ids, memory_ids, upper, lower = refs[:5]
        first_sum, second_sum, query, memory_keys, memory_values, cross_t, logs, vectors = refs[5:13]
        scratch = refs[13:]
        query_t, value_t, hot, penalty = scratch[:4]
        if packed:
            for i in range(5):
                unpack(me_ref[0], pieces, stride, i * narrow, narrow, scratch[4 + i])
            output_w, query_w, key_w, value_w, source_w = scratch[4:]
            vectors[...] = vector_sum(pieces, stride, 5 * narrow)
        else:
            output_w, query_w, key_w, value_w, source_w = pieces[:5]
            vectors[...] = pieces[5][...]

        def vector(i):
            return vectors[i : i + 1, :]

        own = jnp.concatenate([t[:block, :] for t in tokens], axis=0)
        mixture_t = jnp.concatenate([upper[...], lower[...]], axis=0)
        h = own.astype(F32) + dot_tn(mixture_t, output_w[...]) + vector(OUTPUT_BIAS)
        first_sum[...] = h
        first = normalize(h)[0] * vector(ATTENTION_GAIN) + vector(ATTENTION_SHIFT)
        scaled = (dot(first.astype(BF16), query_w[...]) + vector(SOURCE_QUERY_BIAS)).astype(BF16) * BF16(HEAD_DIM**-0.5)
        query[...] = scaled
        query_t[...] = scaled.T
        memory_keys[...] = dot(memory[...], key_w[...]).astype(BF16)
        memory_values[...] = (dot(memory[...], value_w[...]) + vector(SOURCE_VALUE_BIAS)).astype(BF16)
        value_t[...] = memory_values[...].T
        hot[...] = one_hot(memory_ids[...])
        penalty[...] = penalties(ids[:, :share])
        attend(query_t, memory_keys, value_t, hot, penalty, cross_t, logs)
        first = normalize(first_sum[...])[0] * vector(ATTENTION_GAIN) + vector(ATTENTION_SHIFT)
        second_sum[...] = first + dot_tn(cross_t[...], source_w[...]) + vector(SOURCE_OUTPUT_BIAS)

    outs = [
        ((share, width), F32),
        ((share, width), F32),
        ((share, width), BF16),
        ((memory_length, width), BF16),
        ((memory_length, width), BF16),
        ((width, share), BF16),
        ((HEADS, 1, share), F32),
        ((16, width), F32),
    ]
    scratch = [((width, share), BF16), ((width, memory_length), BF16), ((memory_length, PAIR), BF16), ((PAIR, share), BF16)]
    if packed:
        scratch += [((width, width), BF16)] * 5
    return kernel, outs, scratch


def make_inner(packed, parts, rows, block, width, hidden, narrow, n_pieces):
    blocks = hidden // width
    share = rows * block
    per = width // (blocks * narrow)

    def kernel(*refs):
        me_ref, refs = refs[0], list(refs[1:])
        pieces, refs = refs[:n_pieces], refs[n_pieces:]
        second_sum, cot_own, cot_came, vectors = refs[:4]
        turn = lax.rem(lax.div(me_ref[0], parts), rows)
        out_own, out_send, back, sums = refs[4:8]
        grads, scratch = refs[8:10], refs[10:]
        low, active, gate, slope = scratch[:4]
        if packed:
            inner_w, outer_w, gathered = scratch[4:7]
            tall = blocks * narrow
            for core, far, slot, device in places(me_ref[0]):
                ref, at = pieces[2 * core + far], slot * 2 * tall
                row = pl.multiple_of(device * narrow, narrow)
                for i in range(blocks):
                    inner_w[i, pl.ds(row, narrow), :] = ref[at + i * narrow : at + (i + 1) * narrow, :]
                row = pl.multiple_of(lax.rem(device, per) * tall, tall)
                outer_w[lax.div(device, per), pl.ds(row, tall), :] = ref[at + tall : at + 2 * tall, :]
        else:
            inner_w, outer_w = pieces

        def vector(i):
            return vectors[i : i + 1, :]

        second = normalize(second_sum[...])[0] * vector(SOURCE_GAIN) + vector(SOURCE_SHIFT)
        low[...] = second.astype(BF16)
        back[...] = second + vector(OUTER_BIAS)

        def forward(i, carry):
            inner = dot(low[...], inner_w[i]) + vectors[pl.ds(INNER_BIAS + i, 1), :]
            chance, density = normal_parts(inner)
            found = (inner * chance).astype(BF16)
            active[i] = found
            gate[i] = chance + inner * density
            back[...] += dot(found, outer_w[i])
            return carry

        lax.fori_loop(0, blocks, forward, 0)
        normed, inverse = normalize(back[...])
        final = normed * vector(FINAL_GAIN) + vector(FINAL_SHIFT)
        out_own[...] = final[:block, :]
        out_send[...] = final[block:, :].astype(BF16)
        upstream = jnp.concatenate([cot_own[turn], cot_came[turn]], axis=0).astype(F32)
        sums[0:1, :] = total(upstream * normed)
        sums[1:2, :] = total(upstream)
        back3 = normalize_back(upstream, normed, inverse, vector(FINAL_GAIN))
        slope[...] = back3.astype(BF16)
        sums[2:3, :] = total(slope[...])
        sums[7:8, :] = jnp.zeros_like(sums[7:8, :])
        back[...] = back3

        def backward(i, carry):
            grad = dot_nt(slope[...], outer_w[i]) * gate[i]
            inner_low = grad.astype(BF16)
            sums[pl.ds(3 + i, 1), :] = total(inner_low)
            outer_grad = dot_tn(active[i], slope[...])
            inner_grad = dot_tn(low[...], inner_low)
            back[...] += dot_nt(inner_low, inner_w[i])
            if packed:
                gathered[i] = inner_grad
                gathered[blocks + i] = outer_grad
            else:
                grads[0][i] = inner_grad
                grads[1][i] = outer_grad
            return carry

        lax.fori_loop(0, blocks, backward, 0)
        if packed:
            tall = blocks * narrow
            for core, far, slot, device in places(me_ref[0]):
                ref, at = grads[core], far * 8 + slot
                row = pl.multiple_of(device * narrow, narrow)
                for i in range(blocks):
                    ref[at, i * narrow : (i + 1) * narrow, :] = gathered[i, pl.ds(row, narrow), :].astype(BF16)
                row = pl.multiple_of(lax.rem(device, per) * tall, tall)
                ref[at, tall:, :] = gathered[blocks + lax.div(device, per), pl.ds(row, tall), :].astype(BF16)

    outs = [((block, width), F32), ((block, width), BF16), ((share, width), F32), ((8, width), F32)]
    if packed:
        outs += [((16, 2 * blocks * narrow, width), BF16)] * 2
    else:
        outs += [((blocks, width, width), F32)] * 2
    scratch = [((share, width), BF16), ((blocks, share, width), BF16), ((blocks, share, width), F32), ((share, width), BF16)]
    if packed:
        scratch += [((blocks, width, width), BF16)] * 2 + [((2 * blocks, width, width), F32)]
    return kernel, outs, scratch


def make_cross_back(packed, parts, share, memory_share, width, narrow, n_pieces):
    memory_length = parts * memory_share
    stride = 5 * narrow + 16

    def kernel(*refs):
        me_ref, refs = refs[0], list(refs[1:])
        pieces, refs = refs[:n_pieces], refs[n_pieces:]
        (back2_in, first_sum, second_sum, query, memory_keys, memory_values, cross_t, logs, ids,
         memory_ids, vectors, sums_inner) = refs[:12]
        mixtures, refs = refs[12:14], refs[14:]
        back1, key_own, value_own, sums = refs[:4]
        self_slope, self_slope_t, self_deltas = (refs[4 + 2 * i : 6 + 2 * i] for i in range(3))
        sends, refs = refs[10 : 10 + parts - 1], refs[10 + parts - 1 :]
        grads, scratch = refs[:3], refs[3:]
        (slope_t, slope, key_t, hot, penalty, query_t, deltas, query_grad_t, key_grad, value_grad) = scratch[:10]
        upper, lower = mixtures
        if packed:
            for i, at in enumerate((0, 1, 4)):
                unpack(me_ref[0], pieces, stride, at * narrow, narrow, scratch[10 + i])
            output_w, query_w, source_w = scratch[10:13]
        else:
            output_w, query_w, source_w = pieces

        def vector(i):
            return vectors[i : i + 1, :]

        sums[0:7, :] = sums_inner[0:7, :]
        upstream = back2_in[...]
        normed, inverse = normalize(second_sum[...])
        sums[7:8, :] = total(upstream * normed)
        sums[8:9, :] = total(upstream)
        back2 = normalize_back(upstream, normed, inverse, vector(SOURCE_GAIN))
        back1[...] = back2
        cross_low = back2.astype(BF16)
        sums[9:10, :] = total(cross_low)
        grads[0][...] = dot(cross_t[...], cross_low).astype(BF16)
        found = dot_nt(cross_low, source_w[...]).astype(BF16)
        slope[...] = found
        slope_t[...] = found.T
        deltas_of(slope_t, cross_t, deltas)
        query_t[...] = query[...].T
        key_t[...] = memory_keys[...].T
        hot[...] = one_hot(memory_ids[...])
        penalty[...] = penalties(ids[:, :share])
        attend_back(query_t, query, memory_keys, key_t, memory_values, slope_t, slope, hot, penalty,
                    logs, deltas, query_grad_t, key_grad, value_grad)
        key_own[...] = key_grad[:memory_share, :]
        value_own[...] = value_grad[:memory_share, :]
        for i in range(1, parts):
            here = slice(i * memory_share, (i + 1) * memory_share)
            sends[i - 1][:memory_share, :] = key_grad[here, :].astype(BF16)
            sends[i - 1][memory_share:, :] = value_grad[here, :].astype(BF16)
        query_low = query_grad_t[...].T.astype(BF16)
        sums[10:11, :] = total(query_low)
        normed, inverse = normalize(first_sum[...])
        first_low = (normed * vector(ATTENTION_GAIN) + vector(ATTENTION_SHIFT)).astype(BF16)
        grads[1][...] = dot_tn(first_low, query_low).astype(BF16)
        upstream = back1[...] + dot_nt(query_low, query_w[...])
        sums[11:12, :] = total(upstream * normed)
        sums[12:13, :] = total(upstream)
        grad = normalize_back(upstream, normed, inverse, vector(ATTENTION_GAIN))
        back1[...] = grad
        branch_low = grad.astype(BF16)
        sums[13:14, :] = total(branch_low)
        sums[14:16, :] = jnp.zeros_like(sums[14:16, :])
        mixture_t = jnp.concatenate([upper[...], lower[...]], axis=0)
        grads[2][...] = dot(mixture_t, branch_low).astype(BF16)
        found = dot_nt(branch_low, output_w[...]).astype(BF16)
        for side in range(2):
            columns = slice(side * width // 2, (side + 1) * width // 2)
            self_slope[side][...] = found[:, columns]
            self_slope_t[side][...] = found[:, columns].T
            deltas_of(self_slope_t[side], mixtures[side], self_deltas[side])

    half = width // 2
    outs = [
        ((share, width), F32),
        ((memory_share, width), F32),
        ((memory_share, width), F32),
        ((16, width), F32),
    ]
    outs += [((share, half), BF16)] * 2 + [((half, share), BF16)] * 2
    outs += [((HEADS // 2, 1, share), F32)] * 2
    outs += [((2 * memory_share, width), BF16)] * (parts - 1)
    outs += [((width, width), BF16)] * 3
    scratch = [
        ((width, share), BF16),
        ((share, width), BF16),
        ((width, memory_length), BF16),
        ((memory_length, PAIR), BF16),
        ((PAIR, share), BF16),
        ((width, share), BF16),
        ((HEADS, 1, share), F32),
        ((width, share), F32),
        ((memory_length, width), F32),
        ((memory_length, width), F32),
    ]
    if packed:
        scratch += [((width, width), BF16)] * 3
    return kernel, outs, scratch


def attention_back_half(refs, share, scratch):
    query, keys, values, slope, slope_t, logs, deltas, ids = refs
    query_t, key_t, hot, penalty, query_grad_t, key_grad, value_grad = scratch
    query_t[...] = query[...].T
    key_t[...] = keys[...].T
    hot[...] = one_hot(ids[...])
    penalty[...] = penalties(ids[:, :share])
    attend_back(query_t, query, keys, key_t, values, slope_t, slope, hot, penalty, logs, deltas,
                query_grad_t, key_grad, value_grad)


def half_scratch(share, length, half):
    return [
        ((half, share), BF16),
        ((half, length), BF16),
        ((length, PAIR), BF16),
        ((PAIR, share), BF16),
        ((half, share), F32),
        ((length, half), F32),
        ((length, half), F32),
    ]


def give_half(share, scratch, own, sends):
    key_grad, value_grad = scratch[5:7]
    own[:share, :] = key_grad[:share, :]
    own[share:, :] = value_grad[:share, :]
    for i, send in enumerate(sends):
        here = slice((i + 1) * share, (i + 2) * share)
        send[:share, :] = key_grad[here, :].astype(BF16)
        send[share:, :] = value_grad[here, :].astype(BF16)


def make_self_back_upper(packed, parts, rows, block, memory_block, width, narrow, n_pieces):
    share, memory_share = rows * block, rows * memory_block
    length, half = parts * share, width // 2

    def kernel(*refs):
        me_ref, refs = refs[0], list(refs[1:])
        pieces, refs = refs[:n_pieces], refs[n_pieces:]
        tokens, refs = refs[:rows], refs[rows:]
        operands, refs = refs[:8], refs[8:]
        memory_key_own, memory_value_own, sums_in = refs[:3]
        early, refs = refs[3:6], refs[6:]
        memory_received, refs = refs[: parts - 1], refs[parts - 1 :]
        query_grad, own, memory_own, memory_send = refs[:4]
        sends, refs = refs[4 : 4 + parts - 1], refs[4 + parts - 1 :]
        n_grads = 2 if packed else 3
        grad_refs, scratch = refs[:n_grads], refs[n_grads:]
        sums = scratch[7]
        me = me_ref[0]
        if packed:
            for i in range(2):
                unpack(me, pieces, 5 * narrow + 16, (2 + i) * narrow, narrow, scratch[8 + i])
            source_key, source_value = scratch[8:10]
        else:
            source_key, source_value = pieces
        grads = Grads(me, grad_refs, scratch[10] if packed else None, narrow)
        memory = jnp.concatenate([t[block : block + memory_block, :] for t in tokens], axis=0)
        key_sum, value_sum = memory_key_own[...], memory_value_own[...]
        for ref in memory_received:
            key_sum = key_sum + ref[:memory_share, :].astype(F32)
            value_sum = value_sum + ref[memory_share:, :].astype(F32)
        key_low, value_low = key_sum.astype(BF16), value_sum.astype(BF16)
        sums[...] = sums_in[...]
        sums[14:15, :] = total(value_low)
        grads.put_sums(5 * narrow, sums[...])
        grads.put(0, dot_tn(memory, key_low))
        grads.put(1, dot_tn(memory, value_low))
        if packed:
            for i, ref in enumerate(early):
                grads.put(2 + i, ref[...].astype(F32))
        grad = dot_nt(key_low, source_key[...]) + dot_nt(value_low, source_value[...])
        memory_own[...] = grad[:memory_block, :]
        memory_send[...] = grad[memory_block:, :].astype(BF16)
        attention_back_half(operands, share, scratch[:7])
        query_grad[...] = scratch[4][...].T.astype(BF16)
        give_half(share, scratch, own, sends)

    outs = [
        ((share, half), BF16),
        ((2 * share, half), F32),
        ((memory_block, width), F32),
        ((memory_block, width), BF16),
    ]
    outs += [((2 * share, half), BF16)] * (parts - 1)
    if packed:
        outs += [((16, 5 * narrow + 16, width), BF16)] * 2
    else:
        outs += [((width, width), F32)] * 2 + [((16, width), F32)]
    scratch = half_scratch(share, length, half) + [((16, width), F32)]
    if packed:
        scratch += [((width, width), BF16)] * 2 + [((width, width), F32)]
    return kernel, outs, scratch


def make_self_back_lower(packed, parts, rows, block, width, narrow, n_pieces):
    share = rows * block
    length, half = parts * share, width // 2

    def kernel(*refs):
        me_ref, refs = refs[0], list(refs[1:])
        pieces, refs = refs[:n_pieces], refs[n_pieces:]
        tokens, refs = refs[:rows], refs[rows:]
        operands, refs = refs[:8], refs[8:]
        back1, query_upper = refs[:2]
        in_part, query_sum, query_w_grad, own = refs[2:6]
        sends, scratch = refs[6 : 6 + parts - 1], refs[6 + parts - 1 :]
        if packed:
            unpack(me_ref[0], pieces, 3 * narrow + 8, 0, narrow, scratch[7])
            query_w = scratch[7]
        else:
            (query_w,) = pieces
        attention_back_half(operands, share, scratch[:7])
        give_half(share, scratch, own, sends)
        query_low = jnp.concatenate([query_upper[...], scratch[4][...].T.astype(BF16)], axis=1)
        tokens_own = jnp.concatenate([t[:block, :] for t in tokens], axis=0)
        in_part[...] = back1[...] + dot_nt(query_low, query_w[...])
        query_sum[...] = jnp.concatenate([total(query_low), jnp.zeros((7, width), F32)], axis=0)
        query_w_grad[...] = dot_tn(tokens_own, query_low).astype(query_w_grad.dtype)

    outs = [
        ((share, width), F32),
        ((8, width), F32),
        ((width, width), BF16 if packed else F32),
        ((2 * share, half), F32),
    ]
    outs += [((2 * share, half), BF16)] * (parts - 1)
    scratch = half_scratch(share, length, half)
    if packed:
        scratch += [((width, width), BF16)]
    return kernel, outs, scratch


def make_last(packed, parts, rows, block, memory_block, width, narrow, n_pieces):
    share = rows * block

    def kernel(*refs):
        me_ref, refs = refs[0], list(refs[1:])
        pieces, refs = refs[:n_pieces], refs[n_pieces:]
        tokens, refs = refs[:rows], refs[rows:]
        in_part, query_sum, query_w_grad, memory_send = refs[:4]
        owns, refs = refs[4:6], refs[6:]
        received = [refs[: parts - 1], refs[parts - 1 : 2 * (parts - 1)]]
        refs = refs[2 * (parts - 1) :]
        in_own, in_send = refs[:2]
        n_grads = 2 if packed else 3
        grad_refs, scratch = refs[2 : 2 + n_grads], refs[2 + n_grads :]
        sums = scratch[0]
        me = me_ref[0]
        if packed:
            for i in range(2):
                unpack(me, pieces, 3 * narrow + 8, (1 + i) * narrow, narrow, scratch[1 + i])
            key_w, value_w = scratch[1:3]
        else:
            key_w, value_w = pieces
        grads = Grads(me, grad_refs, scratch[3] if packed else None, narrow)
        if packed:
            grads.put(2, query_w_grad[...].astype(F32))
        lows = []
        for own, others in zip(owns, received):
            found = own[...]
            for ref in others:
                found = found + ref[...].astype(F32)
            lows.append(found.astype(BF16))
        key_low = jnp.concatenate([low[:share, :] for low in lows], axis=1)
        value_low = jnp.concatenate([low[share:, :] for low in lows], axis=1)
        tokens_own = jnp.concatenate([t[:block, :] for t in tokens], axis=0)
        sums[...] = query_sum[...]
        sums[1:2, :] = total(value_low)
        grads.put_sums(3 * narrow, sums[...])
        grads.put(0, dot_tn(tokens_own, key_low))
        grads.put(1, dot_tn(tokens_own, value_low))
        grad = in_part[...] + dot_nt(key_low, key_w[...]) + dot_nt(value_low, value_w[...])
        in_own[...] = grad[:block, :]
        in_send[:block, :] = grad[block:, :].astype(BF16)
        in_send[block:, :] = memory_send[...]

    outs = [((block, width), F32), ((block + memory_block, width), BF16)]
    if packed:
        outs += [((16, 3 * narrow + 8, width), BF16)] * 2
    else:
        outs += [((width, width), F32)] * 2 + [((8, width), F32)]
    scratch = [((8, width), F32)]
    if packed:
        scratch += [((width, width), BF16)] * 2 + [((width, width), F32)]
    return kernel, outs, scratch


def combine(arrays, splits):
    count = arrays[0].shape[0] // splits
    shape = (count,) + arrays[0].shape[1:]

    def kernel(*refs):
        given, outs = refs[: len(arrays)], refs[len(arrays) :]
        for i, out in enumerate(outs):
            here = slice(i * count, (i + 1) * count)
            found = given[0][here].astype(F32)
            for ref in given[1:]:
                found = found + ref[here].astype(F32)
            out[...] = found.astype(out.dtype)

    return pl.pallas_call(
        kernel,
        out_shape=[jax.ShapeDtypeStruct(shape, BF16)] * splits,
        in_specs=[VM] * len(arrays),
        out_specs=[VM] * splits,
        compiler_params=pltpu.CompilerParams(vmem_limit_bytes=20 << 20),
        cost_estimate=pl.CostEstimate(flops=1 << 20, bytes_accessed=0, transcendentals=0),
        name="combine",
    )(*arrays)


def chosen(me, rows, wide):
    width = rows.shape[1]
    line = lax.broadcasted_iota(jnp.int32, (width, wide), 0)
    here = lax.broadcasted_iota(jnp.int32, (width, wide), 1) + me * wide
    choice = jnp.where(line == here, 1.0, 0.0)
    return lax.dot_general(rows, choice, (((1,), (0,)), ((), ())), precision=lax.Precision.HIGHEST, preferred_element_type=F32)


def reduce_all(array, devices):
    mask = 1
    while mask < devices:
        array = array + swap(array, mask, devices)
        mask *= 2
    return array


def per_device(
    tokens, memory, target_ids, source_ids, cotangent,
    query_weight, key_weight, value_weight, output_weight, query_bias, value_bias, output_bias,
    attention_gain, attention_shift,
    source_query, source_key, source_value, source_output, source_query_bias, source_value_bias,
    source_output_bias, source_gain, source_shift,
    inner_weight, inner_bias, outer_weight, outer_bias, final_gain, final_shift,
    *, devices, sequence,
):
    packed = devices == 32
    rows, block, width = tokens.shape
    memory_block = memory.shape[1]
    parts = sequence // rows
    share, memory_share = rows * block, rows * memory_block
    hidden = inner_weight.shape[1]
    blocks = hidden // width
    me = lax.axis_index(AXES)
    me_array = me.reshape(1).astype(jnp.int32)
    turn = lax.rem(lax.div(me, parts), rows)
    narrow, wide = width // devices, hidden // devices

    def run(made, micros, name, *args):
        kernel, outs, *scratch = made
        return call(kernel, outs, (me_array,) + args, scratch[0] if scratch else [], micros, name)

    turn_array = turn.reshape(1).astype(jnp.int32)

    def turned(made, name, *args):
        kernel, outs = made
        return call(kernel, outs, (turn_array,) + args, [], 1.0, name)

    short = jnp.stack([query_bias, value_bias, output_bias, attention_gain, attention_shift,
                       source_query_bias, source_value_bias, source_output_bias, source_gain,
                       source_shift, outer_bias, final_gain, final_shift])

    def whole(array):
        return lax.all_gather(array, AXES, axis=0, tiled=True)

    sent, kept = turned(
        make_tokens_packet(block, memory_block, width), "tokens_packet",
        tokens, memory, target_ids, source_ids,
    )
    came = swap(sent, parts, devices)
    row_tokens = [kept, came]
    kept_swaps = [swap(kept, m, devices) for m in range(1, parts)]
    came_swaps = [swap(came, m, devices) for m in range(1, parts)]
    for pair in zip(kept_swaps, came_swaps):
        row_tokens += pair
    own_tokens = row_tokens[:rows]

    if packed:
        (block_own,) = run(make_weights_packet(narrow, width, blocks), 1.0, "weights_packet",
                           query_weight, key_weight, value_weight, output_weight, source_query,
                           source_key, source_value, source_output, inner_weight, outer_weight,
                           short, inner_bias.reshape(1, wide))
        block_own = after(block_own, sent)
        sizes = (3 * narrow + 8, 5 * narrow + 16, 2 * blocks * narrow)
        first_a, second_a, third_a = run(
            make_sort(sizes, width), 1.0, "sort", block_own, *[swap(block_own, m, 32) for m in Z_MASKS[1:]]
        )
        first_b, second_b = turned_swap(first_a, 1), turned_swap(second_a, 1)
        first_c = join(after([first_a, first_b], came, *kept_swaps))
        first_d = turned_swap(first_c, 2)
        second_c = join([second_a, second_b])
        second_d = turned_swap(second_c, 2)
        third_b = turned_swap(third_a, 1)
        first_d = after(first_d, second_c, *came_swaps)
        set_self = [first_c, first_d, swap(first_c, 1, 32), swap(first_d, 1, 32)]
        second_b = turned_swap(second_a, 1)
    else:
        full = [whole(w) for w in (query_weight, key_weight, value_weight, output_weight, source_query, source_key, source_value, source_output)]
        lane = lax.broadcasted_iota(jnp.int32, (1, width), 1)
        place = lax.broadcasted_iota(jnp.int32, (blocks, width), 0) * width + lane
        spread_wide = jnp.where(place // wide == me, jnp.tile(inner_bias.reshape(1, wide), (blocks, width // wide)), 0)

        def natural(rows):
            return jnp.where(lane // narrow == me, jnp.tile(rows, (1, devices)), 0)

        vectors = jnp.concatenate([natural(short[:2]), jnp.zeros((6, width), BF16), natural(short[2:]), spread_wide, jnp.zeros((1, width), BF16)])
        vectors = reduce_all(vectors, devices).astype(F32)
        set_self = full[:3] + [vectors[:8]]
        set_cross = full[3:] + [vectors[8:]]
        set_inner = [
            whole(inner_weight).reshape(width, blocks, width).transpose(1, 0, 2),
            whole(outer_weight).reshape(blocks, width, width),
        ]
    found = run(
        make_project(packed, parts, rows, block, memory_block, width, narrow, len(set_self)), 5.0,
        "project", *set_self, *row_tokens,
    )
    query, query_t, keys, values, value_t = (found[2 * i : 2 * i + 2] for i in range(5))
    row_memory, ids, memory_ids = found[10:]
    query_t = list(query_t)
    if packed:
        third_c = join(after([third_a, third_b], query_t[0]))
        third_d = turned_swap(third_c, 2)
        second_d = after(second_d, query_t[0])
        set_cross = [second_c, second_d, swap(second_c, 1, 32), swap(second_d, 1, 32)]
        query_t[0] = after(query_t[0], third_c, second_d)
        set_back, set_query, set_last, set_memory = set_cross, set_self, set_self, set_cross
    else:
        set_back, set_query, set_last, set_memory = [full[3], full[4], full[7]], full[:1], full[1:3], full[5:7]
    cot_came = swap(cotangent, parts, devices)
    found = run(
        make_self_attention(share, parts * share, width), 12.0, "self_attention",
        *query_t, *keys, *value_t, ids,
    )
    mixtures, logs = found[:2], found[2:]
    if packed:
        third_d = after(third_d, mixtures[0])
        set_inner = [third_c, third_d, swap(third_c, 1, 32), swap(third_d, 1, 32)]
        mixtures = [after(mixtures[0], third_d, cot_came), mixtures[1]]
    first_sum, second_sum, cross_query, memory_keys, memory_values, cross_t, cross_logs, vectors = run(
        make_cross_forward(packed, rows, block, parts * memory_share, width, narrow, len(set_cross)),
        9.0, "cross_forward", *set_cross, *own_tokens, row_memory, ids, memory_ids, *mixtures,
    )
    out_own, out_send, back2_in, sums_inner, *grads_inner = run(
        make_inner(packed, parts, rows, block, width, hidden, narrow, len(set_inner)), 18.0, "inner",
        *set_inner, second_sum, cotangent, cot_came, vectors,
    )
    out_came = swap(out_send, parts, devices)
    found = run(
        make_cross_back(packed, parts, share, memory_share, width, narrow, len(set_back)), 14.0,
        "cross_back", *set_back, back2_in, first_sum, second_sum, cross_query, memory_keys,
        memory_values, cross_t, cross_logs, ids, memory_ids, vectors, sums_inner, *mixtures,
    )
    back1, memory_key_own, memory_value_own, sums_cross = found[:4]
    slope, slope_t, deltas = (found[4 + 2 * i : 6 + 2 * i] for i in range(3))
    memory_received = [swap(a, m + 1, devices) for m, a in enumerate(found[10 : 10 + parts - 1])]
    grads_early = found[10 + parts - 1 :]
    query = list(query)
    if packed:
        keep, send = combine([grads_inner[0], swap(grads_inner[1], 1, 32)], 2)
        query[0] = after(query[0], keep, out_came)
        inner_step = [keep, turned_swap(send, 2)]
    found = run(
        make_self_back_upper(packed, parts, rows, block, memory_block, width, narrow, len(set_memory)),
        12.0, "self_back_upper", *set_memory, *own_tokens, query[0], keys[0], values[0], slope[0],
        slope_t[0], logs[0], deltas[0], ids, memory_key_own, memory_value_own, sums_cross,
        *grads_early, *memory_received,
    )
    query_upper, own_upper, memory_own, memory_send = found[:4]
    received_upper = [swap(a, m + 1, devices) for m, a in enumerate(found[4 : 4 + parts - 1])]
    grads_cross = found[4 + parts - 1 :]
    if packed:
        keep, send = combine(inner_step, 2)
        inner_step = [keep, turned_swap(send, 1)]
        keep_cross, send = combine([grads_cross[0], swap(grads_cross[1], 1, 32)], 2)
        cross_step = [keep_cross, turned_swap(send, 2)]
        query[1] = after(query[1], keep, keep_cross)
    in_part, query_sum, query_w_grad, own_lower, *sends = run(
        make_self_back_lower(packed, parts, rows, block, width, narrow, len(set_query)), 11.0,
        "self_back_lower", *set_query, *own_tokens, query[1], keys[1], values[1], slope[1],
        slope_t[1], logs[1], deltas[1], ids, back1, query_upper,
    )
    received_lower = [swap(a, m + 1, devices) for m, a in enumerate(sends)]
    if packed:
        def lowest(arrays):
            found = combine(arrays, 4)
            return [found[0]] + [swap(a, m, 32) for a, m in zip(found[1:], Z_MASKS[1:])]

        inner_step = lowest(inner_step)
        keep_cross, send = combine(cross_step, 2)
        cross_step = [keep_cross, turned_swap(send, 1)]
        in_part = after(in_part, keep_cross, inner_step[0])
    in_own, in_send, *grads_last = run(
        make_last(packed, parts, rows, block, memory_block, width, narrow, len(set_last)), 6.0,
        "last", *set_last, *own_tokens, in_part, query_sum, query_w_grad, memory_send, own_upper,
        own_lower, *received_upper, *received_lower,
    )

    def regroup(mine, came):
        came = came.astype(F32)
        return jnp.where(turn == 0, jnp.stack([mine, came]), jnp.stack([came, mine]))

    output = regroup(out_own, out_came)
    in_came = swap(in_send, parts, devices)
    input_gradient = regroup(in_own, in_came[:block])
    memory_gradient = regroup(memory_own, in_came[block:])

    if packed:
        grads_last[1] = after(grads_last[1], *cross_step, *inner_step)
        keep, send = combine([grads_last[0], swap(grads_last[1], 1, 32)], 2)
        last_step = [keep, turned_swap(send, 2)]
        cross_step = lowest(cross_step)
        keep, send = combine(after(last_step, cross_step[0]), 2)
        last_step = lowest(after([keep, turned_swap(send, 1)], *cross_step))

        def plan(me_ref, *refs):
            me = me_ref[0]
            steps, outs = [refs[:4], refs[4:8], refs[8:12]], refs[12:]
            inner, cross, last = (sum(r[0].astype(F32) for r in given) for given in steps)
            for i in range(blocks):
                outs[0][:, i * width : (i + 1) * width] = inner[i * narrow : (i + 1) * narrow, :]
            outs[1][...] = inner[blocks * narrow :, :]
            for i in range(5):
                outs[2 + i][...] = cross[i * narrow : (i + 1) * narrow, :]
            for i in range(3):
                outs[7 + i][...] = last[i * narrow : (i + 1) * narrow, :]
            rows_in = jnp.concatenate([cross[5 * narrow :, :], last[3 * narrow :, :]], axis=0)
            outs[10][...] = chosen(me, rows_in, narrow)
            per = width // wide
            line = lax.broadcasted_iota(jnp.int32, (blocks, width), 0)
            row = jnp.sum(jnp.where(line == lax.div(me, per), rows_in[3 : 3 + blocks, :], 0.0), axis=0, keepdims=True)
            outs[11][...] = chosen(lax.rem(me, per), row, wide)

        part = (narrow, width)
        shapes = [(narrow, hidden), (wide, width)] + [part] * 8 + [(24, narrow), (1, wide)]
        (inner_share, outer_share, source_key_share, source_value_share, source_output_share,
         source_query_share, output_share, key_share, value_share, query_share, sums,
         inner_bias_share) = call(
            plan, [(s, F32) for s in shapes], (me_array, *inner_step, *cross_step, *last_step), [], 2.0,
            "finish",
        )
        inner_bias_share = inner_bias_share.reshape(wide)
    else:
        def scatter(array):
            return lax.psum_scatter(array, AXES, scatter_dimension=0, tiled=True)

        inner_share = scatter(grads_inner[0].transpose(1, 0, 2).reshape(width, hidden))
        outer_share = scatter(grads_inner[1].reshape(hidden, width))
        source_output_share, source_query_share, output_share = (scatter(g.astype(F32)) for g in grads_early)
        source_key_share, source_value_share = (scatter(g) for g in grads_cross[:2])
        key_share, value_share = (scatter(g) for g in grads_last[:2])
        query_share = scatter(query_w_grad)
        sums = reduce_all(jnp.concatenate([grads_cross[2], grads_last[2]], axis=0), devices)
        inner_bias_share = lax.dynamic_slice(sums[3 : 3 + blocks].reshape(hidden), (me * wide,), (wide,))
        sums = lax.dynamic_slice(sums, (0, me * narrow), (sums.shape[0], narrow))
    return (
        output,
        input_gradient,
        memory_gradient,
        query_share,
        key_share,
        value_share,
        output_share,
        sums[16],
        sums[17],
        sums[13],
        sums[11],
        sums[12],
        source_query_share,
        source_key_share,
        source_value_share,
        source_output_share,
        sums[10],
        sums[14],
        sums[9],
        sums[7],
        sums[8],
        inner_share,
        inner_bias_share,
        outer_share,
        sums[2],
        sums[0],
        sums[1],
    )


def solution(mesh):
    sequence, devices = mesh.shape["seq"], mesh.size
    tokens, ids = P("dp", "seq", None), P("dp", "seq")
    matrix, vector = P(AXES, None), P(AXES)
    attention = (matrix,) * 4 + (vector,) * 5
    inner = (matrix, vector, matrix, vector, vector, vector)
    return jax.shard_map(
        functools.partial(per_device, devices=devices, sequence=sequence),
        mesh=mesh,
        in_specs=(tokens, tokens, ids, ids, tokens) + attention + attention + inner,
        out_specs=(tokens, tokens, tokens) + attention + attention + inner,
        check_vma=False,
    )
```

```python
import functools
import math

import jax
import jax.numpy as jnp
from jax import lax
from jax.experimental import pallas as pl
from jax.experimental.pallas import tpu as pltpu
from jax.sharding import PartitionSpec as P

HEADS = 8
HEAD_DIM = 64
PAIR = 128
EPSILON = 1e-05
MASKED = 1e9
AXES = ("dp", "seq")
F32 = jnp.float32
BF16 = jnp.bfloat16

(
    OUTPUT_BIAS,
    ATTENTION_GAIN,
    ATTENTION_SHIFT,
    SOURCE_QUERY_BIAS,
    SOURCE_VALUE_BIAS,
    SOURCE_OUTPUT_BIAS,
    SOURCE_GAIN,
    SOURCE_SHIFT,
    OUTER_BIAS,
    FINAL_GAIN,
    FINAL_SHIFT,
    INNER_BIAS,
) = range(12)
Z_MASKS = (0, 8, 16, 24)
VM = pl.BlockSpec(memory_space=pltpu.VMEM)
SM = pl.BlockSpec(memory_space=pltpu.SMEM)


def dot(a, b):
    return lax.dot_general(a, b, (((1,), (0,)), ((), ())), preferred_element_type=F32)


def dot_nt(a, b):
    return lax.dot_general(a, b, (((1,), (1,)), ((), ())), preferred_element_type=F32)


def dot_tn(a, b):
    return lax.dot_general(a, b, (((0,), (0,)), ((), ())), preferred_element_type=F32)


def total(values):
    return jnp.sum(values.astype(F32), axis=0, keepdims=True)


def normalize(h):
    average = jnp.mean(h, axis=-1, keepdims=True)
    centered = h - average
    variance = jnp.mean(centered * centered, axis=-1, keepdims=True)
    inverse = lax.rsqrt(variance + EPSILON)
    return centered * inverse, inverse


def normalize_back(upstream, normed, inverse, gain):
    scaled = upstream * gain
    first_mean = jnp.mean(scaled, axis=-1, keepdims=True)
    second_mean = jnp.mean(scaled * normed, axis=-1, keepdims=True)
    return inverse * (scaled - first_mean - normed * second_mean)


def normal_parts(v):
    density = 0.3989422804014327 * jnp.exp(-0.5 * v * v)
    t = 1.0 / (1.0 + 0.2316419 * jnp.abs(v))
    series = t * (
        0.319381530
        + t * (-0.356563782 + t * (1.781477937 + t * (-1.821255978 + t * 1.330274429)))
    )
    tail = density * series
    return jnp.where(v >= 0.0, 1.0 - tail, tail), density


def penalties(ids):
    place = lax.broadcasted_iota(jnp.int32, (PAIR, ids.shape[1]), 0)
    return jnp.where((place == ids) | (place >= 4), 0.0, -MASKED).astype(BF16)


def one_hot(ids):
    place = lax.broadcasted_iota(jnp.int32, (PAIR, ids.shape[1]), 0)
    return jnp.where(place == ids, 1.0, 0.0).astype(F32).T.astype(BF16)


def spread(part, half):
    empty = jnp.zeros_like(part)
    return [part, empty] if half == 0 else [empty, part]


def attend(query_t, keys, value_t, hot, penalty, mixture_t, logs):
    length = keys.shape[0]

    def pair(p, carry):
        columns = pl.ds(pl.multiple_of(p * PAIR, PAIR), PAIR)
        left = jnp.concatenate([keys[:, columns], hot[...]], axis=1)
        for half in range(2):
            rows = pl.ds(pl.multiple_of(p * PAIR + half * HEAD_DIM, HEAD_DIM), HEAD_DIM)
            right = jnp.concatenate(spread(query_t[rows, :], half) + [penalty[...]], axis=0)
            scores = dot(left, right)
            highest = jnp.max(scores, axis=0, keepdims=True)
            weights = jnp.exp(scores - highest).astype(BF16)
            values = jnp.concatenate(
                [value_t[rows, :], jnp.ones((16, length), BF16)], axis=0
            )
            found = dot(values, weights)
            denominator = found[HEAD_DIM : HEAD_DIM + 1, :]
            mixture_t[rows, :] = (found[:HEAD_DIM, :] / denominator).astype(BF16)
            logs[2 * p + half] = highest + jnp.log(denominator)
        return carry

    lax.fori_loop(0, keys.shape[1] // PAIR, pair, 0)


def attend_back(
    query_t, query, keys, key_t, values, slope_t, slope, hot, penalty, logs, deltas,
    query_grad_t, key_grad, value_grad,
):
    tokens = query.shape[0]
    lane = lax.broadcasted_iota(jnp.int32, (tokens, PAIR), 1)

    def pair(p, carry):
        columns = pl.ds(pl.multiple_of(p * PAIR, PAIR), PAIR)
        left = jnp.concatenate([keys[:, columns], hot[...]], axis=1)
        value_pair = values[:, columns]
        key_sum, value_sum = None, None
        for half in range(2):
            rows = pl.ds(pl.multiple_of(p * PAIR + half * HEAD_DIM, HEAD_DIM), HEAD_DIM)
            right = jnp.concatenate(spread(query_t[rows, :], half) + [penalty[...]], axis=0)
            chances = jnp.exp(dot(left, right) - logs[2 * p + half])
            slopes = dot(value_pair, jnp.concatenate(spread(slope_t[rows, :], half), axis=0))
            grads = (chances * (slopes - deltas[2 * p + half])).astype(BF16)
            query_grad_t[rows, :] = dot(key_t[rows, :], grads) * HEAD_DIM**-0.5
            mine = (lane < HEAD_DIM) if half == 0 else (lane >= HEAD_DIM)
            none = jnp.zeros((tokens, PAIR), BF16)
            value_part = dot(chances.astype(BF16), jnp.where(mine, slope[:, columns], none))
            key_part = dot(grads, jnp.where(mine, query[:, columns], none))
            value_sum = value_part if value_sum is None else value_sum + value_part
            key_sum = key_part if key_sum is None else key_sum + key_part
        key_grad[:, columns] = key_sum
        value_grad[:, columns] = value_sum
        return carry

    lax.fori_loop(0, keys.shape[1] // PAIR, pair, 0)


def deltas_of(slope_t, mixture_t, deltas):
    for head in range(slope_t.shape[0] // HEAD_DIM):
        rows = slice(head * HEAD_DIM, (head + 1) * HEAD_DIM)
        deltas[head] = jnp.sum(
            slope_t[rows, :].astype(F32) * mixture_t[rows, :].astype(F32), axis=0, keepdims=True
        )


def swap(array, mask, devices):
    return lax.ppermute(array, AXES, [(i, i ^ mask) for i in range(devices)])


ORDERS = ((8, 16, 2, 4), (16, 8, 4, 2))


def turned_swap(array, step):
    return lax.ppermute(array, AXES, [(i, i ^ ORDERS[i % 2][step]) for i in range(32)])


def after(value, *others):
    return lax.optimization_barrier((value, others))[0]


def places(me):
    found = []
    for core in range(2):
        even = ((me & 1) ^ core) == 0
        masks = [jnp.where(even, first, second) for first, second in zip(*ORDERS)]
        for far in range(2):
            for slot in range(8):
                device = me ^ core if core else me
                for step, bit in enumerate((slot & 1, slot & 2, slot & 4, far)):
                    if bit:
                        device = device ^ masks[step]
                found.append((core, far, slot, device))
    return found


def unpack(me, pieces, stride, first, rows, scratch):
    for core, far, slot, device in places(me):
        ref = pieces[2 * core + far]
        at = slot * stride + first
        scratch[pl.ds(pl.multiple_of(device * rows, rows), rows), :] = ref[at : at + rows, :]


def vector_sum(pieces, stride, first):
    found = None
    for ref in pieces:
        for slot in range(8):
            part = ref[slot * stride + first : (slot + 1) * stride, :].astype(F32)
            found = part if found is None else found + part
    return found


class Grads:
    def __init__(self, me, refs, dense, rows):
        self.me, self.refs, self.dense, self.rows = me, refs, dense, rows

    def put(self, index, grad):
        if self.dense is None:
            self.refs[index][...] = grad
            return
        self.dense[...] = grad
        rows = self.rows
        for core, far, slot, device in places(self.me):
            found = self.dense[pl.ds(pl.multiple_of(device * rows, rows), rows), :]
            self.refs[core][far * 8 + slot, index * rows : (index + 1) * rows, :] = found.astype(BF16)

    def put_sums(self, first, sums):
        if self.dense is None:
            self.refs[-1][...] = sums
            return
        low = sums.astype(BF16)
        for ref in self.refs:
            for slot in range(16):
                ref[slot, first : first + sums.shape[0], :] = low


def grad_outs(packed, count, rows, width, sums):
    if packed:
        return [((16, count * rows + sums, width), BF16)] * 2
    return [((width, width), F32)] * count + [((sums, width), F32)]


def padded(shape, dtype):
    last = -(-shape[-1] // 128) * 128
    tall = -(-shape[-2] // 16) * 16 if len(shape) > 1 else 16
    return math.prod(shape[:-2]) * tall * last * jnp.dtype(dtype).itemsize


def call(kernel, outs, args, scratch, micros, name, room=10):
    moved = sum(math.prod(a.shape) * a.dtype.itemsize for a in args[1:])
    moved += sum(math.prod(s) * jnp.dtype(d).itemsize for s, d in outs)
    need = sum(padded(a.shape, a.dtype) for a in args[1:])
    need += sum(padded(s, d) for s, d in list(outs) + list(scratch))
    return pl.pallas_call(
        kernel,
        out_shape=[jax.ShapeDtypeStruct(s, d) for s, d in outs],
        in_specs=[SM] + [VM] * (len(args) - 1),
        out_specs=[VM] * len(outs),
        scratch_shapes=[pltpu.VMEM(s, d) for s, d in scratch],
        compiler_params=pltpu.CompilerParams(vmem_limit_bytes=min(need + (room << 20), 58 << 20)),
        cost_estimate=pl.CostEstimate(
            flops=int(micros * 1.15e9), bytes_accessed=moved, transcendentals=0
        ),
        name=name,
    )(*args)


def make_tokens_packet(block, memory_block, width):
    first = block + memory_block + 8

    def kernel(turn, tokens, memory, target_ids, source_ids, cotangent, sent, kept):
        mine = turn[0]
        for row, out in ((1 - mine, sent), (mine, kept)):
            out[:block, :] = tokens[row]
            out[block : block + memory_block, :] = memory[row]
            ids = target_ids[pl.ds(row, 1), :].astype(F32)
            ids = jnp.concatenate([ids, jnp.zeros((1, width - block), F32)], axis=1)
            others = source_ids[pl.ds(row, 1), :].astype(F32)
            others = jnp.concatenate([others, jnp.zeros((1, width - memory_block), F32)], axis=1)
            place = lax.broadcasted_iota(jnp.int32, (8, width), 0)
            found = jnp.where(place == 0, ids, jnp.where(place == 1, others, 0.0))
            out[block + memory_block : first, :] = found.astype(BF16)
            out[first:, :] = cotangent[row]

    return kernel, [((first + block, width), BF16)] * 2


def placed(me, parts, width):
    here = lax.broadcasted_iota(jnp.int32, (parts.shape[1], width), 0) + me * parts.shape[1]
    lane = lax.broadcasted_iota(jnp.int32, (parts.shape[1], width), 1)
    return dot(parts, jnp.where(lane == here, 1.0, 0.0).astype(BF16))


def make_weights_packet(narrow, width, blocks):
    tall = blocks * narrow

    def kernel(me_ref, *refs):
        weights, inner, outer, short, wide = refs[:8], refs[8], refs[9], refs[10], refs[11]
        first, second, third = refs[12:]
        me = me_ref[0]
        for i, ref in enumerate(weights):
            if i < 3:
                first[i * narrow : (i + 1) * narrow, :] = ref[...]
            else:
                second[(i - 3) * narrow : (i - 2) * narrow, :] = ref[...]
        found = placed(me, short[...], width)
        first[3 * narrow :, :] = jnp.concatenate([found[:2, :], jnp.zeros((6, width), F32)], axis=0).astype(BF16)
        per = width // wide.shape[1]
        row = placed(lax.rem(me, per), wide[...], width)
        place = lax.broadcasted_iota(jnp.int32, (blocks, width), 0)
        spread_row = jnp.where(place == lax.div(me, per), row, 0.0)
        rest = jnp.zeros((16 - (found.shape[0] - 2) - blocks, width), F32)
        second[5 * narrow :, :] = jnp.concatenate([found[2:, :], spread_row, rest], axis=0).astype(BF16)
        for i in range(blocks):
            third[i * narrow : (i + 1) * narrow, :] = inner[:, i * width : (i + 1) * width]
        third[tall:, :] = outer[...]

    return kernel, [((rows, width), BF16) for rows in (3 * narrow + 8, 5 * narrow + 16, 2 * tall)]


def join(arrays):
    def kernel(*refs):
        at = 0
        for ref in refs[:-1]:
            refs[-1][at : at + ref.shape[0], :] = ref[...]
            at += ref.shape[0]

    rows = sum(a.shape[0] for a in arrays)
    return pl.pallas_call(
        kernel,
        out_shape=jax.ShapeDtypeStruct((rows, arrays[0].shape[1]), arrays[0].dtype),
        in_specs=[VM] * len(arrays),
        out_specs=VM,
        compiler_params=pltpu.CompilerParams(vmem_limit_bytes=16 << 20),
        cost_estimate=pl.CostEstimate(flops=1 << 20, bytes_accessed=0, transcendentals=0),
        name="join",
    )(*arrays)


def make_project(packed, parts, rows, block, memory_block, width, narrow, n_pieces):
    share = rows * block
    length = parts * share
    memory_share = rows * memory_block
    stride = 3 * narrow + 8
    half = width // 2

    def kernel(*refs):
        me_ref, refs = refs[0], list(refs[1:])
        pieces, refs = refs[:n_pieces], refs[n_pieces:]
        tokens, refs = refs[: parts * rows], refs[parts * rows :]
        query, query_t, keys, values, value_t = (refs[2 * i : 2 * i + 2] for i in range(5))
        memory, ids, memory_ids = refs[10:13]
        scratch = refs[13:]
        me = me_ref[0]
        if packed:
            for i in range(3):
                unpack(me, pieces, stride, i * narrow, narrow, scratch[i])
            query_w, key_w, value_w = scratch
            biases = vector_sum(pieces, stride, 3 * narrow)
        else:
            query_w, key_w, value_w = pieces[:3]
            biases = pieces[3][...]
        for i in range(parts):
            here = slice(i * share, (i + 1) * share)
            some = tokens[i * rows : (i + 1) * rows]
            own = jnp.concatenate([t[:block, :] for t in some], axis=0)
            if i == 0:
                scaled = (dot(own, query_w[...]) + biases[0:1, :]).astype(BF16) * BF16(HEAD_DIM**-0.5)
            key = dot(own, key_w[...]).astype(BF16)
            found = (dot(own, value_w[...]) + biases[1:2, :]).astype(BF16)
            for side in range(2):
                columns = slice(side * half, (side + 1) * half)
                if i == 0:
                    query[side][...] = scaled[:, columns]
                    query_t[side][...] = scaled[:, columns].T
                keys[side][here, :] = key[:, columns]
                values[side][here, :] = found[:, columns]
                value_t[side][:, here] = found[:, columns].T
        for i, t in enumerate(tokens):
            memory[i * memory_block : (i + 1) * memory_block, :] = t[block : block + memory_block, :]
            found = t[block + memory_block : block + memory_block + 8, :].astype(F32).astype(jnp.int32)
            ids[:, i * block : (i + 1) * block] = found[0:1, :block]
        found = [t[block + memory_block : block + memory_block + 8, :].astype(F32).astype(jnp.int32)[1:2, :memory_block] for t in tokens]
        memory_ids[...] = jnp.concatenate(found, axis=1)

    outs = [((share, half), BF16)] * 2 + [((half, share), BF16)] * 2
    outs += [((length, half), BF16)] * 4 + [((half, length), BF16)] * 2
    outs += [
        ((parts * memory_share, width), BF16),
        ((1, length), jnp.int32),
        ((1, parts * memory_share), jnp.int32),
    ]
    return kernel, outs, [((width, width), BF16)] * 3 if packed else []


def make_self_attention(share, length, width):
    def kernel(me_ref, *refs):
        query_t, keys, value_t, ids = refs[:2], refs[2:4], refs[4:6], refs[6]
        mixture_t, logs, hot, penalty = refs[7:9], refs[9:11], refs[11], refs[12]
        hot[...] = one_hot(ids[...])
        penalty[...] = penalties(ids[:, :share])
        for side in range(2):
            attend(query_t[side], keys[side], value_t[side], hot, penalty, mixture_t[side], logs[side])

    outs = [((width // 2, share), BF16)] * 2 + [((HEADS // 2, 1, share), F32)] * 2
    return kernel, outs, [((length, PAIR), BF16), ((PAIR, share), BF16)]


def make_cross_forward(packed, rows, block, memory_length, width, narrow, n_pieces):
    share = rows * block
    stride = 5 * narrow + 16

    def kernel(*refs):
        me_ref, refs = refs[0], list(refs[1:])
        pieces, refs = refs[:n_pieces], refs[n_pieces:]
        tokens, refs = refs[:rows], refs[rows:]
        memory, ids, memory_ids, upper, lower = refs[:5]
        first_sum, second_sum, query, memory_keys, memory_values, cross_t, logs, vectors = refs[5:13]
        scratch = refs[13:]
        query_t, value_t, hot, penalty = scratch[:4]
        if packed:
            for i in range(5):
                unpack(me_ref[0], pieces, stride, i * narrow, narrow, scratch[4 + i])
            output_w, query_w, key_w, value_w, source_w = scratch[4:]
            vectors[...] = vector_sum(pieces, stride, 5 * narrow)
        else:
            output_w, query_w, key_w, value_w, source_w = pieces[:5]
            vectors[...] = pieces[5][...]

        def vector(i):
            return vectors[i : i + 1, :]

        own = jnp.concatenate([t[:block, :] for t in tokens], axis=0)
        mixture_t = jnp.concatenate([upper[...], lower[...]], axis=0)
        h = own.astype(F32) + dot_tn(mixture_t, output_w[...]) + vector(OUTPUT_BIAS)
        first_sum[...] = h
        first = normalize(h)[0] * vector(ATTENTION_GAIN) + vector(ATTENTION_SHIFT)
        scaled = (dot(first.astype(BF16), query_w[...]) + vector(SOURCE_QUERY_BIAS)).astype(BF16) * BF16(HEAD_DIM**-0.5)
        query[...] = scaled
        query_t[...] = scaled.T
        memory_keys[...] = dot(memory[...], key_w[...]).astype(BF16)
        memory_values[...] = (dot(memory[...], value_w[...]) + vector(SOURCE_VALUE_BIAS)).astype(BF16)
        value_t[...] = memory_values[...].T
        hot[...] = one_hot(memory_ids[...])
        penalty[...] = penalties(ids[:, :share])
        attend(query_t, memory_keys, value_t, hot, penalty, cross_t, logs)
        first = normalize(first_sum[...])[0] * vector(ATTENTION_GAIN) + vector(ATTENTION_SHIFT)
        second_sum[...] = first + dot_tn(cross_t[...], source_w[...]) + vector(SOURCE_OUTPUT_BIAS)

    outs = [
        ((share, width), F32),
        ((share, width), F32),
        ((share, width), BF16),
        ((memory_length, width), BF16),
        ((memory_length, width), BF16),
        ((width, share), BF16),
        ((HEADS, 1, share), F32),
        ((16, width), F32),
    ]
    scratch = [((width, share), BF16), ((width, memory_length), BF16), ((memory_length, PAIR), BF16), ((PAIR, share), BF16)]
    if packed:
        scratch += [((width, width), BF16)] * 5
    return kernel, outs, scratch


def make_inner(packed, rows, block, width, hidden, narrow, n_pieces):
    blocks = hidden // width
    share = rows * block
    per = width // (blocks * narrow)

    def kernel(*refs):
        me_ref, refs = refs[0], list(refs[1:])
        pieces, refs = refs[:n_pieces], refs[n_pieces:]
        second_sum, cot_own, cot_came, vectors = refs[:4]
        out_own, out_send, back, sums = refs[4:8]
        grads, scratch = refs[8:10], refs[10:]
        low, active, gate, slope = scratch[:4]
        if packed:
            inner_w, outer_w, gathered, dense = scratch[4:8]
            tall = blocks * narrow
            for core, far, slot, device in places(me_ref[0]):
                ref, at = pieces[2 * core + far], slot * 2 * tall
                row = pl.multiple_of(device * narrow, narrow)
                for i in range(blocks):
                    inner_w[i, pl.ds(row, narrow), :] = ref[at + i * narrow : at + (i + 1) * narrow, :]
                row = pl.multiple_of(lax.rem(device, per) * tall, tall)
                outer_w[lax.div(device, per), pl.ds(row, tall), :] = ref[at + tall : at + 2 * tall, :]
        else:
            inner_w, outer_w = pieces

        def vector(i):
            return vectors[i : i + 1, :]

        second = normalize(second_sum[...])[0] * vector(SOURCE_GAIN) + vector(SOURCE_SHIFT)
        low[...] = second.astype(BF16)
        back[...] = second + vector(OUTER_BIAS)

        def forward(i, carry):
            inner = dot(low[...], inner_w[i]) + vectors[pl.ds(INNER_BIAS + i, 1), :]
            chance, density = normal_parts(inner)
            found = (inner * chance).astype(BF16)
            active[i] = found
            gate[i] = chance + inner * density
            back[...] += dot(found, outer_w[i])
            return carry

        lax.fori_loop(0, blocks, forward, 0)
        normed, inverse = normalize(back[...])
        final = normed * vector(FINAL_GAIN) + vector(FINAL_SHIFT)
        out_own[...] = final[:block, :]
        out_send[...] = final[block:, :].astype(BF16)
        upstream = jnp.concatenate([cot_own[-block:, :], cot_came[-block:, :]], axis=0).astype(F32)
        sums[0:1, :] = total(upstream * normed)
        sums[1:2, :] = total(upstream)
        back3 = normalize_back(upstream, normed, inverse, vector(FINAL_GAIN))
        slope[...] = back3.astype(BF16)
        sums[2:3, :] = total(slope[...])
        sums[7:8, :] = jnp.zeros_like(sums[7:8, :])
        back[...] = back3

        def backward(i, carry):
            grad = dot_nt(slope[...], outer_w[i]) * gate[i]
            inner_low = grad.astype(BF16)
            sums[pl.ds(3 + i, 1), :] = total(inner_low)
            outer_grad = dot_tn(active[i], slope[...])
            inner_grad = dot_tn(low[...], inner_low)
            back[...] += dot_nt(inner_low, inner_w[i])
            if packed:
                dense[...] = inner_grad
                gathered[i] = outer_grad.astype(BF16)
                here = pl.ds(pl.multiple_of(i * narrow, narrow), narrow)
                for core, far, slot, device in places(me_ref[0]):
                    row = pl.multiple_of(device * narrow, narrow)
                    grads[core][far * 8 + slot, here, :] = dense[pl.ds(row, narrow), :].astype(BF16)
            else:
                grads[0][i] = inner_grad
                grads[1][i] = outer_grad
            return carry

        lax.fori_loop(0, blocks, backward, 0)
        if packed:
            tall = blocks * narrow
            for core, far, slot, device in places(me_ref[0]):
                row = pl.multiple_of(lax.rem(device, per) * tall, tall)
                grads[core][far * 8 + slot, tall:, :] = gathered[lax.div(device, per), pl.ds(row, tall), :]

    outs = [((block, width), F32), ((block, width), BF16), ((share, width), F32), ((8, width), F32)]
    if packed:
        outs += [((16, 2 * blocks * narrow, width), BF16)] * 2
    else:
        outs += [((blocks, width, width), F32)] * 2
    scratch = [((share, width), BF16), ((blocks, share, width), BF16), ((blocks, share, width), F32), ((share, width), BF16)]
    if packed:
        scratch += [((blocks, width, width), BF16)] * 3 + [((width, width), F32)]
    return kernel, outs, scratch


def make_cross_back(packed, parts, share, memory_share, width, narrow, n_pieces):
    memory_length = parts * memory_share
    stride = 5 * narrow + 16

    def kernel(*refs):
        me_ref, refs = refs[0], list(refs[1:])
        pieces, refs = refs[:n_pieces], refs[n_pieces:]
        (back2_in, first_sum, second_sum, query, memory_keys, memory_values, cross_t, logs, ids,
         memory_ids, vectors, sums_inner) = refs[:12]
        mixtures, refs = refs[12:14], refs[14:]
        back1, key_own, value_own, sums = refs[:4]
        self_slope, self_slope_t, self_deltas = (refs[4 + 2 * i : 6 + 2 * i] for i in range(3))
        sends, refs = refs[10 : 10 + parts - 1], refs[10 + parts - 1 :]
        grads, scratch = refs[:3], refs[3:]
        (slope_t, slope, key_t, hot, penalty, query_t, deltas, query_grad_t, key_grad, value_grad) = scratch[:10]
        upper, lower = mixtures
        if packed:
            for i, at in enumerate((0, 1, 4)):
                unpack(me_ref[0], pieces, stride, at * narrow, narrow, scratch[10 + i])
            output_w, query_w, source_w = scratch[10:13]
        else:
            output_w, query_w, source_w = pieces

        def vector(i):
            return vectors[i : i + 1, :]

        sums[0:7, :] = sums_inner[0:7, :]
        upstream = back2_in[...]
        normed, inverse = normalize(second_sum[...])
        sums[7:8, :] = total(upstream * normed)
        sums[8:9, :] = total(upstream)
        back2 = normalize_back(upstream, normed, inverse, vector(SOURCE_GAIN))
        back1[...] = back2
        cross_low = back2.astype(BF16)
        sums[9:10, :] = total(cross_low)
        grads[0][...] = dot(cross_t[...], cross_low).astype(BF16)
        found = dot_nt(cross_low, source_w[...]).astype(BF16)
        slope[...] = found
        slope_t[...] = found.T
        deltas_of(slope_t, cross_t, deltas)
        query_t[...] = query[...].T
        key_t[...] = memory_keys[...].T
        hot[...] = one_hot(memory_ids[...])
        penalty[...] = penalties(ids[:, :share])
        attend_back(query_t, query, memory_keys, key_t, memory_values, slope_t, slope, hot, penalty,
                    logs, deltas, query_grad_t, key_grad, value_grad)
        key_own[...] = key_grad[:memory_share, :]
        value_own[...] = value_grad[:memory_share, :]
        for i in range(1, parts):
            here = slice(i * memory_share, (i + 1) * memory_share)
            sends[i - 1][:memory_share, :] = key_grad[here, :].astype(BF16)
            sends[i - 1][memory_share:, :] = value_grad[here, :].astype(BF16)
        query_low = query_grad_t[...].T.astype(BF16)
        sums[10:11, :] = total(query_low)
        normed, inverse = normalize(first_sum[...])
        first_low = (normed * vector(ATTENTION_GAIN) + vector(ATTENTION_SHIFT)).astype(BF16)
        grads[1][...] = dot_tn(first_low, query_low).astype(BF16)
        upstream = back1[...] + dot_nt(query_low, query_w[...])
        sums[11:12, :] = total(upstream * normed)
        sums[12:13, :] = total(upstream)
        grad = normalize_back(upstream, normed, inverse, vector(ATTENTION_GAIN))
        back1[...] = grad
        branch_low = grad.astype(BF16)
        sums[13:14, :] = total(branch_low)
        sums[14:16, :] = jnp.zeros_like(sums[14:16, :])
        mixture_t = jnp.concatenate([upper[...], lower[...]], axis=0)
        grads[2][...] = dot(mixture_t, branch_low).astype(BF16)
        found = dot_nt(branch_low, output_w[...]).astype(BF16)
        for side in range(2):
            columns = slice(side * width // 2, (side + 1) * width // 2)
            self_slope[side][...] = found[:, columns]
            self_slope_t[side][...] = found[:, columns].T
            deltas_of(self_slope_t[side], mixtures[side], self_deltas[side])

    half = width // 2
    outs = [
        ((share, width), F32),
        ((memory_share, width), F32),
        ((memory_share, width), F32),
        ((16, width), F32),
    ]
    outs += [((share, half), BF16)] * 2 + [((half, share), BF16)] * 2
    outs += [((HEADS // 2, 1, share), F32)] * 2
    outs += [((2 * memory_share, width), BF16)] * (parts - 1)
    outs += [((width, width), BF16)] * 3
    scratch = [
        ((width, share), BF16),
        ((share, width), BF16),
        ((width, memory_length), BF16),
        ((memory_length, PAIR), BF16),
        ((PAIR, share), BF16),
        ((width, share), BF16),
        ((HEADS, 1, share), F32),
        ((width, share), F32),
        ((memory_length, width), F32),
        ((memory_length, width), F32),
    ]
    if packed:
        scratch += [((width, width), BF16)] * 3
    return kernel, outs, scratch


def attention_back_half(refs, share, scratch):
    query, keys, values, slope, slope_t, logs, deltas, ids = refs
    query_t, key_t, hot, penalty, query_grad_t, key_grad, value_grad = scratch
    query_t[...] = query[...].T
    key_t[...] = keys[...].T
    hot[...] = one_hot(ids[...])
    penalty[...] = penalties(ids[:, :share])
    attend_back(query_t, query, keys, key_t, values, slope_t, slope, hot, penalty, logs, deltas,
                query_grad_t, key_grad, value_grad)


def half_scratch(share, length, half):
    return [
        ((half, share), BF16),
        ((half, length), BF16),
        ((length, PAIR), BF16),
        ((PAIR, share), BF16),
        ((half, share), F32),
        ((length, half), F32),
        ((length, half), F32),
    ]


def give_half(share, scratch, own, sends):
    key_grad, value_grad = scratch[5:7]
    own[:share, :] = key_grad[:share, :]
    own[share:, :] = value_grad[:share, :]
    for i, send in enumerate(sends):
        here = slice((i + 1) * share, (i + 2) * share)
        send[:share, :] = key_grad[here, :].astype(BF16)
        send[share:, :] = value_grad[here, :].astype(BF16)


def make_self_back_upper(packed, parts, rows, block, memory_block, width, narrow, n_pieces):
    share, memory_share = rows * block, rows * memory_block
    length, half = parts * share, width // 2

    def kernel(*refs):
        me_ref, refs = refs[0], list(refs[1:])
        pieces, refs = refs[:n_pieces], refs[n_pieces:]
        tokens, refs = refs[:rows], refs[rows:]
        operands, refs = refs[:8], refs[8:]
        memory_key_own, memory_value_own, sums_in = refs[:3]
        early, refs = refs[3:6], refs[6:]
        memory_received, refs = refs[: parts - 1], refs[parts - 1 :]
        query_grad, own, memory_own, memory_send = refs[:4]
        sends, refs = refs[4 : 4 + parts - 1], refs[4 + parts - 1 :]
        n_grads = 2 if packed else 3
        grad_refs, scratch = refs[:n_grads], refs[n_grads:]
        sums = scratch[7]
        me = me_ref[0]
        if packed:
            for i in range(2):
                unpack(me, pieces, 5 * narrow + 16, (2 + i) * narrow, narrow, scratch[8 + i])
            source_key, source_value = scratch[8:10]
        else:
            source_key, source_value = pieces
        grads = Grads(me, grad_refs, scratch[10] if packed else None, narrow)
        memory = jnp.concatenate([t[block : block + memory_block, :] for t in tokens], axis=0)
        key_sum, value_sum = memory_key_own[...], memory_value_own[...]
        for ref in memory_received:
            key_sum = key_sum + ref[:memory_share, :].astype(F32)
            value_sum = value_sum + ref[memory_share:, :].astype(F32)
        key_low, value_low = key_sum.astype(BF16), value_sum.astype(BF16)
        sums[...] = sums_in[...]
        sums[14:15, :] = total(value_low)
        grads.put_sums(5 * narrow, sums[...])
        grads.put(0, dot_tn(memory, key_low))
        grads.put(1, dot_tn(memory, value_low))
        if packed:
            for i, ref in enumerate(early):
                grads.put(2 + i, ref[...].astype(F32))
        grad = dot_nt(key_low, source_key[...]) + dot_nt(value_low, source_value[...])
        memory_own[...] = grad[:memory_block, :]
        memory_send[...] = grad[memory_block:, :].astype(BF16)
        attention_back_half(operands, share, scratch[:7])
        query_grad[...] = scratch[4][...].T.astype(BF16)
        give_half(share, scratch, own, sends)

    outs = [
        ((share, half), BF16),
        ((2 * share, half), F32),
        ((memory_block, width), F32),
        ((memory_block, width), BF16),
    ]
    outs += [((2 * share, half), BF16)] * (parts - 1)
    if packed:
        outs += [((16, 5 * narrow + 16, width), BF16)] * 2
    else:
        outs += [((width, width), F32)] * 2 + [((16, width), F32)]
    scratch = half_scratch(share, length, half) + [((16, width), F32)]
    if packed:
        scratch += [((width, width), BF16)] * 2 + [((width, width), F32)]
    return kernel, outs, scratch


def make_self_back_lower(packed, parts, rows, block, width, narrow, n_pieces):
    share = rows * block
    length, half = parts * share, width // 2

    def kernel(*refs):
        me_ref, refs = refs[0], list(refs[1:])
        pieces, refs = refs[:n_pieces], refs[n_pieces:]
        tokens, refs = refs[:rows], refs[rows:]
        operands, refs = refs[:8], refs[8:]
        back1, query_upper = refs[:2]
        in_part, query_sum, query_w_grad, own = refs[2:6]
        sends, scratch = refs[6 : 6 + parts - 1], refs[6 + parts - 1 :]
        if packed:
            unpack(me_ref[0], pieces, 3 * narrow + 8, 0, narrow, scratch[7])
            query_w = scratch[7]
        else:
            (query_w,) = pieces
        attention_back_half(operands, share, scratch[:7])
        give_half(share, scratch, own, sends)
        query_low = jnp.concatenate([query_upper[...], scratch[4][...].T.astype(BF16)], axis=1)
        tokens_own = jnp.concatenate([t[:block, :] for t in tokens], axis=0)
        in_part[...] = back1[...] + dot_nt(query_low, query_w[...])
        query_sum[...] = jnp.concatenate([total(query_low), jnp.zeros((7, width), F32)], axis=0)
        query_w_grad[...] = dot_tn(tokens_own, query_low).astype(query_w_grad.dtype)

    outs = [
        ((share, width), F32),
        ((8, width), F32),
        ((width, width), BF16 if packed else F32),
        ((2 * share, half), F32),
    ]
    outs += [((2 * share, half), BF16)] * (parts - 1)
    scratch = half_scratch(share, length, half)
    if packed:
        scratch += [((width, width), BF16)]
    return kernel, outs, scratch


def make_last(packed, parts, rows, block, memory_block, width, narrow, n_pieces):
    share = rows * block

    def kernel(*refs):
        me_ref, refs = refs[0], list(refs[1:])
        pieces, refs = refs[:n_pieces], refs[n_pieces:]
        tokens, refs = refs[:rows], refs[rows:]
        in_part, query_sum, query_w_grad, memory_send = refs[:4]
        owns, refs = refs[4:6], refs[6:]
        received = [refs[: parts - 1], refs[parts - 1 : 2 * (parts - 1)]]
        refs = refs[2 * (parts - 1) :]
        in_own, in_send = refs[:2]
        n_grads = 2 if packed else 3
        grad_refs, scratch = refs[2 : 2 + n_grads], refs[2 + n_grads :]
        sums = scratch[0]
        me = me_ref[0]
        if packed:
            for i in range(2):
                unpack(me, pieces, 3 * narrow + 8, (1 + i) * narrow, narrow, scratch[1 + i])
            key_w, value_w = scratch[1:3]
        else:
            key_w, value_w = pieces
        grads = Grads(me, grad_refs, scratch[3] if packed else None, narrow)
        if packed:
            grads.put(2, query_w_grad[...].astype(F32))
        lows = []
        for own, others in zip(owns, received):
            found = own[...]
            for ref in others:
                found = found + ref[...].astype(F32)
            lows.append(found.astype(BF16))
        key_low = jnp.concatenate([low[:share, :] for low in lows], axis=1)
        value_low = jnp.concatenate([low[share:, :] for low in lows], axis=1)
        tokens_own = jnp.concatenate([t[:block, :] for t in tokens], axis=0)
        sums[...] = query_sum[...]
        sums[1:2, :] = total(value_low)
        grads.put_sums(3 * narrow, sums[...])
        grads.put(0, dot_tn(tokens_own, key_low))
        grads.put(1, dot_tn(tokens_own, value_low))
        grad = in_part[...] + dot_nt(key_low, key_w[...]) + dot_nt(value_low, value_w[...])
        in_own[...] = grad[:block, :]
        in_send[:block, :] = grad[block:, :].astype(BF16)
        in_send[block:, :] = memory_send[...]

    outs = [((block, width), F32), ((block + memory_block, width), BF16)]
    if packed:
        outs += [((16, 3 * narrow + 8, width), BF16)] * 2
    else:
        outs += [((width, width), F32)] * 2 + [((8, width), F32)]
    scratch = [((8, width), F32)]
    if packed:
        scratch += [((width, width), BF16)] * 2 + [((width, width), F32)]
    return kernel, outs, scratch


def combine(arrays, splits):
    count = arrays[0].shape[0] // splits
    shape = (count,) + arrays[0].shape[1:]

    def kernel(*refs):
        given, outs = refs[: len(arrays)], refs[len(arrays) :]
        for i, out in enumerate(outs):
            here = slice(i * count, (i + 1) * count)
            found = given[0][here].astype(F32)
            for ref in given[1:]:
                found = found + ref[here].astype(F32)
            out[...] = found.astype(out.dtype)

    return pl.pallas_call(
        kernel,
        out_shape=[jax.ShapeDtypeStruct(shape, BF16)] * splits,
        in_specs=[VM] * len(arrays),
        out_specs=[VM] * splits,
        compiler_params=pltpu.CompilerParams(vmem_limit_bytes=20 << 20),
        cost_estimate=pl.CostEstimate(flops=2 << 30, bytes_accessed=0, transcendentals=0),
        name="combine",
    )(*arrays)


def chosen(me, rows, wide):
    width = rows.shape[1]
    line = lax.broadcasted_iota(jnp.int32, (width, wide), 0)
    here = lax.broadcasted_iota(jnp.int32, (width, wide), 1) + me * wide
    choice = jnp.where(line == here, 1.0, 0.0)
    return lax.dot_general(rows, choice, (((1,), (0,)), ((), ())), precision=lax.Precision.HIGHEST, preferred_element_type=F32)


def reduce_all(array, devices):
    mask = 1
    while mask < devices:
        array = array + swap(array, mask, devices)
        mask *= 2
    return array


def per_device(
    tokens, memory, target_ids, source_ids, cotangent,
    query_weight, key_weight, value_weight, output_weight, query_bias, value_bias, output_bias,
    attention_gain, attention_shift,
    source_query, source_key, source_value, source_output, source_query_bias, source_value_bias,
    source_output_bias, source_gain, source_shift,
    inner_weight, inner_bias, outer_weight, outer_bias, final_gain, final_shift,
    *, devices, sequence,
):
    packed = devices == 32
    rows, block, width = tokens.shape
    memory_block = memory.shape[1]
    parts = sequence // rows
    share, memory_share = rows * block, rows * memory_block
    hidden = inner_weight.shape[1]
    blocks = hidden // width
    me = lax.axis_index(AXES)
    me_array = me.reshape(1).astype(jnp.int32)
    turn = lax.rem(lax.div(me, parts), rows)
    narrow, wide = width // devices, hidden // devices

    def run(made, micros, name, *args):
        kernel, outs, *scratch = made
        return call(kernel, outs, (me_array,) + args, scratch[0] if scratch else [], micros, name)

    turn_array = turn.reshape(1).astype(jnp.int32)

    def turned(made, name, *args):
        kernel, outs = made
        return call(kernel, outs, (turn_array,) + args, [], 1.0, name)

    short = jnp.stack([query_bias, value_bias, output_bias, attention_gain, attention_shift,
                       source_query_bias, source_value_bias, source_output_bias, source_gain,
                       source_shift, outer_bias, final_gain, final_shift])

    def whole(array):
        return lax.all_gather(array, AXES, axis=0, tiled=True)

    sent, kept = turned(
        make_tokens_packet(block, memory_block, width), "tokens_packet", tokens, memory,
        target_ids, source_ids, cotangent,
    )
    came = swap(sent, parts, devices)
    row_tokens = [kept, came]
    kept_swaps = [swap(kept, m, devices) for m in range(1, parts)]
    came_swaps = [swap(came, m, devices) for m in range(1, parts)]
    for pair in zip(kept_swaps, came_swaps):
        row_tokens += pair
    own_tokens = row_tokens[:rows]

    if packed:
        first, second, third = run(make_weights_packet(narrow, width, blocks), 1.0, "weights_packet",
                                   query_weight, key_weight, value_weight, output_weight,
                                   source_query, source_key, source_value, source_output,
                                   inner_weight, outer_weight, short, inner_bias.reshape(1, wide))
        first = after(first, sent)
        first = join([first, turned_swap(first, 0)])
        first_b = turned_swap(first, 1)
        second = after(second, first)
        second_b = turned_swap(second, 0)
        first = join(after([first, first_b], second_b))
        second = join([second, second_b])
        third = after(third, second)
        first_b, second_b, third_b = turned_swap(first, 2), turned_swap(second, 1), turned_swap(third, 0)
        first_c = join(after([first, first_b], second_b, third_b, came, *kept_swaps))
        second, third = join([second, second_b]), join([third, third_b])
        first_d, second_b, third_b = turned_swap(first_c, 3), turned_swap(second, 2), turned_swap(third, 1)
        second_c, third = join([second, second_b]), join([third, third_b])
        first_d = after(first_d, second_c, third, *came_swaps)
        second_d, third_b = turned_swap(second_c, 3), turned_swap(third, 2)
        set_self = [first_c, first_d, swap(first_c, 1, 32), swap(first_d, 1, 32)]
    else:
        full = [whole(w) for w in (query_weight, key_weight, value_weight, output_weight, source_query, source_key, source_value, source_output)]
        lane = lax.broadcasted_iota(jnp.int32, (1, width), 1)
        place = lax.broadcasted_iota(jnp.int32, (blocks, width), 0) * width + lane
        spread_wide = jnp.where(place // wide == me, jnp.tile(inner_bias.reshape(1, wide), (blocks, width // wide)), 0)

        def natural(rows):
            return jnp.where(lane // narrow == me, jnp.tile(rows, (1, devices)), 0)

        vectors = jnp.concatenate([natural(short[:2]), jnp.zeros((6, width), BF16), natural(short[2:]), spread_wide, jnp.zeros((1, width), BF16)])
        vectors = reduce_all(vectors, devices).astype(F32)
        set_self = full[:3] + [vectors[:8]]
        set_cross = full[3:] + [vectors[8:]]
        set_inner = [
            whole(inner_weight).reshape(width, blocks, width).transpose(1, 0, 2),
            whole(outer_weight).reshape(blocks, width, width),
        ]
    found = run(
        make_project(packed, parts, rows, block, memory_block, width, narrow, len(set_self)), 5.0,
        "project", *set_self, *row_tokens,
    )
    query, query_t, keys, values, value_t = (found[2 * i : 2 * i + 2] for i in range(5))
    row_memory, ids, memory_ids = found[10:]
    query_t = list(query_t)
    if packed:
        third_c = join(after([third, third_b], query_t[0]))
        third_d = turned_swap(third_c, 3)
        second_d = after(second_d, query_t[0])
        set_cross = [second_c, second_d, swap(second_c, 1, 32), swap(second_d, 1, 32)]
        query_t[0] = after(query_t[0], third_c, second_d)
        set_back, set_query, set_last, set_memory = set_cross, set_self, set_self, set_cross
    else:
        set_back, set_query, set_last, set_memory = [full[3], full[4], full[7]], full[:1], full[1:3], full[5:7]
    found = run(
        make_self_attention(share, parts * share, width), 12.0, "self_attention",
        *query_t, *keys, *value_t, ids,
    )
    mixtures, logs = found[:2], found[2:]
    if packed:
        third_d = after(third_d, mixtures[0])
        set_inner = [third_c, third_d, swap(third_c, 1, 32), swap(third_d, 1, 32)]
        mixtures = [after(mixtures[0], third_d), mixtures[1]]
    first_sum, second_sum, cross_query, memory_keys, memory_values, cross_t, cross_logs, vectors = run(
        make_cross_forward(packed, rows, block, parts * memory_share, width, narrow, len(set_cross)),
        9.0, "cross_forward", *set_cross, *own_tokens, row_memory, ids, memory_ids, *mixtures,
    )
    out_own, out_send, back2_in, sums_inner, *grads_inner = run(
        make_inner(packed, rows, block, width, hidden, narrow, len(set_inner)), 18.0, "inner",
        *set_inner, second_sum, kept, came, vectors,
    )
    out_came = swap(out_send, parts, devices)
    found = run(
        make_cross_back(packed, parts, share, memory_share, width, narrow, len(set_back)), 14.0,
        "cross_back", *set_back, back2_in, first_sum, second_sum, cross_query, memory_keys,
        memory_values, cross_t, cross_logs, ids, memory_ids, vectors, sums_inner, *mixtures,
    )
    back1, memory_key_own, memory_value_own, sums_cross = found[:4]
    slope, slope_t, deltas = (found[4 + 2 * i : 6 + 2 * i] for i in range(3))
    memory_received = [swap(a, m + 1, devices) for m, a in enumerate(found[10 : 10 + parts - 1])]
    grads_early = found[10 + parts - 1 :]
    query = list(query)
    if packed:
        keep, send = combine([grads_inner[0], swap(grads_inner[1], 1, 32)], 2)
        query[0] = after(query[0], keep, out_came)
        inner_step = [keep, turned_swap(send, 3)]
    found = run(
        make_self_back_upper(packed, parts, rows, block, memory_block, width, narrow, len(set_memory)),
        12.0, "self_back_upper", *set_memory, *own_tokens, query[0], keys[0], values[0], slope[0],
        slope_t[0], logs[0], deltas[0], ids, memory_key_own, memory_value_own, sums_cross,
        *grads_early, *memory_received,
    )
    query_upper, own_upper, memory_own, memory_send = found[:4]
    received_upper = [swap(a, m + 1, devices) for m, a in enumerate(found[4 : 4 + parts - 1])]
    grads_cross = found[4 + parts - 1 :]
    if packed:
        keep, send = combine(inner_step, 2)
        inner_step = [keep, turned_swap(send, 2)]
        query[1] = after(query[1], keep)
    in_part, query_sum, query_w_grad, own_lower, *sends = run(
        make_self_back_lower(packed, parts, rows, block, width, narrow, len(set_query)), 11.0,
        "self_back_lower", *set_query, *own_tokens, query[1], keys[1], values[1], slope[1],
        slope_t[1], logs[1], deltas[1], ids, back1, query_upper,
    )
    received_lower = [swap(a, m + 1, devices) for m, a in enumerate(sends)]
    if packed:
        keep, send = combine(inner_step, 2)
        inner_step = [keep, turned_swap(send, 1)]
        keep_cross, send = combine([grads_cross[0], swap(grads_cross[1], 1, 32)], 2)
        cross_step = [keep_cross, turned_swap(send, 3)]
        in_part = after(in_part, keep, keep_cross)
    in_own, in_send, *grads_last = run(
        make_last(packed, parts, rows, block, memory_block, width, narrow, len(set_last)), 6.0,
        "last", *set_last, *own_tokens, in_part, query_sum, query_w_grad, memory_send, own_upper,
        own_lower, *received_upper, *received_lower,
    )

    if packed:
        keep_inner, send = combine(inner_step, 2)
        inner_step = [keep_inner, turned_swap(send, 0)]
        keep_cross, send = combine(cross_step, 2)
        cross_step = [keep_cross, turned_swap(send, 2)]
        keep, send = combine(after([grads_last[0], swap(grads_last[1], 1, 32)], keep_inner, keep_cross), 2)
        last_step = [keep, turned_swap(send, 3)]
        in_send = after(in_send, last_step[1])
        keep_cross, send = combine(cross_step, 2)
        cross_step = [keep_cross, turned_swap(send, 1)]
        keep, send = combine(after(last_step, keep_cross), 2)
        last_step = [keep, turned_swap(send, 2)]
        keep_cross, send = combine(cross_step, 2)
        cross_step = [keep_cross, turned_swap(send, 0)]
        keep, send = combine(after(last_step, keep_cross), 2)
        last_step = [keep, turned_swap(send, 1)]
        keep, send = combine(last_step, 2)
        last_step = [keep, turned_swap(send, 0)]

        def plan(me_ref, *refs):
            me = me_ref[0]
            steps, outs = [refs[:2], refs[2:4], refs[4:6]], refs[6:]
            inner, cross, last = (sum(r[0].astype(F32) for r in given) for given in steps)
            for i in range(blocks):
                outs[0][:, i * width : (i + 1) * width] = inner[i * narrow : (i + 1) * narrow, :]
            outs[1][...] = inner[blocks * narrow :, :]
            for i in range(5):
                outs[2 + i][...] = cross[i * narrow : (i + 1) * narrow, :]
            for i in range(3):
                outs[7 + i][...] = last[i * narrow : (i + 1) * narrow, :]
            rows_in = jnp.concatenate([cross[5 * narrow :, :], last[3 * narrow :, :]], axis=0)
            outs[10][...] = chosen(me, rows_in, narrow)
            per = width // wide
            line = lax.broadcasted_iota(jnp.int32, (blocks, width), 0)
            row = jnp.sum(jnp.where(line == lax.div(me, per), rows_in[3 : 3 + blocks, :], 0.0), axis=0, keepdims=True)
            outs[11][...] = chosen(lax.rem(me, per), row, wide)

        part = (narrow, width)
        shapes = [(narrow, hidden), (wide, width)] + [part] * 8 + [(24, narrow), (1, wide)]
        (inner_share, outer_share, source_key_share, source_value_share, source_output_share,
         source_query_share, output_share, key_share, value_share, query_share, sums,
         inner_bias_share) = call(
            plan, [(s, F32) for s in shapes], (me_array, *inner_step, *cross_step, *last_step), [], 2.0,
            "finish",
        )
        inner_bias_share = inner_bias_share.reshape(wide)
    else:
        def scatter(array):
            return lax.psum_scatter(array, AXES, scatter_dimension=0, tiled=True)

        inner_share = scatter(grads_inner[0].transpose(1, 0, 2).reshape(width, hidden))
        outer_share = scatter(grads_inner[1].reshape(hidden, width))
        source_output_share, source_query_share, output_share = (scatter(g.astype(F32)) for g in grads_early)
        source_key_share, source_value_share = (scatter(g) for g in grads_cross[:2])
        key_share, value_share = (scatter(g) for g in grads_last[:2])
        query_share = scatter(query_w_grad)
        sums = reduce_all(jnp.concatenate([grads_cross[2], grads_last[2]], axis=0), devices)
        inner_bias_share = lax.dynamic_slice(sums[3 : 3 + blocks].reshape(hidden), (me * wide,), (wide,))
        sums = lax.dynamic_slice(sums, (0, me * narrow), (sums.shape[0], narrow))
    def regroup(mine, came):
        came = came.astype(F32)
        return jnp.where(turn == 0, jnp.stack([mine, came]), jnp.stack([came, mine]))

    output = regroup(out_own, out_came)
    in_came = swap(in_send, parts, devices)
    input_gradient = regroup(in_own, in_came[:block])
    memory_gradient = regroup(memory_own, in_came[block:])

    return (
        output,
        input_gradient,
        memory_gradient,
        query_share,
        key_share,
        value_share,
        output_share,
        sums[16],
        sums[17],
        sums[13],
        sums[11],
        sums[12],
        source_query_share,
        source_key_share,
        source_value_share,
        source_output_share,
        sums[10],
        sums[14],
        sums[9],
        sums[7],
        sums[8],
        inner_share,
        inner_bias_share,
        outer_share,
        sums[2],
        sums[0],
        sums[1],
    )


def solution(mesh):
    sequence, devices = mesh.shape["seq"], mesh.size
    tokens, ids = P("dp", "seq", None), P("dp", "seq")
    matrix, vector = P(AXES, None), P(AXES)
    attention = (matrix,) * 4 + (vector,) * 5
    inner = (matrix, vector, matrix, vector, vector, vector)
    return jax.shard_map(
        functools.partial(per_device, devices=devices, sequence=sequence),
        mesh=mesh,
        in_specs=(tokens, tokens, ids, ids, tokens) + attention + attention + inner,
        out_specs=(tokens, tokens, tokens) + attention + attention + inner,
        check_vma=False,
    )
```

```python
import functools
import math

import jax
import jax.numpy as jnp
from jax import lax
from jax.experimental import pallas as pl
from jax.experimental.pallas import tpu as pltpu
from jax.sharding import PartitionSpec as P

HEADS = 8
HEAD_DIM = 64
PAIR = 128
EPSILON = 1e-05
MASKED = 1e9
AXES = ("dp", "seq")
F32 = jnp.float32
BF16 = jnp.bfloat16

(
    OUTPUT_BIAS,
    ATTENTION_GAIN,
    ATTENTION_SHIFT,
    SOURCE_QUERY_BIAS,
    SOURCE_VALUE_BIAS,
    SOURCE_OUTPUT_BIAS,
    SOURCE_GAIN,
    SOURCE_SHIFT,
    OUTER_BIAS,
    FINAL_GAIN,
    FINAL_SHIFT,
    INNER_BIAS,
) = range(12)
Z_MASKS = (0, 8, 16, 24)
VM = pl.BlockSpec(memory_space=pltpu.VMEM)
SM = pl.BlockSpec(memory_space=pltpu.SMEM)


def dot(a, b):
    return lax.dot_general(a, b, (((1,), (0,)), ((), ())), preferred_element_type=F32)


def dot_nt(a, b):
    return lax.dot_general(a, b, (((1,), (1,)), ((), ())), preferred_element_type=F32)


def dot_tn(a, b):
    return lax.dot_general(a, b, (((0,), (0,)), ((), ())), preferred_element_type=F32)


def total(values):
    return jnp.sum(values.astype(F32), axis=0, keepdims=True)


def normalize(h):
    average = jnp.mean(h, axis=-1, keepdims=True)
    centered = h - average
    variance = jnp.mean(centered * centered, axis=-1, keepdims=True)
    inverse = lax.rsqrt(variance + EPSILON)
    return centered * inverse, inverse


def normalize_back(upstream, normed, inverse, gain):
    scaled = upstream * gain
    first_mean = jnp.mean(scaled, axis=-1, keepdims=True)
    second_mean = jnp.mean(scaled * normed, axis=-1, keepdims=True)
    return inverse * (scaled - first_mean - normed * second_mean)


def normal_parts(v):
    density = 0.3989422804014327 * jnp.exp(-0.5 * v * v)
    t = 1.0 / (1.0 + 0.2316419 * jnp.abs(v))
    series = t * (
        0.319381530
        + t * (-0.356563782 + t * (1.781477937 + t * (-1.821255978 + t * 1.330274429)))
    )
    tail = density * series
    return jnp.where(v >= 0.0, 1.0 - tail, tail), density


def penalties(ids):
    place = lax.broadcasted_iota(jnp.int32, (PAIR, ids.shape[1]), 0)
    return jnp.where((place == ids) | (place >= 4), 0.0, -MASKED).astype(BF16)


def one_hot(ids):
    place = lax.broadcasted_iota(jnp.int32, (PAIR, ids.shape[1]), 0)
    return jnp.where(place == ids, 1.0, 0.0).astype(F32).T.astype(BF16)


def spread(part, half):
    empty = jnp.zeros_like(part)
    return [part, empty] if half == 0 else [empty, part]


def attend(query_t, keys, value_t, hot, penalty, mixture_t, logs):
    length = keys.shape[0]

    def pair(p, carry):
        columns = pl.ds(pl.multiple_of(p * PAIR, PAIR), PAIR)
        left = jnp.concatenate([keys[:, columns], hot[...]], axis=1)
        for half in range(2):
            rows = pl.ds(pl.multiple_of(p * PAIR + half * HEAD_DIM, HEAD_DIM), HEAD_DIM)
            right = jnp.concatenate(spread(query_t[rows, :], half) + [penalty[...]], axis=0)
            scores = dot(left, right)
            highest = jnp.max(scores, axis=0, keepdims=True)
            weights = jnp.exp(scores - highest).astype(BF16)
            values = jnp.concatenate(
                [value_t[rows, :], jnp.ones((16, length), BF16)], axis=0
            )
            found = dot(values, weights)
            denominator = found[HEAD_DIM : HEAD_DIM + 1, :]
            mixture_t[rows, :] = (found[:HEAD_DIM, :] / denominator).astype(BF16)
            logs[2 * p + half] = highest + jnp.log(denominator)
        return carry

    lax.fori_loop(0, keys.shape[1] // PAIR, pair, 0)


def attend_back(
    query_t, query, keys, key_t, values, slope_t, slope, hot, penalty, logs, deltas,
    query_grad_t, key_grad, value_grad,
):
    tokens = query.shape[0]
    lane = lax.broadcasted_iota(jnp.int32, (tokens, PAIR), 1)

    def pair(p, carry):
        columns = pl.ds(pl.multiple_of(p * PAIR, PAIR), PAIR)
        left = jnp.concatenate([keys[:, columns], hot[...]], axis=1)
        value_pair = values[:, columns]
        key_sum, value_sum = None, None
        for half in range(2):
            rows = pl.ds(pl.multiple_of(p * PAIR + half * HEAD_DIM, HEAD_DIM), HEAD_DIM)
            right = jnp.concatenate(spread(query_t[rows, :], half) + [penalty[...]], axis=0)
            chances = jnp.exp(dot(left, right) - logs[2 * p + half])
            slopes = dot(value_pair, jnp.concatenate(spread(slope_t[rows, :], half), axis=0))
            grads = (chances * (slopes - deltas[2 * p + half])).astype(BF16)
            query_grad_t[rows, :] = dot(key_t[rows, :], grads) * HEAD_DIM**-0.5
            mine = (lane < HEAD_DIM) if half == 0 else (lane >= HEAD_DIM)
            none = jnp.zeros((tokens, PAIR), BF16)
            value_part = dot(chances.astype(BF16), jnp.where(mine, slope[:, columns], none))
            key_part = dot(grads, jnp.where(mine, query[:, columns], none))
            value_sum = value_part if value_sum is None else value_sum + value_part
            key_sum = key_part if key_sum is None else key_sum + key_part
        key_grad[:, columns] = key_sum
        value_grad[:, columns] = value_sum
        return carry

    lax.fori_loop(0, keys.shape[1] // PAIR, pair, 0)


def deltas_of(slope_t, mixture_t, deltas):
    for head in range(slope_t.shape[0] // HEAD_DIM):
        rows = slice(head * HEAD_DIM, (head + 1) * HEAD_DIM)
        deltas[head] = jnp.sum(
            slope_t[rows, :].astype(F32) * mixture_t[rows, :].astype(F32), axis=0, keepdims=True
        )


def swap(array, mask, devices):
    return lax.ppermute(array, AXES, [(i, i ^ mask) for i in range(devices)])


ORDERS = ((8, 16, 2, 4), (16, 8, 4, 2))


def turned_swap(array, step):
    return lax.ppermute(array, AXES, [(i, i ^ ORDERS[i % 2][step]) for i in range(32)])


def after(value, *others):
    return lax.optimization_barrier((value, others))[0]


def places(me):
    found = []
    for core in range(2):
        even = ((me & 1) ^ core) == 0
        masks = [jnp.where(even, first, second) for first, second in zip(*ORDERS)]
        for far in range(2):
            for slot in range(8):
                device = me ^ core if core else me
                for step, bit in enumerate((slot & 1, slot & 2, slot & 4, far)):
                    if bit:
                        device = device ^ masks[step]
                found.append((core, far, slot, device))
    return found


def unpack(me, pieces, stride, first, rows, scratch):
    for core, far, slot, device in places(me):
        ref = pieces[2 * core + far]
        at = slot * stride + first
        scratch[pl.ds(pl.multiple_of(device * rows, rows), rows), :] = ref[at : at + rows, :]


def vector_sum(pieces, stride, first):
    found = None
    for ref in pieces:
        for slot in range(8):
            part = ref[slot * stride + first : (slot + 1) * stride, :].astype(F32)
            found = part if found is None else found + part
    return found


class Grads:
    def __init__(self, me, refs, dense, rows):
        self.me, self.refs, self.dense, self.rows = me, refs, dense, rows

    def put(self, index, grad):
        if self.dense is None:
            self.refs[index][...] = grad
            return
        self.dense[...] = grad
        rows = self.rows
        for core, far, slot, device in places(self.me):
            found = self.dense[pl.ds(pl.multiple_of(device * rows, rows), rows), :]
            self.refs[core][far * 8 + slot, index * rows : (index + 1) * rows, :] = found.astype(BF16)

    def put_sums(self, first, sums):
        if self.dense is None:
            self.refs[-1][...] = sums
            return
        low = sums.astype(BF16)
        for ref in self.refs:
            for slot in range(16):
                ref[slot, first : first + sums.shape[0], :] = low


def grad_outs(packed, count, rows, width, sums):
    if packed:
        return [((16, count * rows + sums, width), BF16)] * 2
    return [((width, width), F32)] * count + [((sums, width), F32)]


def padded(shape, dtype):
    last = -(-shape[-1] // 128) * 128
    tall = -(-shape[-2] // 16) * 16 if len(shape) > 1 else 16
    return math.prod(shape[:-2]) * tall * last * jnp.dtype(dtype).itemsize


def snug(arrays):
    return 2 * sum(padded(a.shape, a.dtype) for a in arrays) + (3 << 20)


def call(kernel, outs, args, scratch, micros, name, room=10):
    moved = sum(math.prod(a.shape) * a.dtype.itemsize for a in args[1:])
    moved += sum(math.prod(s) * jnp.dtype(d).itemsize for s, d in outs)
    need = sum(padded(a.shape, a.dtype) for a in args[1:])
    need += sum(padded(s, d) for s, d in list(outs) + list(scratch))
    return pl.pallas_call(
        kernel,
        out_shape=[jax.ShapeDtypeStruct(s, d) for s, d in outs],
        in_specs=[SM] + [VM] * (len(args) - 1),
        out_specs=[VM] * len(outs),
        scratch_shapes=[pltpu.VMEM(s, d) for s, d in scratch],
        compiler_params=pltpu.CompilerParams(vmem_limit_bytes=min(need + (room << 20), 58 << 20)),
        cost_estimate=pl.CostEstimate(
            flops=int(micros * 1.15e9), bytes_accessed=moved, transcendentals=0
        ),
        name=name,
    )(*args)


def tokens_packet(turn, tokens, memory, target_ids, source_ids, cotangent):
    block, width = tokens.shape[1:]
    memory_block = memory.shape[1]
    first = block + memory_block + 8

    def kernel(turn_ref, targets, sources, tokens_ref, memory_ref, cot_ref, sent, kept, semaphores):
        mine = turn_ref[0]
        copies = []
        for i, (row, out) in enumerate(((1 - mine, sent), (mine, kept))):
            pieces = ((tokens_ref, 0, block), (memory_ref, block, memory_block), (cot_ref, first, block))
            for j, (ref, at, count) in enumerate(pieces):
                copies.append(pltpu.make_async_copy(ref.at[row], out.at[pl.ds(at, count), :], semaphores.at[i, j]))
        for copy in copies:
            copy.start()
        for row, out in ((1 - mine, sent), (mine, kept)):
            ids = targets[pl.ds(row, 1), :].astype(F32)
            ids = jnp.concatenate([ids, jnp.zeros((1, width - block), F32)], axis=1)
            others = sources[pl.ds(row, 1), :].astype(F32)
            others = jnp.concatenate([others, jnp.zeros((1, width - memory_block), F32)], axis=1)
            place = lax.broadcasted_iota(jnp.int32, (8, width), 0)
            found = jnp.where(place == 0, ids, jnp.where(place == 1, others, 0.0))
            out[block + memory_block : first, :] = found.astype(BF16)
        for copy in copies:
            copy.wait()

    anywhere = pl.BlockSpec(memory_space=pl.ANY)
    return pl.pallas_call(
        kernel,
        out_shape=[jax.ShapeDtypeStruct((first + block, width), BF16)] * 2,
        in_specs=[SM, VM, VM, anywhere, anywhere, anywhere],
        out_specs=[VM, VM],
        scratch_shapes=[pltpu.SemaphoreType.DMA((2, 3))],
        compiler_params=pltpu.CompilerParams(vmem_limit_bytes=4 << 20),
        cost_estimate=pl.CostEstimate(flops=1 << 30, bytes_accessed=0, transcendentals=0),
        name="tokens_packet",
    )(turn, target_ids, source_ids, tokens, memory, cotangent)


def placed(me, parts, width):
    here = lax.broadcasted_iota(jnp.int32, (parts.shape[1], width), 0) + me * parts.shape[1]
    lane = lax.broadcasted_iota(jnp.int32, (parts.shape[1], width), 1)
    return dot(parts, jnp.where(lane == here, 1.0, 0.0).astype(BF16))


def make_weights_packet(narrow, width, blocks):
    tall = blocks * narrow

    def kernel(me_ref, *refs):
        weights, inner, outer, short, wide = refs[:8], refs[8], refs[9], refs[10], refs[11]
        first, rest = refs[12:]
        me, middle = me_ref[0], 5 * narrow + 16
        for i, ref in enumerate(weights):
            if i < 3:
                first[i * narrow : (i + 1) * narrow, :] = ref[...]
            else:
                rest[(i - 3) * narrow : (i - 2) * narrow, :] = ref[...]
        found = placed(me, short[...], width)
        first[3 * narrow :, :] = jnp.concatenate([found[:2, :], jnp.zeros((6, width), F32)], axis=0).astype(BF16)
        per = width // wide.shape[1]
        row = placed(lax.rem(me, per), wide[...], width)
        place = lax.broadcasted_iota(jnp.int32, (blocks, width), 0)
        spread_row = jnp.where(place == lax.div(me, per), row, 0.0)
        none = jnp.zeros((16 - (found.shape[0] - 2) - blocks, width), F32)
        rest[5 * narrow : middle, :] = jnp.concatenate([found[2:, :], spread_row, none], axis=0).astype(BF16)
        for i in range(blocks):
            rest[middle + i * narrow : middle + (i + 1) * narrow, :] = inner[:, i * width : (i + 1) * width]
        rest[middle + tall :, :] = outer[...]

    return kernel, [((rows, width), BF16) for rows in (3 * narrow + 8, 5 * narrow + 16 + 2 * tall)]


def make_part(sizes, width):
    tall = sum(sizes)

    def kernel(me_ref, upper, lower, *outs):
        for i in range(4):
            ref, at = (upper, lower)[i // 2], i % 2 * tall
            for size, out in zip(sizes, outs):
                out[i * size : (i + 1) * size, :] = ref[at : at + size, :]
                at += size

    return kernel, [((4 * size, width), BF16) for size in sizes]


def join(arrays):
    def kernel(*refs):
        at = 0
        for ref in refs[:-1]:
            refs[-1][at : at + ref.shape[0], :] = ref[...]
            at += ref.shape[0]

    rows = sum(a.shape[0] for a in arrays)
    return pl.pallas_call(
        kernel,
        out_shape=jax.ShapeDtypeStruct((rows, arrays[0].shape[1]), arrays[0].dtype),
        in_specs=[VM] * len(arrays),
        out_specs=VM,
        compiler_params=pltpu.CompilerParams(vmem_limit_bytes=snug(arrays)),
        cost_estimate=pl.CostEstimate(flops=1 << 20, bytes_accessed=0, transcendentals=0),
        name="join",
    )(*arrays)


def make_project(packed, parts, rows, block, memory_block, width, narrow, n_pieces):
    share = rows * block
    length = parts * share
    memory_share = rows * memory_block
    stride = 3 * narrow + 8
    half = width // 2

    def kernel(*refs):
        me_ref, refs = refs[0], list(refs[1:])
        pieces, refs = refs[:n_pieces], refs[n_pieces:]
        tokens, refs = refs[: parts * rows], refs[parts * rows :]
        query, query_t, keys, values, value_t = (refs[2 * i : 2 * i + 2] for i in range(5))
        memory, ids, memory_ids = refs[10:13]
        scratch = refs[13:]
        me = me_ref[0]
        if packed:
            for i in range(3):
                unpack(me, pieces, stride, i * narrow, narrow, scratch[i])
            query_w, key_w, value_w = scratch
            biases = vector_sum(pieces, stride, 3 * narrow)
        else:
            query_w, key_w, value_w = pieces[:3]
            biases = pieces[3][...]
        for i in range(parts):
            here = slice(i * share, (i + 1) * share)
            some = tokens[i * rows : (i + 1) * rows]
            own = jnp.concatenate([t[:block, :] for t in some], axis=0)
            if i == 0:
                scaled = (dot(own, query_w[...]) + biases[0:1, :]).astype(BF16) * BF16(HEAD_DIM**-0.5)
            key = dot(own, key_w[...]).astype(BF16)
            found = (dot(own, value_w[...]) + biases[1:2, :]).astype(BF16)
            for side in range(2):
                columns = slice(side * half, (side + 1) * half)
                if i == 0:
                    query[side][...] = scaled[:, columns]
                    query_t[side][...] = scaled[:, columns].T
                keys[side][here, :] = key[:, columns]
                values[side][here, :] = found[:, columns]
                value_t[side][:, here] = found[:, columns].T
        for i, t in enumerate(tokens):
            memory[i * memory_block : (i + 1) * memory_block, :] = t[block : block + memory_block, :]
            found = t[block + memory_block : block + memory_block + 8, :].astype(F32).astype(jnp.int32)
            ids[:, i * block : (i + 1) * block] = found[0:1, :block]
        found = [t[block + memory_block : block + memory_block + 8, :].astype(F32).astype(jnp.int32)[1:2, :memory_block] for t in tokens]
        memory_ids[...] = jnp.concatenate(found, axis=1)

    outs = [((share, half), BF16)] * 2 + [((half, share), BF16)] * 2
    outs += [((length, half), BF16)] * 4 + [((half, length), BF16)] * 2
    outs += [
        ((parts * memory_share, width), BF16),
        ((1, length), jnp.int32),
        ((1, parts * memory_share), jnp.int32),
    ]
    return kernel, outs, [((width, width), BF16)] * 3 if packed else []


def make_self_attention(share, length, width):
    def kernel(me_ref, *refs):
        query_t, keys, value_t, ids = refs[:2], refs[2:4], refs[4:6], refs[6]
        mixture_t, logs, hot, penalty = refs[7:9], refs[9:11], refs[11], refs[12]
        hot[...] = one_hot(ids[...])
        penalty[...] = penalties(ids[:, :share])
        for side in range(2):
            attend(query_t[side], keys[side], value_t[side], hot, penalty, mixture_t[side], logs[side])

    outs = [((width // 2, share), BF16)] * 2 + [((HEADS // 2, 1, share), F32)] * 2
    return kernel, outs, [((length, PAIR), BF16), ((PAIR, share), BF16)]


def make_cross_forward(packed, rows, block, memory_length, width, narrow, n_pieces):
    share = rows * block
    stride = 5 * narrow + 16

    def kernel(*refs):
        me_ref, refs = refs[0], list(refs[1:])
        pieces, refs = refs[:n_pieces], refs[n_pieces:]
        tokens, refs = refs[:rows], refs[rows:]
        memory, ids, memory_ids, upper, lower = refs[:5]
        first_sum, second_sum, query, memory_keys, memory_values, cross_t, logs, vectors = refs[5:13]
        scratch = refs[13:]
        query_t, value_t, hot, penalty = scratch[:4]
        if packed:
            for i in range(5):
                unpack(me_ref[0], pieces, stride, i * narrow, narrow, scratch[4 + i])
            output_w, query_w, key_w, value_w, source_w = scratch[4:]
            vectors[...] = vector_sum(pieces, stride, 5 * narrow)
        else:
            output_w, query_w, key_w, value_w, source_w = pieces[:5]
            vectors[...] = pieces[5][...]

        def vector(i):
            return vectors[i : i + 1, :]

        own = jnp.concatenate([t[:block, :] for t in tokens], axis=0)
        mixture_t = jnp.concatenate([upper[...], lower[...]], axis=0)
        h = own.astype(F32) + dot_tn(mixture_t, output_w[...]) + vector(OUTPUT_BIAS)
        first_sum[...] = h
        first = normalize(h)[0] * vector(ATTENTION_GAIN) + vector(ATTENTION_SHIFT)
        scaled = (dot(first.astype(BF16), query_w[...]) + vector(SOURCE_QUERY_BIAS)).astype(BF16) * BF16(HEAD_DIM**-0.5)
        query[...] = scaled
        query_t[...] = scaled.T
        memory_keys[...] = dot(memory[...], key_w[...]).astype(BF16)
        memory_values[...] = (dot(memory[...], value_w[...]) + vector(SOURCE_VALUE_BIAS)).astype(BF16)
        value_t[...] = memory_values[...].T
        hot[...] = one_hot(memory_ids[...])
        penalty[...] = penalties(ids[:, :share])
        attend(query_t, memory_keys, value_t, hot, penalty, cross_t, logs)
        first = normalize(first_sum[...])[0] * vector(ATTENTION_GAIN) + vector(ATTENTION_SHIFT)
        second_sum[...] = first + dot_tn(cross_t[...], source_w[...]) + vector(SOURCE_OUTPUT_BIAS)

    outs = [
        ((share, width), F32),
        ((share, width), F32),
        ((share, width), BF16),
        ((memory_length, width), BF16),
        ((memory_length, width), BF16),
        ((width, share), BF16),
        ((HEADS, 1, share), F32),
        ((16, width), F32),
    ]
    scratch = [((width, share), BF16), ((width, memory_length), BF16), ((memory_length, PAIR), BF16), ((PAIR, share), BF16)]
    if packed:
        scratch += [((width, width), BF16)] * 5
    return kernel, outs, scratch


def make_inner(packed, rows, block, width, hidden, narrow, n_pieces):
    blocks = hidden // width
    share = rows * block
    per = width // (blocks * narrow)

    def kernel(*refs):
        me_ref, refs = refs[0], list(refs[1:])
        pieces, refs = refs[:n_pieces], refs[n_pieces:]
        second_sum, cot_own, cot_came, vectors = refs[:4]
        out_own, out_send, back, sums = refs[4:8]
        grads, scratch = refs[8:10], refs[10:]
        low, active, gate, slope = scratch[:4]
        if packed:
            inner_w, outer_w, gathered, dense = scratch[4:8]
            tall = blocks * narrow
            for core, far, slot, device in places(me_ref[0]):
                ref, at = pieces[2 * core + far], slot * 2 * tall
                row = pl.multiple_of(device * narrow, narrow)
                for i in range(blocks):
                    inner_w[i, pl.ds(row, narrow), :] = ref[at + i * narrow : at + (i + 1) * narrow, :]
                row = pl.multiple_of(lax.rem(device, per) * tall, tall)
                outer_w[lax.div(device, per), pl.ds(row, tall), :] = ref[at + tall : at + 2 * tall, :]
        else:
            inner_w, outer_w = pieces

        def vector(i):
            return vectors[i : i + 1, :]

        second = normalize(second_sum[...])[0] * vector(SOURCE_GAIN) + vector(SOURCE_SHIFT)
        low[...] = second.astype(BF16)
        back[...] = second + vector(OUTER_BIAS)

        def forward(i, carry):
            inner = dot(low[...], inner_w[i]) + vectors[pl.ds(INNER_BIAS + i, 1), :]
            chance, density = normal_parts(inner)
            found = (inner * chance).astype(BF16)
            active[i] = found
            gate[i] = chance + inner * density
            back[...] += dot(found, outer_w[i])
            return carry

        lax.fori_loop(0, blocks, forward, 0)
        normed, inverse = normalize(back[...])
        final = normed * vector(FINAL_GAIN) + vector(FINAL_SHIFT)
        out_own[...] = final[:block, :]
        out_send[...] = final[block:, :].astype(BF16)
        upstream = jnp.concatenate([cot_own[-block:, :], cot_came[-block:, :]], axis=0).astype(F32)
        sums[0:1, :] = total(upstream * normed)
        sums[1:2, :] = total(upstream)
        back3 = normalize_back(upstream, normed, inverse, vector(FINAL_GAIN))
        slope[...] = back3.astype(BF16)
        sums[2:3, :] = total(slope[...])
        sums[7:8, :] = jnp.zeros_like(sums[7:8, :])
        back[...] = back3

        def backward(i, carry):
            grad = dot_nt(slope[...], outer_w[i]) * gate[i]
            inner_low = grad.astype(BF16)
            sums[pl.ds(3 + i, 1), :] = total(inner_low)
            outer_grad = dot_tn(active[i], slope[...])
            inner_grad = dot_tn(low[...], inner_low)
            back[...] += dot_nt(inner_low, inner_w[i])
            if packed:
                dense[...] = inner_grad
                gathered[i] = outer_grad.astype(BF16)
                here = pl.ds(pl.multiple_of(i * narrow, narrow), narrow)
                for core, far, slot, device in places(me_ref[0]):
                    row = pl.multiple_of(device * narrow, narrow)
                    grads[core][far * 8 + slot, here, :] = dense[pl.ds(row, narrow), :].astype(BF16)
            else:
                grads[0][i] = inner_grad
                grads[1][i] = outer_grad
            return carry

        lax.fori_loop(0, blocks, backward, 0)
        if packed:
            tall = blocks * narrow
            for core, far, slot, device in places(me_ref[0]):
                row = pl.multiple_of(lax.rem(device, per) * tall, tall)
                grads[core][far * 8 + slot, tall:, :] = gathered[lax.div(device, per), pl.ds(row, tall), :]

    outs = [((block, width), F32), ((block, width), BF16), ((share, width), F32), ((8, width), F32)]
    if packed:
        outs += [((16, 2 * blocks * narrow, width), BF16)] * 2
    else:
        outs += [((blocks, width, width), F32)] * 2
    scratch = [((share, width), BF16), ((blocks, share, width), BF16), ((blocks, share, width), F32), ((share, width), BF16)]
    if packed:
        scratch += [((blocks, width, width), BF16)] * 3 + [((width, width), F32)]
    return kernel, outs, scratch


def make_cross_back(packed, parts, share, memory_share, width, narrow, n_pieces):
    memory_length = parts * memory_share
    stride = 5 * narrow + 16

    def kernel(*refs):
        me_ref, refs = refs[0], list(refs[1:])
        pieces, refs = refs[:n_pieces], refs[n_pieces:]
        (back2_in, first_sum, second_sum, query, memory_keys, memory_values, cross_t, logs, ids,
         memory_ids, vectors, sums_inner) = refs[:12]
        mixtures, refs = refs[12:14], refs[14:]
        back1, key_own, value_own, sums = refs[:4]
        self_slope, self_slope_t, self_deltas = (refs[4 + 2 * i : 6 + 2 * i] for i in range(3))
        sends, refs = refs[10 : 10 + parts - 1], refs[10 + parts - 1 :]
        grads, scratch = refs[:3], refs[3:]
        (slope_t, slope, key_t, hot, penalty, query_t, deltas, query_grad_t, key_grad, value_grad) = scratch[:10]
        upper, lower = mixtures
        if packed:
            for i, at in enumerate((0, 1, 4)):
                unpack(me_ref[0], pieces, stride, at * narrow, narrow, scratch[10 + i])
            output_w, query_w, source_w = scratch[10:13]
        else:
            output_w, query_w, source_w = pieces

        def vector(i):
            return vectors[i : i + 1, :]

        sums[0:7, :] = sums_inner[0:7, :]
        upstream = back2_in[...]
        normed, inverse = normalize(second_sum[...])
        sums[7:8, :] = total(upstream * normed)
        sums[8:9, :] = total(upstream)
        back2 = normalize_back(upstream, normed, inverse, vector(SOURCE_GAIN))
        back1[...] = back2
        cross_low = back2.astype(BF16)
        sums[9:10, :] = total(cross_low)
        grads[0][...] = dot(cross_t[...], cross_low).astype(BF16)
        found = dot_nt(cross_low, source_w[...]).astype(BF16)
        slope[...] = found
        slope_t[...] = found.T
        deltas_of(slope_t, cross_t, deltas)
        query_t[...] = query[...].T
        key_t[...] = memory_keys[...].T
        hot[...] = one_hot(memory_ids[...])
        penalty[...] = penalties(ids[:, :share])
        attend_back(query_t, query, memory_keys, key_t, memory_values, slope_t, slope, hot, penalty,
                    logs, deltas, query_grad_t, key_grad, value_grad)
        key_own[...] = key_grad[:memory_share, :]
        value_own[...] = value_grad[:memory_share, :]
        for i in range(1, parts):
            here = slice(i * memory_share, (i + 1) * memory_share)
            sends[i - 1][:memory_share, :] = key_grad[here, :].astype(BF16)
            sends[i - 1][memory_share:, :] = value_grad[here, :].astype(BF16)
        query_low = query_grad_t[...].T.astype(BF16)
        sums[10:11, :] = total(query_low)
        normed, inverse = normalize(first_sum[...])
        first_low = (normed * vector(ATTENTION_GAIN) + vector(ATTENTION_SHIFT)).astype(BF16)
        grads[1][...] = dot_tn(first_low, query_low).astype(BF16)
        upstream = back1[...] + dot_nt(query_low, query_w[...])
        sums[11:12, :] = total(upstream * normed)
        sums[12:13, :] = total(upstream)
        grad = normalize_back(upstream, normed, inverse, vector(ATTENTION_GAIN))
        back1[...] = grad
        branch_low = grad.astype(BF16)
        sums[13:14, :] = total(branch_low)
        sums[14:16, :] = jnp.zeros_like(sums[14:16, :])
        mixture_t = jnp.concatenate([upper[...], lower[...]], axis=0)
        grads[2][...] = dot(mixture_t, branch_low).astype(BF16)
        found = dot_nt(branch_low, output_w[...]).astype(BF16)
        for side in range(2):
            columns = slice(side * width // 2, (side + 1) * width // 2)
            self_slope[side][...] = found[:, columns]
            self_slope_t[side][...] = found[:, columns].T
            deltas_of(self_slope_t[side], mixtures[side], self_deltas[side])

    half = width // 2
    outs = [
        ((share, width), F32),
        ((memory_share, width), F32),
        ((memory_share, width), F32),
        ((16, width), F32),
    ]
    outs += [((share, half), BF16)] * 2 + [((half, share), BF16)] * 2
    outs += [((HEADS // 2, 1, share), F32)] * 2
    outs += [((2 * memory_share, width), BF16)] * (parts - 1)
    outs += [((width, width), BF16)] * 3
    scratch = [
        ((width, share), BF16),
        ((share, width), BF16),
        ((width, memory_length), BF16),
        ((memory_length, PAIR), BF16),
        ((PAIR, share), BF16),
        ((width, share), BF16),
        ((HEADS, 1, share), F32),
        ((width, share), F32),
        ((memory_length, width), F32),
        ((memory_length, width), F32),
    ]
    if packed:
        scratch += [((width, width), BF16)] * 3
    return kernel, outs, scratch


def attention_back_half(refs, share, scratch):
    query, keys, values, slope, slope_t, logs, deltas, ids = refs
    query_t, key_t, hot, penalty, query_grad_t, key_grad, value_grad = scratch
    query_t[...] = query[...].T
    key_t[...] = keys[...].T
    hot[...] = one_hot(ids[...])
    penalty[...] = penalties(ids[:, :share])
    attend_back(query_t, query, keys, key_t, values, slope_t, slope, hot, penalty, logs, deltas,
                query_grad_t, key_grad, value_grad)


def half_scratch(share, length, half):
    return [
        ((half, share), BF16),
        ((half, length), BF16),
        ((length, PAIR), BF16),
        ((PAIR, share), BF16),
        ((half, share), F32),
        ((length, half), F32),
        ((length, half), F32),
    ]


def give_half(share, scratch, own, sends):
    key_grad, value_grad = scratch[5:7]
    own[:share, :] = key_grad[:share, :]
    own[share:, :] = value_grad[:share, :]
    for i, send in enumerate(sends):
        here = slice((i + 1) * share, (i + 2) * share)
        send[:share, :] = key_grad[here, :].astype(BF16)
        send[share:, :] = value_grad[here, :].astype(BF16)


def make_memory_back(packed, parts, rows, block, memory_block, width, narrow, n_pieces):
    memory_share = rows * memory_block

    def kernel(*refs):
        me_ref, refs = refs[0], list(refs[1:])
        pieces, refs = refs[:n_pieces], refs[n_pieces:]
        tokens, refs = refs[:rows], refs[rows:]
        memory_key_own, memory_value_own, sums_in = refs[:3]
        early, refs = refs[3:6], refs[6:]
        memory_received, refs = refs[: parts - 1], refs[parts - 1 :]
        memory_own, memory_send = refs[:2]
        n_grads = 2 if packed else 3
        grad_refs, scratch = refs[2 : 2 + n_grads], refs[2 + n_grads :]
        sums = scratch[0]
        me = me_ref[0]
        if packed:
            for i in range(2):
                unpack(me, pieces, 5 * narrow + 16, (2 + i) * narrow, narrow, scratch[1 + i])
            source_key, source_value = scratch[1:3]
        else:
            source_key, source_value = pieces
        grads = Grads(me, grad_refs, scratch[3] if packed else None, narrow)
        memory = jnp.concatenate([t[block : block + memory_block, :] for t in tokens], axis=0)
        key_sum, value_sum = memory_key_own[...], memory_value_own[...]
        for ref in memory_received:
            key_sum = key_sum + ref[:memory_share, :].astype(F32)
            value_sum = value_sum + ref[memory_share:, :].astype(F32)
        key_low, value_low = key_sum.astype(BF16), value_sum.astype(BF16)
        sums[...] = sums_in[...]
        sums[14:15, :] = total(value_low)
        grads.put_sums(5 * narrow, sums[...])
        grads.put(0, dot_tn(memory, key_low))
        grads.put(1, dot_tn(memory, value_low))
        if packed:
            for i, ref in enumerate(early):
                grads.put(2 + i, ref[...].astype(F32))
        grad = dot_nt(key_low, source_key[...]) + dot_nt(value_low, source_value[...])
        memory_own[...] = grad[:memory_block, :]
        memory_send[...] = grad[memory_block:, :].astype(BF16)

    outs = [((memory_block, width), F32), ((memory_block, width), BF16)]
    if packed:
        outs += [((16, 5 * narrow + 16, width), BF16)] * 2
    else:
        outs += [((width, width), F32)] * 2 + [((16, width), F32)]
    scratch = [((16, width), F32)]
    if packed:
        scratch += [((width, width), BF16)] * 2 + [((width, width), F32)]
    return kernel, outs, scratch


def make_self_back_upper(parts, share, width):
    length, half = parts * share, width // 2

    def kernel(*refs):
        operands, (query_grad, own), refs = refs[1:9], refs[9:11], refs[11:]
        sends, scratch = refs[: parts - 1], refs[parts - 1 :]
        attention_back_half(operands, share, scratch)
        query_grad[...] = scratch[4][...].T.astype(BF16)
        give_half(share, scratch, own, sends)

    outs = [((share, half), BF16), ((2 * share, half), F32)] + [((2 * share, half), BF16)] * (parts - 1)
    return kernel, outs, half_scratch(share, length, half)


def make_self_back_lower(packed, parts, rows, block, width, narrow, n_pieces):
    share = rows * block
    length, half = parts * share, width // 2

    def kernel(*refs):
        me_ref, refs = refs[0], list(refs[1:])
        pieces, refs = refs[:n_pieces], refs[n_pieces:]
        tokens, refs = refs[:rows], refs[rows:]
        operands, refs = refs[:8], refs[8:]
        back1, query_upper = refs[:2]
        in_part, query_sum, query_w_grad, own = refs[2:6]
        sends, scratch = refs[6 : 6 + parts - 1], refs[6 + parts - 1 :]
        if packed:
            unpack(me_ref[0], pieces, 3 * narrow + 8, 0, narrow, scratch[7])
            query_w = scratch[7]
        else:
            (query_w,) = pieces
        attention_back_half(operands, share, scratch[:7])
        give_half(share, scratch, own, sends)
        query_low = jnp.concatenate([query_upper[...], scratch[4][...].T.astype(BF16)], axis=1)
        tokens_own = jnp.concatenate([t[:block, :] for t in tokens], axis=0)
        in_part[...] = back1[...] + dot_nt(query_low, query_w[...])
        query_sum[...] = jnp.concatenate([total(query_low), jnp.zeros((7, width), F32)], axis=0)
        query_w_grad[...] = dot_tn(tokens_own, query_low).astype(query_w_grad.dtype)

    outs = [
        ((share, width), F32),
        ((8, width), F32),
        ((width, width), BF16 if packed else F32),
        ((2 * share, half), F32),
    ]
    outs += [((2 * share, half), BF16)] * (parts - 1)
    scratch = half_scratch(share, length, half)
    if packed:
        scratch += [((width, width), BF16)]
    return kernel, outs, scratch


def make_last(packed, parts, rows, block, memory_block, width, narrow, n_pieces):
    share = rows * block

    def kernel(*refs):
        me_ref, refs = refs[0], list(refs[1:])
        pieces, refs = refs[:n_pieces], refs[n_pieces:]
        tokens, refs = refs[:rows], refs[rows:]
        in_part, query_sum, query_w_grad, memory_send = refs[:4]
        owns, refs = refs[4:6], refs[6:]
        received = [refs[: parts - 1], refs[parts - 1 : 2 * (parts - 1)]]
        refs = refs[2 * (parts - 1) :]
        in_own, in_send = refs[:2]
        n_grads = 2 if packed else 3
        grad_refs, scratch = refs[2 : 2 + n_grads], refs[2 + n_grads :]
        sums = scratch[0]
        me = me_ref[0]
        if packed:
            for i in range(2):
                unpack(me, pieces, 3 * narrow + 8, (1 + i) * narrow, narrow, scratch[1 + i])
            key_w, value_w = scratch[1:3]
        else:
            key_w, value_w = pieces
        grads = Grads(me, grad_refs, scratch[3] if packed else None, narrow)
        if packed:
            grads.put(2, query_w_grad[...].astype(F32))
        lows = []
        for own, others in zip(owns, received):
            found = own[...]
            for ref in others:
                found = found + ref[...].astype(F32)
            lows.append(found.astype(BF16))
        key_low = jnp.concatenate([low[:share, :] for low in lows], axis=1)
        value_low = jnp.concatenate([low[share:, :] for low in lows], axis=1)
        tokens_own = jnp.concatenate([t[:block, :] for t in tokens], axis=0)
        sums[...] = query_sum[...]
        sums[1:2, :] = total(value_low)
        grads.put_sums(3 * narrow, sums[...])
        grads.put(0, dot_tn(tokens_own, key_low))
        grads.put(1, dot_tn(tokens_own, value_low))
        grad = in_part[...] + dot_nt(key_low, key_w[...]) + dot_nt(value_low, value_w[...])
        in_own[...] = grad[:block, :]
        in_send[:block, :] = grad[block:, :].astype(BF16)
        in_send[block:, :] = memory_send[...]

    outs = [((block, width), F32), ((block + memory_block, width), BF16)]
    if packed:
        outs += [((16, 3 * narrow + 8, width), BF16)] * 2
    else:
        outs += [((width, width), F32)] * 2 + [((8, width), F32)]
    scratch = [((8, width), F32)]
    if packed:
        scratch += [((width, width), BF16)] * 2 + [((width, width), F32)]
    return kernel, outs, scratch


def combine(arrays, splits):
    count = arrays[0].shape[0] // splits
    shape = (count,) + arrays[0].shape[1:]

    def kernel(*refs):
        given, outs = refs[: len(arrays)], refs[len(arrays) :]
        for i, out in enumerate(outs):
            here = slice(i * count, (i + 1) * count)
            found = given[0][here].astype(F32)
            for ref in given[1:]:
                found = found + ref[here].astype(F32)
            out[...] = found.astype(out.dtype)

    return pl.pallas_call(
        kernel,
        out_shape=[jax.ShapeDtypeStruct(shape, BF16)] * splits,
        in_specs=[VM] * len(arrays),
        out_specs=[VM] * splits,
        compiler_params=pltpu.CompilerParams(vmem_limit_bytes=snug(arrays)),
        cost_estimate=pl.CostEstimate(flops=2 << 30, bytes_accessed=0, transcendentals=0),
        name="combine",
    )(*arrays)


def chosen(me, rows, wide):
    width = rows.shape[1]
    line = lax.broadcasted_iota(jnp.int32, (width, wide), 0)
    here = lax.broadcasted_iota(jnp.int32, (width, wide), 1) + me * wide
    choice = jnp.where(line == here, 1.0, 0.0)
    return lax.dot_general(rows, choice, (((1,), (0,)), ((), ())), precision=lax.Precision.HIGHEST, preferred_element_type=F32)


def reduce_all(array, devices):
    mask = 1
    while mask < devices:
        array = array + swap(array, mask, devices)
        mask *= 2
    return array


def per_device(
    tokens, memory, target_ids, source_ids, cotangent,
    query_weight, key_weight, value_weight, output_weight, query_bias, value_bias, output_bias,
    attention_gain, attention_shift,
    source_query, source_key, source_value, source_output, source_query_bias, source_value_bias,
    source_output_bias, source_gain, source_shift,
    inner_weight, inner_bias, outer_weight, outer_bias, final_gain, final_shift,
    *, devices, sequence,
):
    packed = devices == 32
    rows, block, width = tokens.shape
    memory_block = memory.shape[1]
    parts = sequence // rows
    share, memory_share = rows * block, rows * memory_block
    hidden = inner_weight.shape[1]
    blocks = hidden // width
    me = lax.axis_index(AXES)
    me_array = me.reshape(1).astype(jnp.int32)
    turn = lax.rem(lax.div(me, parts), rows)
    narrow, wide = width // devices, hidden // devices

    def run(made, micros, name, *args):
        kernel, outs, *scratch = made
        return call(kernel, outs, (me_array,) + args, scratch[0] if scratch else [], micros, name)

    short = jnp.stack([query_bias, value_bias, output_bias, attention_gain, attention_shift,
                       source_query_bias, source_value_bias, source_output_bias, source_gain,
                       source_shift, outer_bias, final_gain, final_shift])

    def whole(array):
        return lax.all_gather(array, AXES, axis=0, tiled=True)

    sent, kept = tokens_packet(
        turn.reshape(1).astype(jnp.int32), tokens, memory, target_ids, source_ids, cotangent
    )
    came = swap(sent, parts, devices)
    row_tokens = [kept, came]
    kept_swaps = [swap(kept, m, devices) for m in range(1, parts)]
    came_swaps = [swap(came, m, devices) for m in range(1, parts)]
    for pair in zip(kept_swaps, came_swaps):
        row_tokens += pair
    own_tokens = row_tokens[:rows]

    if packed:
        first, rest = run(make_weights_packet(narrow, width, blocks), 1.0, "weights_packet",
                          query_weight, key_weight, value_weight, output_weight, source_query,
                          source_key, source_value, source_output, inner_weight, outer_weight,
                          short, inner_bias.reshape(1, wide))
        first = after(first, sent)
        first = join([first, turned_swap(first, 0)])
        first_b = turned_swap(first, 1)
        rest = after(rest, first)
        rest_b = turned_swap(rest, 0)
        first = join(after([first, first_b], rest_b))
        rest = join(after([rest, rest_b], first_b, came, *kept_swaps))
        first_b, rest_b = turned_swap(first, 2), turned_swap(rest, 1)
        first_c = join(after([first, first_b], rest_b))
        second, third = run(make_part((5 * narrow + 16, 2 * blocks * narrow), width), 1.0, "part", rest, rest_b)
        first_d, second_b, third_b = turned_swap(first_c, 3), turned_swap(second, 2), turned_swap(third, 2)
        second_c, third_c = join([second, second_b]), join([third, third_b])
        first_d = after(first_d, second_c, third_c, *came_swaps)
        second_d, third_d = turned_swap(second_c, 3), turned_swap(third_c, 3)
        set_self = [first_c, first_d, swap(first_c, 1, 32), swap(first_d, 1, 32)]
    else:
        full = [whole(w) for w in (query_weight, key_weight, value_weight, output_weight, source_query, source_key, source_value, source_output)]
        lane = lax.broadcasted_iota(jnp.int32, (1, width), 1)
        place = lax.broadcasted_iota(jnp.int32, (blocks, width), 0) * width + lane
        spread_wide = jnp.where(place // wide == me, jnp.tile(inner_bias.reshape(1, wide), (blocks, width // wide)), 0)

        def natural(rows):
            return jnp.where(lane // narrow == me, jnp.tile(rows, (1, devices)), 0)

        vectors = jnp.concatenate([natural(short[:2]), jnp.zeros((6, width), BF16), natural(short[2:]), spread_wide, jnp.zeros((1, width), BF16)])
        vectors = reduce_all(vectors, devices).astype(F32)
        set_self = full[:3] + [vectors[:8]]
        set_cross = full[3:] + [vectors[8:]]
        set_inner = [
            whole(inner_weight).reshape(width, blocks, width).transpose(1, 0, 2),
            whole(outer_weight).reshape(blocks, width, width),
        ]
    found = run(
        make_project(packed, parts, rows, block, memory_block, width, narrow, len(set_self)), 5.0,
        "project", *set_self, *row_tokens,
    )
    query, query_t, keys, values, value_t = (found[2 * i : 2 * i + 2] for i in range(5))
    row_memory, ids, memory_ids = found[10:]
    query_t = list(query_t)
    if packed:
        set_cross = [second_c, second_d, swap(second_c, 1, 32), swap(second_d, 1, 32)]
        query_t[0] = after(query_t[0], second_d)
        set_back, set_query, set_last, set_memory = set_cross, set_self, set_self, set_cross
    else:
        set_back, set_query, set_last, set_memory = [full[3], full[4], full[7]], full[:1], full[1:3], full[5:7]
    found = run(
        make_self_attention(share, parts * share, width), 12.0, "self_attention",
        *query_t, *keys, *value_t, ids,
    )
    mixtures, logs = found[:2], found[2:]
    if packed:
        third_d = after(third_d, mixtures[0])
        set_inner = [third_c, third_d, swap(third_c, 1, 32), swap(third_d, 1, 32)]
        mixtures = [after(mixtures[0], third_d), mixtures[1]]
    first_sum, second_sum, cross_query, memory_keys, memory_values, cross_t, cross_logs, vectors = run(
        make_cross_forward(packed, rows, block, parts * memory_share, width, narrow, len(set_cross)),
        9.0, "cross_forward", *set_cross, *own_tokens, row_memory, ids, memory_ids, *mixtures,
    )
    out_own, out_send, back2_in, sums_inner, *grads_inner = run(
        make_inner(packed, rows, block, width, hidden, narrow, len(set_inner)), 18.0, "inner",
        *set_inner, second_sum, kept, came, vectors,
    )
    out_came = swap(out_send, parts, devices)
    found = run(
        make_cross_back(packed, parts, share, memory_share, width, narrow, len(set_back)), 14.0,
        "cross_back", *set_back, back2_in, first_sum, second_sum, cross_query, memory_keys,
        memory_values, cross_t, cross_logs, ids, memory_ids, vectors, sums_inner, *mixtures,
    )
    back1, memory_key_own, memory_value_own, sums_cross = found[:4]
    slope, slope_t, deltas = (found[4 + 2 * i : 6 + 2 * i] for i in range(3))
    memory_received = [swap(a, m + 1, devices) for m, a in enumerate(found[10 : 10 + parts - 1])]
    grads_early = found[10 + parts - 1 :]
    query = list(query)
    if packed:
        keep, send = combine([grads_inner[0], swap(grads_inner[1], 1, 32)], 2)
        inner_step = [keep, turned_swap(send, 3)]
        memory_key_own = after(memory_key_own, keep, out_came)
    memory_own, memory_send, *grads_cross = run(
        make_memory_back(packed, parts, rows, block, memory_block, width, narrow, len(set_memory)),
        2.0, "memory_back", *set_memory, *own_tokens, memory_key_own, memory_value_own, sums_cross,
        *grads_early, *memory_received,
    )
    if packed:
        cross_came = swap(grads_cross[1], 1, 32)
        query[0] = after(query[0], grads_cross[0])
    found = run(
        make_self_back_upper(parts, share, width), 7.0, "self_back_upper", query[0], keys[0],
        values[0], slope[0], slope_t[0], logs[0], deltas[0], ids,
    )
    query_upper, own_upper = found[:2]
    received_upper = [swap(a, m + 1, devices) for m, a in enumerate(found[2:])]
    if packed:
        keep, send = combine(inner_step, 2)
        inner_step = [keep, turned_swap(send, 2)]
        keep_cross, send = combine([grads_cross[0], cross_came], 2)
        cross_step = [keep_cross, turned_swap(send, 3)]
        query[1] = after(query[1], keep, keep_cross)
    in_part, query_sum, query_w_grad, own_lower, *sends = run(
        make_self_back_lower(packed, parts, rows, block, width, narrow, len(set_query)), 11.0,
        "self_back_lower", *set_query, *own_tokens, query[1], keys[1], values[1], slope[1],
        slope_t[1], logs[1], deltas[1], ids, back1, query_upper,
    )
    received_lower = [swap(a, m + 1, devices) for m, a in enumerate(sends)]
    if packed:
        keep, send = combine(inner_step, 2)
        inner_step = [keep, turned_swap(send, 1)]
        keep_cross, send = combine(cross_step, 2)
        cross_step = [keep_cross, turned_swap(send, 2)]
        in_part = after(in_part, keep, keep_cross)
    in_own, in_send, *grads_last = run(
        make_last(packed, parts, rows, block, memory_block, width, narrow, len(set_last)), 6.0,
        "last", *set_last, *own_tokens, in_part, query_sum, query_w_grad, memory_send, own_upper,
        own_lower, *received_upper, *received_lower,
    )

    if packed:
        keep, send = combine([grads_last[0], swap(grads_last[1], 1, 32)], 2)
        last_step = [keep, turned_swap(send, 3)]
        in_send = after(in_send, last_step[1])
        keep_inner, send = combine(inner_step, 2)
        inner_step = [keep_inner, turned_swap(send, 0)]
        keep_cross, send = combine(cross_step, 2)
        cross_step = [keep_cross, turned_swap(send, 1)]
        keep, send = combine(after(last_step, keep_inner, keep_cross), 2)
        last_step = [keep, turned_swap(send, 2)]
        keep_cross, send = combine(cross_step, 2)
        cross_step = [keep_cross, turned_swap(send, 0)]
        keep, send = combine(after(last_step, keep_cross), 2)
        last_step = [keep, turned_swap(send, 1)]
        keep, send = combine(last_step, 2)
        last_step = [keep, turned_swap(send, 0)]

        def plan(me_ref, *refs):
            me = me_ref[0]
            steps, outs = [refs[:2], refs[2:4], refs[4:6]], refs[6:]
            inner, cross, last = (sum(r[0].astype(F32) for r in given) for given in steps)
            for i in range(blocks):
                outs[0][:, i * width : (i + 1) * width] = inner[i * narrow : (i + 1) * narrow, :]
            outs[1][...] = inner[blocks * narrow :, :]
            for i in range(5):
                outs[2 + i][...] = cross[i * narrow : (i + 1) * narrow, :]
            for i in range(3):
                outs[7 + i][...] = last[i * narrow : (i + 1) * narrow, :]
            rows_in = jnp.concatenate([cross[5 * narrow :, :], last[3 * narrow :, :]], axis=0)
            outs[10][...] = chosen(me, rows_in, narrow)
            per = width // wide
            line = lax.broadcasted_iota(jnp.int32, (blocks, width), 0)
            row = jnp.sum(jnp.where(line == lax.div(me, per), rows_in[3 : 3 + blocks, :], 0.0), axis=0, keepdims=True)
            outs[11][...] = chosen(lax.rem(me, per), row, wide)

        part = (narrow, width)
        shapes = [(narrow, hidden), (wide, width)] + [part] * 8 + [(24, narrow), (1, wide)]
        (inner_share, outer_share, source_key_share, source_value_share, source_output_share,
         source_query_share, output_share, key_share, value_share, query_share, sums,
         inner_bias_share) = call(
            plan, [(s, F32) for s in shapes], (me_array, *inner_step, *cross_step, *last_step), [], 2.0,
            "finish",
        )
        inner_bias_share = inner_bias_share.reshape(wide)
    else:
        def scatter(array):
            return lax.psum_scatter(array, AXES, scatter_dimension=0, tiled=True)

        inner_share = scatter(grads_inner[0].transpose(1, 0, 2).reshape(width, hidden))
        outer_share = scatter(grads_inner[1].reshape(hidden, width))
        source_output_share, source_query_share, output_share = (scatter(g.astype(F32)) for g in grads_early)
        source_key_share, source_value_share = (scatter(g) for g in grads_cross[:2])
        key_share, value_share = (scatter(g) for g in grads_last[:2])
        query_share = scatter(query_w_grad)
        sums = reduce_all(jnp.concatenate([grads_cross[2], grads_last[2]], axis=0), devices)
        inner_bias_share = lax.dynamic_slice(sums[3 : 3 + blocks].reshape(hidden), (me * wide,), (wide,))
        sums = lax.dynamic_slice(sums, (0, me * narrow), (sums.shape[0], narrow))
    def regroup(mine, came):
        came = came.astype(F32)
        return jnp.where(turn == 0, jnp.stack([mine, came]), jnp.stack([came, mine]))

    output = regroup(out_own, out_came)
    in_came = swap(in_send, parts, devices)
    input_gradient = regroup(in_own, in_came[:block])
    memory_gradient = regroup(memory_own, in_came[block:])

    return (
        output,
        input_gradient,
        memory_gradient,
        query_share,
        key_share,
        value_share,
        output_share,
        sums[16],
        sums[17],
        sums[13],
        sums[11],
        sums[12],
        source_query_share,
        source_key_share,
        source_value_share,
        source_output_share,
        sums[10],
        sums[14],
        sums[9],
        sums[7],
        sums[8],
        inner_share,
        inner_bias_share,
        outer_share,
        sums[2],
        sums[0],
        sums[1],
    )


def solution(mesh):
    sequence, devices = mesh.shape["seq"], mesh.size
    tokens, ids = P("dp", "seq", None), P("dp", "seq")
    matrix, vector = P(AXES, None), P(AXES)
    attention = (matrix,) * 4 + (vector,) * 5
    inner = (matrix, vector, matrix, vector, vector, vector)
    return jax.shard_map(
        functools.partial(per_device, devices=devices, sequence=sequence),
        mesh=mesh,
        in_specs=(tokens, tokens, ids, ids, tokens) + attention + attention + inner,
        out_specs=(tokens, tokens, tokens) + attention + attention + inner,
        check_vma=False,
    )
```

```python
import functools
import math

import jax
import jax.numpy as jnp
from jax import lax
from jax.experimental import pallas as pl
from jax.experimental.pallas import tpu as pltpu
from jax.sharding import PartitionSpec as P

HEADS = 8
HEAD_DIM = 64
PAIR = 128
EPSILON = 1e-05
MASKED = 1e9
AXES = ("dp", "seq")
F32 = jnp.float32
BF16 = jnp.bfloat16

(
    OUTPUT_BIAS,
    ATTENTION_GAIN,
    ATTENTION_SHIFT,
    SOURCE_QUERY_BIAS,
    SOURCE_VALUE_BIAS,
    SOURCE_OUTPUT_BIAS,
    SOURCE_GAIN,
    SOURCE_SHIFT,
    OUTER_BIAS,
    FINAL_GAIN,
    FINAL_SHIFT,
    INNER_BIAS,
) = range(12)
Z_MASKS = (0, 8, 16, 24)
VM = pl.BlockSpec(memory_space=pltpu.VMEM)
SM = pl.BlockSpec(memory_space=pltpu.SMEM)


def dot(a, b):
    return lax.dot_general(a, b, (((1,), (0,)), ((), ())), preferred_element_type=F32)


def dot_nt(a, b):
    return lax.dot_general(a, b, (((1,), (1,)), ((), ())), preferred_element_type=F32)


def dot_tn(a, b):
    return lax.dot_general(a, b, (((0,), (0,)), ((), ())), preferred_element_type=F32)


def total(values):
    return jnp.sum(values.astype(F32), axis=0, keepdims=True)


def normalize(h):
    average = jnp.mean(h, axis=-1, keepdims=True)
    centered = h - average
    variance = jnp.mean(centered * centered, axis=-1, keepdims=True)
    inverse = lax.rsqrt(variance + EPSILON)
    return centered * inverse, inverse


def normalize_back(upstream, normed, inverse, gain):
    scaled = upstream * gain
    first_mean = jnp.mean(scaled, axis=-1, keepdims=True)
    second_mean = jnp.mean(scaled * normed, axis=-1, keepdims=True)
    return inverse * (scaled - first_mean - normed * second_mean)


def normal_parts(v):
    density = 0.3989422804014327 * jnp.exp(-0.5 * v * v)
    t = 1.0 / (1.0 + 0.2316419 * jnp.abs(v))
    series = t * (
        0.319381530
        + t * (-0.356563782 + t * (1.781477937 + t * (-1.821255978 + t * 1.330274429)))
    )
    tail = density * series
    return jnp.where(v >= 0.0, 1.0 - tail, tail), density


def penalties(ids):
    place = lax.broadcasted_iota(jnp.int32, (PAIR, ids.shape[1]), 0)
    return jnp.where((place == ids) | (place >= 4), 0.0, -MASKED).astype(BF16)


def one_hot(ids):
    place = lax.broadcasted_iota(jnp.int32, (PAIR, ids.shape[1]), 0)
    return jnp.where(place == ids, 1.0, 0.0).astype(F32).T.astype(BF16)


def spread(part, half):
    empty = jnp.zeros_like(part)
    return [part, empty] if half == 0 else [empty, part]


def attend(query_t, keys, value_t, hot, penalty, mixture_t, logs):
    length = keys.shape[0]

    def pair(p, carry):
        columns = pl.ds(pl.multiple_of(p * PAIR, PAIR), PAIR)
        left = jnp.concatenate([keys[:, columns], hot[...]], axis=1)
        for half in range(2):
            rows = pl.ds(pl.multiple_of(p * PAIR + half * HEAD_DIM, HEAD_DIM), HEAD_DIM)
            right = jnp.concatenate(spread(query_t[rows, :], half) + [penalty[...]], axis=0)
            scores = dot(left, right)
            highest = jnp.max(scores, axis=0, keepdims=True)
            weights = jnp.exp(scores - highest).astype(BF16)
            values = jnp.concatenate(
                [value_t[rows, :], jnp.ones((16, length), BF16)], axis=0
            )
            found = dot(values, weights)
            denominator = found[HEAD_DIM : HEAD_DIM + 1, :]
            mixture_t[rows, :] = (found[:HEAD_DIM, :] / denominator).astype(BF16)
            logs[2 * p + half] = highest + jnp.log(denominator)
        return carry

    lax.fori_loop(0, keys.shape[1] // PAIR, pair, 0)


def attend_back(
    query_t, query, keys, key_t, values, slope_t, slope, hot, penalty, logs, deltas,
    query_grad_t, key_grad, value_grad,
):
    tokens = query.shape[0]
    lane = lax.broadcasted_iota(jnp.int32, (tokens, PAIR), 1)

    def pair(p, carry):
        columns = pl.ds(pl.multiple_of(p * PAIR, PAIR), PAIR)
        left = jnp.concatenate([keys[:, columns], hot[...]], axis=1)
        value_pair = values[:, columns]
        key_sum, value_sum = None, None
        for half in range(2):
            rows = pl.ds(pl.multiple_of(p * PAIR + half * HEAD_DIM, HEAD_DIM), HEAD_DIM)
            right = jnp.concatenate(spread(query_t[rows, :], half) + [penalty[...]], axis=0)
            chances = jnp.exp(dot(left, right) - logs[2 * p + half])
            slopes = dot(value_pair, jnp.concatenate(spread(slope_t[rows, :], half), axis=0))
            grads = (chances * (slopes - deltas[2 * p + half])).astype(BF16)
            query_grad_t[rows, :] = dot(key_t[rows, :], grads) * HEAD_DIM**-0.5
            mine = (lane < HEAD_DIM) if half == 0 else (lane >= HEAD_DIM)
            none = jnp.zeros((tokens, PAIR), BF16)
            value_part = dot(chances.astype(BF16), jnp.where(mine, slope[:, columns], none))
            key_part = dot(grads, jnp.where(mine, query[:, columns], none))
            value_sum = value_part if value_sum is None else value_sum + value_part
            key_sum = key_part if key_sum is None else key_sum + key_part
        key_grad[:, columns] = key_sum
        value_grad[:, columns] = value_sum
        return carry

    lax.fori_loop(0, keys.shape[1] // PAIR, pair, 0)


def deltas_of(slope_t, mixture_t, deltas):
    for head in range(slope_t.shape[0] // HEAD_DIM):
        rows = slice(head * HEAD_DIM, (head + 1) * HEAD_DIM)
        deltas[head] = jnp.sum(
            slope_t[rows, :].astype(F32) * mixture_t[rows, :].astype(F32), axis=0, keepdims=True
        )


def swap(array, mask, devices):
    return lax.ppermute(array, AXES, [(i, i ^ mask) for i in range(devices)])


Z_FIRST = ((8, 16, 2, 4), (16, 8, 4, 2))
Z_LAST = ((2, 4, 8, 16), (4, 2, 16, 8))


def turned_swap(array, step, orders=Z_FIRST):
    return lax.ppermute(array, AXES, [(i, i ^ orders[i % 2][step]) for i in range(32)])


def after(value, *others):
    return lax.optimization_barrier((value, others))[0]


def places(me, orders=Z_FIRST):
    found = []
    for core in range(2):
        even = ((me & 1) ^ core) == 0
        masks = [jnp.where(even, first, second) for first, second in zip(*orders)]
        for far in range(2):
            for slot in range(8):
                device = me ^ core if core else me
                for step, bit in enumerate((slot & 1, slot & 2, slot & 4, far)):
                    if bit:
                        device = device ^ masks[step]
                found.append((core, far, slot, device))
    return found


def unpack(me, pieces, stride, first, rows, scratch, orders=Z_FIRST):
    for core, far, slot, device in places(me, orders):
        ref = pieces[2 * core + far]
        at = slot * stride + first
        scratch[pl.ds(pl.multiple_of(device * rows, rows), rows), :] = ref[at : at + rows, :]


def vector_sum(pieces, stride, first):
    found = None
    for ref in pieces:
        for slot in range(8):
            part = ref[slot * stride + first : (slot + 1) * stride, :].astype(F32)
            found = part if found is None else found + part
    return found


class Grads:
    def __init__(self, me, refs, dense, rows, orders=Z_FIRST):
        self.me, self.refs, self.dense, self.rows, self.orders = me, refs, dense, rows, orders

    def put(self, index, grad):
        if self.dense is None:
            self.refs[index][...] = grad
            return
        self.dense[...] = grad
        rows = self.rows
        for core, far, slot, device in places(self.me, self.orders):
            found = self.dense[pl.ds(pl.multiple_of(device * rows, rows), rows), :]
            self.refs[core][far * 8 + slot, index * rows : (index + 1) * rows, :] = found.astype(BF16)

    def put_sums(self, first, sums):
        if self.dense is None:
            self.refs[-1][...] = sums
            return
        low = sums.astype(BF16)
        for ref in self.refs:
            for slot in range(16):
                ref[slot, first : first + sums.shape[0], :] = low


def grad_outs(packed, count, rows, width, sums):
    if packed:
        return [((16, count * rows + sums, width), BF16)] * 2
    return [((width, width), F32)] * count + [((sums, width), F32)]


def padded(shape, dtype):
    last = -(-shape[-1] // 128) * 128
    tall = -(-shape[-2] // 16) * 16 if len(shape) > 1 else 16
    return math.prod(shape[:-2]) * tall * last * jnp.dtype(dtype).itemsize


def snug(arrays):
    return 2 * sum(padded(a.shape, a.dtype) for a in arrays) + (3 << 20)


def call(kernel, outs, args, scratch, micros, name, room=10):
    moved = sum(math.prod(a.shape) * a.dtype.itemsize for a in args[1:])
    moved += sum(math.prod(s) * jnp.dtype(d).itemsize for s, d in outs)
    need = sum(padded(a.shape, a.dtype) for a in args[1:])
    need += sum(padded(s, d) for s, d in list(outs) + list(scratch))
    return pl.pallas_call(
        kernel,
        out_shape=[jax.ShapeDtypeStruct(s, d) for s, d in outs],
        in_specs=[SM] + [VM] * (len(args) - 1),
        out_specs=[VM] * len(outs),
        scratch_shapes=[pltpu.VMEM(s, d) for s, d in scratch],
        compiler_params=pltpu.CompilerParams(vmem_limit_bytes=min(need + (room << 20), 58 << 20)),
        cost_estimate=pl.CostEstimate(
            flops=int(micros * 0.15e9), bytes_accessed=moved // 8, transcendentals=0
        ),
        name=name,
    )(*args)


def tokens_packet(turn, tokens, memory, target_ids, source_ids, cotangent):
    block, width = tokens.shape[1:]
    memory_block = memory.shape[1]
    first = block + memory_block + 8

    def kernel(turn_ref, target_ref, source_ref, tokens_ref, memory_ref, cot_ref, sent, kept,
               targets, sources, semaphores):
        mine = turn_ref[0]
        copies = [
            pltpu.make_async_copy(target_ref, targets, semaphores.at[2, 0]),
            pltpu.make_async_copy(source_ref, sources, semaphores.at[2, 1]),
        ]
        for i, (row, out) in enumerate(((1 - mine, sent), (mine, kept))):
            pieces = ((tokens_ref, 0, block), (memory_ref, block, memory_block), (cot_ref, first, block))
            for j, (ref, at, count) in enumerate(pieces):
                copies.append(pltpu.make_async_copy(ref.at[row], out.at[pl.ds(at, count), :], semaphores.at[i, j]))
        for copy in copies:
            copy.start()
        for copy in copies[:2]:
            copy.wait()
        for row, out in ((1 - mine, sent), (mine, kept)):
            ids = targets[pl.ds(row, 1), :].astype(F32)
            ids = jnp.concatenate([ids, jnp.zeros((1, width - block), F32)], axis=1)
            others = sources[pl.ds(row, 1), :].astype(F32)
            others = jnp.concatenate([others, jnp.zeros((1, width - memory_block), F32)], axis=1)
            place = lax.broadcasted_iota(jnp.int32, (8, width), 0)
            found = jnp.where(place == 0, ids, jnp.where(place == 1, others, 0.0))
            out[block + memory_block : first, :] = found.astype(BF16)
        for copy in copies[2:]:
            copy.wait()

    return pl.pallas_call(
        kernel,
        out_shape=[jax.ShapeDtypeStruct((first + block, width), BF16)] * 2,
        in_specs=[SM] + [pl.BlockSpec(memory_space=pltpu.HBM)] * 5,
        out_specs=[VM, VM],
        scratch_shapes=[
            pltpu.VMEM(target_ids.shape, jnp.int32),
            pltpu.VMEM(source_ids.shape, jnp.int32),
            pltpu.SemaphoreType.DMA((3, 3)),
        ],
        compiler_params=pltpu.CompilerParams(vmem_limit_bytes=4 << 20),
        cost_estimate=pl.CostEstimate(flops=1 << 27, bytes_accessed=0, transcendentals=0),
        name="tokens_packet",
    )(turn, target_ids, source_ids, tokens, memory, cotangent)


def placed(me, parts, width):
    here = lax.broadcasted_iota(jnp.int32, (parts.shape[1], width), 0) + me * parts.shape[1]
    lane = lax.broadcasted_iota(jnp.int32, (parts.shape[1], width), 1)
    return dot(parts, jnp.where(lane == here, 1.0, 0.0).astype(BF16))


def make_weights_packet(narrow, width, blocks):
    tall = blocks * narrow

    def kernel(me_ref, *refs):
        weights, inner, outer, short, wide = refs[:8], refs[8], refs[9], refs[10], refs[11]
        first, rest = refs[12:]
        me, middle = me_ref[0], 5 * narrow + 16
        for i, ref in enumerate(weights):
            if i < 3:
                first[i * narrow : (i + 1) * narrow, :] = ref[...]
            else:
                rest[(i - 3) * narrow : (i - 2) * narrow, :] = ref[...]
        found = placed(me, short[...], width)
        first[3 * narrow :, :] = jnp.concatenate([found[:2, :], jnp.zeros((6, width), F32)], axis=0).astype(BF16)
        per = width // wide.shape[1]
        row = placed(lax.rem(me, per), wide[...], width)
        place = lax.broadcasted_iota(jnp.int32, (blocks, width), 0)
        spread_row = jnp.where(place == lax.div(me, per), row, 0.0)
        none = jnp.zeros((16 - (found.shape[0] - 2) - blocks, width), F32)
        rest[5 * narrow : middle, :] = jnp.concatenate([found[2:, :], spread_row, none], axis=0).astype(BF16)
        for i in range(blocks):
            rest[middle + i * narrow : middle + (i + 1) * narrow, :] = inner[:, i * width : (i + 1) * width]
        rest[middle + tall :, :] = outer[...]

    return kernel, [((rows, width), BF16) for rows in (3 * narrow + 8, 5 * narrow + 16 + 2 * tall)]


def make_part(sizes, width):
    tall = sum(sizes)

    def kernel(me_ref, upper, lower, *outs):
        for i in range(8):
            ref, at = (upper, lower)[i // 4], i % 4 * tall
            for size, out in zip(sizes, outs):
                out[i * size : (i + 1) * size, :] = ref[at : at + size, :]
                at += size

    return kernel, [((8 * size, width), BF16) for size in sizes]


def join(arrays):
    def kernel(*refs):
        at = 0
        for ref in refs[:-1]:
            refs[-1][at : at + ref.shape[0], :] = ref[...]
            at += ref.shape[0]

    rows = sum(a.shape[0] for a in arrays)
    return pl.pallas_call(
        kernel,
        out_shape=jax.ShapeDtypeStruct((rows, arrays[0].shape[1]), arrays[0].dtype),
        in_specs=[VM] * len(arrays),
        out_specs=VM,
        compiler_params=pltpu.CompilerParams(vmem_limit_bytes=snug(arrays)),
        cost_estimate=pl.CostEstimate(flops=1 << 20, bytes_accessed=0, transcendentals=0),
        name="join",
    )(*arrays)


def make_project(packed, parts, rows, block, memory_block, width, narrow, n_pieces):
    share = rows * block
    length = parts * share
    memory_share = rows * memory_block
    stride = 3 * narrow + 8
    half = width // 2

    def kernel(*refs):
        me_ref, refs = refs[0], list(refs[1:])
        pieces, refs = refs[:n_pieces], refs[n_pieces:]
        tokens, refs = refs[: parts * rows], refs[parts * rows :]
        query, query_t, keys, values, value_t = (refs[2 * i : 2 * i + 2] for i in range(5))
        memory, ids, memory_ids = refs[10:13]
        scratch = refs[13:]
        me = me_ref[0]
        if packed:
            for i in range(3):
                unpack(me, pieces, stride, i * narrow, narrow, scratch[i], Z_LAST)
            query_w, key_w, value_w = scratch
            biases = vector_sum(pieces, stride, 3 * narrow)
        else:
            query_w, key_w, value_w = pieces[:3]
            biases = pieces[3][...]
        for i in range(parts):
            here = slice(i * share, (i + 1) * share)
            some = tokens[i * rows : (i + 1) * rows]
            own = jnp.concatenate([t[:block, :] for t in some], axis=0)
            if i == 0:
                scaled = (dot(own, query_w[...]) + biases[0:1, :]).astype(BF16) * BF16(HEAD_DIM**-0.5)
            key = dot(own, key_w[...]).astype(BF16)
            found = (dot(own, value_w[...]) + biases[1:2, :]).astype(BF16)
            for side in range(2):
                columns = slice(side * half, (side + 1) * half)
                if i == 0:
                    query[side][...] = scaled[:, columns]
                    query_t[side][...] = scaled[:, columns].T
                keys[side][here, :] = key[:, columns]
                values[side][here, :] = found[:, columns]
                value_t[side][:, here] = found[:, columns].T
        for i, t in enumerate(tokens):
            memory[i * memory_block : (i + 1) * memory_block, :] = t[block : block + memory_block, :]
            found = t[block + memory_block : block + memory_block + 8, :].astype(F32).astype(jnp.int32)
            ids[:, i * block : (i + 1) * block] = found[0:1, :block]
        found = [t[block + memory_block : block + memory_block + 8, :].astype(F32).astype(jnp.int32)[1:2, :memory_block] for t in tokens]
        memory_ids[...] = jnp.concatenate(found, axis=1)

    outs = [((share, half), BF16)] * 2 + [((half, share), BF16)] * 2
    outs += [((length, half), BF16)] * 4 + [((half, length), BF16)] * 2
    outs += [
        ((parts * memory_share, width), BF16),
        ((1, length), jnp.int32),
        ((1, parts * memory_share), jnp.int32),
    ]
    return kernel, outs, [((width, width), BF16)] * 3 if packed else []


def make_self_attention(share, length, width):
    def kernel(me_ref, *refs):
        query_t, keys, value_t, ids = refs[:2], refs[2:4], refs[4:6], refs[6]
        mixture_t, logs, hot, penalty = refs[7:9], refs[9:11], refs[11], refs[12]
        hot[...] = one_hot(ids[...])
        penalty[...] = penalties(ids[:, :share])
        for side in range(2):
            attend(query_t[side], keys[side], value_t[side], hot, penalty, mixture_t[side], logs[side])

    outs = [((width // 2, share), BF16)] * 2 + [((HEADS // 2, 1, share), F32)] * 2
    return kernel, outs, [((length, PAIR), BF16), ((PAIR, share), BF16)]


def make_cross_forward(packed, rows, block, memory_length, width, narrow, n_pieces):
    share = rows * block
    stride = 5 * narrow + 16

    def kernel(*refs):
        me_ref, refs = refs[0], list(refs[1:])
        pieces, refs = refs[:n_pieces], refs[n_pieces:]
        tokens, refs = refs[:rows], refs[rows:]
        memory, ids, memory_ids, upper, lower = refs[:5]
        first_sum, second_sum, query, memory_keys, memory_values, cross_t, logs, vectors = refs[5:13]
        scratch = refs[13:]
        query_t, value_t, hot, penalty = scratch[:4]
        if packed:
            for i in range(5):
                unpack(me_ref[0], pieces, stride, i * narrow, narrow, scratch[4 + i])
            output_w, query_w, key_w, value_w, source_w = scratch[4:]
            vectors[...] = vector_sum(pieces, stride, 5 * narrow)
        else:
            output_w, query_w, key_w, value_w, source_w = pieces[:5]
            vectors[...] = pieces[5][...]

        def vector(i):
            return vectors[i : i + 1, :]

        own = jnp.concatenate([t[:block, :] for t in tokens], axis=0)
        mixture_t = jnp.concatenate([upper[...], lower[...]], axis=0)
        h = own.astype(F32) + dot_tn(mixture_t, output_w[...]) + vector(OUTPUT_BIAS)
        first_sum[...] = h
        first = normalize(h)[0] * vector(ATTENTION_GAIN) + vector(ATTENTION_SHIFT)
        scaled = (dot(first.astype(BF16), query_w[...]) + vector(SOURCE_QUERY_BIAS)).astype(BF16) * BF16(HEAD_DIM**-0.5)
        query[...] = scaled
        query_t[...] = scaled.T
        memory_keys[...] = dot(memory[...], key_w[...]).astype(BF16)
        memory_values[...] = (dot(memory[...], value_w[...]) + vector(SOURCE_VALUE_BIAS)).astype(BF16)
        value_t[...] = memory_values[...].T
        hot[...] = one_hot(memory_ids[...])
        penalty[...] = penalties(ids[:, :share])
        attend(query_t, memory_keys, value_t, hot, penalty, cross_t, logs)
        first = normalize(first_sum[...])[0] * vector(ATTENTION_GAIN) + vector(ATTENTION_SHIFT)
        second_sum[...] = first + dot_tn(cross_t[...], source_w[...]) + vector(SOURCE_OUTPUT_BIAS)

    outs = [
        ((share, width), F32),
        ((share, width), F32),
        ((share, width), BF16),
        ((memory_length, width), BF16),
        ((memory_length, width), BF16),
        ((width, share), BF16),
        ((HEADS, 1, share), F32),
        ((16, width), F32),
    ]
    scratch = [((width, share), BF16), ((width, memory_length), BF16), ((memory_length, PAIR), BF16), ((PAIR, share), BF16)]
    if packed:
        scratch += [((width, width), BF16)] * 5
    return kernel, outs, scratch


def make_inner(packed, rows, block, width, hidden, narrow, n_pieces):
    blocks = hidden // width
    share = rows * block
    per = width // (blocks * narrow)

    def kernel(*refs):
        me_ref, refs = refs[0], list(refs[1:])
        pieces, refs = refs[:n_pieces], refs[n_pieces:]
        second_sum, cot_own, cot_came, vectors = refs[:4]
        out_own, out_send, back, sums = refs[4:8]
        grads, scratch = refs[8:10], refs[10:]
        low, active, gate, slope = scratch[:4]
        if packed:
            inner_w, outer_w, gathered, dense = scratch[4:8]
            tall = blocks * narrow
            for core, far, slot, device in places(me_ref[0]):
                ref, at = pieces[2 * core + far], slot * 2 * tall
                row = pl.multiple_of(device * narrow, narrow)
                for i in range(blocks):
                    inner_w[i, pl.ds(row, narrow), :] = ref[at + i * narrow : at + (i + 1) * narrow, :]
                row = pl.multiple_of(lax.rem(device, per) * tall, tall)
                outer_w[lax.div(device, per), pl.ds(row, tall), :] = ref[at + tall : at + 2 * tall, :]
        else:
            inner_w, outer_w = pieces

        def vector(i):
            return vectors[i : i + 1, :]

        second = normalize(second_sum[...])[0] * vector(SOURCE_GAIN) + vector(SOURCE_SHIFT)
        low[...] = second.astype(BF16)
        back[...] = second + vector(OUTER_BIAS)

        def forward(i, carry):
            inner = dot(low[...], inner_w[i]) + vectors[pl.ds(INNER_BIAS + i, 1), :]
            chance, density = normal_parts(inner)
            found = (inner * chance).astype(BF16)
            active[i] = found
            gate[i] = chance + inner * density
            back[...] += dot(found, outer_w[i])
            return carry

        lax.fori_loop(0, blocks, forward, 0)
        normed, inverse = normalize(back[...])
        final = normed * vector(FINAL_GAIN) + vector(FINAL_SHIFT)
        out_own[...] = final[:block, :]
        out_send[...] = final[block:, :].astype(BF16)
        upstream = jnp.concatenate([cot_own[-block:, :], cot_came[-block:, :]], axis=0).astype(F32)
        sums[0:1, :] = total(upstream * normed)
        sums[1:2, :] = total(upstream)
        back3 = normalize_back(upstream, normed, inverse, vector(FINAL_GAIN))
        slope[...] = back3.astype(BF16)
        sums[2:3, :] = total(slope[...])
        sums[7:8, :] = jnp.zeros_like(sums[7:8, :])
        back[...] = back3

        def backward(i, carry):
            grad = dot_nt(slope[...], outer_w[i]) * gate[i]
            inner_low = grad.astype(BF16)
            sums[pl.ds(3 + i, 1), :] = total(inner_low)
            outer_grad = dot_tn(active[i], slope[...])
            inner_grad = dot_tn(low[...], inner_low)
            back[...] += dot_nt(inner_low, inner_w[i])
            if packed:
                dense[...] = inner_grad
                gathered[i] = outer_grad.astype(BF16)
                here = pl.ds(pl.multiple_of(i * narrow, narrow), narrow)
                for core, far, slot, device in places(me_ref[0]):
                    row = pl.multiple_of(device * narrow, narrow)
                    grads[core][far * 8 + slot, here, :] = dense[pl.ds(row, narrow), :].astype(BF16)
            else:
                grads[0][i] = inner_grad
                grads[1][i] = outer_grad
            return carry

        lax.fori_loop(0, blocks, backward, 0)
        if packed:
            tall = blocks * narrow
            for core, far, slot, device in places(me_ref[0]):
                row = pl.multiple_of(lax.rem(device, per) * tall, tall)
                grads[core][far * 8 + slot, tall:, :] = gathered[lax.div(device, per), pl.ds(row, tall), :]

    outs = [((block, width), F32), ((block, width), BF16), ((share, width), F32), ((8, width), F32)]
    if packed:
        outs += [((16, 2 * blocks * narrow, width), BF16)] * 2
    else:
        outs += [((blocks, width, width), F32)] * 2
    scratch = [((share, width), BF16), ((blocks, share, width), BF16), ((blocks, share, width), F32), ((share, width), BF16)]
    if packed:
        scratch += [((blocks, width, width), BF16)] * 3 + [((width, width), F32)]
    return kernel, outs, scratch


def make_cross_back(packed, parts, share, memory_share, width, narrow, n_pieces):
    memory_length = parts * memory_share
    stride = 5 * narrow + 16

    def kernel(*refs):
        me_ref, refs = refs[0], list(refs[1:])
        pieces, refs = refs[:n_pieces], refs[n_pieces:]
        (back2_in, first_sum, second_sum, query, memory_keys, memory_values, cross_t, logs, ids,
         memory_ids, vectors, sums_inner) = refs[:12]
        mixtures, refs = refs[12:14], refs[14:]
        back1, key_own, value_own, sums = refs[:4]
        self_slope, self_slope_t, self_deltas = (refs[4 + 2 * i : 6 + 2 * i] for i in range(3))
        sends, refs = refs[10 : 10 + parts - 1], refs[10 + parts - 1 :]
        grads, scratch = refs[:3], refs[3:]
        (slope_t, slope, key_t, hot, penalty, query_t, deltas, query_grad_t, key_grad, value_grad) = scratch[:10]
        upper, lower = mixtures
        if packed:
            for i, at in enumerate((0, 1, 4)):
                unpack(me_ref[0], pieces, stride, at * narrow, narrow, scratch[10 + i])
            output_w, query_w, source_w = scratch[10:13]
        else:
            output_w, query_w, source_w = pieces

        def vector(i):
            return vectors[i : i + 1, :]

        sums[0:7, :] = sums_inner[0:7, :]
        upstream = back2_in[...]
        normed, inverse = normalize(second_sum[...])
        sums[7:8, :] = total(upstream * normed)
        sums[8:9, :] = total(upstream)
        back2 = normalize_back(upstream, normed, inverse, vector(SOURCE_GAIN))
        back1[...] = back2
        cross_low = back2.astype(BF16)
        sums[9:10, :] = total(cross_low)
        grads[0][...] = dot(cross_t[...], cross_low).astype(BF16)
        found = dot_nt(cross_low, source_w[...]).astype(BF16)
        slope[...] = found
        slope_t[...] = found.T
        deltas_of(slope_t, cross_t, deltas)
        query_t[...] = query[...].T
        key_t[...] = memory_keys[...].T
        hot[...] = one_hot(memory_ids[...])
        penalty[...] = penalties(ids[:, :share])
        attend_back(query_t, query, memory_keys, key_t, memory_values, slope_t, slope, hot, penalty,
                    logs, deltas, query_grad_t, key_grad, value_grad)
        key_own[...] = key_grad[:memory_share, :]
        value_own[...] = value_grad[:memory_share, :]
        for i in range(1, parts):
            here = slice(i * memory_share, (i + 1) * memory_share)
            sends[i - 1][:memory_share, :] = key_grad[here, :].astype(BF16)
            sends[i - 1][memory_share:, :] = value_grad[here, :].astype(BF16)
        query_low = query_grad_t[...].T.astype(BF16)
        sums[10:11, :] = total(query_low)
        normed, inverse = normalize(first_sum[...])
        first_low = (normed * vector(ATTENTION_GAIN) + vector(ATTENTION_SHIFT)).astype(BF16)
        grads[1][...] = dot_tn(first_low, query_low).astype(BF16)
        upstream = back1[...] + dot_nt(query_low, query_w[...])
        sums[11:12, :] = total(upstream * normed)
        sums[12:13, :] = total(upstream)
        grad = normalize_back(upstream, normed, inverse, vector(ATTENTION_GAIN))
        back1[...] = grad
        branch_low = grad.astype(BF16)
        sums[13:14, :] = total(branch_low)
        sums[14:16, :] = jnp.zeros_like(sums[14:16, :])
        mixture_t = jnp.concatenate([upper[...], lower[...]], axis=0)
        grads[2][...] = dot(mixture_t, branch_low).astype(BF16)
        found = dot_nt(branch_low, output_w[...]).astype(BF16)
        for side in range(2):
            columns = slice(side * width // 2, (side + 1) * width // 2)
            self_slope[side][...] = found[:, columns]
            self_slope_t[side][...] = found[:, columns].T
            deltas_of(self_slope_t[side], mixtures[side], self_deltas[side])

    half = width // 2
    outs = [
        ((share, width), F32),
        ((memory_share, width), F32),
        ((memory_share, width), F32),
        ((16, width), F32),
    ]
    outs += [((share, half), BF16)] * 2 + [((half, share), BF16)] * 2
    outs += [((HEADS // 2, 1, share), F32)] * 2
    outs += [((2 * memory_share, width), BF16)] * (parts - 1)
    outs += [((width, width), BF16)] * 3
    scratch = [
        ((width, share), BF16),
        ((share, width), BF16),
        ((width, memory_length), BF16),
        ((memory_length, PAIR), BF16),
        ((PAIR, share), BF16),
        ((width, share), BF16),
        ((HEADS, 1, share), F32),
        ((width, share), F32),
        ((memory_length, width), F32),
        ((memory_length, width), F32),
    ]
    if packed:
        scratch += [((width, width), BF16)] * 3
    return kernel, outs, scratch


def attention_back_half(refs, share, scratch):
    query, keys, values, slope, slope_t, logs, deltas, ids = refs
    query_t, key_t, hot, penalty, query_grad_t, key_grad, value_grad = scratch
    query_t[...] = query[...].T
    key_t[...] = keys[...].T
    hot[...] = one_hot(ids[...])
    penalty[...] = penalties(ids[:, :share])
    attend_back(query_t, query, keys, key_t, values, slope_t, slope, hot, penalty, logs, deltas,
                query_grad_t, key_grad, value_grad)


def half_scratch(share, length, half):
    return [
        ((half, share), BF16),
        ((half, length), BF16),
        ((length, PAIR), BF16),
        ((PAIR, share), BF16),
        ((half, share), F32),
        ((length, half), F32),
        ((length, half), F32),
    ]


def give_half(share, scratch, own, sends):
    key_grad, value_grad = scratch[5:7]
    own[:share, :] = key_grad[:share, :]
    own[share:, :] = value_grad[:share, :]
    for i, send in enumerate(sends):
        here = slice((i + 1) * share, (i + 2) * share)
        send[:share, :] = key_grad[here, :].astype(BF16)
        send[share:, :] = value_grad[here, :].astype(BF16)


def make_memory_back(packed, parts, rows, block, memory_block, width, narrow, n_pieces):
    memory_share = rows * memory_block

    def kernel(*refs):
        me_ref, refs = refs[0], list(refs[1:])
        pieces, refs = refs[:n_pieces], refs[n_pieces:]
        tokens, refs = refs[:rows], refs[rows:]
        memory_key_own, memory_value_own, sums_in = refs[:3]
        early, refs = refs[3:6], refs[6:]
        memory_received, refs = refs[: parts - 1], refs[parts - 1 :]
        memory_own, memory_send = refs[:2]
        n_grads = 2 if packed else 3
        grad_refs, scratch = refs[2 : 2 + n_grads], refs[2 + n_grads :]
        sums = scratch[0]
        me = me_ref[0]
        if packed:
            for i in range(2):
                unpack(me, pieces, 5 * narrow + 16, (2 + i) * narrow, narrow, scratch[1 + i])
            source_key, source_value = scratch[1:3]
        else:
            source_key, source_value = pieces
        grads = Grads(me, grad_refs, scratch[3] if packed else None, narrow, Z_LAST)
        memory = jnp.concatenate([t[block : block + memory_block, :] for t in tokens], axis=0)
        key_sum, value_sum = memory_key_own[...], memory_value_own[...]
        for ref in memory_received:
            key_sum = key_sum + ref[:memory_share, :].astype(F32)
            value_sum = value_sum + ref[memory_share:, :].astype(F32)
        key_low, value_low = key_sum.astype(BF16), value_sum.astype(BF16)
        sums[...] = sums_in[...]
        sums[14:15, :] = total(value_low)
        grads.put_sums(5 * narrow, sums[...])
        grads.put(0, dot_tn(memory, key_low))
        grads.put(1, dot_tn(memory, value_low))
        if packed:
            for i, ref in enumerate(early):
                grads.put(2 + i, ref[...].astype(F32))
        grad = dot_nt(key_low, source_key[...]) + dot_nt(value_low, source_value[...])
        memory_own[...] = grad[:memory_block, :]
        memory_send[...] = grad[memory_block:, :].astype(BF16)

    outs = [((memory_block, width), F32), ((memory_block, width), BF16)]
    if packed:
        outs += [((16, 5 * narrow + 16, width), BF16)] * 2
    else:
        outs += [((width, width), F32)] * 2 + [((16, width), F32)]
    scratch = [((16, width), F32)]
    if packed:
        scratch += [((width, width), BF16)] * 2 + [((width, width), F32)]
    return kernel, outs, scratch


def make_self_back_upper(parts, share, width):
    length, half = parts * share, width // 2

    def kernel(*refs):
        operands, (query_grad, own), refs = refs[1:9], refs[9:11], refs[11:]
        sends, scratch = refs[: parts - 1], refs[parts - 1 :]
        attention_back_half(operands, share, scratch)
        query_grad[...] = scratch[4][...].T.astype(BF16)
        give_half(share, scratch, own, sends)

    outs = [((share, half), BF16), ((2 * share, half), F32)] + [((2 * share, half), BF16)] * (parts - 1)
    return kernel, outs, half_scratch(share, length, half)


def make_self_back_lower(packed, parts, rows, block, width, narrow, n_pieces):
    share = rows * block
    length, half = parts * share, width // 2

    def kernel(*refs):
        me_ref, refs = refs[0], list(refs[1:])
        pieces, refs = refs[:n_pieces], refs[n_pieces:]
        tokens, refs = refs[:rows], refs[rows:]
        operands, refs = refs[:8], refs[8:]
        back1, query_upper = refs[:2]
        in_part, query_sum, query_w_grad, own = refs[2:6]
        sends, scratch = refs[6 : 6 + parts - 1], refs[6 + parts - 1 :]
        if packed:
            unpack(me_ref[0], pieces, 3 * narrow + 8, 0, narrow, scratch[7], Z_LAST)
            query_w = scratch[7]
        else:
            (query_w,) = pieces
        attention_back_half(operands, share, scratch[:7])
        give_half(share, scratch, own, sends)
        query_low = jnp.concatenate([query_upper[...], scratch[4][...].T.astype(BF16)], axis=1)
        tokens_own = jnp.concatenate([t[:block, :] for t in tokens], axis=0)
        in_part[...] = back1[...] + dot_nt(query_low, query_w[...])
        query_sum[...] = jnp.concatenate([total(query_low), jnp.zeros((7, width), F32)], axis=0)
        query_w_grad[...] = dot_tn(tokens_own, query_low).astype(query_w_grad.dtype)

    outs = [
        ((share, width), F32),
        ((8, width), F32),
        ((width, width), BF16 if packed else F32),
        ((2 * share, half), F32),
    ]
    outs += [((2 * share, half), BF16)] * (parts - 1)
    scratch = half_scratch(share, length, half)
    if packed:
        scratch += [((width, width), BF16)]
    return kernel, outs, scratch


def make_last(packed, parts, rows, block, memory_block, width, narrow, n_pieces):
    share = rows * block

    def kernel(*refs):
        me_ref, refs = refs[0], list(refs[1:])
        pieces, refs = refs[:n_pieces], refs[n_pieces:]
        tokens, refs = refs[:rows], refs[rows:]
        in_part, query_sum, query_w_grad, memory_send = refs[:4]
        owns, refs = refs[4:6], refs[6:]
        received = [refs[: parts - 1], refs[parts - 1 : 2 * (parts - 1)]]
        refs = refs[2 * (parts - 1) :]
        in_own, in_send = refs[:2]
        n_grads = 2 if packed else 3
        grad_refs, scratch = refs[2 : 2 + n_grads], refs[2 + n_grads :]
        sums = scratch[0]
        me = me_ref[0]
        if packed:
            for i in range(2):
                unpack(me, pieces, 3 * narrow + 8, (1 + i) * narrow, narrow, scratch[1 + i], Z_LAST)
            key_w, value_w = scratch[1:3]
        else:
            key_w, value_w = pieces
        grads = Grads(me, grad_refs, scratch[3] if packed else None, narrow)
        if packed:
            grads.put(2, query_w_grad[...].astype(F32))
        lows = []
        for own, others in zip(owns, received):
            found = own[...]
            for ref in others:
                found = found + ref[...].astype(F32)
            lows.append(found.astype(BF16))
        key_low = jnp.concatenate([low[:share, :] for low in lows], axis=1)
        value_low = jnp.concatenate([low[share:, :] for low in lows], axis=1)
        tokens_own = jnp.concatenate([t[:block, :] for t in tokens], axis=0)
        sums[...] = query_sum[...]
        sums[1:2, :] = total(value_low)
        grads.put_sums(3 * narrow, sums[...])
        grads.put(0, dot_tn(tokens_own, key_low))
        grads.put(1, dot_tn(tokens_own, value_low))
        grad = in_part[...] + dot_nt(key_low, key_w[...]) + dot_nt(value_low, value_w[...])
        in_own[...] = grad[:block, :]
        in_send[:block, :] = grad[block:, :].astype(BF16)
        in_send[block:, :] = memory_send[...]

    outs = [((block, width), F32), ((block + memory_block, width), BF16)]
    if packed:
        outs += [((16, 3 * narrow + 8, width), BF16)] * 2
    else:
        outs += [((width, width), F32)] * 2 + [((8, width), F32)]
    scratch = [((8, width), F32)]
    if packed:
        scratch += [((width, width), BF16)] * 2 + [((width, width), F32)]
    return kernel, outs, scratch


def combine(arrays, splits, micros=0.1):
    count = arrays[0].shape[0] // splits
    shape = (count,) + arrays[0].shape[1:]

    def kernel(*refs):
        given, outs = refs[: len(arrays)], refs[len(arrays) :]
        for i, out in enumerate(outs):
            here = slice(i * count, (i + 1) * count)
            found = given[0][here].astype(F32)
            for ref in given[1:]:
                found = found + ref[here].astype(F32)
            out[...] = found.astype(out.dtype)

    return pl.pallas_call(
        kernel,
        out_shape=[jax.ShapeDtypeStruct(shape, BF16)] * splits,
        in_specs=[VM] * len(arrays),
        out_specs=[VM] * splits,
        compiler_params=pltpu.CompilerParams(vmem_limit_bytes=snug(arrays)),
        cost_estimate=pl.CostEstimate(flops=int(micros * 1.15e9), bytes_accessed=0, transcendentals=0),
        name="combine",
    )(*arrays)


def chosen(me, rows, wide):
    width = rows.shape[1]
    line = lax.broadcasted_iota(jnp.int32, (width, wide), 0)
    here = lax.broadcasted_iota(jnp.int32, (width, wide), 1) + me * wide
    choice = jnp.where(line == here, 1.0, 0.0)
    return lax.dot_general(rows, choice, (((1,), (0,)), ((), ())), precision=lax.Precision.HIGHEST, preferred_element_type=F32)


def reduce_all(array, devices):
    mask = 1
    while mask < devices:
        array = array + swap(array, mask, devices)
        mask *= 2
    return array


def per_device(
    tokens, memory, target_ids, source_ids, cotangent,
    query_weight, key_weight, value_weight, output_weight, query_bias, value_bias, output_bias,
    attention_gain, attention_shift,
    source_query, source_key, source_value, source_output, source_query_bias, source_value_bias,
    source_output_bias, source_gain, source_shift,
    inner_weight, inner_bias, outer_weight, outer_bias, final_gain, final_shift,
    *, devices, sequence,
):
    packed = devices == 32
    rows, block, width = tokens.shape
    memory_block = memory.shape[1]
    parts = sequence // rows
    share, memory_share = rows * block, rows * memory_block
    hidden = inner_weight.shape[1]
    blocks = hidden // width
    me = lax.axis_index(AXES)
    me_array = me.reshape(1).astype(jnp.int32)
    turn = lax.rem(lax.div(me, parts), rows)
    narrow, wide = width // devices, hidden // devices

    def run(made, micros, name, *args):
        kernel, outs, *scratch = made
        return call(kernel, outs, (me_array,) + args, scratch[0] if scratch else [], micros, name)

    short = jnp.stack([query_bias, value_bias, output_bias, attention_gain, attention_shift,
                       source_query_bias, source_value_bias, source_output_bias, source_gain,
                       source_shift, outer_bias, final_gain, final_shift])

    def whole(array):
        return lax.all_gather(array, AXES, axis=0, tiled=True)

    sent, kept = tokens_packet(
        turn.reshape(1).astype(jnp.int32), tokens, memory, target_ids, source_ids, cotangent
    )
    came = swap(sent, parts, devices)
    row_tokens = [kept, came]
    kept_swaps = [swap(kept, m, devices) for m in range(1, parts)]
    came_swaps = [swap(came, m, devices) for m in range(1, parts)]
    for pair in zip(kept_swaps, came_swaps):
        row_tokens += pair
    own_tokens = row_tokens[:rows]

    if packed:
        first, rest = run(make_weights_packet(narrow, width, blocks), 1.0, "weights_packet",
                          query_weight, key_weight, value_weight, output_weight, source_query,
                          source_key, source_value, source_output, inner_weight, outer_weight,
                          short, inner_bias.reshape(1, wide))
        first = after(first, sent)
        first_b, rest_b = turned_swap(first, 0, Z_LAST), turned_swap(rest, 0)
        first, rest = join(after([first, first_b], rest_b)), join(after([rest, rest_b], first_b))
        first_b, rest_b = turned_swap(first, 1, Z_LAST), turned_swap(rest, 1)
        first = join(after([first, first_b], came, *kept_swaps))
        first_b = turned_swap(first, 2, Z_LAST)
        first_c, rest = join(after([first, first_b], rest_b)), join(after([rest, rest_b], first_b))
        first_d, rest_b = turned_swap(first_c, 3, Z_LAST), turned_swap(rest, 2)
        second_c, third_c = run(
            make_part((5 * narrow + 16, 2 * blocks * narrow), width), 1.0, "part", rest, rest_b
        )
        first_d = after(first_d, second_c, *came_swaps)
        second_d, third_d = turned_swap(second_c, 3), turned_swap(after(third_c, first_d), 3)
        set_self = [first_c, first_d, swap(first_c, 1, 32), swap(first_d, 1, 32)]
    else:
        full = [whole(w) for w in (query_weight, key_weight, value_weight, output_weight, source_query, source_key, source_value, source_output)]
        lane = lax.broadcasted_iota(jnp.int32, (1, width), 1)
        place = lax.broadcasted_iota(jnp.int32, (blocks, width), 0) * width + lane
        spread_wide = jnp.where(place // wide == me, jnp.tile(inner_bias.reshape(1, wide), (blocks, width // wide)), 0)

        def natural(rows):
            return jnp.where(lane // narrow == me, jnp.tile(rows, (1, devices)), 0)

        vectors = jnp.concatenate([natural(short[:2]), jnp.zeros((6, width), BF16), natural(short[2:]), spread_wide, jnp.zeros((1, width), BF16)])
        vectors = reduce_all(vectors, devices).astype(F32)
        set_self = full[:3] + [vectors[:8]]
        set_cross = full[3:] + [vectors[8:]]
        set_inner = [
            whole(inner_weight).reshape(width, blocks, width).transpose(1, 0, 2),
            whole(outer_weight).reshape(blocks, width, width),
        ]
    found = run(
        make_project(packed, parts, rows, block, memory_block, width, narrow, len(set_self)), 5.0,
        "project", *set_self, *row_tokens,
    )
    query, query_t, keys, values, value_t = (found[2 * i : 2 * i + 2] for i in range(5))
    row_memory, ids, memory_ids = found[10:]
    query_t = list(query_t)
    if packed:
        set_cross = [second_c, second_d, swap(second_c, 1, 32), swap(second_d, 1, 32)]
        query_t[0] = after(query_t[0], second_d)
        set_back, set_query, set_last, set_memory = set_cross, set_self, set_self, set_cross
    else:
        set_back, set_query, set_last, set_memory = [full[3], full[4], full[7]], full[:1], full[1:3], full[5:7]
    found = run(
        make_self_attention(share, parts * share, width), 12.0, "self_attention",
        *query_t, *keys, *value_t, ids,
    )
    mixtures, logs = found[:2], found[2:]
    if packed:
        third_d = after(third_d, mixtures[0])
        set_inner = [third_c, third_d, swap(third_c, 1, 32), swap(third_d, 1, 32)]
        mixtures = [after(mixtures[0], third_d), mixtures[1]]
    first_sum, second_sum, cross_query, memory_keys, memory_values, cross_t, cross_logs, vectors = run(
        make_cross_forward(packed, rows, block, parts * memory_share, width, narrow, len(set_cross)),
        9.0, "cross_forward", *set_cross, *own_tokens, row_memory, ids, memory_ids, *mixtures,
    )
    out_own, out_send, back2_in, sums_inner, *grads_inner = run(
        make_inner(packed, rows, block, width, hidden, narrow, len(set_inner)), 18.0, "inner",
        *set_inner, second_sum, kept, came, vectors,
    )
    out_came = swap(out_send, parts, devices)
    found = run(
        make_cross_back(packed, parts, share, memory_share, width, narrow, len(set_back)), 14.0,
        "cross_back", *set_back, back2_in, first_sum, second_sum, cross_query, memory_keys,
        memory_values, cross_t, cross_logs, ids, memory_ids, vectors, sums_inner, *mixtures,
    )
    back1, memory_key_own, memory_value_own, sums_cross = found[:4]
    slope, slope_t, deltas = (found[4 + 2 * i : 6 + 2 * i] for i in range(3))
    memory_received = [swap(a, m + 1, devices) for m, a in enumerate(found[10 : 10 + parts - 1])]
    grads_early = found[10 + parts - 1 :]
    query = list(query)
    if packed:
        keep, send = combine([grads_inner[0], swap(grads_inner[1], 1, 32)], 2)
        inner_step = [keep, turned_swap(send, 3)]
        memory_key_own = after(memory_key_own, keep, out_came)
    memory_own, memory_send, *grads_cross = run(
        make_memory_back(packed, parts, rows, block, memory_block, width, narrow, len(set_memory)),
        2.0, "memory_back", *set_memory, *own_tokens, memory_key_own, memory_value_own, sums_cross,
        *grads_early, *memory_received,
    )
    if packed:
        cross_came = swap(grads_cross[1], 1, 32)
        query[0] = after(query[0], grads_cross[0])
    found = run(
        make_self_back_upper(parts, share, width), 7.0, "self_back_upper", query[0], keys[0],
        values[0], slope[0], slope_t[0], logs[0], deltas[0], ids,
    )
    query_upper, own_upper = found[:2]
    received_upper = [swap(a, m + 1, devices) for m, a in enumerate(found[2:])]
    if packed:
        keep_cross, send = combine([grads_cross[0], cross_came], 2)
        cross_step = [keep_cross, turned_swap(send, 3, Z_LAST)]
        keep, send = combine(after(inner_step, keep_cross), 2)
        inner_step = [keep, turned_swap(send, 2)]
        query[1] = after(query[1], keep, keep_cross)
    in_part, query_sum, query_w_grad, own_lower, *sends = run(
        make_self_back_lower(packed, parts, rows, block, width, narrow, len(set_query)), 11.0,
        "self_back_lower", *set_query, *own_tokens, query[1], keys[1], values[1], slope[1],
        slope_t[1], logs[1], deltas[1], ids, back1, query_upper,
    )
    received_lower = [swap(a, m + 1, devices) for m, a in enumerate(sends)]
    if packed:
        keep, send = combine(inner_step, 2)
        inner_step = [keep, turned_swap(send, 1)]
        in_part = after(in_part, keep)
    in_own, in_send, *grads_last = run(
        make_last(packed, parts, rows, block, memory_block, width, narrow, len(set_last)), 6.0,
        "last", *set_last, *own_tokens, in_part, query_sum, query_w_grad, memory_send, own_upper,
        own_lower, *received_upper, *received_lower,
    )

    if packed:
        keep_cross, send = combine(cross_step, 2, 8.0)
        cross_step = [keep_cross, turned_swap(send, 2, Z_LAST)]
        keep, send = combine(after([grads_last[0], swap(grads_last[1], 1, 32)], keep_cross), 2)
        last_step = [keep, turned_swap(send, 3)]
        in_send = after(in_send, last_step[1])
        keep, send = combine(last_step, 2)
        last_step = [keep, turned_swap(send, 2)]
        keep_inner, send = combine(inner_step, 2)
        inner_step = [keep_inner, turned_swap(send, 0)]
        keep_cross, send = combine(cross_step, 2)
        cross_step = [keep_cross, turned_swap(send, 1, Z_LAST)]
        keep, send = combine(after(last_step, keep_cross, keep_inner), 2)
        last_step = [keep, turned_swap(send, 1)]
        keep_cross, send = combine(cross_step, 2)
        cross_step = [keep_cross, turned_swap(send, 0, Z_LAST)]
        keep, send = combine(after(last_step, keep_cross), 2)
        last_step = [keep, turned_swap(send, 0)]

        def plan(me_ref, *refs):
            me = me_ref[0]
            steps, outs = [refs[:2], refs[2:4], refs[4:6]], refs[6:]
            inner, cross, last = (sum(r[0].astype(F32) for r in given) for given in steps)
            for i in range(blocks):
                outs[0][:, i * width : (i + 1) * width] = inner[i * narrow : (i + 1) * narrow, :]
            outs[1][...] = inner[blocks * narrow :, :]
            for i in range(5):
                outs[2 + i][...] = cross[i * narrow : (i + 1) * narrow, :]
            for i in range(3):
                outs[7 + i][...] = last[i * narrow : (i + 1) * narrow, :]
            rows_in = jnp.concatenate([cross[5 * narrow :, :], last[3 * narrow :, :]], axis=0)
            outs[10][...] = chosen(me, rows_in, narrow)
            per = width // wide
            line = lax.broadcasted_iota(jnp.int32, (blocks, width), 0)
            row = jnp.sum(jnp.where(line == lax.div(me, per), rows_in[3 : 3 + blocks, :], 0.0), axis=0, keepdims=True)
            outs[11][...] = chosen(lax.rem(me, per), row, wide)

        part = (narrow, width)
        shapes = [(narrow, hidden), (wide, width)] + [part] * 8 + [(24, narrow), (1, wide)]
        (inner_share, outer_share, source_key_share, source_value_share, source_output_share,
         source_query_share, output_share, key_share, value_share, query_share, sums,
         inner_bias_share) = call(
            plan, [(s, F32) for s in shapes], (me_array, *inner_step, *cross_step, *last_step), [], 2.0,
            "finish",
        )
        inner_bias_share = inner_bias_share.reshape(wide)
    else:
        def scatter(array):
            return lax.psum_scatter(array, AXES, scatter_dimension=0, tiled=True)

        inner_share = scatter(grads_inner[0].transpose(1, 0, 2).reshape(width, hidden))
        outer_share = scatter(grads_inner[1].reshape(hidden, width))
        source_output_share, source_query_share, output_share = (scatter(g.astype(F32)) for g in grads_early)
        source_key_share, source_value_share = (scatter(g) for g in grads_cross[:2])
        key_share, value_share = (scatter(g) for g in grads_last[:2])
        query_share = scatter(query_w_grad)
        sums = reduce_all(jnp.concatenate([grads_cross[2], grads_last[2]], axis=0), devices)
        inner_bias_share = lax.dynamic_slice(sums[3 : 3 + blocks].reshape(hidden), (me * wide,), (wide,))
        sums = lax.dynamic_slice(sums, (0, me * narrow), (sums.shape[0], narrow))
    def regroup(mine, came):
        came = came.astype(F32)
        return jnp.where(turn == 0, jnp.stack([mine, came]), jnp.stack([came, mine]))

    output = regroup(out_own, out_came)
    in_came = swap(in_send, parts, devices)
    input_gradient = regroup(in_own, in_came[:block])
    memory_gradient = regroup(memory_own, in_came[block:])

    return (
        output,
        input_gradient,
        memory_gradient,
        query_share,
        key_share,
        value_share,
        output_share,
        sums[16],
        sums[17],
        sums[13],
        sums[11],
        sums[12],
        source_query_share,
        source_key_share,
        source_value_share,
        source_output_share,
        sums[10],
        sums[14],
        sums[9],
        sums[7],
        sums[8],
        inner_share,
        inner_bias_share,
        outer_share,
        sums[2],
        sums[0],
        sums[1],
    )


def solution(mesh):
    sequence, devices = mesh.shape["seq"], mesh.size
    tokens, ids = P("dp", "seq", None), P("dp", "seq")
    matrix, vector = P(AXES, None), P(AXES)
    attention = (matrix,) * 4 + (vector,) * 5
    inner = (matrix, vector, matrix, vector, vector, vector)
    return jax.shard_map(
        functools.partial(per_device, devices=devices, sequence=sequence),
        mesh=mesh,
        in_specs=(tokens, tokens, ids, ids, tokens) + attention + attention + inner,
        out_specs=(tokens, tokens, tokens) + attention + attention + inner,
        check_vma=False,
    )
```

```python
import functools
import math

import jax
import jax.numpy as jnp
from jax import lax
from jax.experimental import pallas as pl
from jax.experimental.pallas import tpu as pltpu
from jax.sharding import PartitionSpec as P

HEADS = 8
HEAD_DIM = 64
PAIR = 128
EPSILON = 1e-05
MASKED = 1e9
AXES = ("dp", "seq")
F32 = jnp.float32
BF16 = jnp.bfloat16

(
    OUTPUT_BIAS,
    ATTENTION_GAIN,
    ATTENTION_SHIFT,
    SOURCE_QUERY_BIAS,
    SOURCE_VALUE_BIAS,
    SOURCE_OUTPUT_BIAS,
    SOURCE_GAIN,
    SOURCE_SHIFT,
    OUTER_BIAS,
    FINAL_GAIN,
    FINAL_SHIFT,
    INNER_BIAS,
) = range(12)
Z_MASKS = (0, 8, 16, 24)
VM = pl.BlockSpec(memory_space=pltpu.VMEM)
SM = pl.BlockSpec(memory_space=pltpu.SMEM)


def dot(a, b):
    return lax.dot_general(a, b, (((1,), (0,)), ((), ())), preferred_element_type=F32)


def dot_nt(a, b):
    return lax.dot_general(a, b, (((1,), (1,)), ((), ())), preferred_element_type=F32)


def dot_tn(a, b):
    return lax.dot_general(a, b, (((0,), (0,)), ((), ())), preferred_element_type=F32)


def total(values):
    return jnp.sum(values.astype(F32), axis=0, keepdims=True)


def normalize(h):
    average = jnp.mean(h, axis=-1, keepdims=True)
    centered = h - average
    variance = jnp.mean(centered * centered, axis=-1, keepdims=True)
    inverse = lax.rsqrt(variance + EPSILON)
    return centered * inverse, inverse


def normalize_back(upstream, normed, inverse, gain):
    scaled = upstream * gain
    first_mean = jnp.mean(scaled, axis=-1, keepdims=True)
    second_mean = jnp.mean(scaled * normed, axis=-1, keepdims=True)
    return inverse * (scaled - first_mean - normed * second_mean)


def normal_parts(v):
    density = 0.3989422804014327 * jnp.exp(-0.5 * v * v)
    t = 1.0 / (1.0 + 0.2316419 * jnp.abs(v))
    series = t * (
        0.319381530
        + t * (-0.356563782 + t * (1.781477937 + t * (-1.821255978 + t * 1.330274429)))
    )
    tail = density * series
    return jnp.where(v >= 0.0, 1.0 - tail, tail), density


def penalties(ids):
    place = lax.broadcasted_iota(jnp.int32, (PAIR, ids.shape[1]), 0)
    return jnp.where((place == ids) | (place >= 4), 0.0, -MASKED).astype(BF16)


def one_hot(ids):
    place = lax.broadcasted_iota(jnp.int32, (PAIR, ids.shape[1]), 0)
    return jnp.where(place == ids, 1.0, 0.0).astype(F32).T.astype(BF16)


def spread(part, half):
    empty = jnp.zeros_like(part)
    return [part, empty] if half == 0 else [empty, part]


def attend(query_t, keys, value_t, hot, penalty, mixture_t, logs):
    length = keys.shape[0]

    def pair(p, carry):
        columns = pl.ds(pl.multiple_of(p * PAIR, PAIR), PAIR)
        left = jnp.concatenate([keys[:, columns], hot[...]], axis=1)
        for half in range(2):
            rows = pl.ds(pl.multiple_of(p * PAIR + half * HEAD_DIM, HEAD_DIM), HEAD_DIM)
            right = jnp.concatenate(spread(query_t[rows, :], half) + [penalty[...]], axis=0)
            scores = dot(left, right)
            highest = jnp.max(scores, axis=0, keepdims=True)
            weights = jnp.exp(scores - highest).astype(BF16)
            values = jnp.concatenate(
                [value_t[rows, :], jnp.ones((16, length), BF16)], axis=0
            )
            found = dot(values, weights)
            denominator = found[HEAD_DIM : HEAD_DIM + 1, :]
            mixture_t[rows, :] = (found[:HEAD_DIM, :] / denominator).astype(BF16)
            logs[2 * p + half] = highest + jnp.log(denominator)
        return carry

    lax.fori_loop(0, keys.shape[1] // PAIR, pair, 0)


def attend_back(
    query_t, query, keys, key_t, values, slope_t, slope, hot, penalty, logs, deltas,
    query_grad_t, key_grad, value_grad,
):
    tokens = query.shape[0]
    lane = lax.broadcasted_iota(jnp.int32, (tokens, PAIR), 1)

    def pair(p, carry):
        columns = pl.ds(pl.multiple_of(p * PAIR, PAIR), PAIR)
        left = jnp.concatenate([keys[:, columns], hot[...]], axis=1)
        value_pair = values[:, columns]
        key_sum, value_sum = None, None
        for half in range(2):
            rows = pl.ds(pl.multiple_of(p * PAIR + half * HEAD_DIM, HEAD_DIM), HEAD_DIM)
            right = jnp.concatenate(spread(query_t[rows, :], half) + [penalty[...]], axis=0)
            chances = jnp.exp(dot(left, right) - logs[2 * p + half])
            slopes = dot(value_pair, jnp.concatenate(spread(slope_t[rows, :], half), axis=0))
            grads = (chances * (slopes - deltas[2 * p + half])).astype(BF16)
            query_grad_t[rows, :] = dot(key_t[rows, :], grads) * HEAD_DIM**-0.5
            mine = (lane < HEAD_DIM) if half == 0 else (lane >= HEAD_DIM)
            none = jnp.zeros((tokens, PAIR), BF16)
            value_part = dot(chances.astype(BF16), jnp.where(mine, slope[:, columns], none))
            key_part = dot(grads, jnp.where(mine, query[:, columns], none))
            value_sum = value_part if value_sum is None else value_sum + value_part
            key_sum = key_part if key_sum is None else key_sum + key_part
        key_grad[:, columns] = key_sum
        value_grad[:, columns] = value_sum
        return carry

    lax.fori_loop(0, keys.shape[1] // PAIR, pair, 0)


def deltas_of(slope_t, mixture_t, deltas):
    for head in range(slope_t.shape[0] // HEAD_DIM):
        rows = slice(head * HEAD_DIM, (head + 1) * HEAD_DIM)
        deltas[head] = jnp.sum(
            slope_t[rows, :].astype(F32) * mixture_t[rows, :].astype(F32), axis=0, keepdims=True
        )


def swap(array, mask, devices):
    return lax.ppermute(array, AXES, [(i, i ^ mask) for i in range(devices)])


ORDERS = ((8, 16, 2, 4), (16, 8, 4, 2))


def turned_swap(array, step):
    return lax.ppermute(array, AXES, [(i, i ^ ORDERS[i % 2][step]) for i in range(32)])


def after(value, *others):
    return lax.optimization_barrier((value, others))[0]


def places(me):
    found = []
    for core in range(2):
        even = ((me & 1) ^ core) == 0
        masks = [jnp.where(even, first, second) for first, second in zip(*ORDERS)]
        for far in range(2):
            for slot in range(8):
                device = me ^ core if core else me
                for step, bit in enumerate((slot & 1, slot & 2, slot & 4, far)):
                    if bit:
                        device = device ^ masks[step]
                found.append((core, far, slot, device))
    return found


def unpack(me, pieces, stride, first, rows, scratch):
    for core, far, slot, device in places(me):
        ref = pieces[2 * core + far]
        at = slot * stride + first
        scratch[pl.ds(pl.multiple_of(device * rows, rows), rows), :] = ref[at : at + rows, :]


def vector_sum(pieces, stride, first):
    found = None
    for ref in pieces:
        for slot in range(8):
            part = ref[slot * stride + first : (slot + 1) * stride, :].astype(F32)
            found = part if found is None else found + part
    return found


class Grads:
    def __init__(self, me, refs, dense, rows):
        self.me, self.refs, self.dense, self.rows = me, refs, dense, rows

    def put(self, index, grad):
        if self.dense is None:
            self.refs[index][...] = grad
            return
        self.dense[...] = grad
        rows = self.rows
        for core, far, slot, device in places(self.me):
            found = self.dense[pl.ds(pl.multiple_of(device * rows, rows), rows), :]
            self.refs[core][far * 8 + slot, index * rows : (index + 1) * rows, :] = found.astype(BF16)

    def put_sums(self, first, sums):
        if self.dense is None:
            self.refs[-1][...] = sums
            return
        low = sums.astype(BF16)
        for ref in self.refs:
            for slot in range(16):
                ref[slot, first : first + sums.shape[0], :] = low


def grad_outs(packed, count, rows, width, sums):
    if packed:
        return [((16, count * rows + sums, width), BF16)] * 2
    return [((width, width), F32)] * count + [((sums, width), F32)]


def padded(shape, dtype):
    last = -(-shape[-1] // 128) * 128
    tall = -(-shape[-2] // 16) * 16 if len(shape) > 1 else 16
    return math.prod(shape[:-2]) * tall * last * jnp.dtype(dtype).itemsize


def snug(arrays):
    return 2 * sum(padded(a.shape, a.dtype) for a in arrays) + (3 << 20)


def call(kernel, outs, args, scratch, micros, name, room=10):
    moved = sum(math.prod(a.shape) * a.dtype.itemsize for a in args[1:])
    moved += sum(math.prod(s) * jnp.dtype(d).itemsize for s, d in outs)
    need = sum(padded(a.shape, a.dtype) for a in args[1:])
    need += sum(padded(s, d) for s, d in list(outs) + list(scratch))
    return pl.pallas_call(
        kernel,
        out_shape=[jax.ShapeDtypeStruct(s, d) for s, d in outs],
        in_specs=[SM] + [VM] * (len(args) - 1),
        out_specs=[VM] * len(outs),
        scratch_shapes=[pltpu.VMEM(s, d) for s, d in scratch],
        compiler_params=pltpu.CompilerParams(vmem_limit_bytes=min(need + (room << 20), 58 << 20)),
        cost_estimate=pl.CostEstimate(
            flops=1, bytes_accessed=1, transcendentals=0
        ),
        name=name,
    )(*args)


def tokens_packet(turn, tokens, memory, target_ids, source_ids, cotangent):
    block, width = tokens.shape[1:]
    memory_block = memory.shape[1]
    first = block + memory_block + 8

    def kernel(turn_ref, targets, sources, tokens_ref, memory_ref, cot_ref, sent, kept):
        mine = turn_ref[0]
        for row, out in ((1 - mine, sent), (mine, kept)):
            out[:block, :] = tokens_ref[row]
            out[block : block + memory_block, :] = memory_ref[row]
            ids = targets[pl.ds(row, 1), :].astype(F32)
            ids = jnp.concatenate([ids, jnp.zeros((1, width - block), F32)], axis=1)
            others = sources[pl.ds(row, 1), :].astype(F32)
            others = jnp.concatenate([others, jnp.zeros((1, width - memory_block), F32)], axis=1)
            place = lax.broadcasted_iota(jnp.int32, (8, width), 0)
            found = jnp.where(place == 0, ids, jnp.where(place == 1, others, 0.0))
            out[block + memory_block : first, :] = found.astype(BF16)
            out[first:, :] = cot_ref[row]

    shape = (first + block, width)
    return call(kernel, [(shape, BF16)] * 2, (turn, target_ids, source_ids, tokens, memory, cotangent),
                [], 1.0, "tokens_packet", 58)


def placed(me, parts, width):
    here = lax.broadcasted_iota(jnp.int32, (parts.shape[1], width), 0) + me * parts.shape[1]
    lane = lax.broadcasted_iota(jnp.int32, (parts.shape[1], width), 1)
    return dot(parts, jnp.where(lane == here, 1.0, 0.0).astype(BF16))


def make_weights_packet(narrow, width, blocks):
    tall = blocks * narrow

    def kernel(me_ref, *refs):
        weights, inner, outer, short, wide = refs[:8], refs[8], refs[9], refs[10], refs[11]
        first, rest = refs[12:]
        me, middle = me_ref[0], 5 * narrow + 16
        for i, ref in enumerate(weights):
            if i < 3:
                first[i * narrow : (i + 1) * narrow, :] = ref[...]
            else:
                rest[(i - 3) * narrow : (i - 2) * narrow, :] = ref[...]
        found = placed(me, short[...], width)
        first[3 * narrow :, :] = jnp.concatenate([found[:2, :], jnp.zeros((6, width), F32)], axis=0).astype(BF16)
        per = width // wide.shape[1]
        row = placed(lax.rem(me, per), wide[...], width)
        place = lax.broadcasted_iota(jnp.int32, (blocks, width), 0)
        spread_row = jnp.where(place == lax.div(me, per), row, 0.0)
        none = jnp.zeros((16 - (found.shape[0] - 2) - blocks, width), F32)
        rest[5 * narrow : middle, :] = jnp.concatenate([found[2:, :], spread_row, none], axis=0).astype(BF16)
        for i in range(blocks):
            rest[middle + i * narrow : middle + (i + 1) * narrow, :] = inner[:, i * width : (i + 1) * width]
        rest[middle + tall :, :] = outer[...]

    return kernel, [((rows, width), BF16) for rows in (3 * narrow + 8, 5 * narrow + 16 + 2 * tall)]


def make_part(sizes, width):
    tall = sum(sizes)

    def kernel(me_ref, upper, lower, *outs):
        for i in range(4):
            ref, at = (upper, lower)[i // 2], i % 2 * tall
            for size, out in zip(sizes, outs):
                out[i * size : (i + 1) * size, :] = ref[at : at + size, :]
                at += size

    return kernel, [((4 * size, width), BF16) for size in sizes]


def join(arrays):
    def kernel(*refs):
        at = 0
        for ref in refs[:-1]:
            refs[-1][at : at + ref.shape[0], :] = ref[...]
            at += ref.shape[0]

    rows = sum(a.shape[0] for a in arrays)
    return pl.pallas_call(
        kernel,
        out_shape=jax.ShapeDtypeStruct((rows, arrays[0].shape[1]), arrays[0].dtype),
        in_specs=[VM] * len(arrays),
        out_specs=VM,
        compiler_params=pltpu.CompilerParams(vmem_limit_bytes=snug(arrays)),
        cost_estimate=pl.CostEstimate(flops=1 << 20, bytes_accessed=0, transcendentals=0),
        name="join",
    )(*arrays)


def make_project(packed, parts, rows, block, memory_block, width, narrow, n_pieces):
    share = rows * block
    length = parts * share
    memory_share = rows * memory_block
    stride = 3 * narrow + 8
    half = width // 2

    def kernel(*refs):
        me_ref, refs = refs[0], list(refs[1:])
        pieces, refs = refs[:n_pieces], refs[n_pieces:]
        tokens, refs = refs[: parts * rows], refs[parts * rows :]
        query, query_t, keys, values, value_t = (refs[2 * i : 2 * i + 2] for i in range(5))
        memory, ids, memory_ids = refs[10:13]
        scratch = refs[13:]
        me = me_ref[0]
        if packed:
            for i in range(3):
                unpack(me, pieces, stride, i * narrow, narrow, scratch[i])
            query_w, key_w, value_w = scratch
            biases = vector_sum(pieces, stride, 3 * narrow)
        else:
            query_w, key_w, value_w = pieces[:3]
            biases = pieces[3][...]
        for i in range(parts):
            here = slice(i * share, (i + 1) * share)
            some = tokens[i * rows : (i + 1) * rows]
            own = jnp.concatenate([t[:block, :] for t in some], axis=0)
            if i == 0:
                scaled = (dot(own, query_w[...]) + biases[0:1, :]).astype(BF16) * BF16(HEAD_DIM**-0.5)
            key = dot(own, key_w[...]).astype(BF16)
            found = (dot(own, value_w[...]) + biases[1:2, :]).astype(BF16)
            for side in range(2):
                columns = slice(side * half, (side + 1) * half)
                if i == 0:
                    query[side][...] = scaled[:, columns]
                    query_t[side][...] = scaled[:, columns].T
                keys[side][here, :] = key[:, columns]
                values[side][here, :] = found[:, columns]
                value_t[side][:, here] = found[:, columns].T
        for i, t in enumerate(tokens):
            memory[i * memory_block : (i + 1) * memory_block, :] = t[block : block + memory_block, :]
            found = t[block + memory_block : block + memory_block + 8, :].astype(F32).astype(jnp.int32)
            ids[:, i * block : (i + 1) * block] = found[0:1, :block]
        found = [t[block + memory_block : block + memory_block + 8, :].astype(F32).astype(jnp.int32)[1:2, :memory_block] for t in tokens]
        memory_ids[...] = jnp.concatenate(found, axis=1)

    outs = [((share, half), BF16)] * 2 + [((half, share), BF16)] * 2
    outs += [((length, half), BF16)] * 4 + [((half, length), BF16)] * 2
    outs += [
        ((parts * memory_share, width), BF16),
        ((1, length), jnp.int32),
        ((1, parts * memory_share), jnp.int32),
    ]
    return kernel, outs, [((width, width), BF16)] * 3 if packed else []


def make_self_attention(share, length, width):
    def kernel(me_ref, *refs):
        query_t, keys, value_t, ids = refs[:2], refs[2:4], refs[4:6], refs[6]
        mixture_t, logs, hot, penalty = refs[7:9], refs[9:11], refs[11], refs[12]
        hot[...] = one_hot(ids[...])
        penalty[...] = penalties(ids[:, :share])
        for side in range(2):
            attend(query_t[side], keys[side], value_t[side], hot, penalty, mixture_t[side], logs[side])

    outs = [((width // 2, share), BF16)] * 2 + [((HEADS // 2, 1, share), F32)] * 2
    return kernel, outs, [((length, PAIR), BF16), ((PAIR, share), BF16)]


def make_cross_forward(packed, rows, block, memory_length, width, narrow, n_pieces):
    share = rows * block
    stride = 5 * narrow + 16

    def kernel(*refs):
        me_ref, refs = refs[0], list(refs[1:])
        pieces, refs = refs[:n_pieces], refs[n_pieces:]
        tokens, refs = refs[:rows], refs[rows:]
        memory, ids, memory_ids, upper, lower = refs[:5]
        first_sum, second_sum, query, memory_keys, memory_values, cross_t, logs, vectors = refs[5:13]
        scratch = refs[13:]
        query_t, value_t, hot, penalty = scratch[:4]
        if packed:
            for i in range(5):
                unpack(me_ref[0], pieces, stride, i * narrow, narrow, scratch[4 + i])
            output_w, query_w, key_w, value_w, source_w = scratch[4:]
            vectors[...] = vector_sum(pieces, stride, 5 * narrow)
        else:
            output_w, query_w, key_w, value_w, source_w = pieces[:5]
            vectors[...] = pieces[5][...]

        def vector(i):
            return vectors[i : i + 1, :]

        own = jnp.concatenate([t[:block, :] for t in tokens], axis=0)
        mixture_t = jnp.concatenate([upper[...], lower[...]], axis=0)
        h = own.astype(F32) + dot_tn(mixture_t, output_w[...]) + vector(OUTPUT_BIAS)
        first_sum[...] = h
        first = normalize(h)[0] * vector(ATTENTION_GAIN) + vector(ATTENTION_SHIFT)
        scaled = (dot(first.astype(BF16), query_w[...]) + vector(SOURCE_QUERY_BIAS)).astype(BF16) * BF16(HEAD_DIM**-0.5)
        query[...] = scaled
        query_t[...] = scaled.T
        memory_keys[...] = dot(memory[...], key_w[...]).astype(BF16)
        memory_values[...] = (dot(memory[...], value_w[...]) + vector(SOURCE_VALUE_BIAS)).astype(BF16)
        value_t[...] = memory_values[...].T
        hot[...] = one_hot(memory_ids[...])
        penalty[...] = penalties(ids[:, :share])
        attend(query_t, memory_keys, value_t, hot, penalty, cross_t, logs)
        first = normalize(first_sum[...])[0] * vector(ATTENTION_GAIN) + vector(ATTENTION_SHIFT)
        second_sum[...] = first + dot_tn(cross_t[...], source_w[...]) + vector(SOURCE_OUTPUT_BIAS)

    outs = [
        ((share, width), F32),
        ((share, width), F32),
        ((share, width), BF16),
        ((memory_length, width), BF16),
        ((memory_length, width), BF16),
        ((width, share), BF16),
        ((HEADS, 1, share), F32),
        ((16, width), F32),
    ]
    scratch = [((width, share), BF16), ((width, memory_length), BF16), ((memory_length, PAIR), BF16), ((PAIR, share), BF16)]
    if packed:
        scratch += [((width, width), BF16)] * 5
    return kernel, outs, scratch


def make_inner(packed, rows, block, width, hidden, narrow, n_pieces):
    blocks = hidden // width
    share = rows * block
    per = width // (blocks * narrow)

    def kernel(*refs):
        me_ref, refs = refs[0], list(refs[1:])
        pieces, refs = refs[:n_pieces], refs[n_pieces:]
        second_sum, cot_own, cot_came, vectors = refs[:4]
        out_own, out_send, back, sums = refs[4:8]
        grads, scratch = refs[8:10], refs[10:]
        low, active, gate, slope = scratch[:4]
        if packed:
            inner_w, outer_w, gathered, dense = scratch[4:8]
            tall = blocks * narrow
            for core, far, slot, device in places(me_ref[0]):
                ref, at = pieces[2 * core + far], slot * 2 * tall
                row = pl.multiple_of(device * narrow, narrow)
                for i in range(blocks):
                    inner_w[i, pl.ds(row, narrow), :] = ref[at + i * narrow : at + (i + 1) * narrow, :]
                row = pl.multiple_of(lax.rem(device, per) * tall, tall)
                outer_w[lax.div(device, per), pl.ds(row, tall), :] = ref[at + tall : at + 2 * tall, :]
        else:
            inner_w, outer_w = pieces

        def vector(i):
            return vectors[i : i + 1, :]

        second = normalize(second_sum[...])[0] * vector(SOURCE_GAIN) + vector(SOURCE_SHIFT)
        low[...] = second.astype(BF16)
        back[...] = second + vector(OUTER_BIAS)

        def forward(i, carry):
            inner = dot(low[...], inner_w[i]) + vectors[pl.ds(INNER_BIAS + i, 1), :]
            chance, density = normal_parts(inner)
            found = (inner * chance).astype(BF16)
            active[i] = found
            gate[i] = chance + inner * density
            back[...] += dot(found, outer_w[i])
            return carry

        lax.fori_loop(0, blocks, forward, 0)
        normed, inverse = normalize(back[...])
        final = normed * vector(FINAL_GAIN) + vector(FINAL_SHIFT)
        out_own[...] = final[:block, :]
        out_send[...] = final[block:, :].astype(BF16)
        upstream = jnp.concatenate([cot_own[-block:, :], cot_came[-block:, :]], axis=0).astype(F32)
        sums[0:1, :] = total(upstream * normed)
        sums[1:2, :] = total(upstream)
        back3 = normalize_back(upstream, normed, inverse, vector(FINAL_GAIN))
        slope[...] = back3.astype(BF16)
        sums[2:3, :] = total(slope[...])
        sums[7:8, :] = jnp.zeros_like(sums[7:8, :])
        back[...] = back3

        def backward(i, carry):
            grad = dot_nt(slope[...], outer_w[i]) * gate[i]
            inner_low = grad.astype(BF16)
            sums[pl.ds(3 + i, 1), :] = total(inner_low)
            outer_grad = dot_tn(active[i], slope[...])
            inner_grad = dot_tn(low[...], inner_low)
            back[...] += dot_nt(inner_low, inner_w[i])
            if packed:
                dense[...] = inner_grad
                gathered[i] = outer_grad.astype(BF16)
                here = pl.ds(pl.multiple_of(i * narrow, narrow), narrow)
                for core, far, slot, device in places(me_ref[0]):
                    row = pl.multiple_of(device * narrow, narrow)
                    grads[core][far * 8 + slot, here, :] = dense[pl.ds(row, narrow), :].astype(BF16)
            else:
                grads[0][i] = inner_grad
                grads[1][i] = outer_grad
            return carry

        lax.fori_loop(0, blocks, backward, 0)
        if packed:
            tall = blocks * narrow
            for core, far, slot, device in places(me_ref[0]):
                row = pl.multiple_of(lax.rem(device, per) * tall, tall)
                grads[core][far * 8 + slot, tall:, :] = gathered[lax.div(device, per), pl.ds(row, tall), :]

    outs = [((block, width), F32), ((block, width), BF16), ((share, width), F32), ((8, width), F32)]
    if packed:
        outs += [((16, 2 * blocks * narrow, width), BF16)] * 2
    else:
        outs += [((blocks, width, width), F32)] * 2
    scratch = [((share, width), BF16), ((blocks, share, width), BF16), ((blocks, share, width), F32), ((share, width), BF16)]
    if packed:
        scratch += [((blocks, width, width), BF16)] * 3 + [((width, width), F32)]
    return kernel, outs, scratch


def make_cross_back(packed, parts, share, memory_share, width, narrow, n_pieces):
    memory_length = parts * memory_share
    stride = 5 * narrow + 16

    def kernel(*refs):
        me_ref, refs = refs[0], list(refs[1:])
        pieces, refs = refs[:n_pieces], refs[n_pieces:]
        (back2_in, first_sum, second_sum, query, memory_keys, memory_values, cross_t, logs, ids,
         memory_ids, vectors, sums_inner) = refs[:12]
        mixtures, refs = refs[12:14], refs[14:]
        back1, key_own, value_own, sums = refs[:4]
        self_slope, self_slope_t, self_deltas = (refs[4 + 2 * i : 6 + 2 * i] for i in range(3))
        sends, refs = refs[10 : 10 + parts - 1], refs[10 + parts - 1 :]
        grads, scratch = refs[:3], refs[3:]
        (slope_t, slope, key_t, hot, penalty, query_t, deltas, query_grad_t, key_grad, value_grad) = scratch[:10]
        upper, lower = mixtures
        if packed:
            for i, at in enumerate((0, 1, 4)):
                unpack(me_ref[0], pieces, stride, at * narrow, narrow, scratch[10 + i])
            output_w, query_w, source_w = scratch[10:13]
        else:
            output_w, query_w, source_w = pieces

        def vector(i):
            return vectors[i : i + 1, :]

        sums[0:7, :] = sums_inner[0:7, :]
        upstream = back2_in[...]
        normed, inverse = normalize(second_sum[...])
        sums[7:8, :] = total(upstream * normed)
        sums[8:9, :] = total(upstream)
        back2 = normalize_back(upstream, normed, inverse, vector(SOURCE_GAIN))
        back1[...] = back2
        cross_low = back2.astype(BF16)
        sums[9:10, :] = total(cross_low)
        grads[0][...] = dot(cross_t[...], cross_low).astype(BF16)
        found = dot_nt(cross_low, source_w[...]).astype(BF16)
        slope[...] = found
        slope_t[...] = found.T
        deltas_of(slope_t, cross_t, deltas)
        query_t[...] = query[...].T
        key_t[...] = memory_keys[...].T
        hot[...] = one_hot(memory_ids[...])
        penalty[...] = penalties(ids[:, :share])
        attend_back(query_t, query, memory_keys, key_t, memory_values, slope_t, slope, hot, penalty,
                    logs, deltas, query_grad_t, key_grad, value_grad)
        key_own[...] = key_grad[:memory_share, :]
        value_own[...] = value_grad[:memory_share, :]
        for i in range(1, parts):
            here = slice(i * memory_share, (i + 1) * memory_share)
            sends[i - 1][:memory_share, :] = key_grad[here, :].astype(BF16)
            sends[i - 1][memory_share:, :] = value_grad[here, :].astype(BF16)
        query_low = query_grad_t[...].T.astype(BF16)
        sums[10:11, :] = total(query_low)
        normed, inverse = normalize(first_sum[...])
        first_low = (normed * vector(ATTENTION_GAIN) + vector(ATTENTION_SHIFT)).astype(BF16)
        grads[1][...] = dot_tn(first_low, query_low).astype(BF16)
        upstream = back1[...] + dot_nt(query_low, query_w[...])
        sums[11:12, :] = total(upstream * normed)
        sums[12:13, :] = total(upstream)
        grad = normalize_back(upstream, normed, inverse, vector(ATTENTION_GAIN))
        back1[...] = grad
        branch_low = grad.astype(BF16)
        sums[13:14, :] = total(branch_low)
        sums[14:16, :] = jnp.zeros_like(sums[14:16, :])
        mixture_t = jnp.concatenate([upper[...], lower[...]], axis=0)
        grads[2][...] = dot(mixture_t, branch_low).astype(BF16)
        found = dot_nt(branch_low, output_w[...]).astype(BF16)
        for side in range(2):
            columns = slice(side * width // 2, (side + 1) * width // 2)
            self_slope[side][...] = found[:, columns]
            self_slope_t[side][...] = found[:, columns].T
            deltas_of(self_slope_t[side], mixtures[side], self_deltas[side])

    half = width // 2
    outs = [
        ((share, width), F32),
        ((memory_share, width), F32),
        ((memory_share, width), F32),
        ((16, width), F32),
    ]
    outs += [((share, half), BF16)] * 2 + [((half, share), BF16)] * 2
    outs += [((HEADS // 2, 1, share), F32)] * 2
    outs += [((2 * memory_share, width), BF16)] * (parts - 1)
    outs += [((width, width), BF16)] * 3
    scratch = [
        ((width, share), BF16),
        ((share, width), BF16),
        ((width, memory_length), BF16),
        ((memory_length, PAIR), BF16),
        ((PAIR, share), BF16),
        ((width, share), BF16),
        ((HEADS, 1, share), F32),
        ((width, share), F32),
        ((memory_length, width), F32),
        ((memory_length, width), F32),
    ]
    if packed:
        scratch += [((width, width), BF16)] * 3
    return kernel, outs, scratch


def attention_back_half(refs, share, scratch):
    query, keys, values, slope, slope_t, logs, deltas, ids = refs
    query_t, key_t, hot, penalty, query_grad_t, key_grad, value_grad = scratch
    query_t[...] = query[...].T
    key_t[...] = keys[...].T
    hot[...] = one_hot(ids[...])
    penalty[...] = penalties(ids[:, :share])
    attend_back(query_t, query, keys, key_t, values, slope_t, slope, hot, penalty, logs, deltas,
                query_grad_t, key_grad, value_grad)


def half_scratch(share, length, half):
    return [
        ((half, share), BF16),
        ((half, length), BF16),
        ((length, PAIR), BF16),
        ((PAIR, share), BF16),
        ((half, share), F32),
        ((length, half), F32),
        ((length, half), F32),
    ]


def give_half(share, scratch, own, sends):
    key_grad, value_grad = scratch[5:7]
    own[:share, :] = key_grad[:share, :]
    own[share:, :] = value_grad[:share, :]
    for i, send in enumerate(sends):
        here = slice((i // 2 + 1) * share, (i // 2 + 2) * share)
        send[...] = (key_grad, value_grad)[i % 2][here, :].astype(BF16)


def make_memory_back(packed, parts, rows, block, memory_block, width, narrow, n_pieces):
    memory_share = rows * memory_block

    def kernel(*refs):
        me_ref, refs = refs[0], list(refs[1:])
        pieces, refs = refs[:n_pieces], refs[n_pieces:]
        tokens, refs = refs[:rows], refs[rows:]
        memory_key_own, memory_value_own, sums_in = refs[:3]
        early, refs = refs[3:6], refs[6:]
        memory_received, refs = refs[: parts - 1], refs[parts - 1 :]
        memory_own, memory_send = refs[:2]
        n_grads = 2 if packed else 3
        grad_refs, scratch = refs[2 : 2 + n_grads], refs[2 + n_grads :]
        sums = scratch[0]
        me = me_ref[0]
        if packed:
            for i in range(2):
                unpack(me, pieces, 5 * narrow + 16, (2 + i) * narrow, narrow, scratch[1 + i])
            source_key, source_value = scratch[1:3]
        else:
            source_key, source_value = pieces
        grads = Grads(me, grad_refs, scratch[3] if packed else None, narrow)
        memory = jnp.concatenate([t[block : block + memory_block, :] for t in tokens], axis=0)
        key_sum, value_sum = memory_key_own[...], memory_value_own[...]
        for ref in memory_received:
            key_sum = key_sum + ref[:memory_share, :].astype(F32)
            value_sum = value_sum + ref[memory_share:, :].astype(F32)
        key_low, value_low = key_sum.astype(BF16), value_sum.astype(BF16)
        sums[...] = sums_in[...]
        sums[14:15, :] = total(value_low)
        grads.put_sums(5 * narrow, sums[...])
        grads.put(0, dot_tn(memory, key_low))
        grads.put(1, dot_tn(memory, value_low))
        if packed:
            for i, ref in enumerate(early):
                grads.put(2 + i, ref[...].astype(F32))
        grad = dot_nt(key_low, source_key[...]) + dot_nt(value_low, source_value[...])
        memory_own[...] = grad[:memory_block, :]
        memory_send[...] = grad[memory_block:, :].astype(BF16)

    outs = [((memory_block, width), F32), ((memory_block, width), BF16)]
    if packed:
        outs += [((16, 5 * narrow + 16, width), BF16)] * 2
    else:
        outs += [((width, width), F32)] * 2 + [((16, width), F32)]
    scratch = [((16, width), F32)]
    if packed:
        scratch += [((width, width), BF16)] * 2 + [((width, width), F32)]
    return kernel, outs, scratch


def make_self_back_upper(parts, share, width):
    length, half = parts * share, width // 2

    def kernel(*refs):
        operands, (query_grad, own), refs = refs[1:9], refs[9:11], refs[11:]
        sends, scratch = refs[: 2 * parts - 2], refs[2 * parts - 2 :]
        attention_back_half(operands, share, scratch)
        query_grad[...] = scratch[4][...].T.astype(BF16)
        give_half(share, scratch, own, sends)

    outs = [((share, half), BF16), ((2 * share, half), F32)] + [((share, half), BF16)] * (2 * parts - 2)
    return kernel, outs, half_scratch(share, length, half)


def make_self_back_lower(packed, parts, rows, block, width, narrow, n_pieces):
    share = rows * block
    length, half = parts * share, width // 2

    def kernel(*refs):
        me_ref, refs = refs[0], list(refs[1:])
        pieces, refs = refs[:n_pieces], refs[n_pieces:]
        tokens, refs = refs[:rows], refs[rows:]
        operands, refs = refs[:8], refs[8:]
        back1, query_upper = refs[:2]
        in_part, query_sum, query_w_grad, own = refs[2:6]
        sends, scratch = refs[6 : 4 + 2 * parts], refs[4 + 2 * parts :]
        if packed:
            unpack(me_ref[0], pieces, 3 * narrow + 8, 0, narrow, scratch[7])
            query_w = scratch[7]
        else:
            (query_w,) = pieces
        attention_back_half(operands, share, scratch[:7])
        give_half(share, scratch, own, sends)
        query_low = jnp.concatenate([query_upper[...], scratch[4][...].T.astype(BF16)], axis=1)
        tokens_own = jnp.concatenate([t[:block, :] for t in tokens], axis=0)
        in_part[...] = back1[...] + dot_nt(query_low, query_w[...])
        query_sum[...] = jnp.concatenate([total(query_low), jnp.zeros((7, width), F32)], axis=0)
        query_w_grad[...] = dot_tn(tokens_own, query_low).astype(query_w_grad.dtype)

    outs = [
        ((share, width), F32),
        ((8, width), F32),
        ((width, width), BF16 if packed else F32),
        ((2 * share, half), F32),
    ]
    outs += [((share, half), BF16)] * (2 * parts - 2)
    scratch = half_scratch(share, length, half)
    if packed:
        scratch += [((width, width), BF16)]
    return kernel, outs, scratch


def make_last(packed, parts, rows, block, memory_block, width, narrow, n_pieces):
    share = rows * block

    def kernel(*refs):
        me_ref, refs = refs[0], list(refs[1:])
        pieces, refs = refs[:n_pieces], refs[n_pieces:]
        tokens, refs = refs[:rows], refs[rows:]
        in_part, query_sum, query_w_grad, memory_send = refs[:4]
        owns, refs = refs[4:6], refs[6:]
        received = [refs[: 2 * parts - 2], refs[2 * parts - 2 : 4 * parts - 4]]
        refs = refs[4 * parts - 4 :]
        in_own, in_send = refs[:2]
        n_grads = 2 if packed else 3
        grad_refs, scratch = refs[2 : 2 + n_grads], refs[2 + n_grads :]
        sums = scratch[0]
        me = me_ref[0]
        if packed:
            for i in range(2):
                unpack(me, pieces, 3 * narrow + 8, (1 + i) * narrow, narrow, scratch[1 + i])
            key_w, value_w = scratch[1:3]
        else:
            key_w, value_w = pieces
        grads = Grads(me, grad_refs, scratch[3] if packed else None, narrow)
        if packed:
            grads.put(2, query_w_grad[...].astype(F32))
        lows = []
        for own, others in zip(owns, received):
            found = own[...]
            for key, value in zip(others[::2], others[1::2]):
                found = found + jnp.concatenate([key[...], value[...]], axis=0).astype(F32)
            lows.append(found.astype(BF16))
        key_low = jnp.concatenate([low[:share, :] for low in lows], axis=1)
        value_low = jnp.concatenate([low[share:, :] for low in lows], axis=1)
        tokens_own = jnp.concatenate([t[:block, :] for t in tokens], axis=0)
        sums[...] = query_sum[...]
        sums[1:2, :] = total(value_low)
        grads.put_sums(3 * narrow, sums[...])
        grads.put(0, dot_tn(tokens_own, key_low))
        grads.put(1, dot_tn(tokens_own, value_low))
        grad = in_part[...] + dot_nt(key_low, key_w[...]) + dot_nt(value_low, value_w[...])
        in_own[...] = grad[:block, :]
        in_send[:block, :] = grad[block:, :].astype(BF16)
        in_send[block:, :] = memory_send[...]

    outs = [((block, width), F32), ((block + memory_block, width), BF16)]
    if packed:
        outs += [((16, 3 * narrow + 8, width), BF16)] * 2
    else:
        outs += [((width, width), F32)] * 2 + [((8, width), F32)]
    scratch = [((8, width), F32)]
    if packed:
        scratch += [((width, width), BF16)] * 2 + [((width, width), F32)]
    return kernel, outs, scratch


def combine(arrays, splits, micros=0.1):
    count = arrays[0].shape[0] // splits
    shape = (count,) + arrays[0].shape[1:]

    def kernel(*refs):
        given, outs = refs[: len(arrays)], refs[len(arrays) :]
        for i, out in enumerate(outs):
            here = slice(i * count, (i + 1) * count)
            found = given[0][here].astype(F32)
            for ref in given[1:]:
                found = found + ref[here].astype(F32)
            out[...] = found.astype(out.dtype)

    return pl.pallas_call(
        kernel,
        out_shape=[jax.ShapeDtypeStruct(shape, BF16)] * splits,
        in_specs=[VM] * len(arrays),
        out_specs=[VM] * splits,
        compiler_params=pltpu.CompilerParams(vmem_limit_bytes=snug(arrays)),
        cost_estimate=pl.CostEstimate(flops=int(micros * 1.15e9), bytes_accessed=0, transcendentals=0),
        name="combine",
    )(*arrays)


def chosen(me, rows, wide):
    width = rows.shape[1]
    line = lax.broadcasted_iota(jnp.int32, (width, wide), 0)
    here = lax.broadcasted_iota(jnp.int32, (width, wide), 1) + me * wide
    choice = jnp.where(line == here, 1.0, 0.0)
    return lax.dot_general(rows, choice, (((1,), (0,)), ((), ())), precision=lax.Precision.HIGHEST, preferred_element_type=F32)


def reduce_all(array, devices):
    mask = 1
    while mask < devices:
        array = array + swap(array, mask, devices)
        mask *= 2
    return array


def per_device(
    tokens, memory, target_ids, source_ids, cotangent,
    query_weight, key_weight, value_weight, output_weight, query_bias, value_bias, output_bias,
    attention_gain, attention_shift,
    source_query, source_key, source_value, source_output, source_query_bias, source_value_bias,
    source_output_bias, source_gain, source_shift,
    inner_weight, inner_bias, outer_weight, outer_bias, final_gain, final_shift,
    *, devices, sequence,
):
    packed = devices == 32
    rows, block, width = tokens.shape
    memory_block = memory.shape[1]
    parts = sequence // rows
    share, memory_share = rows * block, rows * memory_block
    hidden = inner_weight.shape[1]
    blocks = hidden // width
    me = lax.axis_index(AXES)
    me_array = me.reshape(1).astype(jnp.int32)
    turn = lax.rem(lax.div(me, parts), rows)
    narrow, wide = width // devices, hidden // devices

    def run(made, micros, name, *args, room=10):
        kernel, outs, *scratch = made
        return call(kernel, outs, (me_array,) + args, scratch[0] if scratch else [], micros, name, room)

    short = jnp.stack([query_bias, value_bias, output_bias, attention_gain, attention_shift,
                       source_query_bias, source_value_bias, source_output_bias, source_gain,
                       source_shift, outer_bias, final_gain, final_shift])

    def whole(array):
        return lax.all_gather(array, AXES, axis=0, tiled=True)

    sent, kept = tokens_packet(
        turn.reshape(1).astype(jnp.int32), tokens, memory, target_ids, source_ids, cotangent
    )
    came = swap(sent, parts, devices)
    row_tokens = [kept, came]
    kept_swaps = [swap(kept, m, devices) for m in range(1, parts)]
    came_swaps = [swap(came, m, devices) for m in range(1, parts)]
    for pair in zip(kept_swaps, came_swaps):
        row_tokens += pair
    own_tokens = row_tokens[:rows]

    if packed:
        first, rest = run(make_weights_packet(narrow, width, blocks), 1.0, "weights_packet",
                          query_weight, key_weight, value_weight, output_weight, source_query,
                          source_key, source_value, source_output, inner_weight, outer_weight,
                          short, inner_bias.reshape(1, wide), room=58)
        first = after(first, sent)
        first = join([first, turned_swap(first, 0)])
        first_b = turned_swap(first, 1)
        rest = after(rest, first)
        rest_b = turned_swap(rest, 0)
        first = join(after([first, first_b], rest_b))
        rest = join(after([rest, rest_b], first_b, came, *kept_swaps))
        first_b, rest_b = turned_swap(first, 2), turned_swap(rest, 1)
        first_c = join([first, first_b])
        first_d = turned_swap(first_c, 3)
        second, third = run(make_part((5 * narrow + 16, 2 * blocks * narrow), width), 1.0, "part", rest, rest_b)
        second_b, third_b = turned_swap(second, 2), turned_swap(third, 2)
        second_c = join([second, second_b])
        second_d = turned_swap(second_c, 3)
        first_d = after(first_d, second_c, *came_swaps)
        set_self = [first_c, first_d, swap(first_c, 1, 32), swap(first_d, 1, 32)]
    else:
        full = [whole(w) for w in (query_weight, key_weight, value_weight, output_weight, source_query, source_key, source_value, source_output)]
        lane = lax.broadcasted_iota(jnp.int32, (1, width), 1)
        place = lax.broadcasted_iota(jnp.int32, (blocks, width), 0) * width + lane
        spread_wide = jnp.where(place // wide == me, jnp.tile(inner_bias.reshape(1, wide), (blocks, width // wide)), 0)

        def natural(rows):
            return jnp.where(lane // narrow == me, jnp.tile(rows, (1, devices)), 0)

        vectors = jnp.concatenate([natural(short[:2]), jnp.zeros((6, width), BF16), natural(short[2:]), spread_wide, jnp.zeros((1, width), BF16)])
        vectors = reduce_all(vectors, devices).astype(F32)
        set_self = full[:3] + [vectors[:8]]
        set_cross = full[3:] + [vectors[8:]]
        set_inner = [
            whole(inner_weight).reshape(width, blocks, width).transpose(1, 0, 2),
            whole(outer_weight).reshape(blocks, width, width),
        ]
    found = run(
        make_project(packed, parts, rows, block, memory_block, width, narrow, len(set_self)), 5.0,
        "project", *set_self, *row_tokens,
    )
    query, query_t, keys, values, value_t = (found[2 * i : 2 * i + 2] for i in range(5))
    row_memory, ids, memory_ids = found[10:]
    query_t = list(query_t)
    if packed:
        third_c = join(after([third, third_b], query_t[0]))
        third_d = turned_swap(third_c, 3)
        second_d = after(second_d, query_t[0])
        set_cross = [second_c, second_d, swap(second_c, 1, 32), swap(second_d, 1, 32)]
        query_t[0] = after(query_t[0], third_c, second_d)
        set_back, set_query, set_last, set_memory = set_cross, set_self, set_self, set_cross
    else:
        set_back, set_query, set_last, set_memory = [full[3], full[4], full[7]], full[:1], full[1:3], full[5:7]
    found = run(
        make_self_attention(share, parts * share, width), 12.0, "self_attention",
        *query_t, *keys, *value_t, ids,
    )
    mixtures, logs = found[:2], found[2:]
    if packed:
        third_d = after(third_d, mixtures[0])
        set_inner = [third_c, third_d, swap(third_c, 1, 32), swap(third_d, 1, 32)]
    first_sum, second_sum, cross_query, memory_keys, memory_values, cross_t, cross_logs, vectors = run(
        make_cross_forward(packed, rows, block, parts * memory_share, width, narrow, len(set_cross)),
        9.0, "cross_forward", *set_cross, *own_tokens, row_memory, ids, memory_ids, *mixtures,
    )
    out_own, out_send, back2_in, sums_inner, *grads_inner = run(
        make_inner(packed, rows, block, width, hidden, narrow, len(set_inner)), 18.0, "inner",
        *set_inner, second_sum, kept, came, vectors,
    )
    out_came = swap(out_send, parts, devices)
    found = run(
        make_cross_back(packed, parts, share, memory_share, width, narrow, len(set_back)), 14.0,
        "cross_back", *set_back, back2_in, first_sum, second_sum, cross_query, memory_keys,
        memory_values, cross_t, cross_logs, ids, memory_ids, vectors, sums_inner, *mixtures,
    )
    back1, memory_key_own, memory_value_own, sums_cross = found[:4]
    slope, slope_t, deltas = (found[4 + 2 * i : 6 + 2 * i] for i in range(3))
    memory_received = [swap(a, m + 1, devices) for m, a in enumerate(found[10 : 10 + parts - 1])]
    grads_early = found[10 + parts - 1 :]
    query = list(query)
    if packed:
        keep, send = combine(after([grads_inner[0], swap(grads_inner[1], 1, 32)], back1, out_came), 2)
        inner_step = [keep, turned_swap(send, 3)]
        memory_key_own = after(memory_key_own, keep)
    memory_own, memory_send, *grads_cross = run(
        make_memory_back(packed, parts, rows, block, memory_block, width, narrow, len(set_memory)),
        2.0, "memory_back", *set_memory, *own_tokens, memory_key_own, memory_value_own, sums_cross,
        *grads_early, *memory_received,
    )
    if packed:
        cross_came = swap(grads_cross[1], 1, 32)
        query[0] = after(query[0], grads_cross[0])
    found = run(
        make_self_back_upper(parts, share, width), 7.0, "self_back_upper", query[0], keys[0],
        values[0], slope[0], slope_t[0], logs[0], deltas[0], ids,
    )
    query_upper, own_upper = found[:2]
    received_upper = [swap(a, m // 2 + 1, devices) for m, a in enumerate(found[2:])]
    if packed:
        keep, send = combine(after(inner_step, query_upper), 2, 8.0)
        inner_step = [keep, turned_swap(send, 2)]
        keep_cross, send = combine(after([grads_cross[0], cross_came], keep), 2)
        cross_step = [keep_cross, turned_swap(send, 3)]
        query[1] = after(query[1], keep, keep_cross)
    in_part, query_sum, query_w_grad, own_lower, *sends = run(
        make_self_back_lower(packed, parts, rows, block, width, narrow, len(set_query)), 11.0,
        "self_back_lower", *set_query, *own_tokens, query[1], keys[1], values[1], slope[1],
        slope_t[1], logs[1], deltas[1], ids, back1, query_upper,
    )
    received_lower = [swap(a, m // 2 + 1, devices) for m, a in enumerate(sends)]
    in_own, in_send, *grads_last = run(
        make_last(packed, parts, rows, block, memory_block, width, narrow, len(set_last)), 6.0,
        "last", *set_last, *own_tokens, in_part, query_sum, query_w_grad, memory_send, own_upper,
        own_lower, *received_upper, *received_lower,
    )

    if packed:
        keep_inner, send = combine(after(inner_step, in_own), 2)
        inner_step = [keep_inner, turned_swap(send, 1)]
        keep_cross, send = combine(after(cross_step, keep_inner), 2)
        cross_step = [keep_cross, turned_swap(send, 2)]
        grads_last[1] = after(grads_last[1], keep_cross)
        keep, send = combine([grads_last[0], swap(grads_last[1], 1, 32)], 2)
        last_step = [keep, turned_swap(send, 3)]
        in_send = after(in_send, last_step[1])
        keep_inner, send = combine(inner_step, 2)
        inner_step = [keep_inner, turned_swap(send, 0)]
        keep_cross, send = combine(cross_step, 2)
        cross_step = [keep_cross, turned_swap(send, 1)]
        keep, send = combine(after(last_step, keep_inner, keep_cross), 2)
        last_step = [keep, turned_swap(send, 2)]
        keep_cross, send = combine(cross_step, 2)
        cross_step = [keep_cross, turned_swap(send, 0)]
        keep, send = combine(after(last_step, keep_cross), 2)
        last_step = [keep, turned_swap(send, 1)]
        keep, send = combine(last_step, 2)
        last_step = [keep, turned_swap(send, 0)]

        def plan(me_ref, *refs):
            me = me_ref[0]
            steps, outs = [refs[:2], refs[2:4], refs[4:6]], refs[6:]
            inner, cross, last = (sum(r[0].astype(F32) for r in given) for given in steps)
            for i in range(blocks):
                outs[0][:, i * width : (i + 1) * width] = inner[i * narrow : (i + 1) * narrow, :]
            outs[1][...] = inner[blocks * narrow :, :]
            for i in range(5):
                outs[2 + i][...] = cross[i * narrow : (i + 1) * narrow, :]
            for i in range(3):
                outs[7 + i][...] = last[i * narrow : (i + 1) * narrow, :]
            rows_in = jnp.concatenate([cross[5 * narrow :, :], last[3 * narrow :, :]], axis=0)
            outs[10][...] = chosen(me, rows_in, narrow)
            per = width // wide
            line = lax.broadcasted_iota(jnp.int32, (blocks, width), 0)
            row = jnp.sum(jnp.where(line == lax.div(me, per), rows_in[3 : 3 + blocks, :], 0.0), axis=0, keepdims=True)
            outs[11][...] = chosen(lax.rem(me, per), row, wide)

        part = (narrow, width)
        shapes = [(narrow, hidden), (wide, width)] + [part] * 8 + [(24, narrow), (1, wide)]
        (inner_share, outer_share, source_key_share, source_value_share, source_output_share,
         source_query_share, output_share, key_share, value_share, query_share, sums,
         inner_bias_share) = call(
            plan, [(s, F32) for s in shapes], (me_array, *inner_step, *cross_step, *last_step), [], 2.0,
            "finish",
        )
        inner_bias_share = inner_bias_share.reshape(wide)
    else:
        def scatter(array):
            return lax.psum_scatter(array, AXES, scatter_dimension=0, tiled=True)

        inner_share = scatter(grads_inner[0].transpose(1, 0, 2).reshape(width, hidden))
        outer_share = scatter(grads_inner[1].reshape(hidden, width))
        source_output_share, source_query_share, output_share = (scatter(g.astype(F32)) for g in grads_early)
        source_key_share, source_value_share = (scatter(g) for g in grads_cross[:2])
        key_share, value_share = (scatter(g) for g in grads_last[:2])
        query_share = scatter(query_w_grad)
        sums = reduce_all(jnp.concatenate([grads_cross[2], grads_last[2]], axis=0), devices)
        inner_bias_share = lax.dynamic_slice(sums[3 : 3 + blocks].reshape(hidden), (me * wide,), (wide,))
        sums = lax.dynamic_slice(sums, (0, me * narrow), (sums.shape[0], narrow))
    def regroup(mine, came):
        came = came.astype(F32)
        return jnp.where(turn == 0, jnp.stack([mine, came]), jnp.stack([came, mine]))

    output = regroup(out_own, out_came)
    in_came = swap(in_send, parts, devices)
    input_gradient = regroup(in_own, in_came[:block])
    memory_gradient = regroup(memory_own, in_came[block:])

    return (
        output,
        input_gradient,
        memory_gradient,
        query_share,
        key_share,
        value_share,
        output_share,
        sums[16],
        sums[17],
        sums[13],
        sums[11],
        sums[12],
        source_query_share,
        source_key_share,
        source_value_share,
        source_output_share,
        sums[10],
        sums[14],
        sums[9],
        sums[7],
        sums[8],
        inner_share,
        inner_bias_share,
        outer_share,
        sums[2],
        sums[0],
        sums[1],
    )


def solution(mesh):
    sequence, devices = mesh.shape["seq"], mesh.size
    tokens, ids = P("dp", "seq", None), P("dp", "seq")
    matrix, vector = P(AXES, None), P(AXES)
    attention = (matrix,) * 4 + (vector,) * 5
    inner = (matrix, vector, matrix, vector, vector, vector)
    return jax.shard_map(
        functools.partial(per_device, devices=devices, sequence=sequence),
        mesh=mesh,
        in_specs=(tokens, tokens, ids, ids, tokens) + attention + attention + inner,
        out_specs=(tokens, tokens, tokens) + attention + attention + inner,
        check_vma=False,
    )
```

```python
import functools
import math

import jax
import jax.numpy as jnp
from jax import lax
from jax.experimental import pallas as pl
from jax.experimental.pallas import tpu as pltpu
from jax.sharding import PartitionSpec as P

HEADS = 8
HEAD_DIM = 64
PAIR = 128
EPSILON = 1e-05
MASKED = 1e9
AXES = ("dp", "seq")
F32 = jnp.float32
BF16 = jnp.bfloat16

(
    OUTPUT_BIAS,
    ATTENTION_GAIN,
    ATTENTION_SHIFT,
    SOURCE_QUERY_BIAS,
    SOURCE_VALUE_BIAS,
    SOURCE_OUTPUT_BIAS,
    SOURCE_GAIN,
    SOURCE_SHIFT,
    OUTER_BIAS,
    FINAL_GAIN,
    FINAL_SHIFT,
    INNER_BIAS,
) = range(12)
Z_MASKS = (0, 8, 16, 24)
VM = pl.BlockSpec(memory_space=pltpu.VMEM)
SM = pl.BlockSpec(memory_space=pltpu.SMEM)


def dot(a, b):
    return lax.dot_general(a, b, (((1,), (0,)), ((), ())), preferred_element_type=F32)


def dot_nt(a, b):
    return lax.dot_general(a, b, (((1,), (1,)), ((), ())), preferred_element_type=F32)


def dot_tn(a, b):
    return lax.dot_general(a, b, (((0,), (0,)), ((), ())), preferred_element_type=F32)


def total(values):
    return jnp.sum(values.astype(F32), axis=0, keepdims=True)


def normalize(h):
    average = jnp.mean(h, axis=-1, keepdims=True)
    centered = h - average
    variance = jnp.mean(centered * centered, axis=-1, keepdims=True)
    inverse = lax.rsqrt(variance + EPSILON)
    return centered * inverse, inverse


def normalize_back(upstream, normed, inverse, gain):
    scaled = upstream * gain
    first_mean = jnp.mean(scaled, axis=-1, keepdims=True)
    second_mean = jnp.mean(scaled * normed, axis=-1, keepdims=True)
    return inverse * (scaled - first_mean - normed * second_mean)


def normal_parts(v):
    density = 0.3989422804014327 * jnp.exp(-0.5 * v * v)
    t = 1.0 / (1.0 + 0.2316419 * jnp.abs(v))
    series = t * (
        0.319381530
        + t * (-0.356563782 + t * (1.781477937 + t * (-1.821255978 + t * 1.330274429)))
    )
    tail = density * series
    return jnp.where(v >= 0.0, 1.0 - tail, tail), density


def penalties(ids):
    place = lax.broadcasted_iota(jnp.int32, (PAIR, ids.shape[1]), 0)
    return jnp.where((place == ids) | (place >= 4), 0.0, -MASKED).astype(BF16)


def one_hot(ids):
    place = lax.broadcasted_iota(jnp.int32, (PAIR, ids.shape[1]), 0)
    return jnp.where(place == ids, 1.0, 0.0).astype(F32).T.astype(BF16)


def spread(part, half):
    empty = jnp.zeros_like(part)
    return [part, empty] if half == 0 else [empty, part]


def attend(query_t, keys, value_t, hot, penalty, mixture_t, logs):
    length = keys.shape[0]

    def pair(p, carry):
        columns = pl.ds(pl.multiple_of(p * PAIR, PAIR), PAIR)
        left = jnp.concatenate([keys[:, columns], hot[...]], axis=1)
        for half in range(2):
            rows = pl.ds(pl.multiple_of(p * PAIR + half * HEAD_DIM, HEAD_DIM), HEAD_DIM)
            right = jnp.concatenate(spread(query_t[rows, :], half) + [penalty[...]], axis=0)
            scores = dot(left, right)
            highest = jnp.max(scores, axis=0, keepdims=True)
            weights = jnp.exp(scores - highest).astype(BF16)
            values = jnp.concatenate(
                [value_t[rows, :], jnp.ones((16, length), BF16)], axis=0
            )
            found = dot(values, weights)
            denominator = found[HEAD_DIM : HEAD_DIM + 1, :]
            mixture_t[rows, :] = (found[:HEAD_DIM, :] / denominator).astype(BF16)
            logs[2 * p + half] = highest + jnp.log(denominator)
        return carry

    lax.fori_loop(0, keys.shape[1] // PAIR, pair, 0)


def attend_back(
    query_t, query, keys, key_t, values, slope_t, slope, hot, penalty, logs, deltas,
    query_grad_t, key_grad, value_grad,
):
    tokens = query.shape[0]
    lane = lax.broadcasted_iota(jnp.int32, (tokens, PAIR), 1)

    def pair(p, carry):
        columns = pl.ds(pl.multiple_of(p * PAIR, PAIR), PAIR)
        left = jnp.concatenate([keys[:, columns], hot[...]], axis=1)
        value_pair = values[:, columns]
        key_sum, value_sum = None, None
        for half in range(2):
            rows = pl.ds(pl.multiple_of(p * PAIR + half * HEAD_DIM, HEAD_DIM), HEAD_DIM)
            right = jnp.concatenate(spread(query_t[rows, :], half) + [penalty[...]], axis=0)
            chances = jnp.exp(dot(left, right) - logs[2 * p + half])
            slopes = dot(value_pair, jnp.concatenate(spread(slope_t[rows, :], half), axis=0))
            grads = (chances * (slopes - deltas[2 * p + half])).astype(BF16)
            query_grad_t[rows, :] = dot(key_t[rows, :], grads) * HEAD_DIM**-0.5
            mine = (lane < HEAD_DIM) if half == 0 else (lane >= HEAD_DIM)
            none = jnp.zeros((tokens, PAIR), BF16)
            value_part = dot(chances.astype(BF16), jnp.where(mine, slope[:, columns], none))
            key_part = dot(grads, jnp.where(mine, query[:, columns], none))
            value_sum = value_part if value_sum is None else value_sum + value_part
            key_sum = key_part if key_sum is None else key_sum + key_part
        key_grad[:, columns] = key_sum
        value_grad[:, columns] = value_sum
        return carry

    lax.fori_loop(0, keys.shape[1] // PAIR, pair, 0)


def deltas_of(slope_t, mixture_t, deltas):
    for head in range(slope_t.shape[0] // HEAD_DIM):
        rows = slice(head * HEAD_DIM, (head + 1) * HEAD_DIM)
        deltas[head] = jnp.sum(
            slope_t[rows, :].astype(F32) * mixture_t[rows, :].astype(F32), axis=0, keepdims=True
        )


def swap(array, mask, devices):
    return lax.ppermute(array, AXES, [(i, i ^ mask) for i in range(devices)])


ORDERS = ((8, 16, 2, 4), (16, 8, 4, 2))


def turned_swap(array, step):
    return lax.ppermute(array, AXES, [(i, i ^ ORDERS[i % 2][step]) for i in range(32)])


def after(value, *others):
    return lax.optimization_barrier((value, others))[0]


def places(me):
    found = []
    for core in range(2):
        even = ((me & 1) ^ core) == 0
        masks = [jnp.where(even, first, second) for first, second in zip(*ORDERS)]
        for far in range(2):
            for slot in range(8):
                device = me ^ core if core else me
                for step, bit in enumerate((slot & 1, slot & 2, slot & 4, far)):
                    if bit:
                        device = device ^ masks[step]
                found.append((core, far, slot, device))
    return found


def unpack(me, pieces, stride, first, rows, scratch):
    for core, far, slot, device in places(me):
        ref = pieces[2 * core + far]
        at = slot * stride + first
        scratch[pl.ds(pl.multiple_of(device * rows, rows), rows), :] = ref[at : at + rows, :]


def vector_sum(pieces, stride, first):
    found = None
    for ref in pieces:
        for slot in range(8):
            part = ref[slot * stride + first : (slot + 1) * stride, :].astype(F32)
            found = part if found is None else found + part
    return found


class Grads:
    def __init__(self, me, refs, dense, rows):
        self.me, self.refs, self.dense, self.rows = me, refs, dense, rows

    def put(self, index, grad):
        if self.dense is None:
            self.refs[index][...] = grad
            return
        self.dense[...] = grad
        rows = self.rows
        for core, far, slot, device in places(self.me):
            found = self.dense[pl.ds(pl.multiple_of(device * rows, rows), rows), :]
            self.refs[core][far * 8 + slot, index * rows : (index + 1) * rows, :] = found.astype(BF16)

    def put_sums(self, first, sums):
        if self.dense is None:
            self.refs[-1][...] = sums
            return
        low = sums.astype(BF16)
        for ref in self.refs:
            for slot in range(16):
                ref[slot, first : first + sums.shape[0], :] = low


def grad_outs(packed, count, rows, width, sums):
    if packed:
        return [((16, count * rows + sums, width), BF16)] * 2
    return [((width, width), F32)] * count + [((sums, width), F32)]


COSTS = {"self_attention": 8.0}


def padded(shape, dtype):
    last = -(-shape[-1] // 128) * 128
    tall = -(-shape[-2] // 16) * 16 if len(shape) > 1 else 16
    return math.prod(shape[:-2]) * tall * last * jnp.dtype(dtype).itemsize


def snug(arrays):
    return 2 * sum(padded(a.shape, a.dtype) for a in arrays) + (3 << 20)


def call(kernel, outs, args, scratch, micros, name, room=10):
    moved = sum(math.prod(a.shape) * a.dtype.itemsize for a in args[1:])
    moved += sum(math.prod(s) * jnp.dtype(d).itemsize for s, d in outs)
    need = sum(padded(a.shape, a.dtype) for a in args[1:])
    need += sum(padded(s, d) for s, d in list(outs) + list(scratch))
    return pl.pallas_call(
        kernel,
        out_shape=[jax.ShapeDtypeStruct(s, d) for s, d in outs],
        in_specs=[SM] + [VM] * (len(args) - 1),
        out_specs=[VM] * len(outs),
        scratch_shapes=[pltpu.VMEM(s, d) for s, d in scratch],
        compiler_params=pltpu.CompilerParams(vmem_limit_bytes=min(need + (room << 20), 58 << 20)),
        cost_estimate=pl.CostEstimate(
            flops=int(COSTS.get(name, 0) * 1.15e9) + 1, bytes_accessed=1, transcendentals=0
        ),
        name=name,
    )(*args)


def tokens_packet(turn, tokens, memory, target_ids, source_ids, cotangent):
    block, width = tokens.shape[1:]
    memory_block = memory.shape[1]
    first = block + memory_block + 8

    def kernel(turn_ref, targets, sources, tokens_ref, memory_ref, cot_ref, sent, kept):
        mine = turn_ref[0]
        for row, out in ((1 - mine, sent), (mine, kept)):
            out[:block, :] = tokens_ref[row]
            out[block : block + memory_block, :] = memory_ref[row]
            ids = targets[pl.ds(row, 1), :].astype(F32)
            ids = jnp.concatenate([ids, jnp.zeros((1, width - block), F32)], axis=1)
            others = sources[pl.ds(row, 1), :].astype(F32)
            others = jnp.concatenate([others, jnp.zeros((1, width - memory_block), F32)], axis=1)
            place = lax.broadcasted_iota(jnp.int32, (8, width), 0)
            found = jnp.where(place == 0, ids, jnp.where(place == 1, others, 0.0))
            out[block + memory_block : first, :] = found.astype(BF16)
            out[first:, :] = cot_ref[row]

    shape = (first + block, width)
    return call(kernel, [(shape, BF16)] * 2, (turn, target_ids, source_ids, tokens, memory, cotangent),
                [], 1.0, "tokens_packet", 58)


def placed(me, parts, width):
    here = lax.broadcasted_iota(jnp.int32, (parts.shape[1], width), 0) + me * parts.shape[1]
    lane = lax.broadcasted_iota(jnp.int32, (parts.shape[1], width), 1)
    return dot(parts, jnp.where(lane == here, 1.0, 0.0).astype(BF16))


def make_weights_packet(narrow, width, blocks):
    tall = blocks * narrow

    def kernel(me_ref, *refs):
        weights, inner, outer, wide, short = refs[:8], refs[8], refs[9], refs[10], refs[11:24]
        first, rest = refs[24:]
        me, middle = me_ref[0], 5 * narrow + 16
        for i, ref in enumerate(weights):
            if i < 3:
                first[i * narrow : (i + 1) * narrow, :] = ref[...]
            else:
                rest[(i - 3) * narrow : (i - 2) * narrow, :] = ref[...]
        short = jnp.concatenate([ref[...].astype(F32) for ref in short], axis=0).astype(BF16)
        found = placed(me, short, width)
        first[3 * narrow :, :] = jnp.concatenate([found[:2, :], jnp.zeros((6, width), F32)], axis=0).astype(BF16)
        per = width // wide.shape[1]
        row = placed(lax.rem(me, per), wide[...], width)
        place = lax.broadcasted_iota(jnp.int32, (blocks, width), 0)
        spread_row = jnp.where(place == lax.div(me, per), row, 0.0)
        none = jnp.zeros((16 - (found.shape[0] - 2) - blocks, width), F32)
        rest[5 * narrow : middle, :] = jnp.concatenate([found[2:, :], spread_row, none], axis=0).astype(BF16)
        for i in range(blocks):
            rest[middle + i * narrow : middle + (i + 1) * narrow, :] = inner[:, i * width : (i + 1) * width]
        rest[middle + tall :, :] = outer[...]

    return kernel, [((rows, width), BF16) for rows in (3 * narrow + 8, 5 * narrow + 16 + 2 * tall)]


def make_part(sizes, width):
    tall = sum(sizes)

    def kernel(me_ref, upper, lower, *outs):
        for i in range(4):
            ref, at = (upper, lower)[i // 2], i % 2 * tall
            for size, out in zip(sizes, outs):
                out[i * size : (i + 1) * size, :] = ref[at : at + size, :]
                at += size

    return kernel, [((4 * size, width), BF16) for size in sizes]


def join(arrays):
    def kernel(*refs):
        at = 0
        for ref in refs[:-1]:
            refs[-1][at : at + ref.shape[0], :] = ref[...]
            at += ref.shape[0]

    rows = sum(a.shape[0] for a in arrays)
    return pl.pallas_call(
        kernel,
        out_shape=jax.ShapeDtypeStruct((rows, arrays[0].shape[1]), arrays[0].dtype),
        in_specs=[VM] * len(arrays),
        out_specs=VM,
        compiler_params=pltpu.CompilerParams(vmem_limit_bytes=snug(arrays)),
        cost_estimate=pl.CostEstimate(flops=1 << 20, bytes_accessed=0, transcendentals=0),
        name="join",
    )(*arrays)


def make_project(packed, parts, rows, block, memory_block, width, narrow, n_pieces):
    share = rows * block
    length = parts * share
    memory_share = rows * memory_block
    stride = 3 * narrow + 8
    half = width // 2

    def kernel(*refs):
        me_ref, refs = refs[0], list(refs[1:])
        pieces, refs = refs[:n_pieces], refs[n_pieces:]
        tokens, refs = refs[: parts * rows], refs[parts * rows :]
        query, query_t, keys, values, value_t = (refs[2 * i : 2 * i + 2] for i in range(5))
        memory, ids, memory_ids = refs[10:13]
        scratch = refs[13:]
        me = me_ref[0]
        if packed:
            for i in range(3):
                unpack(me, pieces, stride, i * narrow, narrow, scratch[i])
            query_w, key_w, value_w = scratch
            biases = vector_sum(pieces, stride, 3 * narrow)
        else:
            query_w, key_w, value_w = pieces[:3]
            biases = pieces[3][...]
        for i in range(parts):
            here = slice(i * share, (i + 1) * share)
            some = tokens[i * rows : (i + 1) * rows]
            own = jnp.concatenate([t[:block, :] for t in some], axis=0)
            if i == 0:
                scaled = (dot(own, query_w[...]) + biases[0:1, :]).astype(BF16) * BF16(HEAD_DIM**-0.5)
            key = dot(own, key_w[...]).astype(BF16)
            found = (dot(own, value_w[...]) + biases[1:2, :]).astype(BF16)
            for side in range(2):
                columns = slice(side * half, (side + 1) * half)
                if i == 0:
                    query[side][...] = scaled[:, columns]
                    query_t[side][...] = scaled[:, columns].T
                keys[side][here, :] = key[:, columns]
                values[side][here, :] = found[:, columns]
                value_t[side][:, here] = found[:, columns].T
        for i, t in enumerate(tokens):
            memory[i * memory_block : (i + 1) * memory_block, :] = t[block : block + memory_block, :]
            found = t[block + memory_block : block + memory_block + 8, :].astype(F32).astype(jnp.int32)
            ids[:, i * block : (i + 1) * block] = found[0:1, :block]
        found = [t[block + memory_block : block + memory_block + 8, :].astype(F32).astype(jnp.int32)[1:2, :memory_block] for t in tokens]
        memory_ids[...] = jnp.concatenate(found, axis=1)

    outs = [((share, half), BF16)] * 2 + [((half, share), BF16)] * 2
    outs += [((length, half), BF16)] * 4 + [((half, length), BF16)] * 2
    outs += [
        ((parts * memory_share, width), BF16),
        ((1, length), jnp.int32),
        ((1, parts * memory_share), jnp.int32),
    ]
    return kernel, outs, [((width, width), BF16)] * 3 if packed else []


def make_self_attention(share, length, width):
    def kernel(me_ref, *refs):
        query_t, keys, value_t, ids = refs[:2], refs[2:4], refs[4:6], refs[6]
        mixture_t, logs, hot, penalty = refs[7:9], refs[9:11], refs[11], refs[12]
        hot[...] = one_hot(ids[...])
        penalty[...] = penalties(ids[:, :share])
        for side in range(2):
            attend(query_t[side], keys[side], value_t[side], hot, penalty, mixture_t[side], logs[side])

    outs = [((width // 2, share), BF16)] * 2 + [((HEADS // 2, 1, share), F32)] * 2
    return kernel, outs, [((length, PAIR), BF16), ((PAIR, share), BF16)]


def make_cross_forward(packed, rows, block, memory_length, width, narrow, n_pieces):
    share = rows * block
    stride = 5 * narrow + 16

    def kernel(*refs):
        me_ref, refs = refs[0], list(refs[1:])
        pieces, refs = refs[:n_pieces], refs[n_pieces:]
        tokens, refs = refs[:rows], refs[rows:]
        memory, ids, memory_ids, upper, lower = refs[:5]
        first_sum, second_sum, query, memory_keys, memory_values, cross_t, logs, vectors = refs[5:13]
        scratch = refs[13:]
        query_t, value_t, hot, penalty = scratch[:4]
        if packed:
            for i in range(5):
                unpack(me_ref[0], pieces, stride, i * narrow, narrow, scratch[4 + i])
            output_w, query_w, key_w, value_w, source_w = scratch[4:]
            vectors[...] = vector_sum(pieces, stride, 5 * narrow)
        else:
            output_w, query_w, key_w, value_w, source_w = pieces[:5]
            vectors[...] = pieces[5][...]

        def vector(i):
            return vectors[i : i + 1, :]

        own = jnp.concatenate([t[:block, :] for t in tokens], axis=0)
        mixture_t = jnp.concatenate([upper[...], lower[...]], axis=0)
        h = own.astype(F32) + dot_tn(mixture_t, output_w[...]) + vector(OUTPUT_BIAS)
        first_sum[...] = h
        first = normalize(h)[0] * vector(ATTENTION_GAIN) + vector(ATTENTION_SHIFT)
        scaled = (dot(first.astype(BF16), query_w[...]) + vector(SOURCE_QUERY_BIAS)).astype(BF16) * BF16(HEAD_DIM**-0.5)
        query[...] = scaled
        query_t[...] = scaled.T
        memory_keys[...] = dot(memory[...], key_w[...]).astype(BF16)
        memory_values[...] = (dot(memory[...], value_w[...]) + vector(SOURCE_VALUE_BIAS)).astype(BF16)
        value_t[...] = memory_values[...].T
        hot[...] = one_hot(memory_ids[...])
        penalty[...] = penalties(ids[:, :share])
        attend(query_t, memory_keys, value_t, hot, penalty, cross_t, logs)
        first = normalize(first_sum[...])[0] * vector(ATTENTION_GAIN) + vector(ATTENTION_SHIFT)
        second_sum[...] = first + dot_tn(cross_t[...], source_w[...]) + vector(SOURCE_OUTPUT_BIAS)

    outs = [
        ((share, width), F32),
        ((share, width), F32),
        ((share, width), BF16),
        ((memory_length, width), BF16),
        ((memory_length, width), BF16),
        ((width, share), BF16),
        ((HEADS, 1, share), F32),
        ((16, width), F32),
    ]
    scratch = [((width, share), BF16), ((width, memory_length), BF16), ((memory_length, PAIR), BF16), ((PAIR, share), BF16)]
    if packed:
        scratch += [((width, width), BF16)] * 5
    return kernel, outs, scratch


def make_inner(packed, rows, block, width, hidden, narrow, n_pieces):
    blocks = hidden // width
    share = rows * block
    per = width // (blocks * narrow)

    def kernel(*refs):
        me_ref, refs = refs[0], list(refs[1:])
        pieces, refs = refs[:n_pieces], refs[n_pieces:]
        second_sum, cot_own, cot_came, vectors = refs[:4]
        out_own, out_send, back, sums = refs[4:8]
        grads, scratch = refs[8:10], refs[10:]
        low, active, gate, slope = scratch[:4]
        if packed:
            inner_w, outer_w, gathered, dense = scratch[4:8]
            tall = blocks * narrow
            for core, far, slot, device in places(me_ref[0]):
                ref, at = pieces[2 * core + far], slot * 2 * tall
                row = pl.multiple_of(device * narrow, narrow)
                for i in range(blocks):
                    inner_w[i, pl.ds(row, narrow), :] = ref[at + i * narrow : at + (i + 1) * narrow, :]
                row = pl.multiple_of(lax.rem(device, per) * tall, tall)
                outer_w[lax.div(device, per), pl.ds(row, tall), :] = ref[at + tall : at + 2 * tall, :]
        else:
            inner_w, outer_w = pieces

        def vector(i):
            return vectors[i : i + 1, :]

        second = normalize(second_sum[...])[0] * vector(SOURCE_GAIN) + vector(SOURCE_SHIFT)
        low[...] = second.astype(BF16)
        back[...] = second + vector(OUTER_BIAS)

        def forward(i, carry):
            inner = dot(low[...], inner_w[i]) + vectors[pl.ds(INNER_BIAS + i, 1), :]
            chance, density = normal_parts(inner)
            found = (inner * chance).astype(BF16)
            active[i] = found
            gate[i] = chance + inner * density
            back[...] += dot(found, outer_w[i])
            return carry

        lax.fori_loop(0, blocks, forward, 0)
        normed, inverse = normalize(back[...])
        final = normed * vector(FINAL_GAIN) + vector(FINAL_SHIFT)
        out_own[...] = final[:block, :]
        out_send[...] = final[block:, :].astype(BF16)
        upstream = jnp.concatenate([cot_own[-block:, :], cot_came[-block:, :]], axis=0).astype(F32)
        sums[0:1, :] = total(upstream * normed)
        sums[1:2, :] = total(upstream)
        back3 = normalize_back(upstream, normed, inverse, vector(FINAL_GAIN))
        slope[...] = back3.astype(BF16)
        sums[2:3, :] = total(slope[...])
        sums[7:8, :] = jnp.zeros_like(sums[7:8, :])
        back[...] = back3

        def backward(i, carry):
            grad = dot_nt(slope[...], outer_w[i]) * gate[i]
            inner_low = grad.astype(BF16)
            sums[pl.ds(3 + i, 1), :] = total(inner_low)
            outer_grad = dot_tn(active[i], slope[...])
            inner_grad = dot_tn(low[...], inner_low)
            back[...] += dot_nt(inner_low, inner_w[i])
            if packed:
                dense[...] = inner_grad
                gathered[i] = outer_grad.astype(BF16)
                here = pl.ds(pl.multiple_of(i * narrow, narrow), narrow)
                for core, far, slot, device in places(me_ref[0]):
                    row = pl.multiple_of(device * narrow, narrow)
                    grads[core][far * 8 + slot, here, :] = dense[pl.ds(row, narrow), :].astype(BF16)
            else:
                grads[0][i] = inner_grad
                grads[1][i] = outer_grad
            return carry

        lax.fori_loop(0, blocks, backward, 0)
        if packed:
            tall = blocks * narrow
            for core, far, slot, device in places(me_ref[0]):
                row = pl.multiple_of(lax.rem(device, per) * tall, tall)
                grads[core][far * 8 + slot, tall:, :] = gathered[lax.div(device, per), pl.ds(row, tall), :]

    outs = [((block, width), F32), ((block, width), BF16), ((share, width), F32), ((8, width), F32)]
    if packed:
        outs += [((16, 2 * blocks * narrow, width), BF16)] * 2
    else:
        outs += [((blocks, width, width), F32)] * 2
    scratch = [((share, width), BF16), ((blocks, share, width), BF16), ((blocks, share, width), F32), ((share, width), BF16)]
    if packed:
        scratch += [((blocks, width, width), BF16)] * 3 + [((width, width), F32)]
    return kernel, outs, scratch


def make_cross_back(packed, parts, share, memory_share, width, narrow, n_pieces):
    memory_length = parts * memory_share
    stride = 5 * narrow + 16

    def kernel(*refs):
        me_ref, refs = refs[0], list(refs[1:])
        pieces, refs = refs[:n_pieces], refs[n_pieces:]
        (back2_in, first_sum, second_sum, query, memory_keys, memory_values, cross_t, logs, ids,
         memory_ids, vectors, sums_inner) = refs[:12]
        mixtures, refs = refs[12:14], refs[14:]
        back1, key_own, value_own, sums = refs[:4]
        self_slope, self_slope_t, self_deltas = (refs[4 + 2 * i : 6 + 2 * i] for i in range(3))
        sends, refs = refs[10 : 10 + parts - 1], refs[10 + parts - 1 :]
        grads, scratch = refs[:3], refs[3:]
        (slope_t, slope, key_t, hot, penalty, query_t, deltas, query_grad_t, key_grad, value_grad) = scratch[:10]
        upper, lower = mixtures
        if packed:
            for i, at in enumerate((0, 1, 4)):
                unpack(me_ref[0], pieces, stride, at * narrow, narrow, scratch[10 + i])
            output_w, query_w, source_w = scratch[10:13]
        else:
            output_w, query_w, source_w = pieces

        def vector(i):
            return vectors[i : i + 1, :]

        sums[0:7, :] = sums_inner[0:7, :]
        upstream = back2_in[...]
        normed, inverse = normalize(second_sum[...])
        sums[7:8, :] = total(upstream * normed)
        sums[8:9, :] = total(upstream)
        back2 = normalize_back(upstream, normed, inverse, vector(SOURCE_GAIN))
        back1[...] = back2
        cross_low = back2.astype(BF16)
        sums[9:10, :] = total(cross_low)
        grads[0][...] = dot(cross_t[...], cross_low).astype(BF16)
        found = dot_nt(cross_low, source_w[...]).astype(BF16)
        slope[...] = found
        slope_t[...] = found.T
        deltas_of(slope_t, cross_t, deltas)
        query_t[...] = query[...].T
        key_t[...] = memory_keys[...].T
        hot[...] = one_hot(memory_ids[...])
        penalty[...] = penalties(ids[:, :share])
        attend_back(query_t, query, memory_keys, key_t, memory_values, slope_t, slope, hot, penalty,
                    logs, deltas, query_grad_t, key_grad, value_grad)
        key_own[...] = key_grad[:memory_share, :]
        value_own[...] = value_grad[:memory_share, :]
        for i in range(1, parts):
            here = slice(i * memory_share, (i + 1) * memory_share)
            sends[i - 1][:memory_share, :] = key_grad[here, :].astype(BF16)
            sends[i - 1][memory_share:, :] = value_grad[here, :].astype(BF16)
        query_low = query_grad_t[...].T.astype(BF16)
        sums[10:11, :] = total(query_low)
        normed, inverse = normalize(first_sum[...])
        first_low = (normed * vector(ATTENTION_GAIN) + vector(ATTENTION_SHIFT)).astype(BF16)
        grads[1][...] = dot_tn(first_low, query_low).astype(BF16)
        upstream = back1[...] + dot_nt(query_low, query_w[...])
        sums[11:12, :] = total(upstream * normed)
        sums[12:13, :] = total(upstream)
        grad = normalize_back(upstream, normed, inverse, vector(ATTENTION_GAIN))
        back1[...] = grad
        branch_low = grad.astype(BF16)
        sums[13:14, :] = total(branch_low)
        sums[14:16, :] = jnp.zeros_like(sums[14:16, :])
        mixture_t = jnp.concatenate([upper[...], lower[...]], axis=0)
        grads[2][...] = dot(mixture_t, branch_low).astype(BF16)
        found = dot_nt(branch_low, output_w[...]).astype(BF16)
        for side in range(2):
            columns = slice(side * width // 2, (side + 1) * width // 2)
            self_slope[side][...] = found[:, columns]
            self_slope_t[side][...] = found[:, columns].T
            deltas_of(self_slope_t[side], mixtures[side], self_deltas[side])

    half = width // 2
    outs = [
        ((share, width), F32),
        ((memory_share, width), F32),
        ((memory_share, width), F32),
        ((16, width), F32),
    ]
    outs += [((share, half), BF16)] * 2 + [((half, share), BF16)] * 2
    outs += [((HEADS // 2, 1, share), F32)] * 2
    outs += [((2 * memory_share, width), BF16)] * (parts - 1)
    outs += [((width, width), BF16)] * 3
    scratch = [
        ((width, share), BF16),
        ((share, width), BF16),
        ((width, memory_length), BF16),
        ((memory_length, PAIR), BF16),
        ((PAIR, share), BF16),
        ((width, share), BF16),
        ((HEADS, 1, share), F32),
        ((width, share), F32),
        ((memory_length, width), F32),
        ((memory_length, width), F32),
    ]
    if packed:
        scratch += [((width, width), BF16)] * 3
    return kernel, outs, scratch


def attention_back_half(refs, share, scratch):
    query, keys, values, slope, slope_t, logs, deltas, ids = refs
    query_t, key_t, hot, penalty, query_grad_t, key_grad, value_grad = scratch
    query_t[...] = query[...].T
    key_t[...] = keys[...].T
    hot[...] = one_hot(ids[...])
    penalty[...] = penalties(ids[:, :share])
    attend_back(query_t, query, keys, key_t, values, slope_t, slope, hot, penalty, logs, deltas,
                query_grad_t, key_grad, value_grad)


def half_scratch(share, length, half):
    return [
        ((half, share), BF16),
        ((half, length), BF16),
        ((length, PAIR), BF16),
        ((PAIR, share), BF16),
        ((half, share), F32),
        ((length, half), F32),
        ((length, half), F32),
    ]


def give_half(share, scratch, own, sends):
    key_grad, value_grad = scratch[5:7]
    own[:share, :] = key_grad[:share, :]
    own[share:, :] = value_grad[:share, :]
    for i, send in enumerate(sends):
        here = slice((i // 2 + 1) * share, (i // 2 + 2) * share)
        send[...] = (key_grad, value_grad)[i % 2][here, :].astype(BF16)


def make_memory_back(packed, parts, rows, block, memory_block, width, narrow, n_pieces):
    memory_share = rows * memory_block

    def kernel(*refs):
        me_ref, refs = refs[0], list(refs[1:])
        pieces, refs = refs[:n_pieces], refs[n_pieces:]
        tokens, refs = refs[:rows], refs[rows:]
        memory_key_own, memory_value_own, sums_in = refs[:3]
        early, refs = refs[3:6], refs[6:]
        memory_received, refs = refs[: parts - 1], refs[parts - 1 :]
        memory_own, memory_send = refs[:2]
        n_grads = 2 if packed else 3
        grad_refs, scratch = refs[2 : 2 + n_grads], refs[2 + n_grads :]
        sums = scratch[0]
        me = me_ref[0]
        if packed:
            for i in range(2):
                unpack(me, pieces, 5 * narrow + 16, (2 + i) * narrow, narrow, scratch[1 + i])
            source_key, source_value = scratch[1:3]
        else:
            source_key, source_value = pieces
        grads = Grads(me, grad_refs, scratch[3] if packed else None, narrow)
        memory = jnp.concatenate([t[block : block + memory_block, :] for t in tokens], axis=0)
        key_sum, value_sum = memory_key_own[...], memory_value_own[...]
        for ref in memory_received:
            key_sum = key_sum + ref[:memory_share, :].astype(F32)
            value_sum = value_sum + ref[memory_share:, :].astype(F32)
        key_low, value_low = key_sum.astype(BF16), value_sum.astype(BF16)
        sums[...] = sums_in[...]
        sums[14:15, :] = total(value_low)
        grads.put_sums(5 * narrow, sums[...])
        grads.put(0, dot_tn(memory, key_low))
        grads.put(1, dot_tn(memory, value_low))
        if packed:
            for i, ref in enumerate(early):
                grads.put(2 + i, ref[...].astype(F32))
        grad = dot_nt(key_low, source_key[...]) + dot_nt(value_low, source_value[...])
        memory_own[...] = grad[:memory_block, :]
        memory_send[...] = grad[memory_block:, :].astype(BF16)

    outs = [((memory_block, width), F32), ((memory_block, width), BF16)]
    if packed:
        outs += [((16, 5 * narrow + 16, width), BF16)] * 2
    else:
        outs += [((width, width), F32)] * 2 + [((16, width), F32)]
    scratch = [((16, width), F32)]
    if packed:
        scratch += [((width, width), BF16)] * 2 + [((width, width), F32)]
    return kernel, outs, scratch


def make_self_back_upper(parts, share, width):
    length, half = parts * share, width // 2

    def kernel(*refs):
        operands, (query_grad, own), refs = refs[1:9], refs[9:11], refs[11:]
        sends, scratch = refs[: 2 * parts - 2], refs[2 * parts - 2 :]
        attention_back_half(operands, share, scratch)
        query_grad[...] = scratch[4][...].T.astype(BF16)
        give_half(share, scratch, own, sends)

    outs = [((share, half), BF16), ((2 * share, half), F32)] + [((share, half), BF16)] * (2 * parts - 2)
    return kernel, outs, half_scratch(share, length, half)


def make_self_back_lower(packed, parts, rows, block, width, narrow, n_pieces):
    share = rows * block
    length, half = parts * share, width // 2

    def kernel(*refs):
        me_ref, refs = refs[0], list(refs[1:])
        pieces, refs = refs[:n_pieces], refs[n_pieces:]
        tokens, refs = refs[:rows], refs[rows:]
        operands, refs = refs[:8], refs[8:]
        back1, query_upper = refs[:2]
        in_part, query_sum, query_w_grad, own = refs[2:6]
        sends, scratch = refs[6 : 4 + 2 * parts], refs[4 + 2 * parts :]
        if packed:
            unpack(me_ref[0], pieces, 3 * narrow + 8, 0, narrow, scratch[7])
            query_w = scratch[7]
        else:
            (query_w,) = pieces
        attention_back_half(operands, share, scratch[:7])
        give_half(share, scratch, own, sends)
        query_low = jnp.concatenate([query_upper[...], scratch[4][...].T.astype(BF16)], axis=1)
        tokens_own = jnp.concatenate([t[:block, :] for t in tokens], axis=0)
        in_part[...] = back1[...] + dot_nt(query_low, query_w[...])
        query_sum[...] = jnp.concatenate([total(query_low), jnp.zeros((7, width), F32)], axis=0)
        query_w_grad[...] = dot_tn(tokens_own, query_low).astype(query_w_grad.dtype)

    outs = [
        ((share, width), F32),
        ((8, width), F32),
        ((width, width), BF16 if packed else F32),
        ((2 * share, half), F32),
    ]
    outs += [((share, half), BF16)] * (2 * parts - 2)
    scratch = half_scratch(share, length, half)
    if packed:
        scratch += [((width, width), BF16)]
    return kernel, outs, scratch


def make_last(packed, parts, rows, block, memory_block, width, narrow, n_pieces):
    share = rows * block

    def kernel(*refs):
        me_ref, refs = refs[0], list(refs[1:])
        pieces, refs = refs[:n_pieces], refs[n_pieces:]
        tokens, refs = refs[:rows], refs[rows:]
        in_part, query_sum, query_w_grad, memory_send = refs[:4]
        owns, refs = refs[4:6], refs[6:]
        received = [refs[: 2 * parts - 2], refs[2 * parts - 2 : 4 * parts - 4]]
        refs = refs[4 * parts - 4 :]
        in_own, in_send = refs[:2]
        n_grads = 2 if packed else 3
        grad_refs, scratch = refs[2 : 2 + n_grads], refs[2 + n_grads :]
        sums = scratch[0]
        me = me_ref[0]
        if packed:
            for i in range(2):
                unpack(me, pieces, 3 * narrow + 8, (1 + i) * narrow, narrow, scratch[1 + i])
            key_w, value_w = scratch[1:3]
        else:
            key_w, value_w = pieces
        grads = Grads(me, grad_refs, scratch[3] if packed else None, narrow)
        if packed:
            grads.put(2, query_w_grad[...].astype(F32))
        lows = []
        for own, others in zip(owns, received):
            found = own[...]
            for key, value in zip(others[::2], others[1::2]):
                found = found + jnp.concatenate([key[...], value[...]], axis=0).astype(F32)
            lows.append(found.astype(BF16))
        key_low = jnp.concatenate([low[:share, :] for low in lows], axis=1)
        value_low = jnp.concatenate([low[share:, :] for low in lows], axis=1)
        tokens_own = jnp.concatenate([t[:block, :] for t in tokens], axis=0)
        sums[...] = query_sum[...]
        sums[1:2, :] = total(value_low)
        grads.put_sums(3 * narrow, sums[...])
        grads.put(0, dot_tn(tokens_own, key_low))
        grads.put(1, dot_tn(tokens_own, value_low))
        grad = in_part[...] + dot_nt(key_low, key_w[...]) + dot_nt(value_low, value_w[...])
        in_own[...] = grad[:block, :]
        in_send[:block, :] = grad[block:, :].astype(BF16)
        in_send[block:, :] = memory_send[...]

    outs = [((block, width), F32), ((block + memory_block, width), BF16)]
    if packed:
        outs += [((16, 3 * narrow + 8, width), BF16)] * 2
    else:
        outs += [((width, width), F32)] * 2 + [((8, width), F32)]
    scratch = [((8, width), F32)]
    if packed:
        scratch += [((width, width), BF16)] * 2 + [((width, width), F32)]
    return kernel, outs, scratch


def combine(arrays, splits, micros=0.1):
    count = arrays[0].shape[0] // splits
    shape = (count,) + arrays[0].shape[1:]

    def kernel(*refs):
        given, outs = refs[: len(arrays)], refs[len(arrays) :]
        for i, out in enumerate(outs):
            here = slice(i * count, (i + 1) * count)
            found = given[0][here].astype(F32)
            for ref in given[1:]:
                found = found + ref[here].astype(F32)
            out[...] = found.astype(out.dtype)

    return pl.pallas_call(
        kernel,
        out_shape=[jax.ShapeDtypeStruct(shape, BF16)] * splits,
        in_specs=[VM] * len(arrays),
        out_specs=[VM] * splits,
        compiler_params=pltpu.CompilerParams(vmem_limit_bytes=snug(arrays)),
        cost_estimate=pl.CostEstimate(flops=int(micros * 1.15e9), bytes_accessed=0, transcendentals=0),
        name="combine",
    )(*arrays)


def combine_joint(groups, splits):
    count, sizes = groups[0][0].shape[0] // splits, [g[0].shape[1] for g in groups]
    shape = (count, sum(sizes)) + groups[0][0].shape[2:]
    flat = [a for group in groups for a in group]

    def kernel(*refs):
        outs, at, row = refs[len(flat) :], 0, 0
        for group, size in zip(groups, sizes):
            given = refs[at : at + len(group)]
            at += len(group)
            for i, out in enumerate(outs):
                here = slice(i * count, (i + 1) * count)
                found = given[0][here].astype(F32)
                for ref in given[1:]:
                    found = found + ref[here].astype(F32)
                out[:, row : row + size, :] = found.astype(BF16)
            row += size

    return pl.pallas_call(
        kernel,
        out_shape=[jax.ShapeDtypeStruct(shape, BF16)] * splits,
        in_specs=[VM] * len(flat),
        out_specs=[VM] * splits,
        compiler_params=pltpu.CompilerParams(vmem_limit_bytes=snug(flat)),
        cost_estimate=pl.CostEstimate(flops=1, bytes_accessed=1, transcendentals=0),
        name="combine_joint",
    )(*flat)


def chosen(me, rows, wide):
    width = rows.shape[1]
    line = lax.broadcasted_iota(jnp.int32, (width, wide), 0)
    here = lax.broadcasted_iota(jnp.int32, (width, wide), 1) + me * wide
    choice = jnp.where(line == here, 1.0, 0.0)
    return lax.dot_general(rows, choice, (((1,), (0,)), ((), ())), precision=lax.Precision.HIGHEST, preferred_element_type=F32)


def reduce_all(array, devices):
    mask = 1
    while mask < devices:
        array = array + swap(array, mask, devices)
        mask *= 2
    return array


def per_device(
    tokens, memory, target_ids, source_ids, cotangent,
    query_weight, key_weight, value_weight, output_weight, query_bias, value_bias, output_bias,
    attention_gain, attention_shift,
    source_query, source_key, source_value, source_output, source_query_bias, source_value_bias,
    source_output_bias, source_gain, source_shift,
    inner_weight, inner_bias, outer_weight, outer_bias, final_gain, final_shift,
    *, devices, sequence,
):
    packed = devices == 32
    rows, block, width = tokens.shape
    memory_block = memory.shape[1]
    parts = sequence // rows
    share, memory_share = rows * block, rows * memory_block
    hidden = inner_weight.shape[1]
    blocks = hidden // width
    me = lax.axis_index(AXES)
    me_array = me.reshape(1).astype(jnp.int32)
    turn = lax.rem(lax.div(me, parts), rows)
    narrow, wide = width // devices, hidden // devices

    def run(made, micros, name, *args, room=10):
        kernel, outs, *scratch = made
        return call(kernel, outs, (me_array,) + args, scratch[0] if scratch else [], micros, name, room)

    short = [query_bias, value_bias, output_bias, attention_gain, attention_shift, source_query_bias,
             source_value_bias, source_output_bias, source_gain, source_shift, outer_bias, final_gain,
             final_shift]

    def whole(array):
        return lax.all_gather(array, AXES, axis=0, tiled=True)

    sent, kept = tokens_packet(
        turn.reshape(1).astype(jnp.int32), tokens, memory, target_ids, source_ids, cotangent
    )
    came = swap(sent, parts, devices)
    row_tokens = [kept, came]
    kept_swaps = [swap(kept, m, devices) for m in range(1, parts)]
    came_swaps = [swap(came, m, devices) for m in range(1, parts)]
    for pair in zip(kept_swaps, came_swaps):
        row_tokens += pair
    own_tokens = row_tokens[:rows]

    if packed:
        first, rest = run(make_weights_packet(narrow, width, blocks), 1.0, "weights_packet",
                          query_weight, key_weight, value_weight, output_weight, source_query,
                          source_key, source_value, source_output, inner_weight, outer_weight,
                          inner_bias.reshape(1, wide), *[v.reshape(1, narrow) for v in short], room=58)
        first = after(first, sent)
        first = join([first, turned_swap(first, 0)])
        first_b = turned_swap(first, 1)
        rest = after(rest, first)
        rest_b = turned_swap(rest, 0)
        first = join(after([first, first_b], rest_b))
        rest = join(after([rest, rest_b], first_b, came, *kept_swaps))
        first_b, rest_b = turned_swap(first, 2), turned_swap(rest, 1)
        first_c = join([first, first_b])
        first_d = turned_swap(first_c, 3)
        second, third = run(make_part((5 * narrow + 16, 2 * blocks * narrow), width), 1.0, "part", rest, rest_b)
        second_b, third_b = turned_swap(second, 2), turned_swap(third, 2)
        second_c = join([second, second_b])
        second_d = turned_swap(second_c, 3)
        first_d = after(first_d, second_c, *came_swaps)
        set_self = [first_c, first_d, swap(first_c, 1, 32), swap(first_d, 1, 32)]
    else:
        full = [whole(w) for w in (query_weight, key_weight, value_weight, output_weight, source_query, source_key, source_value, source_output)]
        lane = lax.broadcasted_iota(jnp.int32, (1, width), 1)
        place = lax.broadcasted_iota(jnp.int32, (blocks, width), 0) * width + lane
        spread_wide = jnp.where(place // wide == me, jnp.tile(inner_bias.reshape(1, wide), (blocks, width // wide)), 0)

        def natural(rows):
            return jnp.where(lane // narrow == me, jnp.tile(rows, (1, devices)), 0)

        vectors = jnp.concatenate([natural(jnp.stack(short[:2])), jnp.zeros((6, width), BF16), natural(jnp.stack(short[2:])), spread_wide, jnp.zeros((1, width), BF16)])
        vectors = reduce_all(vectors, devices).astype(F32)
        set_self = full[:3] + [vectors[:8]]
        set_cross = full[3:] + [vectors[8:]]
        set_inner = [
            whole(inner_weight).reshape(width, blocks, width).transpose(1, 0, 2),
            whole(outer_weight).reshape(blocks, width, width),
        ]
    found = run(
        make_project(packed, parts, rows, block, memory_block, width, narrow, len(set_self)), 5.0,
        "project", *set_self, *row_tokens,
    )
    query, query_t, keys, values, value_t = (found[2 * i : 2 * i + 2] for i in range(5))
    row_memory, ids, memory_ids = found[10:]
    query_t = list(query_t)
    if packed:
        third_c = join(after([third, third_b], query_t[0]))
        third_d = turned_swap(third_c, 3)
        second_d = after(second_d, query_t[0])
        set_cross = [second_c, second_d, swap(second_c, 1, 32), swap(second_d, 1, 32)]
        query_t[0] = after(query_t[0], third_c, second_d)
        set_back, set_query, set_last, set_memory = set_cross, set_self, set_self, set_cross
    else:
        set_back, set_query, set_last, set_memory = [full[3], full[4], full[7]], full[:1], full[1:3], full[5:7]
    found = run(
        make_self_attention(share, parts * share, width), 12.0, "self_attention",
        *query_t, *keys, *value_t, ids,
    )
    mixtures, logs = found[:2], found[2:]
    if packed:
        third_d = after(third_d, mixtures[0])
        set_inner = [third_c, third_d, swap(third_c, 1, 32), swap(third_d, 1, 32)]
    first_sum, second_sum, cross_query, memory_keys, memory_values, cross_t, cross_logs, vectors = run(
        make_cross_forward(packed, rows, block, parts * memory_share, width, narrow, len(set_cross)),
        9.0, "cross_forward", *set_cross, *own_tokens, row_memory, ids, memory_ids, *mixtures,
    )
    out_own, out_send, back2_in, sums_inner, *grads_inner = run(
        make_inner(packed, rows, block, width, hidden, narrow, len(set_inner)), 18.0, "inner",
        *set_inner, second_sum, kept, came, vectors,
    )
    out_came = swap(out_send, parts, devices)
    found = run(
        make_cross_back(packed, parts, share, memory_share, width, narrow, len(set_back)), 14.0,
        "cross_back", *set_back, back2_in, first_sum, second_sum, cross_query, memory_keys,
        memory_values, cross_t, cross_logs, ids, memory_ids, vectors, sums_inner, *mixtures,
    )
    back1, memory_key_own, memory_value_own, sums_cross = found[:4]
    slope, slope_t, deltas = (found[4 + 2 * i : 6 + 2 * i] for i in range(3))
    memory_received = [swap(a, m + 1, devices) for m, a in enumerate(found[10 : 10 + parts - 1])]
    grads_early = found[10 + parts - 1 :]
    query = list(query)
    if packed:
        keep, send = combine(after([grads_inner[0], swap(grads_inner[1], 1, 32)], back1, out_came), 2)
        inner_step = [keep, turned_swap(send, 3)]
        memory_key_own = after(memory_key_own, keep)
    memory_own, memory_send, *grads_cross = run(
        make_memory_back(packed, parts, rows, block, memory_block, width, narrow, len(set_memory)),
        2.0, "memory_back", *set_memory, *own_tokens, memory_key_own, memory_value_own, sums_cross,
        *grads_early, *memory_received,
    )
    if packed:
        cross_came = swap(grads_cross[1], 1, 32)
        query[0] = after(query[0], grads_cross[0])
    found = run(
        make_self_back_upper(parts, share, width), 7.0, "self_back_upper", query[0], keys[0],
        values[0], slope[0], slope_t[0], logs[0], deltas[0], ids,
    )
    query_upper, own_upper = found[:2]
    received_upper = [swap(a, m // 2 + 1, devices) for m, a in enumerate(found[2:])]
    if packed:
        keep_cross, send = combine(after([grads_cross[0], cross_came], query_upper), 2)
        cross_step = [keep_cross, turned_swap(send, 3)]
        query[1] = after(query[1], keep_cross)
    in_part, query_sum, query_w_grad, own_lower, *sends = run(
        make_self_back_lower(packed, parts, rows, block, width, narrow, len(set_query)), 11.0,
        "self_back_lower", *set_query, *own_tokens, query[1], keys[1], values[1], slope[1],
        slope_t[1], logs[1], deltas[1], ids, back1, query_upper,
    )
    received_lower = [swap(a, m // 2 + 1, devices) for m, a in enumerate(sends)]
    if packed:
        keep_joint, send = combine_joint(after([inner_step, cross_step], in_part), 2)
        joint_step = [keep_joint, turned_swap(send, 2)]
        in_part = after(in_part, keep_joint)
    in_own, in_send, *grads_last = run(
        make_last(packed, parts, rows, block, memory_block, width, narrow, len(set_last)), 6.0,
        "last", *set_last, *own_tokens, in_part, query_sum, query_w_grad, memory_send, own_upper,
        own_lower, *received_upper, *received_lower,
    )

    if packed:
        keep, send = combine([grads_last[0], swap(grads_last[1], 1, 32)], 2)
        last_step = [keep, turned_swap(send, 3)]
        in_send = after(in_send, last_step[1])
        keep_joint, send = combine(after(joint_step, in_own), 2)
        joint_step = [keep_joint, turned_swap(send, 1)]
        keep, send = combine(after(last_step, keep_joint), 2)
        last_step = [keep, turned_swap(send, 2)]
        keep_joint, send = combine(joint_step, 2)
        joint_step = [keep_joint, turned_swap(send, 0)]
        keep, send = combine(after(last_step, keep_joint), 2)
        last_step = [keep, turned_swap(send, 1)]
        keep, send = combine(last_step, 2)
        last_step = [keep, turned_swap(send, 0)]

        def plan(me_ref, *refs):
            me = me_ref[0]
            joint, last = (sum(r[0].astype(F32) for r in given) for given in (refs[:2], refs[2:4]))
            outs = refs[4:]
            inner, cross = joint[: 2 * blocks * narrow, :], joint[2 * blocks * narrow :, :]
            for i in range(blocks):
                outs[0][:, i * width : (i + 1) * width] = inner[i * narrow : (i + 1) * narrow, :]
            outs[1][...] = inner[blocks * narrow :, :]
            for i in range(5):
                outs[2 + i][...] = cross[i * narrow : (i + 1) * narrow, :]
            for i in range(3):
                outs[7 + i][...] = last[i * narrow : (i + 1) * narrow, :]
            rows_in = jnp.concatenate([cross[5 * narrow :, :], last[3 * narrow :, :]], axis=0)
            outs[10][...] = chosen(me, rows_in, narrow)
            per = width // wide
            line = lax.broadcasted_iota(jnp.int32, (blocks, width), 0)
            row = jnp.sum(jnp.where(line == lax.div(me, per), rows_in[3 : 3 + blocks, :], 0.0), axis=0, keepdims=True)
            outs[11][...] = chosen(lax.rem(me, per), row, wide)

        part = (narrow, width)
        shapes = [(narrow, hidden), (wide, width)] + [part] * 8 + [(24, narrow), (1, wide)]
        (inner_share, outer_share, source_key_share, source_value_share, source_output_share,
         source_query_share, output_share, key_share, value_share, query_share, sums,
         inner_bias_share) = call(
            plan, [(s, F32) for s in shapes], (me_array, *joint_step, *last_step), [], 2.0,
            "finish",
        )
        inner_bias_share = inner_bias_share.reshape(wide)
    else:
        def scatter(array):
            return lax.psum_scatter(array, AXES, scatter_dimension=0, tiled=True)

        inner_share = scatter(grads_inner[0].transpose(1, 0, 2).reshape(width, hidden))
        outer_share = scatter(grads_inner[1].reshape(hidden, width))
        source_output_share, source_query_share, output_share = (scatter(g.astype(F32)) for g in grads_early)
        source_key_share, source_value_share = (scatter(g) for g in grads_cross[:2])
        key_share, value_share = (scatter(g) for g in grads_last[:2])
        query_share = scatter(query_w_grad)
        sums = reduce_all(jnp.concatenate([grads_cross[2], grads_last[2]], axis=0), devices)
        inner_bias_share = lax.dynamic_slice(sums[3 : 3 + blocks].reshape(hidden), (me * wide,), (wide,))
        sums = lax.dynamic_slice(sums, (0, me * narrow), (sums.shape[0], narrow))
    def regroup(mine, came):
        came = came.astype(F32)
        return jnp.where(turn == 0, jnp.stack([mine, came]), jnp.stack([came, mine]))

    output = regroup(out_own, out_came)
    in_came = swap(in_send, parts, devices)
    input_gradient = regroup(in_own, in_came[:block])
    memory_gradient = regroup(memory_own, in_came[block:])

    return (
        output,
        input_gradient,
        memory_gradient,
        query_share,
        key_share,
        value_share,
        output_share,
        sums[16],
        sums[17],
        sums[13],
        sums[11],
        sums[12],
        source_query_share,
        source_key_share,
        source_value_share,
        source_output_share,
        sums[10],
        sums[14],
        sums[9],
        sums[7],
        sums[8],
        inner_share,
        inner_bias_share,
        outer_share,
        sums[2],
        sums[0],
        sums[1],
    )


def solution(mesh):
    sequence, devices = mesh.shape["seq"], mesh.size
    tokens, ids = P("dp", "seq", None), P("dp", "seq")
    matrix, vector = P(AXES, None), P(AXES)
    attention = (matrix,) * 4 + (vector,) * 5
    inner = (matrix, vector, matrix, vector, vector, vector)
    return jax.shard_map(
        functools.partial(per_device, devices=devices, sequence=sequence),
        mesh=mesh,
        in_specs=(tokens, tokens, ids, ids, tokens) + attention + attention + inner,
        out_specs=(tokens, tokens, tokens) + attention + attention + inner,
        check_vma=False,
    )
```

```python
import functools
import math

import jax
import jax.numpy as jnp
from jax import lax
from jax.experimental import pallas as pl
from jax.experimental.pallas import tpu as pltpu
from jax.sharding import PartitionSpec as P

HEADS = 8
HEAD_DIM = 64
PAIR = 128
EPSILON = 1e-05
MASKED = 1e9
AXES = ("dp", "seq")
F32 = jnp.float32
BF16 = jnp.bfloat16

(
    OUTPUT_BIAS,
    ATTENTION_GAIN,
    ATTENTION_SHIFT,
    SOURCE_QUERY_BIAS,
    SOURCE_VALUE_BIAS,
    SOURCE_OUTPUT_BIAS,
    SOURCE_GAIN,
    SOURCE_SHIFT,
    OUTER_BIAS,
    FINAL_GAIN,
    FINAL_SHIFT,
    INNER_BIAS,
) = range(12)
Z_MASKS = (0, 8, 16, 24)
VM = pl.BlockSpec(memory_space=pltpu.VMEM)
SM = pl.BlockSpec(memory_space=pltpu.SMEM)


def dot(a, b):
    return lax.dot_general(a, b, (((1,), (0,)), ((), ())), preferred_element_type=F32)


def dot_nt(a, b):
    return lax.dot_general(a, b, (((1,), (1,)), ((), ())), preferred_element_type=F32)


def dot_tn(a, b):
    return lax.dot_general(a, b, (((0,), (0,)), ((), ())), preferred_element_type=F32)


def total(values):
    return jnp.sum(values.astype(F32), axis=0, keepdims=True)


def normalize(h):
    average = jnp.mean(h, axis=-1, keepdims=True)
    centered = h - average
    variance = jnp.mean(centered * centered, axis=-1, keepdims=True)
    inverse = lax.rsqrt(variance + EPSILON)
    return centered * inverse, inverse


def normalize_back(upstream, normed, inverse, gain):
    scaled = upstream * gain
    first_mean = jnp.mean(scaled, axis=-1, keepdims=True)
    second_mean = jnp.mean(scaled * normed, axis=-1, keepdims=True)
    return inverse * (scaled - first_mean - normed * second_mean)


def normal_parts(v):
    density = 0.3989422804014327 * jnp.exp(-0.5 * v * v)
    t = 1.0 / (1.0 + 0.2316419 * jnp.abs(v))
    series = t * (
        0.319381530
        + t * (-0.356563782 + t * (1.781477937 + t * (-1.821255978 + t * 1.330274429)))
    )
    tail = density * series
    return jnp.where(v >= 0.0, 1.0 - tail, tail), density


def penalties(ids):
    place = lax.broadcasted_iota(jnp.int32, (PAIR, ids.shape[1]), 0)
    return jnp.where((place == ids) | (place >= 4), 0.0, -MASKED).astype(BF16)


def one_hot(ids):
    place = lax.broadcasted_iota(jnp.int32, (PAIR, ids.shape[1]), 0)
    return jnp.where(place == ids, 1.0, 0.0).astype(F32).T.astype(BF16)


def spread(part, half):
    empty = jnp.zeros_like(part)
    return [part, empty] if half == 0 else [empty, part]


def attend(query_t, keys, value_t, hot, penalty, mixture_t, logs):
    length = keys.shape[0]

    def pair(p, carry):
        columns = pl.ds(pl.multiple_of(p * PAIR, PAIR), PAIR)
        left = jnp.concatenate([keys[:, columns], hot[...]], axis=1)
        for half in range(2):
            rows = pl.ds(pl.multiple_of(p * PAIR + half * HEAD_DIM, HEAD_DIM), HEAD_DIM)
            right = jnp.concatenate(spread(query_t[rows, :], half) + [penalty[...]], axis=0)
            scores = dot(left, right)
            highest = jnp.max(scores, axis=0, keepdims=True)
            weights = jnp.exp(scores - highest).astype(BF16)
            values = jnp.concatenate(
                [value_t[rows, :], jnp.ones((16, length), BF16)], axis=0
            )
            found = dot(values, weights)
            denominator = found[HEAD_DIM : HEAD_DIM + 1, :]
            mixture_t[rows, :] = (found[:HEAD_DIM, :] / denominator).astype(BF16)
            logs[2 * p + half] = highest + jnp.log(denominator)
        return carry

    lax.fori_loop(0, keys.shape[1] // PAIR, pair, 0)


def attend_back(
    query_t, query, keys, key_t, values, slope_t, slope, hot, penalty, logs, deltas,
    query_grad_t, key_grad, value_grad,
):
    tokens = query.shape[0]
    lane = lax.broadcasted_iota(jnp.int32, (tokens, PAIR), 1)

    def pair(p, carry):
        columns = pl.ds(pl.multiple_of(p * PAIR, PAIR), PAIR)
        left = jnp.concatenate([keys[:, columns], hot[...]], axis=1)
        value_pair = values[:, columns]
        key_sum, value_sum = None, None
        for half in range(2):
            rows = pl.ds(pl.multiple_of(p * PAIR + half * HEAD_DIM, HEAD_DIM), HEAD_DIM)
            right = jnp.concatenate(spread(query_t[rows, :], half) + [penalty[...]], axis=0)
            chances = jnp.exp(dot(left, right) - logs[2 * p + half])
            slopes = dot(value_pair, jnp.concatenate(spread(slope_t[rows, :], half), axis=0))
            grads = (chances * (slopes - deltas[2 * p + half])).astype(BF16)
            query_grad_t[rows, :] = dot(key_t[rows, :], grads) * HEAD_DIM**-0.5
            mine = (lane < HEAD_DIM) if half == 0 else (lane >= HEAD_DIM)
            none = jnp.zeros((tokens, PAIR), BF16)
            value_part = dot(chances.astype(BF16), jnp.where(mine, slope[:, columns], none))
            key_part = dot(grads, jnp.where(mine, query[:, columns], none))
            value_sum = value_part if value_sum is None else value_sum + value_part
            key_sum = key_part if key_sum is None else key_sum + key_part
        key_grad[:, columns] = key_sum
        value_grad[:, columns] = value_sum
        return carry

    lax.fori_loop(0, keys.shape[1] // PAIR, pair, 0)


def deltas_of(slope_t, mixture_t, deltas):
    for head in range(slope_t.shape[0] // HEAD_DIM):
        rows = slice(head * HEAD_DIM, (head + 1) * HEAD_DIM)
        deltas[head] = jnp.sum(
            slope_t[rows, :].astype(F32) * mixture_t[rows, :].astype(F32), axis=0, keepdims=True
        )


def swap(array, mask, devices):
    return lax.ppermute(array, AXES, [(i, i ^ mask) for i in range(devices)])


Z_FIRST = ((8, 16, 2, 4), (16, 8, 4, 2))
CROSSED = ((8, 16, 4, 2), (16, 8, 2, 4))


def turned_swap(array, step, orders=Z_FIRST):
    return lax.ppermute(array, AXES, [(i, i ^ orders[i % 2][step]) for i in range(32)])


def after(value, *others):
    return lax.optimization_barrier((value, others))[0]


def places(me, orders=Z_FIRST):
    found = []
    for core in range(2):
        even = ((me & 1) ^ core) == 0
        masks = [jnp.where(even, first, second) for first, second in zip(*orders)]
        for far in range(2):
            for slot in range(8):
                device = me ^ core if core else me
                for step, bit in enumerate((slot & 1, slot & 2, slot & 4, far)):
                    if bit:
                        device = device ^ masks[step]
                found.append((core, far, slot, device))
    return found


def unpack(me, pieces, stride, first, rows, scratch, orders=Z_FIRST):
    for core, far, slot, device in places(me, orders):
        ref = pieces[2 * core + far]
        at = slot * stride + first
        scratch[pl.ds(pl.multiple_of(device * rows, rows), rows), :] = ref[at : at + rows, :]


def vector_sum(pieces, stride, first):
    found = None
    for ref in pieces:
        for slot in range(8):
            part = ref[slot * stride + first : (slot + 1) * stride, :].astype(F32)
            found = part if found is None else found + part
    return found


class Grads:
    def __init__(self, me, refs, dense, rows, orders=Z_FIRST):
        self.me, self.refs, self.dense, self.rows, self.orders = me, refs, dense, rows, orders

    def put(self, index, grad):
        if self.dense is None:
            self.refs[index][...] = grad
            return
        self.dense[...] = grad
        rows = self.rows
        for core, far, slot, device in places(self.me, self.orders):
            found = self.dense[pl.ds(pl.multiple_of(device * rows, rows), rows), :]
            self.refs[core][far * 8 + slot, index * rows : (index + 1) * rows, :] = found.astype(BF16)

    def put_sums(self, first, sums):
        if self.dense is None:
            self.refs[-1][...] = sums
            return
        low = sums.astype(BF16)
        for ref in self.refs:
            for slot in range(16):
                ref[slot, first : first + sums.shape[0], :] = low


def grad_outs(packed, count, rows, width, sums):
    if packed:
        return [((16, count * rows + sums, width), BF16)] * 2
    return [((width, width), F32)] * count + [((sums, width), F32)]


COSTS = {}


def padded(shape, dtype):
    last = -(-shape[-1] // 128) * 128
    tall = -(-shape[-2] // 16) * 16 if len(shape) > 1 else 16
    return math.prod(shape[:-2]) * tall * last * jnp.dtype(dtype).itemsize


def snug(arrays):
    return 2 * sum(padded(a.shape, a.dtype) for a in arrays) + (3 << 20)


def call(kernel, outs, args, scratch, micros, name, room=10):
    moved = sum(math.prod(a.shape) * a.dtype.itemsize for a in args[1:])
    moved += sum(math.prod(s) * jnp.dtype(d).itemsize for s, d in outs)
    need = sum(padded(a.shape, a.dtype) for a in args[1:])
    need += sum(padded(s, d) for s, d in list(outs) + list(scratch))
    return pl.pallas_call(
        kernel,
        out_shape=[jax.ShapeDtypeStruct(s, d) for s, d in outs],
        in_specs=[SM] + [VM] * (len(args) - 1),
        out_specs=[VM] * len(outs),
        scratch_shapes=[pltpu.VMEM(s, d) for s, d in scratch],
        compiler_params=pltpu.CompilerParams(vmem_limit_bytes=min(need + (room << 20), 58 << 20)),
        cost_estimate=pl.CostEstimate(
            flops=int(COSTS.get(name, 0) * 1.15e9) + 1, bytes_accessed=1, transcendentals=0
        ),
        name=name,
    )(*args)


def tokens_packet(turn, tokens, memory, target_ids, source_ids, cotangent):
    block, width = tokens.shape[1:]
    memory_block = memory.shape[1]
    first = block + memory_block + 8

    def kernel(turn_ref, targets, sources, tokens_ref, memory_ref, cot_ref, sent, kept):
        mine = turn_ref[0]
        for row, out in ((1 - mine, sent), (mine, kept)):
            out[:block, :] = tokens_ref[row]
            out[block : block + memory_block, :] = memory_ref[row]
            ids = targets[pl.ds(row, 1), :].astype(F32)
            ids = jnp.concatenate([ids, jnp.zeros((1, width - block), F32)], axis=1)
            others = sources[pl.ds(row, 1), :].astype(F32)
            others = jnp.concatenate([others, jnp.zeros((1, width - memory_block), F32)], axis=1)
            place = lax.broadcasted_iota(jnp.int32, (8, width), 0)
            found = jnp.where(place == 0, ids, jnp.where(place == 1, others, 0.0))
            out[block + memory_block : first, :] = found.astype(BF16)
            out[first:, :] = cot_ref[row]

    shape = (first + block, width)
    return call(kernel, [(shape, BF16)] * 2, (turn, target_ids, source_ids, tokens, memory, cotangent),
                [], 1.0, "tokens_packet", 58)


def placed(me, parts, width):
    here = lax.broadcasted_iota(jnp.int32, (parts.shape[1], width), 0) + me * parts.shape[1]
    lane = lax.broadcasted_iota(jnp.int32, (parts.shape[1], width), 1)
    return dot(parts, jnp.where(lane == here, 1.0, 0.0).astype(BF16))


def make_weights_packet(narrow, width, blocks):
    tall = blocks * narrow

    def kernel(me_ref, *refs):
        weights, inner, outer, wide, short = refs[:8], refs[8], refs[9], refs[10], refs[11:24]
        first, rest = refs[24:]
        me, middle = me_ref[0], 5 * narrow + 16
        for i, ref in enumerate(weights):
            if i < 3:
                first[i * narrow : (i + 1) * narrow, :] = ref[...]
            else:
                rest[(i - 3) * narrow : (i - 2) * narrow, :] = ref[...]
        short = jnp.concatenate([ref[...].astype(F32) for ref in short], axis=0).astype(BF16)
        found = placed(me, short, width)
        first[3 * narrow :, :] = jnp.concatenate([found[:2, :], jnp.zeros((6, width), F32)], axis=0).astype(BF16)
        per = width // wide.shape[1]
        row = placed(lax.rem(me, per), wide[...], width)
        place = lax.broadcasted_iota(jnp.int32, (blocks, width), 0)
        spread_row = jnp.where(place == lax.div(me, per), row, 0.0)
        none = jnp.zeros((16 - (found.shape[0] - 2) - blocks, width), F32)
        rest[5 * narrow : middle, :] = jnp.concatenate([found[2:, :], spread_row, none], axis=0).astype(BF16)
        for i in range(blocks):
            rest[middle + i * narrow : middle + (i + 1) * narrow, :] = inner[:, i * width : (i + 1) * width]
        rest[middle + tall :, :] = outer[...]

    return kernel, [((rows, width), BF16) for rows in (3 * narrow + 8, 5 * narrow + 16 + 2 * tall)]


def make_part(sizes, width):
    tall = sum(sizes)

    def kernel(me_ref, upper, lower, *outs):
        for i in range(4):
            ref, at = (upper, lower)[i // 2], i % 2 * tall
            for size, out in zip(sizes, outs):
                out[i * size : (i + 1) * size, :] = ref[at : at + size, :]
                at += size

    return kernel, [((4 * size, width), BF16) for size in sizes]


def join(arrays):
    def kernel(*refs):
        at = 0
        for ref in refs[:-1]:
            refs[-1][at : at + ref.shape[0], :] = ref[...]
            at += ref.shape[0]

    rows = sum(a.shape[0] for a in arrays)
    return pl.pallas_call(
        kernel,
        out_shape=jax.ShapeDtypeStruct((rows, arrays[0].shape[1]), arrays[0].dtype),
        in_specs=[VM] * len(arrays),
        out_specs=VM,
        compiler_params=pltpu.CompilerParams(vmem_limit_bytes=snug(arrays)),
        cost_estimate=pl.CostEstimate(flops=1 << 20, bytes_accessed=0, transcendentals=0),
        name="join",
    )(*arrays)


def make_project(packed, parts, rows, block, memory_block, width, narrow, n_pieces):
    share = rows * block
    length = parts * share
    memory_share = rows * memory_block
    stride = 3 * narrow + 8
    half = width // 2

    def kernel(*refs):
        me_ref, refs = refs[0], list(refs[1:])
        pieces, refs = refs[:n_pieces], refs[n_pieces:]
        tokens, refs = refs[: parts * rows], refs[parts * rows :]
        query, query_t, keys, values, value_t = (refs[2 * i : 2 * i + 2] for i in range(5))
        memory, ids, memory_ids = refs[10:13]
        scratch = refs[13:]
        me = me_ref[0]
        if packed:
            for i in range(3):
                unpack(me, pieces, stride, i * narrow, narrow, scratch[i], CROSSED)
            query_w, key_w, value_w = scratch
            biases = vector_sum(pieces, stride, 3 * narrow)
        else:
            query_w, key_w, value_w = pieces[:3]
            biases = pieces[3][...]
        for i in range(parts):
            here = slice(i * share, (i + 1) * share)
            some = tokens[i * rows : (i + 1) * rows]
            own = jnp.concatenate([t[:block, :] for t in some], axis=0)
            if i == 0:
                scaled = (dot(own, query_w[...]) + biases[0:1, :]).astype(BF16) * BF16(HEAD_DIM**-0.5)
            key = dot(own, key_w[...]).astype(BF16)
            found = (dot(own, value_w[...]) + biases[1:2, :]).astype(BF16)
            for side in range(2):
                columns = slice(side * half, (side + 1) * half)
                if i == 0:
                    query[side][...] = scaled[:, columns]
                    query_t[side][...] = scaled[:, columns].T
                keys[side][here, :] = key[:, columns]
                values[side][here, :] = found[:, columns]
                value_t[side][:, here] = found[:, columns].T
        for i, t in enumerate(tokens):
            memory[i * memory_block : (i + 1) * memory_block, :] = t[block : block + memory_block, :]
            found = t[block + memory_block : block + memory_block + 8, :].astype(F32).astype(jnp.int32)
            ids[:, i * block : (i + 1) * block] = found[0:1, :block]
        found = [t[block + memory_block : block + memory_block + 8, :].astype(F32).astype(jnp.int32)[1:2, :memory_block] for t in tokens]
        memory_ids[...] = jnp.concatenate(found, axis=1)

    outs = [((share, half), BF16)] * 2 + [((half, share), BF16)] * 2
    outs += [((length, half), BF16)] * 4 + [((half, length), BF16)] * 2
    outs += [
        ((parts * memory_share, width), BF16),
        ((1, length), jnp.int32),
        ((1, parts * memory_share), jnp.int32),
    ]
    return kernel, outs, [((width, width), BF16)] * 3 if packed else []


def make_self_attention(share, length, width):
    def kernel(me_ref, *refs):
        query_t, keys, value_t, ids = refs[:2], refs[2:4], refs[4:6], refs[6]
        mixture_t, logs, hot, penalty = refs[7:9], refs[9:11], refs[11], refs[12]
        hot[...] = one_hot(ids[...])
        penalty[...] = penalties(ids[:, :share])
        for side in range(2):
            attend(query_t[side], keys[side], value_t[side], hot, penalty, mixture_t[side], logs[side])

    outs = [((width // 2, share), BF16)] * 2 + [((HEADS // 2, 1, share), F32)] * 2
    return kernel, outs, [((length, PAIR), BF16), ((PAIR, share), BF16)]


def make_cross_forward(packed, rows, block, memory_length, width, narrow, n_pieces):
    share = rows * block
    stride = 5 * narrow + 16

    def kernel(*refs):
        me_ref, refs = refs[0], list(refs[1:])
        pieces, refs = refs[:n_pieces], refs[n_pieces:]
        tokens, refs = refs[:rows], refs[rows:]
        memory, ids, memory_ids, upper, lower = refs[:5]
        first_sum, second_sum, query, memory_keys, memory_values, cross_t, logs, vectors = refs[5:13]
        scratch = refs[13:]
        query_t, value_t, hot, penalty = scratch[:4]
        if packed:
            for i in range(5):
                unpack(me_ref[0], pieces, stride, i * narrow, narrow, scratch[4 + i])
            output_w, query_w, key_w, value_w, source_w = scratch[4:]
            vectors[...] = vector_sum(pieces, stride, 5 * narrow)
        else:
            output_w, query_w, key_w, value_w, source_w = pieces[:5]
            vectors[...] = pieces[5][...]

        def vector(i):
            return vectors[i : i + 1, :]

        own = jnp.concatenate([t[:block, :] for t in tokens], axis=0)
        mixture_t = jnp.concatenate([upper[...], lower[...]], axis=0)
        h = own.astype(F32) + dot_tn(mixture_t, output_w[...]) + vector(OUTPUT_BIAS)
        first_sum[...] = h
        first = normalize(h)[0] * vector(ATTENTION_GAIN) + vector(ATTENTION_SHIFT)
        scaled = (dot(first.astype(BF16), query_w[...]) + vector(SOURCE_QUERY_BIAS)).astype(BF16) * BF16(HEAD_DIM**-0.5)
        query[...] = scaled
        query_t[...] = scaled.T
        memory_keys[...] = dot(memory[...], key_w[...]).astype(BF16)
        memory_values[...] = (dot(memory[...], value_w[...]) + vector(SOURCE_VALUE_BIAS)).astype(BF16)
        value_t[...] = memory_values[...].T
        hot[...] = one_hot(memory_ids[...])
        penalty[...] = penalties(ids[:, :share])
        attend(query_t, memory_keys, value_t, hot, penalty, cross_t, logs)
        first = normalize(first_sum[...])[0] * vector(ATTENTION_GAIN) + vector(ATTENTION_SHIFT)
        second_sum[...] = first + dot_tn(cross_t[...], source_w[...]) + vector(SOURCE_OUTPUT_BIAS)

    outs = [
        ((share, width), F32),
        ((share, width), F32),
        ((share, width), BF16),
        ((memory_length, width), BF16),
        ((memory_length, width), BF16),
        ((width, share), BF16),
        ((HEADS, 1, share), F32),
        ((16, width), F32),
    ]
    scratch = [((width, share), BF16), ((width, memory_length), BF16), ((memory_length, PAIR), BF16), ((PAIR, share), BF16)]
    if packed:
        scratch += [((width, width), BF16)] * 5
    return kernel, outs, scratch


def make_inner(packed, rows, block, width, hidden, narrow, n_pieces):
    blocks = hidden // width
    share = rows * block
    per = width // (blocks * narrow)

    def kernel(*refs):
        me_ref, refs = refs[0], list(refs[1:])
        pieces, refs = refs[:n_pieces], refs[n_pieces:]
        second_sum, cot_own, cot_came, vectors = refs[:4]
        out_own, out_send, back, sums = refs[4:8]
        grads, scratch = refs[8:10], refs[10:]
        low, active, gate, slope = scratch[:4]
        if packed:
            inner_w, outer_w, gathered, dense = scratch[4:8]
            tall = blocks * narrow
            for core, far, slot, device in places(me_ref[0], CROSSED):
                ref, at = pieces[2 * core + far], slot * 2 * tall
                row = pl.multiple_of(device * narrow, narrow)
                for i in range(blocks):
                    inner_w[i, pl.ds(row, narrow), :] = ref[at + i * narrow : at + (i + 1) * narrow, :]
                row = pl.multiple_of(lax.rem(device, per) * tall, tall)
                outer_w[lax.div(device, per), pl.ds(row, tall), :] = ref[at + tall : at + 2 * tall, :]
        else:
            inner_w, outer_w = pieces

        def vector(i):
            return vectors[i : i + 1, :]

        second = normalize(second_sum[...])[0] * vector(SOURCE_GAIN) + vector(SOURCE_SHIFT)
        low[...] = second.astype(BF16)
        back[...] = second + vector(OUTER_BIAS)

        def forward(i, carry):
            inner = dot(low[...], inner_w[i]) + vectors[pl.ds(INNER_BIAS + i, 1), :]
            chance, density = normal_parts(inner)
            found = (inner * chance).astype(BF16)
            active[i] = found
            gate[i] = chance + inner * density
            back[...] += dot(found, outer_w[i])
            return carry

        lax.fori_loop(0, blocks, forward, 0)
        normed, inverse = normalize(back[...])
        final = normed * vector(FINAL_GAIN) + vector(FINAL_SHIFT)
        out_own[...] = final[:block, :]
        out_send[...] = final[block:, :].astype(BF16)
        upstream = jnp.concatenate([cot_own[-block:, :], cot_came[-block:, :]], axis=0).astype(F32)
        sums[0:1, :] = total(upstream * normed)
        sums[1:2, :] = total(upstream)
        back3 = normalize_back(upstream, normed, inverse, vector(FINAL_GAIN))
        slope[...] = back3.astype(BF16)
        sums[2:3, :] = total(slope[...])
        sums[7:8, :] = jnp.zeros_like(sums[7:8, :])
        back[...] = back3

        def backward(i, carry):
            grad = dot_nt(slope[...], outer_w[i]) * gate[i]
            inner_low = grad.astype(BF16)
            sums[pl.ds(3 + i, 1), :] = total(inner_low)
            outer_grad = dot_tn(active[i], slope[...])
            inner_grad = dot_tn(low[...], inner_low)
            back[...] += dot_nt(inner_low, inner_w[i])
            if packed:
                dense[...] = inner_grad
                gathered[i] = outer_grad.astype(BF16)
                here = pl.ds(pl.multiple_of(i * narrow, narrow), narrow)
                for core, far, slot, device in places(me_ref[0]):
                    row = pl.multiple_of(device * narrow, narrow)
                    grads[core][far * 8 + slot, here, :] = dense[pl.ds(row, narrow), :].astype(BF16)
            else:
                grads[0][i] = inner_grad
                grads[1][i] = outer_grad
            return carry

        lax.fori_loop(0, blocks, backward, 0)
        if packed:
            tall = blocks * narrow
            for core, far, slot, device in places(me_ref[0]):
                row = pl.multiple_of(lax.rem(device, per) * tall, tall)
                grads[core][far * 8 + slot, tall:, :] = gathered[lax.div(device, per), pl.ds(row, tall), :]

    outs = [((block, width), F32), ((block, width), BF16), ((share, width), F32), ((8, width), F32)]
    if packed:
        outs += [((16, 2 * blocks * narrow, width), BF16)] * 2
    else:
        outs += [((blocks, width, width), F32)] * 2
    scratch = [((share, width), BF16), ((blocks, share, width), BF16), ((blocks, share, width), F32), ((share, width), BF16)]
    if packed:
        scratch += [((blocks, width, width), BF16)] * 3 + [((width, width), F32)]
    return kernel, outs, scratch


def make_cross_back(packed, parts, share, memory_share, width, narrow, n_pieces):
    memory_length = parts * memory_share
    stride = 5 * narrow + 16

    def kernel(*refs):
        me_ref, refs = refs[0], list(refs[1:])
        pieces, refs = refs[:n_pieces], refs[n_pieces:]
        (back2_in, first_sum, second_sum, query, memory_keys, memory_values, cross_t, logs, ids,
         memory_ids, vectors, sums_inner) = refs[:12]
        mixtures, refs = refs[12:14], refs[14:]
        back1, key_own, value_own, sums = refs[:4]
        self_slope, self_slope_t, self_deltas = (refs[4 + 2 * i : 6 + 2 * i] for i in range(3))
        sends, refs = refs[10 : 10 + parts - 1], refs[10 + parts - 1 :]
        grads, scratch = refs[:3], refs[3:]
        (slope_t, slope, key_t, hot, penalty, query_t, deltas, query_grad_t, key_grad, value_grad) = scratch[:10]
        upper, lower = mixtures
        if packed:
            for i, at in enumerate((0, 1, 4)):
                unpack(me_ref[0], pieces, stride, at * narrow, narrow, scratch[10 + i])
            output_w, query_w, source_w = scratch[10:13]
        else:
            output_w, query_w, source_w = pieces

        def vector(i):
            return vectors[i : i + 1, :]

        sums[0:7, :] = sums_inner[0:7, :]
        upstream = back2_in[...]
        normed, inverse = normalize(second_sum[...])
        sums[7:8, :] = total(upstream * normed)
        sums[8:9, :] = total(upstream)
        back2 = normalize_back(upstream, normed, inverse, vector(SOURCE_GAIN))
        back1[...] = back2
        cross_low = back2.astype(BF16)
        sums[9:10, :] = total(cross_low)
        grads[0][...] = dot(cross_t[...], cross_low).astype(BF16)
        found = dot_nt(cross_low, source_w[...]).astype(BF16)
        slope[...] = found
        slope_t[...] = found.T
        deltas_of(slope_t, cross_t, deltas)
        query_t[...] = query[...].T
        key_t[...] = memory_keys[...].T
        hot[...] = one_hot(memory_ids[...])
        penalty[...] = penalties(ids[:, :share])
        attend_back(query_t, query, memory_keys, key_t, memory_values, slope_t, slope, hot, penalty,
                    logs, deltas, query_grad_t, key_grad, value_grad)
        key_own[...] = key_grad[:memory_share, :]
        value_own[...] = value_grad[:memory_share, :]
        for i in range(1, parts):
            here = slice(i * memory_share, (i + 1) * memory_share)
            sends[i - 1][:memory_share, :] = key_grad[here, :].astype(BF16)
            sends[i - 1][memory_share:, :] = value_grad[here, :].astype(BF16)
        query_low = query_grad_t[...].T.astype(BF16)
        sums[10:11, :] = total(query_low)
        normed, inverse = normalize(first_sum[...])
        first_low = (normed * vector(ATTENTION_GAIN) + vector(ATTENTION_SHIFT)).astype(BF16)
        grads[1][...] = dot_tn(first_low, query_low).astype(BF16)
        upstream = back1[...] + dot_nt(query_low, query_w[...])
        sums[11:12, :] = total(upstream * normed)
        sums[12:13, :] = total(upstream)
        grad = normalize_back(upstream, normed, inverse, vector(ATTENTION_GAIN))
        back1[...] = grad
        branch_low = grad.astype(BF16)
        sums[13:14, :] = total(branch_low)
        sums[14:16, :] = jnp.zeros_like(sums[14:16, :])
        mixture_t = jnp.concatenate([upper[...], lower[...]], axis=0)
        grads[2][...] = dot(mixture_t, branch_low).astype(BF16)
        found = dot_nt(branch_low, output_w[...]).astype(BF16)
        for side in range(2):
            columns = slice(side * width // 2, (side + 1) * width // 2)
            self_slope[side][...] = found[:, columns]
            self_slope_t[side][...] = found[:, columns].T
            deltas_of(self_slope_t[side], mixtures[side], self_deltas[side])

    half = width // 2
    outs = [
        ((share, width), F32),
        ((memory_share, width), F32),
        ((memory_share, width), F32),
        ((16, width), F32),
    ]
    outs += [((share, half), BF16)] * 2 + [((half, share), BF16)] * 2
    outs += [((HEADS // 2, 1, share), F32)] * 2
    outs += [((2 * memory_share, width), BF16)] * (parts - 1)
    outs += [((width, width), BF16)] * 3
    scratch = [
        ((width, share), BF16),
        ((share, width), BF16),
        ((width, memory_length), BF16),
        ((memory_length, PAIR), BF16),
        ((PAIR, share), BF16),
        ((width, share), BF16),
        ((HEADS, 1, share), F32),
        ((width, share), F32),
        ((memory_length, width), F32),
        ((memory_length, width), F32),
    ]
    if packed:
        scratch += [((width, width), BF16)] * 3
    return kernel, outs, scratch


def attention_back_half(refs, share, scratch):
    query, keys, values, slope, slope_t, logs, deltas, ids = refs
    query_t, key_t, hot, penalty, query_grad_t, key_grad, value_grad = scratch
    query_t[...] = query[...].T
    key_t[...] = keys[...].T
    hot[...] = one_hot(ids[...])
    penalty[...] = penalties(ids[:, :share])
    attend_back(query_t, query, keys, key_t, values, slope_t, slope, hot, penalty, logs, deltas,
                query_grad_t, key_grad, value_grad)


def half_scratch(share, length, half):
    return [
        ((half, share), BF16),
        ((half, length), BF16),
        ((length, PAIR), BF16),
        ((PAIR, share), BF16),
        ((half, share), F32),
        ((length, half), F32),
        ((length, half), F32),
    ]


def give_half(share, scratch, own, sends):
    key_grad, value_grad = scratch[5:7]
    own[:share, :] = key_grad[:share, :]
    own[share:, :] = value_grad[:share, :]
    for i, send in enumerate(sends):
        here = slice((i // 2 + 1) * share, (i // 2 + 2) * share)
        send[...] = (key_grad, value_grad)[i % 2][here, :].astype(BF16)


def make_memory_back(packed, parts, rows, block, memory_block, width, narrow, n_pieces):
    memory_share = rows * memory_block

    def kernel(*refs):
        me_ref, refs = refs[0], list(refs[1:])
        pieces, refs = refs[:n_pieces], refs[n_pieces:]
        tokens, refs = refs[:rows], refs[rows:]
        memory_key_own, memory_value_own, sums_in = refs[:3]
        early, refs = refs[3:6], refs[6:]
        memory_received, refs = refs[: parts - 1], refs[parts - 1 :]
        memory_own, memory_send = refs[:2]
        n_grads = 2 if packed else 3
        grad_refs, scratch = refs[2 : 2 + n_grads], refs[2 + n_grads :]
        sums = scratch[0]
        me = me_ref[0]
        if packed:
            for i in range(2):
                unpack(me, pieces, 5 * narrow + 16, (2 + i) * narrow, narrow, scratch[1 + i])
            source_key, source_value = scratch[1:3]
        else:
            source_key, source_value = pieces
        grads = Grads(me, grad_refs, scratch[3] if packed else None, narrow, CROSSED)
        memory = jnp.concatenate([t[block : block + memory_block, :] for t in tokens], axis=0)
        key_sum, value_sum = memory_key_own[...], memory_value_own[...]
        for ref in memory_received:
            key_sum = key_sum + ref[:memory_share, :].astype(F32)
            value_sum = value_sum + ref[memory_share:, :].astype(F32)
        key_low, value_low = key_sum.astype(BF16), value_sum.astype(BF16)
        sums[...] = sums_in[...]
        sums[14:15, :] = total(value_low)
        grads.put_sums(5 * narrow, sums[...])
        grads.put(0, dot_tn(memory, key_low))
        grads.put(1, dot_tn(memory, value_low))
        if packed:
            for i, ref in enumerate(early):
                grads.put(2 + i, ref[...].astype(F32))
        grad = dot_nt(key_low, source_key[...]) + dot_nt(value_low, source_value[...])
        memory_own[...] = grad[:memory_block, :]
        memory_send[...] = grad[memory_block:, :].astype(BF16)

    outs = [((memory_block, width), F32), ((memory_block, width), BF16)]
    if packed:
        outs += [((16, 5 * narrow + 16, width), BF16)] * 2
    else:
        outs += [((width, width), F32)] * 2 + [((16, width), F32)]
    scratch = [((16, width), F32)]
    if packed:
        scratch += [((width, width), BF16)] * 2 + [((width, width), F32)]
    return kernel, outs, scratch


def make_self_back_upper(parts, share, width):
    length, half = parts * share, width // 2

    def kernel(*refs):
        operands, (query_grad, own), refs = refs[1:9], refs[9:11], refs[11:]
        sends, scratch = refs[: 2 * parts - 2], refs[2 * parts - 2 :]
        attention_back_half(operands, share, scratch)
        query_grad[...] = scratch[4][...].T.astype(BF16)
        give_half(share, scratch, own, sends)

    outs = [((share, half), BF16), ((2 * share, half), F32)] + [((share, half), BF16)] * (2 * parts - 2)
    return kernel, outs, half_scratch(share, length, half)


def make_self_back_lower(packed, parts, rows, block, width, narrow, n_pieces):
    share = rows * block
    length, half = parts * share, width // 2

    def kernel(*refs):
        me_ref, refs = refs[0], list(refs[1:])
        pieces, refs = refs[:n_pieces], refs[n_pieces:]
        tokens, refs = refs[:rows], refs[rows:]
        operands, refs = refs[:8], refs[8:]
        back1, query_upper = refs[:2]
        in_part, query_sum, query_w_grad, own = refs[2:6]
        sends, scratch = refs[6 : 4 + 2 * parts], refs[4 + 2 * parts :]
        if packed:
            unpack(me_ref[0], pieces, 3 * narrow + 8, 0, narrow, scratch[7], CROSSED)
            query_w = scratch[7]
        else:
            (query_w,) = pieces
        attention_back_half(operands, share, scratch[:7])
        give_half(share, scratch, own, sends)
        query_low = jnp.concatenate([query_upper[...], scratch[4][...].T.astype(BF16)], axis=1)
        tokens_own = jnp.concatenate([t[:block, :] for t in tokens], axis=0)
        in_part[...] = back1[...] + dot_nt(query_low, query_w[...])
        query_sum[...] = jnp.concatenate([total(query_low), jnp.zeros((7, width), F32)], axis=0)
        query_w_grad[...] = dot_tn(tokens_own, query_low).astype(query_w_grad.dtype)

    outs = [
        ((share, width), F32),
        ((8, width), F32),
        ((width, width), BF16 if packed else F32),
        ((2 * share, half), F32),
    ]
    outs += [((share, half), BF16)] * (2 * parts - 2)
    scratch = half_scratch(share, length, half)
    if packed:
        scratch += [((width, width), BF16)]
    return kernel, outs, scratch


def make_last(packed, parts, rows, block, memory_block, width, narrow, n_pieces):
    share = rows * block

    def kernel(*refs):
        me_ref, refs = refs[0], list(refs[1:])
        pieces, refs = refs[:n_pieces], refs[n_pieces:]
        tokens, refs = refs[:rows], refs[rows:]
        in_part, query_sum, query_w_grad, memory_send = refs[:4]
        owns, refs = refs[4:6], refs[6:]
        received = [refs[: 2 * parts - 2], refs[2 * parts - 2 : 4 * parts - 4]]
        refs = refs[4 * parts - 4 :]
        in_own, in_send = refs[:2]
        n_grads = 2 if packed else 3
        grad_refs, scratch = refs[2 : 2 + n_grads], refs[2 + n_grads :]
        sums = scratch[0]
        me = me_ref[0]
        if packed:
            for i in range(2):
                unpack(me, pieces, 3 * narrow + 8, (1 + i) * narrow, narrow, scratch[1 + i], CROSSED)
            key_w, value_w = scratch[1:3]
        else:
            key_w, value_w = pieces
        grads = Grads(me, grad_refs, scratch[3] if packed else None, narrow)
        if packed:
            grads.put(2, query_w_grad[...].astype(F32))
        lows = []
        for own, others in zip(owns, received):
            found = own[...]
            for key, value in zip(others[::2], others[1::2]):
                found = found + jnp.concatenate([key[...], value[...]], axis=0).astype(F32)
            lows.append(found.astype(BF16))
        key_low = jnp.concatenate([low[:share, :] for low in lows], axis=1)
        value_low = jnp.concatenate([low[share:, :] for low in lows], axis=1)
        tokens_own = jnp.concatenate([t[:block, :] for t in tokens], axis=0)
        sums[...] = query_sum[...]
        sums[1:2, :] = total(value_low)
        grads.put_sums(3 * narrow, sums[...])
        grads.put(0, dot_tn(tokens_own, key_low))
        grads.put(1, dot_tn(tokens_own, value_low))
        grad = in_part[...] + dot_nt(key_low, key_w[...]) + dot_nt(value_low, value_w[...])
        in_own[...] = grad[:block, :]
        in_send[:block, :] = grad[block:, :].astype(BF16)
        in_send[block:, :] = memory_send[...]

    outs = [((block, width), F32), ((block + memory_block, width), BF16)]
    if packed:
        outs += [((16, 3 * narrow + 8, width), BF16)] * 2
    else:
        outs += [((width, width), F32)] * 2 + [((8, width), F32)]
    scratch = [((8, width), F32)]
    if packed:
        scratch += [((width, width), BF16)] * 2 + [((width, width), F32)]
    return kernel, outs, scratch


def combine(arrays, splits, micros=0.1):
    count = arrays[0].shape[0] // splits
    shape = (count,) + arrays[0].shape[1:]

    def kernel(*refs):
        given, outs = refs[: len(arrays)], refs[len(arrays) :]
        for i, out in enumerate(outs):
            here = slice(i * count, (i + 1) * count)
            found = given[0][here].astype(F32)
            for ref in given[1:]:
                found = found + ref[here].astype(F32)
            out[...] = found.astype(out.dtype)

    return pl.pallas_call(
        kernel,
        out_shape=[jax.ShapeDtypeStruct(shape, BF16)] * splits,
        in_specs=[VM] * len(arrays),
        out_specs=[VM] * splits,
        compiler_params=pltpu.CompilerParams(vmem_limit_bytes=snug(arrays)),
        cost_estimate=pl.CostEstimate(flops=int(micros * 1.15e9), bytes_accessed=0, transcendentals=0),
        name="combine",
    )(*arrays)


def combine_joint(groups, splits):
    count, sizes = groups[0][0].shape[0] // splits, [g[0].shape[1] for g in groups]
    shape = (count, sum(sizes)) + groups[0][0].shape[2:]
    flat = [a for group in groups for a in group]

    def kernel(*refs):
        outs, at, row = refs[len(flat) :], 0, 0
        for group, size in zip(groups, sizes):
            given = refs[at : at + len(group)]
            at += len(group)
            for i, out in enumerate(outs):
                here = slice(i * count, (i + 1) * count)
                found = given[0][here].astype(F32)
                for ref in given[1:]:
                    found = found + ref[here].astype(F32)
                out[:, row : row + size, :] = found.astype(BF16)
            row += size

    return pl.pallas_call(
        kernel,
        out_shape=[jax.ShapeDtypeStruct(shape, BF16)] * splits,
        in_specs=[VM] * len(flat),
        out_specs=[VM] * splits,
        compiler_params=pltpu.CompilerParams(vmem_limit_bytes=snug(flat)),
        cost_estimate=pl.CostEstimate(flops=1, bytes_accessed=1, transcendentals=0),
        name="combine_joint",
    )(*flat)


def chosen(me, rows, wide):
    width = rows.shape[1]
    line = lax.broadcasted_iota(jnp.int32, (width, wide), 0)
    here = lax.broadcasted_iota(jnp.int32, (width, wide), 1) + me * wide
    choice = jnp.where(line == here, 1.0, 0.0)
    return lax.dot_general(rows, choice, (((1,), (0,)), ((), ())), precision=lax.Precision.HIGHEST, preferred_element_type=F32)


def reduce_all(array, devices):
    mask = 1
    while mask < devices:
        array = array + swap(array, mask, devices)
        mask *= 2
    return array


def per_device(
    tokens, memory, target_ids, source_ids, cotangent,
    query_weight, key_weight, value_weight, output_weight, query_bias, value_bias, output_bias,
    attention_gain, attention_shift,
    source_query, source_key, source_value, source_output, source_query_bias, source_value_bias,
    source_output_bias, source_gain, source_shift,
    inner_weight, inner_bias, outer_weight, outer_bias, final_gain, final_shift,
    *, devices, sequence,
):
    packed = devices == 32
    rows, block, width = tokens.shape
    memory_block = memory.shape[1]
    parts = sequence // rows
    share, memory_share = rows * block, rows * memory_block
    hidden = inner_weight.shape[1]
    blocks = hidden // width
    me = lax.axis_index(AXES)
    me_array = me.reshape(1).astype(jnp.int32)
    turn = lax.rem(lax.div(me, parts), rows)
    narrow, wide = width // devices, hidden // devices

    def run(made, micros, name, *args, room=10):
        kernel, outs, *scratch = made
        return call(kernel, outs, (me_array,) + args, scratch[0] if scratch else [], micros, name, room)

    short = [query_bias, value_bias, output_bias, attention_gain, attention_shift, source_query_bias,
             source_value_bias, source_output_bias, source_gain, source_shift, outer_bias, final_gain,
             final_shift]

    def whole(array):
        return lax.all_gather(array, AXES, axis=0, tiled=True)

    sent, kept = tokens_packet(
        turn.reshape(1).astype(jnp.int32), tokens, memory, target_ids, source_ids, cotangent
    )
    came = swap(sent, parts, devices)
    row_tokens = [kept, came]
    kept_swaps = [swap(kept, m, devices) for m in range(1, parts)]
    came_swaps = [swap(came, m, devices) for m in range(1, parts)]
    for pair in zip(kept_swaps, came_swaps):
        row_tokens += pair
    own_tokens = row_tokens[:rows]

    if packed:
        first, rest = run(make_weights_packet(narrow, width, blocks), 1.0, "weights_packet",
                          query_weight, key_weight, value_weight, output_weight, source_query,
                          source_key, source_value, source_output, inner_weight, outer_weight,
                          inner_bias.reshape(1, wide), *[v.reshape(1, narrow) for v in short], room=58)
        first = after(first, sent)
        first = join([first, turned_swap(first, 0)])
        first_b = turned_swap(first, 1)
        rest = after(rest, first)
        rest_b = turned_swap(rest, 0)
        first = join(after([first, first_b], rest_b))
        rest = join(after([rest, rest_b], first_b, came, *kept_swaps))
        first_b, rest_b = turned_swap(first, 2, CROSSED), turned_swap(rest, 1)
        first_c = join([first, first_b])
        first_d = turned_swap(first_c, 3, CROSSED)
        second, third = run(make_part((5 * narrow + 16, 2 * blocks * narrow), width), 1.0, "part", rest, after(rest_b, first_b))
        second_b, third_b = turned_swap(second, 2), turned_swap(third, 2, CROSSED)
        second_c = join(after([second, second_b], first_d, third_b))
        third_c = join(after([third, third_b], first_d, second_b))
        second_d, third_d = turned_swap(second_c, 3), turned_swap(third_c, 3, CROSSED)
        first_d = after(first_d, second_c, third_c, *came_swaps)
        set_self = [first_c, first_d, swap(first_c, 1, 32), swap(first_d, 1, 32)]
    else:
        full = [whole(w) for w in (query_weight, key_weight, value_weight, output_weight, source_query, source_key, source_value, source_output)]
        lane = lax.broadcasted_iota(jnp.int32, (1, width), 1)
        place = lax.broadcasted_iota(jnp.int32, (blocks, width), 0) * width + lane
        spread_wide = jnp.where(place // wide == me, jnp.tile(inner_bias.reshape(1, wide), (blocks, width // wide)), 0)

        def natural(rows):
            return jnp.where(lane // narrow == me, jnp.tile(rows, (1, devices)), 0)

        vectors = jnp.concatenate([natural(jnp.stack(short[:2])), jnp.zeros((6, width), BF16), natural(jnp.stack(short[2:])), spread_wide, jnp.zeros((1, width), BF16)])
        vectors = reduce_all(vectors, devices).astype(F32)
        set_self = full[:3] + [vectors[:8]]
        set_cross = full[3:] + [vectors[8:]]
        set_inner = [
            whole(inner_weight).reshape(width, blocks, width).transpose(1, 0, 2),
            whole(outer_weight).reshape(blocks, width, width),
        ]
    found = run(
        make_project(packed, parts, rows, block, memory_block, width, narrow, len(set_self)), 5.0,
        "project", *set_self, *row_tokens,
    )
    query, query_t, keys, values, value_t = (found[2 * i : 2 * i + 2] for i in range(5))
    row_memory, ids, memory_ids = found[10:]
    query_t = list(query_t)
    if packed:
        set_query, set_last = set_self, set_self
    else:
        set_back, set_query, set_last, set_memory = [full[3], full[4], full[7]], full[:1], full[1:3], full[5:7]
    found = run(
        make_self_attention(share, parts * share, width), 12.0, "self_attention",
        *query_t, *keys, *value_t, ids,
    )
    mixtures, logs = found[:2], found[2:]
    if packed:
        second_d, third_d = after(second_d, mixtures[0]), after(third_d, mixtures[0])
        set_cross = [second_c, second_d, swap(second_c, 1, 32), swap(second_d, 1, 32)]
        set_inner = [third_c, third_d, swap(third_c, 1, 32), swap(third_d, 1, 32)]
        set_back, set_memory = set_cross, set_cross
    first_sum, second_sum, cross_query, memory_keys, memory_values, cross_t, cross_logs, vectors = run(
        make_cross_forward(packed, rows, block, parts * memory_share, width, narrow, len(set_cross)),
        9.0, "cross_forward", *set_cross, *own_tokens, row_memory, ids, memory_ids, *mixtures,
    )
    out_own, out_send, back2_in, sums_inner, *grads_inner = run(
        make_inner(packed, rows, block, width, hidden, narrow, len(set_inner)), 18.0, "inner",
        *set_inner, second_sum, kept, came, vectors,
    )
    out_came = swap(out_send, parts, devices)
    found = run(
        make_cross_back(packed, parts, share, memory_share, width, narrow, len(set_back)), 14.0,
        "cross_back", *set_back, back2_in, first_sum, second_sum, cross_query, memory_keys,
        memory_values, cross_t, cross_logs, ids, memory_ids, vectors, sums_inner, *mixtures,
    )
    back1, memory_key_own, memory_value_own, sums_cross = found[:4]
    slope, slope_t, deltas = (found[4 + 2 * i : 6 + 2 * i] for i in range(3))
    memory_received = [swap(a, m + 1, devices) for m, a in enumerate(found[10 : 10 + parts - 1])]
    grads_early = found[10 + parts - 1 :]
    query = list(query)
    if packed:
        keep, send = combine(after([grads_inner[0], swap(grads_inner[1], 1, 32)], back1, out_came), 2)
        inner_step = [keep, turned_swap(send, 3)]
        memory_key_own = after(memory_key_own, keep)
    memory_own, memory_send, *grads_cross = run(
        make_memory_back(packed, parts, rows, block, memory_block, width, narrow, len(set_memory)),
        2.0, "memory_back", *set_memory, *own_tokens, memory_key_own, memory_value_own, sums_cross,
        *grads_early, *memory_received,
    )
    if packed:
        cross_came = swap(grads_cross[1], 1, 32)
        query[0] = after(query[0], grads_cross[0])
    found = run(
        make_self_back_upper(parts, share, width), 7.0, "self_back_upper", query[0], keys[0],
        values[0], slope[0], slope_t[0], logs[0], deltas[0], ids,
    )
    query_upper, own_upper = found[:2]
    received_upper = [swap(a, m // 2 + 1, devices) for m, a in enumerate(found[2:])]
    if packed:
        keep_cross, send = combine(after([grads_cross[0], cross_came], query_upper), 2)
        cross_step = [keep_cross, turned_swap(send, 3, CROSSED)]
        query[1] = after(query[1], keep_cross)
    in_part, query_sum, query_w_grad, own_lower, *sends = run(
        make_self_back_lower(packed, parts, rows, block, width, narrow, len(set_query)), 11.0,
        "self_back_lower", *set_query, *own_tokens, query[1], keys[1], values[1], slope[1],
        slope_t[1], logs[1], deltas[1], ids, back1, query_upper,
    )
    received_lower = [swap(a, m // 2 + 1, devices) for m, a in enumerate(sends)]
    if packed:
        keep, send = combine(after(inner_step, query_sum), 2)
        inner_step = [keep, turned_swap(send, 2)]
        keep_cross, send = combine(after(cross_step, query_sum), 2)
        cross_step = [keep_cross, turned_swap(send, 2, CROSSED)]
        in_part = after(in_part, keep, keep_cross)
    in_own, in_send, *grads_last = run(
        make_last(packed, parts, rows, block, memory_block, width, narrow, len(set_last)), 6.0,
        "last", *set_last, *own_tokens, in_part, query_sum, query_w_grad, memory_send, own_upper,
        own_lower, *received_upper, *received_lower,
    )

    if packed:
        keep, send = combine([grads_last[0], swap(grads_last[1], 1, 32)], 2)
        last_step = [keep, turned_swap(send, 3)]
        in_send = after(in_send, last_step[1])
        keep_joint, send = combine_joint(after([inner_step, cross_step], in_own), 2)
        joint_step = [keep_joint, turned_swap(send, 1)]
        keep, send = combine(after(last_step, keep_joint), 2)
        last_step = [keep, turned_swap(send, 2)]
        keep_joint, send = combine(joint_step, 2)
        joint_step = [keep_joint, turned_swap(send, 0)]
        keep, send = combine(after(last_step, keep_joint), 2)
        last_step = [keep, turned_swap(send, 1)]
        keep, send = combine(last_step, 2)
        last_step = [keep, turned_swap(send, 0)]

        def plan(me_ref, *refs):
            me = me_ref[0]
            joint, last = (sum(r[0].astype(F32) for r in given) for given in (refs[:2], refs[2:4]))
            outs = refs[4:]
            inner, cross = joint[: 2 * blocks * narrow, :], joint[2 * blocks * narrow :, :]
            for i in range(blocks):
                outs[0][:, i * width : (i + 1) * width] = inner[i * narrow : (i + 1) * narrow, :]
            outs[1][...] = inner[blocks * narrow :, :]
            for i in range(5):
                outs[2 + i][...] = cross[i * narrow : (i + 1) * narrow, :]
            for i in range(3):
                outs[7 + i][...] = last[i * narrow : (i + 1) * narrow, :]
            rows_in = jnp.concatenate([cross[5 * narrow :, :], last[3 * narrow :, :]], axis=0)
            outs[10][...] = chosen(me, rows_in, narrow)
            per = width // wide
            line = lax.broadcasted_iota(jnp.int32, (blocks, width), 0)
            row = jnp.sum(jnp.where(line == lax.div(me, per), rows_in[3 : 3 + blocks, :], 0.0), axis=0, keepdims=True)
            outs[11][...] = chosen(lax.rem(me, per), row, wide)

        part = (narrow, width)
        shapes = [(narrow, hidden), (wide, width)] + [part] * 8 + [(24, narrow), (1, wide)]
        (inner_share, outer_share, source_key_share, source_value_share, source_output_share,
         source_query_share, output_share, key_share, value_share, query_share, sums,
         inner_bias_share) = call(
            plan, [(s, F32) for s in shapes], (me_array, *joint_step, *last_step), [], 2.0,
            "finish",
        )
        inner_bias_share = inner_bias_share.reshape(wide)
    else:
        def scatter(array):
            return lax.psum_scatter(array, AXES, scatter_dimension=0, tiled=True)

        inner_share = scatter(grads_inner[0].transpose(1, 0, 2).reshape(width, hidden))
        outer_share = scatter(grads_inner[1].reshape(hidden, width))
        source_output_share, source_query_share, output_share = (scatter(g.astype(F32)) for g in grads_early)
        source_key_share, source_value_share = (scatter(g) for g in grads_cross[:2])
        key_share, value_share = (scatter(g) for g in grads_last[:2])
        query_share = scatter(query_w_grad)
        sums = reduce_all(jnp.concatenate([grads_cross[2], grads_last[2]], axis=0), devices)
        inner_bias_share = lax.dynamic_slice(sums[3 : 3 + blocks].reshape(hidden), (me * wide,), (wide,))
        sums = lax.dynamic_slice(sums, (0, me * narrow), (sums.shape[0], narrow))
    def regroup(mine, came):
        came = came.astype(F32)
        return jnp.where(turn == 0, jnp.stack([mine, came]), jnp.stack([came, mine]))

    output = regroup(out_own, out_came)
    in_came = swap(in_send, parts, devices)
    input_gradient = regroup(in_own, in_came[:block])
    memory_gradient = regroup(memory_own, in_came[block:])

    return (
        output,
        input_gradient,
        memory_gradient,
        query_share,
        key_share,
        value_share,
        output_share,
        sums[16],
        sums[17],
        sums[13],
        sums[11],
        sums[12],
        source_query_share,
        source_key_share,
        source_value_share,
        source_output_share,
        sums[10],
        sums[14],
        sums[9],
        sums[7],
        sums[8],
        inner_share,
        inner_bias_share,
        outer_share,
        sums[2],
        sums[0],
        sums[1],
    )


def solution(mesh):
    sequence, devices = mesh.shape["seq"], mesh.size
    tokens, ids = P("dp", "seq", None), P("dp", "seq")
    matrix, vector = P(AXES, None), P(AXES)
    attention = (matrix,) * 4 + (vector,) * 5
    inner = (matrix, vector, matrix, vector, vector, vector)
    return jax.shard_map(
        functools.partial(per_device, devices=devices, sequence=sequence),
        mesh=mesh,
        in_specs=(tokens, tokens, ids, ids, tokens) + attention + attention + inner,
        out_specs=(tokens, tokens, tokens) + attention + attention + inner,
        check_vma=False,
    )
```

```python
import functools
import math

import jax
import jax.numpy as jnp
from jax import lax
from jax.experimental import pallas as pl
from jax.experimental.pallas import tpu as pltpu
from jax.sharding import PartitionSpec as P

HEADS = 8
HEAD_DIM = 64
PAIR = 128
EPSILON = 1e-05
MASKED = 1e9
AXES = ("dp", "seq")
F32 = jnp.float32
BF16 = jnp.bfloat16

(
    OUTPUT_BIAS,
    ATTENTION_GAIN,
    ATTENTION_SHIFT,
    SOURCE_QUERY_BIAS,
    SOURCE_VALUE_BIAS,
    SOURCE_OUTPUT_BIAS,
    SOURCE_GAIN,
    SOURCE_SHIFT,
    OUTER_BIAS,
    FINAL_GAIN,
    FINAL_SHIFT,
    INNER_BIAS,
) = range(12)
Z_MASKS = (0, 8, 16, 24)
VM = pl.BlockSpec(memory_space=pltpu.VMEM)
SM = pl.BlockSpec(memory_space=pltpu.SMEM)


def dot(a, b):
    return lax.dot_general(a, b, (((1,), (0,)), ((), ())), preferred_element_type=F32)


def dot_nt(a, b):
    return lax.dot_general(a, b, (((1,), (1,)), ((), ())), preferred_element_type=F32)


def dot_tn(a, b):
    return lax.dot_general(a, b, (((0,), (0,)), ((), ())), preferred_element_type=F32)


def total(values):
    return jnp.sum(values.astype(F32), axis=0, keepdims=True)


def normalize(h):
    average = jnp.mean(h, axis=-1, keepdims=True)
    centered = h - average
    variance = jnp.mean(centered * centered, axis=-1, keepdims=True)
    inverse = lax.rsqrt(variance + EPSILON)
    return centered * inverse, inverse


def normalize_back(upstream, normed, inverse, gain):
    scaled = upstream * gain
    first_mean = jnp.mean(scaled, axis=-1, keepdims=True)
    second_mean = jnp.mean(scaled * normed, axis=-1, keepdims=True)
    return inverse * (scaled - first_mean - normed * second_mean)


def normal_parts(v):
    density = 0.3989422804014327 * jnp.exp(-0.5 * v * v)
    t = 1.0 / (1.0 + 0.2316419 * jnp.abs(v))
    series = t * (
        0.319381530
        + t * (-0.356563782 + t * (1.781477937 + t * (-1.821255978 + t * 1.330274429)))
    )
    tail = density * series
    return jnp.where(v >= 0.0, 1.0 - tail, tail), density


def penalties(ids):
    place = lax.broadcasted_iota(jnp.int32, (PAIR, ids.shape[1]), 0)
    return jnp.where((place == ids) | (place >= 4), 0.0, -MASKED).astype(BF16)


def one_hot(ids):
    place = lax.broadcasted_iota(jnp.int32, (PAIR, ids.shape[1]), 0)
    return jnp.where(place == ids, 1.0, 0.0).astype(F32).T.astype(BF16)


def spread(part, half):
    empty = jnp.zeros_like(part)
    return [part, empty] if half == 0 else [empty, part]


def attend(query_t, keys, value_t, hot, penalty, mixture_t, logs):
    length = keys.shape[0]

    def pair(p, carry):
        columns = pl.ds(pl.multiple_of(p * PAIR, PAIR), PAIR)
        left = jnp.concatenate([keys[:, columns], hot[...]], axis=1)
        for half in range(2):
            rows = pl.ds(pl.multiple_of(p * PAIR + half * HEAD_DIM, HEAD_DIM), HEAD_DIM)
            right = jnp.concatenate(spread(query_t[rows, :], half) + [penalty[...]], axis=0)
            scores = dot(left, right)
            highest = jnp.max(scores, axis=0, keepdims=True)
            weights = jnp.exp(scores - highest).astype(BF16)
            values = jnp.concatenate(
                [value_t[rows, :], jnp.ones((16, length), BF16)], axis=0
            )
            found = dot(values, weights)
            denominator = found[HEAD_DIM : HEAD_DIM + 1, :]
            mixture_t[rows, :] = (found[:HEAD_DIM, :] / denominator).astype(BF16)
            logs[2 * p + half] = highest + jnp.log(denominator)
        return carry

    lax.fori_loop(0, keys.shape[1] // PAIR, pair, 0)


def attend_back(
    query_t, query, keys, key_t, values, slope_t, slope, hot, penalty, logs, deltas,
    query_grad_t, key_grad, value_grad,
):
    tokens = query.shape[0]
    lane = lax.broadcasted_iota(jnp.int32, (tokens, PAIR), 1)

    def pair(p, carry):
        columns = pl.ds(pl.multiple_of(p * PAIR, PAIR), PAIR)
        left = jnp.concatenate([keys[:, columns], hot[...]], axis=1)
        value_pair = values[:, columns]
        key_sum, value_sum = None, None
        for half in range(2):
            rows = pl.ds(pl.multiple_of(p * PAIR + half * HEAD_DIM, HEAD_DIM), HEAD_DIM)
            right = jnp.concatenate(spread(query_t[rows, :], half) + [penalty[...]], axis=0)
            chances = jnp.exp(dot(left, right) - logs[2 * p + half])
            slopes = dot(value_pair, jnp.concatenate(spread(slope_t[rows, :], half), axis=0))
            grads = (chances * (slopes - deltas[2 * p + half])).astype(BF16)
            query_grad_t[rows, :] = dot(key_t[rows, :], grads) * HEAD_DIM**-0.5
            mine = (lane < HEAD_DIM) if half == 0 else (lane >= HEAD_DIM)
            none = jnp.zeros((tokens, PAIR), BF16)
            value_part = dot(chances.astype(BF16), jnp.where(mine, slope[:, columns], none))
            key_part = dot(grads, jnp.where(mine, query[:, columns], none))
            value_sum = value_part if value_sum is None else value_sum + value_part
            key_sum = key_part if key_sum is None else key_sum + key_part
        key_grad[:, columns] = key_sum
        value_grad[:, columns] = value_sum
        return carry

    lax.fori_loop(0, keys.shape[1] // PAIR, pair, 0)


def deltas_of(slope_t, mixture_t, deltas):
    for head in range(slope_t.shape[0] // HEAD_DIM):
        rows = slice(head * HEAD_DIM, (head + 1) * HEAD_DIM)
        deltas[head] = jnp.sum(
            slope_t[rows, :].astype(F32) * mixture_t[rows, :].astype(F32), axis=0, keepdims=True
        )


def swap(array, mask, devices):
    return lax.ppermute(array, AXES, [(i, i ^ mask) for i in range(devices)])


Z_FIRST = ((8, 24, 2, 4), (24, 8, 4, 2))
CROSSED = ((8, 24, 4, 2), (24, 8, 2, 4))


def turned_swap(array, step, orders=Z_FIRST):
    return lax.ppermute(array, AXES, [(i, i ^ orders[i % 2][step]) for i in range(32)])


def after(value, *others):
    return lax.optimization_barrier((value, others))[0]


def places(me, orders=Z_FIRST):
    found = []
    for core in range(2):
        even = ((me & 1) ^ core) == 0
        masks = [jnp.where(even, first, second) for first, second in zip(*orders)]
        for far in range(2):
            for slot in range(8):
                device = me ^ core if core else me
                for step, bit in enumerate((slot & 1, slot & 2, slot & 4, far)):
                    if bit:
                        device = device ^ masks[step]
                found.append((core, far, slot, device))
    return found


def unpack(me, pieces, stride, first, rows, scratch, orders=Z_FIRST):
    for core, far, slot, device in places(me, orders):
        ref = pieces[2 * core + far]
        at = slot * stride + first
        scratch[pl.ds(pl.multiple_of(device * rows, rows), rows), :] = ref[at : at + rows, :]


def vector_sum(pieces, stride, first):
    found = None
    for ref in pieces:
        for slot in range(8):
            part = ref[slot * stride + first : (slot + 1) * stride, :].astype(F32)
            found = part if found is None else found + part
    return found


class Grads:
    def __init__(self, me, refs, dense, rows, orders=Z_FIRST):
        self.me, self.refs, self.dense, self.rows, self.orders = me, refs, dense, rows, orders

    def put(self, index, grad):
        if self.dense is None:
            self.refs[index][...] = grad
            return
        self.dense[...] = grad
        rows = self.rows
        for core, far, slot, device in places(self.me, self.orders):
            found = self.dense[pl.ds(pl.multiple_of(device * rows, rows), rows), :]
            self.refs[core][far * 8 + slot, index * rows : (index + 1) * rows, :] = found.astype(BF16)

    def put_sums(self, first, sums):
        if self.dense is None:
            self.refs[-1][...] = sums
            return
        low = sums.astype(BF16)
        for ref in self.refs:
            for slot in range(16):
                ref[slot, first : first + sums.shape[0], :] = low


def grad_outs(packed, count, rows, width, sums):
    if packed:
        return [((16, count * rows + sums, width), BF16)] * 2
    return [((width, width), F32)] * count + [((sums, width), F32)]


COSTS = {}


def padded(shape, dtype):
    last = -(-shape[-1] // 128) * 128
    tall = -(-shape[-2] // 16) * 16 if len(shape) > 1 else 16
    return math.prod(shape[:-2]) * tall * last * jnp.dtype(dtype).itemsize


def snug(arrays):
    return 2 * sum(padded(a.shape, a.dtype) for a in arrays) + (3 << 20)


def call(kernel, outs, args, scratch, micros, name, room=10):
    moved = sum(math.prod(a.shape) * a.dtype.itemsize for a in args[1:])
    moved += sum(math.prod(s) * jnp.dtype(d).itemsize for s, d in outs)
    need = sum(padded(a.shape, a.dtype) for a in args[1:])
    need += sum(padded(s, d) for s, d in list(outs) + list(scratch))
    return pl.pallas_call(
        kernel,
        out_shape=[jax.ShapeDtypeStruct(s, d) for s, d in outs],
        in_specs=[SM] + [VM] * (len(args) - 1),
        out_specs=[VM] * len(outs),
        scratch_shapes=[pltpu.VMEM(s, d) for s, d in scratch],
        compiler_params=pltpu.CompilerParams(vmem_limit_bytes=min(need + (room << 20), 58 << 20)),
        cost_estimate=pl.CostEstimate(
            flops=int(COSTS.get(name, 0) * 1.15e9) + 1, bytes_accessed=1, transcendentals=0
        ),
        name=name,
    )(*args)


def tokens_packet(turn, tokens, memory, target_ids, source_ids, cotangent):
    block, width = tokens.shape[1:]
    memory_block = memory.shape[1]
    first = block + memory_block + 8

    def kernel(turn_ref, targets, sources, tokens_ref, memory_ref, cot_ref, sent, kept):
        mine = turn_ref[0]
        for row, out in ((1 - mine, sent), (mine, kept)):
            out[:block, :] = tokens_ref[row]
            out[block : block + memory_block, :] = memory_ref[row]
            ids = targets[pl.ds(row, 1), :].astype(F32)
            ids = jnp.concatenate([ids, jnp.zeros((1, width - block), F32)], axis=1)
            others = sources[pl.ds(row, 1), :].astype(F32)
            others = jnp.concatenate([others, jnp.zeros((1, width - memory_block), F32)], axis=1)
            place = lax.broadcasted_iota(jnp.int32, (8, width), 0)
            found = jnp.where(place == 0, ids, jnp.where(place == 1, others, 0.0))
            out[block + memory_block : first, :] = found.astype(BF16)
            out[first:, :] = cot_ref[row]

    shape = (first + block, width)
    return call(kernel, [(shape, BF16)] * 2, (turn, target_ids, source_ids, tokens, memory, cotangent),
                [], 1.0, "tokens_packet", 58)


def placed(me, parts, width):
    here = lax.broadcasted_iota(jnp.int32, (parts.shape[1], width), 0) + me * parts.shape[1]
    lane = lax.broadcasted_iota(jnp.int32, (parts.shape[1], width), 1)
    return dot(parts, jnp.where(lane == here, 1.0, 0.0).astype(BF16))


def make_weights_packet(narrow, width, blocks):
    tall = blocks * narrow

    def kernel(me_ref, *refs):
        weights, inner, outer, wide, short = refs[:8], refs[8], refs[9], refs[10], refs[11:24]
        first, rest = refs[24:]
        me, middle = me_ref[0], 5 * narrow + 16
        for i, ref in enumerate(weights):
            if i < 3:
                first[i * narrow : (i + 1) * narrow, :] = ref[...]
            else:
                rest[(i - 3) * narrow : (i - 2) * narrow, :] = ref[...]
        short = jnp.concatenate([ref[...].astype(F32) for ref in short], axis=0).astype(BF16)
        found = placed(me, short, width)
        first[3 * narrow :, :] = jnp.concatenate([found[:2, :], jnp.zeros((6, width), F32)], axis=0).astype(BF16)
        per = width // wide.shape[1]
        row = placed(lax.rem(me, per), wide[...], width)
        place = lax.broadcasted_iota(jnp.int32, (blocks, width), 0)
        spread_row = jnp.where(place == lax.div(me, per), row, 0.0)
        none = jnp.zeros((16 - (found.shape[0] - 2) - blocks, width), F32)
        rest[5 * narrow : middle, :] = jnp.concatenate([found[2:, :], spread_row, none], axis=0).astype(BF16)
        for i in range(blocks):
            rest[middle + i * narrow : middle + (i + 1) * narrow, :] = inner[:, i * width : (i + 1) * width]
        rest[middle + tall :, :] = outer[...]

    return kernel, [((rows, width), BF16) for rows in (3 * narrow + 8, 5 * narrow + 16 + 2 * tall)]


def make_part(sizes, width):
    tall = sum(sizes)

    def kernel(me_ref, upper, lower, *outs):
        for i in range(4):
            ref, at = (upper, lower)[i // 2], i % 2 * tall
            for size, out in zip(sizes, outs):
                out[i * size : (i + 1) * size, :] = ref[at : at + size, :]
                at += size

    return kernel, [((4 * size, width), BF16) for size in sizes]


def join(arrays):
    def kernel(*refs):
        at = 0
        for ref in refs[:-1]:
            refs[-1][at : at + ref.shape[0], :] = ref[...]
            at += ref.shape[0]

    rows = sum(a.shape[0] for a in arrays)
    return pl.pallas_call(
        kernel,
        out_shape=jax.ShapeDtypeStruct((rows, arrays[0].shape[1]), arrays[0].dtype),
        in_specs=[VM] * len(arrays),
        out_specs=VM,
        compiler_params=pltpu.CompilerParams(vmem_limit_bytes=snug(arrays)),
        cost_estimate=pl.CostEstimate(flops=1 << 20, bytes_accessed=0, transcendentals=0),
        name="join",
    )(*arrays)


def make_project(packed, parts, rows, block, memory_block, width, narrow, n_pieces):
    share = rows * block
    length = parts * share
    memory_share = rows * memory_block
    stride = 3 * narrow + 8
    half = width // 2

    def kernel(*refs):
        me_ref, refs = refs[0], list(refs[1:])
        pieces, refs = refs[:n_pieces], refs[n_pieces:]
        tokens, refs = refs[: parts * rows], refs[parts * rows :]
        query, query_t, keys, values, value_t = (refs[2 * i : 2 * i + 2] for i in range(5))
        memory, ids, memory_ids = refs[10:13]
        scratch = refs[13:]
        me = me_ref[0]
        if packed:
            for i in range(3):
                unpack(me, pieces, stride, i * narrow, narrow, scratch[i], CROSSED)
            query_w, key_w, value_w = scratch
            biases = vector_sum(pieces, stride, 3 * narrow)
        else:
            query_w, key_w, value_w = pieces[:3]
            biases = pieces[3][...]
        for i in range(parts):
            here = slice(i * share, (i + 1) * share)
            some = tokens[i * rows : (i + 1) * rows]
            own = jnp.concatenate([t[:block, :] for t in some], axis=0)
            if i == 0:
                scaled = (dot(own, query_w[...]) + biases[0:1, :]).astype(BF16) * BF16(HEAD_DIM**-0.5)
            key = dot(own, key_w[...]).astype(BF16)
            found = (dot(own, value_w[...]) + biases[1:2, :]).astype(BF16)
            for side in range(2):
                columns = slice(side * half, (side + 1) * half)
                if i == 0:
                    query[side][...] = scaled[:, columns]
                    query_t[side][...] = scaled[:, columns].T
                keys[side][here, :] = key[:, columns]
                values[side][here, :] = found[:, columns]
                value_t[side][:, here] = found[:, columns].T
        for i, t in enumerate(tokens):
            memory[i * memory_block : (i + 1) * memory_block, :] = t[block : block + memory_block, :]
            found = t[block + memory_block : block + memory_block + 8, :].astype(F32).astype(jnp.int32)
            ids[:, i * block : (i + 1) * block] = found[0:1, :block]
        found = [t[block + memory_block : block + memory_block + 8, :].astype(F32).astype(jnp.int32)[1:2, :memory_block] for t in tokens]
        memory_ids[...] = jnp.concatenate(found, axis=1)

    outs = [((share, half), BF16)] * 2 + [((half, share), BF16)] * 2
    outs += [((length, half), BF16)] * 4 + [((half, length), BF16)] * 2
    outs += [
        ((parts * memory_share, width), BF16),
        ((1, length), jnp.int32),
        ((1, parts * memory_share), jnp.int32),
    ]
    return kernel, outs, [((width, width), BF16)] * 3 if packed else []


def make_self_attention(share, length, width):
    def kernel(me_ref, *refs):
        query_t, keys, value_t, ids = refs[:2], refs[2:4], refs[4:6], refs[6]
        mixture_t, logs, hot, penalty = refs[7:9], refs[9:11], refs[11], refs[12]
        hot[...] = one_hot(ids[...])
        penalty[...] = penalties(ids[:, :share])
        for side in range(2):
            attend(query_t[side], keys[side], value_t[side], hot, penalty, mixture_t[side], logs[side])

    outs = [((width // 2, share), BF16)] * 2 + [((HEADS // 2, 1, share), F32)] * 2
    return kernel, outs, [((length, PAIR), BF16), ((PAIR, share), BF16)]


def make_cross_forward(packed, rows, block, memory_length, width, narrow, n_pieces):
    share = rows * block
    stride = 5 * narrow + 16

    def kernel(*refs):
        me_ref, refs = refs[0], list(refs[1:])
        pieces, refs = refs[:n_pieces], refs[n_pieces:]
        tokens, refs = refs[:rows], refs[rows:]
        memory, ids, memory_ids, upper, lower = refs[:5]
        first_sum, second_sum, query, memory_keys, memory_values, cross_t, logs, vectors = refs[5:13]
        scratch = refs[13:]
        query_t, value_t, hot, penalty = scratch[:4]
        if packed:
            for i in range(5):
                unpack(me_ref[0], pieces, stride, i * narrow, narrow, scratch[4 + i])
            output_w, query_w, key_w, value_w, source_w = scratch[4:]
            vectors[...] = vector_sum(pieces, stride, 5 * narrow)
        else:
            output_w, query_w, key_w, value_w, source_w = pieces[:5]
            vectors[...] = pieces[5][...]

        def vector(i):
            return vectors[i : i + 1, :]

        own = jnp.concatenate([t[:block, :] for t in tokens], axis=0)
        mixture_t = jnp.concatenate([upper[...], lower[...]], axis=0)
        h = own.astype(F32) + dot_tn(mixture_t, output_w[...]) + vector(OUTPUT_BIAS)
        first_sum[...] = h
        first = normalize(h)[0] * vector(ATTENTION_GAIN) + vector(ATTENTION_SHIFT)
        scaled = (dot(first.astype(BF16), query_w[...]) + vector(SOURCE_QUERY_BIAS)).astype(BF16) * BF16(HEAD_DIM**-0.5)
        query[...] = scaled
        query_t[...] = scaled.T
        memory_keys[...] = dot(memory[...], key_w[...]).astype(BF16)
        memory_values[...] = (dot(memory[...], value_w[...]) + vector(SOURCE_VALUE_BIAS)).astype(BF16)
        value_t[...] = memory_values[...].T
        hot[...] = one_hot(memory_ids[...])
        penalty[...] = penalties(ids[:, :share])
        attend(query_t, memory_keys, value_t, hot, penalty, cross_t, logs)
        first = normalize(first_sum[...])[0] * vector(ATTENTION_GAIN) + vector(ATTENTION_SHIFT)
        second_sum[...] = first + dot_tn(cross_t[...], source_w[...]) + vector(SOURCE_OUTPUT_BIAS)

    outs = [
        ((share, width), F32),
        ((share, width), F32),
        ((share, width), BF16),
        ((memory_length, width), BF16),
        ((memory_length, width), BF16),
        ((width, share), BF16),
        ((HEADS, 1, share), F32),
        ((16, width), F32),
    ]
    scratch = [((width, share), BF16), ((width, memory_length), BF16), ((memory_length, PAIR), BF16), ((PAIR, share), BF16)]
    if packed:
        scratch += [((width, width), BF16)] * 5
    return kernel, outs, scratch


def make_inner(packed, rows, block, width, hidden, narrow, n_pieces):
    blocks = hidden // width
    share = rows * block
    per = width // (blocks * narrow)

    def kernel(*refs):
        me_ref, refs = refs[0], list(refs[1:])
        pieces, refs = refs[:n_pieces], refs[n_pieces:]
        second_sum, cot_own, cot_came, vectors = refs[:4]
        out_own, out_send, back, sums = refs[4:8]
        grads, scratch = refs[8:10], refs[10:]
        low, active, gate, slope = scratch[:4]
        if packed:
            inner_w, outer_w, gathered, dense = scratch[4:8]
            tall = blocks * narrow
            for core, far, slot, device in places(me_ref[0], CROSSED):
                ref, at = pieces[2 * core + far], slot * 2 * tall
                row = pl.multiple_of(device * narrow, narrow)
                for i in range(blocks):
                    inner_w[i, pl.ds(row, narrow), :] = ref[at + i * narrow : at + (i + 1) * narrow, :]
                row = pl.multiple_of(lax.rem(device, per) * tall, tall)
                outer_w[lax.div(device, per), pl.ds(row, tall), :] = ref[at + tall : at + 2 * tall, :]
        else:
            inner_w, outer_w = pieces

        def vector(i):
            return vectors[i : i + 1, :]

        second = normalize(second_sum[...])[0] * vector(SOURCE_GAIN) + vector(SOURCE_SHIFT)
        low[...] = second.astype(BF16)
        back[...] = second + vector(OUTER_BIAS)

        def forward(i, carry):
            inner = dot(low[...], inner_w[i]) + vectors[pl.ds(INNER_BIAS + i, 1), :]
            chance, density = normal_parts(inner)
            found = (inner * chance).astype(BF16)
            active[i] = found
            gate[i] = chance + inner * density
            back[...] += dot(found, outer_w[i])
            return carry

        lax.fori_loop(0, blocks, forward, 0)
        normed, inverse = normalize(back[...])
        final = normed * vector(FINAL_GAIN) + vector(FINAL_SHIFT)
        out_own[...] = final[:block, :]
        out_send[...] = final[block:, :].astype(BF16)
        upstream = jnp.concatenate([cot_own[-block:, :], cot_came[-block:, :]], axis=0).astype(F32)
        sums[0:1, :] = total(upstream * normed)
        sums[1:2, :] = total(upstream)
        back3 = normalize_back(upstream, normed, inverse, vector(FINAL_GAIN))
        slope[...] = back3.astype(BF16)
        sums[2:3, :] = total(slope[...])
        sums[7:8, :] = jnp.zeros_like(sums[7:8, :])
        back[...] = back3

        def backward(i, carry):
            grad = dot_nt(slope[...], outer_w[i]) * gate[i]
            inner_low = grad.astype(BF16)
            sums[pl.ds(3 + i, 1), :] = total(inner_low)
            outer_grad = dot_tn(active[i], slope[...])
            inner_grad = dot_tn(low[...], inner_low)
            back[...] += dot_nt(inner_low, inner_w[i])
            if packed:
                dense[...] = inner_grad
                gathered[i] = outer_grad.astype(BF16)
                here = pl.ds(pl.multiple_of(i * narrow, narrow), narrow)
                for core, far, slot, device in places(me_ref[0]):
                    row = pl.multiple_of(device * narrow, narrow)
                    grads[core][far * 8 + slot, here, :] = dense[pl.ds(row, narrow), :].astype(BF16)
            else:
                grads[0][i] = inner_grad
                grads[1][i] = outer_grad
            return carry

        lax.fori_loop(0, blocks, backward, 0)
        if packed:
            tall = blocks * narrow
            for core, far, slot, device in places(me_ref[0]):
                row = pl.multiple_of(lax.rem(device, per) * tall, tall)
                grads[core][far * 8 + slot, tall:, :] = gathered[lax.div(device, per), pl.ds(row, tall), :]

    outs = [((block, width), F32), ((block, width), BF16), ((share, width), F32), ((8, width), F32)]
    if packed:
        outs += [((16, 2 * blocks * narrow, width), BF16)] * 2
    else:
        outs += [((blocks, width, width), F32)] * 2
    scratch = [((share, width), BF16), ((blocks, share, width), BF16), ((blocks, share, width), F32), ((share, width), BF16)]
    if packed:
        scratch += [((blocks, width, width), BF16)] * 3 + [((width, width), F32)]
    return kernel, outs, scratch


def make_cross_back(packed, parts, share, memory_share, width, narrow, n_pieces):
    memory_length = parts * memory_share
    stride = 5 * narrow + 16

    def kernel(*refs):
        me_ref, refs = refs[0], list(refs[1:])
        pieces, refs = refs[:n_pieces], refs[n_pieces:]
        (back2_in, first_sum, second_sum, query, memory_keys, memory_values, cross_t, logs, ids,
         memory_ids, vectors, sums_inner) = refs[:12]
        mixtures, refs = refs[12:14], refs[14:]
        back1, key_own, value_own, sums = refs[:4]
        self_slope, self_slope_t, self_deltas = (refs[4 + 2 * i : 6 + 2 * i] for i in range(3))
        sends, refs = refs[10 : 10 + parts - 1], refs[10 + parts - 1 :]
        grads, scratch = refs[:3], refs[3:]
        (slope_t, slope, key_t, hot, penalty, query_t, deltas, query_grad_t, key_grad, value_grad) = scratch[:10]
        upper, lower = mixtures
        if packed:
            for i, at in enumerate((0, 1, 4)):
                unpack(me_ref[0], pieces, stride, at * narrow, narrow, scratch[10 + i])
            output_w, query_w, source_w = scratch[10:13]
        else:
            output_w, query_w, source_w = pieces

        def vector(i):
            return vectors[i : i + 1, :]

        sums[0:7, :] = sums_inner[0:7, :]
        upstream = back2_in[...]
        normed, inverse = normalize(second_sum[...])
        sums[7:8, :] = total(upstream * normed)
        sums[8:9, :] = total(upstream)
        back2 = normalize_back(upstream, normed, inverse, vector(SOURCE_GAIN))
        back1[...] = back2
        cross_low = back2.astype(BF16)
        sums[9:10, :] = total(cross_low)
        grads[0][...] = dot(cross_t[...], cross_low).astype(BF16)
        found = dot_nt(cross_low, source_w[...]).astype(BF16)
        slope[...] = found
        slope_t[...] = found.T
        deltas_of(slope_t, cross_t, deltas)
        query_t[...] = query[...].T
        key_t[...] = memory_keys[...].T
        hot[...] = one_hot(memory_ids[...])
        penalty[...] = penalties(ids[:, :share])
        attend_back(query_t, query, memory_keys, key_t, memory_values, slope_t, slope, hot, penalty,
                    logs, deltas, query_grad_t, key_grad, value_grad)
        key_own[...] = key_grad[:memory_share, :]
        value_own[...] = value_grad[:memory_share, :]
        for i in range(1, parts):
            here = slice(i * memory_share, (i + 1) * memory_share)
            sends[i - 1][:memory_share, :] = key_grad[here, :].astype(BF16)
            sends[i - 1][memory_share:, :] = value_grad[here, :].astype(BF16)
        query_low = query_grad_t[...].T.astype(BF16)
        sums[10:11, :] = total(query_low)
        normed, inverse = normalize(first_sum[...])
        first_low = (normed * vector(ATTENTION_GAIN) + vector(ATTENTION_SHIFT)).astype(BF16)
        grads[1][...] = dot_tn(first_low, query_low).astype(BF16)
        upstream = back1[...] + dot_nt(query_low, query_w[...])
        sums[11:12, :] = total(upstream * normed)
        sums[12:13, :] = total(upstream)
        grad = normalize_back(upstream, normed, inverse, vector(ATTENTION_GAIN))
        back1[...] = grad
        branch_low = grad.astype(BF16)
        sums[13:14, :] = total(branch_low)
        sums[14:16, :] = jnp.zeros_like(sums[14:16, :])
        mixture_t = jnp.concatenate([upper[...], lower[...]], axis=0)
        grads[2][...] = dot(mixture_t, branch_low).astype(BF16)
        found = dot_nt(branch_low, output_w[...]).astype(BF16)
        for side in range(2):
            columns = slice(side * width // 2, (side + 1) * width // 2)
            self_slope[side][...] = found[:, columns]
            self_slope_t[side][...] = found[:, columns].T
            deltas_of(self_slope_t[side], mixtures[side], self_deltas[side])

    half = width // 2
    outs = [
        ((share, width), F32),
        ((memory_share, width), F32),
        ((memory_share, width), F32),
        ((16, width), F32),
    ]
    outs += [((share, half), BF16)] * 2 + [((half, share), BF16)] * 2
    outs += [((HEADS // 2, 1, share), F32)] * 2
    outs += [((2 * memory_share, width), BF16)] * (parts - 1)
    outs += [((width, width), BF16)] * 3
    scratch = [
        ((width, share), BF16),
        ((share, width), BF16),
        ((width, memory_length), BF16),
        ((memory_length, PAIR), BF16),
        ((PAIR, share), BF16),
        ((width, share), BF16),
        ((HEADS, 1, share), F32),
        ((width, share), F32),
        ((memory_length, width), F32),
        ((memory_length, width), F32),
    ]
    if packed:
        scratch += [((width, width), BF16)] * 3
    return kernel, outs, scratch


def attention_back_half(refs, share, scratch):
    query, keys, values, slope, slope_t, logs, deltas, ids = refs
    query_t, key_t, hot, penalty, query_grad_t, key_grad, value_grad = scratch
    query_t[...] = query[...].T
    key_t[...] = keys[...].T
    hot[...] = one_hot(ids[...])
    penalty[...] = penalties(ids[:, :share])
    attend_back(query_t, query, keys, key_t, values, slope_t, slope, hot, penalty, logs, deltas,
                query_grad_t, key_grad, value_grad)


def half_scratch(share, length, half):
    return [
        ((half, share), BF16),
        ((half, length), BF16),
        ((length, PAIR), BF16),
        ((PAIR, share), BF16),
        ((half, share), F32),
        ((length, half), F32),
        ((length, half), F32),
    ]


def give_half(share, scratch, own, sends):
    key_grad, value_grad = scratch[5:7]
    own[:share, :] = key_grad[:share, :]
    own[share:, :] = value_grad[:share, :]
    for i, send in enumerate(sends):
        here = slice((i // 2 + 1) * share, (i // 2 + 2) * share)
        send[...] = (key_grad, value_grad)[i % 2][here, :].astype(BF16)


def make_memory_back(packed, parts, rows, block, memory_block, width, narrow, n_pieces):
    memory_share = rows * memory_block

    def kernel(*refs):
        me_ref, refs = refs[0], list(refs[1:])
        pieces, refs = refs[:n_pieces], refs[n_pieces:]
        tokens, refs = refs[:rows], refs[rows:]
        memory_key_own, memory_value_own, sums_in = refs[:3]
        early, refs = refs[3:6], refs[6:]
        memory_received, refs = refs[: parts - 1], refs[parts - 1 :]
        memory_own, memory_send = refs[:2]
        n_grads = 2 if packed else 3
        grad_refs, scratch = refs[2 : 2 + n_grads], refs[2 + n_grads :]
        sums = scratch[0]
        me = me_ref[0]
        if packed:
            for i in range(2):
                unpack(me, pieces, 5 * narrow + 16, (2 + i) * narrow, narrow, scratch[1 + i])
            source_key, source_value = scratch[1:3]
        else:
            source_key, source_value = pieces
        grads = Grads(me, grad_refs, scratch[3] if packed else None, narrow, CROSSED)
        memory = jnp.concatenate([t[block : block + memory_block, :] for t in tokens], axis=0)
        key_sum, value_sum = memory_key_own[...], memory_value_own[...]
        for ref in memory_received:
            key_sum = key_sum + ref[:memory_share, :].astype(F32)
            value_sum = value_sum + ref[memory_share:, :].astype(F32)
        key_low, value_low = key_sum.astype(BF16), value_sum.astype(BF16)
        sums[...] = sums_in[...]
        sums[14:15, :] = total(value_low)
        grads.put_sums(5 * narrow, sums[...])
        grads.put(0, dot_tn(memory, key_low))
        grads.put(1, dot_tn(memory, value_low))
        if packed:
            for i, ref in enumerate(early):
                grads.put(2 + i, ref[...].astype(F32))
        grad = dot_nt(key_low, source_key[...]) + dot_nt(value_low, source_value[...])
        memory_own[...] = grad[:memory_block, :]
        memory_send[...] = grad[memory_block:, :].astype(BF16)

    outs = [((memory_block, width), F32), ((memory_block, width), BF16)]
    if packed:
        outs += [((16, 5 * narrow + 16, width), BF16)] * 2
    else:
        outs += [((width, width), F32)] * 2 + [((16, width), F32)]
    scratch = [((16, width), F32)]
    if packed:
        scratch += [((width, width), BF16)] * 2 + [((width, width), F32)]
    return kernel, outs, scratch


def make_self_back_upper(parts, share, width):
    length, half = parts * share, width // 2

    def kernel(*refs):
        operands, (query_grad, own), refs = refs[1:9], refs[9:11], refs[11:]
        sends, scratch = refs[: 2 * parts - 2], refs[2 * parts - 2 :]
        attention_back_half(operands, share, scratch)
        query_grad[...] = scratch[4][...].T.astype(BF16)
        give_half(share, scratch, own, sends)

    outs = [((share, half), BF16), ((2 * share, half), F32)] + [((share, half), BF16)] * (2 * parts - 2)
    return kernel, outs, half_scratch(share, length, half)


def make_self_back_lower(packed, parts, rows, block, width, narrow, n_pieces):
    share = rows * block
    length, half = parts * share, width // 2

    def kernel(*refs):
        me_ref, refs = refs[0], list(refs[1:])
        pieces, refs = refs[:n_pieces], refs[n_pieces:]
        tokens, refs = refs[:rows], refs[rows:]
        operands, refs = refs[:8], refs[8:]
        back1, query_upper = refs[:2]
        in_part, query_sum, query_w_grad, own = refs[2:6]
        sends, scratch = refs[6 : 4 + 2 * parts], refs[4 + 2 * parts :]
        if packed:
            unpack(me_ref[0], pieces, 3 * narrow + 8, 0, narrow, scratch[7], CROSSED)
            query_w = scratch[7]
        else:
            (query_w,) = pieces
        attention_back_half(operands, share, scratch[:7])
        give_half(share, scratch, own, sends)
        query_low = jnp.concatenate([query_upper[...], scratch[4][...].T.astype(BF16)], axis=1)
        tokens_own = jnp.concatenate([t[:block, :] for t in tokens], axis=0)
        in_part[...] = back1[...] + dot_nt(query_low, query_w[...])
        query_sum[...] = jnp.concatenate([total(query_low), jnp.zeros((7, width), F32)], axis=0)
        query_w_grad[...] = dot_tn(tokens_own, query_low).astype(query_w_grad.dtype)

    outs = [
        ((share, width), F32),
        ((8, width), F32),
        ((width, width), BF16 if packed else F32),
        ((2 * share, half), F32),
    ]
    outs += [((share, half), BF16)] * (2 * parts - 2)
    scratch = half_scratch(share, length, half)
    if packed:
        scratch += [((width, width), BF16)]
    return kernel, outs, scratch


def make_last(packed, parts, rows, block, memory_block, width, narrow, n_pieces):
    share = rows * block

    def kernel(*refs):
        me_ref, refs = refs[0], list(refs[1:])
        pieces, refs = refs[:n_pieces], refs[n_pieces:]
        tokens, refs = refs[:rows], refs[rows:]
        in_part, query_sum, query_w_grad, memory_send = refs[:4]
        owns, refs = refs[4:6], refs[6:]
        received = [refs[: 2 * parts - 2], refs[2 * parts - 2 : 4 * parts - 4]]
        refs = refs[4 * parts - 4 :]
        in_own, in_send = refs[:2]
        n_grads = 2 if packed else 3
        grad_refs, scratch = refs[2 : 2 + n_grads], refs[2 + n_grads :]
        sums = scratch[0]
        me = me_ref[0]
        if packed:
            for i in range(2):
                unpack(me, pieces, 3 * narrow + 8, (1 + i) * narrow, narrow, scratch[1 + i], CROSSED)
            key_w, value_w = scratch[1:3]
        else:
            key_w, value_w = pieces
        grads = Grads(me, grad_refs, scratch[3] if packed else None, narrow)
        if packed:
            grads.put(2, query_w_grad[...].astype(F32))
        lows = []
        for own, others in zip(owns, received):
            found = own[...]
            for key, value in zip(others[::2], others[1::2]):
                found = found + jnp.concatenate([key[...], value[...]], axis=0).astype(F32)
            lows.append(found.astype(BF16))
        key_low = jnp.concatenate([low[:share, :] for low in lows], axis=1)
        value_low = jnp.concatenate([low[share:, :] for low in lows], axis=1)
        tokens_own = jnp.concatenate([t[:block, :] for t in tokens], axis=0)
        sums[...] = query_sum[...]
        sums[1:2, :] = total(value_low)
        grads.put_sums(3 * narrow, sums[...])
        grads.put(0, dot_tn(tokens_own, key_low))
        grads.put(1, dot_tn(tokens_own, value_low))
        grad = in_part[...] + dot_nt(key_low, key_w[...]) + dot_nt(value_low, value_w[...])
        in_own[...] = grad[:block, :]
        in_send[:block, :] = grad[block:, :].astype(BF16)
        in_send[block:, :] = memory_send[...]

    outs = [((block, width), F32), ((block + memory_block, width), BF16)]
    if packed:
        outs += [((16, 3 * narrow + 8, width), BF16)] * 2
    else:
        outs += [((width, width), F32)] * 2 + [((8, width), F32)]
    scratch = [((8, width), F32)]
    if packed:
        scratch += [((width, width), BF16)] * 2 + [((width, width), F32)]
    return kernel, outs, scratch


def combine(arrays, splits, micros=0.1):
    count = arrays[0].shape[0] // splits
    shape = (count,) + arrays[0].shape[1:]

    def kernel(*refs):
        given, outs = refs[: len(arrays)], refs[len(arrays) :]
        for i, out in enumerate(outs):
            here = slice(i * count, (i + 1) * count)
            found = given[0][here].astype(F32)
            for ref in given[1:]:
                found = found + ref[here].astype(F32)
            out[...] = found.astype(out.dtype)

    return pl.pallas_call(
        kernel,
        out_shape=[jax.ShapeDtypeStruct(shape, BF16)] * splits,
        in_specs=[VM] * len(arrays),
        out_specs=[VM] * splits,
        compiler_params=pltpu.CompilerParams(vmem_limit_bytes=snug(arrays)),
        cost_estimate=pl.CostEstimate(flops=int(micros * 1.15e9), bytes_accessed=0, transcendentals=0),
        name="combine",
    )(*arrays)


def combine_joint(groups, splits):
    count, sizes = groups[0][0].shape[0] // splits, [g[0].shape[1] for g in groups]
    shape = (count, sum(sizes)) + groups[0][0].shape[2:]
    flat = [a for group in groups for a in group]

    def kernel(*refs):
        outs, at, row = refs[len(flat) :], 0, 0
        for group, size in zip(groups, sizes):
            given = refs[at : at + len(group)]
            at += len(group)
            for i, out in enumerate(outs):
                here = slice(i * count, (i + 1) * count)
                found = given[0][here].astype(F32)
                for ref in given[1:]:
                    found = found + ref[here].astype(F32)
                out[:, row : row + size, :] = found.astype(BF16)
            row += size

    return pl.pallas_call(
        kernel,
        out_shape=[jax.ShapeDtypeStruct(shape, BF16)] * splits,
        in_specs=[VM] * len(flat),
        out_specs=[VM] * splits,
        compiler_params=pltpu.CompilerParams(vmem_limit_bytes=snug(flat)),
        cost_estimate=pl.CostEstimate(flops=1, bytes_accessed=1, transcendentals=0),
        name="combine_joint",
    )(*flat)


def chosen(me, rows, wide):
    width = rows.shape[1]
    line = lax.broadcasted_iota(jnp.int32, (width, wide), 0)
    here = lax.broadcasted_iota(jnp.int32, (width, wide), 1) + me * wide
    choice = jnp.where(line == here, 1.0, 0.0)
    return lax.dot_general(rows, choice, (((1,), (0,)), ((), ())), precision=lax.Precision.HIGHEST, preferred_element_type=F32)


def reduce_all(array, devices):
    mask = 1
    while mask < devices:
        array = array + swap(array, mask, devices)
        mask *= 2
    return array


def per_device(
    tokens, memory, target_ids, source_ids, cotangent,
    query_weight, key_weight, value_weight, output_weight, query_bias, value_bias, output_bias,
    attention_gain, attention_shift,
    source_query, source_key, source_value, source_output, source_query_bias, source_value_bias,
    source_output_bias, source_gain, source_shift,
    inner_weight, inner_bias, outer_weight, outer_bias, final_gain, final_shift,
    *, devices, sequence,
):
    packed = devices == 32
    rows, block, width = tokens.shape
    memory_block = memory.shape[1]
    parts = sequence // rows
    share, memory_share = rows * block, rows * memory_block
    hidden = inner_weight.shape[1]
    blocks = hidden // width
    me = lax.axis_index(AXES)
    me_array = me.reshape(1).astype(jnp.int32)
    turn = lax.rem(lax.div(me, parts), rows)
    narrow, wide = width // devices, hidden // devices

    def run(made, micros, name, *args, room=10):
        kernel, outs, *scratch = made
        return call(kernel, outs, (me_array,) + args, scratch[0] if scratch else [], micros, name, room)

    short = [query_bias, value_bias, output_bias, attention_gain, attention_shift, source_query_bias,
             source_value_bias, source_output_bias, source_gain, source_shift, outer_bias, final_gain,
             final_shift]

    def whole(array):
        return lax.all_gather(array, AXES, axis=0, tiled=True)

    sent, kept = tokens_packet(
        turn.reshape(1).astype(jnp.int32), tokens, memory, target_ids, source_ids, cotangent
    )
    came = swap(sent, parts, devices)
    row_tokens = [kept, came]
    kept_swaps = [swap(kept, m, devices) for m in range(1, parts)]
    came_swaps = [swap(came, m, devices) for m in range(1, parts)]
    for pair in zip(kept_swaps, came_swaps):
        row_tokens += pair
    own_tokens = row_tokens[:rows]

    if packed:
        first, rest = run(make_weights_packet(narrow, width, blocks), 1.0, "weights_packet",
                          query_weight, key_weight, value_weight, output_weight, source_query,
                          source_key, source_value, source_output, inner_weight, outer_weight,
                          inner_bias.reshape(1, wide), *[v.reshape(1, narrow) for v in short], room=58)
        first = after(first, sent)
        first = join([first, turned_swap(first, 0)])
        first_b = turned_swap(first, 1)
        rest = after(rest, first)
        rest_b = turned_swap(rest, 0)
        first = join(after([first, first_b], rest_b))
        rest = join(after([rest, rest_b], first_b, came, *kept_swaps))
        first_b, rest_b = turned_swap(first, 2, CROSSED), turned_swap(rest, 1)
        first_c = join([first, first_b])
        first_d = turned_swap(first_c, 3, CROSSED)
        second, third = run(make_part((5 * narrow + 16, 2 * blocks * narrow), width), 1.0, "part", rest, after(rest_b, first_b))
        second_b, third_b = turned_swap(second, 2), turned_swap(third, 2, CROSSED)
        second_c = join(after([second, second_b], first_d, third_b))
        third_c = join(after([third, third_b], first_d, second_b))
        second_d, third_d = turned_swap(second_c, 3), turned_swap(third_c, 3, CROSSED)
        first_d = after(first_d, second_c, third_c, *came_swaps)
        set_self = [first_c, first_d, swap(first_c, 1, 32), swap(first_d, 1, 32)]
    else:
        full = [whole(w) for w in (query_weight, key_weight, value_weight, output_weight, source_query, source_key, source_value, source_output)]
        lane = lax.broadcasted_iota(jnp.int32, (1, width), 1)
        place = lax.broadcasted_iota(jnp.int32, (blocks, width), 0) * width + lane
        spread_wide = jnp.where(place // wide == me, jnp.tile(inner_bias.reshape(1, wide), (blocks, width // wide)), 0)

        def natural(rows):
            return jnp.where(lane // narrow == me, jnp.tile(rows, (1, devices)), 0)

        vectors = jnp.concatenate([natural(jnp.stack(short[:2])), jnp.zeros((6, width), BF16), natural(jnp.stack(short[2:])), spread_wide, jnp.zeros((1, width), BF16)])
        vectors = reduce_all(vectors, devices).astype(F32)
        set_self = full[:3] + [vectors[:8]]
        set_cross = full[3:] + [vectors[8:]]
        set_inner = [
            whole(inner_weight).reshape(width, blocks, width).transpose(1, 0, 2),
            whole(outer_weight).reshape(blocks, width, width),
        ]
    found = run(
        make_project(packed, parts, rows, block, memory_block, width, narrow, len(set_self)), 5.0,
        "project", *set_self, *row_tokens,
    )
    query, query_t, keys, values, value_t = (found[2 * i : 2 * i + 2] for i in range(5))
    row_memory, ids, memory_ids = found[10:]
    query_t = list(query_t)
    if packed:
        set_query, set_last = set_self, set_self
    else:
        set_back, set_query, set_last, set_memory = [full[3], full[4], full[7]], full[:1], full[1:3], full[5:7]
    found = run(
        make_self_attention(share, parts * share, width), 12.0, "self_attention",
        *query_t, *keys, *value_t, ids,
    )
    mixtures, logs = found[:2], found[2:]
    if packed:
        second_d = after(second_d, mixtures[0])
        second_e = swap(after(second_c, mixtures[0]), 1, 32)
        set_cross = [second_c, second_d, second_e, swap(second_d, 1, 32)]
        set_back, set_memory = set_cross, set_cross
    first_sum, second_sum, cross_query, memory_keys, memory_values, cross_t, cross_logs, vectors = run(
        make_cross_forward(packed, rows, block, parts * memory_share, width, narrow, len(set_cross)),
        9.0, "cross_forward", *set_cross, *own_tokens, row_memory, ids, memory_ids, *mixtures,
    )
    if packed:
        third_d = after(third_d, second_sum)
        third_e = swap(after(third_c, mixtures[0]), 1, 32)
        set_inner = [third_c, third_d, third_e, swap(third_d, 1, 32)]
    out_own, out_send, back2_in, sums_inner, *grads_inner = run(
        make_inner(packed, rows, block, width, hidden, narrow, len(set_inner)), 18.0, "inner",
        *set_inner, second_sum, kept, came, vectors,
    )
    out_came = swap(out_send, parts, devices)
    found = run(
        make_cross_back(packed, parts, share, memory_share, width, narrow, len(set_back)), 14.0,
        "cross_back", *set_back, back2_in, first_sum, second_sum, cross_query, memory_keys,
        memory_values, cross_t, cross_logs, ids, memory_ids, vectors, sums_inner, *mixtures,
    )
    back1, memory_key_own, memory_value_own, sums_cross = found[:4]
    slope, slope_t, deltas = (found[4 + 2 * i : 6 + 2 * i] for i in range(3))
    memory_received = [swap(a, m + 1, devices) for m, a in enumerate(found[10 : 10 + parts - 1])]
    grads_early = found[10 + parts - 1 :]
    query = list(query)
    if packed:
        keep, send = combine(after([grads_inner[0], swap(grads_inner[1], 1, 32)], back1, out_came), 2)
        inner_step = [keep, turned_swap(send, 3)]
        query[0] = after(query[0], keep)
    found = run(
        make_self_back_upper(parts, share, width), 7.0, "self_back_upper", query[0], keys[0],
        values[0], slope[0], slope_t[0], logs[0], deltas[0], ids,
    )
    query_upper, own_upper = found[:2]
    received_upper = [swap(a, m // 2 + 1, devices) for m, a in enumerate(found[2:])]
    memory_own, memory_send, *grads_cross = run(
        make_memory_back(packed, parts, rows, block, memory_block, width, narrow, len(set_memory)),
        2.0, "memory_back", *set_memory, *own_tokens, after(memory_key_own, query_upper),
        memory_value_own, sums_cross, *grads_early, *memory_received,
    )
    if packed:
        cross_came = swap(grads_cross[1], 1, 32)
        keep, send = combine(after(inner_step, grads_cross[0]), 2, 8.0)
        inner_step = [keep, turned_swap(send, 2)]
        keep_cross, send = combine(after([grads_cross[0], cross_came], keep), 2)
        cross_step = [keep_cross, turned_swap(send, 3, CROSSED)]
        query[1] = after(query[1], keep, keep_cross)
    in_part, query_sum, query_w_grad, own_lower, *sends = run(
        make_self_back_lower(packed, parts, rows, block, width, narrow, len(set_query)), 11.0,
        "self_back_lower", *set_query, *own_tokens, query[1], keys[1], values[1], slope[1],
        slope_t[1], logs[1], deltas[1], ids, back1, query_upper,
    )
    received_lower = [swap(a, m // 2 + 1, devices) for m, a in enumerate(sends)]
    if packed:
        keep_cross, send = combine(after(cross_step, query_sum), 2)
        cross_step = [keep_cross, turned_swap(send, 2, CROSSED)]
        in_part = after(in_part, keep_cross, inner_step[1])
    in_own, in_send, *grads_last = run(
        make_last(packed, parts, rows, block, memory_block, width, narrow, len(set_last)), 6.0,
        "last", *set_last, *own_tokens, in_part, query_sum, query_w_grad, memory_send, own_upper,
        own_lower, *received_upper, *received_lower,
    )

    if packed:
        keep, send = combine([grads_last[0], swap(grads_last[1], 1, 32)], 2)
        last_step = [keep, turned_swap(send, 3)]
        in_send = after(in_send, last_step[1])
        keep_joint, send = combine_joint(after([inner_step, cross_step], keep), 2)
        joint_step = [keep_joint, turned_swap(send, 1)]
        keep, send = combine(after(last_step, keep_joint), 2)
        last_step = [keep, turned_swap(send, 2)]
        keep_joint, send = combine(after(joint_step, keep), 2)
        joint_step = [keep_joint, turned_swap(send, 0)]
        keep, send = combine(after(last_step, keep_joint), 2)
        last_step = [keep, turned_swap(send, 1)]
        keep, send = combine(last_step, 2)
        last_step = [keep, turned_swap(send, 0)]

        def plan(me_ref, *refs):
            me = me_ref[0]
            joint, last = (sum(r[0].astype(F32) for r in given) for given in (refs[:2], refs[2:4]))
            outs = refs[4:]
            inner, cross = joint[: 2 * blocks * narrow, :], joint[2 * blocks * narrow :, :]
            for i in range(blocks):
                outs[0][:, i * width : (i + 1) * width] = inner[i * narrow : (i + 1) * narrow, :]
            outs[1][...] = inner[blocks * narrow :, :]
            for i in range(5):
                outs[2 + i][...] = cross[i * narrow : (i + 1) * narrow, :]
            for i in range(3):
                outs[7 + i][...] = last[i * narrow : (i + 1) * narrow, :]
            rows_in = jnp.concatenate([cross[5 * narrow :, :], last[3 * narrow :, :]], axis=0)
            outs[10][...] = chosen(me, rows_in, narrow)
            per = width // wide
            line = lax.broadcasted_iota(jnp.int32, (blocks, width), 0)
            row = jnp.sum(jnp.where(line == lax.div(me, per), rows_in[3 : 3 + blocks, :], 0.0), axis=0, keepdims=True)
            outs[11][...] = chosen(lax.rem(me, per), row, wide)

        part = (narrow, width)
        shapes = [(narrow, hidden), (wide, width)] + [part] * 8 + [(24, narrow), (1, wide)]
        (inner_share, outer_share, source_key_share, source_value_share, source_output_share,
         source_query_share, output_share, key_share, value_share, query_share, sums,
         inner_bias_share) = call(
            plan, [(s, F32) for s in shapes], (me_array, *joint_step, *last_step), [], 2.0,
            "finish",
        )
        inner_bias_share = inner_bias_share.reshape(wide)
    else:
        def scatter(array):
            return lax.psum_scatter(array, AXES, scatter_dimension=0, tiled=True)

        inner_share = scatter(grads_inner[0].transpose(1, 0, 2).reshape(width, hidden))
        outer_share = scatter(grads_inner[1].reshape(hidden, width))
        source_output_share, source_query_share, output_share = (scatter(g.astype(F32)) for g in grads_early)
        source_key_share, source_value_share = (scatter(g) for g in grads_cross[:2])
        key_share, value_share = (scatter(g) for g in grads_last[:2])
        query_share = scatter(query_w_grad)
        sums = reduce_all(jnp.concatenate([grads_cross[2], grads_last[2]], axis=0), devices)
        inner_bias_share = lax.dynamic_slice(sums[3 : 3 + blocks].reshape(hidden), (me * wide,), (wide,))
        sums = lax.dynamic_slice(sums, (0, me * narrow), (sums.shape[0], narrow))
    def regroup(mine, came):
        came = came.astype(F32)
        return jnp.where(turn == 0, jnp.stack([mine, came]), jnp.stack([came, mine]))

    output = regroup(out_own, out_came)
    in_came = swap(in_send, parts, devices)
    input_gradient = regroup(in_own, in_came[:block])
    memory_gradient = regroup(memory_own, in_came[block:])

    return (
        output,
        input_gradient,
        memory_gradient,
        query_share,
        key_share,
        value_share,
        output_share,
        sums[16],
        sums[17],
        sums[13],
        sums[11],
        sums[12],
        source_query_share,
        source_key_share,
        source_value_share,
        source_output_share,
        sums[10],
        sums[14],
        sums[9],
        sums[7],
        sums[8],
        inner_share,
        inner_bias_share,
        outer_share,
        sums[2],
        sums[0],
        sums[1],
    )


def solution(mesh):
    sequence, devices = mesh.shape["seq"], mesh.size
    tokens, ids = P("dp", "seq", None), P("dp", "seq")
    matrix, vector = P(AXES, None), P(AXES)
    attention = (matrix,) * 4 + (vector,) * 5
    inner = (matrix, vector, matrix, vector, vector, vector)
    return jax.shard_map(
        functools.partial(per_device, devices=devices, sequence=sequence),
        mesh=mesh,
        in_specs=(tokens, tokens, ids, ids, tokens) + attention + attention + inner,
        out_specs=(tokens, tokens, tokens) + attention + attention + inner,
        check_vma=False,
    )
```

```python
import functools
import math

import jax
import jax.numpy as jnp
from jax import lax
from jax.experimental import pallas as pl
from jax.experimental.pallas import tpu as pltpu
from jax.sharding import PartitionSpec as P

HEADS = 8
HEAD_DIM = 64
PAIR = 128
EPSILON = 1e-05
MASKED = 1e9
AXES = ("dp", "seq")
F32 = jnp.float32
BF16 = jnp.bfloat16

(
    OUTPUT_BIAS,
    ATTENTION_GAIN,
    ATTENTION_SHIFT,
    SOURCE_QUERY_BIAS,
    SOURCE_VALUE_BIAS,
    SOURCE_OUTPUT_BIAS,
    SOURCE_GAIN,
    SOURCE_SHIFT,
    OUTER_BIAS,
    FINAL_GAIN,
    FINAL_SHIFT,
    INNER_BIAS,
) = range(12)
Z_MASKS = (0, 8, 16, 24)
VM = pl.BlockSpec(memory_space=pltpu.VMEM)
SM = pl.BlockSpec(memory_space=pltpu.SMEM)


def dot(a, b):
    return lax.dot_general(a, b, (((1,), (0,)), ((), ())), preferred_element_type=F32)


def dot_nt(a, b):
    return lax.dot_general(a, b, (((1,), (1,)), ((), ())), preferred_element_type=F32)


def dot_tn(a, b):
    return lax.dot_general(a, b, (((0,), (0,)), ((), ())), preferred_element_type=F32)


def total(values):
    return jnp.sum(values.astype(F32), axis=0, keepdims=True)


def normalize(h):
    average = jnp.mean(h, axis=-1, keepdims=True)
    centered = h - average
    variance = jnp.mean(centered * centered, axis=-1, keepdims=True)
    inverse = lax.rsqrt(variance + EPSILON)
    return centered * inverse, inverse


def normalize_back(upstream, normed, inverse, gain):
    scaled = upstream * gain
    first_mean = jnp.mean(scaled, axis=-1, keepdims=True)
    second_mean = jnp.mean(scaled * normed, axis=-1, keepdims=True)
    return inverse * (scaled - first_mean - normed * second_mean)


def normal_parts(v):
    density = 0.3989422804014327 * jnp.exp(-0.5 * v * v)
    t = 1.0 / (1.0 + 0.2316419 * jnp.abs(v))
    series = t * (
        0.319381530
        + t * (-0.356563782 + t * (1.781477937 + t * (-1.821255978 + t * 1.330274429)))
    )
    tail = density * series
    return jnp.where(v >= 0.0, 1.0 - tail, tail), density


def penalties(ids):
    place = lax.broadcasted_iota(jnp.int32, (PAIR, ids.shape[1]), 0)
    return jnp.where((place == ids) | (place >= 4), 0.0, -MASKED).astype(BF16)


def one_hot(ids):
    place = lax.broadcasted_iota(jnp.int32, (PAIR, ids.shape[1]), 0)
    return jnp.where(place == ids, 1.0, 0.0).astype(F32).T.astype(BF16)


def spread(part, half):
    empty = jnp.zeros_like(part)
    return [part, empty] if half == 0 else [empty, part]


def attend(query_t, keys, value_t, hot, penalty, mixture_t, logs):
    length = keys.shape[0]

    def pair(p, carry):
        columns = pl.ds(pl.multiple_of(p * PAIR, PAIR), PAIR)
        left = jnp.concatenate([keys[:, columns], hot[...]], axis=1)
        for half in range(2):
            rows = pl.ds(pl.multiple_of(p * PAIR + half * HEAD_DIM, HEAD_DIM), HEAD_DIM)
            right = jnp.concatenate(spread(query_t[rows, :], half) + [penalty[...]], axis=0)
            scores = dot(left, right)
            highest = jnp.max(scores, axis=0, keepdims=True)
            weights = jnp.exp(scores - highest).astype(BF16)
            values = jnp.concatenate(
                [value_t[rows, :], jnp.ones((16, length), BF16)], axis=0
            )
            found = dot(values, weights)
            denominator = found[HEAD_DIM : HEAD_DIM + 1, :]
            mixture_t[rows, :] = (found[:HEAD_DIM, :] / denominator).astype(BF16)
            logs[2 * p + half] = highest + jnp.log(denominator)
        return carry

    lax.fori_loop(0, keys.shape[1] // PAIR, pair, 0)


def attend_back(
    query_t, query, keys, key_t, values, slope_t, slope, hot, penalty, logs, deltas,
    query_grad_t, key_grad, value_grad,
):
    tokens = query.shape[0]
    lane = lax.broadcasted_iota(jnp.int32, (tokens, PAIR), 1)

    def pair(p, carry):
        columns = pl.ds(pl.multiple_of(p * PAIR, PAIR), PAIR)
        left = jnp.concatenate([keys[:, columns], hot[...]], axis=1)
        value_pair = values[:, columns]
        key_sum, value_sum = None, None
        for half in range(2):
            rows = pl.ds(pl.multiple_of(p * PAIR + half * HEAD_DIM, HEAD_DIM), HEAD_DIM)
            right = jnp.concatenate(spread(query_t[rows, :], half) + [penalty[...]], axis=0)
            chances = jnp.exp(dot(left, right) - logs[2 * p + half])
            slopes = dot(value_pair, jnp.concatenate(spread(slope_t[rows, :], half), axis=0))
            grads = (chances * (slopes - deltas[2 * p + half])).astype(BF16)
            query_grad_t[rows, :] = dot(key_t[rows, :], grads) * HEAD_DIM**-0.5
            mine = (lane < HEAD_DIM) if half == 0 else (lane >= HEAD_DIM)
            none = jnp.zeros((tokens, PAIR), BF16)
            value_part = dot(chances.astype(BF16), jnp.where(mine, slope[:, columns], none))
            key_part = dot(grads, jnp.where(mine, query[:, columns], none))
            value_sum = value_part if value_sum is None else value_sum + value_part
            key_sum = key_part if key_sum is None else key_sum + key_part
        key_grad[:, columns] = key_sum
        value_grad[:, columns] = value_sum
        return carry

    lax.fori_loop(0, keys.shape[1] // PAIR, pair, 0)


def deltas_of(slope_t, mixture_t, deltas):
    for head in range(slope_t.shape[0] // HEAD_DIM):
        rows = slice(head * HEAD_DIM, (head + 1) * HEAD_DIM)
        deltas[head] = jnp.sum(
            slope_t[rows, :].astype(F32) * mixture_t[rows, :].astype(F32), axis=0, keepdims=True
        )


def swap(array, mask, devices):
    return lax.ppermute(array, AXES, [(i, i ^ mask) for i in range(devices)])


PLANE = (0, 2, 4, 6)
TURNS = ((8, 24), (24, 8))


def exchanged(array):
    return [array] + [swap(array, mask, 32) for mask in PLANE[1:]]


def handed(arrays):
    return [arrays[0]] + [swap(array, mask, 32) for array, mask in zip(arrays[1:], PLANE[1:])]


def turned_swap(array, step):
    return lax.ppermute(array, AXES, [(i, i ^ TURNS[i % 2][step]) for i in range(32)])


def after(value, *others):
    return lax.optimization_barrier((value, others))[0]


def places(me):
    found = []
    for core in range(2):
        even = ((me & 1) ^ core) == 0
        lines = (0, jnp.where(even, 8, 24), jnp.where(even, 24, 8), 16)
        for i, plane in enumerate(PLANE):
            for j, line in enumerate(lines):
                device = me ^ (core | plane) if core | plane else me
                found.append((core, i, j, device ^ line if j else device))
    return found


def unpack(me, pieces, stride, first, rows, scratch):
    for core, plane, line, device in places(me):
        at = line * stride + first
        found = pieces[4 * core + plane][at : at + rows, :]
        scratch[pl.ds(pl.multiple_of(device * rows, rows), rows), :] = found


def vector_sum(pieces, stride, first):
    found = None
    for ref in pieces:
        for line in range(4):
            part = ref[line * stride + first : (line + 1) * stride, :].astype(F32)
            found = part if found is None else found + part
    return found


class Grads:
    def __init__(self, me, refs, dense, rows):
        self.me, self.refs, self.dense, self.rows = me, refs, dense, rows

    def put(self, index, grad):
        if self.dense is None:
            self.refs[index][...] = grad
            return
        self.dense[...] = grad
        rows = self.rows
        for core, plane, line, device in places(self.me):
            found = self.dense[pl.ds(pl.multiple_of(device * rows, rows), rows), :]
            self.refs[core][plane * 4 + line, index * rows : (index + 1) * rows, :] = found.astype(BF16)

    def put_sums(self, first, sums):
        if self.dense is None:
            self.refs[-1][...] = sums
            return
        low = sums.astype(BF16)
        for ref in self.refs:
            for slot in range(16):
                ref[slot, first : first + sums.shape[0], :] = low


def grad_outs(packed, count, rows, width, sums):
    if packed:
        return [((16, count * rows + sums, width), BF16)] * 2
    return [((width, width), F32)] * count + [((sums, width), F32)]


COSTS = {}


def padded(shape, dtype):
    last = -(-shape[-1] // 128) * 128
    tall = -(-shape[-2] // 16) * 16 if len(shape) > 1 else 16
    return math.prod(shape[:-2]) * tall * last * jnp.dtype(dtype).itemsize


def snug(arrays):
    return 2 * sum(padded(a.shape, a.dtype) for a in arrays) + (3 << 20)


def call(kernel, outs, args, scratch, micros, name, room=10):
    moved = sum(math.prod(a.shape) * a.dtype.itemsize for a in args[1:])
    moved += sum(math.prod(s) * jnp.dtype(d).itemsize for s, d in outs)
    need = sum(padded(a.shape, a.dtype) for a in args[1:])
    need += sum(padded(s, d) for s, d in list(outs) + list(scratch))
    return pl.pallas_call(
        kernel,
        out_shape=[jax.ShapeDtypeStruct(s, d) for s, d in outs],
        in_specs=[SM] + [VM] * (len(args) - 1),
        out_specs=[VM] * len(outs),
        scratch_shapes=[pltpu.VMEM(s, d) for s, d in scratch],
        compiler_params=pltpu.CompilerParams(vmem_limit_bytes=min(need + (room << 20), 58 << 20)),
        cost_estimate=pl.CostEstimate(
            flops=int(COSTS.get(name, 0) * 1.15e9) + 1, bytes_accessed=1, transcendentals=0
        ),
        name=name,
    )(*args)


def tokens_packet(turn, tokens, memory, target_ids, source_ids, cotangent):
    block, width = tokens.shape[1:]
    memory_block = memory.shape[1]
    first = block + memory_block + 8

    def kernel(turn_ref, targets, sources, tokens_ref, memory_ref, cot_ref, sent, kept):
        mine = turn_ref[0]
        for row, out in ((1 - mine, sent), (mine, kept)):
            out[:block, :] = tokens_ref[row]
            out[block : block + memory_block, :] = memory_ref[row]
            ids = targets[pl.ds(row, 1), :].astype(F32)
            ids = jnp.concatenate([ids, jnp.zeros((1, width - block), F32)], axis=1)
            others = sources[pl.ds(row, 1), :].astype(F32)
            others = jnp.concatenate([others, jnp.zeros((1, width - memory_block), F32)], axis=1)
            place = lax.broadcasted_iota(jnp.int32, (8, width), 0)
            found = jnp.where(place == 0, ids, jnp.where(place == 1, others, 0.0))
            out[block + memory_block : first, :] = found.astype(BF16)
            out[first:, :] = cot_ref[row]

    shape = (first + block, width)
    return call(kernel, [(shape, BF16)] * 2, (turn, target_ids, source_ids, tokens, memory, cotangent),
                [], 1.0, "tokens_packet", 58)


def placed(me, parts, width):
    here = lax.broadcasted_iota(jnp.int32, (parts.shape[1], width), 0) + me * parts.shape[1]
    lane = lax.broadcasted_iota(jnp.int32, (parts.shape[1], width), 1)
    return dot(parts, jnp.where(lane == here, 1.0, 0.0).astype(BF16))


def make_weights_packet(narrow, width, blocks):
    tall = blocks * narrow

    def kernel(me_ref, *refs):
        weights, inner, outer, wide, short = refs[:8], refs[8], refs[9], refs[10], refs[11:24]
        first, rest = refs[24:]
        me, middle = me_ref[0], 5 * narrow + 16
        for i, ref in enumerate(weights):
            if i < 3:
                first[i * narrow : (i + 1) * narrow, :] = ref[...]
            else:
                rest[(i - 3) * narrow : (i - 2) * narrow, :] = ref[...]
        short = jnp.concatenate([ref[...].astype(F32) for ref in short], axis=0).astype(BF16)
        found = placed(me, short, width)
        first[3 * narrow :, :] = jnp.concatenate([found[:2, :], jnp.zeros((6, width), F32)], axis=0).astype(BF16)
        per = width // wide.shape[1]
        row = placed(lax.rem(me, per), wide[...], width)
        place = lax.broadcasted_iota(jnp.int32, (blocks, width), 0)
        spread_row = jnp.where(place == lax.div(me, per), row, 0.0)
        none = jnp.zeros((16 - (found.shape[0] - 2) - blocks, width), F32)
        rest[5 * narrow : middle, :] = jnp.concatenate([found[2:, :], spread_row, none], axis=0).astype(BF16)
        for i in range(blocks):
            rest[middle + i * narrow : middle + (i + 1) * narrow, :] = inner[:, i * width : (i + 1) * width]
        rest[middle + tall :, :] = outer[...]

    return kernel, [((rows, width), BF16) for rows in (3 * narrow + 8, 5 * narrow + 16 + 2 * tall)]


def make_part(sizes, width):
    tall = sum(sizes)

    def kernel(me_ref, upper, lower, *outs):
        for i in range(4):
            ref, at = (upper, lower)[i // 2], i % 2 * tall
            for size, out in zip(sizes, outs):
                out[i * size : (i + 1) * size, :] = ref[at : at + size, :]
                at += size

    return kernel, [((4 * size, width), BF16) for size in sizes]


def join(arrays):
    def kernel(*refs):
        at = 0
        for ref in refs[:-1]:
            refs[-1][at : at + ref.shape[0], :] = ref[...]
            at += ref.shape[0]

    rows = sum(a.shape[0] for a in arrays)
    return pl.pallas_call(
        kernel,
        out_shape=jax.ShapeDtypeStruct((rows, arrays[0].shape[1]), arrays[0].dtype),
        in_specs=[VM] * len(arrays),
        out_specs=VM,
        compiler_params=pltpu.CompilerParams(vmem_limit_bytes=snug(arrays)),
        cost_estimate=pl.CostEstimate(flops=1 << 20, bytes_accessed=0, transcendentals=0),
        name="join",
    )(*arrays)


def make_project(packed, parts, rows, block, memory_block, width, narrow, n_pieces):
    share = rows * block
    length = parts * share
    memory_share = rows * memory_block
    stride = 3 * narrow + 8
    half = width // 2

    def kernel(*refs):
        me_ref, refs = refs[0], list(refs[1:])
        pieces, refs = refs[:n_pieces], refs[n_pieces:]
        tokens, refs = refs[: parts * rows], refs[parts * rows :]
        query, query_t, keys, values, value_t = (refs[2 * i : 2 * i + 2] for i in range(5))
        memory, ids, memory_ids = refs[10:13]
        scratch = refs[13:]
        me = me_ref[0]
        if packed:
            for i in range(3):
                unpack(me, pieces, stride, i * narrow, narrow, scratch[i])
            query_w, key_w, value_w = scratch
            biases = vector_sum(pieces, stride, 3 * narrow)
        else:
            query_w, key_w, value_w = pieces[:3]
            biases = pieces[3][...]
        for i in range(parts):
            here = slice(i * share, (i + 1) * share)
            some = tokens[i * rows : (i + 1) * rows]
            own = jnp.concatenate([t[:block, :] for t in some], axis=0)
            if i == 0:
                scaled = (dot(own, query_w[...]) + biases[0:1, :]).astype(BF16) * BF16(HEAD_DIM**-0.5)
            key = dot(own, key_w[...]).astype(BF16)
            found = (dot(own, value_w[...]) + biases[1:2, :]).astype(BF16)
            for side in range(2):
                columns = slice(side * half, (side + 1) * half)
                if i == 0:
                    query[side][...] = scaled[:, columns]
                    query_t[side][...] = scaled[:, columns].T
                keys[side][here, :] = key[:, columns]
                values[side][here, :] = found[:, columns]
                value_t[side][:, here] = found[:, columns].T
        for i, t in enumerate(tokens):
            memory[i * memory_block : (i + 1) * memory_block, :] = t[block : block + memory_block, :]
            found = t[block + memory_block : block + memory_block + 8, :].astype(F32).astype(jnp.int32)
            ids[:, i * block : (i + 1) * block] = found[0:1, :block]
        found = [t[block + memory_block : block + memory_block + 8, :].astype(F32).astype(jnp.int32)[1:2, :memory_block] for t in tokens]
        memory_ids[...] = jnp.concatenate(found, axis=1)

    outs = [((share, half), BF16)] * 2 + [((half, share), BF16)] * 2
    outs += [((length, half), BF16)] * 4 + [((half, length), BF16)] * 2
    outs += [
        ((parts * memory_share, width), BF16),
        ((1, length), jnp.int32),
        ((1, parts * memory_share), jnp.int32),
    ]
    return kernel, outs, [((width, width), BF16)] * 3 if packed else []


def make_self_attention(share, length, width):
    def kernel(me_ref, *refs):
        query_t, keys, value_t, ids = refs[:2], refs[2:4], refs[4:6], refs[6]
        mixture_t, logs, hot, penalty = refs[7:9], refs[9:11], refs[11], refs[12]
        hot[...] = one_hot(ids[...])
        penalty[...] = penalties(ids[:, :share])
        for side in range(2):
            attend(query_t[side], keys[side], value_t[side], hot, penalty, mixture_t[side], logs[side])

    outs = [((width // 2, share), BF16)] * 2 + [((HEADS // 2, 1, share), F32)] * 2
    return kernel, outs, [((length, PAIR), BF16), ((PAIR, share), BF16)]


def make_cross_forward(packed, rows, block, memory_length, width, narrow, n_pieces):
    share = rows * block
    stride = 5 * narrow + 16

    def kernel(*refs):
        me_ref, refs = refs[0], list(refs[1:])
        pieces, refs = refs[:n_pieces], refs[n_pieces:]
        tokens, refs = refs[:rows], refs[rows:]
        memory, ids, memory_ids, upper, lower = refs[:5]
        first_sum, second_sum, query, memory_keys, memory_values, cross_t, logs, vectors = refs[5:13]
        scratch = refs[13:]
        query_t, value_t, hot, penalty = scratch[:4]
        if packed:
            for i in range(5):
                unpack(me_ref[0], pieces, stride, i * narrow, narrow, scratch[4 + i])
            output_w, query_w, key_w, value_w, source_w = scratch[4:]
            vectors[...] = vector_sum(pieces, stride, 5 * narrow)
        else:
            output_w, query_w, key_w, value_w, source_w = pieces[:5]
            vectors[...] = pieces[5][...]

        def vector(i):
            return vectors[i : i + 1, :]

        own = jnp.concatenate([t[:block, :] for t in tokens], axis=0)
        mixture_t = jnp.concatenate([upper[...], lower[...]], axis=0)
        h = own.astype(F32) + dot_tn(mixture_t, output_w[...]) + vector(OUTPUT_BIAS)
        first_sum[...] = h
        first = normalize(h)[0] * vector(ATTENTION_GAIN) + vector(ATTENTION_SHIFT)
        scaled = (dot(first.astype(BF16), query_w[...]) + vector(SOURCE_QUERY_BIAS)).astype(BF16) * BF16(HEAD_DIM**-0.5)
        query[...] = scaled
        query_t[...] = scaled.T
        memory_keys[...] = dot(memory[...], key_w[...]).astype(BF16)
        memory_values[...] = (dot(memory[...], value_w[...]) + vector(SOURCE_VALUE_BIAS)).astype(BF16)
        value_t[...] = memory_values[...].T
        hot[...] = one_hot(memory_ids[...])
        penalty[...] = penalties(ids[:, :share])
        attend(query_t, memory_keys, value_t, hot, penalty, cross_t, logs)
        first = normalize(first_sum[...])[0] * vector(ATTENTION_GAIN) + vector(ATTENTION_SHIFT)
        second_sum[...] = first + dot_tn(cross_t[...], source_w[...]) + vector(SOURCE_OUTPUT_BIAS)

    outs = [
        ((share, width), F32),
        ((share, width), F32),
        ((share, width), BF16),
        ((memory_length, width), BF16),
        ((memory_length, width), BF16),
        ((width, share), BF16),
        ((HEADS, 1, share), F32),
        ((16, width), F32),
    ]
    scratch = [((width, share), BF16), ((width, memory_length), BF16), ((memory_length, PAIR), BF16), ((PAIR, share), BF16)]
    if packed:
        scratch += [((width, width), BF16)] * 5
    return kernel, outs, scratch


def make_inner(packed, rows, block, width, hidden, narrow, n_pieces):
    blocks = hidden // width
    share = rows * block
    per = width // (blocks * narrow)

    def kernel(*refs):
        me_ref, refs = refs[0], list(refs[1:])
        pieces, refs = refs[:n_pieces], refs[n_pieces:]
        second_sum, cot_own, cot_came, vectors = refs[:4]
        out_own, out_send, back, sums = refs[4:8]
        grads, scratch = refs[8:10], refs[10:]
        low, active, gate, slope = scratch[:4]
        if packed:
            inner_w, outer_w, gathered, dense = scratch[4:8]
            tall = blocks * narrow
            for core, plane, line, device in places(me_ref[0]):
                ref, at = pieces[4 * core + plane], line * 2 * tall
                row = pl.multiple_of(device * narrow, narrow)
                for i in range(blocks):
                    inner_w[i, pl.ds(row, narrow), :] = ref[at + i * narrow : at + (i + 1) * narrow, :]
                row = pl.multiple_of(lax.rem(device, per) * tall, tall)
                outer_w[lax.div(device, per), pl.ds(row, tall), :] = ref[at + tall : at + 2 * tall, :]
        else:
            inner_w, outer_w = pieces

        def vector(i):
            return vectors[i : i + 1, :]

        second = normalize(second_sum[...])[0] * vector(SOURCE_GAIN) + vector(SOURCE_SHIFT)
        low[...] = second.astype(BF16)
        back[...] = second + vector(OUTER_BIAS)

        def forward(i, carry):
            inner = dot(low[...], inner_w[i]) + vectors[pl.ds(INNER_BIAS + i, 1), :]
            chance, density = normal_parts(inner)
            found = (inner * chance).astype(BF16)
            active[i] = found
            gate[i] = chance + inner * density
            back[...] += dot(found, outer_w[i])
            return carry

        lax.fori_loop(0, blocks, forward, 0)
        normed, inverse = normalize(back[...])
        final = normed * vector(FINAL_GAIN) + vector(FINAL_SHIFT)
        out_own[...] = final[:block, :]
        out_send[...] = final[block:, :].astype(BF16)
        upstream = jnp.concatenate([cot_own[-block:, :], cot_came[-block:, :]], axis=0).astype(F32)
        sums[0:1, :] = total(upstream * normed)
        sums[1:2, :] = total(upstream)
        back3 = normalize_back(upstream, normed, inverse, vector(FINAL_GAIN))
        slope[...] = back3.astype(BF16)
        sums[2:3, :] = total(slope[...])
        sums[7:8, :] = jnp.zeros_like(sums[7:8, :])
        back[...] = back3

        def backward(i, carry):
            grad = dot_nt(slope[...], outer_w[i]) * gate[i]
            inner_low = grad.astype(BF16)
            sums[pl.ds(3 + i, 1), :] = total(inner_low)
            outer_grad = dot_tn(active[i], slope[...])
            inner_grad = dot_tn(low[...], inner_low)
            back[...] += dot_nt(inner_low, inner_w[i])
            if packed:
                dense[...] = inner_grad
                gathered[i] = outer_grad.astype(BF16)
                here = pl.ds(pl.multiple_of(i * narrow, narrow), narrow)
                for core, plane, line, device in places(me_ref[0]):
                    row = pl.multiple_of(device * narrow, narrow)
                    grads[core][plane * 4 + line, here, :] = dense[pl.ds(row, narrow), :].astype(BF16)
            else:
                grads[0][i] = inner_grad
                grads[1][i] = outer_grad
            return carry

        lax.fori_loop(0, blocks, backward, 0)
        if packed:
            tall = blocks * narrow
            for core, plane, line, device in places(me_ref[0]):
                row = pl.multiple_of(lax.rem(device, per) * tall, tall)
                grads[core][plane * 4 + line, tall:, :] = gathered[lax.div(device, per), pl.ds(row, tall), :]

    outs = [((block, width), F32), ((block, width), BF16), ((share, width), F32), ((8, width), F32)]
    if packed:
        outs += [((16, 2 * blocks * narrow, width), BF16)] * 2
    else:
        outs += [((blocks, width, width), F32)] * 2
    scratch = [((share, width), BF16), ((blocks, share, width), BF16), ((blocks, share, width), F32), ((share, width), BF16)]
    if packed:
        scratch += [((blocks, width, width), BF16)] * 3 + [((width, width), F32)]
    return kernel, outs, scratch


def make_cross_back(packed, parts, share, memory_share, width, narrow, n_pieces):
    memory_length = parts * memory_share
    stride = 5 * narrow + 16

    def kernel(*refs):
        me_ref, refs = refs[0], list(refs[1:])
        pieces, refs = refs[:n_pieces], refs[n_pieces:]
        (back2_in, first_sum, second_sum, query, memory_keys, memory_values, cross_t, logs, ids,
         memory_ids, vectors, sums_inner) = refs[:12]
        mixtures, refs = refs[12:14], refs[14:]
        back1, key_own, value_own, sums = refs[:4]
        self_slope, self_slope_t, self_deltas = (refs[4 + 2 * i : 6 + 2 * i] for i in range(3))
        sends, refs = refs[10 : 10 + parts - 1], refs[10 + parts - 1 :]
        grads, scratch = refs[:3], refs[3:]
        (slope_t, slope, key_t, hot, penalty, query_t, deltas, query_grad_t, key_grad, value_grad) = scratch[:10]
        upper, lower = mixtures
        if packed:
            for i, at in enumerate((0, 1, 4)):
                unpack(me_ref[0], pieces, stride, at * narrow, narrow, scratch[10 + i])
            output_w, query_w, source_w = scratch[10:13]
        else:
            output_w, query_w, source_w = pieces

        def vector(i):
            return vectors[i : i + 1, :]

        sums[0:7, :] = sums_inner[0:7, :]
        upstream = back2_in[...]
        normed, inverse = normalize(second_sum[...])
        sums[7:8, :] = total(upstream * normed)
        sums[8:9, :] = total(upstream)
        back2 = normalize_back(upstream, normed, inverse, vector(SOURCE_GAIN))
        back1[...] = back2
        cross_low = back2.astype(BF16)
        sums[9:10, :] = total(cross_low)
        grads[0][...] = dot(cross_t[...], cross_low).astype(BF16)
        found = dot_nt(cross_low, source_w[...]).astype(BF16)
        slope[...] = found
        slope_t[...] = found.T
        deltas_of(slope_t, cross_t, deltas)
        query_t[...] = query[...].T
        key_t[...] = memory_keys[...].T
        hot[...] = one_hot(memory_ids[...])
        penalty[...] = penalties(ids[:, :share])
        attend_back(query_t, query, memory_keys, key_t, memory_values, slope_t, slope, hot, penalty,
                    logs, deltas, query_grad_t, key_grad, value_grad)
        key_own[...] = key_grad[:memory_share, :]
        value_own[...] = value_grad[:memory_share, :]
        for i in range(1, parts):
            here = slice(i * memory_share, (i + 1) * memory_share)
            sends[i - 1][:memory_share, :] = key_grad[here, :].astype(BF16)
            sends[i - 1][memory_share:, :] = value_grad[here, :].astype(BF16)
        query_low = query_grad_t[...].T.astype(BF16)
        sums[10:11, :] = total(query_low)
        normed, inverse = normalize(first_sum[...])
        first_low = (normed * vector(ATTENTION_GAIN) + vector(ATTENTION_SHIFT)).astype(BF16)
        grads[1][...] = dot_tn(first_low, query_low).astype(BF16)
        upstream = back1[...] + dot_nt(query_low, query_w[...])
        sums[11:12, :] = total(upstream * normed)
        sums[12:13, :] = total(upstream)
        grad = normalize_back(upstream, normed, inverse, vector(ATTENTION_GAIN))
        back1[...] = grad
        branch_low = grad.astype(BF16)
        sums[13:14, :] = total(branch_low)
        sums[14:16, :] = jnp.zeros_like(sums[14:16, :])
        mixture_t = jnp.concatenate([upper[...], lower[...]], axis=0)
        grads[2][...] = dot(mixture_t, branch_low).astype(BF16)
        found = dot_nt(branch_low, output_w[...]).astype(BF16)
        for side in range(2):
            columns = slice(side * width // 2, (side + 1) * width // 2)
            self_slope[side][...] = found[:, columns]
            self_slope_t[side][...] = found[:, columns].T
            deltas_of(self_slope_t[side], mixtures[side], self_deltas[side])

    half = width // 2
    outs = [
        ((share, width), F32),
        ((memory_share, width), F32),
        ((memory_share, width), F32),
        ((16, width), F32),
    ]
    outs += [((share, half), BF16)] * 2 + [((half, share), BF16)] * 2
    outs += [((HEADS // 2, 1, share), F32)] * 2
    outs += [((2 * memory_share, width), BF16)] * (parts - 1)
    outs += [((width, width), BF16)] * 3
    scratch = [
        ((width, share), BF16),
        ((share, width), BF16),
        ((width, memory_length), BF16),
        ((memory_length, PAIR), BF16),
        ((PAIR, share), BF16),
        ((width, share), BF16),
        ((HEADS, 1, share), F32),
        ((width, share), F32),
        ((memory_length, width), F32),
        ((memory_length, width), F32),
    ]
    if packed:
        scratch += [((width, width), BF16)] * 3
    return kernel, outs, scratch


def attention_back_half(refs, share, scratch):
    query, keys, values, slope, slope_t, logs, deltas, ids = refs
    query_t, key_t, hot, penalty, query_grad_t, key_grad, value_grad = scratch
    query_t[...] = query[...].T
    key_t[...] = keys[...].T
    hot[...] = one_hot(ids[...])
    penalty[...] = penalties(ids[:, :share])
    attend_back(query_t, query, keys, key_t, values, slope_t, slope, hot, penalty, logs, deltas,
                query_grad_t, key_grad, value_grad)


def half_scratch(share, length, half):
    return [
        ((half, share), BF16),
        ((half, length), BF16),
        ((length, PAIR), BF16),
        ((PAIR, share), BF16),
        ((half, share), F32),
        ((length, half), F32),
        ((length, half), F32),
    ]


def give_half(share, scratch, own, sends):
    key_grad, value_grad = scratch[5:7]
    own[:share, :] = key_grad[:share, :]
    own[share:, :] = value_grad[:share, :]
    for i, send in enumerate(sends):
        here = slice((i // 2 + 1) * share, (i // 2 + 2) * share)
        send[...] = (key_grad, value_grad)[i % 2][here, :].astype(BF16)


def make_memory_back(packed, parts, rows, block, memory_block, width, narrow, n_pieces):
    memory_share = rows * memory_block

    def kernel(*refs):
        me_ref, refs = refs[0], list(refs[1:])
        pieces, refs = refs[:n_pieces], refs[n_pieces:]
        tokens, refs = refs[:rows], refs[rows:]
        memory_key_own, memory_value_own, sums_in = refs[:3]
        early, refs = refs[3:6], refs[6:]
        memory_received, refs = refs[: parts - 1], refs[parts - 1 :]
        memory_own, memory_send = refs[:2]
        n_grads = 2 if packed else 3
        grad_refs, scratch = refs[2 : 2 + n_grads], refs[2 + n_grads :]
        sums = scratch[0]
        me = me_ref[0]
        if packed:
            for i in range(2):
                unpack(me, pieces, 5 * narrow + 16, (2 + i) * narrow, narrow, scratch[1 + i])
            source_key, source_value = scratch[1:3]
        else:
            source_key, source_value = pieces
        grads = Grads(me, grad_refs, scratch[3] if packed else None, narrow)
        memory = jnp.concatenate([t[block : block + memory_block, :] for t in tokens], axis=0)
        key_sum, value_sum = memory_key_own[...], memory_value_own[...]
        for ref in memory_received:
            key_sum = key_sum + ref[:memory_share, :].astype(F32)
            value_sum = value_sum + ref[memory_share:, :].astype(F32)
        key_low, value_low = key_sum.astype(BF16), value_sum.astype(BF16)
        sums[...] = sums_in[...]
        sums[14:15, :] = total(value_low)
        grads.put_sums(5 * narrow, sums[...])
        grads.put(0, dot_tn(memory, key_low))
        grads.put(1, dot_tn(memory, value_low))
        if packed:
            for i, ref in enumerate(early):
                grads.put(2 + i, ref[...].astype(F32))
        grad = dot_nt(key_low, source_key[...]) + dot_nt(value_low, source_value[...])
        memory_own[...] = grad[:memory_block, :]
        memory_send[...] = grad[memory_block:, :].astype(BF16)

    outs = [((memory_block, width), F32), ((memory_block, width), BF16)]
    if packed:
        outs += [((16, 5 * narrow + 16, width), BF16)] * 2
    else:
        outs += [((width, width), F32)] * 2 + [((16, width), F32)]
    scratch = [((16, width), F32)]
    if packed:
        scratch += [((width, width), BF16)] * 2 + [((width, width), F32)]
    return kernel, outs, scratch


def make_self_back_upper(parts, share, width):
    length, half = parts * share, width // 2

    def kernel(*refs):
        operands, (query_grad, own), refs = refs[1:9], refs[9:11], refs[11:]
        sends, scratch = refs[: 2 * parts - 2], refs[2 * parts - 2 :]
        attention_back_half(operands, share, scratch)
        query_grad[...] = scratch[4][...].T.astype(BF16)
        give_half(share, scratch, own, sends)

    outs = [((share, half), BF16), ((2 * share, half), F32)] + [((share, half), BF16)] * (2 * parts - 2)
    return kernel, outs, half_scratch(share, length, half)


def make_self_back_lower(packed, parts, rows, block, width, narrow, n_pieces):
    share = rows * block
    length, half = parts * share, width // 2

    def kernel(*refs):
        me_ref, refs = refs[0], list(refs[1:])
        pieces, refs = refs[:n_pieces], refs[n_pieces:]
        tokens, refs = refs[:rows], refs[rows:]
        operands, refs = refs[:8], refs[8:]
        back1, query_upper = refs[:2]
        in_part, query_sum, query_w_grad, own = refs[2:6]
        sends, scratch = refs[6 : 4 + 2 * parts], refs[4 + 2 * parts :]
        if packed:
            unpack(me_ref[0], pieces, 3 * narrow + 8, 0, narrow, scratch[7])
            query_w = scratch[7]
        else:
            (query_w,) = pieces
        attention_back_half(operands, share, scratch[:7])
        give_half(share, scratch, own, sends)
        query_low = jnp.concatenate([query_upper[...], scratch[4][...].T.astype(BF16)], axis=1)
        tokens_own = jnp.concatenate([t[:block, :] for t in tokens], axis=0)
        in_part[...] = back1[...] + dot_nt(query_low, query_w[...])
        query_sum[...] = jnp.concatenate([total(query_low), jnp.zeros((7, width), F32)], axis=0)
        query_w_grad[...] = dot_tn(tokens_own, query_low).astype(query_w_grad.dtype)

    outs = [
        ((share, width), F32),
        ((8, width), F32),
        ((width, width), BF16 if packed else F32),
        ((2 * share, half), F32),
    ]
    outs += [((share, half), BF16)] * (2 * parts - 2)
    scratch = half_scratch(share, length, half)
    if packed:
        scratch += [((width, width), BF16)]
    return kernel, outs, scratch


def make_last(packed, parts, rows, block, memory_block, width, narrow, n_pieces):
    share = rows * block

    def kernel(*refs):
        me_ref, refs = refs[0], list(refs[1:])
        pieces, refs = refs[:n_pieces], refs[n_pieces:]
        tokens, refs = refs[:rows], refs[rows:]
        in_part, query_sum, query_w_grad, memory_send = refs[:4]
        owns, refs = refs[4:6], refs[6:]
        received = [refs[: 2 * parts - 2], refs[2 * parts - 2 : 4 * parts - 4]]
        refs = refs[4 * parts - 4 :]
        in_own, in_send = refs[:2]
        n_grads = 2 if packed else 3
        grad_refs, scratch = refs[2 : 2 + n_grads], refs[2 + n_grads :]
        sums = scratch[0]
        me = me_ref[0]
        if packed:
            for i in range(2):
                unpack(me, pieces, 3 * narrow + 8, (1 + i) * narrow, narrow, scratch[1 + i])
            key_w, value_w = scratch[1:3]
        else:
            key_w, value_w = pieces
        grads = Grads(me, grad_refs, scratch[3] if packed else None, narrow)
        if packed:
            grads.put(2, query_w_grad[...].astype(F32))
        lows = []
        for own, others in zip(owns, received):
            found = own[...]
            for key, value in zip(others[::2], others[1::2]):
                found = found + jnp.concatenate([key[...], value[...]], axis=0).astype(F32)
            lows.append(found.astype(BF16))
        key_low = jnp.concatenate([low[:share, :] for low in lows], axis=1)
        value_low = jnp.concatenate([low[share:, :] for low in lows], axis=1)
        tokens_own = jnp.concatenate([t[:block, :] for t in tokens], axis=0)
        sums[...] = query_sum[...]
        sums[1:2, :] = total(value_low)
        grads.put_sums(3 * narrow, sums[...])
        grads.put(0, dot_tn(tokens_own, key_low))
        grads.put(1, dot_tn(tokens_own, value_low))
        grad = in_part[...] + dot_nt(key_low, key_w[...]) + dot_nt(value_low, value_w[...])
        in_own[...] = grad[:block, :]
        in_send[:block, :] = grad[block:, :].astype(BF16)
        in_send[block:, :] = memory_send[...]

    outs = [((block, width), F32), ((block + memory_block, width), BF16)]
    if packed:
        outs += [((16, 3 * narrow + 8, width), BF16)] * 2
    else:
        outs += [((width, width), F32)] * 2 + [((8, width), F32)]
    scratch = [((8, width), F32)]
    if packed:
        scratch += [((width, width), BF16)] * 2 + [((width, width), F32)]
    return kernel, outs, scratch


def combine(arrays, splits, micros=0.1):
    count = arrays[0].shape[0] // splits
    shape = (count,) + arrays[0].shape[1:]

    def kernel(*refs):
        given, outs = refs[: len(arrays)], refs[len(arrays) :]
        for i, out in enumerate(outs):
            here = slice(i * count, (i + 1) * count)
            found = given[0][here].astype(F32)
            for ref in given[1:]:
                found = found + ref[here].astype(F32)
            out[...] = found.astype(out.dtype)

    return pl.pallas_call(
        kernel,
        out_shape=[jax.ShapeDtypeStruct(shape, BF16)] * splits,
        in_specs=[VM] * len(arrays),
        out_specs=[VM] * splits,
        compiler_params=pltpu.CompilerParams(vmem_limit_bytes=snug(arrays)),
        cost_estimate=pl.CostEstimate(flops=int(micros * 1.15e9), bytes_accessed=0, transcendentals=0),
        name="combine",
    )(*arrays)


def chosen(me, rows, wide):
    width = rows.shape[1]
    line = lax.broadcasted_iota(jnp.int32, (width, wide), 0)
    here = lax.broadcasted_iota(jnp.int32, (width, wide), 1) + me * wide
    choice = jnp.where(line == here, 1.0, 0.0)
    return lax.dot_general(rows, choice, (((1,), (0,)), ((), ())), precision=lax.Precision.HIGHEST, preferred_element_type=F32)


def reduce_all(array, devices):
    mask = 1
    while mask < devices:
        array = array + swap(array, mask, devices)
        mask *= 2
    return array


def per_device(
    tokens, memory, target_ids, source_ids, cotangent,
    query_weight, key_weight, value_weight, output_weight, query_bias, value_bias, output_bias,
    attention_gain, attention_shift,
    source_query, source_key, source_value, source_output, source_query_bias, source_value_bias,
    source_output_bias, source_gain, source_shift,
    inner_weight, inner_bias, outer_weight, outer_bias, final_gain, final_shift,
    *, devices, sequence,
):
    packed = devices == 32
    rows, block, width = tokens.shape
    memory_block = memory.shape[1]
    parts = sequence // rows
    share, memory_share = rows * block, rows * memory_block
    hidden = inner_weight.shape[1]
    blocks = hidden // width
    me = lax.axis_index(AXES)
    me_array = me.reshape(1).astype(jnp.int32)
    turn = lax.rem(lax.div(me, parts), rows)
    narrow, wide = width // devices, hidden // devices

    def run(made, micros, name, *args, room=10):
        kernel, outs, *scratch = made
        return call(kernel, outs, (me_array,) + args, scratch[0] if scratch else [], micros, name, room)

    short = [query_bias, value_bias, output_bias, attention_gain, attention_shift, source_query_bias,
             source_value_bias, source_output_bias, source_gain, source_shift, outer_bias, final_gain,
             final_shift]

    def whole(array):
        return lax.all_gather(array, AXES, axis=0, tiled=True)

    sent, kept = tokens_packet(
        turn.reshape(1).astype(jnp.int32), tokens, memory, target_ids, source_ids, cotangent
    )
    came = swap(sent, parts, devices)
    row_tokens = [kept, came]
    kept_swaps = [swap(kept, m, devices) for m in range(1, parts)]
    came_swaps = [swap(came, m, devices) for m in range(1, parts)]
    for pair in zip(kept_swaps, came_swaps):
        row_tokens += pair
    own_tokens = row_tokens[:rows]

    if packed:
        first, rest = run(make_weights_packet(narrow, width, blocks), 1.0, "weights_packet",
                          query_weight, key_weight, value_weight, output_weight, source_query,
                          source_key, source_value, source_output, inner_weight, outer_weight,
                          inner_bias.reshape(1, wide), *[v.reshape(1, narrow) for v in short], room=58)
        first = after(first, sent)
        first = join([first, turned_swap(first, 0)])
        first_b = turned_swap(first, 1)
        rest = after(rest, first)
        rest_b = turned_swap(rest, 0)
        first = join(after([first, first_b], rest_b))
        rest = join(after([rest, rest_b], first_b, came, *kept_swaps))
        first_plane, rest_b = exchanged(first), turned_swap(rest, 1)
        second, third = run(
            make_part((5 * narrow + 16, 2 * blocks * narrow), width), 1.0, "part", rest,
            after(rest_b, first_plane[1:]),
        )
        first_plane[1:] = after(first_plane[1:], rest_b, *came_swaps)
        set_self = first_plane + [swap(a, 1, 32) for a in first_plane]
        second_plane = exchanged(second)
    else:
        full = [whole(w) for w in (query_weight, key_weight, value_weight, output_weight, source_query, source_key, source_value, source_output)]
        lane = lax.broadcasted_iota(jnp.int32, (1, width), 1)
        place = lax.broadcasted_iota(jnp.int32, (blocks, width), 0) * width + lane
        spread_wide = jnp.where(place // wide == me, jnp.tile(inner_bias.reshape(1, wide), (blocks, width // wide)), 0)

        def natural(rows):
            return jnp.where(lane // narrow == me, jnp.tile(rows, (1, devices)), 0)

        vectors = jnp.concatenate([natural(jnp.stack(short[:2])), jnp.zeros((6, width), BF16), natural(jnp.stack(short[2:])), spread_wide, jnp.zeros((1, width), BF16)])
        vectors = reduce_all(vectors, devices).astype(F32)
        set_self = full[:3] + [vectors[:8]]
        set_cross = full[3:] + [vectors[8:]]
        set_inner = [
            whole(inner_weight).reshape(width, blocks, width).transpose(1, 0, 2),
            whole(outer_weight).reshape(blocks, width, width),
        ]
    found = run(
        make_project(packed, parts, rows, block, memory_block, width, narrow, len(set_self)), 5.0,
        "project", *set_self, *row_tokens,
    )
    query, query_t, keys, values, value_t = (found[2 * i : 2 * i + 2] for i in range(5))
    row_memory, ids, memory_ids = found[10:]
    query_t = list(query_t)
    if packed:
        set_query, set_last = set_self, set_self
    else:
        set_back, set_query, set_last, set_memory = [full[3], full[4], full[7]], full[:1], full[1:3], full[5:7]
    found = run(
        make_self_attention(share, parts * share, width), 12.0, "self_attention",
        *query_t, *keys, *value_t, ids,
    )
    mixtures, logs = found[:2], found[2:]
    if packed:
        third_plane = exchanged(after(third, mixtures[0]))
        second_plane = after(second_plane, mixtures[0])
        set_cross = second_plane + [swap(a, 1, 32) for a in second_plane]
        set_back, set_memory = set_cross, set_cross
    first_sum, second_sum, cross_query, memory_keys, memory_values, cross_t, cross_logs, vectors = run(
        make_cross_forward(packed, rows, block, parts * memory_share, width, narrow, len(set_cross)),
        9.0, "cross_forward", *set_cross, *own_tokens, row_memory, ids, memory_ids, *mixtures,
    )
    if packed:
        third_plane[1:] = after(third_plane[1:], second_sum)
        set_inner = third_plane + [swap(a, 1, 32) for a in third_plane]
    out_own, out_send, back2_in, sums_inner, *grads_inner = run(
        make_inner(packed, rows, block, width, hidden, narrow, len(set_inner)), 18.0, "inner",
        *set_inner, second_sum, kept, came, vectors,
    )
    out_came = swap(out_send, parts, devices)
    found = run(
        make_cross_back(packed, parts, share, memory_share, width, narrow, len(set_back)), 14.0,
        "cross_back", *set_back, back2_in, first_sum, second_sum, cross_query, memory_keys,
        memory_values, cross_t, cross_logs, ids, memory_ids, vectors, sums_inner, *mixtures,
    )
    back1, memory_key_own, memory_value_own, sums_cross = found[:4]
    slope, slope_t, deltas = (found[4 + 2 * i : 6 + 2 * i] for i in range(3))
    memory_received = [swap(a, m + 1, devices) for m, a in enumerate(found[10 : 10 + parts - 1])]
    grads_early = found[10 + parts - 1 :]
    query = list(query)
    if packed:
        parts_inner = combine(after([grads_inner[0], swap(grads_inner[1], 1, 32)], back1, out_came), 4)
        step_inner = handed(parts_inner)
        memory_key_own = after(memory_key_own, parts_inner[0])
    memory_own, memory_send, *grads_cross = run(
        make_memory_back(packed, parts, rows, block, memory_block, width, narrow, len(set_memory)),
        2.0, "memory_back", *set_memory, *own_tokens, memory_key_own,
        memory_value_own, sums_cross, *grads_early, *memory_received,
    )
    if packed:
        query[0] = after(query[0], grads_cross[0])
        cross_came = swap(grads_cross[1], 1, 32)
    found = run(
        make_self_back_upper(parts, share, width), 7.0, "self_back_upper", query[0], keys[0],
        values[0], slope[0], slope_t[0], logs[0], deltas[0], ids,
    )
    query_upper, own_upper = found[:2]
    received_upper = [swap(a, m // 2 + 1, devices) for m, a in enumerate(found[2:])]
    in_part, query_sum, query_w_grad, own_lower, *sends = run(
        make_self_back_lower(packed, parts, rows, block, width, narrow, len(set_query)), 11.0,
        "self_back_lower", *set_query, *own_tokens, query[1], keys[1], values[1], slope[1],
        slope_t[1], logs[1], deltas[1], ids, back1, query_upper,
    )
    received_lower = [swap(a, m // 2 + 1, devices) for m, a in enumerate(sends)]
    if packed:
        parts_inner = combine(after(step_inner, query_sum), 2)
        keep_inner, send = parts_inner
        step_inner = [keep_inner, turned_swap(send, 1)]
        in_part = after(in_part, keep_inner)
    in_own, in_send, *grads_last = run(
        make_last(packed, parts, rows, block, memory_block, width, narrow, len(set_last)), 6.0,
        "last", *set_last, *own_tokens, in_part, query_sum, query_w_grad, memory_send, own_upper,
        own_lower, *received_upper, *received_lower,
    )

    if packed:
        parts_cross = combine(after([grads_cross[0], cross_came], in_own), 4)
        step_cross = handed(parts_cross)
        parts_last = combine(after([grads_last[0], swap(grads_last[1], 1, 32)], parts_cross[0]), 4)
        step_last = handed(parts_last)
        keep_inner, send = combine(after(step_inner, parts_last[0]), 2)
        step_inner = [keep_inner, turned_swap(send, 0)]
        keep_cross, send = combine(after(step_cross, keep_inner), 2)
        step_cross = [keep_cross, turned_swap(send, 1)]
        in_send = after(in_send, keep_cross)
        keep, send = combine(after(step_last, keep_cross), 2)
        step_last = [keep, turned_swap(send, 1)]
        keep_cross, send = combine(after(step_cross, keep), 2)
        step_cross = [keep_cross, turned_swap(send, 0)]
        keep, send = combine(after(step_last, keep_cross), 2)
        step_last = [keep, turned_swap(send, 0)]

        def plan(me_ref, *refs):
            me = me_ref[0]
            steps, outs = (refs[:2], refs[2:4], refs[4:6]), refs[6:]
            inner, cross, last = (sum(r[0].astype(F32) for r in given) for given in steps)
            for i in range(blocks):
                outs[0][:, i * width : (i + 1) * width] = inner[i * narrow : (i + 1) * narrow, :]
            outs[1][...] = inner[blocks * narrow :, :]
            for i in range(5):
                outs[2 + i][...] = cross[i * narrow : (i + 1) * narrow, :]
            for i in range(3):
                outs[7 + i][...] = last[i * narrow : (i + 1) * narrow, :]
            rows_in = jnp.concatenate([cross[5 * narrow :, :], last[3 * narrow :, :]], axis=0)
            outs[10][...] = chosen(me, rows_in, narrow)
            per = width // wide
            line = lax.broadcasted_iota(jnp.int32, (blocks, width), 0)
            row = jnp.sum(jnp.where(line == lax.div(me, per), rows_in[3 : 3 + blocks, :], 0.0), axis=0, keepdims=True)
            outs[11][...] = chosen(lax.rem(me, per), row, wide)

        part = (narrow, width)
        shapes = [(narrow, hidden), (wide, width)] + [part] * 8 + [(24, narrow), (1, wide)]
        (inner_share, outer_share, source_key_share, source_value_share, source_output_share,
         source_query_share, output_share, key_share, value_share, query_share, sums,
         inner_bias_share) = call(
            plan, [(s, F32) for s in shapes], (me_array, *step_inner, *step_cross, *step_last), [], 2.0,
            "finish",
        )
        inner_bias_share = inner_bias_share.reshape(wide)
    else:
        def scatter(array):
            return lax.psum_scatter(array, AXES, scatter_dimension=0, tiled=True)

        inner_share = scatter(grads_inner[0].transpose(1, 0, 2).reshape(width, hidden))
        outer_share = scatter(grads_inner[1].reshape(hidden, width))
        source_output_share, source_query_share, output_share = (scatter(g.astype(F32)) for g in grads_early)
        source_key_share, source_value_share = (scatter(g) for g in grads_cross[:2])
        key_share, value_share = (scatter(g) for g in grads_last[:2])
        query_share = scatter(query_w_grad)
        sums = reduce_all(jnp.concatenate([grads_cross[2], grads_last[2]], axis=0), devices)
        inner_bias_share = lax.dynamic_slice(sums[3 : 3 + blocks].reshape(hidden), (me * wide,), (wide,))
        sums = lax.dynamic_slice(sums, (0, me * narrow), (sums.shape[0], narrow))
    def regroup(mine, came):
        came = came.astype(F32)
        return jnp.where(turn == 0, jnp.stack([mine, came]), jnp.stack([came, mine]))

    output = regroup(out_own, out_came)
    in_came = swap(in_send, parts, devices)
    input_gradient = regroup(in_own, in_came[:block])
    memory_gradient = regroup(memory_own, in_came[block:])

    return (
        output,
        input_gradient,
        memory_gradient,
        query_share,
        key_share,
        value_share,
        output_share,
        sums[16],
        sums[17],
        sums[13],
        sums[11],
        sums[12],
        source_query_share,
        source_key_share,
        source_value_share,
        source_output_share,
        sums[10],
        sums[14],
        sums[9],
        sums[7],
        sums[8],
        inner_share,
        inner_bias_share,
        outer_share,
        sums[2],
        sums[0],
        sums[1],
    )


def solution(mesh):
    sequence, devices = mesh.shape["seq"], mesh.size
    tokens, ids = P("dp", "seq", None), P("dp", "seq")
    matrix, vector = P(AXES, None), P(AXES)
    attention = (matrix,) * 4 + (vector,) * 5
    inner = (matrix, vector, matrix, vector, vector, vector)
    return jax.shard_map(
        functools.partial(per_device, devices=devices, sequence=sequence),
        mesh=mesh,
        in_specs=(tokens, tokens, ids, ids, tokens) + attention + attention + inner,
        out_specs=(tokens, tokens, tokens) + attention + attention + inner,
        check_vma=False,
    )
```

```python
import functools
import math

import jax
import jax.numpy as jnp
from jax import lax
from jax.experimental import pallas as pl
from jax.experimental.pallas import tpu as pltpu
from jax.sharding import PartitionSpec as P

HEADS = 8
HEAD_DIM = 64
PAIR = 128
EPSILON = 1e-05
MASKED = 1e9
AXES = ("dp", "seq")
F32 = jnp.float32
BF16 = jnp.bfloat16

(
    OUTPUT_BIAS,
    ATTENTION_GAIN,
    ATTENTION_SHIFT,
    SOURCE_QUERY_BIAS,
    SOURCE_VALUE_BIAS,
    SOURCE_OUTPUT_BIAS,
    SOURCE_GAIN,
    SOURCE_SHIFT,
    OUTER_BIAS,
    FINAL_GAIN,
    FINAL_SHIFT,
    INNER_BIAS,
) = range(12)
Z_MASKS = (0, 8, 16, 24)
VM = pl.BlockSpec(memory_space=pltpu.VMEM)
SM = pl.BlockSpec(memory_space=pltpu.SMEM)


def dot(a, b):
    return lax.dot_general(a, b, (((1,), (0,)), ((), ())), preferred_element_type=F32)


def dot_nt(a, b):
    return lax.dot_general(a, b, (((1,), (1,)), ((), ())), preferred_element_type=F32)


def dot_tn(a, b):
    return lax.dot_general(a, b, (((0,), (0,)), ((), ())), preferred_element_type=F32)


def total(values):
    return jnp.sum(values.astype(F32), axis=0, keepdims=True)


def normalize(h):
    average = jnp.mean(h, axis=-1, keepdims=True)
    centered = h - average
    variance = jnp.mean(centered * centered, axis=-1, keepdims=True)
    inverse = lax.rsqrt(variance + EPSILON)
    return centered * inverse, inverse


def normalize_back(upstream, normed, inverse, gain):
    scaled = upstream * gain
    first_mean = jnp.mean(scaled, axis=-1, keepdims=True)
    second_mean = jnp.mean(scaled * normed, axis=-1, keepdims=True)
    return inverse * (scaled - first_mean - normed * second_mean)


def normal_parts(v):
    density = 0.3989422804014327 * jnp.exp(-0.5 * v * v)
    t = 1.0 / (1.0 + 0.2316419 * jnp.abs(v))
    series = t * (
        0.319381530
        + t * (-0.356563782 + t * (1.781477937 + t * (-1.821255978 + t * 1.330274429)))
    )
    tail = density * series
    return jnp.where(v >= 0.0, 1.0 - tail, tail), density


def penalties(ids):
    place = lax.broadcasted_iota(jnp.int32, (PAIR, ids.shape[1]), 0)
    return jnp.where((place == ids) | (place >= 4), 0.0, -MASKED).astype(BF16)


def one_hot(ids):
    place = lax.broadcasted_iota(jnp.int32, (PAIR, ids.shape[1]), 0)
    return jnp.where(place == ids, 1.0, 0.0).astype(F32).T.astype(BF16)


def spread(part, half):
    empty = jnp.zeros_like(part)
    return [part, empty] if half == 0 else [empty, part]


def attend(query_t, keys, value_t, hot, penalty, mixture_t, logs):
    length = keys.shape[0]

    def pair(p, carry):
        columns = pl.ds(pl.multiple_of(p * PAIR, PAIR), PAIR)
        left = jnp.concatenate([keys[:, columns], hot[...]], axis=1)
        for half in range(2):
            rows = pl.ds(pl.multiple_of(p * PAIR + half * HEAD_DIM, HEAD_DIM), HEAD_DIM)
            right = jnp.concatenate(spread(query_t[rows, :], half) + [penalty[...]], axis=0)
            scores = dot(left, right)
            highest = jnp.max(scores, axis=0, keepdims=True)
            weights = jnp.exp(scores - highest).astype(BF16)
            values = jnp.concatenate(
                [value_t[rows, :], jnp.ones((16, length), BF16)], axis=0
            )
            found = dot(values, weights)
            denominator = found[HEAD_DIM : HEAD_DIM + 1, :]
            mixture_t[rows, :] = (found[:HEAD_DIM, :] / denominator).astype(BF16)
            logs[2 * p + half] = highest + jnp.log(denominator)
        return carry

    lax.fori_loop(0, keys.shape[1] // PAIR, pair, 0)


def attend_back(
    query_t, query, keys, key_t, values, slope_t, slope, hot, penalty, logs, deltas,
    query_grad_t, key_grad, value_grad,
):
    tokens = query.shape[0]
    lane = lax.broadcasted_iota(jnp.int32, (tokens, PAIR), 1)

    def pair(p, carry):
        columns = pl.ds(pl.multiple_of(p * PAIR, PAIR), PAIR)
        left = jnp.concatenate([keys[:, columns], hot[...]], axis=1)
        value_pair = values[:, columns]
        key_sum, value_sum = None, None
        for half in range(2):
            rows = pl.ds(pl.multiple_of(p * PAIR + half * HEAD_DIM, HEAD_DIM), HEAD_DIM)
            right = jnp.concatenate(spread(query_t[rows, :], half) + [penalty[...]], axis=0)
            chances = jnp.exp(dot(left, right) - logs[2 * p + half])
            slopes = dot(value_pair, jnp.concatenate(spread(slope_t[rows, :], half), axis=0))
            grads = (chances * (slopes - deltas[2 * p + half])).astype(BF16)
            query_grad_t[rows, :] = dot(key_t[rows, :], grads) * HEAD_DIM**-0.5
            mine = (lane < HEAD_DIM) if half == 0 else (lane >= HEAD_DIM)
            none = jnp.zeros((tokens, PAIR), BF16)
            value_part = dot(chances.astype(BF16), jnp.where(mine, slope[:, columns], none))
            key_part = dot(grads, jnp.where(mine, query[:, columns], none))
            value_sum = value_part if value_sum is None else value_sum + value_part
            key_sum = key_part if key_sum is None else key_sum + key_part
        key_grad[:, columns] = key_sum
        value_grad[:, columns] = value_sum
        return carry

    lax.fori_loop(0, keys.shape[1] // PAIR, pair, 0)


def deltas_of(slope_t, mixture_t, deltas):
    for head in range(slope_t.shape[0] // HEAD_DIM):
        rows = slice(head * HEAD_DIM, (head + 1) * HEAD_DIM)
        deltas[head] = jnp.sum(
            slope_t[rows, :].astype(F32) * mixture_t[rows, :].astype(F32), axis=0, keepdims=True
        )


def swap(array, mask, devices):
    return lax.ppermute(array, AXES, [(i, i ^ mask) for i in range(devices)])


Z_FIRST = ((8, 24, 2, 4), (24, 8, 4, 2))
CROSSED = ((8, 24, 4, 2), (24, 8, 2, 4))


def turned_swap(array, step, orders=Z_FIRST):
    return lax.ppermute(array, AXES, [(i, i ^ orders[i % 2][step]) for i in range(32)])


def after(value, *others):
    return lax.optimization_barrier((value, others))[0]


def places(me, orders=Z_FIRST):
    found = []
    for core in range(2):
        even = ((me & 1) ^ core) == 0
        masks = [jnp.where(even, first, second) for first, second in zip(*orders)]
        for far in range(2):
            for slot in range(8):
                device = me ^ core if core else me
                for step, bit in enumerate((slot & 1, slot & 2, slot & 4, far)):
                    if bit:
                        device = device ^ masks[step]
                found.append((core, far, slot, device))
    return found


def unpack(me, pieces, stride, first, rows, scratch, orders=Z_FIRST):
    for core, far, slot, device in places(me, orders):
        ref = pieces[2 * core + far]
        at = slot * stride + first
        scratch[pl.ds(pl.multiple_of(device * rows, rows), rows), :] = ref[at : at + rows, :]


def vector_sum(pieces, stride, first):
    found = None
    for ref in pieces:
        for slot in range(8):
            part = ref[slot * stride + first : (slot + 1) * stride, :].astype(F32)
            found = part if found is None else found + part
    return found


class Grads:
    def __init__(self, me, refs, dense, rows, orders=Z_FIRST):
        self.me, self.refs, self.dense, self.rows, self.orders = me, refs, dense, rows, orders

    def put(self, index, grad):
        if self.dense is None:
            self.refs[index][...] = grad
            return
        self.dense[...] = grad
        rows = self.rows
        for core, far, slot, device in places(self.me, self.orders):
            found = self.dense[pl.ds(pl.multiple_of(device * rows, rows), rows), :]
            self.refs[core][far * 8 + slot, index * rows : (index + 1) * rows, :] = found.astype(BF16)

    def put_sums(self, first, sums):
        if self.dense is None:
            self.refs[-1][...] = sums
            return
        low = sums.astype(BF16)
        for ref in self.refs:
            for slot in range(16):
                ref[slot, first : first + sums.shape[0], :] = low


def grad_outs(packed, count, rows, width, sums):
    if packed:
        return [((16, count * rows + sums, width), BF16)] * 2
    return [((width, width), F32)] * count + [((sums, width), F32)]


COSTS = {}


def padded(shape, dtype):
    last = -(-shape[-1] // 128) * 128
    tall = -(-shape[-2] // 16) * 16 if len(shape) > 1 else 16
    return math.prod(shape[:-2]) * tall * last * jnp.dtype(dtype).itemsize


def snug(arrays):
    return 2 * sum(padded(a.shape, a.dtype) for a in arrays) + (3 << 20)


def call(kernel, outs, args, scratch, micros, name, room=10):
    moved = sum(math.prod(a.shape) * a.dtype.itemsize for a in args[1:])
    moved += sum(math.prod(s) * jnp.dtype(d).itemsize for s, d in outs)
    need = sum(padded(a.shape, a.dtype) for a in args[1:])
    need += sum(padded(s, d) for s, d in list(outs) + list(scratch))
    return pl.pallas_call(
        kernel,
        out_shape=[jax.ShapeDtypeStruct(s, d) for s, d in outs],
        in_specs=[SM] + [VM] * (len(args) - 1),
        out_specs=[VM] * len(outs),
        scratch_shapes=[pltpu.VMEM(s, d) for s, d in scratch],
        compiler_params=pltpu.CompilerParams(vmem_limit_bytes=min(need + (room << 20), 58 << 20)),
        cost_estimate=pl.CostEstimate(
            flops=int(COSTS.get(name, 0) * 1.15e9) + 1, bytes_accessed=1, transcendentals=0
        ),
        name=name,
    )(*args)


def tokens_packet(turn, tokens, memory, target_ids, source_ids, cotangent):
    block, width = tokens.shape[1:]
    memory_block = memory.shape[1]
    first = block + memory_block + 8

    def kernel(turn_ref, targets, sources, tokens_ref, memory_ref, cot_ref, sent, kept):
        mine = turn_ref[0]
        for row, out in ((1 - mine, sent), (mine, kept)):
            out[:block, :] = tokens_ref[row]
            out[block : block + memory_block, :] = memory_ref[row]
            ids = targets[pl.ds(row, 1), :].astype(F32)
            ids = jnp.concatenate([ids, jnp.zeros((1, width - block), F32)], axis=1)
            others = sources[pl.ds(row, 1), :].astype(F32)
            others = jnp.concatenate([others, jnp.zeros((1, width - memory_block), F32)], axis=1)
            place = lax.broadcasted_iota(jnp.int32, (8, width), 0)
            found = jnp.where(place == 0, ids, jnp.where(place == 1, others, 0.0))
            out[block + memory_block : first, :] = found.astype(BF16)
            out[first:, :] = cot_ref[row]

    shape = (first + block, width)
    return call(kernel, [(shape, BF16)] * 2, (turn, target_ids, source_ids, tokens, memory, cotangent),
                [], 1.0, "tokens_packet", 58)


def placed(me, parts, width):
    here = lax.broadcasted_iota(jnp.int32, (parts.shape[1], width), 0) + me * parts.shape[1]
    lane = lax.broadcasted_iota(jnp.int32, (parts.shape[1], width), 1)
    return dot(parts, jnp.where(lane == here, 1.0, 0.0).astype(BF16))


def make_weights_packet(narrow, width, blocks):
    tall = blocks * narrow

    def kernel(me_ref, *refs):
        weights, inner, outer, wide, short = refs[:8], refs[8], refs[9], refs[10], refs[11:24]
        first, second, third = refs[24:]
        me = me_ref[0]
        for i, ref in enumerate(weights):
            if i < 3:
                first[i * narrow : (i + 1) * narrow, :] = ref[...]
            else:
                second[(i - 3) * narrow : (i - 2) * narrow, :] = ref[...]
        short = jnp.concatenate([ref[...].astype(F32) for ref in short], axis=0).astype(BF16)
        found = placed(me, short, width)
        first[3 * narrow :, :] = jnp.concatenate([found[:2, :], jnp.zeros((6, width), F32)], axis=0).astype(BF16)
        per = width // wide.shape[1]
        row = placed(lax.rem(me, per), wide[...], width)
        place = lax.broadcasted_iota(jnp.int32, (blocks, width), 0)
        spread_row = jnp.where(place == lax.div(me, per), row, 0.0)
        none = jnp.zeros((16 - (found.shape[0] - 2) - blocks, width), F32)
        second[5 * narrow :, :] = jnp.concatenate([found[2:, :], spread_row, none], axis=0).astype(BF16)
        for i in range(blocks):
            third[i * narrow : (i + 1) * narrow, :] = inner[:, i * width : (i + 1) * width]
        third[tall:, :] = outer[...]

    return kernel, [((rows, width), BF16) for rows in (3 * narrow + 8, 5 * narrow + 16, 2 * tall)]


def join(arrays):
    def kernel(*refs):
        at = 0
        for ref in refs[:-1]:
            refs[-1][at : at + ref.shape[0], :] = ref[...]
            at += ref.shape[0]

    rows = sum(a.shape[0] for a in arrays)
    return pl.pallas_call(
        kernel,
        out_shape=jax.ShapeDtypeStruct((rows, arrays[0].shape[1]), arrays[0].dtype),
        in_specs=[VM] * len(arrays),
        out_specs=VM,
        compiler_params=pltpu.CompilerParams(vmem_limit_bytes=snug(arrays)),
        cost_estimate=pl.CostEstimate(flops=1 << 20, bytes_accessed=0, transcendentals=0),
        name="join",
    )(*arrays)


def make_project(packed, parts, rows, block, memory_block, width, narrow, n_pieces):
    share = rows * block
    length = parts * share
    memory_share = rows * memory_block
    stride = 3 * narrow + 8
    half = width // 2

    def kernel(*refs):
        me_ref, refs = refs[0], list(refs[1:])
        pieces, refs = refs[:n_pieces], refs[n_pieces:]
        tokens, refs = refs[: parts * rows], refs[parts * rows :]
        query, query_t, keys, values, value_t = (refs[2 * i : 2 * i + 2] for i in range(5))
        memory, ids, memory_ids = refs[10:13]
        scratch = refs[13:]
        me = me_ref[0]
        if packed:
            for i in range(3):
                unpack(me, pieces, stride, i * narrow, narrow, scratch[i])
            query_w, key_w, value_w = scratch
            biases = vector_sum(pieces, stride, 3 * narrow)
        else:
            query_w, key_w, value_w = pieces[:3]
            biases = pieces[3][...]
        for i in range(parts):
            here = slice(i * share, (i + 1) * share)
            some = tokens[i * rows : (i + 1) * rows]
            own = jnp.concatenate([t[:block, :] for t in some], axis=0)
            if i == 0:
                scaled = (dot(own, query_w[...]) + biases[0:1, :]).astype(BF16) * BF16(HEAD_DIM**-0.5)
            key = dot(own, key_w[...]).astype(BF16)
            found = (dot(own, value_w[...]) + biases[1:2, :]).astype(BF16)
            for side in range(2):
                columns = slice(side * half, (side + 1) * half)
                if i == 0:
                    query[side][...] = scaled[:, columns]
                    query_t[side][...] = scaled[:, columns].T
                keys[side][here, :] = key[:, columns]
                values[side][here, :] = found[:, columns]
                value_t[side][:, here] = found[:, columns].T
        for i, t in enumerate(tokens):
            memory[i * memory_block : (i + 1) * memory_block, :] = t[block : block + memory_block, :]
            found = t[block + memory_block : block + memory_block + 8, :].astype(F32).astype(jnp.int32)
            ids[:, i * block : (i + 1) * block] = found[0:1, :block]
        found = [t[block + memory_block : block + memory_block + 8, :].astype(F32).astype(jnp.int32)[1:2, :memory_block] for t in tokens]
        memory_ids[...] = jnp.concatenate(found, axis=1)

    outs = [((share, half), BF16)] * 2 + [((half, share), BF16)] * 2
    outs += [((length, half), BF16)] * 4 + [((half, length), BF16)] * 2
    outs += [
        ((parts * memory_share, width), BF16),
        ((1, length), jnp.int32),
        ((1, parts * memory_share), jnp.int32),
    ]
    return kernel, outs, [((width, width), BF16)] * 3 if packed else []


def make_self_attention(share, length, width):
    def kernel(me_ref, *refs):
        query_t, keys, value_t, ids = refs[:2], refs[2:4], refs[4:6], refs[6]
        mixture_t, logs, hot, penalty = refs[7:9], refs[9:11], refs[11], refs[12]
        hot[...] = one_hot(ids[...])
        penalty[...] = penalties(ids[:, :share])
        for side in range(2):
            attend(query_t[side], keys[side], value_t[side], hot, penalty, mixture_t[side], logs[side])

    outs = [((width // 2, share), BF16)] * 2 + [((HEADS // 2, 1, share), F32)] * 2
    return kernel, outs, [((length, PAIR), BF16), ((PAIR, share), BF16)]


def make_cross_forward(packed, rows, block, memory_length, width, narrow, n_pieces):
    share = rows * block
    stride = 5 * narrow + 16

    def kernel(*refs):
        me_ref, refs = refs[0], list(refs[1:])
        pieces, refs = refs[:n_pieces], refs[n_pieces:]
        tokens, refs = refs[:rows], refs[rows:]
        memory, ids, memory_ids, upper, lower = refs[:5]
        first_sum, second_sum, query, memory_keys, memory_values, cross_t, logs, vectors = refs[5:13]
        scratch = refs[13:]
        query_t, value_t, hot, penalty = scratch[:4]
        if packed:
            for i in range(5):
                unpack(me_ref[0], pieces, stride, i * narrow, narrow, scratch[4 + i])
            output_w, query_w, key_w, value_w, source_w = scratch[4:]
            vectors[...] = vector_sum(pieces, stride, 5 * narrow)
        else:
            output_w, query_w, key_w, value_w, source_w = pieces[:5]
            vectors[...] = pieces[5][...]

        def vector(i):
            return vectors[i : i + 1, :]

        own = jnp.concatenate([t[:block, :] for t in tokens], axis=0)
        mixture_t = jnp.concatenate([upper[...], lower[...]], axis=0)
        h = own.astype(F32) + dot_tn(mixture_t, output_w[...]) + vector(OUTPUT_BIAS)
        first_sum[...] = h
        first = normalize(h)[0] * vector(ATTENTION_GAIN) + vector(ATTENTION_SHIFT)
        scaled = (dot(first.astype(BF16), query_w[...]) + vector(SOURCE_QUERY_BIAS)).astype(BF16) * BF16(HEAD_DIM**-0.5)
        query[...] = scaled
        query_t[...] = scaled.T
        memory_keys[...] = dot(memory[...], key_w[...]).astype(BF16)
        memory_values[...] = (dot(memory[...], value_w[...]) + vector(SOURCE_VALUE_BIAS)).astype(BF16)
        value_t[...] = memory_values[...].T
        hot[...] = one_hot(memory_ids[...])
        penalty[...] = penalties(ids[:, :share])
        attend(query_t, memory_keys, value_t, hot, penalty, cross_t, logs)
        first = normalize(first_sum[...])[0] * vector(ATTENTION_GAIN) + vector(ATTENTION_SHIFT)
        second_sum[...] = first + dot_tn(cross_t[...], source_w[...]) + vector(SOURCE_OUTPUT_BIAS)

    outs = [
        ((share, width), F32),
        ((share, width), F32),
        ((share, width), BF16),
        ((memory_length, width), BF16),
        ((memory_length, width), BF16),
        ((width, share), BF16),
        ((HEADS, 1, share), F32),
        ((16, width), F32),
    ]
    scratch = [((width, share), BF16), ((width, memory_length), BF16), ((memory_length, PAIR), BF16), ((PAIR, share), BF16)]
    if packed:
        scratch += [((width, width), BF16)] * 5
    return kernel, outs, scratch


def make_inner(packed, rows, block, width, hidden, narrow, n_pieces):
    blocks = hidden // width
    share = rows * block
    per = width // (blocks * narrow)

    def kernel(*refs):
        me_ref, refs = refs[0], list(refs[1:])
        pieces, refs = refs[:n_pieces], refs[n_pieces:]
        second_sum, cot_own, cot_came, vectors = refs[:4]
        out_own, out_send, back, sums = refs[4:8]
        grads, scratch = refs[8:10], refs[10:]
        low, active, gate, slope = scratch[:4]
        if packed:
            inner_w, outer_w, gathered, dense = scratch[4:8]
            tall = blocks * narrow
            for core, far, slot, device in places(me_ref[0]):
                ref, at = pieces[2 * core + far], slot * 2 * tall
                row = pl.multiple_of(device * narrow, narrow)
                for i in range(blocks):
                    inner_w[i, pl.ds(row, narrow), :] = ref[at + i * narrow : at + (i + 1) * narrow, :]
                row = pl.multiple_of(lax.rem(device, per) * tall, tall)
                outer_w[lax.div(device, per), pl.ds(row, tall), :] = ref[at + tall : at + 2 * tall, :]
        else:
            inner_w, outer_w = pieces

        def vector(i):
            return vectors[i : i + 1, :]

        second = normalize(second_sum[...])[0] * vector(SOURCE_GAIN) + vector(SOURCE_SHIFT)
        low[...] = second.astype(BF16)
        back[...] = second + vector(OUTER_BIAS)

        def forward(i, carry):
            inner = dot(low[...], inner_w[i]) + vectors[pl.ds(INNER_BIAS + i, 1), :]
            chance, density = normal_parts(inner)
            found = (inner * chance).astype(BF16)
            active[i] = found
            gate[i] = chance + inner * density
            back[...] += dot(found, outer_w[i])
            return carry

        lax.fori_loop(0, blocks, forward, 0)
        normed, inverse = normalize(back[...])
        final = normed * vector(FINAL_GAIN) + vector(FINAL_SHIFT)
        out_own[...] = final[:block, :]
        out_send[...] = final[block:, :].astype(BF16)
        upstream = jnp.concatenate([cot_own[-block:, :], cot_came[-block:, :]], axis=0).astype(F32)
        sums[0:1, :] = total(upstream * normed)
        sums[1:2, :] = total(upstream)
        back3 = normalize_back(upstream, normed, inverse, vector(FINAL_GAIN))
        slope[...] = back3.astype(BF16)
        sums[2:3, :] = total(slope[...])
        sums[7:8, :] = jnp.zeros_like(sums[7:8, :])
        back[...] = back3

        def backward(i, carry):
            grad = dot_nt(slope[...], outer_w[i]) * gate[i]
            inner_low = grad.astype(BF16)
            sums[pl.ds(3 + i, 1), :] = total(inner_low)
            outer_grad = dot_tn(active[i], slope[...])
            inner_grad = dot_tn(low[...], inner_low)
            back[...] += dot_nt(inner_low, inner_w[i])
            if packed:
                dense[...] = inner_grad
                gathered[i] = outer_grad.astype(BF16)
                here = pl.ds(pl.multiple_of(i * narrow, narrow), narrow)
                for core, far, slot, device in places(me_ref[0]):
                    row = pl.multiple_of(device * narrow, narrow)
                    grads[core][far * 8 + slot, here, :] = dense[pl.ds(row, narrow), :].astype(BF16)
            else:
                grads[0][i] = inner_grad
                grads[1][i] = outer_grad
            return carry

        lax.fori_loop(0, blocks, backward, 0)
        if packed:
            tall = blocks * narrow
            for core, far, slot, device in places(me_ref[0]):
                row = pl.multiple_of(lax.rem(device, per) * tall, tall)
                grads[core][far * 8 + slot, tall:, :] = gathered[lax.div(device, per), pl.ds(row, tall), :]

    outs = [((block, width), F32), ((block, width), BF16), ((share, width), F32), ((8, width), F32)]
    if packed:
        outs += [((16, 2 * blocks * narrow, width), BF16)] * 2
    else:
        outs += [((blocks, width, width), F32)] * 2
    scratch = [((share, width), BF16), ((blocks, share, width), BF16), ((blocks, share, width), F32), ((share, width), BF16)]
    if packed:
        scratch += [((blocks, width, width), BF16)] * 3 + [((width, width), F32)]
    return kernel, outs, scratch


def make_cross_back(packed, parts, share, memory_share, width, narrow, n_pieces):
    memory_length = parts * memory_share
    stride = 5 * narrow + 16

    def kernel(*refs):
        me_ref, refs = refs[0], list(refs[1:])
        pieces, refs = refs[:n_pieces], refs[n_pieces:]
        (back2_in, first_sum, second_sum, query, memory_keys, memory_values, cross_t, logs, ids,
         memory_ids, vectors, sums_inner) = refs[:12]
        mixtures, refs = refs[12:14], refs[14:]
        back1, key_own, value_own, sums = refs[:4]
        self_slope, self_slope_t, self_deltas = (refs[4 + 2 * i : 6 + 2 * i] for i in range(3))
        sends, refs = refs[10 : 10 + parts - 1], refs[10 + parts - 1 :]
        grads, scratch = refs[:3], refs[3:]
        (slope_t, slope, key_t, hot, penalty, query_t, deltas, query_grad_t, key_grad, value_grad) = scratch[:10]
        upper, lower = mixtures
        if packed:
            for i, at in enumerate((0, 1, 4)):
                unpack(me_ref[0], pieces, stride, at * narrow, narrow, scratch[10 + i])
            output_w, query_w, source_w = scratch[10:13]
        else:
            output_w, query_w, source_w = pieces

        def vector(i):
            return vectors[i : i + 1, :]

        sums[0:7, :] = sums_inner[0:7, :]
        upstream = back2_in[...]
        normed, inverse = normalize(second_sum[...])
        sums[7:8, :] = total(upstream * normed)
        sums[8:9, :] = total(upstream)
        back2 = normalize_back(upstream, normed, inverse, vector(SOURCE_GAIN))
        back1[...] = back2
        cross_low = back2.astype(BF16)
        sums[9:10, :] = total(cross_low)
        grads[0][...] = dot(cross_t[...], cross_low).astype(BF16)
        found = dot_nt(cross_low, source_w[...]).astype(BF16)
        slope[...] = found
        slope_t[...] = found.T
        deltas_of(slope_t, cross_t, deltas)
        query_t[...] = query[...].T
        key_t[...] = memory_keys[...].T
        hot[...] = one_hot(memory_ids[...])
        penalty[...] = penalties(ids[:, :share])
        attend_back(query_t, query, memory_keys, key_t, memory_values, slope_t, slope, hot, penalty,
                    logs, deltas, query_grad_t, key_grad, value_grad)
        key_own[...] = key_grad[:memory_share, :]
        value_own[...] = value_grad[:memory_share, :]
        for i in range(1, parts):
            here = slice(i * memory_share, (i + 1) * memory_share)
            sends[i - 1][:memory_share, :] = key_grad[here, :].astype(BF16)
            sends[i - 1][memory_share:, :] = value_grad[here, :].astype(BF16)
        query_low = query_grad_t[...].T.astype(BF16)
        sums[10:11, :] = total(query_low)
        normed, inverse = normalize(first_sum[...])
        first_low = (normed * vector(ATTENTION_GAIN) + vector(ATTENTION_SHIFT)).astype(BF16)
        grads[1][...] = dot_tn(first_low, query_low).astype(BF16)
        upstream = back1[...] + dot_nt(query_low, query_w[...])
        sums[11:12, :] = total(upstream * normed)
        sums[12:13, :] = total(upstream)
        grad = normalize_back(upstream, normed, inverse, vector(ATTENTION_GAIN))
        back1[...] = grad
        branch_low = grad.astype(BF16)
        sums[13:14, :] = total(branch_low)
        sums[14:16, :] = jnp.zeros_like(sums[14:16, :])
        mixture_t = jnp.concatenate([upper[...], lower[...]], axis=0)
        grads[2][...] = dot(mixture_t, branch_low).astype(BF16)
        found = dot_nt(branch_low, output_w[...]).astype(BF16)
        for side in range(2):
            columns = slice(side * width // 2, (side + 1) * width // 2)
            self_slope[side][...] = found[:, columns]
            self_slope_t[side][...] = found[:, columns].T
            deltas_of(self_slope_t[side], mixtures[side], self_deltas[side])

    half = width // 2
    outs = [
        ((share, width), F32),
        ((memory_share, width), F32),
        ((memory_share, width), F32),
        ((16, width), F32),
    ]
    outs += [((share, half), BF16)] * 2 + [((half, share), BF16)] * 2
    outs += [((HEADS // 2, 1, share), F32)] * 2
    outs += [((2 * memory_share, width), BF16)] * (parts - 1)
    outs += [((width, width), BF16)] * 3
    scratch = [
        ((width, share), BF16),
        ((share, width), BF16),
        ((width, memory_length), BF16),
        ((memory_length, PAIR), BF16),
        ((PAIR, share), BF16),
        ((width, share), BF16),
        ((HEADS, 1, share), F32),
        ((width, share), F32),
        ((memory_length, width), F32),
        ((memory_length, width), F32),
    ]
    if packed:
        scratch += [((width, width), BF16)] * 3
    return kernel, outs, scratch


def attention_back_half(refs, share, scratch):
    query, keys, values, slope, slope_t, logs, deltas, ids = refs
    query_t, key_t, hot, penalty, query_grad_t, key_grad, value_grad = scratch
    query_t[...] = query[...].T
    key_t[...] = keys[...].T
    hot[...] = one_hot(ids[...])
    penalty[...] = penalties(ids[:, :share])
    attend_back(query_t, query, keys, key_t, values, slope_t, slope, hot, penalty, logs, deltas,
                query_grad_t, key_grad, value_grad)


def half_scratch(share, length, half):
    return [
        ((half, share), BF16),
        ((half, length), BF16),
        ((length, PAIR), BF16),
        ((PAIR, share), BF16),
        ((half, share), F32),
        ((length, half), F32),
        ((length, half), F32),
    ]


def give_half(share, scratch, own, sends):
    key_grad, value_grad = scratch[5:7]
    own[:share, :] = key_grad[:share, :]
    own[share:, :] = value_grad[:share, :]
    for i, send in enumerate(sends):
        here = slice((i // 2 + 1) * share, (i // 2 + 2) * share)
        send[...] = (key_grad, value_grad)[i % 2][here, :].astype(BF16)


def make_memory_back(packed, parts, rows, block, memory_block, width, narrow, n_pieces):
    memory_share = rows * memory_block

    def kernel(*refs):
        me_ref, refs = refs[0], list(refs[1:])
        pieces, refs = refs[:n_pieces], refs[n_pieces:]
        tokens, refs = refs[:rows], refs[rows:]
        memory_key_own, memory_value_own, sums_in = refs[:3]
        early, refs = refs[3:6], refs[6:]
        memory_received, refs = refs[: parts - 1], refs[parts - 1 :]
        memory_own, memory_send = refs[:2]
        n_grads = 2 if packed else 3
        grad_refs, scratch = refs[2 : 2 + n_grads], refs[2 + n_grads :]
        sums = scratch[0]
        me = me_ref[0]
        if packed:
            for i in range(2):
                unpack(me, pieces, 5 * narrow + 16, (2 + i) * narrow, narrow, scratch[1 + i])
            source_key, source_value = scratch[1:3]
        else:
            source_key, source_value = pieces
        grads = Grads(me, grad_refs, scratch[3] if packed else None, narrow, CROSSED)
        memory = jnp.concatenate([t[block : block + memory_block, :] for t in tokens], axis=0)
        key_sum, value_sum = memory_key_own[...], memory_value_own[...]
        for ref in memory_received:
            key_sum = key_sum + ref[:memory_share, :].astype(F32)
            value_sum = value_sum + ref[memory_share:, :].astype(F32)
        key_low, value_low = key_sum.astype(BF16), value_sum.astype(BF16)
        sums[...] = sums_in[...]
        sums[14:15, :] = total(value_low)
        grads.put_sums(5 * narrow, sums[...])
        grads.put(0, dot_tn(memory, key_low))
        grads.put(1, dot_tn(memory, value_low))
        if packed:
            for i, ref in enumerate(early):
                grads.put(2 + i, ref[...].astype(F32))
        grad = dot_nt(key_low, source_key[...]) + dot_nt(value_low, source_value[...])
        memory_own[...] = grad[:memory_block, :]
        memory_send[...] = grad[memory_block:, :].astype(BF16)

    outs = [((memory_block, width), F32), ((memory_block, width), BF16)]
    if packed:
        outs += [((16, 5 * narrow + 16, width), BF16)] * 2
    else:
        outs += [((width, width), F32)] * 2 + [((16, width), F32)]
    scratch = [((16, width), F32)]
    if packed:
        scratch += [((width, width), BF16)] * 2 + [((width, width), F32)]
    return kernel, outs, scratch


def make_self_back_upper(parts, share, width):
    length, half = parts * share, width // 2

    def kernel(*refs):
        operands, (query_grad, own), refs = refs[1:9], refs[9:11], refs[11:]
        sends, scratch = refs[: 2 * parts - 2], refs[2 * parts - 2 :]
        attention_back_half(operands, share, scratch)
        query_grad[...] = scratch[4][...].T.astype(BF16)
        give_half(share, scratch, own, sends)

    outs = [((share, half), BF16), ((2 * share, half), F32)] + [((share, half), BF16)] * (2 * parts - 2)
    return kernel, outs, half_scratch(share, length, half)


def make_self_back_lower(packed, parts, rows, block, width, narrow, n_pieces):
    share = rows * block
    length, half = parts * share, width // 2

    def kernel(*refs):
        me_ref, refs = refs[0], list(refs[1:])
        pieces, refs = refs[:n_pieces], refs[n_pieces:]
        tokens, refs = refs[:rows], refs[rows:]
        operands, refs = refs[:8], refs[8:]
        back1, query_upper = refs[:2]
        in_part, query_sum, query_w_grad, own = refs[2:6]
        sends, scratch = refs[6 : 4 + 2 * parts], refs[4 + 2 * parts :]
        if packed:
            unpack(me_ref[0], pieces, 3 * narrow + 8, 0, narrow, scratch[7])
            query_w = scratch[7]
        else:
            (query_w,) = pieces
        attention_back_half(operands, share, scratch[:7])
        give_half(share, scratch, own, sends)
        query_low = jnp.concatenate([query_upper[...], scratch[4][...].T.astype(BF16)], axis=1)
        tokens_own = jnp.concatenate([t[:block, :] for t in tokens], axis=0)
        in_part[...] = back1[...] + dot_nt(query_low, query_w[...])
        query_sum[...] = jnp.concatenate([total(query_low), jnp.zeros((7, width), F32)], axis=0)
        query_w_grad[...] = dot_tn(tokens_own, query_low).astype(query_w_grad.dtype)

    outs = [
        ((share, width), F32),
        ((8, width), F32),
        ((width, width), BF16 if packed else F32),
        ((2 * share, half), F32),
    ]
    outs += [((share, half), BF16)] * (2 * parts - 2)
    scratch = half_scratch(share, length, half)
    if packed:
        scratch += [((width, width), BF16)]
    return kernel, outs, scratch


def make_last(packed, parts, rows, block, memory_block, width, narrow, n_pieces):
    share = rows * block

    def kernel(*refs):
        me_ref, refs = refs[0], list(refs[1:])
        pieces, refs = refs[:n_pieces], refs[n_pieces:]
        tokens, refs = refs[:rows], refs[rows:]
        in_part, query_sum, query_w_grad, memory_send = refs[:4]
        owns, refs = refs[4:6], refs[6:]
        received = [refs[: 2 * parts - 2], refs[2 * parts - 2 : 4 * parts - 4]]
        refs = refs[4 * parts - 4 :]
        in_own, in_send = refs[:2]
        n_grads = 2 if packed else 3
        grad_refs, scratch = refs[2 : 2 + n_grads], refs[2 + n_grads :]
        sums = scratch[0]
        me = me_ref[0]
        if packed:
            for i in range(2):
                unpack(me, pieces, 3 * narrow + 8, (1 + i) * narrow, narrow, scratch[1 + i])
            key_w, value_w = scratch[1:3]
        else:
            key_w, value_w = pieces
        grads = Grads(me, grad_refs, scratch[3] if packed else None, narrow)
        if packed:
            grads.put(2, query_w_grad[...].astype(F32))
        lows = []
        for own, others in zip(owns, received):
            found = own[...]
            for key, value in zip(others[::2], others[1::2]):
                found = found + jnp.concatenate([key[...], value[...]], axis=0).astype(F32)
            lows.append(found.astype(BF16))
        key_low = jnp.concatenate([low[:share, :] for low in lows], axis=1)
        value_low = jnp.concatenate([low[share:, :] for low in lows], axis=1)
        tokens_own = jnp.concatenate([t[:block, :] for t in tokens], axis=0)
        sums[...] = query_sum[...]
        sums[1:2, :] = total(value_low)
        grads.put_sums(3 * narrow, sums[...])
        grads.put(0, dot_tn(tokens_own, key_low))
        grads.put(1, dot_tn(tokens_own, value_low))
        grad = in_part[...] + dot_nt(key_low, key_w[...]) + dot_nt(value_low, value_w[...])
        in_own[...] = grad[:block, :]
        in_send[:block, :] = grad[block:, :].astype(BF16)
        in_send[block:, :] = memory_send[...]

    outs = [((block, width), F32), ((block + memory_block, width), BF16)]
    if packed:
        outs += [((16, 3 * narrow + 8, width), BF16)] * 2
    else:
        outs += [((width, width), F32)] * 2 + [((8, width), F32)]
    scratch = [((8, width), F32)]
    if packed:
        scratch += [((width, width), BF16)] * 2 + [((width, width), F32)]
    return kernel, outs, scratch


def combine(arrays, splits, micros=0.1):
    count = arrays[0].shape[0] // splits
    shape = (count,) + arrays[0].shape[1:]

    def kernel(*refs):
        given, outs = refs[: len(arrays)], refs[len(arrays) :]
        for i, out in enumerate(outs):
            here = slice(i * count, (i + 1) * count)
            found = given[0][here].astype(F32)
            for ref in given[1:]:
                found = found + ref[here].astype(F32)
            out[...] = found.astype(out.dtype)

    return pl.pallas_call(
        kernel,
        out_shape=[jax.ShapeDtypeStruct(shape, BF16)] * splits,
        in_specs=[VM] * len(arrays),
        out_specs=[VM] * splits,
        compiler_params=pltpu.CompilerParams(vmem_limit_bytes=snug(arrays)),
        cost_estimate=pl.CostEstimate(flops=int(micros * 1.15e9), bytes_accessed=0, transcendentals=0),
        name="combine",
    )(*arrays)


def combine_joint(groups, splits):
    count, sizes = groups[0][0].shape[0] // splits, [g[0].shape[1] for g in groups]
    shape = (count, sum(sizes)) + groups[0][0].shape[2:]
    flat = [a for group in groups for a in group]

    def kernel(*refs):
        outs, at, row = refs[len(flat) :], 0, 0
        for group, size in zip(groups, sizes):
            given = refs[at : at + len(group)]
            at += len(group)
            for i, out in enumerate(outs):
                here = slice(i * count, (i + 1) * count)
                found = given[0][here].astype(F32)
                for ref in given[1:]:
                    found = found + ref[here].astype(F32)
                out[:, row : row + size, :] = found.astype(BF16)
            row += size

    return pl.pallas_call(
        kernel,
        out_shape=[jax.ShapeDtypeStruct(shape, BF16)] * splits,
        in_specs=[VM] * len(flat),
        out_specs=[VM] * splits,
        compiler_params=pltpu.CompilerParams(vmem_limit_bytes=snug(flat)),
        cost_estimate=pl.CostEstimate(flops=1, bytes_accessed=1, transcendentals=0),
        name="combine_joint",
    )(*flat)


def chosen(me, rows, wide):
    width = rows.shape[1]
    line = lax.broadcasted_iota(jnp.int32, (width, wide), 0)
    here = lax.broadcasted_iota(jnp.int32, (width, wide), 1) + me * wide
    choice = jnp.where(line == here, 1.0, 0.0)
    return lax.dot_general(rows, choice, (((1,), (0,)), ((), ())), precision=lax.Precision.HIGHEST, preferred_element_type=F32)


def reduce_all(array, devices):
    mask = 1
    while mask < devices:
        array = array + swap(array, mask, devices)
        mask *= 2
    return array


def per_device(
    tokens, memory, target_ids, source_ids, cotangent,
    query_weight, key_weight, value_weight, output_weight, query_bias, value_bias, output_bias,
    attention_gain, attention_shift,
    source_query, source_key, source_value, source_output, source_query_bias, source_value_bias,
    source_output_bias, source_gain, source_shift,
    inner_weight, inner_bias, outer_weight, outer_bias, final_gain, final_shift,
    *, devices, sequence,
):
    packed = devices == 32
    rows, block, width = tokens.shape
    memory_block = memory.shape[1]
    parts = sequence // rows
    share, memory_share = rows * block, rows * memory_block
    hidden = inner_weight.shape[1]
    blocks = hidden // width
    me = lax.axis_index(AXES)
    me_array = me.reshape(1).astype(jnp.int32)
    turn = lax.rem(lax.div(me, parts), rows)
    narrow, wide = width // devices, hidden // devices

    def run(made, micros, name, *args, room=10):
        kernel, outs, *scratch = made
        return call(kernel, outs, (me_array,) + args, scratch[0] if scratch else [], micros, name, room)

    short = [query_bias, value_bias, output_bias, attention_gain, attention_shift, source_query_bias,
             source_value_bias, source_output_bias, source_gain, source_shift, outer_bias, final_gain,
             final_shift]

    def whole(array):
        return lax.all_gather(array, AXES, axis=0, tiled=True)

    sent, kept = tokens_packet(
        turn.reshape(1).astype(jnp.int32), tokens, memory, target_ids, source_ids, cotangent
    )
    came = swap(sent, parts, devices)
    row_tokens = [kept, came]
    kept_swaps = [swap(kept, m, devices) for m in range(1, parts)]
    came_swaps = [swap(came, m, devices) for m in range(1, parts)]
    for pair in zip(kept_swaps, came_swaps):
        row_tokens += pair
    own_tokens = row_tokens[:rows]

    if packed:
        first, second, third = run(make_weights_packet(narrow, width, blocks), 1.0, "weights_packet",
                          query_weight, key_weight, value_weight, output_weight, source_query,
                          source_key, source_value, source_output, inner_weight, outer_weight,
                          inner_bias.reshape(1, wide), *[v.reshape(1, narrow) for v in short], room=58)
        first = after(first, sent)
        first = join([first, turned_swap(first, 0)])
        first_b = turned_swap(first, 1)
        second = after(second, first)
        second_b = turned_swap(second, 0)
        first, second = join(after([first, first_b], second_b)), join(after([second, second_b], first_b))
        third = after(third, second)
        first_b, second_b, third_b = turned_swap(first, 2), turned_swap(second, 1), turned_swap(third, 0)
        first_c = join(after([first, first_b], second_b, third_b, came, *kept_swaps))
        second = join(after([second, second_b], first_b, third_b))
        third = join(after([third, third_b], first_b, second_b))
        first_d, second_b, third_b = turned_swap(first_c, 3), turned_swap(second, 2), turned_swap(third, 1)
        second_c = join(after([second, second_b], first_d, third_b))
        third = join(after([third, third_b], first_d, second_b))
        first_d = after(first_d, second_c, third, *came_swaps)
        second_d, third_b = turned_swap(second_c, 3), turned_swap(third, 2)
        set_self = [first_c, first_d, swap(first_c, 1, 32), swap(first_d, 1, 32)]
    else:
        full = [whole(w) for w in (query_weight, key_weight, value_weight, output_weight, source_query, source_key, source_value, source_output)]
        lane = lax.broadcasted_iota(jnp.int32, (1, width), 1)
        place = lax.broadcasted_iota(jnp.int32, (blocks, width), 0) * width + lane
        spread_wide = jnp.where(place // wide == me, jnp.tile(inner_bias.reshape(1, wide), (blocks, width // wide)), 0)

        def natural(rows):
            return jnp.where(lane // narrow == me, jnp.tile(rows, (1, devices)), 0)

        vectors = jnp.concatenate([natural(jnp.stack(short[:2])), jnp.zeros((6, width), BF16), natural(jnp.stack(short[2:])), spread_wide, jnp.zeros((1, width), BF16)])
        vectors = reduce_all(vectors, devices).astype(F32)
        set_self = full[:3] + [vectors[:8]]
        set_cross = full[3:] + [vectors[8:]]
        set_inner = [
            whole(inner_weight).reshape(width, blocks, width).transpose(1, 0, 2),
            whole(outer_weight).reshape(blocks, width, width),
        ]
    found = run(
        make_project(packed, parts, rows, block, memory_block, width, narrow, len(set_self)), 5.0,
        "project", *set_self, *row_tokens,
    )
    query, query_t, keys, values, value_t = (found[2 * i : 2 * i + 2] for i in range(5))
    row_memory, ids, memory_ids = found[10:]
    query_t = list(query_t)
    if packed:
        set_query, set_last = set_self, set_self
    else:
        set_back, set_query, set_last, set_memory = [full[3], full[4], full[7]], full[:1], full[1:3], full[5:7]
    found = run(
        make_self_attention(share, parts * share, width), 12.0, "self_attention",
        *query_t, *keys, *value_t, ids,
    )
    mixtures, logs = found[:2], found[2:]
    if packed:
        third_c = join(after([third, third_b], mixtures[0]))
        third_d = turned_swap(third_c, 3)
        second_d = after(second_d, mixtures[0])
        set_cross = [second_c, second_d, swap(second_c, 1, 32), swap(second_d, 1, 32)]
        set_back, set_memory = set_cross, set_cross
    first_sum, second_sum, cross_query, memory_keys, memory_values, cross_t, cross_logs, vectors = run(
        make_cross_forward(packed, rows, block, parts * memory_share, width, narrow, len(set_cross)),
        9.0, "cross_forward", *set_cross, *own_tokens, row_memory, ids, memory_ids, *mixtures,
    )
    if packed:
        third_d = after(third_d, second_sum)
        set_inner = [third_c, third_d, swap(third_c, 1, 32), swap(third_d, 1, 32)]
    out_own, out_send, back2_in, sums_inner, *grads_inner = run(
        make_inner(packed, rows, block, width, hidden, narrow, len(set_inner)), 18.0, "inner",
        *set_inner, second_sum, kept, came, vectors,
    )
    out_came = swap(out_send, parts, devices)
    found = run(
        make_cross_back(packed, parts, share, memory_share, width, narrow, len(set_back)), 14.0,
        "cross_back", *set_back, back2_in, first_sum, second_sum, cross_query, memory_keys,
        memory_values, cross_t, cross_logs, ids, memory_ids, vectors, sums_inner, *mixtures,
    )
    back1, memory_key_own, memory_value_own, sums_cross = found[:4]
    slope, slope_t, deltas = (found[4 + 2 * i : 6 + 2 * i] for i in range(3))
    memory_received = [swap(a, m + 1, devices) for m, a in enumerate(found[10 : 10 + parts - 1])]
    grads_early = found[10 + parts - 1 :]
    query = list(query)
    if packed:
        keep, send = combine(after([grads_inner[0], swap(grads_inner[1], 1, 32)], back1, out_came), 2)
        inner_step = [keep, turned_swap(send, 3)]
        memory_key_own = after(memory_key_own, keep)
    memory_own, memory_send, *grads_cross = run(
        make_memory_back(packed, parts, rows, block, memory_block, width, narrow, len(set_memory)),
        2.0, "memory_back", *set_memory, *own_tokens, memory_key_own, memory_value_own, sums_cross,
        *grads_early, *memory_received,
    )
    if packed:
        cross_came = swap(grads_cross[1], 1, 32)
        query[0] = after(query[0], grads_cross[0])
    found = run(
        make_self_back_upper(parts, share, width), 7.0, "self_back_upper", query[0], keys[0],
        values[0], slope[0], slope_t[0], logs[0], deltas[0], ids,
    )
    query_upper, own_upper = found[:2]
    received_upper = [swap(a, m // 2 + 1, devices) for m, a in enumerate(found[2:])]
    if packed:
        keep_cross, send = combine(after([grads_cross[0], cross_came], query_upper), 2)
        cross_step = [keep_cross, turned_swap(send, 3, CROSSED)]
        query[1] = after(query[1], keep_cross)
    in_part, query_sum, query_w_grad, own_lower, *sends = run(
        make_self_back_lower(packed, parts, rows, block, width, narrow, len(set_query)), 11.0,
        "self_back_lower", *set_query, *own_tokens, query[1], keys[1], values[1], slope[1],
        slope_t[1], logs[1], deltas[1], ids, back1, query_upper,
    )
    received_lower = [swap(a, m // 2 + 1, devices) for m, a in enumerate(sends)]
    if packed:
        keep, send = combine(after(inner_step, query_sum), 2)
        inner_step = [keep, turned_swap(send, 2)]
        keep_cross, send = combine(after(cross_step, query_sum), 2)
        cross_step = [keep_cross, turned_swap(send, 2, CROSSED)]
        in_part = after(in_part, keep, keep_cross)
    in_own, in_send, *grads_last = run(
        make_last(packed, parts, rows, block, memory_block, width, narrow, len(set_last)), 6.0,
        "last", *set_last, *own_tokens, in_part, query_sum, query_w_grad, memory_send, own_upper,
        own_lower, *received_upper, *received_lower,
    )

    if packed:
        keep, send = combine([grads_last[0], swap(grads_last[1], 1, 32)], 2)
        last_step = [keep, turned_swap(send, 3)]
        in_send = after(in_send, last_step[1])
        keep_joint, send = combine_joint(after([inner_step, cross_step], in_own), 2)
        joint_step = [keep_joint, turned_swap(send, 1)]
        keep, send = combine(after(last_step, keep_joint), 2)
        last_step = [keep, turned_swap(send, 2)]
        keep_joint, send = combine(joint_step, 2)
        joint_step = [keep_joint, turned_swap(send, 0)]
        keep, send = combine(after(last_step, keep_joint), 2)
        last_step = [keep, turned_swap(send, 1)]
        keep, send = combine(last_step, 2)
        last_step = [keep, turned_swap(send, 0)]

        def plan(me_ref, *refs):
            me = me_ref[0]
            joint, last = (sum(r[0].astype(F32) for r in given) for given in (refs[:2], refs[2:4]))
            outs = refs[4:]
            inner, cross = joint[: 2 * blocks * narrow, :], joint[2 * blocks * narrow :, :]
            for i in range(blocks):
                outs[0][:, i * width : (i + 1) * width] = inner[i * narrow : (i + 1) * narrow, :]
            outs[1][...] = inner[blocks * narrow :, :]
            for i in range(5):
                outs[2 + i][...] = cross[i * narrow : (i + 1) * narrow, :]
            for i in range(3):
                outs[7 + i][...] = last[i * narrow : (i + 1) * narrow, :]
            rows_in = jnp.concatenate([cross[5 * narrow :, :], last[3 * narrow :, :]], axis=0)
            outs[10][...] = chosen(me, rows_in, narrow)
            per = width // wide
            line = lax.broadcasted_iota(jnp.int32, (blocks, width), 0)
            row = jnp.sum(jnp.where(line == lax.div(me, per), rows_in[3 : 3 + blocks, :], 0.0), axis=0, keepdims=True)
            outs[11][...] = chosen(lax.rem(me, per), row, wide)

        part = (narrow, width)
        shapes = [(narrow, hidden), (wide, width)] + [part] * 8 + [(24, narrow), (1, wide)]
        (inner_share, outer_share, source_key_share, source_value_share, source_output_share,
         source_query_share, output_share, key_share, value_share, query_share, sums,
         inner_bias_share) = call(
            plan, [(s, F32) for s in shapes], (me_array, *joint_step, *last_step), [], 2.0,
            "finish",
        )
        inner_bias_share = inner_bias_share.reshape(wide)
    else:
        def scatter(array):
            return lax.psum_scatter(array, AXES, scatter_dimension=0, tiled=True)

        inner_share = scatter(grads_inner[0].transpose(1, 0, 2).reshape(width, hidden))
        outer_share = scatter(grads_inner[1].reshape(hidden, width))
        source_output_share, source_query_share, output_share = (scatter(g.astype(F32)) for g in grads_early)
        source_key_share, source_value_share = (scatter(g) for g in grads_cross[:2])
        key_share, value_share = (scatter(g) for g in grads_last[:2])
        query_share = scatter(query_w_grad)
        sums = reduce_all(jnp.concatenate([grads_cross[2], grads_last[2]], axis=0), devices)
        inner_bias_share = lax.dynamic_slice(sums[3 : 3 + blocks].reshape(hidden), (me * wide,), (wide,))
        sums = lax.dynamic_slice(sums, (0, me * narrow), (sums.shape[0], narrow))
    def regroup(mine, came):
        came = came.astype(F32)
        return jnp.where(turn == 0, jnp.stack([mine, came]), jnp.stack([came, mine]))

    output = regroup(out_own, out_came)
    in_came = swap(in_send, parts, devices)
    input_gradient = regroup(in_own, in_came[:block])
    memory_gradient = regroup(memory_own, in_came[block:])

    return (
        output,
        input_gradient,
        memory_gradient,
        query_share,
        key_share,
        value_share,
        output_share,
        sums[16],
        sums[17],
        sums[13],
        sums[11],
        sums[12],
        source_query_share,
        source_key_share,
        source_value_share,
        source_output_share,
        sums[10],
        sums[14],
        sums[9],
        sums[7],
        sums[8],
        inner_share,
        inner_bias_share,
        outer_share,
        sums[2],
        sums[0],
        sums[1],
    )


def solution(mesh):
    sequence, devices = mesh.shape["seq"], mesh.size
    tokens, ids = P("dp", "seq", None), P("dp", "seq")
    matrix, vector = P(AXES, None), P(AXES)
    attention = (matrix,) * 4 + (vector,) * 5
    inner = (matrix, vector, matrix, vector, vector, vector)
    return jax.shard_map(
        functools.partial(per_device, devices=devices, sequence=sequence),
        mesh=mesh,
        in_specs=(tokens, tokens, ids, ids, tokens) + attention + attention + inner,
        out_specs=(tokens, tokens, tokens) + attention + attention + inner,
        check_vma=False,
    )
```

```python
import functools
import math

import jax
import jax.numpy as jnp
from jax import lax
from jax.experimental import pallas as pl
from jax.experimental.pallas import tpu as pltpu
from jax.sharding import PartitionSpec as P

HEADS = 8
HEAD_DIM = 64
PAIR = 128
EPSILON = 1e-05
MASKED = 1e9
AXES = ("dp", "seq")
F32 = jnp.float32
BF16 = jnp.bfloat16

(
    OUTPUT_BIAS,
    ATTENTION_GAIN,
    ATTENTION_SHIFT,
    SOURCE_QUERY_BIAS,
    SOURCE_VALUE_BIAS,
    SOURCE_OUTPUT_BIAS,
    SOURCE_GAIN,
    SOURCE_SHIFT,
    OUTER_BIAS,
    FINAL_GAIN,
    FINAL_SHIFT,
    INNER_BIAS,
) = range(12)
Z_MASKS = (0, 8, 16, 24)
VM = pl.BlockSpec(memory_space=pltpu.VMEM)
SM = pl.BlockSpec(memory_space=pltpu.SMEM)


def dot(a, b):
    return lax.dot_general(a, b, (((1,), (0,)), ((), ())), preferred_element_type=F32)


def dot_nt(a, b):
    return lax.dot_general(a, b, (((1,), (1,)), ((), ())), preferred_element_type=F32)


def dot_tn(a, b):
    return lax.dot_general(a, b, (((0,), (0,)), ((), ())), preferred_element_type=F32)


def total(values):
    return jnp.sum(values.astype(F32), axis=0, keepdims=True)


def normalize(h):
    average = jnp.mean(h, axis=-1, keepdims=True)
    centered = h - average
    variance = jnp.mean(centered * centered, axis=-1, keepdims=True)
    inverse = lax.rsqrt(variance + EPSILON)
    return centered * inverse, inverse


def normalize_back(upstream, normed, inverse, gain):
    scaled = upstream * gain
    first_mean = jnp.mean(scaled, axis=-1, keepdims=True)
    second_mean = jnp.mean(scaled * normed, axis=-1, keepdims=True)
    return inverse * (scaled - first_mean - normed * second_mean)


def normal_parts(v):
    density = 0.3989422804014327 * jnp.exp(-0.5 * v * v)
    t = 1.0 / (1.0 + 0.2316419 * jnp.abs(v))
    series = t * (
        0.319381530
        + t * (-0.356563782 + t * (1.781477937 + t * (-1.821255978 + t * 1.330274429)))
    )
    tail = density * series
    return jnp.where(v >= 0.0, 1.0 - tail, tail), density


def penalties(ids):
    place = lax.broadcasted_iota(jnp.int32, (PAIR, ids.shape[1]), 0)
    return jnp.where((place == ids) | (place >= 4), 0.0, -MASKED).astype(BF16)


def one_hot(ids):
    place = lax.broadcasted_iota(jnp.int32, (PAIR, ids.shape[1]), 0)
    return jnp.where(place == ids, 1.0, 0.0).astype(F32).T.astype(BF16)


def spread(part, half):
    empty = jnp.zeros_like(part)
    return [part, empty] if half == 0 else [empty, part]


def attend(query_t, keys, value_t, hot, penalty, mixture_t, logs):
    length = keys.shape[0]

    def pair(p, carry):
        columns = pl.ds(pl.multiple_of(p * PAIR, PAIR), PAIR)
        left = jnp.concatenate([keys[:, columns], hot[...]], axis=1)
        for half in range(2):
            rows = pl.ds(pl.multiple_of(p * PAIR + half * HEAD_DIM, HEAD_DIM), HEAD_DIM)
            right = jnp.concatenate(spread(query_t[rows, :], half) + [penalty[...]], axis=0)
            scores = dot(left, right)
            highest = jnp.max(scores, axis=0, keepdims=True)
            weights = jnp.exp(scores - highest).astype(BF16)
            values = jnp.concatenate(
                [value_t[rows, :], jnp.ones((16, length), BF16)], axis=0
            )
            found = dot(values, weights)
            denominator = found[HEAD_DIM : HEAD_DIM + 1, :]
            mixture_t[rows, :] = (found[:HEAD_DIM, :] / denominator).astype(BF16)
            logs[2 * p + half] = highest + jnp.log(denominator)
        return carry

    lax.fori_loop(0, keys.shape[1] // PAIR, pair, 0)


def attend_back(
    query_t, query, keys, key_t, values, slope_t, slope, hot, penalty, logs, deltas,
    query_grad_t, key_grad, value_grad,
):
    tokens = query.shape[0]
    lane = lax.broadcasted_iota(jnp.int32, (tokens, PAIR), 1)

    def pair(p, carry):
        columns = pl.ds(pl.multiple_of(p * PAIR, PAIR), PAIR)
        left = jnp.concatenate([keys[:, columns], hot[...]], axis=1)
        value_pair = values[:, columns]
        key_sum, value_sum = None, None
        for half in range(2):
            rows = pl.ds(pl.multiple_of(p * PAIR + half * HEAD_DIM, HEAD_DIM), HEAD_DIM)
            right = jnp.concatenate(spread(query_t[rows, :], half) + [penalty[...]], axis=0)
            chances = jnp.exp(dot(left, right) - logs[2 * p + half])
            slopes = dot(value_pair, jnp.concatenate(spread(slope_t[rows, :], half), axis=0))
            grads = (chances * (slopes - deltas[2 * p + half])).astype(BF16)
            query_grad_t[rows, :] = dot(key_t[rows, :], grads) * HEAD_DIM**-0.5
            mine = (lane < HEAD_DIM) if half == 0 else (lane >= HEAD_DIM)
            none = jnp.zeros((tokens, PAIR), BF16)
            value_part = dot(chances.astype(BF16), jnp.where(mine, slope[:, columns], none))
            key_part = dot(grads, jnp.where(mine, query[:, columns], none))
            value_sum = value_part if value_sum is None else value_sum + value_part
            key_sum = key_part if key_sum is None else key_sum + key_part
        key_grad[:, columns] = key_sum
        value_grad[:, columns] = value_sum
        return carry

    lax.fori_loop(0, keys.shape[1] // PAIR, pair, 0)


def deltas_of(slope_t, mixture_t, deltas):
    for head in range(slope_t.shape[0] // HEAD_DIM):
        rows = slice(head * HEAD_DIM, (head + 1) * HEAD_DIM)
        deltas[head] = jnp.sum(
            slope_t[rows, :].astype(F32) * mixture_t[rows, :].astype(F32), axis=0, keepdims=True
        )


def swap(array, mask, devices):
    return lax.ppermute(array, AXES, [(i, i ^ mask) for i in range(devices)])


Z_FIRST = ((8, 24, 2, 4), (24, 8, 4, 2))
CROSSED = ((8, 24, 4, 2), (24, 8, 2, 4))


def turned_swap(array, step, orders=Z_FIRST):
    return lax.ppermute(array, AXES, [(i, i ^ orders[i % 2][step]) for i in range(32)])


def after(value, *others):
    return lax.optimization_barrier((value, others))[0]


def places(me, orders=Z_FIRST):
    found = []
    for core in range(2):
        even = ((me & 1) ^ core) == 0
        masks = [jnp.where(even, first, second) for first, second in zip(*orders)]
        for far in range(2):
            for slot in range(8):
                device = me ^ core if core else me
                for step, bit in enumerate((slot & 1, slot & 2, slot & 4, far)):
                    if bit:
                        device = device ^ masks[step]
                found.append((core, far, slot, device))
    return found


def unpack(me, pieces, stride, first, rows, scratch, orders=Z_FIRST):
    for core, far, slot, device in places(me, orders):
        ref = pieces[2 * core + far]
        at = slot * stride + first
        scratch[pl.ds(pl.multiple_of(device * rows, rows), rows), :] = ref[at : at + rows, :]


def vector_sum(pieces, stride, first):
    found = None
    for ref in pieces:
        for slot in range(8):
            part = ref[slot * stride + first : (slot + 1) * stride, :].astype(F32)
            found = part if found is None else found + part
    return found


class Grads:
    def __init__(self, me, refs, dense, rows, orders=Z_FIRST):
        self.me, self.refs, self.dense, self.rows, self.orders = me, refs, dense, rows, orders

    def put(self, index, grad):
        if self.dense is None:
            self.refs[index][...] = grad
            return
        self.dense[...] = grad
        rows = self.rows
        for core, far, slot, device in places(self.me, self.orders):
            found = self.dense[pl.ds(pl.multiple_of(device * rows, rows), rows), :]
            self.refs[core][far * 8 + slot, index * rows : (index + 1) * rows, :] = found.astype(BF16)

    def put_sums(self, first, sums):
        if self.dense is None:
            self.refs[-1][...] = sums
            return
        low = sums.astype(BF16)
        for ref in self.refs:
            for slot in range(16):
                ref[slot, first : first + sums.shape[0], :] = low


def grad_outs(packed, count, rows, width, sums):
    if packed:
        return [((16, count * rows + sums, width), BF16)] * 2
    return [((width, width), F32)] * count + [((sums, width), F32)]


COSTS = {}


def padded(shape, dtype):
    last = -(-shape[-1] // 128) * 128
    tall = -(-shape[-2] // 16) * 16 if len(shape) > 1 else 16
    return math.prod(shape[:-2]) * tall * last * jnp.dtype(dtype).itemsize


def snug(arrays):
    return 2 * sum(padded(a.shape, a.dtype) for a in arrays) + (3 << 20)


def call(kernel, outs, args, scratch, micros, name, room=10):
    moved = sum(math.prod(a.shape) * a.dtype.itemsize for a in args[1:])
    moved += sum(math.prod(s) * jnp.dtype(d).itemsize for s, d in outs)
    need = sum(padded(a.shape, a.dtype) for a in args[1:])
    need += sum(padded(s, d) for s, d in list(outs) + list(scratch))
    return pl.pallas_call(
        kernel,
        out_shape=[jax.ShapeDtypeStruct(s, d) for s, d in outs],
        in_specs=[SM] + [VM] * (len(args) - 1),
        out_specs=[VM] * len(outs),
        scratch_shapes=[pltpu.VMEM(s, d) for s, d in scratch],
        compiler_params=pltpu.CompilerParams(vmem_limit_bytes=min(need + (room << 20), 58 << 20)),
        cost_estimate=pl.CostEstimate(
            flops=int(COSTS.get(name, 0) * 1.15e9) + 1, bytes_accessed=1, transcendentals=0
        ),
        name=name,
    )(*args)


def tokens_packet(turn, tokens, memory, target_ids, source_ids, cotangent):
    block, width = tokens.shape[1:]
    memory_block = memory.shape[1]
    first = block + memory_block + 8

    def kernel(turn_ref, targets, sources, tokens_ref, memory_ref, cot_ref, sent, kept):
        mine = turn_ref[0]
        for row, out in ((1 - mine, sent), (mine, kept)):
            out[:block, :] = tokens_ref[row]
            out[block : block + memory_block, :] = memory_ref[row]
            ids = targets[pl.ds(row, 1), :].astype(F32)
            ids = jnp.concatenate([ids, jnp.zeros((1, width - block), F32)], axis=1)
            others = sources[pl.ds(row, 1), :].astype(F32)
            others = jnp.concatenate([others, jnp.zeros((1, width - memory_block), F32)], axis=1)
            place = lax.broadcasted_iota(jnp.int32, (8, width), 0)
            found = jnp.where(place == 0, ids, jnp.where(place == 1, others, 0.0))
            out[block + memory_block : first, :] = found.astype(BF16)
            out[first:, :] = cot_ref[row]

    shape = (first + block, width)
    return call(kernel, [(shape, BF16)] * 2, (turn, target_ids, source_ids, tokens, memory, cotangent),
                [], 1.0, "tokens_packet", 58)


def placed(me, parts, width):
    here = lax.broadcasted_iota(jnp.int32, (parts.shape[1], width), 0) + me * parts.shape[1]
    lane = lax.broadcasted_iota(jnp.int32, (parts.shape[1], width), 1)
    return dot(parts, jnp.where(lane == here, 1.0, 0.0).astype(BF16))


def make_weights_packet(narrow, width, blocks):
    tall = blocks * narrow

    def kernel(me_ref, *refs):
        weights, inner, outer, wide, short = refs[:8], refs[8], refs[9], refs[10], refs[11:24]
        first, second, third = refs[24:]
        me = me_ref[0]
        for i, ref in enumerate(weights):
            if i < 3:
                first[i * narrow : (i + 1) * narrow, :] = ref[...]
            else:
                second[(i - 3) * narrow : (i - 2) * narrow, :] = ref[...]
        short = jnp.concatenate([ref[...].astype(F32) for ref in short], axis=0).astype(BF16)
        found = placed(me, short, width)
        first[3 * narrow :, :] = jnp.concatenate([found[:2, :], jnp.zeros((6, width), F32)], axis=0).astype(BF16)
        per = width // wide.shape[1]
        row = placed(lax.rem(me, per), wide[...], width)
        place = lax.broadcasted_iota(jnp.int32, (blocks, width), 0)
        spread_row = jnp.where(place == lax.div(me, per), row, 0.0)
        none = jnp.zeros((16 - (found.shape[0] - 2) - blocks, width), F32)
        second[5 * narrow :, :] = jnp.concatenate([found[2:, :], spread_row, none], axis=0).astype(BF16)
        for i in range(blocks):
            third[i * narrow : (i + 1) * narrow, :] = inner[:, i * width : (i + 1) * width]
        third[tall:, :] = outer[...]

    return kernel, [((rows, width), BF16) for rows in (3 * narrow + 8, 5 * narrow + 16, 2 * tall)]


def join(arrays):
    def kernel(*refs):
        at = 0
        for ref in refs[:-1]:
            refs[-1][at : at + ref.shape[0], :] = ref[...]
            at += ref.shape[0]

    rows = sum(a.shape[0] for a in arrays)
    return pl.pallas_call(
        kernel,
        out_shape=jax.ShapeDtypeStruct((rows, arrays[0].shape[1]), arrays[0].dtype),
        in_specs=[VM] * len(arrays),
        out_specs=VM,
        compiler_params=pltpu.CompilerParams(vmem_limit_bytes=snug(arrays)),
        cost_estimate=pl.CostEstimate(flops=1 << 20, bytes_accessed=0, transcendentals=0),
        name="join",
    )(*arrays)


def make_project(packed, parts, rows, block, memory_block, width, narrow, n_pieces):
    share = rows * block
    length = parts * share
    memory_share = rows * memory_block
    stride = 3 * narrow + 8
    half = width // 2

    def kernel(*refs):
        me_ref, refs = refs[0], list(refs[1:])
        pieces, refs = refs[:n_pieces], refs[n_pieces:]
        tokens, refs = refs[: parts * rows], refs[parts * rows :]
        query, query_t, keys, values, value_t = (refs[2 * i : 2 * i + 2] for i in range(5))
        memory, ids, memory_ids = refs[10:13]
        scratch = refs[13:]
        me = me_ref[0]
        if packed:
            for i in range(3):
                unpack(me, pieces, stride, i * narrow, narrow, scratch[i])
            query_w, key_w, value_w = scratch
            biases = vector_sum(pieces, stride, 3 * narrow)
        else:
            query_w, key_w, value_w = pieces[:3]
            biases = pieces[3][...]
        for i in range(parts):
            here = slice(i * share, (i + 1) * share)
            some = tokens[i * rows : (i + 1) * rows]
            own = jnp.concatenate([t[:block, :] for t in some], axis=0)
            if i == 0:
                scaled = (dot(own, query_w[...]) + biases[0:1, :]).astype(BF16) * BF16(HEAD_DIM**-0.5)
            key = dot(own, key_w[...]).astype(BF16)
            found = (dot(own, value_w[...]) + biases[1:2, :]).astype(BF16)
            for side in range(2):
                columns = slice(side * half, (side + 1) * half)
                if i == 0:
                    query[side][...] = scaled[:, columns]
                    query_t[side][...] = scaled[:, columns].T
                keys[side][here, :] = key[:, columns]
                values[side][here, :] = found[:, columns]
                value_t[side][:, here] = found[:, columns].T
        for i, t in enumerate(tokens):
            memory[i * memory_block : (i + 1) * memory_block, :] = t[block : block + memory_block, :]
            found = t[block + memory_block : block + memory_block + 8, :].astype(F32).astype(jnp.int32)
            ids[:, i * block : (i + 1) * block] = found[0:1, :block]
        found = [t[block + memory_block : block + memory_block + 8, :].astype(F32).astype(jnp.int32)[1:2, :memory_block] for t in tokens]
        memory_ids[...] = jnp.concatenate(found, axis=1)

    outs = [((share, half), BF16)] * 2 + [((half, share), BF16)] * 2
    outs += [((length, half), BF16)] * 4 + [((half, length), BF16)] * 2
    outs += [
        ((parts * memory_share, width), BF16),
        ((1, length), jnp.int32),
        ((1, parts * memory_share), jnp.int32),
    ]
    return kernel, outs, [((width, width), BF16)] * 3 if packed else []


def make_self_attention(share, length, width):
    def kernel(me_ref, *refs):
        query_t, keys, value_t, ids = refs[:2], refs[2:4], refs[4:6], refs[6]
        mixture_t, logs, hot, penalty = refs[7:9], refs[9:11], refs[11], refs[12]
        hot[...] = one_hot(ids[...])
        penalty[...] = penalties(ids[:, :share])
        for side in range(2):
            attend(query_t[side], keys[side], value_t[side], hot, penalty, mixture_t[side], logs[side])

    outs = [((width // 2, share), BF16)] * 2 + [((HEADS // 2, 1, share), F32)] * 2
    return kernel, outs, [((length, PAIR), BF16), ((PAIR, share), BF16)]


def make_cross_forward(packed, rows, block, memory_length, width, narrow, n_pieces):
    share = rows * block
    stride = 5 * narrow + 16

    def kernel(*refs):
        me_ref, refs = refs[0], list(refs[1:])
        pieces, refs = refs[:n_pieces], refs[n_pieces:]
        tokens, refs = refs[:rows], refs[rows:]
        memory, ids, memory_ids, upper, lower = refs[:5]
        first_sum, second_sum, query, memory_keys, memory_values, cross_t, logs, vectors = refs[5:13]
        scratch = refs[13:]
        query_t, value_t, hot, penalty = scratch[:4]
        if packed:
            for i in range(5):
                unpack(me_ref[0], pieces, stride, i * narrow, narrow, scratch[4 + i])
            output_w, query_w, key_w, value_w, source_w = scratch[4:]
            vectors[...] = vector_sum(pieces, stride, 5 * narrow)
        else:
            output_w, query_w, key_w, value_w, source_w = pieces[:5]
            vectors[...] = pieces[5][...]

        def vector(i):
            return vectors[i : i + 1, :]

        own = jnp.concatenate([t[:block, :] for t in tokens], axis=0)
        mixture_t = jnp.concatenate([upper[...], lower[...]], axis=0)
        h = own.astype(F32) + dot_tn(mixture_t, output_w[...]) + vector(OUTPUT_BIAS)
        first_sum[...] = h
        first = normalize(h)[0] * vector(ATTENTION_GAIN) + vector(ATTENTION_SHIFT)
        scaled = (dot(first.astype(BF16), query_w[...]) + vector(SOURCE_QUERY_BIAS)).astype(BF16) * BF16(HEAD_DIM**-0.5)
        query[...] = scaled
        query_t[...] = scaled.T
        memory_keys[...] = dot(memory[...], key_w[...]).astype(BF16)
        memory_values[...] = (dot(memory[...], value_w[...]) + vector(SOURCE_VALUE_BIAS)).astype(BF16)
        value_t[...] = memory_values[...].T
        hot[...] = one_hot(memory_ids[...])
        penalty[...] = penalties(ids[:, :share])
        attend(query_t, memory_keys, value_t, hot, penalty, cross_t, logs)
        first = normalize(first_sum[...])[0] * vector(ATTENTION_GAIN) + vector(ATTENTION_SHIFT)
        second_sum[...] = first + dot_tn(cross_t[...], source_w[...]) + vector(SOURCE_OUTPUT_BIAS)

    outs = [
        ((share, width), F32),
        ((share, width), F32),
        ((share, width), BF16),
        ((memory_length, width), BF16),
        ((memory_length, width), BF16),
        ((width, share), BF16),
        ((HEADS, 1, share), F32),
        ((16, width), F32),
    ]
    scratch = [((width, share), BF16), ((width, memory_length), BF16), ((memory_length, PAIR), BF16), ((PAIR, share), BF16)]
    if packed:
        scratch += [((width, width), BF16)] * 5
    return kernel, outs, scratch


def make_inner(packed, rows, block, width, hidden, narrow, n_pieces):
    blocks = hidden // width
    share = rows * block
    per = width // (blocks * narrow)

    def kernel(*refs):
        me_ref, refs = refs[0], list(refs[1:])
        pieces, refs = refs[:n_pieces], refs[n_pieces:]
        second_sum, cot_own, cot_came, vectors = refs[:4]
        out_own, out_send, back, sums = refs[4:8]
        grads, scratch = refs[8:10], refs[10:]
        low, active, gate, slope = scratch[:4]
        if packed:
            inner_w, outer_w, gathered, dense = scratch[4:8]
            tall = blocks * narrow
            for core, far, slot, device in places(me_ref[0]):
                ref, at = pieces[2 * core + far], slot * 2 * tall
                row = pl.multiple_of(device * narrow, narrow)
                for i in range(blocks):
                    inner_w[i, pl.ds(row, narrow), :] = ref[at + i * narrow : at + (i + 1) * narrow, :]
                row = pl.multiple_of(lax.rem(device, per) * tall, tall)
                outer_w[lax.div(device, per), pl.ds(row, tall), :] = ref[at + tall : at + 2 * tall, :]
        else:
            inner_w, outer_w = pieces

        def vector(i):
            return vectors[i : i + 1, :]

        second = normalize(second_sum[...])[0] * vector(SOURCE_GAIN) + vector(SOURCE_SHIFT)
        low[...] = second.astype(BF16)
        back[...] = second + vector(OUTER_BIAS)

        def forward(i, carry):
            inner = dot(low[...], inner_w[i]) + vectors[pl.ds(INNER_BIAS + i, 1), :]
            chance, density = normal_parts(inner)
            found = (inner * chance).astype(BF16)
            active[i] = found
            gate[i] = chance + inner * density
            back[...] += dot(found, outer_w[i])
            return carry

        lax.fori_loop(0, blocks, forward, 0)
        normed, inverse = normalize(back[...])
        final = normed * vector(FINAL_GAIN) + vector(FINAL_SHIFT)
        out_own[...] = final[:block, :]
        out_send[...] = final[block:, :].astype(BF16)
        upstream = jnp.concatenate([cot_own[-block:, :], cot_came[-block:, :]], axis=0).astype(F32)
        sums[0:1, :] = total(upstream * normed)
        sums[1:2, :] = total(upstream)
        back3 = normalize_back(upstream, normed, inverse, vector(FINAL_GAIN))
        slope[...] = back3.astype(BF16)
        sums[2:3, :] = total(slope[...])
        sums[7:8, :] = jnp.zeros_like(sums[7:8, :])
        back[...] = back3

        def backward(i, carry):
            grad = dot_nt(slope[...], outer_w[i]) * gate[i]
            inner_low = grad.astype(BF16)
            sums[pl.ds(3 + i, 1), :] = total(inner_low)
            outer_grad = dot_tn(active[i], slope[...])
            inner_grad = dot_tn(low[...], inner_low)
            back[...] += dot_nt(inner_low, inner_w[i])
            if packed:
                dense[...] = inner_grad
                gathered[i] = outer_grad.astype(BF16)
                here = pl.ds(pl.multiple_of(i * narrow, narrow), narrow)
                for core, far, slot, device in places(me_ref[0]):
                    row = pl.multiple_of(device * narrow, narrow)
                    grads[core][far * 8 + slot, here, :] = dense[pl.ds(row, narrow), :].astype(BF16)
            else:
                grads[0][i] = inner_grad
                grads[1][i] = outer_grad
            return carry

        lax.fori_loop(0, blocks, backward, 0)
        if packed:
            tall = blocks * narrow
            for core, far, slot, device in places(me_ref[0]):
                row = pl.multiple_of(lax.rem(device, per) * tall, tall)
                grads[core][far * 8 + slot, tall:, :] = gathered[lax.div(device, per), pl.ds(row, tall), :]

    outs = [((block, width), F32), ((block, width), BF16), ((share, width), F32), ((8, width), F32)]
    if packed:
        outs += [((16, 2 * blocks * narrow, width), BF16)] * 2
    else:
        outs += [((blocks, width, width), F32)] * 2
    scratch = [((share, width), BF16), ((blocks, share, width), BF16), ((blocks, share, width), F32), ((share, width), BF16)]
    if packed:
        scratch += [((blocks, width, width), BF16)] * 3 + [((width, width), F32)]
    return kernel, outs, scratch


def make_cross_back(packed, parts, share, memory_share, width, narrow, n_pieces):
    memory_length = parts * memory_share
    stride = 5 * narrow + 16

    def kernel(*refs):
        me_ref, refs = refs[0], list(refs[1:])
        pieces, refs = refs[:n_pieces], refs[n_pieces:]
        (back2_in, first_sum, second_sum, query, memory_keys, memory_values, cross_t, logs, ids,
         memory_ids, vectors, sums_inner) = refs[:12]
        mixtures, refs = refs[12:14], refs[14:]
        back1, key_own, value_own, sums = refs[:4]
        self_slope, self_slope_t, self_deltas = (refs[4 + 2 * i : 6 + 2 * i] for i in range(3))
        sends, refs = refs[10 : 10 + parts - 1], refs[10 + parts - 1 :]
        grads, scratch = refs[:3], refs[3:]
        (slope_t, slope, key_t, hot, penalty, query_t, deltas, query_grad_t, key_grad, value_grad) = scratch[:10]
        upper, lower = mixtures
        if packed:
            for i, at in enumerate((0, 1, 4)):
                unpack(me_ref[0], pieces, stride, at * narrow, narrow, scratch[10 + i])
            output_w, query_w, source_w = scratch[10:13]
        else:
            output_w, query_w, source_w = pieces

        def vector(i):
            return vectors[i : i + 1, :]

        sums[0:7, :] = sums_inner[0:7, :]
        upstream = back2_in[...]
        normed, inverse = normalize(second_sum[...])
        sums[7:8, :] = total(upstream * normed)
        sums[8:9, :] = total(upstream)
        back2 = normalize_back(upstream, normed, inverse, vector(SOURCE_GAIN))
        back1[...] = back2
        cross_low = back2.astype(BF16)
        sums[9:10, :] = total(cross_low)
        grads[0][...] = dot(cross_t[...], cross_low).astype(BF16)
        found = dot_nt(cross_low, source_w[...]).astype(BF16)
        slope[...] = found
        slope_t[...] = found.T
        deltas_of(slope_t, cross_t, deltas)
        query_t[...] = query[...].T
        key_t[...] = memory_keys[...].T
        hot[...] = one_hot(memory_ids[...])
        penalty[...] = penalties(ids[:, :share])
        attend_back(query_t, query, memory_keys, key_t, memory_values, slope_t, slope, hot, penalty,
                    logs, deltas, query_grad_t, key_grad, value_grad)
        key_own[...] = key_grad[:memory_share, :]
        value_own[...] = value_grad[:memory_share, :]
        for i in range(1, parts):
            here = slice(i * memory_share, (i + 1) * memory_share)
            sends[i - 1][:memory_share, :] = key_grad[here, :].astype(BF16)
            sends[i - 1][memory_share:, :] = value_grad[here, :].astype(BF16)
        query_low = query_grad_t[...].T.astype(BF16)
        sums[10:11, :] = total(query_low)
        normed, inverse = normalize(first_sum[...])
        first_low = (normed * vector(ATTENTION_GAIN) + vector(ATTENTION_SHIFT)).astype(BF16)
        grads[1][...] = dot_tn(first_low, query_low).astype(BF16)
        upstream = back1[...] + dot_nt(query_low, query_w[...])
        sums[11:12, :] = total(upstream * normed)
        sums[12:13, :] = total(upstream)
        grad = normalize_back(upstream, normed, inverse, vector(ATTENTION_GAIN))
        back1[...] = grad
        branch_low = grad.astype(BF16)
        sums[13:14, :] = total(branch_low)
        sums[14:16, :] = jnp.zeros_like(sums[14:16, :])
        mixture_t = jnp.concatenate([upper[...], lower[...]], axis=0)
        grads[2][...] = dot(mixture_t, branch_low).astype(BF16)
        found = dot_nt(branch_low, output_w[...]).astype(BF16)
        for side in range(2):
            columns = slice(side * width // 2, (side + 1) * width // 2)
            self_slope[side][...] = found[:, columns]
            self_slope_t[side][...] = found[:, columns].T
            deltas_of(self_slope_t[side], mixtures[side], self_deltas[side])

    half = width // 2
    outs = [
        ((share, width), F32),
        ((memory_share, width), F32),
        ((memory_share, width), F32),
        ((16, width), F32),
    ]
    outs += [((share, half), BF16)] * 2 + [((half, share), BF16)] * 2
    outs += [((HEADS // 2, 1, share), F32)] * 2
    outs += [((2 * memory_share, width), BF16)] * (parts - 1)
    outs += [((width, width), BF16)] * 3
    scratch = [
        ((width, share), BF16),
        ((share, width), BF16),
        ((width, memory_length), BF16),
        ((memory_length, PAIR), BF16),
        ((PAIR, share), BF16),
        ((width, share), BF16),
        ((HEADS, 1, share), F32),
        ((width, share), F32),
        ((memory_length, width), F32),
        ((memory_length, width), F32),
    ]
    if packed:
        scratch += [((width, width), BF16)] * 3
    return kernel, outs, scratch


def attention_back_half(refs, share, scratch):
    query, keys, values, slope, slope_t, logs, deltas, ids = refs
    query_t, key_t, hot, penalty, query_grad_t, key_grad, value_grad = scratch
    query_t[...] = query[...].T
    key_t[...] = keys[...].T
    hot[...] = one_hot(ids[...])
    penalty[...] = penalties(ids[:, :share])
    attend_back(query_t, query, keys, key_t, values, slope_t, slope, hot, penalty, logs, deltas,
                query_grad_t, key_grad, value_grad)


def half_scratch(share, length, half):
    return [
        ((half, share), BF16),
        ((half, length), BF16),
        ((length, PAIR), BF16),
        ((PAIR, share), BF16),
        ((half, share), F32),
        ((length, half), F32),
        ((length, half), F32),
    ]


def give_half(share, scratch, own, sends):
    key_grad, value_grad = scratch[5:7]
    own[:share, :] = key_grad[:share, :]
    own[share:, :] = value_grad[:share, :]
    for i, send in enumerate(sends):
        here = slice((i // 2 + 1) * share, (i // 2 + 2) * share)
        send[...] = (key_grad, value_grad)[i % 2][here, :].astype(BF16)


def make_memory_back(packed, parts, rows, block, memory_block, width, narrow, n_pieces):
    memory_share = rows * memory_block

    def kernel(*refs):
        me_ref, refs = refs[0], list(refs[1:])
        pieces, refs = refs[:n_pieces], refs[n_pieces:]
        tokens, refs = refs[:rows], refs[rows:]
        memory_key_own, memory_value_own, sums_in = refs[:3]
        early, refs = refs[3:6], refs[6:]
        memory_received, refs = refs[: parts - 1], refs[parts - 1 :]
        memory_own, memory_send = refs[:2]
        n_grads = 2 if packed else 3
        grad_refs, scratch = refs[2 : 2 + n_grads], refs[2 + n_grads :]
        sums = scratch[0]
        me = me_ref[0]
        if packed:
            for i in range(2):
                unpack(me, pieces, 5 * narrow + 16, (2 + i) * narrow, narrow, scratch[1 + i])
            source_key, source_value = scratch[1:3]
        else:
            source_key, source_value = pieces
        grads = Grads(me, grad_refs, scratch[3] if packed else None, narrow, CROSSED)
        memory = jnp.concatenate([t[block : block + memory_block, :] for t in tokens], axis=0)
        key_sum, value_sum = memory_key_own[...], memory_value_own[...]
        for ref in memory_received:
            key_sum = key_sum + ref[:memory_share, :].astype(F32)
            value_sum = value_sum + ref[memory_share:, :].astype(F32)
        key_low, value_low = key_sum.astype(BF16), value_sum.astype(BF16)
        sums[...] = sums_in[...]
        sums[14:15, :] = total(value_low)
        grads.put_sums(5 * narrow, sums[...])
        grads.put(0, dot_tn(memory, key_low))
        grads.put(1, dot_tn(memory, value_low))
        if packed:
            for i, ref in enumerate(early):
                grads.put(2 + i, ref[...].astype(F32))
        grad = dot_nt(key_low, source_key[...]) + dot_nt(value_low, source_value[...])
        memory_own[...] = grad[:memory_block, :]
        memory_send[...] = grad[memory_block:, :].astype(BF16)

    outs = [((memory_block, width), F32), ((memory_block, width), BF16)]
    if packed:
        outs += [((16, 5 * narrow + 16, width), BF16)] * 2
    else:
        outs += [((width, width), F32)] * 2 + [((16, width), F32)]
    scratch = [((16, width), F32)]
    if packed:
        scratch += [((width, width), BF16)] * 2 + [((width, width), F32)]
    return kernel, outs, scratch


def make_self_back_upper(parts, share, width):
    length, half = parts * share, width // 2

    def kernel(*refs):
        operands, (query_grad, own), refs = refs[1:9], refs[9:11], refs[11:]
        sends, scratch = refs[: 2 * parts - 2], refs[2 * parts - 2 :]
        attention_back_half(operands, share, scratch)
        query_grad[...] = scratch[4][...].T.astype(BF16)
        give_half(share, scratch, own, sends)

    outs = [((share, half), BF16), ((2 * share, half), F32)] + [((share, half), BF16)] * (2 * parts - 2)
    return kernel, outs, half_scratch(share, length, half)


def make_self_back_lower(packed, parts, rows, block, width, narrow, n_pieces):
    share = rows * block
    length, half = parts * share, width // 2

    def kernel(*refs):
        me_ref, refs = refs[0], list(refs[1:])
        pieces, refs = refs[:n_pieces], refs[n_pieces:]
        tokens, refs = refs[:rows], refs[rows:]
        operands, refs = refs[:8], refs[8:]
        back1, query_upper = refs[:2]
        in_part, query_sum, query_w_grad, own = refs[2:6]
        sends, scratch = refs[6 : 4 + 2 * parts], refs[4 + 2 * parts :]
        if packed:
            unpack(me_ref[0], pieces, 3 * narrow + 8, 0, narrow, scratch[7])
            query_w = scratch[7]
        else:
            (query_w,) = pieces
        attention_back_half(operands, share, scratch[:7])
        give_half(share, scratch, own, sends)
        query_low = jnp.concatenate([query_upper[...], scratch[4][...].T.astype(BF16)], axis=1)
        tokens_own = jnp.concatenate([t[:block, :] for t in tokens], axis=0)
        in_part[...] = back1[...] + dot_nt(query_low, query_w[...])
        query_sum[...] = jnp.concatenate([total(query_low), jnp.zeros((7, width), F32)], axis=0)
        query_w_grad[...] = dot_tn(tokens_own, query_low).astype(query_w_grad.dtype)

    outs = [
        ((share, width), F32),
        ((8, width), F32),
        ((width, width), BF16 if packed else F32),
        ((2 * share, half), F32),
    ]
    outs += [((share, half), BF16)] * (2 * parts - 2)
    scratch = half_scratch(share, length, half)
    if packed:
        scratch += [((width, width), BF16)]
    return kernel, outs, scratch


def make_last(packed, parts, rows, block, memory_block, width, narrow, n_pieces):
    share = rows * block

    def kernel(*refs):
        me_ref, refs = refs[0], list(refs[1:])
        pieces, refs = refs[:n_pieces], refs[n_pieces:]
        tokens, refs = refs[:rows], refs[rows:]
        in_part, query_sum, query_w_grad, memory_send = refs[:4]
        owns, refs = refs[4:6], refs[6:]
        received = [refs[: 2 * parts - 2], refs[2 * parts - 2 : 4 * parts - 4]]
        refs = refs[4 * parts - 4 :]
        in_own, in_send = refs[:2]
        n_grads = 2 if packed else 3
        grad_refs, scratch = refs[2 : 2 + n_grads], refs[2 + n_grads :]
        sums = scratch[0]
        me = me_ref[0]
        if packed:
            for i in range(2):
                unpack(me, pieces, 3 * narrow + 8, (1 + i) * narrow, narrow, scratch[1 + i])
            key_w, value_w = scratch[1:3]
        else:
            key_w, value_w = pieces
        grads = Grads(me, grad_refs, scratch[3] if packed else None, narrow)
        if packed:
            grads.put(2, query_w_grad[...].astype(F32))
        lows = []
        for own, others in zip(owns, received):
            found = own[...]
            for key, value in zip(others[::2], others[1::2]):
                found = found + jnp.concatenate([key[...], value[...]], axis=0).astype(F32)
            lows.append(found.astype(BF16))
        key_low = jnp.concatenate([low[:share, :] for low in lows], axis=1)
        value_low = jnp.concatenate([low[share:, :] for low in lows], axis=1)
        tokens_own = jnp.concatenate([t[:block, :] for t in tokens], axis=0)
        sums[...] = query_sum[...]
        sums[1:2, :] = total(value_low)
        grads.put_sums(3 * narrow, sums[...])
        grads.put(0, dot_tn(tokens_own, key_low))
        grads.put(1, dot_tn(tokens_own, value_low))
        grad = in_part[...] + dot_nt(key_low, key_w[...]) + dot_nt(value_low, value_w[...])
        in_own[...] = grad[:block, :]
        in_send[:block, :] = grad[block:, :].astype(BF16)
        in_send[block:, :] = memory_send[...]

    outs = [((block, width), F32), ((block + memory_block, width), BF16)]
    if packed:
        outs += [((16, 3 * narrow + 8, width), BF16)] * 2
    else:
        outs += [((width, width), F32)] * 2 + [((8, width), F32)]
    scratch = [((8, width), F32)]
    if packed:
        scratch += [((width, width), BF16)] * 2 + [((width, width), F32)]
    return kernel, outs, scratch


def combine(arrays, splits, micros=0.1):
    count = arrays[0].shape[0] // splits
    shape = (count,) + arrays[0].shape[1:]

    def kernel(*refs):
        given, outs = refs[: len(arrays)], refs[len(arrays) :]
        for i, out in enumerate(outs):
            here = slice(i * count, (i + 1) * count)
            found = given[0][here].astype(F32)
            for ref in given[1:]:
                found = found + ref[here].astype(F32)
            out[...] = found.astype(out.dtype)

    return pl.pallas_call(
        kernel,
        out_shape=[jax.ShapeDtypeStruct(shape, BF16)] * splits,
        in_specs=[VM] * len(arrays),
        out_specs=[VM] * splits,
        compiler_params=pltpu.CompilerParams(vmem_limit_bytes=snug(arrays)),
        cost_estimate=pl.CostEstimate(flops=int(micros * 1.15e9), bytes_accessed=0, transcendentals=0),
        name="combine",
    )(*arrays)


def combine_joint(groups, splits):
    count, sizes = groups[0][0].shape[0] // splits, [g[0].shape[1] for g in groups]
    shape = (count, sum(sizes)) + groups[0][0].shape[2:]
    flat = [a for group in groups for a in group]

    def kernel(*refs):
        outs, at, row = refs[len(flat) :], 0, 0
        for group, size in zip(groups, sizes):
            given = refs[at : at + len(group)]
            at += len(group)
            for i, out in enumerate(outs):
                here = slice(i * count, (i + 1) * count)
                found = given[0][here].astype(F32)
                for ref in given[1:]:
                    found = found + ref[here].astype(F32)
                out[:, row : row + size, :] = found.astype(BF16)
            row += size

    return pl.pallas_call(
        kernel,
        out_shape=[jax.ShapeDtypeStruct(shape, BF16)] * splits,
        in_specs=[VM] * len(flat),
        out_specs=[VM] * splits,
        compiler_params=pltpu.CompilerParams(vmem_limit_bytes=snug(flat)),
        cost_estimate=pl.CostEstimate(flops=1, bytes_accessed=1, transcendentals=0),
        name="combine_joint",
    )(*flat)


def chosen(me, rows, wide):
    width = rows.shape[1]
    line = lax.broadcasted_iota(jnp.int32, (width, wide), 0)
    here = lax.broadcasted_iota(jnp.int32, (width, wide), 1) + me * wide
    choice = jnp.where(line == here, 1.0, 0.0)
    return lax.dot_general(rows, choice, (((1,), (0,)), ((), ())), precision=lax.Precision.HIGHEST, preferred_element_type=F32)


def reduce_all(array, devices):
    mask = 1
    while mask < devices:
        array = array + swap(array, mask, devices)
        mask *= 2
    return array


def per_device(
    tokens, memory, target_ids, source_ids, cotangent,
    query_weight, key_weight, value_weight, output_weight, query_bias, value_bias, output_bias,
    attention_gain, attention_shift,
    source_query, source_key, source_value, source_output, source_query_bias, source_value_bias,
    source_output_bias, source_gain, source_shift,
    inner_weight, inner_bias, outer_weight, outer_bias, final_gain, final_shift,
    *, devices, sequence,
):
    packed = devices == 32
    rows, block, width = tokens.shape
    memory_block = memory.shape[1]
    parts = sequence // rows
    share, memory_share = rows * block, rows * memory_block
    hidden = inner_weight.shape[1]
    blocks = hidden // width
    me = lax.axis_index(AXES)
    me_array = me.reshape(1).astype(jnp.int32)
    turn = lax.rem(lax.div(me, parts), rows)
    narrow, wide = width // devices, hidden // devices

    def run(made, micros, name, *args, room=10):
        kernel, outs, *scratch = made
        return call(kernel, outs, (me_array,) + args, scratch[0] if scratch else [], micros, name, room)

    short = [query_bias, value_bias, output_bias, attention_gain, attention_shift, source_query_bias,
             source_value_bias, source_output_bias, source_gain, source_shift, outer_bias, final_gain,
             final_shift]

    def whole(array):
        return lax.all_gather(array, AXES, axis=0, tiled=True)

    sent, kept = tokens_packet(
        turn.reshape(1).astype(jnp.int32), tokens, memory, target_ids, source_ids, cotangent
    )
    came = swap(sent, parts, devices)
    row_tokens = [kept, came]
    kept_swaps = [swap(kept, m, devices) for m in range(1, parts)]
    came_swaps = [swap(came, m, devices) for m in range(1, parts)]
    for pair in zip(kept_swaps, came_swaps):
        row_tokens += pair
    own_tokens = row_tokens[:rows]

    if packed:
        first, second, third = run(make_weights_packet(narrow, width, blocks), 1.0, "weights_packet",
                          query_weight, key_weight, value_weight, output_weight, source_query,
                          source_key, source_value, source_output, inner_weight, outer_weight,
                          inner_bias.reshape(1, wide), *[v.reshape(1, narrow) for v in short], room=58)
        first = after(first, sent)
        first = join([first, turned_swap(first, 0)])
        first_b = turned_swap(first, 1)
        second = after(second, first)
        second_b = turned_swap(second, 0)
        first, second = join(after([first, first_b], second_b)), join(after([second, second_b], first_b))
        third = after(third, second)
        first_b, second_b, third_b = turned_swap(first, 2), turned_swap(second, 1), turned_swap(third, 0)
        first_c = join(after([first, first_b], second_b, third_b, came, *kept_swaps))
        second = join(after([second, second_b], first_b, third_b))
        third = join(after([third, third_b], first_b, second_b))
        first_d, second_b, third_b = turned_swap(first_c, 3), turned_swap(second, 2), turned_swap(third, 1)
        second_c = join(after([second, second_b], first_d, third_b))
        third = join(after([third, third_b], first_d, second_b))
        first_d = after(first_d, second_c, third, *came_swaps)
        second_d, third_b = turned_swap(second_c, 3), turned_swap(third, 2)
        set_self = [first_c, first_d, swap(first_c, 1, 32), swap(first_d, 1, 32)]
    else:
        full = [whole(w) for w in (query_weight, key_weight, value_weight, output_weight, source_query, source_key, source_value, source_output)]
        lane = lax.broadcasted_iota(jnp.int32, (1, width), 1)
        place = lax.broadcasted_iota(jnp.int32, (blocks, width), 0) * width + lane
        spread_wide = jnp.where(place // wide == me, jnp.tile(inner_bias.reshape(1, wide), (blocks, width // wide)), 0)

        def natural(rows):
            return jnp.where(lane // narrow == me, jnp.tile(rows, (1, devices)), 0)

        vectors = jnp.concatenate([natural(jnp.stack(short[:2])), jnp.zeros((6, width), BF16), natural(jnp.stack(short[2:])), spread_wide, jnp.zeros((1, width), BF16)])
        vectors = reduce_all(vectors, devices).astype(F32)
        set_self = full[:3] + [vectors[:8]]
        set_cross = full[3:] + [vectors[8:]]
        set_inner = [
            whole(inner_weight).reshape(width, blocks, width).transpose(1, 0, 2),
            whole(outer_weight).reshape(blocks, width, width),
        ]
    found = run(
        make_project(packed, parts, rows, block, memory_block, width, narrow, len(set_self)), 5.0,
        "project", *set_self, *row_tokens,
    )
    query, query_t, keys, values, value_t = (found[2 * i : 2 * i + 2] for i in range(5))
    row_memory, ids, memory_ids = found[10:]
    query_t = list(query_t)
    if packed:
        third_c = join(after([third, third_b], query_t[1]))
        third_d = turned_swap(third_c, 3)
        query_t[0] = after(query_t[0], third_c)
        set_query, set_last = set_self, set_self
    else:
        set_back, set_query, set_last, set_memory = [full[3], full[4], full[7]], full[:1], full[1:3], full[5:7]
    found = run(
        make_self_attention(share, parts * share, width), 12.0, "self_attention",
        *query_t, *keys, *value_t, ids,
    )
    mixtures, logs = found[:2], found[2:]
    if packed:
        second_d = after(second_d, mixtures[0])
        set_cross = [second_c, second_d, swap(second_c, 1, 32), swap(second_d, 1, 32)]
        set_back, set_memory = set_cross, set_cross
    first_sum, second_sum, cross_query, memory_keys, memory_values, cross_t, cross_logs, vectors = run(
        make_cross_forward(packed, rows, block, parts * memory_share, width, narrow, len(set_cross)),
        9.0, "cross_forward", *set_cross, *own_tokens, row_memory, ids, memory_ids, *mixtures,
    )
    if packed:
        third_d = after(third_d, second_sum)
        set_inner = [third_c, third_d, swap(third_c, 1, 32), swap(third_d, 1, 32)]
    out_own, out_send, back2_in, sums_inner, *grads_inner = run(
        make_inner(packed, rows, block, width, hidden, narrow, len(set_inner)), 18.0, "inner",
        *set_inner, second_sum, kept, came, vectors,
    )
    out_came = swap(out_send, parts, devices)
    found = run(
        make_cross_back(packed, parts, share, memory_share, width, narrow, len(set_back)), 14.0,
        "cross_back", *set_back, back2_in, first_sum, second_sum, cross_query, memory_keys,
        memory_values, cross_t, cross_logs, ids, memory_ids, vectors, sums_inner, *mixtures,
    )
    back1, memory_key_own, memory_value_own, sums_cross = found[:4]
    slope, slope_t, deltas = (found[4 + 2 * i : 6 + 2 * i] for i in range(3))
    memory_received = [swap(a, m + 1, devices) for m, a in enumerate(found[10 : 10 + parts - 1])]
    grads_early = found[10 + parts - 1 :]
    query = list(query)
    if packed:
        keep, send = combine(after([grads_inner[0], swap(grads_inner[1], 1, 32)], back1, out_came), 2)
        inner_step = [keep, turned_swap(send, 3)]
        memory_key_own = after(memory_key_own, keep)
    memory_own, memory_send, *grads_cross = run(
        make_memory_back(packed, parts, rows, block, memory_block, width, narrow, len(set_memory)),
        2.0, "memory_back", *set_memory, *own_tokens, memory_key_own, memory_value_own, sums_cross,
        *grads_early, *memory_received,
    )
    if packed:
        cross_came = swap(grads_cross[1], 1, 32)
        query[0] = after(query[0], grads_cross[0])
    found = run(
        make_self_back_upper(parts, share, width), 7.0, "self_back_upper", query[0], keys[0],
        values[0], slope[0], slope_t[0], logs[0], deltas[0], ids,
    )
    query_upper, own_upper = found[:2]
    received_upper = [swap(a, m // 2 + 1, devices) for m, a in enumerate(found[2:])]
    if packed:
        keep_cross, send = combine(after([grads_cross[0], cross_came], query_upper), 2)
        cross_step = [keep_cross, turned_swap(send, 3, CROSSED)]
        query[1] = after(query[1], keep_cross)
    in_part, query_sum, query_w_grad, own_lower, *sends = run(
        make_self_back_lower(packed, parts, rows, block, width, narrow, len(set_query)), 11.0,
        "self_back_lower", *set_query, *own_tokens, query[1], keys[1], values[1], slope[1],
        slope_t[1], logs[1], deltas[1], ids, back1, query_upper,
    )
    received_lower = [swap(a, m // 2 + 1, devices) for m, a in enumerate(sends)]
    if packed:
        keep, send = combine(after(inner_step, query_sum), 2)
        inner_step = [keep, turned_swap(send, 2)]
        keep_cross, send = combine(after(cross_step, query_sum), 2)
        cross_step = [keep_cross, turned_swap(send, 2, CROSSED)]
        in_part = after(in_part, keep, keep_cross)
    in_own, in_send, *grads_last = run(
        make_last(packed, parts, rows, block, memory_block, width, narrow, len(set_last)), 6.0,
        "last", *set_last, *own_tokens, in_part, query_sum, query_w_grad, memory_send, own_upper,
        own_lower, *received_upper, *received_lower,
    )

    if packed:
        keep, send = combine([grads_last[0], swap(grads_last[1], 1, 32)], 2)
        last_step = [keep, turned_swap(send, 3)]
        keep, send = combine(last_step, 2)
        last_step = [keep, turned_swap(send, 2)]
        keep_joint, send = combine_joint(after([inner_step, cross_step], in_own, keep), 2)
        joint_step = [keep_joint, turned_swap(send, 1)]
        keep, send = combine(after(last_step, keep_joint), 2)
        last_step = [keep, turned_swap(send, 1)]
        in_send = after(in_send, keep)
        keep_joint, send = combine(after(joint_step, keep), 2)
        joint_step = [keep_joint, turned_swap(send, 0)]
        keep, send = combine(after(last_step, keep_joint), 2)
        last_step = [keep, turned_swap(send, 0)]

        def plan(me_ref, *refs):
            me = me_ref[0]
            joint, last = (sum(r[0].astype(F32) for r in given) for given in (refs[:2], refs[2:4]))
            outs = refs[4:]
            inner, cross = joint[: 2 * blocks * narrow, :], joint[2 * blocks * narrow :, :]
            for i in range(blocks):
                outs[0][:, i * width : (i + 1) * width] = inner[i * narrow : (i + 1) * narrow, :]
            outs[1][...] = inner[blocks * narrow :, :]
            for i in range(5):
                outs[2 + i][...] = cross[i * narrow : (i + 1) * narrow, :]
            for i in range(3):
                outs[7 + i][...] = last[i * narrow : (i + 1) * narrow, :]
            rows_in = jnp.concatenate([cross[5 * narrow :, :], last[3 * narrow :, :]], axis=0)
            outs[10][...] = chosen(me, rows_in, narrow)
            per = width // wide
            line = lax.broadcasted_iota(jnp.int32, (blocks, width), 0)
            row = jnp.sum(jnp.where(line == lax.div(me, per), rows_in[3 : 3 + blocks, :], 0.0), axis=0, keepdims=True)
            outs[11][...] = chosen(lax.rem(me, per), row, wide)

        part = (narrow, width)
        shapes = [(narrow, hidden), (wide, width)] + [part] * 8 + [(24, narrow), (1, wide)]
        (inner_share, outer_share, source_key_share, source_value_share, source_output_share,
         source_query_share, output_share, key_share, value_share, query_share, sums,
         inner_bias_share) = call(
            plan, [(s, F32) for s in shapes], (me_array, *joint_step, *last_step), [], 2.0,
            "finish",
        )
        inner_bias_share = inner_bias_share.reshape(wide)
    else:
        def scatter(array):
            return lax.psum_scatter(array, AXES, scatter_dimension=0, tiled=True)

        inner_share = scatter(grads_inner[0].transpose(1, 0, 2).reshape(width, hidden))
        outer_share = scatter(grads_inner[1].reshape(hidden, width))
        source_output_share, source_query_share, output_share = (scatter(g.astype(F32)) for g in grads_early)
        source_key_share, source_value_share = (scatter(g) for g in grads_cross[:2])
        key_share, value_share = (scatter(g) for g in grads_last[:2])
        query_share = scatter(query_w_grad)
        sums = reduce_all(jnp.concatenate([grads_cross[2], grads_last[2]], axis=0), devices)
        inner_bias_share = lax.dynamic_slice(sums[3 : 3 + blocks].reshape(hidden), (me * wide,), (wide,))
        sums = lax.dynamic_slice(sums, (0, me * narrow), (sums.shape[0], narrow))
    def regroup(mine, came):
        came = came.astype(F32)
        return jnp.where(turn == 0, jnp.stack([mine, came]), jnp.stack([came, mine]))

    output = regroup(out_own, out_came)
    in_came = swap(in_send, parts, devices)
    input_gradient = regroup(in_own, in_came[:block])
    memory_gradient = regroup(memory_own, in_came[block:])

    return (
        output,
        input_gradient,
        memory_gradient,
        query_share,
        key_share,
        value_share,
        output_share,
        sums[16],
        sums[17],
        sums[13],
        sums[11],
        sums[12],
        source_query_share,
        source_key_share,
        source_value_share,
        source_output_share,
        sums[10],
        sums[14],
        sums[9],
        sums[7],
        sums[8],
        inner_share,
        inner_bias_share,
        outer_share,
        sums[2],
        sums[0],
        sums[1],
    )


def solution(mesh):
    sequence, devices = mesh.shape["seq"], mesh.size
    tokens, ids = P("dp", "seq", None), P("dp", "seq")
    matrix, vector = P(AXES, None), P(AXES)
    attention = (matrix,) * 4 + (vector,) * 5
    inner = (matrix, vector, matrix, vector, vector, vector)
    return jax.shard_map(
        functools.partial(per_device, devices=devices, sequence=sequence),
        mesh=mesh,
        in_specs=(tokens, tokens, ids, ids, tokens) + attention + attention + inner,
        out_specs=(tokens, tokens, tokens) + attention + attention + inner,
        check_vma=False,
    )
```

```python
import functools
import math

import jax
import jax.numpy as jnp
from jax import lax
from jax.experimental import pallas as pl
from jax.experimental.pallas import tpu as pltpu
from jax.sharding import PartitionSpec as P

HEADS = 8
HEAD_DIM = 64
PAIR = 128
EPSILON = 1e-05
MASKED = 1e9
AXES = ("dp", "seq")
F32 = jnp.float32
BF16 = jnp.bfloat16

(
    OUTPUT_BIAS,
    ATTENTION_GAIN,
    ATTENTION_SHIFT,
    SOURCE_QUERY_BIAS,
    SOURCE_VALUE_BIAS,
    SOURCE_OUTPUT_BIAS,
    SOURCE_GAIN,
    SOURCE_SHIFT,
    OUTER_BIAS,
    FINAL_GAIN,
    FINAL_SHIFT,
    INNER_BIAS,
) = range(12)
Z_MASKS = (0, 8, 16, 24)
VM = pl.BlockSpec(memory_space=pltpu.VMEM)
SM = pl.BlockSpec(memory_space=pltpu.SMEM)


def dot(a, b):
    return lax.dot_general(a, b, (((1,), (0,)), ((), ())), preferred_element_type=F32)


def dot_nt(a, b):
    return lax.dot_general(a, b, (((1,), (1,)), ((), ())), preferred_element_type=F32)


def dot_tn(a, b):
    return lax.dot_general(a, b, (((0,), (0,)), ((), ())), preferred_element_type=F32)


def total(values):
    return jnp.sum(values.astype(F32), axis=0, keepdims=True)


def normalize(h):
    average = jnp.mean(h, axis=-1, keepdims=True)
    centered = h - average
    variance = jnp.mean(centered * centered, axis=-1, keepdims=True)
    inverse = lax.rsqrt(variance + EPSILON)
    return centered * inverse, inverse


def normalize_back(upstream, normed, inverse, gain):
    scaled = upstream * gain
    first_mean = jnp.mean(scaled, axis=-1, keepdims=True)
    second_mean = jnp.mean(scaled * normed, axis=-1, keepdims=True)
    return inverse * (scaled - first_mean - normed * second_mean)


def normal_parts(v):
    density = 0.3989422804014327 * jnp.exp(-0.5 * v * v)
    t = 1.0 / (1.0 + 0.2316419 * jnp.abs(v))
    series = t * (
        0.319381530
        + t * (-0.356563782 + t * (1.781477937 + t * (-1.821255978 + t * 1.330274429)))
    )
    tail = density * series
    return jnp.where(v >= 0.0, 1.0 - tail, tail), density


def penalties(ids):
    place = lax.broadcasted_iota(jnp.int32, (PAIR, ids.shape[1]), 0)
    return jnp.where((place == ids) | (place >= 4), 0.0, -MASKED).astype(BF16)


def one_hot(ids):
    place = lax.broadcasted_iota(jnp.int32, (PAIR, ids.shape[1]), 0)
    return jnp.where(place == ids, 1.0, 0.0).astype(F32).T.astype(BF16)


def spread(part, half):
    empty = jnp.zeros_like(part)
    return [part, empty] if half == 0 else [empty, part]


def attend(query_t, keys, value_t, hot, penalty, mixture_t, logs):
    length = keys.shape[0]

    def pair(p, carry):
        columns = pl.ds(pl.multiple_of(p * PAIR, PAIR), PAIR)
        left = jnp.concatenate([keys[:, columns], hot[...]], axis=1)
        for half in range(2):
            rows = pl.ds(pl.multiple_of(p * PAIR + half * HEAD_DIM, HEAD_DIM), HEAD_DIM)
            right = jnp.concatenate(spread(query_t[rows, :], half) + [penalty[...]], axis=0)
            scores = dot(left, right)
            highest = jnp.max(scores, axis=0, keepdims=True)
            weights = jnp.exp(scores - highest).astype(BF16)
            values = jnp.concatenate(
                [value_t[rows, :], jnp.ones((16, length), BF16)], axis=0
            )
            found = dot(values, weights)
            denominator = found[HEAD_DIM : HEAD_DIM + 1, :]
            mixture_t[rows, :] = (found[:HEAD_DIM, :] / denominator).astype(BF16)
            logs[2 * p + half] = highest + jnp.log(denominator)
        return carry

    lax.fori_loop(0, keys.shape[1] // PAIR, pair, 0)


def attend_back(
    query_t, query, keys, key_t, values, slope_t, slope, hot, penalty, logs, deltas,
    query_grad_t, key_grad, value_grad,
):
    tokens = query.shape[0]
    lane = lax.broadcasted_iota(jnp.int32, (tokens, PAIR), 1)

    def pair(p, carry):
        columns = pl.ds(pl.multiple_of(p * PAIR, PAIR), PAIR)
        left = jnp.concatenate([keys[:, columns], hot[...]], axis=1)
        value_pair = values[:, columns]
        key_sum, value_sum = None, None
        for half in range(2):
            rows = pl.ds(pl.multiple_of(p * PAIR + half * HEAD_DIM, HEAD_DIM), HEAD_DIM)
            right = jnp.concatenate(spread(query_t[rows, :], half) + [penalty[...]], axis=0)
            chances = jnp.exp(dot(left, right) - logs[2 * p + half])
            slopes = dot(value_pair, jnp.concatenate(spread(slope_t[rows, :], half), axis=0))
            grads = (chances * (slopes - deltas[2 * p + half])).astype(BF16)
            query_grad_t[rows, :] = dot(key_t[rows, :], grads) * HEAD_DIM**-0.5
            mine = (lane < HEAD_DIM) if half == 0 else (lane >= HEAD_DIM)
            none = jnp.zeros((tokens, PAIR), BF16)
            value_part = dot(chances.astype(BF16), jnp.where(mine, slope[:, columns], none))
            key_part = dot(grads, jnp.where(mine, query[:, columns], none))
            value_sum = value_part if value_sum is None else value_sum + value_part
            key_sum = key_part if key_sum is None else key_sum + key_part
        key_grad[:, columns] = key_sum
        value_grad[:, columns] = value_sum
        return carry

    lax.fori_loop(0, keys.shape[1] // PAIR, pair, 0)


def deltas_of(slope_t, mixture_t, deltas):
    for head in range(slope_t.shape[0] // HEAD_DIM):
        rows = slice(head * HEAD_DIM, (head + 1) * HEAD_DIM)
        deltas[head] = jnp.sum(
            slope_t[rows, :].astype(F32) * mixture_t[rows, :].astype(F32), axis=0, keepdims=True
        )


def swap(array, mask, devices):
    return lax.ppermute(array, AXES, [(i, i ^ mask) for i in range(devices)])


Z_FIRST = ((8, 24, 2, 4), (24, 8, 4, 2))
CROSSED = ((8, 24, 4, 2), (24, 8, 2, 4))


def turned_swap(array, step, orders=Z_FIRST):
    return lax.ppermute(array, AXES, [(i, i ^ orders[i % 2][step]) for i in range(32)])


def after(value, *others):
    return lax.optimization_barrier((value, others))[0]


def places(me, orders=Z_FIRST):
    found = []
    for core in range(2):
        even = ((me & 1) ^ core) == 0
        masks = [jnp.where(even, first, second) for first, second in zip(*orders)]
        for far in range(2):
            for slot in range(8):
                device = me ^ core if core else me
                for step, bit in enumerate((slot & 1, slot & 2, slot & 4, far)):
                    if bit:
                        device = device ^ masks[step]
                found.append((core, far, slot, device))
    return found


def unpack(me, pieces, stride, first, rows, scratch, orders=Z_FIRST):
    for core, far, slot, device in places(me, orders):
        ref = pieces[2 * core + far]
        at = slot * stride + first
        scratch[pl.ds(pl.multiple_of(device * rows, rows), rows), :] = ref[at : at + rows, :]


def sort_vectors(me, pieces, stride, first, narrow, sheet):
    width, blocks = sheet.shape[1], sheet.shape[0]
    lane = lax.broadcasted_iota(jnp.int32, (8, width), 1)
    per = width // (blocks * narrow)
    near, far = jnp.zeros((8, width), F32), jnp.zeros((8, width), F32)
    sheet[...] = jnp.zeros_like(sheet)
    for core, distant, slot, device in places(me):
        part = pieces[2 * core + distant][slot * stride + first : (slot + 1) * stride, :].astype(F32)
        group = lane // narrow
        near = near + jnp.where(group == device, part, 0.0)
        far = far + jnp.where(group == lax.rem(device + 1, width // narrow), part, 0.0)
        wide = jnp.where(lane[7:8, :] // (blocks * narrow) == lax.rem(device, per), part[7:8, :], 0.0)
        sheet[pl.ds(lax.div(device, per), 1), :] += wide
    far = pltpu.roll(far, width - narrow, 1)
    return jnp.concatenate([near[:7, :], far[:6, :]], axis=0)


class Grads:
    def __init__(self, me, refs, dense, rows, orders=Z_FIRST):
        self.me, self.refs, self.dense, self.rows, self.orders = me, refs, dense, rows, orders

    def put(self, index, grad):
        if self.dense is None:
            self.refs[index][...] = grad
            return
        self.dense[...] = grad
        rows = self.rows
        for core, far, slot, device in places(self.me, self.orders):
            found = self.dense[pl.ds(pl.multiple_of(device * rows, rows), rows), :]
            self.refs[core][far * 8 + slot, index * rows : (index + 1) * rows, :] = found.astype(BF16)

    def put_sums(self, first, sums):
        if self.dense is None:
            self.refs[-1][...] = sums
            return
        low = sums.astype(BF16)
        for ref in self.refs:
            for slot in range(16):
                ref[slot, first : first + sums.shape[0], :] = low


def grad_outs(packed, count, rows, width, sums):
    if packed:
        return [((16, count * rows + sums, width), BF16)] * 2
    return [((width, width), F32)] * count + [((sums, width), F32)]


COSTS = {}


def padded(shape, dtype):
    last = -(-shape[-1] // 128) * 128
    tall = -(-shape[-2] // 16) * 16 if len(shape) > 1 else 16
    return math.prod(shape[:-2]) * tall * last * jnp.dtype(dtype).itemsize


def snug(arrays):
    return 2 * sum(padded(a.shape, a.dtype) for a in arrays) + (3 << 20)


def call(kernel, outs, args, scratch, micros, name, room=10):
    moved = sum(math.prod(a.shape) * a.dtype.itemsize for a in args[1:])
    moved += sum(math.prod(s) * jnp.dtype(d).itemsize for s, d in outs)
    need = sum(padded(a.shape, a.dtype) for a in args[1:])
    need += sum(padded(s, d) for s, d in list(outs) + list(scratch))
    return pl.pallas_call(
        kernel,
        out_shape=[jax.ShapeDtypeStruct(s, d) for s, d in outs],
        in_specs=[SM] + [VM] * (len(args) - 1),
        out_specs=[VM] * len(outs),
        scratch_shapes=[pltpu.VMEM(s, d) for s, d in scratch],
        compiler_params=pltpu.CompilerParams(vmem_limit_bytes=min(need + (room << 20), 58 << 20)),
        cost_estimate=pl.CostEstimate(
            flops=int(COSTS.get(name, 0) * 1.15e9) + 1, bytes_accessed=1, transcendentals=0
        ),
        name=name,
    )(*args)


def tokens_packet(turn, tokens, memory, target_ids, source_ids, cotangent):
    block, width = tokens.shape[1:]
    memory_block = memory.shape[1]
    first = block + memory_block + 8

    def kernel(turn_ref, targets, sources, tokens_ref, memory_ref, cot_ref, sent, kept):
        mine = turn_ref[0]
        for row, out in ((1 - mine, sent), (mine, kept)):
            out[:block, :] = tokens_ref[row]
            out[block : block + memory_block, :] = memory_ref[row]
            ids = targets[pl.ds(row, 1), :].astype(F32)
            ids = jnp.concatenate([ids, jnp.zeros((1, width - block), F32)], axis=1)
            others = sources[pl.ds(row, 1), :].astype(F32)
            others = jnp.concatenate([others, jnp.zeros((1, width - memory_block), F32)], axis=1)
            place = lax.broadcasted_iota(jnp.int32, (8, width), 0)
            found = jnp.where(place == 0, ids, jnp.where(place == 1, others, 0.0))
            out[block + memory_block : first, :] = found.astype(BF16)
            out[first:, :] = cot_ref[row]

    shape = (first + block, width)
    return call(kernel, [(shape, BF16)] * 2, (turn, target_ids, source_ids, tokens, memory, cotangent),
                [], 1.0, "tokens_packet", 58)


def placed(me, parts, width):
    here = lax.broadcasted_iota(jnp.int32, (parts.shape[1], width), 0) + me * parts.shape[1]
    lane = lax.broadcasted_iota(jnp.int32, (parts.shape[1], width), 1)
    return dot(parts, jnp.where(lane == here, 1.0, 0.0).astype(BF16))


def make_weights_packet(narrow, width, blocks):
    tall = blocks * narrow

    def kernel(me_ref, *refs):
        weights, inner, outer, wide, short = refs[:8], refs[8], refs[9], refs[10], refs[11:24]
        first, second, third = refs[24:]
        me = me_ref[0]
        for i, ref in enumerate(weights):
            if i < 3:
                first[i * narrow : (i + 1) * narrow, :] = ref[...]
            else:
                second[(i - 3) * narrow : (i - 2) * narrow, :] = ref[...]
        short = jnp.concatenate([ref[...].astype(F32) for ref in short], axis=0).astype(BF16)
        near = placed(me, short[:7, :], width)
        far = placed(lax.rem(me + 1, width // narrow), short[7:, :], width)
        far = jnp.concatenate([far, jnp.zeros((1, width), F32)], axis=0)
        row = placed(lax.rem(me, width // wide.shape[1]), wide[...], width)
        first[3 * narrow :, :] = jnp.concatenate([near + far, row], axis=0).astype(BF16)
        for i in range(blocks):
            third[i * narrow : (i + 1) * narrow, :] = inner[:, i * width : (i + 1) * width]
        third[tall:, :] = outer[...]

    return kernel, [((rows, width), BF16) for rows in (3 * narrow + 8, 5 * narrow, 2 * tall)]


def join(arrays):
    def kernel(*refs):
        at = 0
        for ref in refs[:-1]:
            refs[-1][at : at + ref.shape[0], :] = ref[...]
            at += ref.shape[0]

    rows = sum(a.shape[0] for a in arrays)
    return pl.pallas_call(
        kernel,
        out_shape=jax.ShapeDtypeStruct((rows, arrays[0].shape[1]), arrays[0].dtype),
        in_specs=[VM] * len(arrays),
        out_specs=VM,
        compiler_params=pltpu.CompilerParams(vmem_limit_bytes=snug(arrays)),
        cost_estimate=pl.CostEstimate(flops=1 << 20, bytes_accessed=0, transcendentals=0),
        name="join",
    )(*arrays)


def make_project(packed, parts, rows, block, memory_block, width, narrow, blocks, n_pieces):
    share = rows * block
    length = parts * share
    memory_share = rows * memory_block
    stride = 3 * narrow + 8
    half = width // 2

    def kernel(*refs):
        me_ref, refs = refs[0], list(refs[1:])
        pieces, refs = refs[:n_pieces], refs[n_pieces:]
        tokens, refs = refs[: parts * rows], refs[parts * rows :]
        query, query_t, keys, values, value_t = (refs[2 * i : 2 * i + 2] for i in range(5))
        memory, ids, memory_ids, vectors = refs[10:14]
        scratch = refs[14:]
        me = me_ref[0]
        if packed:
            for i in range(3):
                unpack(me, pieces, stride, i * narrow, narrow, scratch[i])
            query_w, key_w, value_w, sheet = scratch
            biases = sort_vectors(me, pieces, stride, 3 * narrow, narrow, sheet)
            rest = jnp.zeros((5 - sheet.shape[0], width), F32)
            vectors[...] = jnp.concatenate([biases[2:, :], sheet[...], rest], axis=0)
        else:
            query_w, key_w, value_w = pieces[:3]
            biases = pieces[3][:8, :]
            vectors[...] = pieces[3][8:, :]
        for i in range(parts):
            here = slice(i * share, (i + 1) * share)
            some = tokens[i * rows : (i + 1) * rows]
            own = jnp.concatenate([t[:block, :] for t in some], axis=0)
            if i == 0:
                scaled = (dot(own, query_w[...]) + biases[0:1, :]).astype(BF16) * BF16(HEAD_DIM**-0.5)
            key = dot(own, key_w[...]).astype(BF16)
            found = (dot(own, value_w[...]) + biases[1:2, :]).astype(BF16)
            for side in range(2):
                columns = slice(side * half, (side + 1) * half)
                if i == 0:
                    query[side][...] = scaled[:, columns]
                    query_t[side][...] = scaled[:, columns].T
                keys[side][here, :] = key[:, columns]
                values[side][here, :] = found[:, columns]
                value_t[side][:, here] = found[:, columns].T
        for i, t in enumerate(tokens):
            memory[i * memory_block : (i + 1) * memory_block, :] = t[block : block + memory_block, :]
            found = t[block + memory_block : block + memory_block + 8, :].astype(F32).astype(jnp.int32)
            ids[:, i * block : (i + 1) * block] = found[0:1, :block]
        found = [t[block + memory_block : block + memory_block + 8, :].astype(F32).astype(jnp.int32)[1:2, :memory_block] for t in tokens]
        memory_ids[...] = jnp.concatenate(found, axis=1)

    outs = [((share, half), BF16)] * 2 + [((half, share), BF16)] * 2
    outs += [((length, half), BF16)] * 4 + [((half, length), BF16)] * 2
    outs += [
        ((parts * memory_share, width), BF16),
        ((1, length), jnp.int32),
        ((1, parts * memory_share), jnp.int32),
        ((16, width), F32),
    ]
    return kernel, outs, [((width, width), BF16)] * 3 + [((blocks, width), F32)] if packed else []


def make_self_attention(share, length, width):
    def kernel(me_ref, *refs):
        query_t, keys, value_t, ids = refs[:2], refs[2:4], refs[4:6], refs[6]
        mixture_t, logs, hot, penalty = refs[7:9], refs[9:11], refs[11], refs[12]
        hot[...] = one_hot(ids[...])
        penalty[...] = penalties(ids[:, :share])
        for side in range(2):
            attend(query_t[side], keys[side], value_t[side], hot, penalty, mixture_t[side], logs[side])

    outs = [((width // 2, share), BF16)] * 2 + [((HEADS // 2, 1, share), F32)] * 2
    return kernel, outs, [((length, PAIR), BF16), ((PAIR, share), BF16)]


def make_cross_forward(packed, rows, block, memory_length, width, narrow, n_pieces):
    share = rows * block
    stride = 5 * narrow

    def kernel(*refs):
        me_ref, refs = refs[0], list(refs[1:])
        pieces, refs = refs[:n_pieces], refs[n_pieces:]
        tokens, refs = refs[:rows], refs[rows:]
        memory, ids, memory_ids, upper, lower, vectors = refs[:6]
        first_sum, second_sum, query, memory_keys, memory_values, cross_t, logs = refs[6:13]
        scratch = refs[13:]
        query_t, value_t, hot, penalty = scratch[:4]
        if packed:
            for i in range(5):
                unpack(me_ref[0], pieces, stride, i * narrow, narrow, scratch[4 + i])
            output_w, query_w, key_w, value_w, source_w = scratch[4:]
        else:
            output_w, query_w, key_w, value_w, source_w = pieces[:5]

        def vector(i):
            return vectors[i : i + 1, :]

        own = jnp.concatenate([t[:block, :] for t in tokens], axis=0)
        mixture_t = jnp.concatenate([upper[...], lower[...]], axis=0)
        h = own.astype(F32) + dot_tn(mixture_t, output_w[...]) + vector(OUTPUT_BIAS)
        first_sum[...] = h
        first = normalize(h)[0] * vector(ATTENTION_GAIN) + vector(ATTENTION_SHIFT)
        scaled = (dot(first.astype(BF16), query_w[...]) + vector(SOURCE_QUERY_BIAS)).astype(BF16) * BF16(HEAD_DIM**-0.5)
        query[...] = scaled
        query_t[...] = scaled.T
        memory_keys[...] = dot(memory[...], key_w[...]).astype(BF16)
        memory_values[...] = (dot(memory[...], value_w[...]) + vector(SOURCE_VALUE_BIAS)).astype(BF16)
        value_t[...] = memory_values[...].T
        hot[...] = one_hot(memory_ids[...])
        penalty[...] = penalties(ids[:, :share])
        attend(query_t, memory_keys, value_t, hot, penalty, cross_t, logs)
        first = normalize(first_sum[...])[0] * vector(ATTENTION_GAIN) + vector(ATTENTION_SHIFT)
        second_sum[...] = first + dot_tn(cross_t[...], source_w[...]) + vector(SOURCE_OUTPUT_BIAS)

    outs = [
        ((share, width), F32),
        ((share, width), F32),
        ((share, width), BF16),
        ((memory_length, width), BF16),
        ((memory_length, width), BF16),
        ((width, share), BF16),
        ((HEADS, 1, share), F32),
    ]
    scratch = [((width, share), BF16), ((width, memory_length), BF16), ((memory_length, PAIR), BF16), ((PAIR, share), BF16)]
    if packed:
        scratch += [((width, width), BF16)] * 5
    return kernel, outs, scratch


def make_inner(packed, rows, block, width, hidden, narrow, n_pieces):
    blocks = hidden // width
    share = rows * block
    per = width // (blocks * narrow)

    def kernel(*refs):
        me_ref, refs = refs[0], list(refs[1:])
        pieces, refs = refs[:n_pieces], refs[n_pieces:]
        second_sum, cot_own, cot_came, vectors = refs[:4]
        out_own, out_send, back, sums = refs[4:8]
        grads, scratch = refs[8:10], refs[10:]
        low, active, gate, slope = scratch[:4]
        if packed:
            inner_w, outer_w, gathered, dense = scratch[4:8]
            tall = blocks * narrow
            for core, far, slot, device in places(me_ref[0]):
                ref, at = pieces[2 * core + far], slot * 2 * tall
                row = pl.multiple_of(device * narrow, narrow)
                for i in range(blocks):
                    inner_w[i, pl.ds(row, narrow), :] = ref[at + i * narrow : at + (i + 1) * narrow, :]
                row = pl.multiple_of(lax.rem(device, per) * tall, tall)
                outer_w[lax.div(device, per), pl.ds(row, tall), :] = ref[at + tall : at + 2 * tall, :]
        else:
            inner_w, outer_w = pieces

        def vector(i):
            return vectors[i : i + 1, :]

        second = normalize(second_sum[...])[0] * vector(SOURCE_GAIN) + vector(SOURCE_SHIFT)
        low[...] = second.astype(BF16)
        back[...] = second + vector(OUTER_BIAS)

        def forward(i, carry):
            inner = dot(low[...], inner_w[i]) + vectors[pl.ds(INNER_BIAS + i, 1), :]
            chance, density = normal_parts(inner)
            found = (inner * chance).astype(BF16)
            active[i] = found
            gate[i] = chance + inner * density
            back[...] += dot(found, outer_w[i])
            return carry

        lax.fori_loop(0, blocks, forward, 0)
        normed, inverse = normalize(back[...])
        final = normed * vector(FINAL_GAIN) + vector(FINAL_SHIFT)
        out_own[...] = final[:block, :]
        out_send[...] = final[block:, :].astype(BF16)
        upstream = jnp.concatenate([cot_own[-block:, :], cot_came[-block:, :]], axis=0).astype(F32)
        sums[0:1, :] = total(upstream * normed)
        sums[1:2, :] = total(upstream)
        back3 = normalize_back(upstream, normed, inverse, vector(FINAL_GAIN))
        slope[...] = back3.astype(BF16)
        sums[2:3, :] = total(slope[...])
        sums[7:8, :] = jnp.zeros_like(sums[7:8, :])
        back[...] = back3

        def backward(i, carry):
            grad = dot_nt(slope[...], outer_w[i]) * gate[i]
            inner_low = grad.astype(BF16)
            sums[pl.ds(3 + i, 1), :] = total(inner_low)
            outer_grad = dot_tn(active[i], slope[...])
            inner_grad = dot_tn(low[...], inner_low)
            back[...] += dot_nt(inner_low, inner_w[i])
            if packed:
                dense[...] = inner_grad
                gathered[i] = outer_grad.astype(BF16)
                here = pl.ds(pl.multiple_of(i * narrow, narrow), narrow)
                for core, far, slot, device in places(me_ref[0]):
                    row = pl.multiple_of(device * narrow, narrow)
                    grads[core][far * 8 + slot, here, :] = dense[pl.ds(row, narrow), :].astype(BF16)
            else:
                grads[0][i] = inner_grad
                grads[1][i] = outer_grad
            return carry

        lax.fori_loop(0, blocks, backward, 0)
        if packed:
            tall = blocks * narrow
            for core, far, slot, device in places(me_ref[0]):
                row = pl.multiple_of(lax.rem(device, per) * tall, tall)
                grads[core][far * 8 + slot, tall:, :] = gathered[lax.div(device, per), pl.ds(row, tall), :]

    outs = [((block, width), F32), ((block, width), BF16), ((share, width), F32), ((8, width), F32)]
    if packed:
        outs += [((16, 2 * blocks * narrow, width), BF16)] * 2
    else:
        outs += [((blocks, width, width), F32)] * 2
    scratch = [((share, width), BF16), ((blocks, share, width), BF16), ((blocks, share, width), F32), ((share, width), BF16)]
    if packed:
        scratch += [((blocks, width, width), BF16)] * 3 + [((width, width), F32)]
    return kernel, outs, scratch


def make_cross_back(packed, parts, share, memory_share, width, narrow, n_pieces):
    memory_length = parts * memory_share
    stride = 5 * narrow

    def kernel(*refs):
        me_ref, refs = refs[0], list(refs[1:])
        pieces, refs = refs[:n_pieces], refs[n_pieces:]
        (back2_in, first_sum, second_sum, query, memory_keys, memory_values, cross_t, logs, ids,
         memory_ids, vectors, sums_inner) = refs[:12]
        mixtures, refs = refs[12:14], refs[14:]
        back1, key_own, value_own, sums = refs[:4]
        self_slope, self_slope_t, self_deltas = (refs[4 + 2 * i : 6 + 2 * i] for i in range(3))
        sends, refs = refs[10 : 10 + parts - 1], refs[10 + parts - 1 :]
        grads, scratch = refs[:3], refs[3:]
        (slope_t, slope, key_t, hot, penalty, query_t, deltas, query_grad_t, key_grad, value_grad) = scratch[:10]
        upper, lower = mixtures
        if packed:
            for i, at in enumerate((0, 1, 4)):
                unpack(me_ref[0], pieces, stride, at * narrow, narrow, scratch[10 + i])
            output_w, query_w, source_w = scratch[10:13]
        else:
            output_w, query_w, source_w = pieces

        def vector(i):
            return vectors[i : i + 1, :]

        sums[0:7, :] = sums_inner[0:7, :]
        upstream = back2_in[...]
        normed, inverse = normalize(second_sum[...])
        sums[7:8, :] = total(upstream * normed)
        sums[8:9, :] = total(upstream)
        back2 = normalize_back(upstream, normed, inverse, vector(SOURCE_GAIN))
        back1[...] = back2
        cross_low = back2.astype(BF16)
        sums[9:10, :] = total(cross_low)
        grads[0][...] = dot(cross_t[...], cross_low).astype(BF16)
        found = dot_nt(cross_low, source_w[...]).astype(BF16)
        slope[...] = found
        slope_t[...] = found.T
        deltas_of(slope_t, cross_t, deltas)
        query_t[...] = query[...].T
        key_t[...] = memory_keys[...].T
        hot[...] = one_hot(memory_ids[...])
        penalty[...] = penalties(ids[:, :share])
        attend_back(query_t, query, memory_keys, key_t, memory_values, slope_t, slope, hot, penalty,
                    logs, deltas, query_grad_t, key_grad, value_grad)
        key_own[...] = key_grad[:memory_share, :]
        value_own[...] = value_grad[:memory_share, :]
        for i in range(1, parts):
            here = slice(i * memory_share, (i + 1) * memory_share)
            sends[i - 1][:memory_share, :] = key_grad[here, :].astype(BF16)
            sends[i - 1][memory_share:, :] = value_grad[here, :].astype(BF16)
        query_low = query_grad_t[...].T.astype(BF16)
        sums[10:11, :] = total(query_low)
        normed, inverse = normalize(first_sum[...])
        first_low = (normed * vector(ATTENTION_GAIN) + vector(ATTENTION_SHIFT)).astype(BF16)
        grads[1][...] = dot_tn(first_low, query_low).astype(BF16)
        upstream = back1[...] + dot_nt(query_low, query_w[...])
        sums[11:12, :] = total(upstream * normed)
        sums[12:13, :] = total(upstream)
        grad = normalize_back(upstream, normed, inverse, vector(ATTENTION_GAIN))
        back1[...] = grad
        branch_low = grad.astype(BF16)
        sums[13:14, :] = total(branch_low)
        sums[14:16, :] = jnp.zeros_like(sums[14:16, :])
        mixture_t = jnp.concatenate([upper[...], lower[...]], axis=0)
        grads[2][...] = dot(mixture_t, branch_low).astype(BF16)
        found = dot_nt(branch_low, output_w[...]).astype(BF16)
        for side in range(2):
            columns = slice(side * width // 2, (side + 1) * width // 2)
            self_slope[side][...] = found[:, columns]
            self_slope_t[side][...] = found[:, columns].T
            deltas_of(self_slope_t[side], mixtures[side], self_deltas[side])

    half = width // 2
    outs = [
        ((share, width), F32),
        ((memory_share, width), F32),
        ((memory_share, width), F32),
        ((16, width), F32),
    ]
    outs += [((share, half), BF16)] * 2 + [((half, share), BF16)] * 2
    outs += [((HEADS // 2, 1, share), F32)] * 2
    outs += [((2 * memory_share, width), BF16)] * (parts - 1)
    outs += [((width, width), BF16)] * 3
    scratch = [
        ((width, share), BF16),
        ((share, width), BF16),
        ((width, memory_length), BF16),
        ((memory_length, PAIR), BF16),
        ((PAIR, share), BF16),
        ((width, share), BF16),
        ((HEADS, 1, share), F32),
        ((width, share), F32),
        ((memory_length, width), F32),
        ((memory_length, width), F32),
    ]
    if packed:
        scratch += [((width, width), BF16)] * 3
    return kernel, outs, scratch


def attention_back_half(refs, share, scratch):
    query, keys, values, slope, slope_t, logs, deltas, ids = refs
    query_t, key_t, hot, penalty, query_grad_t, key_grad, value_grad = scratch
    query_t[...] = query[...].T
    key_t[...] = keys[...].T
    hot[...] = one_hot(ids[...])
    penalty[...] = penalties(ids[:, :share])
    attend_back(query_t, query, keys, key_t, values, slope_t, slope, hot, penalty, logs, deltas,
                query_grad_t, key_grad, value_grad)


def half_scratch(share, length, half):
    return [
        ((half, share), BF16),
        ((half, length), BF16),
        ((length, PAIR), BF16),
        ((PAIR, share), BF16),
        ((half, share), F32),
        ((length, half), F32),
        ((length, half), F32),
    ]


def give_half(share, scratch, own, sends):
    key_grad, value_grad = scratch[5:7]
    own[:share, :] = key_grad[:share, :]
    own[share:, :] = value_grad[:share, :]
    for i, send in enumerate(sends):
        here = slice((i // 2 + 1) * share, (i // 2 + 2) * share)
        send[...] = (key_grad, value_grad)[i % 2][here, :].astype(BF16)


def make_memory_back(packed, parts, rows, block, memory_block, width, narrow, n_pieces):
    memory_share = rows * memory_block

    def kernel(*refs):
        me_ref, refs = refs[0], list(refs[1:])
        pieces, refs = refs[:n_pieces], refs[n_pieces:]
        tokens, refs = refs[:rows], refs[rows:]
        memory_key_own, memory_value_own, sums_in = refs[:3]
        early, refs = refs[3:6], refs[6:]
        memory_received, refs = refs[: parts - 1], refs[parts - 1 :]
        memory_own, memory_send = refs[:2]
        n_grads = 2 if packed else 3
        grad_refs, scratch = refs[2 : 2 + n_grads], refs[2 + n_grads :]
        sums = scratch[0]
        me = me_ref[0]
        if packed:
            for i in range(2):
                unpack(me, pieces, 5 * narrow, (2 + i) * narrow, narrow, scratch[1 + i])
            source_key, source_value = scratch[1:3]
        else:
            source_key, source_value = pieces
        grads = Grads(me, grad_refs, scratch[3] if packed else None, narrow, CROSSED)
        memory = jnp.concatenate([t[block : block + memory_block, :] for t in tokens], axis=0)
        key_sum, value_sum = memory_key_own[...], memory_value_own[...]
        for ref in memory_received:
            key_sum = key_sum + ref[:memory_share, :].astype(F32)
            value_sum = value_sum + ref[memory_share:, :].astype(F32)
        key_low, value_low = key_sum.astype(BF16), value_sum.astype(BF16)
        sums[...] = sums_in[...]
        sums[14:15, :] = total(value_low)
        grads.put_sums(5 * narrow, sums[...])
        grads.put(0, dot_tn(memory, key_low))
        grads.put(1, dot_tn(memory, value_low))
        if packed:
            for i, ref in enumerate(early):
                grads.put(2 + i, ref[...].astype(F32))
        grad = dot_nt(key_low, source_key[...]) + dot_nt(value_low, source_value[...])
        memory_own[...] = grad[:memory_block, :]
        memory_send[...] = grad[memory_block:, :].astype(BF16)

    outs = [((memory_block, width), F32), ((memory_block, width), BF16)]
    if packed:
        outs += [((16, 5 * narrow + 16, width), BF16)] * 2
    else:
        outs += [((width, width), F32)] * 2 + [((16, width), F32)]
    scratch = [((16, width), F32)]
    if packed:
        scratch += [((width, width), BF16)] * 2 + [((width, width), F32)]
    return kernel, outs, scratch


def make_self_back_upper(parts, share, width):
    length, half = parts * share, width // 2

    def kernel(*refs):
        operands, (query_grad, own), refs = refs[1:9], refs[9:11], refs[11:]
        sends, scratch = refs[: 2 * parts - 2], refs[2 * parts - 2 :]
        attention_back_half(operands, share, scratch)
        query_grad[...] = scratch[4][...].T.astype(BF16)
        give_half(share, scratch, own, sends)

    outs = [((share, half), BF16), ((2 * share, half), F32)] + [((share, half), BF16)] * (2 * parts - 2)
    return kernel, outs, half_scratch(share, length, half)


def make_self_back_lower(packed, parts, rows, block, width, narrow, n_pieces):
    share = rows * block
    length, half = parts * share, width // 2

    def kernel(*refs):
        me_ref, refs = refs[0], list(refs[1:])
        pieces, refs = refs[:n_pieces], refs[n_pieces:]
        tokens, refs = refs[:rows], refs[rows:]
        operands, refs = refs[:8], refs[8:]
        back1, query_upper = refs[:2]
        in_part, query_sum, query_w_grad, own = refs[2:6]
        sends, scratch = refs[6 : 4 + 2 * parts], refs[4 + 2 * parts :]
        if packed:
            unpack(me_ref[0], pieces, 3 * narrow + 8, 0, narrow, scratch[7])
            query_w = scratch[7]
        else:
            (query_w,) = pieces
        attention_back_half(operands, share, scratch[:7])
        give_half(share, scratch, own, sends)
        query_low = jnp.concatenate([query_upper[...], scratch[4][...].T.astype(BF16)], axis=1)
        tokens_own = jnp.concatenate([t[:block, :] for t in tokens], axis=0)
        in_part[...] = back1[...] + dot_nt(query_low, query_w[...])
        query_sum[...] = jnp.concatenate([total(query_low), jnp.zeros((7, width), F32)], axis=0)
        query_w_grad[...] = dot_tn(tokens_own, query_low).astype(query_w_grad.dtype)

    outs = [
        ((share, width), F32),
        ((8, width), F32),
        ((width, width), BF16 if packed else F32),
        ((2 * share, half), F32),
    ]
    outs += [((share, half), BF16)] * (2 * parts - 2)
    scratch = half_scratch(share, length, half)
    if packed:
        scratch += [((width, width), BF16)]
    return kernel, outs, scratch


def make_last(packed, parts, rows, block, memory_block, width, narrow, n_pieces):
    share = rows * block

    def kernel(*refs):
        me_ref, refs = refs[0], list(refs[1:])
        pieces, refs = refs[:n_pieces], refs[n_pieces:]
        tokens, refs = refs[:rows], refs[rows:]
        in_part, query_sum, query_w_grad, memory_send = refs[:4]
        owns, refs = refs[4:6], refs[6:]
        received = [refs[: 2 * parts - 2], refs[2 * parts - 2 : 4 * parts - 4]]
        refs = refs[4 * parts - 4 :]
        in_own, in_send = refs[:2]
        n_grads = 2 if packed else 3
        grad_refs, scratch = refs[2 : 2 + n_grads], refs[2 + n_grads :]
        sums = scratch[0]
        me = me_ref[0]
        if packed:
            for i in range(2):
                unpack(me, pieces, 3 * narrow + 8, (1 + i) * narrow, narrow, scratch[1 + i])
            key_w, value_w = scratch[1:3]
        else:
            key_w, value_w = pieces
        grads = Grads(me, grad_refs, scratch[3] if packed else None, narrow)
        if packed:
            grads.put(2, query_w_grad[...].astype(F32))
        lows = []
        for own, others in zip(owns, received):
            found = own[...]
            for key, value in zip(others[::2], others[1::2]):
                found = found + jnp.concatenate([key[...], value[...]], axis=0).astype(F32)
            lows.append(found.astype(BF16))
        key_low = jnp.concatenate([low[:share, :] for low in lows], axis=1)
        value_low = jnp.concatenate([low[share:, :] for low in lows], axis=1)
        tokens_own = jnp.concatenate([t[:block, :] for t in tokens], axis=0)
        sums[...] = query_sum[...]
        sums[1:2, :] = total(value_low)
        grads.put_sums(3 * narrow, sums[...])
        grads.put(0, dot_tn(tokens_own, key_low))
        grads.put(1, dot_tn(tokens_own, value_low))
        grad = in_part[...] + dot_nt(key_low, key_w[...]) + dot_nt(value_low, value_w[...])
        in_own[...] = grad[:block, :]
        in_send[:block, :] = grad[block:, :].astype(BF16)
        in_send[block:, :] = memory_send[...]

    outs = [((block, width), F32), ((block + memory_block, width), BF16)]
    if packed:
        outs += [((16, 3 * narrow + 8, width), BF16)] * 2
    else:
        outs += [((width, width), F32)] * 2 + [((8, width), F32)]
    scratch = [((8, width), F32)]
    if packed:
        scratch += [((width, width), BF16)] * 2 + [((width, width), F32)]
    return kernel, outs, scratch


def combine(arrays, splits, micros=0.1):
    count = arrays[0].shape[0] // splits
    shape = (count,) + arrays[0].shape[1:]

    def kernel(*refs):
        given, outs = refs[: len(arrays)], refs[len(arrays) :]
        for i, out in enumerate(outs):
            here = slice(i * count, (i + 1) * count)
            found = given[0][here].astype(F32)
            for ref in given[1:]:
                found = found + ref[here].astype(F32)
            out[...] = found.astype(out.dtype)

    return pl.pallas_call(
        kernel,
        out_shape=[jax.ShapeDtypeStruct(shape, BF16)] * splits,
        in_specs=[VM] * len(arrays),
        out_specs=[VM] * splits,
        compiler_params=pltpu.CompilerParams(vmem_limit_bytes=snug(arrays)),
        cost_estimate=pl.CostEstimate(flops=int(micros * 1.15e9), bytes_accessed=0, transcendentals=0),
        name="combine",
    )(*arrays)


def combine_joint(groups, splits):
    count, sizes = groups[0][0].shape[0] // splits, [g[0].shape[1] for g in groups]
    shape = (count, sum(sizes)) + groups[0][0].shape[2:]
    flat = [a for group in groups for a in group]

    def kernel(*refs):
        outs, at, row = refs[len(flat) :], 0, 0
        for group, size in zip(groups, sizes):
            given = refs[at : at + len(group)]
            at += len(group)
            for i, out in enumerate(outs):
                here = slice(i * count, (i + 1) * count)
                found = given[0][here].astype(F32)
                for ref in given[1:]:
                    found = found + ref[here].astype(F32)
                out[:, row : row + size, :] = found.astype(BF16)
            row += size

    return pl.pallas_call(
        kernel,
        out_shape=[jax.ShapeDtypeStruct(shape, BF16)] * splits,
        in_specs=[VM] * len(flat),
        out_specs=[VM] * splits,
        compiler_params=pltpu.CompilerParams(vmem_limit_bytes=snug(flat)),
        cost_estimate=pl.CostEstimate(flops=1, bytes_accessed=1, transcendentals=0),
        name="combine_joint",
    )(*flat)


def chosen(me, rows, wide):
    width = rows.shape[1]
    line = lax.broadcasted_iota(jnp.int32, (width, wide), 0)
    here = lax.broadcasted_iota(jnp.int32, (width, wide), 1) + me * wide
    choice = jnp.where(line == here, 1.0, 0.0)
    return lax.dot_general(rows, choice, (((1,), (0,)), ((), ())), precision=lax.Precision.HIGHEST, preferred_element_type=F32)


def reduce_all(array, devices):
    mask = 1
    while mask < devices:
        array = array + swap(array, mask, devices)
        mask *= 2
    return array


def per_device(
    tokens, memory, target_ids, source_ids, cotangent,
    query_weight, key_weight, value_weight, output_weight, query_bias, value_bias, output_bias,
    attention_gain, attention_shift,
    source_query, source_key, source_value, source_output, source_query_bias, source_value_bias,
    source_output_bias, source_gain, source_shift,
    inner_weight, inner_bias, outer_weight, outer_bias, final_gain, final_shift,
    *, devices, sequence,
):
    packed = devices == 32
    rows, block, width = tokens.shape
    memory_block = memory.shape[1]
    parts = sequence // rows
    share, memory_share = rows * block, rows * memory_block
    hidden = inner_weight.shape[1]
    blocks = hidden // width
    me = lax.axis_index(AXES)
    me_array = me.reshape(1).astype(jnp.int32)
    turn = lax.rem(lax.div(me, parts), rows)
    narrow, wide = width // devices, hidden // devices

    def run(made, micros, name, *args, room=10):
        kernel, outs, *scratch = made
        return call(kernel, outs, (me_array,) + args, scratch[0] if scratch else [], micros, name, room)

    short = [query_bias, value_bias, output_bias, attention_gain, attention_shift, source_query_bias,
             source_value_bias, source_output_bias, source_gain, source_shift, outer_bias, final_gain,
             final_shift]

    def whole(array):
        return lax.all_gather(array, AXES, axis=0, tiled=True)

    sent, kept = tokens_packet(
        turn.reshape(1).astype(jnp.int32), tokens, memory, target_ids, source_ids, cotangent
    )
    came = swap(sent, parts, devices)
    row_tokens = [kept, came]
    kept_swaps = [swap(kept, m, devices) for m in range(1, parts)]
    came_swaps = [swap(came, m, devices) for m in range(1, parts)]
    for pair in zip(kept_swaps, came_swaps):
        row_tokens += pair
    own_tokens = row_tokens[:rows]

    if packed:
        first, second, third = run(make_weights_packet(narrow, width, blocks), 1.0, "weights_packet",
                          query_weight, key_weight, value_weight, output_weight, source_query,
                          source_key, source_value, source_output, inner_weight, outer_weight,
                          inner_bias.reshape(1, wide), *[v.reshape(1, narrow) for v in short], room=58)
        first = after(first, sent)
        first = join([first, turned_swap(first, 0)])
        first_b = turned_swap(first, 1)
        second = after(second, first)
        second_b = turned_swap(second, 0)
        first, second = join(after([first, first_b], second_b)), join(after([second, second_b], first_b))
        third = after(third, second)
        first_b, second_b, third_b = turned_swap(first, 2), turned_swap(second, 1), turned_swap(third, 0)
        first_c = join(after([first, first_b], second_b, third_b, came, *kept_swaps))
        second = join(after([second, second_b], first_b, third_b))
        third = join(after([third, third_b], first_b, second_b))
        first_d, second_b, third_b = turned_swap(first_c, 3), turned_swap(second, 2), turned_swap(third, 1)
        second_c = join(after([second, second_b], first_d, third_b))
        third = join(after([third, third_b], first_d, second_b))
        first_d = after(first_d, second_c, third, *came_swaps)
        second_d, third_b = turned_swap(second_c, 3), turned_swap(third, 2)
        set_self = [first_c, first_d, swap(first_c, 1, 32), swap(first_d, 1, 32)]
    else:
        full = [whole(w) for w in (query_weight, key_weight, value_weight, output_weight, source_query, source_key, source_value, source_output)]
        lane = lax.broadcasted_iota(jnp.int32, (1, width), 1)
        place = lax.broadcasted_iota(jnp.int32, (blocks, width), 0) * width + lane
        spread_wide = jnp.where(place // wide == me, jnp.tile(inner_bias.reshape(1, wide), (blocks, width // wide)), 0)

        def natural(rows):
            return jnp.where(lane // narrow == me, jnp.tile(rows, (1, devices)), 0)

        vectors = jnp.concatenate([natural(jnp.stack(short[:2])), jnp.zeros((6, width), BF16), natural(jnp.stack(short[2:])), spread_wide, jnp.zeros((1, width), BF16)])
        vectors = reduce_all(vectors, devices).astype(F32)
        set_self = full[:3] + [vectors]
        set_cross = full[3:]
        set_inner = [
            whole(inner_weight).reshape(width, blocks, width).transpose(1, 0, 2),
            whole(outer_weight).reshape(blocks, width, width),
        ]
    found = run(
        make_project(packed, parts, rows, block, memory_block, width, narrow, blocks, len(set_self)), 5.0,
        "project", *set_self, *row_tokens,
    )
    query, query_t, keys, values, value_t = (found[2 * i : 2 * i + 2] for i in range(5))
    row_memory, ids, memory_ids, vectors = found[10:]
    query_t = list(query_t)
    if packed:
        set_query, set_last = set_self, set_self
    else:
        set_back, set_query, set_last, set_memory = [full[3], full[4], full[7]], full[:1], full[1:3], full[5:7]
    found = run(
        make_self_attention(share, parts * share, width), 12.0, "self_attention",
        *query_t, *keys, *value_t, ids,
    )
    mixtures, logs = found[:2], found[2:]
    if packed:
        third_c = join(after([third, third_b], mixtures[0]))
        third_d = turned_swap(third_c, 3)
        second_d = after(second_d, mixtures[0])
        set_cross = [second_c, second_d, swap(second_c, 1, 32), swap(second_d, 1, 32)]
        set_back, set_memory = set_cross, set_cross
    first_sum, second_sum, cross_query, memory_keys, memory_values, cross_t, cross_logs = run(
        make_cross_forward(packed, rows, block, parts * memory_share, width, narrow, len(set_cross)),
        9.0, "cross_forward", *set_cross, *own_tokens, row_memory, ids, memory_ids, *mixtures, vectors,
    )
    if packed:
        third_d = after(third_d, second_sum)
        set_inner = [third_c, third_d, swap(third_c, 1, 32), swap(third_d, 1, 32)]
    out_own, out_send, back2_in, sums_inner, *grads_inner = run(
        make_inner(packed, rows, block, width, hidden, narrow, len(set_inner)), 18.0, "inner",
        *set_inner, second_sum, kept, came, vectors,
    )
    out_came = swap(out_send, parts, devices)
    found = run(
        make_cross_back(packed, parts, share, memory_share, width, narrow, len(set_back)), 14.0,
        "cross_back", *set_back, back2_in, first_sum, second_sum, cross_query, memory_keys,
        memory_values, cross_t, cross_logs, ids, memory_ids, vectors, sums_inner, *mixtures,
    )
    back1, memory_key_own, memory_value_own, sums_cross = found[:4]
    slope, slope_t, deltas = (found[4 + 2 * i : 6 + 2 * i] for i in range(3))
    memory_received = [swap(a, m + 1, devices) for m, a in enumerate(found[10 : 10 + parts - 1])]
    grads_early = found[10 + parts - 1 :]
    query = list(query)
    if packed:
        keep, send = combine(after([grads_inner[0], swap(grads_inner[1], 1, 32)], back1, out_came), 2)
        inner_step = [keep, turned_swap(send, 3)]
        memory_key_own = after(memory_key_own, keep)
    memory_own, memory_send, *grads_cross = run(
        make_memory_back(packed, parts, rows, block, memory_block, width, narrow, len(set_memory)),
        2.0, "memory_back", *set_memory, *own_tokens, memory_key_own, memory_value_own, sums_cross,
        *grads_early, *memory_received,
    )
    if packed:
        cross_came = swap(grads_cross[1], 1, 32)
        query[0] = after(query[0], grads_cross[0])
    found = run(
        make_self_back_upper(parts, share, width), 7.0, "self_back_upper", query[0], keys[0],
        values[0], slope[0], slope_t[0], logs[0], deltas[0], ids,
    )
    query_upper, own_upper = found[:2]
    received_upper = [swap(a, m // 2 + 1, devices) for m, a in enumerate(found[2:])]
    if packed:
        keep_cross, send = combine(after([grads_cross[0], cross_came], query_upper), 2)
        cross_step = [keep_cross, turned_swap(send, 3, CROSSED)]
        query[1] = after(query[1], keep_cross)
    in_part, query_sum, query_w_grad, own_lower, *sends = run(
        make_self_back_lower(packed, parts, rows, block, width, narrow, len(set_query)), 11.0,
        "self_back_lower", *set_query, *own_tokens, query[1], keys[1], values[1], slope[1],
        slope_t[1], logs[1], deltas[1], ids, back1, query_upper,
    )
    received_lower = [swap(a, m // 2 + 1, devices) for m, a in enumerate(sends)]
    if packed:
        keep, send = combine(after(inner_step, query_sum), 2)
        inner_step = [keep, turned_swap(send, 2)]
        keep_cross, send = combine(after(cross_step, query_sum), 2)
        cross_step = [keep_cross, turned_swap(send, 2, CROSSED)]
        in_part = after(in_part, keep, keep_cross)
    in_own, in_send, *grads_last = run(
        make_last(packed, parts, rows, block, memory_block, width, narrow, len(set_last)), 6.0,
        "last", *set_last, *own_tokens, in_part, query_sum, query_w_grad, memory_send, own_upper,
        own_lower, *received_upper, *received_lower,
    )

    if packed:
        keep, send = combine([grads_last[0], swap(grads_last[1], 1, 32)], 2)
        last_step = [keep, turned_swap(send, 3)]
        in_send = after(in_send, last_step[1])
        keep, send = combine(last_step, 2)
        last_step = [keep, turned_swap(send, 2)]
        keep_joint, send = combine_joint(after([inner_step, cross_step], in_own, keep), 2)
        joint_step = [keep_joint, turned_swap(send, 1)]
        keep_joint, send = combine(joint_step, 2)
        joint_step = [keep_joint, turned_swap(send, 0)]
        keep, send = combine(after(last_step, keep_joint), 2)
        last_step = [keep, turned_swap(send, 1)]
        keep, send = combine(last_step, 2)
        last_step = [keep, turned_swap(send, 0)]

        def plan(me_ref, *refs):
            me = me_ref[0]
            joint, last = (sum(r[0].astype(F32) for r in given) for given in (refs[:2], refs[2:4]))
            outs = refs[4:]
            inner, cross = joint[: 2 * blocks * narrow, :], joint[2 * blocks * narrow :, :]
            for i in range(blocks):
                outs[0][:, i * width : (i + 1) * width] = inner[i * narrow : (i + 1) * narrow, :]
            outs[1][...] = inner[blocks * narrow :, :]
            for i in range(5):
                outs[2 + i][...] = cross[i * narrow : (i + 1) * narrow, :]
            for i in range(3):
                outs[7 + i][...] = last[i * narrow : (i + 1) * narrow, :]
            rows_in = jnp.concatenate([cross[5 * narrow :, :], last[3 * narrow :, :]], axis=0)
            outs[10][...] = chosen(me, rows_in, narrow)
            per = width // wide
            line = lax.broadcasted_iota(jnp.int32, (blocks, width), 0)
            row = jnp.sum(jnp.where(line == lax.div(me, per), rows_in[3 : 3 + blocks, :], 0.0), axis=0, keepdims=True)
            outs[11][...] = chosen(lax.rem(me, per), row, wide)

        part = (narrow, width)
        shapes = [(narrow, hidden), (wide, width)] + [part] * 8 + [(24, narrow), (1, wide)]
        (inner_share, outer_share, source_key_share, source_value_share, source_output_share,
         source_query_share, output_share, key_share, value_share, query_share, sums,
         inner_bias_share) = call(
            plan, [(s, F32) for s in shapes], (me_array, *joint_step, *last_step), [], 2.0,
            "finish",
        )
        inner_bias_share = inner_bias_share.reshape(wide)
    else:
        def scatter(array):
            return lax.psum_scatter(array, AXES, scatter_dimension=0, tiled=True)

        inner_share = scatter(grads_inner[0].transpose(1, 0, 2).reshape(width, hidden))
        outer_share = scatter(grads_inner[1].reshape(hidden, width))
        source_output_share, source_query_share, output_share = (scatter(g.astype(F32)) for g in grads_early)
        source_key_share, source_value_share = (scatter(g) for g in grads_cross[:2])
        key_share, value_share = (scatter(g) for g in grads_last[:2])
        query_share = scatter(query_w_grad)
        sums = reduce_all(jnp.concatenate([grads_cross[2], grads_last[2]], axis=0), devices)
        inner_bias_share = lax.dynamic_slice(sums[3 : 3 + blocks].reshape(hidden), (me * wide,), (wide,))
        sums = lax.dynamic_slice(sums, (0, me * narrow), (sums.shape[0], narrow))
    def regroup(mine, came):
        came = came.astype(F32)
        return jnp.where(turn == 0, jnp.stack([mine, came]), jnp.stack([came, mine]))

    output = regroup(out_own, out_came)
    in_came = swap(in_send, parts, devices)
    input_gradient = regroup(in_own, in_came[:block])
    memory_gradient = regroup(memory_own, in_came[block:])

    return (
        output,
        input_gradient,
        memory_gradient,
        query_share,
        key_share,
        value_share,
        output_share,
        sums[16],
        sums[17],
        sums[13],
        sums[11],
        sums[12],
        source_query_share,
        source_key_share,
        source_value_share,
        source_output_share,
        sums[10],
        sums[14],
        sums[9],
        sums[7],
        sums[8],
        inner_share,
        inner_bias_share,
        outer_share,
        sums[2],
        sums[0],
        sums[1],
    )


def solution(mesh):
    sequence, devices = mesh.shape["seq"], mesh.size
    tokens, ids = P("dp", "seq", None), P("dp", "seq")
    matrix, vector = P(AXES, None), P(AXES)
    attention = (matrix,) * 4 + (vector,) * 5
    inner = (matrix, vector, matrix, vector, vector, vector)
    return jax.shard_map(
        functools.partial(per_device, devices=devices, sequence=sequence),
        mesh=mesh,
        in_specs=(tokens, tokens, ids, ids, tokens) + attention + attention + inner,
        out_specs=(tokens, tokens, tokens) + attention + attention + inner,
        check_vma=False,
    )
```

```python
import functools
import math

import jax
import jax.numpy as jnp
from jax import lax
from jax.experimental import pallas as pl
from jax.experimental.pallas import tpu as pltpu
from jax.sharding import PartitionSpec as P

HEADS = 8
HEAD_DIM = 64
PAIR = 128
EPSILON = 1e-05
MASKED = 1e9
AXES = ("dp", "seq")
F32 = jnp.float32
BF16 = jnp.bfloat16

(
    OUTPUT_BIAS,
    ATTENTION_GAIN,
    ATTENTION_SHIFT,
    SOURCE_QUERY_BIAS,
    SOURCE_VALUE_BIAS,
    SOURCE_OUTPUT_BIAS,
    SOURCE_GAIN,
    SOURCE_SHIFT,
    OUTER_BIAS,
    FINAL_GAIN,
    FINAL_SHIFT,
    INNER_BIAS,
) = range(12)
Z_MASKS = (0, 8, 16, 24)
VM = pl.BlockSpec(memory_space=pltpu.VMEM)
SM = pl.BlockSpec(memory_space=pltpu.SMEM)


def dot(a, b):
    return lax.dot_general(a, b, (((1,), (0,)), ((), ())), preferred_element_type=F32)


def dot_nt(a, b):
    return lax.dot_general(a, b, (((1,), (1,)), ((), ())), preferred_element_type=F32)


def dot_tn(a, b):
    return lax.dot_general(a, b, (((0,), (0,)), ((), ())), preferred_element_type=F32)


def total(values):
    return jnp.sum(values.astype(F32), axis=0, keepdims=True)


def normalize(h):
    average = jnp.mean(h, axis=-1, keepdims=True)
    centered = h - average
    variance = jnp.mean(centered * centered, axis=-1, keepdims=True)
    inverse = lax.rsqrt(variance + EPSILON)
    return centered * inverse, inverse


def normalize_back(upstream, normed, inverse, gain):
    scaled = upstream * gain
    first_mean = jnp.mean(scaled, axis=-1, keepdims=True)
    second_mean = jnp.mean(scaled * normed, axis=-1, keepdims=True)
    return inverse * (scaled - first_mean - normed * second_mean)


def normal_parts(v):
    density = 0.3989422804014327 * jnp.exp(-0.5 * v * v)
    t = 1.0 / (1.0 + 0.2316419 * jnp.abs(v))
    series = t * (
        0.319381530
        + t * (-0.356563782 + t * (1.781477937 + t * (-1.821255978 + t * 1.330274429)))
    )
    tail = density * series
    return jnp.where(v >= 0.0, 1.0 - tail, tail), density


def penalties(ids):
    place = lax.broadcasted_iota(jnp.int32, (PAIR, ids.shape[1]), 0)
    return jnp.where((place == ids) | (place >= 4), 0.0, -MASKED).astype(BF16)


def one_hot(ids):
    place = lax.broadcasted_iota(jnp.int32, (PAIR, ids.shape[1]), 0)
    return jnp.where(place == ids, 1.0, 0.0).astype(F32).T.astype(BF16)


def spread(part, half):
    empty = jnp.zeros_like(part)
    return [part, empty] if half == 0 else [empty, part]


def attend(query_t, keys, value_t, hot, penalty, mixture_t, logs):
    length = keys.shape[0]

    def pair(p, carry):
        columns = pl.ds(pl.multiple_of(p * PAIR, PAIR), PAIR)
        left = jnp.concatenate([keys[:, columns], hot[...]], axis=1)
        for half in range(2):
            rows = pl.ds(pl.multiple_of(p * PAIR + half * HEAD_DIM, HEAD_DIM), HEAD_DIM)
            right = jnp.concatenate(spread(query_t[rows, :], half) + [penalty[...]], axis=0)
            scores = dot(left, right)
            highest = jnp.max(scores, axis=0, keepdims=True)
            weights = jnp.exp(scores - highest).astype(BF16)
            values = jnp.concatenate(
                [value_t[rows, :], jnp.ones((16, length), BF16)], axis=0
            )
            found = dot(values, weights)
            denominator = found[HEAD_DIM : HEAD_DIM + 1, :]
            mixture_t[rows, :] = (found[:HEAD_DIM, :] / denominator).astype(BF16)
            logs[2 * p + half] = highest + jnp.log(denominator)
        return carry

    lax.fori_loop(0, keys.shape[1] // PAIR, pair, 0)


def attend_back(
    query_t, query, keys, key_t, values, slope_t, slope, hot, penalty, logs, deltas,
    query_grad_t, key_grad, value_grad,
):
    tokens = query.shape[0]
    lane = lax.broadcasted_iota(jnp.int32, (tokens, PAIR), 1)

    def pair(p, carry):
        columns = pl.ds(pl.multiple_of(p * PAIR, PAIR), PAIR)
        left = jnp.concatenate([keys[:, columns], hot[...]], axis=1)
        value_pair = values[:, columns]
        key_sum, value_sum = None, None
        for half in range(2):
            rows = pl.ds(pl.multiple_of(p * PAIR + half * HEAD_DIM, HEAD_DIM), HEAD_DIM)
            right = jnp.concatenate(spread(query_t[rows, :], half) + [penalty[...]], axis=0)
            chances = jnp.exp(dot(left, right) - logs[2 * p + half])
            slopes = dot(value_pair, jnp.concatenate(spread(slope_t[rows, :], half), axis=0))
            grads = (chances * (slopes - deltas[2 * p + half])).astype(BF16)
            query_grad_t[rows, :] = dot(key_t[rows, :], grads) * HEAD_DIM**-0.5
            mine = (lane < HEAD_DIM) if half == 0 else (lane >= HEAD_DIM)
            none = jnp.zeros((tokens, PAIR), BF16)
            value_part = dot(chances.astype(BF16), jnp.where(mine, slope[:, columns], none))
            key_part = dot(grads, jnp.where(mine, query[:, columns], none))
            value_sum = value_part if value_sum is None else value_sum + value_part
            key_sum = key_part if key_sum is None else key_sum + key_part
        key_grad[:, columns] = key_sum
        value_grad[:, columns] = value_sum
        return carry

    lax.fori_loop(0, keys.shape[1] // PAIR, pair, 0)


def deltas_of(slope_t, mixture_t, deltas):
    for head in range(slope_t.shape[0] // HEAD_DIM):
        rows = slice(head * HEAD_DIM, (head + 1) * HEAD_DIM)
        deltas[head] = jnp.sum(
            slope_t[rows, :].astype(F32) * mixture_t[rows, :].astype(F32), axis=0, keepdims=True
        )


def swap(array, mask, devices):
    return lax.ppermute(array, AXES, [(i, i ^ mask) for i in range(devices)])


Z_FIRST = ((8, 24, 2, 4), (24, 8, 4, 2))
CROSSED = ((8, 24, 4, 2), (24, 8, 2, 4))


def turned_swap(array, step, orders=Z_FIRST):
    return lax.ppermute(array, AXES, [(i, i ^ orders[i % 2][step]) for i in range(32)])


def after(value, *others):
    return lax.optimization_barrier((value, others))[0]


def places(me, orders=Z_FIRST):
    found = []
    for core in range(2):
        even = ((me & 1) ^ core) == 0
        masks = [jnp.where(even, first, second) for first, second in zip(*orders)]
        for far in range(2):
            for slot in range(8):
                device = me ^ core if core else me
                for step, bit in enumerate((slot & 1, slot & 2, slot & 4, far)):
                    if bit:
                        device = device ^ masks[step]
                found.append((core, far, slot, device))
    return found


def unpack(me, pieces, stride, first, rows, scratch, orders=Z_FIRST):
    for core, far, slot, device in places(me, orders):
        ref = pieces[2 * core + far]
        at = slot * stride + first
        scratch[pl.ds(pl.multiple_of(device * rows, rows), rows), :] = ref[at : at + rows, :]


def sort_vectors(me, pieces, stride, first, narrow, sheet):
    width, blocks = sheet.shape[1], sheet.shape[0]
    lane = lax.broadcasted_iota(jnp.int32, (8, width), 1)
    per = width // (blocks * narrow)
    near, far = jnp.zeros((8, width), F32), jnp.zeros((8, width), F32)
    sheet[...] = jnp.zeros_like(sheet)
    for core, distant, slot, device in places(me):
        part = pieces[2 * core + distant][slot * stride + first : (slot + 1) * stride, :].astype(F32)
        group = lane // narrow
        near = near + jnp.where(group == device, part, 0.0)
        far = far + jnp.where(group == lax.rem(device + 1, width // narrow), part, 0.0)
        wide = jnp.where(lane[7:8, :] // (blocks * narrow) == lax.rem(device, per), part[7:8, :], 0.0)
        sheet[pl.ds(lax.div(device, per), 1), :] += wide
    far = pltpu.roll(far, width - narrow, 1)
    return jnp.concatenate([near[:7, :], far[:6, :]], axis=0)


class Grads:
    def __init__(self, me, refs, dense, rows, orders=Z_FIRST):
        self.me, self.refs, self.dense, self.rows, self.orders = me, refs, dense, rows, orders

    def put(self, index, grad):
        if self.dense is None:
            self.refs[index][...] = grad
            return
        self.dense[...] = grad
        rows = self.rows
        for core, far, slot, device in places(self.me, self.orders):
            found = self.dense[pl.ds(pl.multiple_of(device * rows, rows), rows), :]
            self.refs[core][far * 8 + slot, index * rows : (index + 1) * rows, :] = found.astype(BF16)

    def put_sums(self, first, sums):
        if self.dense is None:
            self.refs[-1][...] = sums
            return
        low = sums.astype(BF16)
        for ref in self.refs:
            for slot in range(16):
                ref[slot, first : first + sums.shape[0], :] = low


def grad_outs(packed, count, rows, width, sums):
    if packed:
        return [((16, count * rows + sums, width), BF16)] * 2
    return [((width, width), F32)] * count + [((sums, width), F32)]


COSTS = {}


def padded(shape, dtype):
    last = -(-shape[-1] // 128) * 128
    tall = -(-shape[-2] // 16) * 16 if len(shape) > 1 else 16
    return math.prod(shape[:-2]) * tall * last * jnp.dtype(dtype).itemsize


def snug(arrays):
    return 2 * sum(padded(a.shape, a.dtype) for a in arrays) + (3 << 20)


def call(kernel, outs, args, scratch, micros, name, room=10):
    moved = sum(math.prod(a.shape) * a.dtype.itemsize for a in args[1:])
    moved += sum(math.prod(s) * jnp.dtype(d).itemsize for s, d in outs)
    need = sum(padded(a.shape, a.dtype) for a in args[1:])
    need += sum(padded(s, d) for s, d in list(outs) + list(scratch))
    return pl.pallas_call(
        kernel,
        out_shape=[jax.ShapeDtypeStruct(s, d) for s, d in outs],
        in_specs=[SM] + [VM] * (len(args) - 1),
        out_specs=[VM] * len(outs),
        scratch_shapes=[pltpu.VMEM(s, d) for s, d in scratch],
        compiler_params=pltpu.CompilerParams(vmem_limit_bytes=min(need + (room << 20), 58 << 20)),
        cost_estimate=pl.CostEstimate(
            flops=int(COSTS.get(name, 0) * 1.15e9) + 1, bytes_accessed=1, transcendentals=0
        ),
        name=name,
    )(*args)


def tokens_packet(turn, tokens, memory, target_ids, source_ids, cotangent):
    block, width = tokens.shape[1:]
    memory_block = memory.shape[1]
    first = block + memory_block + 8

    def kernel(turn_ref, targets, sources, tokens_ref, memory_ref, cot_ref, sent, kept):
        mine = turn_ref[0]
        for row, out in ((1 - mine, sent), (mine, kept)):
            out[:block, :] = tokens_ref[row]
            out[block : block + memory_block, :] = memory_ref[row]
            ids = targets[pl.ds(row, 1), :].astype(F32)
            ids = jnp.concatenate([ids, jnp.zeros((1, width - block), F32)], axis=1)
            others = sources[pl.ds(row, 1), :].astype(F32)
            others = jnp.concatenate([others, jnp.zeros((1, width - memory_block), F32)], axis=1)
            place = lax.broadcasted_iota(jnp.int32, (8, width), 0)
            found = jnp.where(place == 0, ids, jnp.where(place == 1, others, 0.0))
            out[block + memory_block : first, :] = found.astype(BF16)
            out[first:, :] = cot_ref[row]

    shape = (first + block, width)
    return call(kernel, [(shape, BF16)] * 2, (turn, target_ids, source_ids, tokens, memory, cotangent),
                [], 1.0, "tokens_packet", 58)


def placed(me, parts, width):
    here = lax.broadcasted_iota(jnp.int32, (parts.shape[1], width), 0) + me * parts.shape[1]
    lane = lax.broadcasted_iota(jnp.int32, (parts.shape[1], width), 1)
    return dot(parts, jnp.where(lane == here, 1.0, 0.0).astype(BF16))


def make_weights_packet(narrow, width, blocks):
    tall = blocks * narrow

    def kernel(me_ref, *refs):
        weights, inner, outer, wide, short = refs[:8], refs[8], refs[9], refs[10], refs[11:24]
        first, second, third = refs[24:]
        me = me_ref[0]
        for i, ref in enumerate(weights):
            if i < 3:
                first[i * narrow : (i + 1) * narrow, :] = ref[...]
            else:
                second[(i - 3) * narrow : (i - 2) * narrow, :] = ref[...]
        short = jnp.concatenate([ref[...].astype(F32) for ref in short], axis=0).astype(BF16)
        near = placed(me, short[:7, :], width)
        far = placed(lax.rem(me + 1, width // narrow), short[7:, :], width)
        far = jnp.concatenate([far, jnp.zeros((1, width), F32)], axis=0)
        row = placed(lax.rem(me, width // wide.shape[1]), wide[...], width)
        first[3 * narrow :, :] = jnp.concatenate([near + far, row], axis=0).astype(BF16)
        for i in range(blocks):
            third[i * narrow : (i + 1) * narrow, :] = inner[:, i * width : (i + 1) * width]
        third[tall:, :] = outer[...]

    return kernel, [((rows, width), BF16) for rows in (3 * narrow + 8, 5 * narrow, 2 * tall)]


def join(arrays):
    def kernel(*refs):
        at = 0
        for ref in refs[:-1]:
            refs[-1][at : at + ref.shape[0], :] = ref[...]
            at += ref.shape[0]

    rows = sum(a.shape[0] for a in arrays)
    return pl.pallas_call(
        kernel,
        out_shape=jax.ShapeDtypeStruct((rows, arrays[0].shape[1]), arrays[0].dtype),
        in_specs=[VM] * len(arrays),
        out_specs=VM,
        compiler_params=pltpu.CompilerParams(vmem_limit_bytes=snug(arrays)),
        cost_estimate=pl.CostEstimate(flops=1 << 20, bytes_accessed=0, transcendentals=0),
        name="join",
    )(*arrays)


def make_project(packed, parts, rows, block, memory_block, width, narrow, blocks, n_pieces):
    share = rows * block
    length = parts * share
    memory_share = rows * memory_block
    stride = 3 * narrow + 8
    half = width // 2

    def kernel(*refs):
        me_ref, refs = refs[0], list(refs[1:])
        pieces, refs = refs[:n_pieces], refs[n_pieces:]
        tokens, refs = refs[: parts * rows], refs[parts * rows :]
        query, query_t, keys, values, value_t = (refs[2 * i : 2 * i + 2] for i in range(5))
        memory, ids, memory_ids, vectors = refs[10:14]
        scratch = refs[14:]
        me = me_ref[0]
        if packed:
            for i in range(3):
                unpack(me, pieces, stride, i * narrow, narrow, scratch[i])
            query_w, key_w, value_w, sheet = scratch
            biases = sort_vectors(me, pieces, stride, 3 * narrow, narrow, sheet)
            rest = jnp.zeros((5 - sheet.shape[0], width), F32)
            vectors[...] = jnp.concatenate([biases[2:, :], sheet[...], rest], axis=0)
        else:
            query_w, key_w, value_w = pieces[:3]
            biases = pieces[3][:8, :]
            vectors[...] = pieces[3][8:, :]
        for i in range(parts):
            here = slice(i * share, (i + 1) * share)
            some = tokens[i * rows : (i + 1) * rows]
            own = jnp.concatenate([t[:block, :] for t in some], axis=0)
            if i == 0:
                scaled = (dot(own, query_w[...]) + biases[0:1, :]).astype(BF16) * BF16(HEAD_DIM**-0.5)
            key = dot(own, key_w[...]).astype(BF16)
            found = (dot(own, value_w[...]) + biases[1:2, :]).astype(BF16)
            for side in range(2):
                columns = slice(side * half, (side + 1) * half)
                if i == 0:
                    query[side][...] = scaled[:, columns]
                    query_t[side][...] = scaled[:, columns].T
                keys[side][here, :] = key[:, columns]
                values[side][here, :] = found[:, columns]
                value_t[side][:, here] = found[:, columns].T
        for i, t in enumerate(tokens):
            memory[i * memory_block : (i + 1) * memory_block, :] = t[block : block + memory_block, :]
            found = t[block + memory_block : block + memory_block + 8, :].astype(F32).astype(jnp.int32)
            ids[:, i * block : (i + 1) * block] = found[0:1, :block]
        found = [t[block + memory_block : block + memory_block + 8, :].astype(F32).astype(jnp.int32)[1:2, :memory_block] for t in tokens]
        memory_ids[...] = jnp.concatenate(found, axis=1)

    outs = [((share, half), BF16)] * 2 + [((half, share), BF16)] * 2
    outs += [((length, half), BF16)] * 4 + [((half, length), BF16)] * 2
    outs += [
        ((parts * memory_share, width), BF16),
        ((1, length), jnp.int32),
        ((1, parts * memory_share), jnp.int32),
        ((16, width), F32),
    ]
    return kernel, outs, [((width, width), BF16)] * 3 + [((blocks, width), F32)] if packed else []


def make_self_attention(share, length, width):
    def kernel(me_ref, *refs):
        query_t, keys, value_t, ids = refs[:2], refs[2:4], refs[4:6], refs[6]
        mixture_t, logs, hot, penalty = refs[7:9], refs[9:11], refs[11], refs[12]
        hot[...] = one_hot(ids[...])
        penalty[...] = penalties(ids[:, :share])
        for side in range(2):
            attend(query_t[side], keys[side], value_t[side], hot, penalty, mixture_t[side], logs[side])

    outs = [((width // 2, share), BF16)] * 2 + [((HEADS // 2, 1, share), F32)] * 2
    return kernel, outs, [((length, PAIR), BF16), ((PAIR, share), BF16)]


def make_cross_forward(packed, rows, block, memory_length, width, narrow, n_pieces):
    share = rows * block
    stride = 5 * narrow

    def kernel(*refs):
        me_ref, refs = refs[0], list(refs[1:])
        pieces, refs = refs[:n_pieces], refs[n_pieces:]
        tokens, refs = refs[:rows], refs[rows:]
        memory, ids, memory_ids, upper, lower, vectors = refs[:6]
        first_sum, second_sum, query, memory_keys, memory_values, cross_t, logs = refs[6:13]
        scratch = refs[13:]
        query_t, value_t, hot, penalty = scratch[:4]
        if packed:
            for i in range(5):
                unpack(me_ref[0], pieces, stride, i * narrow, narrow, scratch[4 + i])
            output_w, query_w, key_w, value_w, source_w = scratch[4:]
        else:
            output_w, query_w, key_w, value_w, source_w = pieces[:5]

        def vector(i):
            return vectors[i : i + 1, :]

        own = jnp.concatenate([t[:block, :] for t in tokens], axis=0)
        mixture_t = jnp.concatenate([upper[...], lower[...]], axis=0)
        h = own.astype(F32) + dot_tn(mixture_t, output_w[...]) + vector(OUTPUT_BIAS)
        first_sum[...] = h
        first = normalize(h)[0] * vector(ATTENTION_GAIN) + vector(ATTENTION_SHIFT)
        scaled = (dot(first.astype(BF16), query_w[...]) + vector(SOURCE_QUERY_BIAS)).astype(BF16) * BF16(HEAD_DIM**-0.5)
        query[...] = scaled
        query_t[...] = scaled.T
        memory_keys[...] = dot(memory[...], key_w[...]).astype(BF16)
        memory_values[...] = (dot(memory[...], value_w[...]) + vector(SOURCE_VALUE_BIAS)).astype(BF16)
        value_t[...] = memory_values[...].T
        hot[...] = one_hot(memory_ids[...])
        penalty[...] = penalties(ids[:, :share])
        attend(query_t, memory_keys, value_t, hot, penalty, cross_t, logs)
        first = normalize(first_sum[...])[0] * vector(ATTENTION_GAIN) + vector(ATTENTION_SHIFT)
        second_sum[...] = first + dot_tn(cross_t[...], source_w[...]) + vector(SOURCE_OUTPUT_BIAS)

    outs = [
        ((share, width), F32),
        ((share, width), F32),
        ((share, width), BF16),
        ((memory_length, width), BF16),
        ((memory_length, width), BF16),
        ((width, share), BF16),
        ((HEADS, 1, share), F32),
    ]
    scratch = [((width, share), BF16), ((width, memory_length), BF16), ((memory_length, PAIR), BF16), ((PAIR, share), BF16)]
    if packed:
        scratch += [((width, width), BF16)] * 5
    return kernel, outs, scratch


def make_inner(packed, rows, block, width, hidden, narrow, n_pieces):
    blocks = hidden // width
    share = rows * block
    per = width // (blocks * narrow)

    def kernel(*refs):
        me_ref, refs = refs[0], list(refs[1:])
        pieces, refs = refs[:n_pieces], refs[n_pieces:]
        second_sum, cot_own, cot_came, vectors = refs[:4]
        out_own, out_send, back, sums = refs[4:8]
        grads, scratch = refs[8:10], refs[10:]
        low, active, gate, slope = scratch[:4]
        if packed:
            inner_w, outer_w, gathered, dense = scratch[4:8]
            tall = blocks * narrow
            for core, far, slot, device in places(me_ref[0]):
                ref, at = pieces[2 * core + far], slot * 2 * tall
                row = pl.multiple_of(device * narrow, narrow)
                for i in range(blocks):
                    inner_w[i, pl.ds(row, narrow), :] = ref[at + i * narrow : at + (i + 1) * narrow, :]
                row = pl.multiple_of(lax.rem(device, per) * tall, tall)
                outer_w[lax.div(device, per), pl.ds(row, tall), :] = ref[at + tall : at + 2 * tall, :]
        else:
            inner_w, outer_w = pieces

        def vector(i):
            return vectors[i : i + 1, :]

        second = normalize(second_sum[...])[0] * vector(SOURCE_GAIN) + vector(SOURCE_SHIFT)
        low[...] = second.astype(BF16)
        back[...] = second + vector(OUTER_BIAS)

        def forward(i, carry):
            inner = dot(low[...], inner_w[i]) + vectors[pl.ds(INNER_BIAS + i, 1), :]
            chance, density = normal_parts(inner)
            found = (inner * chance).astype(BF16)
            active[i] = found
            gate[i] = chance + inner * density
            back[...] += dot(found, outer_w[i])
            return carry

        lax.fori_loop(0, blocks, forward, 0)
        normed, inverse = normalize(back[...])
        final = normed * vector(FINAL_GAIN) + vector(FINAL_SHIFT)
        out_own[...] = final[:block, :]
        out_send[...] = final[block:, :].astype(BF16)
        upstream = jnp.concatenate([cot_own[-block:, :], cot_came[-block:, :]], axis=0).astype(F32)
        sums[0:1, :] = total(upstream * normed)
        sums[1:2, :] = total(upstream)
        back3 = normalize_back(upstream, normed, inverse, vector(FINAL_GAIN))
        slope[...] = back3.astype(BF16)
        sums[2:3, :] = total(slope[...])
        sums[7:8, :] = jnp.zeros_like(sums[7:8, :])
        back[...] = back3

        def backward(i, carry):
            grad = dot_nt(slope[...], outer_w[i]) * gate[i]
            inner_low = grad.astype(BF16)
            sums[pl.ds(3 + i, 1), :] = total(inner_low)
            outer_grad = dot_tn(active[i], slope[...])
            inner_grad = dot_tn(low[...], inner_low)
            back[...] += dot_nt(inner_low, inner_w[i])
            if packed:
                dense[...] = inner_grad
                gathered[i] = outer_grad.astype(BF16)
                here = pl.ds(pl.multiple_of(i * narrow, narrow), narrow)
                for core, far, slot, device in places(me_ref[0]):
                    row = pl.multiple_of(device * narrow, narrow)
                    grads[core][far * 8 + slot, here, :] = dense[pl.ds(row, narrow), :].astype(BF16)
            else:
                grads[0][i] = inner_grad
                grads[1][i] = outer_grad
            return carry

        lax.fori_loop(0, blocks, backward, 0)
        if packed:
            tall = blocks * narrow
            for core, far, slot, device in places(me_ref[0]):
                row = pl.multiple_of(lax.rem(device, per) * tall, tall)
                grads[core][far * 8 + slot, tall:, :] = gathered[lax.div(device, per), pl.ds(row, tall), :]

    outs = [((block, width), F32), ((block, width), BF16), ((share, width), F32), ((8, width), F32)]
    if packed:
        outs += [((16, 2 * blocks * narrow, width), BF16)] * 2
    else:
        outs += [((blocks, width, width), F32)] * 2
    scratch = [((share, width), BF16), ((blocks, share, width), BF16), ((blocks, share, width), F32), ((share, width), BF16)]
    if packed:
        scratch += [((blocks, width, width), BF16)] * 3 + [((width, width), F32)]
    return kernel, outs, scratch


def make_cross_back(packed, parts, share, memory_share, width, narrow, n_pieces):
    memory_length = parts * memory_share
    stride = 5 * narrow

    def kernel(*refs):
        me_ref, refs = refs[0], list(refs[1:])
        pieces, refs = refs[:n_pieces], refs[n_pieces:]
        (back2_in, first_sum, second_sum, query, memory_keys, memory_values, cross_t, logs, ids,
         memory_ids, vectors, sums_inner) = refs[:12]
        mixtures, refs = refs[12:14], refs[14:]
        back1, key_own, value_own, sums = refs[:4]
        self_slope, self_slope_t, self_deltas = (refs[4 + 2 * i : 6 + 2 * i] for i in range(3))
        sends, refs = refs[10 : 10 + parts - 1], refs[10 + parts - 1 :]
        grads, scratch = refs[:3], refs[3:]
        (slope_t, slope, key_t, hot, penalty, query_t, deltas, query_grad_t, key_grad, value_grad) = scratch[:10]
        upper, lower = mixtures
        if packed:
            for i, at in enumerate((0, 1, 4)):
                unpack(me_ref[0], pieces, stride, at * narrow, narrow, scratch[10 + i])
            output_w, query_w, source_w = scratch[10:13]
        else:
            output_w, query_w, source_w = pieces

        def vector(i):
            return vectors[i : i + 1, :]

        sums[0:7, :] = sums_inner[0:7, :]
        upstream = back2_in[...]
        normed, inverse = normalize(second_sum[...])
        sums[7:8, :] = total(upstream * normed)
        sums[8:9, :] = total(upstream)
        back2 = normalize_back(upstream, normed, inverse, vector(SOURCE_GAIN))
        back1[...] = back2
        cross_low = back2.astype(BF16)
        sums[9:10, :] = total(cross_low)
        grads[0][...] = dot(cross_t[...], cross_low).astype(BF16)
        found = dot_nt(cross_low, source_w[...]).astype(BF16)
        slope[...] = found
        slope_t[...] = found.T
        deltas_of(slope_t, cross_t, deltas)
        query_t[...] = query[...].T
        key_t[...] = memory_keys[...].T
        hot[...] = one_hot(memory_ids[...])
        penalty[...] = penalties(ids[:, :share])
        attend_back(query_t, query, memory_keys, key_t, memory_values, slope_t, slope, hot, penalty,
                    logs, deltas, query_grad_t, key_grad, value_grad)
        key_own[...] = key_grad[:memory_share, :]
        value_own[...] = value_grad[:memory_share, :]
        for i in range(1, parts):
            here = slice(i * memory_share, (i + 1) * memory_share)
            sends[i - 1][:memory_share, :] = key_grad[here, :].astype(BF16)
            sends[i - 1][memory_share:, :] = value_grad[here, :].astype(BF16)
        query_low = query_grad_t[...].T.astype(BF16)
        sums[10:11, :] = total(query_low)
        normed, inverse = normalize(first_sum[...])
        first_low = (normed * vector(ATTENTION_GAIN) + vector(ATTENTION_SHIFT)).astype(BF16)
        grads[1][...] = dot_tn(first_low, query_low).astype(BF16)
        upstream = back1[...] + dot_nt(query_low, query_w[...])
        sums[11:12, :] = total(upstream * normed)
        sums[12:13, :] = total(upstream)
        grad = normalize_back(upstream, normed, inverse, vector(ATTENTION_GAIN))
        back1[...] = grad
        branch_low = grad.astype(BF16)
        sums[13:14, :] = total(branch_low)
        sums[14:16, :] = jnp.zeros_like(sums[14:16, :])
        mixture_t = jnp.concatenate([upper[...], lower[...]], axis=0)
        grads[2][...] = dot(mixture_t, branch_low).astype(BF16)
        found = dot_nt(branch_low, output_w[...]).astype(BF16)
        for side in range(2):
            columns = slice(side * width // 2, (side + 1) * width // 2)
            self_slope[side][...] = found[:, columns]
            self_slope_t[side][...] = found[:, columns].T
            deltas_of(self_slope_t[side], mixtures[side], self_deltas[side])

    half = width // 2
    outs = [
        ((share, width), F32),
        ((memory_share, width), F32),
        ((memory_share, width), F32),
        ((16, width), F32),
    ]
    outs += [((share, half), BF16)] * 2 + [((half, share), BF16)] * 2
    outs += [((HEADS // 2, 1, share), F32)] * 2
    outs += [((2 * memory_share, width), BF16)] * (parts - 1)
    outs += [((width, width), BF16)] * 3
    scratch = [
        ((width, share), BF16),
        ((share, width), BF16),
        ((width, memory_length), BF16),
        ((memory_length, PAIR), BF16),
        ((PAIR, share), BF16),
        ((width, share), BF16),
        ((HEADS, 1, share), F32),
        ((width, share), F32),
        ((memory_length, width), F32),
        ((memory_length, width), F32),
    ]
    if packed:
        scratch += [((width, width), BF16)] * 3
    return kernel, outs, scratch


def attention_back_half(refs, share, scratch):
    query, keys, values, slope, slope_t, logs, deltas, ids = refs
    query_t, key_t, hot, penalty, query_grad_t, key_grad, value_grad = scratch
    query_t[...] = query[...].T
    key_t[...] = keys[...].T
    hot[...] = one_hot(ids[...])
    penalty[...] = penalties(ids[:, :share])
    attend_back(query_t, query, keys, key_t, values, slope_t, slope, hot, penalty, logs, deltas,
                query_grad_t, key_grad, value_grad)


def half_scratch(share, length, half):
    return [
        ((half, share), BF16),
        ((half, length), BF16),
        ((length, PAIR), BF16),
        ((PAIR, share), BF16),
        ((half, share), F32),
        ((length, half), F32),
        ((length, half), F32),
    ]


def give_half(share, scratch, own, sends):
    key_grad, value_grad = scratch[5:7]
    own[:share, :] = key_grad[:share, :]
    own[share:, :] = value_grad[:share, :]
    for i, send in enumerate(sends):
        here = slice((i // 2 + 1) * share, (i // 2 + 2) * share)
        send[...] = (key_grad, value_grad)[i % 2][here, :].astype(BF16)


def make_memory_back(packed, parts, rows, block, memory_block, width, narrow, n_pieces):
    memory_share = rows * memory_block

    def kernel(*refs):
        me_ref, refs = refs[0], list(refs[1:])
        pieces, refs = refs[:n_pieces], refs[n_pieces:]
        tokens, refs = refs[:rows], refs[rows:]
        memory_key_own, memory_value_own, sums_in = refs[:3]
        early, refs = refs[3:6], refs[6:]
        memory_received, refs = refs[: parts - 1], refs[parts - 1 :]
        memory_own, memory_send = refs[:2]
        n_grads = 2 if packed else 3
        grad_refs, scratch = refs[2 : 2 + n_grads], refs[2 + n_grads :]
        sums = scratch[0]
        me = me_ref[0]
        if packed:
            for i in range(2):
                unpack(me, pieces, 5 * narrow, (2 + i) * narrow, narrow, scratch[1 + i])
            source_key, source_value = scratch[1:3]
        else:
            source_key, source_value = pieces
        grads = Grads(me, grad_refs, scratch[3] if packed else None, narrow, CROSSED)
        memory = jnp.concatenate([t[block : block + memory_block, :] for t in tokens], axis=0)
        key_sum, value_sum = memory_key_own[...], memory_value_own[...]
        for ref in memory_received:
            key_sum = key_sum + ref[:memory_share, :].astype(F32)
            value_sum = value_sum + ref[memory_share:, :].astype(F32)
        key_low, value_low = key_sum.astype(BF16), value_sum.astype(BF16)
        sums[...] = sums_in[...]
        sums[14:15, :] = total(value_low)
        grads.put_sums(5 * narrow, sums[...])
        grads.put(0, dot_tn(memory, key_low))
        grads.put(1, dot_tn(memory, value_low))
        if packed:
            for i, ref in enumerate(early):
                grads.put(2 + i, ref[...].astype(F32))
        grad = dot_nt(key_low, source_key[...]) + dot_nt(value_low, source_value[...])
        memory_own[...] = grad[:memory_block, :]
        memory_send[...] = grad[memory_block:, :].astype(BF16)

    outs = [((memory_block, width), F32), ((memory_block, width), BF16)]
    if packed:
        outs += [((16, 5 * narrow + 16, width), BF16)] * 2
    else:
        outs += [((width, width), F32)] * 2 + [((16, width), F32)]
    scratch = [((16, width), F32)]
    if packed:
        scratch += [((width, width), BF16)] * 2 + [((width, width), F32)]
    return kernel, outs, scratch


def make_self_back_upper(parts, share, width):
    length, half = parts * share, width // 2

    def kernel(*refs):
        operands, (query_grad, own), refs = refs[1:9], refs[9:11], refs[11:]
        sends, scratch = refs[: 2 * parts - 2], refs[2 * parts - 2 :]
        attention_back_half(operands, share, scratch)
        query_grad[...] = scratch[4][...].T.astype(BF16)
        give_half(share, scratch, own, sends)

    outs = [((share, half), BF16), ((2 * share, half), F32)] + [((share, half), BF16)] * (2 * parts - 2)
    return kernel, outs, half_scratch(share, length, half)


def make_self_back_lower(packed, parts, rows, block, width, narrow, n_pieces):
    share = rows * block
    length, half = parts * share, width // 2

    def kernel(*refs):
        me_ref, refs = refs[0], list(refs[1:])
        pieces, refs = refs[:n_pieces], refs[n_pieces:]
        tokens, refs = refs[:rows], refs[rows:]
        operands, refs = refs[:8], refs[8:]
        back1, query_upper = refs[:2]
        in_part, query_sum, query_w_grad, own = refs[2:6]
        sends, scratch = refs[6 : 4 + 2 * parts], refs[4 + 2 * parts :]
        if packed:
            unpack(me_ref[0], pieces, 3 * narrow + 8, 0, narrow, scratch[7])
            query_w = scratch[7]
        else:
            (query_w,) = pieces
        attention_back_half(operands, share, scratch[:7])
        give_half(share, scratch, own, sends)
        query_low = jnp.concatenate([query_upper[...], scratch[4][...].T.astype(BF16)], axis=1)
        tokens_own = jnp.concatenate([t[:block, :] for t in tokens], axis=0)
        in_part[...] = back1[...] + dot_nt(query_low, query_w[...])
        query_sum[...] = jnp.concatenate([total(query_low), jnp.zeros((7, width), F32)], axis=0)
        query_w_grad[...] = dot_tn(tokens_own, query_low).astype(query_w_grad.dtype)

    outs = [
        ((share, width), F32),
        ((8, width), F32),
        ((width, width), BF16 if packed else F32),
        ((2 * share, half), F32),
    ]
    outs += [((share, half), BF16)] * (2 * parts - 2)
    scratch = half_scratch(share, length, half)
    if packed:
        scratch += [((width, width), BF16)]
    return kernel, outs, scratch


def make_last(packed, parts, rows, block, memory_block, width, narrow, n_pieces):
    share = rows * block

    def kernel(*refs):
        me_ref, refs = refs[0], list(refs[1:])
        pieces, refs = refs[:n_pieces], refs[n_pieces:]
        tokens, refs = refs[:rows], refs[rows:]
        in_part, query_sum, query_w_grad, memory_send = refs[:4]
        owns, refs = refs[4:6], refs[6:]
        received = [refs[: 2 * parts - 2], refs[2 * parts - 2 : 4 * parts - 4]]
        refs = refs[4 * parts - 4 :]
        in_own, in_send = refs[:2]
        n_grads = 2 if packed else 3
        grad_refs, scratch = refs[2 : 2 + n_grads], refs[2 + n_grads :]
        sums = scratch[0]
        me = me_ref[0]
        if packed:
            for i in range(2):
                unpack(me, pieces, 3 * narrow + 8, (1 + i) * narrow, narrow, scratch[1 + i])
            key_w, value_w = scratch[1:3]
        else:
            key_w, value_w = pieces
        grads = Grads(me, grad_refs, scratch[3] if packed else None, narrow)
        if packed:
            grads.put(2, query_w_grad[...].astype(F32))
        lows = []
        for own, others in zip(owns, received):
            found = own[...]
            for key, value in zip(others[::2], others[1::2]):
                found = found + jnp.concatenate([key[...], value[...]], axis=0).astype(F32)
            lows.append(found.astype(BF16))
        key_low = jnp.concatenate([low[:share, :] for low in lows], axis=1)
        value_low = jnp.concatenate([low[share:, :] for low in lows], axis=1)
        tokens_own = jnp.concatenate([t[:block, :] for t in tokens], axis=0)
        sums[...] = query_sum[...]
        sums[1:2, :] = total(value_low)
        grads.put_sums(3 * narrow, sums[...])
        grads.put(0, dot_tn(tokens_own, key_low))
        grads.put(1, dot_tn(tokens_own, value_low))
        grad = in_part[...] + dot_nt(key_low, key_w[...]) + dot_nt(value_low, value_w[...])
        in_own[...] = grad[:block, :]
        in_send[:block, :] = grad[block:, :].astype(BF16)
        in_send[block:, :] = memory_send[...]

    outs = [((block, width), F32), ((block + memory_block, width), BF16)]
    if packed:
        outs += [((16, 3 * narrow + 8, width), BF16)] * 2
    else:
        outs += [((width, width), F32)] * 2 + [((8, width), F32)]
    scratch = [((8, width), F32)]
    if packed:
        scratch += [((width, width), BF16)] * 2 + [((width, width), F32)]
    return kernel, outs, scratch


def combine(arrays, splits, micros=0.1):
    count = arrays[0].shape[0] // splits
    shape = (count,) + arrays[0].shape[1:]

    def kernel(*refs):
        given, outs = refs[: len(arrays)], refs[len(arrays) :]
        for i, out in enumerate(outs):
            here = slice(i * count, (i + 1) * count)
            found = given[0][here].astype(F32)
            for ref in given[1:]:
                found = found + ref[here].astype(F32)
            out[...] = found.astype(out.dtype)

    return pl.pallas_call(
        kernel,
        out_shape=[jax.ShapeDtypeStruct(shape, BF16)] * splits,
        in_specs=[VM] * len(arrays),
        out_specs=[VM] * splits,
        compiler_params=pltpu.CompilerParams(vmem_limit_bytes=snug(arrays)),
        cost_estimate=pl.CostEstimate(flops=int(micros * 1.15e9), bytes_accessed=0, transcendentals=0),
        name="combine",
    )(*arrays)


def combine_joint(groups, splits):
    count, sizes = groups[0][0].shape[0] // splits, [g[0].shape[1] for g in groups]
    shape = (count, sum(sizes)) + groups[0][0].shape[2:]
    flat = [a for group in groups for a in group]

    def kernel(*refs):
        outs, at, row = refs[len(flat) :], 0, 0
        for group, size in zip(groups, sizes):
            given = refs[at : at + len(group)]
            at += len(group)
            for i, out in enumerate(outs):
                here = slice(i * count, (i + 1) * count)
                found = given[0][here].astype(F32)
                for ref in given[1:]:
                    found = found + ref[here].astype(F32)
                out[:, row : row + size, :] = found.astype(BF16)
            row += size

    return pl.pallas_call(
        kernel,
        out_shape=[jax.ShapeDtypeStruct(shape, BF16)] * splits,
        in_specs=[VM] * len(flat),
        out_specs=[VM] * splits,
        compiler_params=pltpu.CompilerParams(vmem_limit_bytes=snug(flat)),
        cost_estimate=pl.CostEstimate(flops=1, bytes_accessed=1, transcendentals=0),
        name="combine_joint",
    )(*flat)


def chosen(me, rows, wide):
    width = rows.shape[1]
    line = lax.broadcasted_iota(jnp.int32, (width, wide), 0)
    here = lax.broadcasted_iota(jnp.int32, (width, wide), 1) + me * wide
    choice = jnp.where(line == here, 1.0, 0.0)
    return lax.dot_general(rows, choice, (((1,), (0,)), ((), ())), precision=lax.Precision.HIGHEST, preferred_element_type=F32)


def reduce_all(array, devices):
    mask = 1
    while mask < devices:
        array = array + swap(array, mask, devices)
        mask *= 2
    return array


def per_device(
    tokens, memory, target_ids, source_ids, cotangent,
    query_weight, key_weight, value_weight, output_weight, query_bias, value_bias, output_bias,
    attention_gain, attention_shift,
    source_query, source_key, source_value, source_output, source_query_bias, source_value_bias,
    source_output_bias, source_gain, source_shift,
    inner_weight, inner_bias, outer_weight, outer_bias, final_gain, final_shift,
    *, devices, sequence,
):
    packed = devices == 32
    rows, block, width = tokens.shape
    memory_block = memory.shape[1]
    parts = sequence // rows
    share, memory_share = rows * block, rows * memory_block
    hidden = inner_weight.shape[1]
    blocks = hidden // width
    me = lax.axis_index(AXES)
    me_array = me.reshape(1).astype(jnp.int32)
    turn = lax.rem(lax.div(me, parts), rows)
    narrow, wide = width // devices, hidden // devices

    def run(made, micros, name, *args, room=10):
        kernel, outs, *scratch = made
        return call(kernel, outs, (me_array,) + args, scratch[0] if scratch else [], micros, name, room)

    short = [query_bias, value_bias, output_bias, attention_gain, attention_shift, source_query_bias,
             source_value_bias, source_output_bias, source_gain, source_shift, outer_bias, final_gain,
             final_shift]

    def whole(array):
        return lax.all_gather(array, AXES, axis=0, tiled=True)

    sent, kept = tokens_packet(
        turn.reshape(1).astype(jnp.int32), tokens, memory, target_ids, source_ids, cotangent
    )
    came = swap(sent, parts, devices)
    row_tokens = [kept, came]
    kept_swaps = [swap(kept, m, devices) for m in range(1, parts)]
    came_swaps = [swap(came, m, devices) for m in range(1, parts)]
    for pair in zip(kept_swaps, came_swaps):
        row_tokens += pair
    own_tokens = row_tokens[:rows]

    if packed:
        first, second, third = run(make_weights_packet(narrow, width, blocks), 1.0, "weights_packet",
                          query_weight, key_weight, value_weight, output_weight, source_query,
                          source_key, source_value, source_output, inner_weight, outer_weight,
                          inner_bias.reshape(1, wide), *[v.reshape(1, narrow) for v in short], room=58)
        first = after(first, sent)
        first = join([first, turned_swap(first, 0)])
        first_b = turned_swap(first, 1)
        second = after(second, first)
        second_b = turned_swap(second, 0)
        first, second = join(after([first, first_b], second_b)), join(after([second, second_b], first_b))
        third = after(third, second)
        first_b, second_b, third_b = turned_swap(first, 2), turned_swap(second, 1), turned_swap(third, 0)
        first_c = join(after([first, first_b], second_b, third_b, came, *kept_swaps))
        second = join(after([second, second_b], first_b, third_b))
        third = join(after([third, third_b], first_b, second_b))
        first_d, second_b, third_b = turned_swap(first_c, 3), turned_swap(second, 2), turned_swap(third, 1)
        second_c = join(after([second, second_b], first_d, third_b))
        third = join(after([third, third_b], first_d, second_b))
        first_d = after(first_d, second_c, third, *came_swaps)
        second_d, third_b = turned_swap(second_c, 3), turned_swap(third, 2)
        set_self = [first_c, first_d, swap(first_c, 1, 32), swap(first_d, 1, 32)]
    else:
        full = [whole(w) for w in (query_weight, key_weight, value_weight, output_weight, source_query, source_key, source_value, source_output)]
        lane = lax.broadcasted_iota(jnp.int32, (1, width), 1)
        place = lax.broadcasted_iota(jnp.int32, (blocks, width), 0) * width + lane
        spread_wide = jnp.where(place // wide == me, jnp.tile(inner_bias.reshape(1, wide), (blocks, width // wide)), 0)

        def natural(rows):
            return jnp.where(lane // narrow == me, jnp.tile(rows, (1, devices)), 0)

        vectors = jnp.concatenate([natural(jnp.stack(short[:2])), jnp.zeros((6, width), BF16), natural(jnp.stack(short[2:])), spread_wide, jnp.zeros((1, width), BF16)])
        vectors = reduce_all(vectors, devices).astype(F32)
        set_self = full[:3] + [vectors]
        set_cross = full[3:]
        set_inner = [
            whole(inner_weight).reshape(width, blocks, width).transpose(1, 0, 2),
            whole(outer_weight).reshape(blocks, width, width),
        ]
    found = run(
        make_project(packed, parts, rows, block, memory_block, width, narrow, blocks, len(set_self)), 5.0,
        "project", *set_self, *row_tokens,
    )
    query, query_t, keys, values, value_t = (found[2 * i : 2 * i + 2] for i in range(5))
    row_memory, ids, memory_ids, vectors = found[10:]
    query_t = list(query_t)
    if packed:
        set_query, set_last = set_self, set_self
    else:
        set_back, set_query, set_last, set_memory = [full[3], full[4], full[7]], full[:1], full[1:3], full[5:7]
    found = run(
        make_self_attention(share, parts * share, width), 12.0, "self_attention",
        *query_t, *keys, *value_t, ids,
    )
    mixtures, logs = found[:2], found[2:]
    if packed:
        third_c = join(after([third, third_b], mixtures[0]))
        third_d = turned_swap(third_c, 3)
        second_d = after(second_d, mixtures[0])
        set_cross = [second_c, second_d, swap(second_c, 1, 32), swap(second_d, 1, 32)]
        set_back, set_memory = set_cross, set_cross
    first_sum, second_sum, cross_query, memory_keys, memory_values, cross_t, cross_logs = run(
        make_cross_forward(packed, rows, block, parts * memory_share, width, narrow, len(set_cross)),
        9.0, "cross_forward", *set_cross, *own_tokens, row_memory, ids, memory_ids, *mixtures, vectors,
    )
    if packed:
        third_d = after(third_d, second_sum)
        set_inner = [third_c, third_d, swap(third_c, 1, 32), swap(third_d, 1, 32)]
    out_own, out_send, back2_in, sums_inner, *grads_inner = run(
        make_inner(packed, rows, block, width, hidden, narrow, len(set_inner)), 18.0, "inner",
        *set_inner, second_sum, kept, came, vectors,
    )
    out_came = swap(out_send, parts, devices)
    found = run(
        make_cross_back(packed, parts, share, memory_share, width, narrow, len(set_back)), 14.0,
        "cross_back", *set_back, back2_in, first_sum, second_sum, cross_query, memory_keys,
        memory_values, cross_t, cross_logs, ids, memory_ids, vectors, sums_inner, *mixtures,
    )
    back1, memory_key_own, memory_value_own, sums_cross = found[:4]
    slope, slope_t, deltas = (found[4 + 2 * i : 6 + 2 * i] for i in range(3))
    memory_received = [swap(a, m + 1, devices) for m, a in enumerate(found[10 : 10 + parts - 1])]
    grads_early = found[10 + parts - 1 :]
    query = list(query)
    if packed:
        keep, send = combine(after([grads_inner[0], swap(grads_inner[1], 1, 32)], back1, out_came), 2)
        inner_step = [keep, turned_swap(send, 3)]
        memory_key_own = after(memory_key_own, keep)
    memory_own, memory_send, *grads_cross = run(
        make_memory_back(packed, parts, rows, block, memory_block, width, narrow, len(set_memory)),
        2.0, "memory_back", *set_memory, *own_tokens, memory_key_own, memory_value_own, sums_cross,
        *grads_early, *memory_received,
    )
    if packed:
        cross_came = swap(grads_cross[1], 1, 32)
        query[0] = after(query[0], grads_cross[0])
    found = run(
        make_self_back_upper(parts, share, width), 7.0, "self_back_upper", query[0], keys[0],
        values[0], slope[0], slope_t[0], logs[0], deltas[0], ids,
    )
    query_upper, own_upper = found[:2]
    received_upper = [swap(a, m // 2 + 1, devices) for m, a in enumerate(found[2:])]
    if packed:
        keep_cross, send = combine(after([grads_cross[0], cross_came], query_upper), 2)
        cross_step = [keep_cross, turned_swap(send, 3, CROSSED)]
        query[1] = after(query[1], keep_cross)
    in_part, query_sum, query_w_grad, own_lower, *sends = run(
        make_self_back_lower(packed, parts, rows, block, width, narrow, len(set_query)), 11.0,
        "self_back_lower", *set_query, *own_tokens, query[1], keys[1], values[1], slope[1],
        slope_t[1], logs[1], deltas[1], ids, back1, query_upper,
    )
    received_lower = [swap(a, m // 2 + 1, devices) for m, a in enumerate(sends)]
    if packed:
        keep, send = combine(after(inner_step, query_sum), 2)
        inner_step = [keep, turned_swap(send, 2)]
        keep_cross, send = combine(after(cross_step, query_sum), 2)
        cross_step = [keep_cross, turned_swap(send, 2, CROSSED)]
        in_part = after(in_part, keep, keep_cross)
    in_own, in_send, *grads_last = run(
        make_last(packed, parts, rows, block, memory_block, width, narrow, len(set_last)), 6.0,
        "last", *set_last, *own_tokens, in_part, query_sum, query_w_grad, memory_send, own_upper,
        own_lower, *received_upper, *received_lower,
    )

    if packed:
        keep, send = combine([grads_last[0], swap(grads_last[1], 1, 32)], 2)
        last_step = [keep, turned_swap(send, 3)]
        in_send = after(in_send, last_step[1])
        keep_joint, send = combine_joint(after([inner_step, cross_step], in_own), 2)
        joint_step = [keep_joint, turned_swap(send, 1)]
        keep, send = combine(after(last_step, keep_joint), 2)
        last_step = [keep, turned_swap(send, 2)]
        keep_joint, send = combine(joint_step, 2)
        joint_step = [keep_joint, turned_swap(send, 0)]
        keep, send = combine(after(last_step, keep_joint), 2)
        last_step = [keep, turned_swap(send, 1)]
        keep, send = combine(last_step, 2)
        last_step = [keep, turned_swap(send, 0)]

        def plan(me_ref, *refs):
            me = me_ref[0]
            joint, last = (sum(r[0].astype(F32) for r in given) for given in (refs[:2], refs[2:4]))
            outs = refs[4:]
            inner, cross = joint[: 2 * blocks * narrow, :], joint[2 * blocks * narrow :, :]
            for i in range(blocks):
                outs[0][:, i * width : (i + 1) * width] = inner[i * narrow : (i + 1) * narrow, :]
            outs[1][...] = inner[blocks * narrow :, :]
            for i in range(5):
                outs[2 + i][...] = cross[i * narrow : (i + 1) * narrow, :]
            for i in range(3):
                outs[7 + i][...] = last[i * narrow : (i + 1) * narrow, :]
            rows_in = jnp.concatenate([cross[5 * narrow :, :], last[3 * narrow :, :]], axis=0)
            outs[10][...] = chosen(me, rows_in, narrow)
            per = width // wide
            line = lax.broadcasted_iota(jnp.int32, (blocks, width), 0)
            row = jnp.sum(jnp.where(line == lax.div(me, per), rows_in[3 : 3 + blocks, :], 0.0), axis=0, keepdims=True)
            outs[11][...] = chosen(lax.rem(me, per), row, wide)

        part = (narrow, width)
        shapes = [(narrow, hidden), (wide, width)] + [part] * 8 + [(24, narrow), (1, wide)]
        (inner_share, outer_share, source_key_share, source_value_share, source_output_share,
         source_query_share, output_share, key_share, value_share, query_share, sums,
         inner_bias_share) = call(
            plan, [(s, F32) for s in shapes], (me_array, *joint_step, *last_step), [], 2.0,
            "finish",
        )
        inner_bias_share = inner_bias_share.reshape(wide)
    else:
        def scatter(array):
            return lax.psum_scatter(array, AXES, scatter_dimension=0, tiled=True)

        inner_share = scatter(grads_inner[0].transpose(1, 0, 2).reshape(width, hidden))
        outer_share = scatter(grads_inner[1].reshape(hidden, width))
        source_output_share, source_query_share, output_share = (scatter(g.astype(F32)) for g in grads_early)
        source_key_share, source_value_share = (scatter(g) for g in grads_cross[:2])
        key_share, value_share = (scatter(g) for g in grads_last[:2])
        query_share = scatter(query_w_grad)
        sums = reduce_all(jnp.concatenate([grads_cross[2], grads_last[2]], axis=0), devices)
        inner_bias_share = lax.dynamic_slice(sums[3 : 3 + blocks].reshape(hidden), (me * wide,), (wide,))
        sums = lax.dynamic_slice(sums, (0, me * narrow), (sums.shape[0], narrow))
    def regroup(mine, came):
        came = came.astype(F32)
        return jnp.where(turn == 0, jnp.stack([mine, came]), jnp.stack([came, mine]))

    output = regroup(out_own, out_came)
    in_came = swap(in_send, parts, devices)
    input_gradient = regroup(in_own, in_came[:block])
    memory_gradient = regroup(memory_own, in_came[block:])

    return (
        output,
        input_gradient,
        memory_gradient,
        query_share,
        key_share,
        value_share,
        output_share,
        sums[16],
        sums[17],
        sums[13],
        sums[11],
        sums[12],
        source_query_share,
        source_key_share,
        source_value_share,
        source_output_share,
        sums[10],
        sums[14],
        sums[9],
        sums[7],
        sums[8],
        inner_share,
        inner_bias_share,
        outer_share,
        sums[2],
        sums[0],
        sums[1],
    )


def solution(mesh):
    sequence, devices = mesh.shape["seq"], mesh.size
    tokens, ids = P("dp", "seq", None), P("dp", "seq")
    matrix, vector = P(AXES, None), P(AXES)
    attention = (matrix,) * 4 + (vector,) * 5
    inner = (matrix, vector, matrix, vector, vector, vector)
    return jax.shard_map(
        functools.partial(per_device, devices=devices, sequence=sequence),
        mesh=mesh,
        in_specs=(tokens, tokens, ids, ids, tokens) + attention + attention + inner,
        out_specs=(tokens, tokens, tokens) + attention + attention + inner,
        check_vma=False,
    )
```

```python
import functools
import math

import jax
import jax.numpy as jnp
from jax import lax
from jax.experimental import pallas as pl
from jax.experimental.pallas import tpu as pltpu
from jax.sharding import PartitionSpec as P

HEADS = 8
HEAD_DIM = 64
PAIR = 128
EPSILON = 1e-05
MASKED = 1e9
AXES = ("dp", "seq")
F32 = jnp.float32
BF16 = jnp.bfloat16

(
    OUTPUT_BIAS,
    ATTENTION_GAIN,
    ATTENTION_SHIFT,
    SOURCE_QUERY_BIAS,
    SOURCE_VALUE_BIAS,
    SOURCE_OUTPUT_BIAS,
    SOURCE_GAIN,
    SOURCE_SHIFT,
    OUTER_BIAS,
    FINAL_GAIN,
    FINAL_SHIFT,
    INNER_BIAS,
) = range(12)
Z_MASKS = (0, 8, 16, 24)
VM = pl.BlockSpec(memory_space=pltpu.VMEM)
SM = pl.BlockSpec(memory_space=pltpu.SMEM)


def dot(a, b):
    return lax.dot_general(a, b, (((1,), (0,)), ((), ())), preferred_element_type=F32)


def dot_nt(a, b):
    return lax.dot_general(a, b, (((1,), (1,)), ((), ())), preferred_element_type=F32)


def dot_tn(a, b):
    return lax.dot_general(a, b, (((0,), (0,)), ((), ())), preferred_element_type=F32)


def total(values):
    return jnp.sum(values.astype(F32), axis=0, keepdims=True)


def normalize(h):
    average = jnp.mean(h, axis=-1, keepdims=True)
    centered = h - average
    variance = jnp.mean(centered * centered, axis=-1, keepdims=True)
    inverse = lax.rsqrt(variance + EPSILON)
    return centered * inverse, inverse


def normalize_back(upstream, normed, inverse, gain):
    scaled = upstream * gain
    first_mean = jnp.mean(scaled, axis=-1, keepdims=True)
    second_mean = jnp.mean(scaled * normed, axis=-1, keepdims=True)
    return inverse * (scaled - first_mean - normed * second_mean)


def normal_parts(v):
    density = 0.3989422804014327 * jnp.exp(-0.5 * v * v)
    t = 1.0 / (1.0 + 0.2316419 * jnp.abs(v))
    series = t * (
        0.319381530
        + t * (-0.356563782 + t * (1.781477937 + t * (-1.821255978 + t * 1.330274429)))
    )
    tail = density * series
    return jnp.where(v >= 0.0, 1.0 - tail, tail), density


def penalties(ids):
    place = lax.broadcasted_iota(jnp.int32, (PAIR, ids.shape[1]), 0)
    return jnp.where((place == ids) | (place >= 4), 0.0, -MASKED).astype(BF16)


def one_hot(ids):
    place = lax.broadcasted_iota(jnp.int32, (PAIR, ids.shape[1]), 0)
    return jnp.where(place == ids, 1.0, 0.0).astype(F32).T.astype(BF16)


def spread(part, half):
    empty = jnp.zeros_like(part)
    return [part, empty] if half == 0 else [empty, part]


def attend(query_t, keys, value_t, hot, penalty, mixture_t, logs):
    length = keys.shape[0]

    def pair(p, carry):
        columns = pl.ds(pl.multiple_of(p * PAIR, PAIR), PAIR)
        left = jnp.concatenate([keys[:, columns], hot[...]], axis=1)
        for half in range(2):
            rows = pl.ds(pl.multiple_of(p * PAIR + half * HEAD_DIM, HEAD_DIM), HEAD_DIM)
            right = jnp.concatenate(spread(query_t[rows, :], half) + [penalty[...]], axis=0)
            scores = dot(left, right)
            highest = jnp.max(scores, axis=0, keepdims=True)
            weights = jnp.exp(scores - highest).astype(BF16)
            values = jnp.concatenate(
                [value_t[rows, :], jnp.ones((16, length), BF16)], axis=0
            )
            found = dot(values, weights)
            denominator = found[HEAD_DIM : HEAD_DIM + 1, :]
            mixture_t[rows, :] = (found[:HEAD_DIM, :] / denominator).astype(BF16)
            logs[2 * p + half] = highest + jnp.log(denominator)
        return carry

    lax.fori_loop(0, keys.shape[1] // PAIR, pair, 0)


def attend_back(
    query_t, query, keys, key_t, values, slope_t, slope, hot, penalty, logs, deltas,
    query_grad_t, key_grad, value_grad,
):
    tokens = query.shape[0]
    lane = lax.broadcasted_iota(jnp.int32, (tokens, PAIR), 1)

    def pair(p, carry):
        columns = pl.ds(pl.multiple_of(p * PAIR, PAIR), PAIR)
        left = jnp.concatenate([keys[:, columns], hot[...]], axis=1)
        value_pair = values[:, columns]
        key_sum, value_sum = None, None
        for half in range(2):
            rows = pl.ds(pl.multiple_of(p * PAIR + half * HEAD_DIM, HEAD_DIM), HEAD_DIM)
            right = jnp.concatenate(spread(query_t[rows, :], half) + [penalty[...]], axis=0)
            chances = jnp.exp(dot(left, right) - logs[2 * p + half])
            slopes = dot(value_pair, jnp.concatenate(spread(slope_t[rows, :], half), axis=0))
            grads = (chances * (slopes - deltas[2 * p + half])).astype(BF16)
            query_grad_t[rows, :] = dot(key_t[rows, :], grads) * HEAD_DIM**-0.5
            mine = (lane < HEAD_DIM) if half == 0 else (lane >= HEAD_DIM)
            none = jnp.zeros((tokens, PAIR), BF16)
            value_part = dot(chances.astype(BF16), jnp.where(mine, slope[:, columns], none))
            key_part = dot(grads, jnp.where(mine, query[:, columns], none))
            value_sum = value_part if value_sum is None else value_sum + value_part
            key_sum = key_part if key_sum is None else key_sum + key_part
        key_grad[:, columns] = key_sum
        value_grad[:, columns] = value_sum
        return carry

    lax.fori_loop(0, keys.shape[1] // PAIR, pair, 0)


def deltas_of(slope_t, mixture_t, deltas):
    for head in range(slope_t.shape[0] // HEAD_DIM):
        rows = slice(head * HEAD_DIM, (head + 1) * HEAD_DIM)
        deltas[head] = jnp.sum(
            slope_t[rows, :].astype(F32) * mixture_t[rows, :].astype(F32), axis=0, keepdims=True
        )


def swap(array, mask, devices):
    return lax.ppermute(array, AXES, [(i, i ^ mask) for i in range(devices)])


Z_FIRST = ((8, 24, 2, 4), (24, 8, 4, 2))
CROSSED = ((8, 24, 4, 2), (24, 8, 2, 4))


def turned_swap(array, step, orders=Z_FIRST):
    return lax.ppermute(array, AXES, [(i, i ^ orders[i % 2][step]) for i in range(32)])


def after(value, *others):
    return lax.optimization_barrier((value, others))[0]


def places(me, orders=Z_FIRST):
    found = []
    for core in range(2):
        even = ((me & 1) ^ core) == 0
        masks = [jnp.where(even, first, second) for first, second in zip(*orders)]
        for far in range(2):
            for slot in range(8):
                device = me ^ core if core else me
                for step, bit in enumerate((slot & 1, slot & 2, slot & 4, far)):
                    if bit:
                        device = device ^ masks[step]
                found.append((core, far, slot, device))
    return found


def unpack(me, pieces, stride, first, rows, scratch, orders=Z_FIRST):
    for core, far, slot, device in places(me, orders):
        ref = pieces[2 * core + far]
        at = slot * stride + first
        scratch[pl.ds(pl.multiple_of(device * rows, rows), rows), :] = ref[at : at + rows, :]


def sort_vectors(me, pieces, stride, first, narrow, sheet):
    width, blocks = sheet.shape[1], sheet.shape[0]
    lane = lax.broadcasted_iota(jnp.int32, (8, width), 1)
    per = width // (blocks * narrow)
    near, far = jnp.zeros((8, width), F32), jnp.zeros((8, width), F32)
    sheet[...] = jnp.zeros_like(sheet)
    for core, distant, slot, device in places(me):
        part = pieces[2 * core + distant][slot * stride + first : (slot + 1) * stride, :].astype(F32)
        group = lane // narrow
        near = near + jnp.where(group == device, part, 0.0)
        far = far + jnp.where(group == lax.rem(device + 1, width // narrow), part, 0.0)
        wide = jnp.where(lane[7:8, :] // (blocks * narrow) == lax.rem(device, per), part[7:8, :], 0.0)
        sheet[pl.ds(lax.div(device, per), 1), :] += wide
    far = pltpu.roll(far, width - narrow, 1)
    return jnp.concatenate([near[:7, :], far[:6, :]], axis=0)


class Grads:
    def __init__(self, me, refs, dense, rows, orders=Z_FIRST):
        self.me, self.refs, self.dense, self.rows, self.orders = me, refs, dense, rows, orders

    def put(self, index, grad):
        if self.dense is None:
            self.refs[index][...] = grad
            return
        self.dense[...] = grad
        rows = self.rows
        for core, far, slot, device in places(self.me, self.orders):
            found = self.dense[pl.ds(pl.multiple_of(device * rows, rows), rows), :]
            self.refs[core][far * 8 + slot, index * rows : (index + 1) * rows, :] = found.astype(BF16)

    def put_sums(self, first, sums):
        if self.dense is None:
            self.refs[-1][...] = sums
            return
        low = sums.astype(BF16)
        for ref in self.refs:
            for slot in range(16):
                ref[slot, first : first + sums.shape[0], :] = low


def grad_outs(packed, count, rows, width, sums):
    if packed:
        return [((16, count * rows + sums, width), BF16)] * 2
    return [((width, width), F32)] * count + [((sums, width), F32)]


COSTS = {}


def padded(shape, dtype):
    last = -(-shape[-1] // 128) * 128
    tall = -(-shape[-2] // 16) * 16 if len(shape) > 1 else 16
    return math.prod(shape[:-2]) * tall * last * jnp.dtype(dtype).itemsize


def snug(arrays):
    return 2 * sum(padded(a.shape, a.dtype) for a in arrays) + (3 << 20)


def call(kernel, outs, args, scratch, micros, name, room=10):
    moved = sum(math.prod(a.shape) * a.dtype.itemsize for a in args[1:])
    moved += sum(math.prod(s) * jnp.dtype(d).itemsize for s, d in outs)
    need = sum(padded(a.shape, a.dtype) for a in args[1:])
    need += sum(padded(s, d) for s, d in list(outs) + list(scratch))
    return pl.pallas_call(
        kernel,
        out_shape=[jax.ShapeDtypeStruct(s, d) for s, d in outs],
        in_specs=[SM] + [VM] * (len(args) - 1),
        out_specs=[VM] * len(outs),
        scratch_shapes=[pltpu.VMEM(s, d) for s, d in scratch],
        compiler_params=pltpu.CompilerParams(vmem_limit_bytes=min(need + (room << 20), 58 << 20)),
        cost_estimate=pl.CostEstimate(
            flops=int(COSTS.get(name, 0) * 1.15e9) + 1, bytes_accessed=1, transcendentals=0
        ),
        name=name,
    )(*args)


def tokens_packet(turn, tokens, memory, target_ids, source_ids, cotangent):
    block, width = tokens.shape[1:]
    memory_block = memory.shape[1]
    first = block + memory_block + 8

    def kernel(turn_ref, targets, sources, tokens_ref, memory_ref, cot_ref, sent, kept):
        mine = turn_ref[0]
        for row, out in ((1 - mine, sent), (mine, kept)):
            out[:block, :] = tokens_ref[row]
            out[block : block + memory_block, :] = memory_ref[row]
            ids = targets[pl.ds(row, 1), :].astype(F32)
            ids = jnp.concatenate([ids, jnp.zeros((1, width - block), F32)], axis=1)
            others = sources[pl.ds(row, 1), :].astype(F32)
            others = jnp.concatenate([others, jnp.zeros((1, width - memory_block), F32)], axis=1)
            place = lax.broadcasted_iota(jnp.int32, (8, width), 0)
            found = jnp.where(place == 0, ids, jnp.where(place == 1, others, 0.0))
            out[block + memory_block : first, :] = found.astype(BF16)
            out[first:, :] = cot_ref[row]

    shape = (first + block, width)
    return call(kernel, [(shape, BF16)] * 2, (turn, target_ids, source_ids, tokens, memory, cotangent),
                [], 1.0, "tokens_packet", 58)


def placed(me, parts, width):
    here = lax.broadcasted_iota(jnp.int32, (parts.shape[1], width), 0) + me * parts.shape[1]
    lane = lax.broadcasted_iota(jnp.int32, (parts.shape[1], width), 1)
    return dot(parts, jnp.where(lane == here, 1.0, 0.0).astype(BF16))


def make_weights_packet(narrow, width, blocks):
    tall = blocks * narrow

    def kernel(me_ref, *refs):
        weights, inner, outer, wide, short = refs[:8], refs[8], refs[9], refs[10], refs[11:24]
        first, second, third = refs[24:]
        me = me_ref[0]
        for i, ref in enumerate(weights):
            if i < 3:
                first[i * narrow : (i + 1) * narrow, :] = ref[...]
            else:
                second[(i - 3) * narrow : (i - 2) * narrow, :] = ref[...]
        short = jnp.concatenate([ref[...].astype(F32) for ref in short], axis=0).astype(BF16)
        near = placed(me, short[:7, :], width)
        far = placed(lax.rem(me + 1, width // narrow), short[7:, :], width)
        far = jnp.concatenate([far, jnp.zeros((1, width), F32)], axis=0)
        row = placed(lax.rem(me, width // wide.shape[1]), wide[...], width)
        first[3 * narrow :, :] = jnp.concatenate([near + far, row], axis=0).astype(BF16)
        for i in range(blocks):
            third[i * narrow : (i + 1) * narrow, :] = inner[:, i * width : (i + 1) * width]
        third[tall:, :] = outer[...]

    return kernel, [((rows, width), BF16) for rows in (3 * narrow + 8, 5 * narrow, 2 * tall)]


def join(arrays):
    def kernel(*refs):
        at = 0
        for ref in refs[:-1]:
            refs[-1][at : at + ref.shape[0], :] = ref[...]
            at += ref.shape[0]

    rows = sum(a.shape[0] for a in arrays)
    return pl.pallas_call(
        kernel,
        out_shape=jax.ShapeDtypeStruct((rows, arrays[0].shape[1]), arrays[0].dtype),
        in_specs=[VM] * len(arrays),
        out_specs=VM,
        compiler_params=pltpu.CompilerParams(vmem_limit_bytes=snug(arrays)),
        cost_estimate=pl.CostEstimate(flops=1 << 20, bytes_accessed=0, transcendentals=0),
        name="join",
    )(*arrays)


def make_project(packed, parts, rows, block, memory_block, width, narrow, blocks, n_pieces):
    share = rows * block
    length = parts * share
    memory_share = rows * memory_block
    stride = 3 * narrow + 8
    half = width // 2

    def kernel(*refs):
        me_ref, refs = refs[0], list(refs[1:])
        pieces, refs = refs[:n_pieces], refs[n_pieces:]
        tokens, refs = refs[: parts * rows], refs[parts * rows :]
        query, query_t, keys, values, value_t = (refs[2 * i : 2 * i + 2] for i in range(5))
        memory, ids, memory_ids, vectors = refs[10:14]
        scratch = refs[14:]
        me = me_ref[0]
        if packed:
            for i in range(3):
                unpack(me, pieces, stride, i * narrow, narrow, scratch[i])
            query_w, key_w, value_w, sheet = scratch
            biases = sort_vectors(me, pieces, stride, 3 * narrow, narrow, sheet)
            rest = jnp.zeros((5 - sheet.shape[0], width), F32)
            vectors[...] = jnp.concatenate([biases[2:, :], sheet[...], rest], axis=0)
        else:
            query_w, key_w, value_w = pieces[:3]
            biases = pieces[3][:8, :]
            vectors[...] = pieces[3][8:, :]
        for i in range(parts):
            here = slice(i * share, (i + 1) * share)
            some = tokens[i * rows : (i + 1) * rows]
            own = jnp.concatenate([t[:block, :] for t in some], axis=0)
            if i == 0:
                scaled = (dot(own, query_w[...]) + biases[0:1, :]).astype(BF16) * BF16(HEAD_DIM**-0.5)
            key = dot(own, key_w[...]).astype(BF16)
            found = (dot(own, value_w[...]) + biases[1:2, :]).astype(BF16)
            for side in range(2):
                columns = slice(side * half, (side + 1) * half)
                if i == 0:
                    query[side][...] = scaled[:, columns]
                    query_t[side][...] = scaled[:, columns].T
                keys[side][here, :] = key[:, columns]
                values[side][here, :] = found[:, columns]
                value_t[side][:, here] = found[:, columns].T
        for i, t in enumerate(tokens):
            memory[i * memory_block : (i + 1) * memory_block, :] = t[block : block + memory_block, :]
            found = t[block + memory_block : block + memory_block + 8, :].astype(F32).astype(jnp.int32)
            ids[:, i * block : (i + 1) * block] = found[0:1, :block]
        found = [t[block + memory_block : block + memory_block + 8, :].astype(F32).astype(jnp.int32)[1:2, :memory_block] for t in tokens]
        memory_ids[...] = jnp.concatenate(found, axis=1)

    outs = [((share, half), BF16)] * 2 + [((half, share), BF16)] * 2
    outs += [((length, half), BF16)] * 4 + [((half, length), BF16)] * 2
    outs += [
        ((parts * memory_share, width), BF16),
        ((1, length), jnp.int32),
        ((1, parts * memory_share), jnp.int32),
        ((16, width), F32),
    ]
    return kernel, outs, [((width, width), BF16)] * 3 + [((blocks, width), F32)] if packed else []


def make_self_attention(share, length, width):
    def kernel(me_ref, *refs):
        query_t, keys, value_t, ids = refs[:2], refs[2:4], refs[4:6], refs[6]
        mixture_t, logs, hot, penalty = refs[7:9], refs[9:11], refs[11], refs[12]
        hot[...] = one_hot(ids[...])
        penalty[...] = penalties(ids[:, :share])
        for side in range(2):
            attend(query_t[side], keys[side], value_t[side], hot, penalty, mixture_t[side], logs[side])

    outs = [((width // 2, share), BF16)] * 2 + [((HEADS // 2, 1, share), F32)] * 2
    return kernel, outs, [((length, PAIR), BF16), ((PAIR, share), BF16)]


def make_cross_forward(packed, rows, block, memory_length, width, narrow, n_pieces):
    share = rows * block
    stride = 5 * narrow

    def kernel(*refs):
        me_ref, refs = refs[0], list(refs[1:])
        pieces, refs = refs[:n_pieces], refs[n_pieces:]
        tokens, refs = refs[:rows], refs[rows:]
        memory, ids, memory_ids, upper, lower, vectors = refs[:6]
        first_sum, second_sum, query, memory_keys, memory_values, cross_t, logs = refs[6:13]
        scratch = refs[13:]
        query_t, value_t, hot, penalty = scratch[:4]
        if packed:
            for i in range(5):
                unpack(me_ref[0], pieces, stride, i * narrow, narrow, scratch[4 + i])
            output_w, query_w, key_w, value_w, source_w = scratch[4:]
        else:
            output_w, query_w, key_w, value_w, source_w = pieces[:5]

        def vector(i):
            return vectors[i : i + 1, :]

        own = jnp.concatenate([t[:block, :] for t in tokens], axis=0)
        mixture_t = jnp.concatenate([upper[...], lower[...]], axis=0)
        h = own.astype(F32) + dot_tn(mixture_t, output_w[...]) + vector(OUTPUT_BIAS)
        first_sum[...] = h
        first = normalize(h)[0] * vector(ATTENTION_GAIN) + vector(ATTENTION_SHIFT)
        scaled = (dot(first.astype(BF16), query_w[...]) + vector(SOURCE_QUERY_BIAS)).astype(BF16) * BF16(HEAD_DIM**-0.5)
        query[...] = scaled
        query_t[...] = scaled.T
        memory_keys[...] = dot(memory[...], key_w[...]).astype(BF16)
        memory_values[...] = (dot(memory[...], value_w[...]) + vector(SOURCE_VALUE_BIAS)).astype(BF16)
        value_t[...] = memory_values[...].T
        hot[...] = one_hot(memory_ids[...])
        penalty[...] = penalties(ids[:, :share])
        attend(query_t, memory_keys, value_t, hot, penalty, cross_t, logs)
        first = normalize(first_sum[...])[0] * vector(ATTENTION_GAIN) + vector(ATTENTION_SHIFT)
        second_sum[...] = first + dot_tn(cross_t[...], source_w[...]) + vector(SOURCE_OUTPUT_BIAS)

    outs = [
        ((share, width), F32),
        ((share, width), F32),
        ((share, width), BF16),
        ((memory_length, width), BF16),
        ((memory_length, width), BF16),
        ((width, share), BF16),
        ((HEADS, 1, share), F32),
    ]
    scratch = [((width, share), BF16), ((width, memory_length), BF16), ((memory_length, PAIR), BF16), ((PAIR, share), BF16)]
    if packed:
        scratch += [((width, width), BF16)] * 5
    return kernel, outs, scratch


def make_inner(packed, rows, block, width, hidden, narrow, n_pieces):
    blocks = hidden // width
    share = rows * block
    per = width // (blocks * narrow)

    def kernel(*refs):
        me_ref, refs = refs[0], list(refs[1:])
        pieces, refs = refs[:n_pieces], refs[n_pieces:]
        second_sum, cot_own, cot_came, vectors = refs[:4]
        out_own, out_send, back, sums = refs[4:8]
        grads, scratch = refs[8:10], refs[10:]
        low, active, gate, slope = scratch[:4]
        if packed:
            inner_w, outer_w, gathered, dense = scratch[4:8]
            tall = blocks * narrow
            for core, far, slot, device in places(me_ref[0]):
                ref, at = pieces[2 * core + far], slot * 2 * tall
                row = pl.multiple_of(device * narrow, narrow)
                for i in range(blocks):
                    inner_w[i, pl.ds(row, narrow), :] = ref[at + i * narrow : at + (i + 1) * narrow, :]
                row = pl.multiple_of(lax.rem(device, per) * tall, tall)
                outer_w[lax.div(device, per), pl.ds(row, tall), :] = ref[at + tall : at + 2 * tall, :]
        else:
            inner_w, outer_w = pieces

        def vector(i):
            return vectors[i : i + 1, :]

        second = normalize(second_sum[...])[0] * vector(SOURCE_GAIN) + vector(SOURCE_SHIFT)
        low[...] = second.astype(BF16)
        back[...] = second + vector(OUTER_BIAS)

        def forward(i, carry):
            inner = dot(low[...], inner_w[i]) + vectors[pl.ds(INNER_BIAS + i, 1), :]
            chance, density = normal_parts(inner)
            found = (inner * chance).astype(BF16)
            active[i] = found
            gate[i] = chance + inner * density
            back[...] += dot(found, outer_w[i])
            return carry

        lax.fori_loop(0, blocks, forward, 0)
        normed, inverse = normalize(back[...])
        final = normed * vector(FINAL_GAIN) + vector(FINAL_SHIFT)
        out_own[...] = final[:block, :]
        out_send[...] = final[block:, :].astype(BF16)
        upstream = jnp.concatenate([cot_own[-block:, :], cot_came[-block:, :]], axis=0).astype(F32)
        sums[0:1, :] = total(upstream * normed)
        sums[1:2, :] = total(upstream)
        back3 = normalize_back(upstream, normed, inverse, vector(FINAL_GAIN))
        slope[...] = back3.astype(BF16)
        sums[2:3, :] = total(slope[...])
        sums[7:8, :] = jnp.zeros_like(sums[7:8, :])
        back[...] = back3

        def backward(i, carry):
            grad = dot_nt(slope[...], outer_w[i]) * gate[i]
            inner_low = grad.astype(BF16)
            sums[pl.ds(3 + i, 1), :] = total(inner_low)
            outer_grad = dot_tn(active[i], slope[...])
            inner_grad = dot_tn(low[...], inner_low)
            back[...] += dot_nt(inner_low, inner_w[i])
            if packed:
                dense[...] = inner_grad
                gathered[i] = outer_grad.astype(BF16)
                here = pl.ds(pl.multiple_of(i * narrow, narrow), narrow)
                for core, far, slot, device in places(me_ref[0]):
                    row = pl.multiple_of(device * narrow, narrow)
                    grads[core][far * 8 + slot, here, :] = dense[pl.ds(row, narrow), :].astype(BF16)
            else:
                grads[0][i] = inner_grad
                grads[1][i] = outer_grad
            return carry

        lax.fori_loop(0, blocks, backward, 0)
        if packed:
            tall = blocks * narrow
            for core, far, slot, device in places(me_ref[0]):
                row = pl.multiple_of(lax.rem(device, per) * tall, tall)
                grads[core][far * 8 + slot, tall:, :] = gathered[lax.div(device, per), pl.ds(row, tall), :]

    outs = [((block, width), F32), ((block, width), BF16), ((share, width), F32), ((8, width), F32)]
    if packed:
        outs += [((16, 2 * blocks * narrow, width), BF16)] * 2
    else:
        outs += [((blocks, width, width), F32)] * 2
    scratch = [((share, width), BF16), ((blocks, share, width), BF16), ((blocks, share, width), F32), ((share, width), BF16)]
    if packed:
        scratch += [((blocks, width, width), BF16)] * 3 + [((width, width), F32)]
    return kernel, outs, scratch


def make_cross_back(packed, parts, share, memory_share, width, narrow, n_pieces):
    memory_length = parts * memory_share
    stride = 5 * narrow

    def kernel(*refs):
        me_ref, refs = refs[0], list(refs[1:])
        pieces, refs = refs[:n_pieces], refs[n_pieces:]
        (back2_in, first_sum, second_sum, query, memory_keys, memory_values, cross_t, logs, ids,
         memory_ids, vectors, sums_inner) = refs[:12]
        mixtures, refs = refs[12:14], refs[14:]
        back1, key_own, value_own, sums = refs[:4]
        self_slope, self_slope_t, self_deltas = (refs[4 + 2 * i : 6 + 2 * i] for i in range(3))
        sends, refs = refs[10 : 10 + parts - 1], refs[10 + parts - 1 :]
        grads, scratch = refs[:3], refs[3:]
        (slope_t, slope, key_t, hot, penalty, query_t, deltas, query_grad_t, key_grad, value_grad) = scratch[:10]
        upper, lower = mixtures
        if packed:
            for i, at in enumerate((0, 1, 4)):
                unpack(me_ref[0], pieces, stride, at * narrow, narrow, scratch[10 + i])
            output_w, query_w, source_w = scratch[10:13]
        else:
            output_w, query_w, source_w = pieces

        def vector(i):
            return vectors[i : i + 1, :]

        sums[0:7, :] = sums_inner[0:7, :]
        upstream = back2_in[...]
        normed, inverse = normalize(second_sum[...])
        sums[7:8, :] = total(upstream * normed)
        sums[8:9, :] = total(upstream)
        back2 = normalize_back(upstream, normed, inverse, vector(SOURCE_GAIN))
        back1[...] = back2
        cross_low = back2.astype(BF16)
        sums[9:10, :] = total(cross_low)
        grads[0][...] = dot(cross_t[...], cross_low).astype(BF16)
        found = dot_nt(cross_low, source_w[...]).astype(BF16)
        slope[...] = found
        slope_t[...] = found.T
        deltas_of(slope_t, cross_t, deltas)
        query_t[...] = query[...].T
        key_t[...] = memory_keys[...].T
        hot[...] = one_hot(memory_ids[...])
        penalty[...] = penalties(ids[:, :share])
        attend_back(query_t, query, memory_keys, key_t, memory_values, slope_t, slope, hot, penalty,
                    logs, deltas, query_grad_t, key_grad, value_grad)
        key_own[...] = key_grad[:memory_share, :]
        value_own[...] = value_grad[:memory_share, :]
        for i in range(1, parts):
            here = slice(i * memory_share, (i + 1) * memory_share)
            sends[i - 1][:memory_share, :] = key_grad[here, :].astype(BF16)
            sends[i - 1][memory_share:, :] = value_grad[here, :].astype(BF16)
        query_low = query_grad_t[...].T.astype(BF16)
        sums[10:11, :] = total(query_low)
        normed, inverse = normalize(first_sum[...])
        first_low = (normed * vector(ATTENTION_GAIN) + vector(ATTENTION_SHIFT)).astype(BF16)
        grads[1][...] = dot_tn(first_low, query_low).astype(BF16)
        upstream = back1[...] + dot_nt(query_low, query_w[...])
        sums[11:12, :] = total(upstream * normed)
        sums[12:13, :] = total(upstream)
        grad = normalize_back(upstream, normed, inverse, vector(ATTENTION_GAIN))
        back1[...] = grad
        branch_low = grad.astype(BF16)
        sums[13:14, :] = total(branch_low)
        sums[14:16, :] = jnp.zeros_like(sums[14:16, :])
        mixture_t = jnp.concatenate([upper[...], lower[...]], axis=0)
        grads[2][...] = dot(mixture_t, branch_low).astype(BF16)
        found = dot_nt(branch_low, output_w[...]).astype(BF16)
        for side in range(2):
            columns = slice(side * width // 2, (side + 1) * width // 2)
            self_slope[side][...] = found[:, columns]
            self_slope_t[side][...] = found[:, columns].T
            deltas_of(self_slope_t[side], mixtures[side], self_deltas[side])

    half = width // 2
    outs = [
        ((share, width), F32),
        ((memory_share, width), F32),
        ((memory_share, width), F32),
        ((16, width), F32),
    ]
    outs += [((share, half), BF16)] * 2 + [((half, share), BF16)] * 2
    outs += [((HEADS // 2, 1, share), F32)] * 2
    outs += [((2 * memory_share, width), BF16)] * (parts - 1)
    outs += [((width, width), BF16)] * 3
    scratch = [
        ((width, share), BF16),
        ((share, width), BF16),
        ((width, memory_length), BF16),
        ((memory_length, PAIR), BF16),
        ((PAIR, share), BF16),
        ((width, share), BF16),
        ((HEADS, 1, share), F32),
        ((width, share), F32),
        ((memory_length, width), F32),
        ((memory_length, width), F32),
    ]
    if packed:
        scratch += [((width, width), BF16)] * 3
    return kernel, outs, scratch


def attention_back_half(refs, share, scratch):
    query, keys, values, slope, slope_t, logs, deltas, ids = refs
    query_t, key_t, hot, penalty, query_grad_t, key_grad, value_grad = scratch
    query_t[...] = query[...].T
    key_t[...] = keys[...].T
    hot[...] = one_hot(ids[...])
    penalty[...] = penalties(ids[:, :share])
    attend_back(query_t, query, keys, key_t, values, slope_t, slope, hot, penalty, logs, deltas,
                query_grad_t, key_grad, value_grad)


def half_scratch(share, length, half):
    return [
        ((half, share), BF16),
        ((half, length), BF16),
        ((length, PAIR), BF16),
        ((PAIR, share), BF16),
        ((half, share), F32),
        ((length, half), F32),
        ((length, half), F32),
    ]


def give_half(share, scratch, own, sends):
    key_grad, value_grad = scratch[5:7]
    own[:share, :] = key_grad[:share, :]
    own[share:, :] = value_grad[:share, :]
    for i, send in enumerate(sends):
        here = slice((i // 2 + 1) * share, (i // 2 + 2) * share)
        send[...] = (key_grad, value_grad)[i % 2][here, :].astype(BF16)


def make_memory_back(packed, parts, rows, block, memory_block, width, narrow, n_pieces):
    memory_share = rows * memory_block

    def kernel(*refs):
        me_ref, refs = refs[0], list(refs[1:])
        pieces, refs = refs[:n_pieces], refs[n_pieces:]
        tokens, refs = refs[:rows], refs[rows:]
        memory_key_own, memory_value_own, sums_in = refs[:3]
        early, refs = refs[3:6], refs[6:]
        memory_received, refs = refs[: parts - 1], refs[parts - 1 :]
        memory_own, memory_send = refs[:2]
        n_grads = 2 if packed else 3
        grad_refs, scratch = refs[2 : 2 + n_grads], refs[2 + n_grads :]
        sums = scratch[0]
        me = me_ref[0]
        if packed:
            for i in range(2):
                unpack(me, pieces, 5 * narrow, (2 + i) * narrow, narrow, scratch[1 + i])
            source_key, source_value = scratch[1:3]
        else:
            source_key, source_value = pieces
        grads = Grads(me, grad_refs, scratch[3] if packed else None, narrow, CROSSED)
        memory = jnp.concatenate([t[block : block + memory_block, :] for t in tokens], axis=0)
        key_sum, value_sum = memory_key_own[...], memory_value_own[...]
        for ref in memory_received:
            key_sum = key_sum + ref[:memory_share, :].astype(F32)
            value_sum = value_sum + ref[memory_share:, :].astype(F32)
        key_low, value_low = key_sum.astype(BF16), value_sum.astype(BF16)
        sums[...] = sums_in[...]
        sums[14:15, :] = total(value_low)
        grads.put_sums(5 * narrow, sums[...])
        grads.put(0, dot_tn(memory, key_low))
        grads.put(1, dot_tn(memory, value_low))
        if packed:
            for i, ref in enumerate(early):
                grads.put(2 + i, ref[...].astype(F32))
        grad = dot_nt(key_low, source_key[...]) + dot_nt(value_low, source_value[...])
        memory_own[...] = grad[:memory_block, :]
        memory_send[...] = grad[memory_block:, :].astype(BF16)

    outs = [((memory_block, width), F32), ((memory_block, width), BF16)]
    if packed:
        outs += [((16, 5 * narrow + 16, width), BF16)] * 2
    else:
        outs += [((width, width), F32)] * 2 + [((16, width), F32)]
    scratch = [((16, width), F32)]
    if packed:
        scratch += [((width, width), BF16)] * 2 + [((width, width), F32)]
    return kernel, outs, scratch


def make_self_back_upper(parts, share, width):
    length, half = parts * share, width // 2

    def kernel(*refs):
        operands, (query_grad, own), refs = refs[1:9], refs[9:11], refs[11:]
        sends, scratch = refs[: 2 * parts - 2], refs[2 * parts - 2 :]
        attention_back_half(operands, share, scratch)
        query_grad[...] = scratch[4][...].T.astype(BF16)
        give_half(share, scratch, own, sends)

    outs = [((share, half), BF16), ((2 * share, half), F32)] + [((share, half), BF16)] * (2 * parts - 2)
    return kernel, outs, half_scratch(share, length, half)


def make_self_back_lower(packed, parts, rows, block, width, narrow, n_pieces):
    share = rows * block
    length, half = parts * share, width // 2

    def kernel(*refs):
        me_ref, refs = refs[0], list(refs[1:])
        pieces, refs = refs[:n_pieces], refs[n_pieces:]
        tokens, refs = refs[:rows], refs[rows:]
        operands, refs = refs[:8], refs[8:]
        back1, query_upper = refs[:2]
        in_part, query_sum, query_w_grad, own = refs[2:6]
        sends, scratch = refs[6 : 4 + 2 * parts], refs[4 + 2 * parts :]
        if packed:
            unpack(me_ref[0], pieces, 3 * narrow + 8, 0, narrow, scratch[7])
            query_w = scratch[7]
        else:
            (query_w,) = pieces
        attention_back_half(operands, share, scratch[:7])
        give_half(share, scratch, own, sends)
        query_low = jnp.concatenate([query_upper[...], scratch[4][...].T.astype(BF16)], axis=1)
        tokens_own = jnp.concatenate([t[:block, :] for t in tokens], axis=0)
        in_part[...] = back1[...] + dot_nt(query_low, query_w[...])
        query_sum[...] = jnp.concatenate([total(query_low), jnp.zeros((7, width), F32)], axis=0)
        query_w_grad[...] = dot_tn(tokens_own, query_low).astype(query_w_grad.dtype)

    outs = [
        ((share, width), F32),
        ((8, width), F32),
        ((width, width), BF16 if packed else F32),
        ((2 * share, half), F32),
    ]
    outs += [((share, half), BF16)] * (2 * parts - 2)
    scratch = half_scratch(share, length, half)
    if packed:
        scratch += [((width, width), BF16)]
    return kernel, outs, scratch


def make_last(packed, parts, rows, block, memory_block, width, narrow, n_pieces):
    share = rows * block

    def kernel(*refs):
        me_ref, refs = refs[0], list(refs[1:])
        pieces, refs = refs[:n_pieces], refs[n_pieces:]
        tokens, refs = refs[:rows], refs[rows:]
        in_part, query_sum, query_w_grad, memory_send = refs[:4]
        owns, refs = refs[4:6], refs[6:]
        received = [refs[: 2 * parts - 2], refs[2 * parts - 2 : 4 * parts - 4]]
        refs = refs[4 * parts - 4 :]
        in_own, in_send = refs[:2]
        n_grads = 2 if packed else 3
        grad_refs, scratch = refs[2 : 2 + n_grads], refs[2 + n_grads :]
        sums = scratch[0]
        me = me_ref[0]
        if packed:
            for i in range(2):
                unpack(me, pieces, 3 * narrow + 8, (1 + i) * narrow, narrow, scratch[1 + i])
            key_w, value_w = scratch[1:3]
        else:
            key_w, value_w = pieces
        grads = Grads(me, grad_refs, scratch[3] if packed else None, narrow)
        if packed:
            grads.put(2, query_w_grad[...].astype(F32))
        lows = []
        for own, others in zip(owns, received):
            found = own[...]
            for key, value in zip(others[::2], others[1::2]):
                found = found + jnp.concatenate([key[...], value[...]], axis=0).astype(F32)
            lows.append(found.astype(BF16))
        key_low = jnp.concatenate([low[:share, :] for low in lows], axis=1)
        value_low = jnp.concatenate([low[share:, :] for low in lows], axis=1)
        tokens_own = jnp.concatenate([t[:block, :] for t in tokens], axis=0)
        sums[...] = query_sum[...]
        sums[1:2, :] = total(value_low)
        grads.put_sums(3 * narrow, sums[...])
        grads.put(0, dot_tn(tokens_own, key_low))
        grads.put(1, dot_tn(tokens_own, value_low))
        grad = in_part[...] + dot_nt(key_low, key_w[...]) + dot_nt(value_low, value_w[...])
        in_own[...] = grad[:block, :]
        in_send[:block, :] = grad[block:, :].astype(BF16)
        in_send[block:, :] = memory_send[...]

    outs = [((block, width), F32), ((block + memory_block, width), BF16)]
    if packed:
        outs += [((16, 3 * narrow + 8, width), BF16)] * 2
    else:
        outs += [((width, width), F32)] * 2 + [((8, width), F32)]
    scratch = [((8, width), F32)]
    if packed:
        scratch += [((width, width), BF16)] * 2 + [((width, width), F32)]
    return kernel, outs, scratch


def combine(arrays, splits, micros=0.1):
    count = arrays[0].shape[0] // splits
    shape = (count,) + arrays[0].shape[1:]

    def kernel(*refs):
        given, outs = refs[: len(arrays)], refs[len(arrays) :]
        for i, out in enumerate(outs):
            here = slice(i * count, (i + 1) * count)
            found = given[0][here].astype(F32)
            for ref in given[1:]:
                found = found + ref[here].astype(F32)
            out[...] = found.astype(out.dtype)

    return pl.pallas_call(
        kernel,
        out_shape=[jax.ShapeDtypeStruct(shape, BF16)] * splits,
        in_specs=[VM] * len(arrays),
        out_specs=[VM] * splits,
        compiler_params=pltpu.CompilerParams(vmem_limit_bytes=snug(arrays)),
        cost_estimate=pl.CostEstimate(flops=int(micros * 1.15e9), bytes_accessed=0, transcendentals=0),
        name="combine",
    )(*arrays)


def combine_joint(groups, splits):
    count, sizes = groups[0][0].shape[0] // splits, [g[0].shape[1] for g in groups]
    shape = (count, sum(sizes)) + groups[0][0].shape[2:]
    flat = [a for group in groups for a in group]

    def kernel(*refs):
        outs, at, row = refs[len(flat) :], 0, 0
        for group, size in zip(groups, sizes):
            given = refs[at : at + len(group)]
            at += len(group)
            for i, out in enumerate(outs):
                here = slice(i * count, (i + 1) * count)
                found = given[0][here].astype(F32)
                for ref in given[1:]:
                    found = found + ref[here].astype(F32)
                out[:, row : row + size, :] = found.astype(BF16)
            row += size

    return pl.pallas_call(
        kernel,
        out_shape=[jax.ShapeDtypeStruct(shape, BF16)] * splits,
        in_specs=[VM] * len(flat),
        out_specs=[VM] * splits,
        compiler_params=pltpu.CompilerParams(vmem_limit_bytes=snug(flat)),
        cost_estimate=pl.CostEstimate(flops=1, bytes_accessed=1, transcendentals=0),
        name="combine_joint",
    )(*flat)


def chosen(me, rows, wide):
    width = rows.shape[1]
    line = lax.broadcasted_iota(jnp.int32, (width, wide), 0)
    here = lax.broadcasted_iota(jnp.int32, (width, wide), 1) + me * wide
    choice = jnp.where(line == here, 1.0, 0.0)
    return lax.dot_general(rows, choice, (((1,), (0,)), ((), ())), precision=lax.Precision.HIGHEST, preferred_element_type=F32)


def reduce_all(array, devices):
    mask = 1
    while mask < devices:
        array = array + swap(array, mask, devices)
        mask *= 2
    return array


def per_device(
    tokens, memory, target_ids, source_ids, cotangent,
    query_weight, key_weight, value_weight, output_weight, query_bias, value_bias, output_bias,
    attention_gain, attention_shift,
    source_query, source_key, source_value, source_output, source_query_bias, source_value_bias,
    source_output_bias, source_gain, source_shift,
    inner_weight, inner_bias, outer_weight, outer_bias, final_gain, final_shift,
    *, devices, sequence,
):
    packed = devices == 32
    rows, block, width = tokens.shape
    memory_block = memory.shape[1]
    parts = sequence // rows
    share, memory_share = rows * block, rows * memory_block
    hidden = inner_weight.shape[1]
    blocks = hidden // width
    me = lax.axis_index(AXES)
    me_array = me.reshape(1).astype(jnp.int32)
    turn = lax.rem(lax.div(me, parts), rows)
    narrow, wide = width // devices, hidden // devices

    def run(made, micros, name, *args, room=10):
        kernel, outs, *scratch = made
        return call(kernel, outs, (me_array,) + args, scratch[0] if scratch else [], micros, name, room)

    short = [query_bias, value_bias, output_bias, attention_gain, attention_shift, source_query_bias,
             source_value_bias, source_output_bias, source_gain, source_shift, outer_bias, final_gain,
             final_shift]

    def whole(array):
        return lax.all_gather(array, AXES, axis=0, tiled=True)

    sent, kept = tokens_packet(
        turn.reshape(1).astype(jnp.int32), tokens, memory, target_ids, source_ids, cotangent
    )
    came = swap(sent, parts, devices)
    row_tokens = [kept, came]
    kept_swaps = [swap(kept, m, devices) for m in range(1, parts)]
    came_swaps = [swap(came, m, devices) for m in range(1, parts)]
    for pair in zip(kept_swaps, came_swaps):
        row_tokens += pair
    own_tokens = row_tokens[:rows]

    if packed:
        first, second, third = run(make_weights_packet(narrow, width, blocks), 1.0, "weights_packet",
                          query_weight, key_weight, value_weight, output_weight, source_query,
                          source_key, source_value, source_output, inner_weight, outer_weight,
                          inner_bias.reshape(1, wide), *[v.reshape(1, narrow) for v in short], room=58)
        first = after(first, sent)
        first = join([first, turned_swap(first, 0)])
        first_b = turned_swap(first, 1)
        second = after(second, first)
        second_b = turned_swap(second, 0)
        first, second = join(after([first, first_b], second_b)), join(after([second, second_b], first_b))
        third = after(third, second)
        first_b, second_b, third_b = turned_swap(first, 2), turned_swap(second, 1), turned_swap(third, 0)
        first_c = join(after([first, first_b], second_b, third_b, came, *kept_swaps))
        second = join(after([second, second_b], first_b, third_b))
        third = join(after([third, third_b], first_b, second_b))
        first_d, second_b, third_b = turned_swap(first_c, 3), turned_swap(second, 2), turned_swap(third, 1)
        second_c = join(after([second, second_b], first_d, third_b))
        third = join(after([third, third_b], first_d, second_b))
        first_d = after(first_d, second_c, third, *came_swaps)
        second_d, third_b = turned_swap(second_c, 3), turned_swap(third, 2)
        set_self = [first_c, first_d, swap(first_c, 1, 32), swap(first_d, 1, 32)]
    else:
        full = [whole(w) for w in (query_weight, key_weight, value_weight, output_weight, source_query, source_key, source_value, source_output)]
        lane = lax.broadcasted_iota(jnp.int32, (1, width), 1)
        place = lax.broadcasted_iota(jnp.int32, (blocks, width), 0) * width + lane
        spread_wide = jnp.where(place // wide == me, jnp.tile(inner_bias.reshape(1, wide), (blocks, width // wide)), 0)

        def natural(rows):
            return jnp.where(lane // narrow == me, jnp.tile(rows, (1, devices)), 0)

        vectors = jnp.concatenate([natural(jnp.stack(short[:2])), jnp.zeros((6, width), BF16), natural(jnp.stack(short[2:])), spread_wide, jnp.zeros((1, width), BF16)])
        vectors = reduce_all(vectors, devices).astype(F32)
        set_self = full[:3] + [vectors]
        set_cross = full[3:]
        set_inner = [
            whole(inner_weight).reshape(width, blocks, width).transpose(1, 0, 2),
            whole(outer_weight).reshape(blocks, width, width),
        ]
    found = run(
        make_project(packed, parts, rows, block, memory_block, width, narrow, blocks, len(set_self)), 5.0,
        "project", *set_self, *row_tokens,
    )
    query, query_t, keys, values, value_t = (found[2 * i : 2 * i + 2] for i in range(5))
    row_memory, ids, memory_ids, vectors = found[10:]
    query_t = list(query_t)
    if packed:
        set_query, set_last = set_self, set_self
    else:
        set_back, set_query, set_last, set_memory = [full[3], full[4], full[7]], full[:1], full[1:3], full[5:7]
    found = run(
        make_self_attention(share, parts * share, width), 12.0, "self_attention",
        *query_t, *keys, *value_t, ids,
    )
    mixtures, logs = found[:2], found[2:]
    if packed:
        third_c = join(after([third, third_b], mixtures[0]))
        third_d = turned_swap(third_c, 3)
        second_d = after(second_d, mixtures[0])
        set_cross = [second_c, second_d, swap(second_c, 1, 32), swap(second_d, 1, 32)]
        set_back, set_memory = set_cross, set_cross
    first_sum, second_sum, cross_query, memory_keys, memory_values, cross_t, cross_logs = run(
        make_cross_forward(packed, rows, block, parts * memory_share, width, narrow, len(set_cross)),
        9.0, "cross_forward", *set_cross, *own_tokens, row_memory, ids, memory_ids, *mixtures, vectors,
    )
    if packed:
        third_d = after(third_d, second_sum)
        set_inner = [third_c, third_d, swap(third_c, 1, 32), swap(third_d, 1, 32)]
    out_own, out_send, back2_in, sums_inner, *grads_inner = run(
        make_inner(packed, rows, block, width, hidden, narrow, len(set_inner)), 18.0, "inner",
        *set_inner, second_sum, kept, came, vectors,
    )
    found = run(
        make_cross_back(packed, parts, share, memory_share, width, narrow, len(set_back)), 14.0,
        "cross_back", *set_back, back2_in, first_sum, second_sum, cross_query, memory_keys,
        memory_values, cross_t, cross_logs, ids, memory_ids, vectors, sums_inner, *mixtures,
    )
    back1, memory_key_own, memory_value_own, sums_cross = found[:4]
    slope, slope_t, deltas = (found[4 + 2 * i : 6 + 2 * i] for i in range(3))
    memory_received = [swap(a, m + 1, devices) for m, a in enumerate(found[10 : 10 + parts - 1])]
    grads_early = found[10 + parts - 1 :]
    query = list(query)
    if packed:
        keep, send = combine(after([grads_inner[0], swap(grads_inner[1], 1, 32)], back1), 2)
        inner_step = [keep, turned_swap(send, 3)]
        memory_key_own = after(memory_key_own, keep)
    memory_own, memory_send, *grads_cross = run(
        make_memory_back(packed, parts, rows, block, memory_block, width, narrow, len(set_memory)),
        2.0, "memory_back", *set_memory, *own_tokens, memory_key_own, memory_value_own, sums_cross,
        *grads_early, *memory_received,
    )
    if packed:
        cross_came = swap(grads_cross[1], 1, 32)
        query[0] = after(query[0], grads_cross[0])
    found = run(
        make_self_back_upper(parts, share, width), 7.0, "self_back_upper", query[0], keys[0],
        values[0], slope[0], slope_t[0], logs[0], deltas[0], ids,
    )
    query_upper, own_upper = found[:2]
    received_upper = [swap(a, m // 2 + 1, devices) for m, a in enumerate(found[2:])]
    if packed:
        keep_cross, send = combine(after([grads_cross[0], cross_came], query_upper), 2)
        cross_step = [keep_cross, turned_swap(send, 3, CROSSED)]
        query[1] = after(query[1], keep_cross)
    in_part, query_sum, query_w_grad, own_lower, *sends = run(
        make_self_back_lower(packed, parts, rows, block, width, narrow, len(set_query)), 11.0,
        "self_back_lower", *set_query, *own_tokens, query[1], keys[1], values[1], slope[1],
        slope_t[1], logs[1], deltas[1], ids, back1, query_upper,
    )
    received_lower = [swap(a, m // 2 + 1, devices) for m, a in enumerate(sends)]
    if packed:
        keep, send = combine(after(inner_step, query_sum), 2)
        inner_step = [keep, turned_swap(send, 2)]
        keep_cross, send = combine(after(cross_step, query_sum), 2)
        cross_step = [keep_cross, turned_swap(send, 2, CROSSED)]
        in_part = after(in_part, keep, keep_cross)
    in_own, in_send, *grads_last = run(
        make_last(packed, parts, rows, block, memory_block, width, narrow, len(set_last)), 6.0,
        "last", *set_last, *own_tokens, in_part, query_sum, query_w_grad, memory_send, own_upper,
        own_lower, *received_upper, *received_lower,
    )

    if packed:
        keep, send = combine([grads_last[0], swap(grads_last[1], 1, 32)], 2)
        last_step = [keep, turned_swap(send, 3)]
        in_send, out_send = after((in_send, out_send), last_step[1])
        keep_joint, send = combine_joint(after([inner_step, cross_step], in_own), 2)
        joint_step = [keep_joint, turned_swap(send, 1)]
        keep, send = combine(after(last_step, keep_joint), 2)
        last_step = [keep, turned_swap(send, 2)]
        keep_joint, send = combine(joint_step, 2)
        joint_step = [keep_joint, turned_swap(send, 0)]
        keep, send = combine(after(last_step, keep_joint), 2)
        last_step = [keep, turned_swap(send, 1)]
        keep, send = combine(last_step, 2)
        last_step = [keep, turned_swap(send, 0)]

        def plan(me_ref, *refs):
            me = me_ref[0]
            joint, last = (sum(r[0].astype(F32) for r in given) for given in (refs[:2], refs[2:4]))
            outs = refs[4:]
            inner, cross = joint[: 2 * blocks * narrow, :], joint[2 * blocks * narrow :, :]
            for i in range(blocks):
                outs[0][:, i * width : (i + 1) * width] = inner[i * narrow : (i + 1) * narrow, :]
            outs[1][...] = inner[blocks * narrow :, :]
            for i in range(5):
                outs[2 + i][...] = cross[i * narrow : (i + 1) * narrow, :]
            for i in range(3):
                outs[7 + i][...] = last[i * narrow : (i + 1) * narrow, :]
            rows_in = jnp.concatenate([cross[5 * narrow :, :], last[3 * narrow :, :]], axis=0)
            outs[10][...] = chosen(me, rows_in, narrow)
            per = width // wide
            line = lax.broadcasted_iota(jnp.int32, (blocks, width), 0)
            row = jnp.sum(jnp.where(line == lax.div(me, per), rows_in[3 : 3 + blocks, :], 0.0), axis=0, keepdims=True)
            outs[11][...] = chosen(lax.rem(me, per), row, wide)

        part = (narrow, width)
        shapes = [(narrow, hidden), (wide, width)] + [part] * 8 + [(24, narrow), (1, wide)]
        (inner_share, outer_share, source_key_share, source_value_share, source_output_share,
         source_query_share, output_share, key_share, value_share, query_share, sums,
         inner_bias_share) = call(
            plan, [(s, F32) for s in shapes], (me_array, *joint_step, *last_step), [], 2.0,
            "finish",
        )
        inner_bias_share = inner_bias_share.reshape(wide)
    else:
        def scatter(array):
            return lax.psum_scatter(array, AXES, scatter_dimension=0, tiled=True)

        inner_share = scatter(grads_inner[0].transpose(1, 0, 2).reshape(width, hidden))
        outer_share = scatter(grads_inner[1].reshape(hidden, width))
        source_output_share, source_query_share, output_share = (scatter(g.astype(F32)) for g in grads_early)
        source_key_share, source_value_share = (scatter(g) for g in grads_cross[:2])
        key_share, value_share = (scatter(g) for g in grads_last[:2])
        query_share = scatter(query_w_grad)
        sums = reduce_all(jnp.concatenate([grads_cross[2], grads_last[2]], axis=0), devices)
        inner_bias_share = lax.dynamic_slice(sums[3 : 3 + blocks].reshape(hidden), (me * wide,), (wide,))
        sums = lax.dynamic_slice(sums, (0, me * narrow), (sums.shape[0], narrow))
    def regroup(mine, came):
        came = came.astype(F32)
        return jnp.where(turn == 0, jnp.stack([mine, came]), jnp.stack([came, mine]))

    output = regroup(out_own, swap(out_send, parts, devices))
    in_came = swap(in_send, parts, devices)
    input_gradient = regroup(in_own, in_came[:block])
    memory_gradient = regroup(memory_own, in_came[block:])

    return (
        output,
        input_gradient,
        memory_gradient,
        query_share,
        key_share,
        value_share,
        output_share,
        sums[16],
        sums[17],
        sums[13],
        sums[11],
        sums[12],
        source_query_share,
        source_key_share,
        source_value_share,
        source_output_share,
        sums[10],
        sums[14],
        sums[9],
        sums[7],
        sums[8],
        inner_share,
        inner_bias_share,
        outer_share,
        sums[2],
        sums[0],
        sums[1],
    )


def solution(mesh):
    sequence, devices = mesh.shape["seq"], mesh.size
    tokens, ids = P("dp", "seq", None), P("dp", "seq")
    matrix, vector = P(AXES, None), P(AXES)
    attention = (matrix,) * 4 + (vector,) * 5
    inner = (matrix, vector, matrix, vector, vector, vector)
    return jax.shard_map(
        functools.partial(per_device, devices=devices, sequence=sequence),
        mesh=mesh,
        in_specs=(tokens, tokens, ids, ids, tokens) + attention + attention + inner,
        out_specs=(tokens, tokens, tokens) + attention + attention + inner,
        check_vma=False,
    )
```

```python
import functools
import math

import jax
import jax.numpy as jnp
from jax import lax
from jax.experimental import pallas as pl
from jax.experimental.pallas import tpu as pltpu
from jax.sharding import PartitionSpec as P

HEADS = 8
HEAD_DIM = 64
PAIR = 128
EPSILON = 1e-05
MASKED = 1e9
AXES = ("dp", "seq")
F32 = jnp.float32
BF16 = jnp.bfloat16

(
    OUTPUT_BIAS,
    ATTENTION_GAIN,
    ATTENTION_SHIFT,
    SOURCE_QUERY_BIAS,
    SOURCE_VALUE_BIAS,
    SOURCE_OUTPUT_BIAS,
    SOURCE_GAIN,
    SOURCE_SHIFT,
    OUTER_BIAS,
    FINAL_GAIN,
    FINAL_SHIFT,
    INNER_BIAS,
) = range(12)
Z_MASKS = (0, 8, 16, 24)
VM = pl.BlockSpec(memory_space=pltpu.VMEM)
SM = pl.BlockSpec(memory_space=pltpu.SMEM)


def dot(a, b):
    return lax.dot_general(a, b, (((1,), (0,)), ((), ())), preferred_element_type=F32)


def dot_nt(a, b):
    return lax.dot_general(a, b, (((1,), (1,)), ((), ())), preferred_element_type=F32)


def dot_tn(a, b):
    return lax.dot_general(a, b, (((0,), (0,)), ((), ())), preferred_element_type=F32)


def total(values):
    return jnp.sum(values.astype(F32), axis=0, keepdims=True)


def normalize(h):
    average = jnp.mean(h, axis=-1, keepdims=True)
    centered = h - average
    variance = jnp.mean(centered * centered, axis=-1, keepdims=True)
    inverse = lax.rsqrt(variance + EPSILON)
    return centered * inverse, inverse


def normalize_back(upstream, normed, inverse, gain):
    scaled = upstream * gain
    first_mean = jnp.mean(scaled, axis=-1, keepdims=True)
    second_mean = jnp.mean(scaled * normed, axis=-1, keepdims=True)
    return inverse * (scaled - first_mean - normed * second_mean)


def normal_parts(v):
    density = 0.3989422804014327 * jnp.exp(-0.5 * v * v)
    t = 1.0 / (1.0 + 0.2316419 * jnp.abs(v))
    series = t * (
        0.319381530
        + t * (-0.356563782 + t * (1.781477937 + t * (-1.821255978 + t * 1.330274429)))
    )
    tail = density * series
    return jnp.where(v >= 0.0, 1.0 - tail, tail), density


def penalties(ids):
    place = lax.broadcasted_iota(jnp.int32, (PAIR, ids.shape[1]), 0)
    return jnp.where((place == ids) | (place >= 4), 0.0, -MASKED).astype(BF16)


def one_hot(ids):
    place = lax.broadcasted_iota(jnp.int32, (PAIR, ids.shape[1]), 0)
    return jnp.where(place == ids, 1.0, 0.0).astype(F32).T.astype(BF16)


def spread(part, half):
    empty = jnp.zeros_like(part)
    return [part, empty] if half == 0 else [empty, part]


def attend(query_t, keys, value_t, hot, penalty, mixture_t, logs):
    length = keys.shape[0]

    def pair(p, carry):
        columns = pl.ds(pl.multiple_of(p * PAIR, PAIR), PAIR)
        left = jnp.concatenate([keys[:, columns], hot[...]], axis=1)
        for half in range(2):
            rows = pl.ds(pl.multiple_of(p * PAIR + half * HEAD_DIM, HEAD_DIM), HEAD_DIM)
            right = jnp.concatenate(spread(query_t[rows, :], half) + [penalty[...]], axis=0)
            scores = dot(left, right)
            highest = jnp.max(scores, axis=0, keepdims=True)
            weights = jnp.exp(scores - highest).astype(BF16)
            values = jnp.concatenate(
                [value_t[rows, :], jnp.ones((16, length), BF16)], axis=0
            )
            found = dot(values, weights)
            denominator = found[HEAD_DIM : HEAD_DIM + 1, :]
            mixture_t[rows, :] = (found[:HEAD_DIM, :] / denominator).astype(BF16)
            logs[2 * p + half] = highest + jnp.log(denominator)
        return carry

    lax.fori_loop(0, keys.shape[1] // PAIR, pair, 0)


def attend_back(
    query_t, query, keys, key_t, values, slope_t, slope, hot, penalty, logs, deltas,
    query_grad_t, key_grad, value_grad,
):
    tokens = query.shape[0]
    lane = lax.broadcasted_iota(jnp.int32, (tokens, PAIR), 1)

    def pair(p, carry):
        columns = pl.ds(pl.multiple_of(p * PAIR, PAIR), PAIR)
        left = jnp.concatenate([keys[:, columns], hot[...]], axis=1)
        value_pair = values[:, columns]
        key_sum, value_sum = None, None
        for half in range(2):
            rows = pl.ds(pl.multiple_of(p * PAIR + half * HEAD_DIM, HEAD_DIM), HEAD_DIM)
            right = jnp.concatenate(spread(query_t[rows, :], half) + [penalty[...]], axis=0)
            chances = jnp.exp(dot(left, right) - logs[2 * p + half])
            slopes = dot(value_pair, jnp.concatenate(spread(slope_t[rows, :], half), axis=0))
            grads = (chances * (slopes - deltas[2 * p + half])).astype(BF16)
            query_grad_t[rows, :] = dot(key_t[rows, :], grads) * HEAD_DIM**-0.5
            mine = (lane < HEAD_DIM) if half == 0 else (lane >= HEAD_DIM)
            none = jnp.zeros((tokens, PAIR), BF16)
            value_part = dot(chances.astype(BF16), jnp.where(mine, slope[:, columns], none))
            key_part = dot(grads, jnp.where(mine, query[:, columns], none))
            value_sum = value_part if value_sum is None else value_sum + value_part
            key_sum = key_part if key_sum is None else key_sum + key_part
        key_grad[:, columns] = key_sum
        value_grad[:, columns] = value_sum
        return carry

    lax.fori_loop(0, keys.shape[1] // PAIR, pair, 0)


def deltas_of(slope_t, mixture_t, deltas):
    for head in range(slope_t.shape[0] // HEAD_DIM):
        rows = slice(head * HEAD_DIM, (head + 1) * HEAD_DIM)
        deltas[head] = jnp.sum(
            slope_t[rows, :].astype(F32) * mixture_t[rows, :].astype(F32), axis=0, keepdims=True
        )


def swap(array, mask, devices):
    return lax.ppermute(array, AXES, [(i, i ^ mask) for i in range(devices)])


Z_FIRST = ((8, 24, 2, 4), (24, 8, 4, 2))
CROSSED = ((8, 24, 4, 2), (24, 8, 2, 4))


def turned_swap(array, step, orders=Z_FIRST):
    return lax.ppermute(array, AXES, [(i, i ^ orders[i % 2][step]) for i in range(32)])


def after(value, *others):
    return lax.optimization_barrier((value, others))[0]


def places(me, orders=Z_FIRST):
    found = []
    for core in range(2):
        even = ((me & 1) ^ core) == 0
        masks = [jnp.where(even, first, second) for first, second in zip(*orders)]
        for far in range(2):
            for slot in range(8):
                device = me ^ core if core else me
                for step, bit in enumerate((slot & 1, slot & 2, slot & 4, far)):
                    if bit:
                        device = device ^ masks[step]
                found.append((core, far, slot, device))
    return found


def unpack(me, pieces, stride, first, rows, scratch, orders=Z_FIRST):
    for core, far, slot, device in places(me, orders):
        ref = pieces[2 * core + far]
        at = slot * stride + first
        scratch[pl.ds(pl.multiple_of(device * rows, rows), rows), :] = ref[at : at + rows, :]


def sort_vectors(me, pieces, stride, first, narrow, sheet):
    width, blocks = sheet.shape[1], sheet.shape[0]
    lane = lax.broadcasted_iota(jnp.int32, (8, width), 1)
    per = width // (blocks * narrow)
    near, far = jnp.zeros((8, width), F32), jnp.zeros((8, width), F32)
    sheet[...] = jnp.zeros_like(sheet)
    for core, distant, slot, device in places(me):
        part = pieces[2 * core + distant][slot * stride + first : (slot + 1) * stride, :].astype(F32)
        group = lane // narrow
        near = near + jnp.where(group == device, part, 0.0)
        far = far + jnp.where(group == lax.rem(device + 1, width // narrow), part, 0.0)
        wide = jnp.where(lane[7:8, :] // (blocks * narrow) == lax.rem(device, per), part[7:8, :], 0.0)
        sheet[pl.ds(lax.div(device, per), 1), :] += wide
    far = pltpu.roll(far, width - narrow, 1)
    return jnp.concatenate([near[:7, :], far[:6, :]], axis=0)


class Grads:
    def __init__(self, me, refs, dense, rows, orders=Z_FIRST):
        self.me, self.refs, self.dense, self.rows, self.orders = me, refs, dense, rows, orders

    def put(self, index, grad):
        if self.dense is None:
            self.refs[index][...] = grad
            return
        self.dense[...] = grad
        rows = self.rows
        for core, far, slot, device in places(self.me, self.orders):
            found = self.dense[pl.ds(pl.multiple_of(device * rows, rows), rows), :]
            self.refs[core][far * 8 + slot, index * rows : (index + 1) * rows, :] = found.astype(BF16)

    def put_sums(self, first, sums):
        if self.dense is None:
            self.refs[-1][...] = sums
            return
        low = sums.astype(BF16)
        for ref in self.refs:
            for slot in range(16):
                ref[slot, first : first + sums.shape[0], :] = low


def grad_outs(packed, count, rows, width, sums):
    if packed:
        return [((16, count * rows + sums, width), BF16)] * 2
    return [((width, width), F32)] * count + [((sums, width), F32)]


COSTS = {}


def padded(shape, dtype):
    last = -(-shape[-1] // 128) * 128
    tall = -(-shape[-2] // 16) * 16 if len(shape) > 1 else 16
    return math.prod(shape[:-2]) * tall * last * jnp.dtype(dtype).itemsize


def snug(arrays):
    return 2 * sum(padded(a.shape, a.dtype) for a in arrays) + (3 << 20)


def call(kernel, outs, args, scratch, micros, name, room=10):
    moved = sum(math.prod(a.shape) * a.dtype.itemsize for a in args[1:])
    moved += sum(math.prod(s) * jnp.dtype(d).itemsize for s, d in outs)
    need = sum(padded(a.shape, a.dtype) for a in args[1:])
    need += sum(padded(s, d) for s, d in list(outs) + list(scratch))
    return pl.pallas_call(
        kernel,
        out_shape=[jax.ShapeDtypeStruct(s, d) for s, d in outs],
        in_specs=[SM] + [VM] * (len(args) - 1),
        out_specs=[VM] * len(outs),
        scratch_shapes=[pltpu.VMEM(s, d) for s, d in scratch],
        compiler_params=pltpu.CompilerParams(vmem_limit_bytes=min(need + (room << 20), 58 << 20)),
        cost_estimate=pl.CostEstimate(
            flops=int(COSTS.get(name, 0) * 1.15e9) + 1, bytes_accessed=1, transcendentals=0
        ),
        name=name,
    )(*args)


def tokens_packet(turn, tokens, memory, target_ids, source_ids, cotangent):
    block, width = tokens.shape[1:]
    memory_block = memory.shape[1]
    first = block + memory_block + 8

    def kernel(turn_ref, targets, sources, tokens_ref, memory_ref, cot_ref, sent, kept):
        mine = turn_ref[0]
        for row, out in ((1 - mine, sent), (mine, kept)):
            out[:block, :] = tokens_ref[row]
            out[block : block + memory_block, :] = memory_ref[row]
            ids = targets[pl.ds(row, 1), :].astype(F32)
            ids = jnp.concatenate([ids, jnp.zeros((1, width - block), F32)], axis=1)
            others = sources[pl.ds(row, 1), :].astype(F32)
            others = jnp.concatenate([others, jnp.zeros((1, width - memory_block), F32)], axis=1)
            place = lax.broadcasted_iota(jnp.int32, (8, width), 0)
            found = jnp.where(place == 0, ids, jnp.where(place == 1, others, 0.0))
            out[block + memory_block : first, :] = found.astype(BF16)
            out[first:, :] = cot_ref[row]

    shape = (first + block, width)
    return call(kernel, [(shape, BF16)] * 2, (turn, target_ids, source_ids, tokens, memory, cotangent),
                [], 1.0, "tokens_packet", 58)


def placed(me, parts, width):
    here = lax.broadcasted_iota(jnp.int32, (parts.shape[1], width), 0) + me * parts.shape[1]
    lane = lax.broadcasted_iota(jnp.int32, (parts.shape[1], width), 1)
    return dot(parts, jnp.where(lane == here, 1.0, 0.0).astype(BF16))


def make_weights_packet(narrow, width, blocks):
    tall = blocks * narrow

    def kernel(me_ref, *refs):
        weights, inner, outer, wide, short = refs[:8], refs[8], refs[9], refs[10], refs[11:24]
        first, second, third = refs[24:]
        me = me_ref[0]
        for i, ref in enumerate(weights):
            if i < 3:
                first[i * narrow : (i + 1) * narrow, :] = ref[...]
            else:
                second[(i - 3) * narrow : (i - 2) * narrow, :] = ref[...]
        short = jnp.concatenate([ref[...].astype(F32) for ref in short], axis=0).astype(BF16)
        near = placed(me, short[:7, :], width)
        far = placed(lax.rem(me + 1, width // narrow), short[7:, :], width)
        far = jnp.concatenate([far, jnp.zeros((1, width), F32)], axis=0)
        row = placed(lax.rem(me, width // wide.shape[1]), wide[...], width)
        first[3 * narrow :, :] = jnp.concatenate([near + far, row], axis=0).astype(BF16)
        for i in range(blocks):
            third[i * narrow : (i + 1) * narrow, :] = inner[:, i * width : (i + 1) * width]
        third[tall:, :] = outer[...]

    return kernel, [((rows, width), BF16) for rows in (3 * narrow + 8, 5 * narrow, 2 * tall)]


def join(arrays):
    def kernel(*refs):
        at = 0
        for ref in refs[:-1]:
            refs[-1][at : at + ref.shape[0], :] = ref[...]
            at += ref.shape[0]

    rows = sum(a.shape[0] for a in arrays)
    return pl.pallas_call(
        kernel,
        out_shape=jax.ShapeDtypeStruct((rows, arrays[0].shape[1]), arrays[0].dtype),
        in_specs=[VM] * len(arrays),
        out_specs=VM,
        compiler_params=pltpu.CompilerParams(vmem_limit_bytes=snug(arrays)),
        cost_estimate=pl.CostEstimate(flops=1 << 20, bytes_accessed=0, transcendentals=0),
        name="join",
    )(*arrays)


def make_project(packed, parts, rows, block, memory_block, width, narrow, blocks, n_pieces):
    share = rows * block
    length = parts * share
    memory_share = rows * memory_block
    stride = 3 * narrow + 8
    half = width // 2

    def kernel(*refs):
        me_ref, refs = refs[0], list(refs[1:])
        pieces, refs = refs[:n_pieces], refs[n_pieces:]
        tokens, refs = refs[: parts * rows], refs[parts * rows :]
        query, query_t, keys, values, value_t = (refs[2 * i : 2 * i + 2] for i in range(5))
        memory, ids, memory_ids, vectors = refs[10:14]
        scratch = refs[14:]
        me = me_ref[0]
        if packed:
            for i in range(3):
                unpack(me, pieces, stride, i * narrow, narrow, scratch[i])
            query_w, key_w, value_w, sheet = scratch
            biases = sort_vectors(me, pieces, stride, 3 * narrow, narrow, sheet)
            rest = jnp.zeros((5 - sheet.shape[0], width), F32)
            vectors[...] = jnp.concatenate([biases[2:, :], sheet[...], rest], axis=0)
        else:
            query_w, key_w, value_w = pieces[:3]
            biases = pieces[3][:8, :]
            vectors[...] = pieces[3][8:, :]
        for i in range(parts):
            here = slice(i * share, (i + 1) * share)
            some = tokens[i * rows : (i + 1) * rows]
            own = jnp.concatenate([t[:block, :] for t in some], axis=0)
            if i == 0:
                scaled = (dot(own, query_w[...]) + biases[0:1, :]).astype(BF16) * BF16(HEAD_DIM**-0.5)
            key = dot(own, key_w[...]).astype(BF16)
            found = (dot(own, value_w[...]) + biases[1:2, :]).astype(BF16)
            for side in range(2):
                columns = slice(side * half, (side + 1) * half)
                if i == 0:
                    query[side][...] = scaled[:, columns]
                    query_t[side][...] = scaled[:, columns].T
                keys[side][here, :] = key[:, columns]
                values[side][here, :] = found[:, columns]
                value_t[side][:, here] = found[:, columns].T
        for i, t in enumerate(tokens):
            memory[i * memory_block : (i + 1) * memory_block, :] = t[block : block + memory_block, :]
            found = t[block + memory_block : block + memory_block + 8, :].astype(F32).astype(jnp.int32)
            ids[:, i * block : (i + 1) * block] = found[0:1, :block]
        found = [t[block + memory_block : block + memory_block + 8, :].astype(F32).astype(jnp.int32)[1:2, :memory_block] for t in tokens]
        memory_ids[...] = jnp.concatenate(found, axis=1)

    outs = [((share, half), BF16)] * 2 + [((half, share), BF16)] * 2
    outs += [((length, half), BF16)] * 4 + [((half, length), BF16)] * 2
    outs += [
        ((parts * memory_share, width), BF16),
        ((1, length), jnp.int32),
        ((1, parts * memory_share), jnp.int32),
        ((16, width), F32),
    ]
    return kernel, outs, [((width, width), BF16)] * 3 + [((blocks, width), F32)] if packed else []


def make_self_attention(share, length, width):
    def kernel(me_ref, *refs):
        query_t, keys, value_t, ids = refs[:2], refs[2:4], refs[4:6], refs[6]
        mixture_t, logs, hot, penalty = refs[7:9], refs[9:11], refs[11], refs[12]
        hot[...] = one_hot(ids[...])
        penalty[...] = penalties(ids[:, :share])
        for side in range(2):
            attend(query_t[side], keys[side], value_t[side], hot, penalty, mixture_t[side], logs[side])

    outs = [((width // 2, share), BF16)] * 2 + [((HEADS // 2, 1, share), F32)] * 2
    return kernel, outs, [((length, PAIR), BF16), ((PAIR, share), BF16)]


def make_cross_forward(packed, rows, block, memory_length, width, narrow, n_pieces):
    share = rows * block
    stride = 5 * narrow

    def kernel(*refs):
        me_ref, refs = refs[0], list(refs[1:])
        pieces, refs = refs[:n_pieces], refs[n_pieces:]
        tokens, refs = refs[:rows], refs[rows:]
        memory, ids, memory_ids, upper, lower, vectors = refs[:6]
        first_sum, second_sum, query, memory_keys, memory_values, cross_t, logs = refs[6:13]
        scratch = refs[13:]
        query_t, value_t, hot, penalty = scratch[:4]
        if packed:
            for i in range(5):
                unpack(me_ref[0], pieces, stride, i * narrow, narrow, scratch[4 + i])
            output_w, query_w, key_w, value_w, source_w = scratch[4:]
        else:
            output_w, query_w, key_w, value_w, source_w = pieces[:5]

        def vector(i):
            return vectors[i : i + 1, :]

        own = jnp.concatenate([t[:block, :] for t in tokens], axis=0)
        mixture_t = jnp.concatenate([upper[...], lower[...]], axis=0)
        h = own.astype(F32) + dot_tn(mixture_t, output_w[...]) + vector(OUTPUT_BIAS)
        first_sum[...] = h
        first = normalize(h)[0] * vector(ATTENTION_GAIN) + vector(ATTENTION_SHIFT)
        scaled = (dot(first.astype(BF16), query_w[...]) + vector(SOURCE_QUERY_BIAS)).astype(BF16) * BF16(HEAD_DIM**-0.5)
        query[...] = scaled
        query_t[...] = scaled.T
        memory_keys[...] = dot(memory[...], key_w[...]).astype(BF16)
        memory_values[...] = (dot(memory[...], value_w[...]) + vector(SOURCE_VALUE_BIAS)).astype(BF16)
        value_t[...] = memory_values[...].T
        hot[...] = one_hot(memory_ids[...])
        penalty[...] = penalties(ids[:, :share])
        attend(query_t, memory_keys, value_t, hot, penalty, cross_t, logs)
        first = normalize(first_sum[...])[0] * vector(ATTENTION_GAIN) + vector(ATTENTION_SHIFT)
        second_sum[...] = first + dot_tn(cross_t[...], source_w[...]) + vector(SOURCE_OUTPUT_BIAS)

    outs = [
        ((share, width), F32),
        ((share, width), F32),
        ((share, width), BF16),
        ((memory_length, width), BF16),
        ((memory_length, width), BF16),
        ((width, share), BF16),
        ((HEADS, 1, share), F32),
    ]
    scratch = [((width, share), BF16), ((width, memory_length), BF16), ((memory_length, PAIR), BF16), ((PAIR, share), BF16)]
    if packed:
        scratch += [((width, width), BF16)] * 5
    return kernel, outs, scratch


def make_inner(packed, rows, block, width, hidden, narrow, n_pieces):
    blocks = hidden // width
    share = rows * block
    per = width // (blocks * narrow)

    def kernel(*refs):
        me_ref, refs = refs[0], list(refs[1:])
        pieces, refs = refs[:n_pieces], refs[n_pieces:]
        second_sum, cot_own, cot_came, vectors = refs[:4]
        out_own, out_send, back, sums = refs[4:8]
        grads, scratch = refs[8:10], refs[10:]
        low, active, gate, slope = scratch[:4]
        if packed:
            inner_w, outer_w, gathered, dense = scratch[4:8]
            tall = blocks * narrow
            for core, far, slot, device in places(me_ref[0]):
                ref, at = pieces[2 * core + far], slot * 2 * tall
                row = pl.multiple_of(device * narrow, narrow)
                for i in range(blocks):
                    inner_w[i, pl.ds(row, narrow), :] = ref[at + i * narrow : at + (i + 1) * narrow, :]
                row = pl.multiple_of(lax.rem(device, per) * tall, tall)
                outer_w[lax.div(device, per), pl.ds(row, tall), :] = ref[at + tall : at + 2 * tall, :]
        else:
            inner_w, outer_w = pieces

        def vector(i):
            return vectors[i : i + 1, :]

        second = normalize(second_sum[...])[0] * vector(SOURCE_GAIN) + vector(SOURCE_SHIFT)
        low[...] = second.astype(BF16)
        back[...] = second + vector(OUTER_BIAS)

        def forward(i, carry):
            inner = dot(low[...], inner_w[i]) + vectors[pl.ds(INNER_BIAS + i, 1), :]
            chance, density = normal_parts(inner)
            found = (inner * chance).astype(BF16)
            active[i] = found
            gate[i] = chance + inner * density
            back[...] += dot(found, outer_w[i])
            return carry

        lax.fori_loop(0, blocks, forward, 0)
        normed, inverse = normalize(back[...])
        final = normed * vector(FINAL_GAIN) + vector(FINAL_SHIFT)
        out_own[...] = final[:block, :]
        out_send[...] = final[block:, :].astype(BF16)
        upstream = jnp.concatenate([cot_own[-block:, :], cot_came[-block:, :]], axis=0).astype(F32)
        sums[0:1, :] = total(upstream * normed)
        sums[1:2, :] = total(upstream)
        back3 = normalize_back(upstream, normed, inverse, vector(FINAL_GAIN))
        slope[...] = back3.astype(BF16)
        sums[2:3, :] = total(slope[...])
        sums[7:8, :] = jnp.zeros_like(sums[7:8, :])
        back[...] = back3

        def backward(i, carry):
            grad = dot_nt(slope[...], outer_w[i]) * gate[i]
            inner_low = grad.astype(BF16)
            sums[pl.ds(3 + i, 1), :] = total(inner_low)
            outer_grad = dot_tn(active[i], slope[...])
            inner_grad = dot_tn(low[...], inner_low)
            back[...] += dot_nt(inner_low, inner_w[i])
            if packed:
                dense[...] = inner_grad
                gathered[i] = outer_grad.astype(BF16)
                here = pl.ds(pl.multiple_of(i * narrow, narrow), narrow)
                for core, far, slot, device in places(me_ref[0]):
                    row = pl.multiple_of(device * narrow, narrow)
                    grads[core][far * 8 + slot, here, :] = dense[pl.ds(row, narrow), :].astype(BF16)
            else:
                grads[0][i] = inner_grad
                grads[1][i] = outer_grad
            return carry

        lax.fori_loop(0, blocks, backward, 0)
        if packed:
            tall = blocks * narrow
            for core, far, slot, device in places(me_ref[0]):
                row = pl.multiple_of(lax.rem(device, per) * tall, tall)
                grads[core][far * 8 + slot, tall:, :] = gathered[lax.div(device, per), pl.ds(row, tall), :]

    outs = [((block, width), F32), ((block, width), BF16), ((share, width), F32), ((8, width), F32)]
    if packed:
        outs += [((16, 2 * blocks * narrow, width), BF16)] * 2
    else:
        outs += [((blocks, width, width), F32)] * 2
    scratch = [((share, width), BF16), ((blocks, share, width), BF16), ((blocks, share, width), F32), ((share, width), BF16)]
    if packed:
        scratch += [((blocks, width, width), BF16)] * 3 + [((width, width), F32)]
    return kernel, outs, scratch


def make_cross_back(packed, parts, share, memory_share, width, narrow, n_pieces):
    memory_length = parts * memory_share
    stride = 5 * narrow

    def kernel(*refs):
        me_ref, refs = refs[0], list(refs[1:])
        pieces, refs = refs[:n_pieces], refs[n_pieces:]
        (back2_in, first_sum, second_sum, query, memory_keys, memory_values, cross_t, logs, ids,
         memory_ids, vectors, sums_inner) = refs[:12]
        mixtures, refs = refs[12:14], refs[14:]
        back1, key_own, value_own, sums = refs[:4]
        self_slope, self_slope_t, self_deltas = (refs[4 + 2 * i : 6 + 2 * i] for i in range(3))
        sends, refs = refs[10 : 10 + parts - 1], refs[10 + parts - 1 :]
        grads, scratch = refs[:3], refs[3:]
        (slope_t, slope, key_t, hot, penalty, query_t, deltas, query_grad_t, key_grad, value_grad) = scratch[:10]
        upper, lower = mixtures
        if packed:
            for i, at in enumerate((0, 1, 4)):
                unpack(me_ref[0], pieces, stride, at * narrow, narrow, scratch[10 + i])
            output_w, query_w, source_w = scratch[10:13]
        else:
            output_w, query_w, source_w = pieces

        def vector(i):
            return vectors[i : i + 1, :]

        sums[0:7, :] = sums_inner[0:7, :]
        upstream = back2_in[...]
        normed, inverse = normalize(second_sum[...])
        sums[7:8, :] = total(upstream * normed)
        sums[8:9, :] = total(upstream)
        back2 = normalize_back(upstream, normed, inverse, vector(SOURCE_GAIN))
        back1[...] = back2
        cross_low = back2.astype(BF16)
        sums[9:10, :] = total(cross_low)
        grads[0][...] = dot(cross_t[...], cross_low).astype(BF16)
        found = dot_nt(cross_low, source_w[...]).astype(BF16)
        slope[...] = found
        slope_t[...] = found.T
        deltas_of(slope_t, cross_t, deltas)
        query_t[...] = query[...].T
        key_t[...] = memory_keys[...].T
        hot[...] = one_hot(memory_ids[...])
        penalty[...] = penalties(ids[:, :share])
        attend_back(query_t, query, memory_keys, key_t, memory_values, slope_t, slope, hot, penalty,
                    logs, deltas, query_grad_t, key_grad, value_grad)
        key_own[...] = key_grad[:memory_share, :]
        value_own[...] = value_grad[:memory_share, :]
        for i in range(1, parts):
            here = slice(i * memory_share, (i + 1) * memory_share)
            sends[i - 1][:memory_share, :] = key_grad[here, :].astype(BF16)
            sends[i - 1][memory_share:, :] = value_grad[here, :].astype(BF16)
        query_low = query_grad_t[...].T.astype(BF16)
        sums[10:11, :] = total(query_low)
        normed, inverse = normalize(first_sum[...])
        first_low = (normed * vector(ATTENTION_GAIN) + vector(ATTENTION_SHIFT)).astype(BF16)
        grads[1][...] = dot_tn(first_low, query_low).astype(BF16)
        upstream = back1[...] + dot_nt(query_low, query_w[...])
        sums[11:12, :] = total(upstream * normed)
        sums[12:13, :] = total(upstream)
        grad = normalize_back(upstream, normed, inverse, vector(ATTENTION_GAIN))
        back1[...] = grad
        branch_low = grad.astype(BF16)
        sums[13:14, :] = total(branch_low)
        sums[14:16, :] = jnp.zeros_like(sums[14:16, :])
        mixture_t = jnp.concatenate([upper[...], lower[...]], axis=0)
        grads[2][...] = dot(mixture_t, branch_low).astype(BF16)
        found = dot_nt(branch_low, output_w[...]).astype(BF16)
        for side in range(2):
            columns = slice(side * width // 2, (side + 1) * width // 2)
            self_slope[side][...] = found[:, columns]
            self_slope_t[side][...] = found[:, columns].T
            deltas_of(self_slope_t[side], mixtures[side], self_deltas[side])

    half = width // 2
    outs = [
        ((share, width), F32),
        ((memory_share, width), F32),
        ((memory_share, width), F32),
        ((16, width), F32),
    ]
    outs += [((share, half), BF16)] * 2 + [((half, share), BF16)] * 2
    outs += [((HEADS // 2, 1, share), F32)] * 2
    outs += [((2 * memory_share, width), BF16)] * (parts - 1)
    outs += [((width, width), BF16)] * 3
    scratch = [
        ((width, share), BF16),
        ((share, width), BF16),
        ((width, memory_length), BF16),
        ((memory_length, PAIR), BF16),
        ((PAIR, share), BF16),
        ((width, share), BF16),
        ((HEADS, 1, share), F32),
        ((width, share), F32),
        ((memory_length, width), F32),
        ((memory_length, width), F32),
    ]
    if packed:
        scratch += [((width, width), BF16)] * 3
    return kernel, outs, scratch


def attention_back_half(refs, share, scratch):
    query, keys, values, slope, slope_t, logs, deltas, ids = refs
    query_t, key_t, hot, penalty, query_grad_t, key_grad, value_grad = scratch
    query_t[...] = query[...].T
    key_t[...] = keys[...].T
    hot[...] = one_hot(ids[...])
    penalty[...] = penalties(ids[:, :share])
    attend_back(query_t, query, keys, key_t, values, slope_t, slope, hot, penalty, logs, deltas,
                query_grad_t, key_grad, value_grad)


def half_scratch(share, length, half):
    return [
        ((half, share), BF16),
        ((half, length), BF16),
        ((length, PAIR), BF16),
        ((PAIR, share), BF16),
        ((half, share), F32),
        ((length, half), F32),
        ((length, half), F32),
    ]


def give_half(share, scratch, own, sends):
    key_grad, value_grad = scratch[5:7]
    own[:share, :] = key_grad[:share, :]
    own[share:, :] = value_grad[:share, :]
    for i, send in enumerate(sends):
        here = slice((i // 2 + 1) * share, (i // 2 + 2) * share)
        send[...] = (key_grad, value_grad)[i % 2][here, :].astype(BF16)


def make_memory_back(packed, parts, rows, block, memory_block, width, narrow, n_pieces):
    memory_share = rows * memory_block

    def kernel(*refs):
        me_ref, refs = refs[0], list(refs[1:])
        pieces, refs = refs[:n_pieces], refs[n_pieces:]
        tokens, refs = refs[:rows], refs[rows:]
        memory_key_own, memory_value_own, sums_in = refs[:3]
        early, refs = refs[3:6], refs[6:]
        memory_received, refs = refs[: parts - 1], refs[parts - 1 :]
        memory_own, memory_send = refs[:2]
        n_grads = 2 if packed else 3
        grad_refs, scratch = refs[2 : 2 + n_grads], refs[2 + n_grads :]
        sums = scratch[0]
        me = me_ref[0]
        if packed:
            for i in range(2):
                unpack(me, pieces, 5 * narrow, (2 + i) * narrow, narrow, scratch[1 + i])
            source_key, source_value = scratch[1:3]
        else:
            source_key, source_value = pieces
        grads = Grads(me, grad_refs, scratch[3] if packed else None, narrow, CROSSED)
        memory = jnp.concatenate([t[block : block + memory_block, :] for t in tokens], axis=0)
        key_sum, value_sum = memory_key_own[...], memory_value_own[...]
        for ref in memory_received:
            key_sum = key_sum + ref[:memory_share, :].astype(F32)
            value_sum = value_sum + ref[memory_share:, :].astype(F32)
        key_low, value_low = key_sum.astype(BF16), value_sum.astype(BF16)
        sums[...] = sums_in[...]
        sums[14:15, :] = total(value_low)
        grads.put_sums(5 * narrow, sums[...])
        grads.put(0, dot_tn(memory, key_low))
        grads.put(1, dot_tn(memory, value_low))
        if packed:
            for i, ref in enumerate(early):
                grads.put(2 + i, ref[...].astype(F32))
        grad = dot_nt(key_low, source_key[...]) + dot_nt(value_low, source_value[...])
        memory_own[...] = grad[:memory_block, :]
        memory_send[...] = grad[memory_block:, :].astype(BF16)

    outs = [((memory_block, width), F32), ((memory_block, width), BF16)]
    if packed:
        outs += [((16, 5 * narrow + 16, width), BF16)] * 2
    else:
        outs += [((width, width), F32)] * 2 + [((16, width), F32)]
    scratch = [((16, width), F32)]
    if packed:
        scratch += [((width, width), BF16)] * 2 + [((width, width), F32)]
    return kernel, outs, scratch


def make_self_back_upper(parts, share, width):
    length, half = parts * share, width // 2

    def kernel(*refs):
        operands, (query_grad, own), refs = refs[1:9], refs[9:11], refs[11:]
        sends, scratch = refs[: 2 * parts - 2], refs[2 * parts - 2 :]
        attention_back_half(operands, share, scratch)
        query_grad[...] = scratch[4][...].T.astype(BF16)
        give_half(share, scratch, own, sends)

    outs = [((share, half), BF16), ((2 * share, half), F32)] + [((share, half), BF16)] * (2 * parts - 2)
    return kernel, outs, half_scratch(share, length, half)


def make_self_back_lower(packed, parts, rows, block, width, narrow, n_pieces):
    share = rows * block
    length, half = parts * share, width // 2

    def kernel(*refs):
        me_ref, refs = refs[0], list(refs[1:])
        pieces, refs = refs[:n_pieces], refs[n_pieces:]
        tokens, refs = refs[:rows], refs[rows:]
        operands, refs = refs[:8], refs[8:]
        back1, query_upper = refs[:2]
        in_part, query_sum, query_w_grad, own = refs[2:6]
        sends, scratch = refs[6 : 4 + 2 * parts], refs[4 + 2 * parts :]
        if packed:
            unpack(me_ref[0], pieces, 3 * narrow + 8, 0, narrow, scratch[7])
            query_w = scratch[7]
        else:
            (query_w,) = pieces
        attention_back_half(operands, share, scratch[:7])
        give_half(share, scratch, own, sends)
        query_low = jnp.concatenate([query_upper[...], scratch[4][...].T.astype(BF16)], axis=1)
        tokens_own = jnp.concatenate([t[:block, :] for t in tokens], axis=0)
        in_part[...] = back1[...] + dot_nt(query_low, query_w[...])
        query_sum[...] = jnp.concatenate([total(query_low), jnp.zeros((7, width), F32)], axis=0)
        query_w_grad[...] = dot_tn(tokens_own, query_low).astype(query_w_grad.dtype)

    outs = [
        ((share, width), F32),
        ((8, width), F32),
        ((width, width), BF16 if packed else F32),
        ((2 * share, half), F32),
    ]
    outs += [((share, half), BF16)] * (2 * parts - 2)
    scratch = half_scratch(share, length, half)
    if packed:
        scratch += [((width, width), BF16)]
    return kernel, outs, scratch


def make_last(packed, parts, rows, block, memory_block, width, narrow, n_pieces):
    share = rows * block

    def kernel(*refs):
        me_ref, refs = refs[0], list(refs[1:])
        pieces, refs = refs[:n_pieces], refs[n_pieces:]
        tokens, refs = refs[:rows], refs[rows:]
        in_part, query_sum, query_w_grad, memory_send = refs[:4]
        owns, refs = refs[4:6], refs[6:]
        received = [refs[: 2 * parts - 2], refs[2 * parts - 2 : 4 * parts - 4]]
        refs = refs[4 * parts - 4 :]
        in_own, in_send = refs[:2]
        n_grads = 2 if packed else 3
        grad_refs, scratch = refs[2 : 2 + n_grads], refs[2 + n_grads :]
        sums = scratch[0]
        me = me_ref[0]
        if packed:
            for i in range(2):
                unpack(me, pieces, 3 * narrow + 8, (1 + i) * narrow, narrow, scratch[1 + i])
            key_w, value_w = scratch[1:3]
        else:
            key_w, value_w = pieces
        grads = Grads(me, grad_refs, scratch[3] if packed else None, narrow)
        if packed:
            grads.put(2, query_w_grad[...].astype(F32))
        lows = []
        for own, others in zip(owns, received):
            found = own[...]
            for key, value in zip(others[::2], others[1::2]):
                found = found + jnp.concatenate([key[...], value[...]], axis=0).astype(F32)
            lows.append(found.astype(BF16))
        key_low = jnp.concatenate([low[:share, :] for low in lows], axis=1)
        value_low = jnp.concatenate([low[share:, :] for low in lows], axis=1)
        tokens_own = jnp.concatenate([t[:block, :] for t in tokens], axis=0)
        sums[...] = query_sum[...]
        sums[1:2, :] = total(value_low)
        grads.put_sums(3 * narrow, sums[...])
        grads.put(0, dot_tn(tokens_own, key_low))
        grads.put(1, dot_tn(tokens_own, value_low))
        grad = in_part[...] + dot_nt(key_low, key_w[...]) + dot_nt(value_low, value_w[...])
        in_own[...] = grad[:block, :]
        in_send[:block, :] = grad[block:, :].astype(BF16)
        in_send[block:, :] = memory_send[...]

    outs = [((block, width), F32), ((block + memory_block, width), BF16)]
    if packed:
        outs += [((16, 3 * narrow + 8, width), BF16)] * 2
    else:
        outs += [((width, width), F32)] * 2 + [((8, width), F32)]
    scratch = [((8, width), F32)]
    if packed:
        scratch += [((width, width), BF16)] * 2 + [((width, width), F32)]
    return kernel, outs, scratch


def combine(arrays, splits, micros=0.1):
    count = arrays[0].shape[0] // splits
    shape = (count,) + arrays[0].shape[1:]

    def kernel(*refs):
        given, outs = refs[: len(arrays)], refs[len(arrays) :]
        for i, out in enumerate(outs):
            here = slice(i * count, (i + 1) * count)
            found = given[0][here].astype(F32)
            for ref in given[1:]:
                found = found + ref[here].astype(F32)
            out[...] = found.astype(out.dtype)

    return pl.pallas_call(
        kernel,
        out_shape=[jax.ShapeDtypeStruct(shape, BF16)] * splits,
        in_specs=[VM] * len(arrays),
        out_specs=[VM] * splits,
        compiler_params=pltpu.CompilerParams(vmem_limit_bytes=snug(arrays)),
        cost_estimate=pl.CostEstimate(flops=int(micros * 1.15e9), bytes_accessed=0, transcendentals=0),
        name="combine",
    )(*arrays)


def combine_joint(groups, splits):
    count, sizes = groups[0][0].shape[0] // splits, [g[0].shape[1] for g in groups]
    shape = (count, sum(sizes)) + groups[0][0].shape[2:]
    flat = [a for group in groups for a in group]

    def kernel(*refs):
        outs, at, row = refs[len(flat) :], 0, 0
        for group, size in zip(groups, sizes):
            given = refs[at : at + len(group)]
            at += len(group)
            for i, out in enumerate(outs):
                here = slice(i * count, (i + 1) * count)
                found = given[0][here].astype(F32)
                for ref in given[1:]:
                    found = found + ref[here].astype(F32)
                out[:, row : row + size, :] = found.astype(BF16)
            row += size

    return pl.pallas_call(
        kernel,
        out_shape=[jax.ShapeDtypeStruct(shape, BF16)] * splits,
        in_specs=[VM] * len(flat),
        out_specs=[VM] * splits,
        compiler_params=pltpu.CompilerParams(vmem_limit_bytes=snug(flat)),
        cost_estimate=pl.CostEstimate(flops=1, bytes_accessed=1, transcendentals=0),
        name="combine_joint",
    )(*flat)


def chosen(me, rows, wide):
    width = rows.shape[1]
    line = lax.broadcasted_iota(jnp.int32, (width, wide), 0)
    here = lax.broadcasted_iota(jnp.int32, (width, wide), 1) + me * wide
    choice = jnp.where(line == here, 1.0, 0.0)
    return lax.dot_general(rows, choice, (((1,), (0,)), ((), ())), precision=lax.Precision.HIGHEST, preferred_element_type=F32)


def reduce_all(array, devices):
    mask = 1
    while mask < devices:
        array = array + swap(array, mask, devices)
        mask *= 2
    return array


def per_device(
    tokens, memory, target_ids, source_ids, cotangent,
    query_weight, key_weight, value_weight, output_weight, query_bias, value_bias, output_bias,
    attention_gain, attention_shift,
    source_query, source_key, source_value, source_output, source_query_bias, source_value_bias,
    source_output_bias, source_gain, source_shift,
    inner_weight, inner_bias, outer_weight, outer_bias, final_gain, final_shift,
    *, devices, sequence,
):
    packed = devices == 32
    rows, block, width = tokens.shape
    memory_block = memory.shape[1]
    parts = sequence // rows
    share, memory_share = rows * block, rows * memory_block
    hidden = inner_weight.shape[1]
    blocks = hidden // width
    me = lax.axis_index(AXES)
    me_array = me.reshape(1).astype(jnp.int32)
    turn = lax.rem(lax.div(me, parts), rows)
    narrow, wide = width // devices, hidden // devices

    def run(made, micros, name, *args, room=10):
        kernel, outs, *scratch = made
        return call(kernel, outs, (me_array,) + args, scratch[0] if scratch else [], micros, name, room)

    short = [query_bias, value_bias, output_bias, attention_gain, attention_shift, source_query_bias,
             source_value_bias, source_output_bias, source_gain, source_shift, outer_bias, final_gain,
             final_shift]

    def whole(array):
        return lax.all_gather(array, AXES, axis=0, tiled=True)

    sent, kept = tokens_packet(
        turn.reshape(1).astype(jnp.int32), tokens, memory, target_ids, source_ids, cotangent
    )
    came = swap(sent, parts, devices)
    row_tokens = [kept, came]
    kept_swaps = [swap(kept, m, devices) for m in range(1, parts)]
    came_swaps = [swap(came, m, devices) for m in range(1, parts)]
    for pair in zip(kept_swaps, came_swaps):
        row_tokens += pair
    own_tokens = row_tokens[:rows]

    if packed:
        first, second, third = run(make_weights_packet(narrow, width, blocks), 1.0, "weights_packet",
                          query_weight, key_weight, value_weight, output_weight, source_query,
                          source_key, source_value, source_output, inner_weight, outer_weight,
                          inner_bias.reshape(1, wide), *[v.reshape(1, narrow) for v in short], room=58)
        first = after(first, sent)
        first = join([first, turned_swap(first, 0)])
        first_b = turned_swap(first, 1)
        second = after(second, first)
        second_b = turned_swap(second, 0)
        first, second = join(after([first, first_b], second_b)), join(after([second, second_b], first_b))
        third = after(third, second)
        first_b, second_b, third_b = turned_swap(first, 2), turned_swap(second, 1), turned_swap(third, 0)
        first_c = join(after([first, first_b], second_b, third_b, came, *kept_swaps))
        second = join(after([second, second_b], first_b, third_b))
        third = join(after([third, third_b], first_b, second_b))
        first_d, second_b, third_b = turned_swap(first_c, 3), turned_swap(second, 2), turned_swap(third, 1)
        second_c = join(after([second, second_b], first_d, third_b))
        third = join(after([third, third_b], first_d, second_b))
        first_d = after(first_d, second_c, third, *came_swaps)
        second_d, third_b = turned_swap(second_c, 3), turned_swap(third, 2)
        set_self = [first_c, first_d, swap(first_c, 1, 32), swap(first_d, 1, 32)]
    else:
        full = [whole(w) for w in (query_weight, key_weight, value_weight, output_weight, source_query, source_key, source_value, source_output)]
        lane = lax.broadcasted_iota(jnp.int32, (1, width), 1)
        place = lax.broadcasted_iota(jnp.int32, (blocks, width), 0) * width + lane
        spread_wide = jnp.where(place // wide == me, jnp.tile(inner_bias.reshape(1, wide), (blocks, width // wide)), 0)

        def natural(rows):
            return jnp.where(lane // narrow == me, jnp.tile(rows, (1, devices)), 0)

        vectors = jnp.concatenate([natural(jnp.stack(short[:2])), jnp.zeros((6, width), BF16), natural(jnp.stack(short[2:])), spread_wide, jnp.zeros((1, width), BF16)])
        vectors = reduce_all(vectors, devices).astype(F32)
        set_self = full[:3] + [vectors]
        set_cross = full[3:]
        set_inner = [
            whole(inner_weight).reshape(width, blocks, width).transpose(1, 0, 2),
            whole(outer_weight).reshape(blocks, width, width),
        ]
    found = run(
        make_project(packed, parts, rows, block, memory_block, width, narrow, blocks, len(set_self)), 5.0,
        "project", *set_self, *row_tokens,
    )
    query, query_t, keys, values, value_t = (found[2 * i : 2 * i + 2] for i in range(5))
    row_memory, ids, memory_ids, vectors = found[10:]
    query_t = list(query_t)
    if packed:
        set_query, set_last = set_self, set_self
    else:
        set_back, set_query, set_last, set_memory = [full[3], full[4], full[7]], full[:1], full[1:3], full[5:7]
    found = run(
        make_self_attention(share, parts * share, width), 12.0, "self_attention",
        *query_t, *keys, *value_t, ids,
    )
    mixtures, logs = found[:2], found[2:]
    if packed:
        third_c = join(after([third, third_b], mixtures[0]))
        third_d = turned_swap(third_c, 3)
        second_d = after(second_d, mixtures[0])
        set_cross = [second_c, second_d, swap(second_c, 1, 32), swap(second_d, 1, 32)]
        set_back, set_memory = set_cross, set_cross
    first_sum, second_sum, cross_query, memory_keys, memory_values, cross_t, cross_logs = run(
        make_cross_forward(packed, rows, block, parts * memory_share, width, narrow, len(set_cross)),
        9.0, "cross_forward", *set_cross, *own_tokens, row_memory, ids, memory_ids, *mixtures, vectors,
    )
    if packed:
        third_d = after(third_d, second_sum)
        set_inner = [third_c, third_d, swap(third_c, 1, 32), swap(third_d, 1, 32)]
    out_own, out_send, back2_in, sums_inner, *grads_inner = run(
        make_inner(packed, rows, block, width, hidden, narrow, len(set_inner)), 18.0, "inner",
        *set_inner, second_sum, kept, came, vectors,
    )
    found = run(
        make_cross_back(packed, parts, share, memory_share, width, narrow, len(set_back)), 14.0,
        "cross_back", *set_back, back2_in, first_sum, second_sum, cross_query, memory_keys,
        memory_values, cross_t, cross_logs, ids, memory_ids, vectors, sums_inner, *mixtures,
    )
    back1, memory_key_own, memory_value_own, sums_cross = found[:4]
    slope, slope_t, deltas = (found[4 + 2 * i : 6 + 2 * i] for i in range(3))
    memory_received = [swap(a, m + 1, devices) for m, a in enumerate(found[10 : 10 + parts - 1])]
    grads_early = found[10 + parts - 1 :]
    query = list(query)
    if packed:
        keep, send = combine(after([grads_inner[0], swap(grads_inner[1], 1, 32)], back1), 2)
        inner_step = [keep, turned_swap(send, 3)]
        memory_key_own = after(memory_key_own, keep)
    memory_own, memory_send, *grads_cross = run(
        make_memory_back(packed, parts, rows, block, memory_block, width, narrow, len(set_memory)),
        2.0, "memory_back", *set_memory, *own_tokens, memory_key_own, memory_value_own, sums_cross,
        *grads_early, *memory_received,
    )
    if packed:
        cross_came = swap(grads_cross[1], 1, 32)
        query[0] = after(query[0], grads_cross[0])
    found = run(
        make_self_back_upper(parts, share, width), 7.0, "self_back_upper", query[0], keys[0],
        values[0], slope[0], slope_t[0], logs[0], deltas[0], ids,
    )
    query_upper, own_upper = found[:2]
    received_upper = [swap(a, m // 2 + 1, devices) for m, a in enumerate(found[2:])]
    if packed:
        keep_cross, send = combine(after([grads_cross[0], cross_came], query_upper), 2)
        cross_step = [keep_cross, turned_swap(send, 3, CROSSED)]
        query[1] = after(query[1], keep_cross)
    in_part, query_sum, query_w_grad, own_lower, *sends = run(
        make_self_back_lower(packed, parts, rows, block, width, narrow, len(set_query)), 11.0,
        "self_back_lower", *set_query, *own_tokens, query[1], keys[1], values[1], slope[1],
        slope_t[1], logs[1], deltas[1], ids, back1, query_upper,
    )
    received_lower = [swap(a, m // 2 + 1, devices) for m, a in enumerate(sends)]
    if packed:
        keep, send = combine(after(inner_step, query_sum), 2)
        inner_step = [keep, turned_swap(send, 2)]
        keep_cross, send = combine(after(cross_step, query_sum), 2)
        cross_step = [keep_cross, turned_swap(send, 2, CROSSED)]
        in_part = after(in_part, keep, keep_cross)
    in_own, in_send, *grads_last = run(
        make_last(packed, parts, rows, block, memory_block, width, narrow, len(set_last)), 6.0,
        "last", *set_last, *own_tokens, in_part, query_sum, query_w_grad, memory_send, own_upper,
        own_lower, *received_upper, *received_lower,
    )

    if packed:
        keep, send = combine([grads_last[0], swap(grads_last[1], 1, 32)], 2)
        last_step = [keep, turned_swap(send, 3)]
        in_send, out_send = after((in_send, out_send), last_step[1])
        keep_joint, send = combine_joint(after([inner_step, cross_step], in_own), 2)
        joint_step = [keep_joint, turned_swap(send, 1)]
        keep, send = combine(after(last_step, keep_joint), 2)
        last_step = [keep, turned_swap(send, 2)]
        keep, send = combine(after(last_step, *joint_step), 2)
        last_step = [keep, turned_swap(send, 1)]
        keep, send = combine_joint([joint_step, last_step], 2)
        final_step = [keep, turned_swap(send, 0)]

        def plan(me_ref, *refs):
            me = me_ref[0]
            found, outs = refs[0][0].astype(F32) + refs[1][0].astype(F32), refs[2:]
            first, second = 2 * blocks * narrow, 2 * blocks * narrow + 5 * narrow + 16
            inner, cross, last = found[:first, :], found[first:second, :], found[second:, :]
            for i in range(blocks):
                outs[0][:, i * width : (i + 1) * width] = inner[i * narrow : (i + 1) * narrow, :]
            outs[1][...] = inner[blocks * narrow :, :]
            for i in range(5):
                outs[2 + i][...] = cross[i * narrow : (i + 1) * narrow, :]
            for i in range(3):
                outs[7 + i][...] = last[i * narrow : (i + 1) * narrow, :]
            rows_in = jnp.concatenate([cross[5 * narrow :, :], last[3 * narrow :, :]], axis=0)
            outs[10][...] = chosen(me, rows_in, narrow)
            per = width // wide
            line = lax.broadcasted_iota(jnp.int32, (blocks, width), 0)
            row = jnp.sum(jnp.where(line == lax.div(me, per), rows_in[3 : 3 + blocks, :], 0.0), axis=0, keepdims=True)
            outs[11][...] = chosen(lax.rem(me, per), row, wide)

        part = (narrow, width)
        shapes = [(narrow, hidden), (wide, width)] + [part] * 8 + [(24, narrow), (1, wide)]
        (inner_share, outer_share, source_key_share, source_value_share, source_output_share,
         source_query_share, output_share, key_share, value_share, query_share, sums,
         inner_bias_share) = call(
            plan, [(s, F32) for s in shapes], (me_array, *final_step), [], 2.0,
            "finish",
        )
        inner_bias_share = inner_bias_share.reshape(wide)
    else:
        def scatter(array):
            return lax.psum_scatter(array, AXES, scatter_dimension=0, tiled=True)

        inner_share = scatter(grads_inner[0].transpose(1, 0, 2).reshape(width, hidden))
        outer_share = scatter(grads_inner[1].reshape(hidden, width))
        source_output_share, source_query_share, output_share = (scatter(g.astype(F32)) for g in grads_early)
        source_key_share, source_value_share = (scatter(g) for g in grads_cross[:2])
        key_share, value_share = (scatter(g) for g in grads_last[:2])
        query_share = scatter(query_w_grad)
        sums = reduce_all(jnp.concatenate([grads_cross[2], grads_last[2]], axis=0), devices)
        inner_bias_share = lax.dynamic_slice(sums[3 : 3 + blocks].reshape(hidden), (me * wide,), (wide,))
        sums = lax.dynamic_slice(sums, (0, me * narrow), (sums.shape[0], narrow))
    def regroup(mine, came):
        came = came.astype(F32)
        return jnp.where(turn == 0, jnp.stack([mine, came]), jnp.stack([came, mine]))

    output = regroup(out_own, swap(out_send, parts, devices))
    in_came = swap(in_send, parts, devices)
    input_gradient = regroup(in_own, in_came[:block])
    memory_gradient = regroup(memory_own, in_came[block:])

    return (
        output,
        input_gradient,
        memory_gradient,
        query_share,
        key_share,
        value_share,
        output_share,
        sums[16],
        sums[17],
        sums[13],
        sums[11],
        sums[12],
        source_query_share,
        source_key_share,
        source_value_share,
        source_output_share,
        sums[10],
        sums[14],
        sums[9],
        sums[7],
        sums[8],
        inner_share,
        inner_bias_share,
        outer_share,
        sums[2],
        sums[0],
        sums[1],
    )


def solution(mesh):
    sequence, devices = mesh.shape["seq"], mesh.size
    tokens, ids = P("dp", "seq", None), P("dp", "seq")
    matrix, vector = P(AXES, None), P(AXES)
    attention = (matrix,) * 4 + (vector,) * 5
    inner = (matrix, vector, matrix, vector, vector, vector)
    return jax.shard_map(
        functools.partial(per_device, devices=devices, sequence=sequence),
        mesh=mesh,
        in_specs=(tokens, tokens, ids, ids, tokens) + attention + attention + inner,
        out_specs=(tokens, tokens, tokens) + attention + attention + inner,
        check_vma=False,
    )
```

```python
import functools
import math

import jax
import jax.numpy as jnp
from jax import lax
from jax.experimental import pallas as pl
from jax.experimental.pallas import tpu as pltpu
from jax.sharding import PartitionSpec as P

HEADS = 8
HEAD_DIM = 64
PAIR = 128
EPSILON = 1e-05
MASKED = 1e9
AXES = ("dp", "seq")
F32 = jnp.float32
BF16 = jnp.bfloat16

(
    OUTPUT_BIAS,
    ATTENTION_GAIN,
    ATTENTION_SHIFT,
    SOURCE_QUERY_BIAS,
    SOURCE_VALUE_BIAS,
    SOURCE_OUTPUT_BIAS,
    SOURCE_GAIN,
    SOURCE_SHIFT,
    OUTER_BIAS,
    FINAL_GAIN,
    FINAL_SHIFT,
    INNER_BIAS,
) = range(12)
Z_MASKS = (0, 8, 16, 24)
VM = pl.BlockSpec(memory_space=pltpu.VMEM)
SM = pl.BlockSpec(memory_space=pltpu.SMEM)


def dot(a, b):
    return lax.dot_general(a, b, (((1,), (0,)), ((), ())), preferred_element_type=F32)


def dot_nt(a, b):
    return lax.dot_general(a, b, (((1,), (1,)), ((), ())), preferred_element_type=F32)


def dot_tn(a, b):
    return lax.dot_general(a, b, (((0,), (0,)), ((), ())), preferred_element_type=F32)


def total(values):
    return jnp.sum(values.astype(F32), axis=0, keepdims=True)


def normalize(h):
    average = jnp.mean(h, axis=-1, keepdims=True)
    centered = h - average
    variance = jnp.mean(centered * centered, axis=-1, keepdims=True)
    inverse = lax.rsqrt(variance + EPSILON)
    return centered * inverse, inverse


def normalize_back(upstream, normed, inverse, gain):
    scaled = upstream * gain
    first_mean = jnp.mean(scaled, axis=-1, keepdims=True)
    second_mean = jnp.mean(scaled * normed, axis=-1, keepdims=True)
    return inverse * (scaled - first_mean - normed * second_mean)


def normal_parts(v):
    density = 0.3989422804014327 * jnp.exp(-0.5 * v * v)
    t = 1.0 / (1.0 + 0.2316419 * jnp.abs(v))
    series = t * (
        0.319381530
        + t * (-0.356563782 + t * (1.781477937 + t * (-1.821255978 + t * 1.330274429)))
    )
    tail = density * series
    return jnp.where(v >= 0.0, 1.0 - tail, tail), density


def penalties(ids):
    place = lax.broadcasted_iota(jnp.int32, (PAIR, ids.shape[1]), 0)
    return jnp.where((place == ids) | (place >= 4), 0.0, -MASKED).astype(BF16)


def one_hot(ids):
    place = lax.broadcasted_iota(jnp.int32, (PAIR, ids.shape[1]), 0)
    return jnp.where(place == ids, 1.0, 0.0).astype(F32).T.astype(BF16)


def spread(part, half):
    empty = jnp.zeros_like(part)
    return [part, empty] if half == 0 else [empty, part]


def attend(query_t, keys, value_t, hot, penalty, mixture_t, logs):
    length = keys.shape[0]

    def pair(p, carry):
        columns = pl.ds(pl.multiple_of(p * PAIR, PAIR), PAIR)
        left = jnp.concatenate([keys[:, columns], hot[...]], axis=1)
        for half in range(2):
            rows = pl.ds(pl.multiple_of(p * PAIR + half * HEAD_DIM, HEAD_DIM), HEAD_DIM)
            right = jnp.concatenate(spread(query_t[rows, :], half) + [penalty[...]], axis=0)
            scores = dot(left, right)
            highest = jnp.max(scores, axis=0, keepdims=True)
            weights = jnp.exp(scores - highest).astype(BF16)
            values = jnp.concatenate(
                [value_t[rows, :], jnp.ones((16, length), BF16)], axis=0
            )
            found = dot(values, weights)
            denominator = found[HEAD_DIM : HEAD_DIM + 1, :]
            mixture_t[rows, :] = (found[:HEAD_DIM, :] / denominator).astype(BF16)
            logs[2 * p + half] = highest + jnp.log(denominator)
        return carry

    lax.fori_loop(0, keys.shape[1] // PAIR, pair, 0)


def attend_back(
    query_t, query, keys, key_t, values, slope_t, slope, hot, penalty, logs, deltas,
    query_grad_t, key_grad, value_grad,
):
    tokens = query.shape[0]
    lane = lax.broadcasted_iota(jnp.int32, (tokens, PAIR), 1)

    def pair(p, carry):
        columns = pl.ds(pl.multiple_of(p * PAIR, PAIR), PAIR)
        left = jnp.concatenate([keys[:, columns], hot[...]], axis=1)
        value_pair = values[:, columns]
        key_sum, value_sum = None, None
        for half in range(2):
            rows = pl.ds(pl.multiple_of(p * PAIR + half * HEAD_DIM, HEAD_DIM), HEAD_DIM)
            right = jnp.concatenate(spread(query_t[rows, :], half) + [penalty[...]], axis=0)
            chances = jnp.exp(dot(left, right) - logs[2 * p + half])
            slopes = dot(value_pair, jnp.concatenate(spread(slope_t[rows, :], half), axis=0))
            grads = (chances * (slopes - deltas[2 * p + half])).astype(BF16)
            query_grad_t[rows, :] = dot(key_t[rows, :], grads) * HEAD_DIM**-0.5
            mine = (lane < HEAD_DIM) if half == 0 else (lane >= HEAD_DIM)
            none = jnp.zeros((tokens, PAIR), BF16)
            value_part = dot(chances.astype(BF16), jnp.where(mine, slope[:, columns], none))
            key_part = dot(grads, jnp.where(mine, query[:, columns], none))
            value_sum = value_part if value_sum is None else value_sum + value_part
            key_sum = key_part if key_sum is None else key_sum + key_part
        key_grad[:, columns] = key_sum
        value_grad[:, columns] = value_sum
        return carry

    lax.fori_loop(0, keys.shape[1] // PAIR, pair, 0)


def deltas_of(slope_t, mixture_t, deltas):
    for head in range(slope_t.shape[0] // HEAD_DIM):
        rows = slice(head * HEAD_DIM, (head + 1) * HEAD_DIM)
        deltas[head] = jnp.sum(
            slope_t[rows, :].astype(F32) * mixture_t[rows, :].astype(F32), axis=0, keepdims=True
        )


def swap(array, mask, devices):
    return lax.ppermute(array, AXES, [(i, i ^ mask) for i in range(devices)])


Z_FIRST = ((8, 24, 2, 4), (24, 8, 4, 2))
CROSSED = ((8, 24, 4, 2), (24, 8, 2, 4))


def turned_swap(array, step, orders=Z_FIRST):
    return lax.ppermute(array, AXES, [(i, i ^ orders[i % 2][step]) for i in range(32)])


def after(value, *others):
    return lax.optimization_barrier((value, others))[0]


def places(me, orders=Z_FIRST):
    found = []
    for core in range(2):
        even = ((me & 1) ^ core) == 0
        masks = [jnp.where(even, first, second) for first, second in zip(*orders)]
        for far in range(2):
            for slot in range(8):
                device = me ^ core if core else me
                for step, bit in enumerate((slot & 1, slot & 2, slot & 4, far)):
                    if bit:
                        device = device ^ masks[step]
                found.append((core, far, slot, device))
    return found


def unpack(me, pieces, stride, first, rows, scratch, orders=Z_FIRST):
    for core, far, slot, device in places(me, orders):
        ref = pieces[2 * core + far]
        at = slot * stride + first
        scratch[pl.ds(pl.multiple_of(device * rows, rows), rows), :] = ref[at : at + rows, :]


def sort_vectors(me, pieces, stride, first, narrow, sheet):
    width, blocks = sheet.shape[1], sheet.shape[0]
    lane = lax.broadcasted_iota(jnp.int32, (8, width), 1)
    per = width // (blocks * narrow)
    near, far = jnp.zeros((8, width), F32), jnp.zeros((8, width), F32)
    sheet[...] = jnp.zeros_like(sheet)
    for core, distant, slot, device in places(me):
        part = pieces[2 * core + distant][slot * stride + first : (slot + 1) * stride, :].astype(F32)
        group = lane // narrow
        near = near + jnp.where(group == device, part, 0.0)
        far = far + jnp.where(group == lax.rem(device + 1, width // narrow), part, 0.0)
        wide = jnp.where(lane[7:8, :] // (blocks * narrow) == lax.rem(device, per), part[7:8, :], 0.0)
        sheet[pl.ds(lax.div(device, per), 1), :] += wide
    far = pltpu.roll(far, width - narrow, 1)
    return jnp.concatenate([near[:7, :], far[:6, :]], axis=0)


class Grads:
    def __init__(self, me, refs, dense, rows, orders=Z_FIRST):
        self.me, self.refs, self.dense, self.rows, self.orders = me, refs, dense, rows, orders

    def put(self, index, grad):
        if self.dense is None:
            self.refs[index][...] = grad
            return
        self.dense[...] = grad
        rows = self.rows
        for core, far, slot, device in places(self.me, self.orders):
            found = self.dense[pl.ds(pl.multiple_of(device * rows, rows), rows), :]
            self.refs[core][far * 8 + slot, index * rows : (index + 1) * rows, :] = found.astype(BF16)

    def put_sums(self, first, sums):
        if self.dense is None:
            self.refs[-1][...] = sums
            return
        low = sums.astype(BF16)
        for ref in self.refs:
            for slot in range(16):
                ref[slot, first : first + sums.shape[0], :] = low


def grad_outs(packed, count, rows, width, sums):
    if packed:
        return [((16, count * rows + sums, width), BF16)] * 2
    return [((width, width), F32)] * count + [((sums, width), F32)]


COSTS = {}


def padded(shape, dtype):
    last = -(-shape[-1] // 128) * 128
    tall = -(-shape[-2] // 16) * 16 if len(shape) > 1 else 16
    return math.prod(shape[:-2]) * tall * last * jnp.dtype(dtype).itemsize


def snug(arrays):
    return 2 * sum(padded(a.shape, a.dtype) for a in arrays) + (3 << 20)


def call(kernel, outs, args, scratch, micros, name, room=10):
    moved = sum(math.prod(a.shape) * a.dtype.itemsize for a in args[1:])
    moved += sum(math.prod(s) * jnp.dtype(d).itemsize for s, d in outs)
    need = sum(padded(a.shape, a.dtype) for a in args[1:])
    need += sum(padded(s, d) for s, d in list(outs) + list(scratch))
    return pl.pallas_call(
        kernel,
        out_shape=[jax.ShapeDtypeStruct(s, d) for s, d in outs],
        in_specs=[SM] + [VM] * (len(args) - 1),
        out_specs=[VM] * len(outs),
        scratch_shapes=[pltpu.VMEM(s, d) for s, d in scratch],
        compiler_params=pltpu.CompilerParams(vmem_limit_bytes=min(need + (room << 20), 58 << 20)),
        cost_estimate=pl.CostEstimate(
            flops=int(COSTS.get(name, 0) * 1.15e9) + 1, bytes_accessed=1, transcendentals=0
        ),
        name=name,
    )(*args)


def tokens_packet(turn, tokens, memory, target_ids, source_ids, cotangent):
    block, width = tokens.shape[1:]
    memory_block = memory.shape[1]
    first = block + memory_block + 8

    def kernel(turn_ref, targets, sources, tokens_ref, memory_ref, cot_ref, sent, kept):
        mine = turn_ref[0]
        for row, out in ((1 - mine, sent), (mine, kept)):
            out[:block, :] = tokens_ref[row]
            out[block : block + memory_block, :] = memory_ref[row]
            ids = targets[pl.ds(row, 1), :].astype(F32)
            ids = jnp.concatenate([ids, jnp.zeros((1, width - block), F32)], axis=1)
            others = sources[pl.ds(row, 1), :].astype(F32)
            others = jnp.concatenate([others, jnp.zeros((1, width - memory_block), F32)], axis=1)
            place = lax.broadcasted_iota(jnp.int32, (8, width), 0)
            found = jnp.where(place == 0, ids, jnp.where(place == 1, others, 0.0))
            out[block + memory_block : first, :] = found.astype(BF16)
            out[first:, :] = cot_ref[row]

    shape = (first + block, width)
    return call(kernel, [(shape, BF16)] * 2, (turn, target_ids, source_ids, tokens, memory, cotangent),
                [], 1.0, "tokens_packet", 58)


def placed(me, parts, width):
    here = lax.broadcasted_iota(jnp.int32, (parts.shape[1], width), 0) + me * parts.shape[1]
    lane = lax.broadcasted_iota(jnp.int32, (parts.shape[1], width), 1)
    return dot(parts, jnp.where(lane == here, 1.0, 0.0).astype(BF16))


def make_weights_packet(narrow, width, blocks):
    tall = blocks * narrow

    def kernel(me_ref, *refs):
        weights, inner, outer, wide, short = refs[:8], refs[8], refs[9], refs[10], refs[11:24]
        first, second, third = refs[24:]
        me = me_ref[0]
        for i, ref in enumerate(weights):
            if i < 3:
                first[i * narrow : (i + 1) * narrow, :] = ref[...]
            else:
                second[(i - 3) * narrow : (i - 2) * narrow, :] = ref[...]
        short = jnp.concatenate([ref[...].astype(F32) for ref in short], axis=0).astype(BF16)
        near = placed(me, short[:7, :], width)
        far = placed(lax.rem(me + 1, width // narrow), short[7:, :], width)
        far = jnp.concatenate([far, jnp.zeros((1, width), F32)], axis=0)
        row = placed(lax.rem(me, width // wide.shape[1]), wide[...], width)
        first[3 * narrow :, :] = jnp.concatenate([near + far, row], axis=0).astype(BF16)
        for i in range(blocks):
            third[i * narrow : (i + 1) * narrow, :] = inner[:, i * width : (i + 1) * width]
        third[tall:, :] = outer[...]

    return kernel, [((rows, width), BF16) for rows in (3 * narrow + 8, 5 * narrow, 2 * tall)]


def join(arrays):
    def kernel(*refs):
        at = 0
        for ref in refs[:-1]:
            refs[-1][at : at + ref.shape[0], :] = ref[...]
            at += ref.shape[0]

    rows = sum(a.shape[0] for a in arrays)
    return pl.pallas_call(
        kernel,
        out_shape=jax.ShapeDtypeStruct((rows, arrays[0].shape[1]), arrays[0].dtype),
        in_specs=[VM] * len(arrays),
        out_specs=VM,
        compiler_params=pltpu.CompilerParams(vmem_limit_bytes=snug(arrays)),
        cost_estimate=pl.CostEstimate(flops=1 << 20, bytes_accessed=0, transcendentals=0),
        name="join",
    )(*arrays)


def make_project(packed, parts, rows, block, memory_block, width, narrow, blocks, n_pieces):
    share = rows * block
    length = parts * share
    memory_share = rows * memory_block
    stride = 3 * narrow + 8
    half = width // 2

    def kernel(*refs):
        me_ref, refs = refs[0], list(refs[1:])
        pieces, refs = refs[:n_pieces], refs[n_pieces:]
        tokens, refs = refs[: parts * rows], refs[parts * rows :]
        query, query_t, keys, values, value_t = (refs[2 * i : 2 * i + 2] for i in range(5))
        memory, ids, memory_ids, vectors = refs[10:14]
        scratch = refs[14:]
        me = me_ref[0]
        if packed:
            for i in range(3):
                unpack(me, pieces, stride, i * narrow, narrow, scratch[i])
            query_w, key_w, value_w, sheet = scratch
            biases = sort_vectors(me, pieces, stride, 3 * narrow, narrow, sheet)
            rest = jnp.zeros((5 - sheet.shape[0], width), F32)
            vectors[...] = jnp.concatenate([biases[2:, :], sheet[...], rest], axis=0)
        else:
            query_w, key_w, value_w = pieces[:3]
            biases = pieces[3][:8, :]
            vectors[...] = pieces[3][8:, :]
        for i in range(parts):
            here = slice(i * share, (i + 1) * share)
            some = tokens[i * rows : (i + 1) * rows]
            own = jnp.concatenate([t[:block, :] for t in some], axis=0)
            if i == 0:
                scaled = (dot(own, query_w[...]) + biases[0:1, :]).astype(BF16) * BF16(HEAD_DIM**-0.5)
            key = dot(own, key_w[...]).astype(BF16)
            found = (dot(own, value_w[...]) + biases[1:2, :]).astype(BF16)
            for side in range(2):
                columns = slice(side * half, (side + 1) * half)
                if i == 0:
                    query[side][...] = scaled[:, columns]
                    query_t[side][...] = scaled[:, columns].T
                keys[side][here, :] = key[:, columns]
                values[side][here, :] = found[:, columns]
                value_t[side][:, here] = found[:, columns].T
        for i, t in enumerate(tokens):
            memory[i * memory_block : (i + 1) * memory_block, :] = t[block : block + memory_block, :]
            found = t[block + memory_block : block + memory_block + 8, :].astype(F32).astype(jnp.int32)
            ids[:, i * block : (i + 1) * block] = found[0:1, :block]
        found = [t[block + memory_block : block + memory_block + 8, :].astype(F32).astype(jnp.int32)[1:2, :memory_block] for t in tokens]
        memory_ids[...] = jnp.concatenate(found, axis=1)

    outs = [((share, half), BF16)] * 2 + [((half, share), BF16)] * 2
    outs += [((length, half), BF16)] * 4 + [((half, length), BF16)] * 2
    outs += [
        ((parts * memory_share, width), BF16),
        ((1, length), jnp.int32),
        ((1, parts * memory_share), jnp.int32),
        ((16, width), F32),
    ]
    return kernel, outs, [((width, width), BF16)] * 3 + [((blocks, width), F32)] if packed else []


def make_self_attention(share, length, width):
    def kernel(me_ref, *refs):
        query_t, keys, value_t, ids = refs[:2], refs[2:4], refs[4:6], refs[6]
        mixture_t, logs, hot, penalty = refs[7:9], refs[9:11], refs[11], refs[12]
        hot[...] = one_hot(ids[...])
        penalty[...] = penalties(ids[:, :share])
        for side in range(2):
            attend(query_t[side], keys[side], value_t[side], hot, penalty, mixture_t[side], logs[side])

    outs = [((width // 2, share), BF16)] * 2 + [((HEADS // 2, 1, share), F32)] * 2
    return kernel, outs, [((length, PAIR), BF16), ((PAIR, share), BF16)]


def make_cross_forward(packed, rows, block, memory_length, width, narrow, n_pieces):
    share = rows * block
    stride = 5 * narrow

    def kernel(*refs):
        me_ref, refs = refs[0], list(refs[1:])
        pieces, refs = refs[:n_pieces], refs[n_pieces:]
        tokens, refs = refs[:rows], refs[rows:]
        memory, ids, memory_ids, upper, lower, vectors = refs[:6]
        first_sum, second_sum, query, memory_keys, memory_values, cross_t, logs = refs[6:13]
        scratch = refs[13:]
        query_t, value_t, hot, penalty = scratch[:4]
        if packed:
            for i in range(5):
                unpack(me_ref[0], pieces, stride, i * narrow, narrow, scratch[4 + i])
            output_w, query_w, key_w, value_w, source_w = scratch[4:]
        else:
            output_w, query_w, key_w, value_w, source_w = pieces[:5]

        def vector(i):
            return vectors[i : i + 1, :]

        own = jnp.concatenate([t[:block, :] for t in tokens], axis=0)
        mixture_t = jnp.concatenate([upper[...], lower[...]], axis=0)
        h = own.astype(F32) + dot_tn(mixture_t, output_w[...]) + vector(OUTPUT_BIAS)
        first_sum[...] = h
        first = normalize(h)[0] * vector(ATTENTION_GAIN) + vector(ATTENTION_SHIFT)
        scaled = (dot(first.astype(BF16), query_w[...]) + vector(SOURCE_QUERY_BIAS)).astype(BF16) * BF16(HEAD_DIM**-0.5)
        query[...] = scaled
        query_t[...] = scaled.T
        memory_keys[...] = dot(memory[...], key_w[...]).astype(BF16)
        memory_values[...] = (dot(memory[...], value_w[...]) + vector(SOURCE_VALUE_BIAS)).astype(BF16)
        value_t[...] = memory_values[...].T
        hot[...] = one_hot(memory_ids[...])
        penalty[...] = penalties(ids[:, :share])
        attend(query_t, memory_keys, value_t, hot, penalty, cross_t, logs)
        first = normalize(first_sum[...])[0] * vector(ATTENTION_GAIN) + vector(ATTENTION_SHIFT)
        second_sum[...] = first + dot_tn(cross_t[...], source_w[...]) + vector(SOURCE_OUTPUT_BIAS)

    outs = [
        ((share, width), F32),
        ((share, width), F32),
        ((share, width), BF16),
        ((memory_length, width), BF16),
        ((memory_length, width), BF16),
        ((width, share), BF16),
        ((HEADS, 1, share), F32),
    ]
    scratch = [((width, share), BF16), ((width, memory_length), BF16), ((memory_length, PAIR), BF16), ((PAIR, share), BF16)]
    if packed:
        scratch += [((width, width), BF16)] * 5
    return kernel, outs, scratch


def make_inner(packed, rows, block, width, hidden, narrow, n_pieces):
    blocks = hidden // width
    share = rows * block
    per = width // (blocks * narrow)

    def kernel(*refs):
        me_ref, refs = refs[0], list(refs[1:])
        pieces, refs = refs[:n_pieces], refs[n_pieces:]
        second_sum, cot_own, cot_came, vectors = refs[:4]
        out_own, out_send, back, sums = refs[4:8]
        grads, scratch = refs[8:10], refs[10:]
        low, active, gate, slope = scratch[:4]
        if packed:
            inner_w, outer_w, gathered, dense = scratch[4:8]
            tall = blocks * narrow
            for core, far, slot, device in places(me_ref[0]):
                ref, at = pieces[2 * core + far], slot * 2 * tall
                row = pl.multiple_of(device * narrow, narrow)
                for i in range(blocks):
                    inner_w[i, pl.ds(row, narrow), :] = ref[at + i * narrow : at + (i + 1) * narrow, :]
                row = pl.multiple_of(lax.rem(device, per) * tall, tall)
                outer_w[lax.div(device, per), pl.ds(row, tall), :] = ref[at + tall : at + 2 * tall, :]
        else:
            inner_w, outer_w = pieces

        def vector(i):
            return vectors[i : i + 1, :]

        second = normalize(second_sum[...])[0] * vector(SOURCE_GAIN) + vector(SOURCE_SHIFT)
        low[...] = second.astype(BF16)
        back[...] = second + vector(OUTER_BIAS)

        def forward(i, carry):
            inner = dot(low[...], inner_w[i]) + vectors[pl.ds(INNER_BIAS + i, 1), :]
            chance, density = normal_parts(inner)
            found = (inner * chance).astype(BF16)
            active[i] = found
            gate[i] = chance + inner * density
            back[...] += dot(found, outer_w[i])
            return carry

        lax.fori_loop(0, blocks, forward, 0)
        normed, inverse = normalize(back[...])
        final = normed * vector(FINAL_GAIN) + vector(FINAL_SHIFT)
        out_own[...] = final[:block, :]
        out_send[...] = final[block:, :].astype(BF16)
        upstream = jnp.concatenate([cot_own[-block:, :], cot_came[-block:, :]], axis=0).astype(F32)
        sums[0:1, :] = total(upstream * normed)
        sums[1:2, :] = total(upstream)
        back3 = normalize_back(upstream, normed, inverse, vector(FINAL_GAIN))
        slope[...] = back3.astype(BF16)
        sums[2:3, :] = total(slope[...])
        sums[7:8, :] = jnp.zeros_like(sums[7:8, :])
        back[...] = back3

        def backward(i, carry):
            grad = dot_nt(slope[...], outer_w[i]) * gate[i]
            inner_low = grad.astype(BF16)
            sums[pl.ds(3 + i, 1), :] = total(inner_low)
            outer_grad = dot_tn(active[i], slope[...])
            inner_grad = dot_tn(low[...], inner_low)
            back[...] += dot_nt(inner_low, inner_w[i])
            if packed:
                dense[...] = inner_grad
                gathered[i] = outer_grad.astype(BF16)
                here = pl.ds(pl.multiple_of(i * narrow, narrow), narrow)
                for core, far, slot, device in places(me_ref[0]):
                    row = pl.multiple_of(device * narrow, narrow)
                    grads[core][far * 8 + slot, here, :] = dense[pl.ds(row, narrow), :].astype(BF16)
            else:
                grads[0][i] = inner_grad
                grads[1][i] = outer_grad
            return carry

        lax.fori_loop(0, blocks, backward, 0)
        if packed:
            tall = blocks * narrow
            for core, far, slot, device in places(me_ref[0]):
                row = pl.multiple_of(lax.rem(device, per) * tall, tall)
                grads[core][far * 8 + slot, tall:, :] = gathered[lax.div(device, per), pl.ds(row, tall), :]

    outs = [((block, width), F32), ((block, width), BF16), ((share, width), F32), ((8, width), F32)]
    if packed:
        outs += [((16, 2 * blocks * narrow, width), BF16)] * 2
    else:
        outs += [((blocks, width, width), F32)] * 2
    scratch = [((share, width), BF16), ((blocks, share, width), BF16), ((blocks, share, width), F32), ((share, width), BF16)]
    if packed:
        scratch += [((blocks, width, width), BF16)] * 3 + [((width, width), F32)]
    return kernel, outs, scratch


def make_cross_back(packed, parts, share, memory_share, width, narrow, n_pieces):
    memory_length = parts * memory_share
    stride = 5 * narrow

    def kernel(*refs):
        me_ref, refs = refs[0], list(refs[1:])
        pieces, refs = refs[:n_pieces], refs[n_pieces:]
        (back2_in, first_sum, second_sum, query, memory_keys, memory_values, cross_t, logs, ids,
         memory_ids, vectors, sums_inner) = refs[:12]
        mixtures, refs = refs[12:14], refs[14:]
        back1, key_own, value_own, sums = refs[:4]
        self_slope, self_slope_t, self_deltas = (refs[4 + 2 * i : 6 + 2 * i] for i in range(3))
        sends, refs = refs[10 : 10 + parts - 1], refs[10 + parts - 1 :]
        grads, scratch = refs[:3], refs[3:]
        (slope_t, slope, key_t, hot, penalty, query_t, deltas, query_grad_t, key_grad, value_grad) = scratch[:10]
        upper, lower = mixtures
        if packed:
            for i, at in enumerate((0, 1, 4)):
                unpack(me_ref[0], pieces, stride, at * narrow, narrow, scratch[10 + i])
            output_w, query_w, source_w = scratch[10:13]
        else:
            output_w, query_w, source_w = pieces

        def vector(i):
            return vectors[i : i + 1, :]

        sums[0:7, :] = sums_inner[0:7, :]
        upstream = back2_in[...]
        normed, inverse = normalize(second_sum[...])
        sums[7:8, :] = total(upstream * normed)
        sums[8:9, :] = total(upstream)
        back2 = normalize_back(upstream, normed, inverse, vector(SOURCE_GAIN))
        back1[...] = back2
        cross_low = back2.astype(BF16)
        sums[9:10, :] = total(cross_low)
        grads[0][...] = dot(cross_t[...], cross_low).astype(BF16)
        found = dot_nt(cross_low, source_w[...]).astype(BF16)
        slope[...] = found
        slope_t[...] = found.T
        deltas_of(slope_t, cross_t, deltas)
        query_t[...] = query[...].T
        key_t[...] = memory_keys[...].T
        hot[...] = one_hot(memory_ids[...])
        penalty[...] = penalties(ids[:, :share])
        attend_back(query_t, query, memory_keys, key_t, memory_values, slope_t, slope, hot, penalty,
                    logs, deltas, query_grad_t, key_grad, value_grad)
        key_own[...] = key_grad[:memory_share, :]
        value_own[...] = value_grad[:memory_share, :]
        for i in range(1, parts):
            here = slice(i * memory_share, (i + 1) * memory_share)
            sends[i - 1][:memory_share, :] = key_grad[here, :].astype(BF16)
            sends[i - 1][memory_share:, :] = value_grad[here, :].astype(BF16)
        query_low = query_grad_t[...].T.astype(BF16)
        sums[10:11, :] = total(query_low)
        normed, inverse = normalize(first_sum[...])
        first_low = (normed * vector(ATTENTION_GAIN) + vector(ATTENTION_SHIFT)).astype(BF16)
        grads[1][...] = dot_tn(first_low, query_low).astype(BF16)
        upstream = back1[...] + dot_nt(query_low, query_w[...])
        sums[11:12, :] = total(upstream * normed)
        sums[12:13, :] = total(upstream)
        grad = normalize_back(upstream, normed, inverse, vector(ATTENTION_GAIN))
        back1[...] = grad
        branch_low = grad.astype(BF16)
        sums[13:14, :] = total(branch_low)
        sums[14:16, :] = jnp.zeros_like(sums[14:16, :])
        mixture_t = jnp.concatenate([upper[...], lower[...]], axis=0)
        grads[2][...] = dot(mixture_t, branch_low).astype(BF16)
        found = dot_nt(branch_low, output_w[...]).astype(BF16)
        for side in range(2):
            columns = slice(side * width // 2, (side + 1) * width // 2)
            self_slope[side][...] = found[:, columns]
            self_slope_t[side][...] = found[:, columns].T
            deltas_of(self_slope_t[side], mixtures[side], self_deltas[side])

    half = width // 2
    outs = [
        ((share, width), F32),
        ((memory_share, width), F32),
        ((memory_share, width), F32),
        ((16, width), F32),
    ]
    outs += [((share, half), BF16)] * 2 + [((half, share), BF16)] * 2
    outs += [((HEADS // 2, 1, share), F32)] * 2
    outs += [((2 * memory_share, width), BF16)] * (parts - 1)
    outs += [((width, width), BF16)] * 3
    scratch = [
        ((width, share), BF16),
        ((share, width), BF16),
        ((width, memory_length), BF16),
        ((memory_length, PAIR), BF16),
        ((PAIR, share), BF16),
        ((width, share), BF16),
        ((HEADS, 1, share), F32),
        ((width, share), F32),
        ((memory_length, width), F32),
        ((memory_length, width), F32),
    ]
    if packed:
        scratch += [((width, width), BF16)] * 3
    return kernel, outs, scratch


def attention_back_half(refs, share, scratch):
    query, keys, values, slope, slope_t, logs, deltas, ids = refs
    query_t, key_t, hot, penalty, query_grad_t, key_grad, value_grad = scratch
    query_t[...] = query[...].T
    key_t[...] = keys[...].T
    hot[...] = one_hot(ids[...])
    penalty[...] = penalties(ids[:, :share])
    attend_back(query_t, query, keys, key_t, values, slope_t, slope, hot, penalty, logs, deltas,
                query_grad_t, key_grad, value_grad)


def half_scratch(share, length, half):
    return [
        ((half, share), BF16),
        ((half, length), BF16),
        ((length, PAIR), BF16),
        ((PAIR, share), BF16),
        ((half, share), F32),
        ((length, half), F32),
        ((length, half), F32),
    ]


def give_half(share, scratch, own, sends):
    key_grad, value_grad = scratch[5:7]
    own[:share, :] = key_grad[:share, :]
    own[share:, :] = value_grad[:share, :]
    for i, send in enumerate(sends):
        here = slice((i // 2 + 1) * share, (i // 2 + 2) * share)
        send[...] = (key_grad, value_grad)[i % 2][here, :].astype(BF16)


def make_memory_back(packed, parts, rows, block, memory_block, width, narrow, n_pieces):
    memory_share = rows * memory_block

    def kernel(*refs):
        me_ref, refs = refs[0], list(refs[1:])
        pieces, refs = refs[:n_pieces], refs[n_pieces:]
        tokens, refs = refs[:rows], refs[rows:]
        memory_key_own, memory_value_own, sums_in = refs[:3]
        early, refs = refs[3:6], refs[6:]
        memory_received, refs = refs[: parts - 1], refs[parts - 1 :]
        memory_own, memory_send = refs[:2]
        n_grads = 2 if packed else 3
        grad_refs, scratch = refs[2 : 2 + n_grads], refs[2 + n_grads :]
        sums = scratch[0]
        me = me_ref[0]
        if packed:
            for i in range(2):
                unpack(me, pieces, 5 * narrow, (2 + i) * narrow, narrow, scratch[1 + i])
            source_key, source_value = scratch[1:3]
        else:
            source_key, source_value = pieces
        grads = Grads(me, grad_refs, scratch[3] if packed else None, narrow, CROSSED)
        memory = jnp.concatenate([t[block : block + memory_block, :] for t in tokens], axis=0)
        key_sum, value_sum = memory_key_own[...], memory_value_own[...]
        for ref in memory_received:
            key_sum = key_sum + ref[:memory_share, :].astype(F32)
            value_sum = value_sum + ref[memory_share:, :].astype(F32)
        key_low, value_low = key_sum.astype(BF16), value_sum.astype(BF16)
        sums[...] = sums_in[...]
        sums[14:15, :] = total(value_low)
        grads.put_sums(5 * narrow, sums[...])
        grads.put(0, dot_tn(memory, key_low))
        grads.put(1, dot_tn(memory, value_low))
        if packed:
            for i, ref in enumerate(early):
                grads.put(2 + i, ref[...].astype(F32))
        grad = dot_nt(key_low, source_key[...]) + dot_nt(value_low, source_value[...])
        memory_own[...] = grad[:memory_block, :]
        memory_send[...] = grad[memory_block:, :].astype(BF16)

    outs = [((memory_block, width), F32), ((memory_block, width), BF16)]
    if packed:
        outs += [((16, 5 * narrow + 16, width), BF16)] * 2
    else:
        outs += [((width, width), F32)] * 2 + [((16, width), F32)]
    scratch = [((16, width), F32)]
    if packed:
        scratch += [((width, width), BF16)] * 2 + [((width, width), F32)]
    return kernel, outs, scratch


def make_self_back_upper(parts, share, width):
    length, half = parts * share, width // 2

    def kernel(*refs):
        operands, (query_grad, own), refs = refs[1:9], refs[9:11], refs[11:]
        sends, scratch = refs[: 2 * parts - 2], refs[2 * parts - 2 :]
        attention_back_half(operands, share, scratch)
        query_grad[...] = scratch[4][...].T.astype(BF16)
        give_half(share, scratch, own, sends)

    outs = [((share, half), BF16), ((2 * share, half), F32)] + [((share, half), BF16)] * (2 * parts - 2)
    return kernel, outs, half_scratch(share, length, half)


def make_self_back_lower(packed, parts, rows, block, width, narrow, n_pieces):
    share = rows * block
    length, half = parts * share, width // 2

    def kernel(*refs):
        me_ref, refs = refs[0], list(refs[1:])
        pieces, refs = refs[:n_pieces], refs[n_pieces:]
        tokens, refs = refs[:rows], refs[rows:]
        operands, refs = refs[:8], refs[8:]
        back1, query_upper = refs[:2]
        in_part, query_sum, query_w_grad, own = refs[2:6]
        sends, scratch = refs[6 : 4 + 2 * parts], refs[4 + 2 * parts :]
        if packed:
            unpack(me_ref[0], pieces, 3 * narrow + 8, 0, narrow, scratch[7])
            query_w = scratch[7]
        else:
            (query_w,) = pieces
        attention_back_half(operands, share, scratch[:7])
        give_half(share, scratch, own, sends)
        query_low = jnp.concatenate([query_upper[...], scratch[4][...].T.astype(BF16)], axis=1)
        tokens_own = jnp.concatenate([t[:block, :] for t in tokens], axis=0)
        in_part[...] = back1[...] + dot_nt(query_low, query_w[...])
        query_sum[...] = jnp.concatenate([total(query_low), jnp.zeros((7, width), F32)], axis=0)
        query_w_grad[...] = dot_tn(tokens_own, query_low).astype(query_w_grad.dtype)

    outs = [
        ((share, width), F32),
        ((8, width), F32),
        ((width, width), BF16 if packed else F32),
        ((2 * share, half), F32),
    ]
    outs += [((share, half), BF16)] * (2 * parts - 2)
    scratch = half_scratch(share, length, half)
    if packed:
        scratch += [((width, width), BF16)]
    return kernel, outs, scratch


def make_last(packed, parts, rows, block, memory_block, width, narrow, n_pieces):
    share = rows * block

    def kernel(*refs):
        me_ref, refs = refs[0], list(refs[1:])
        pieces, refs = refs[:n_pieces], refs[n_pieces:]
        tokens, refs = refs[:rows], refs[rows:]
        in_part, query_sum, query_w_grad, memory_send = refs[:4]
        owns, refs = refs[4:6], refs[6:]
        received = [refs[: 2 * parts - 2], refs[2 * parts - 2 : 4 * parts - 4]]
        refs = refs[4 * parts - 4 :]
        in_own, in_send = refs[:2]
        n_grads = 2 if packed else 3
        grad_refs, scratch = refs[2 : 2 + n_grads], refs[2 + n_grads :]
        sums = scratch[0]
        me = me_ref[0]
        if packed:
            for i in range(2):
                unpack(me, pieces, 3 * narrow + 8, (1 + i) * narrow, narrow, scratch[1 + i])
            key_w, value_w = scratch[1:3]
        else:
            key_w, value_w = pieces
        grads = Grads(me, grad_refs, scratch[3] if packed else None, narrow)
        if packed:
            grads.put(2, query_w_grad[...].astype(F32))
        lows = []
        for own, others in zip(owns, received):
            found = own[...]
            for key, value in zip(others[::2], others[1::2]):
                found = found + jnp.concatenate([key[...], value[...]], axis=0).astype(F32)
            lows.append(found.astype(BF16))
        key_low = jnp.concatenate([low[:share, :] for low in lows], axis=1)
        value_low = jnp.concatenate([low[share:, :] for low in lows], axis=1)
        tokens_own = jnp.concatenate([t[:block, :] for t in tokens], axis=0)
        sums[...] = query_sum[...]
        sums[1:2, :] = total(value_low)
        grads.put_sums(3 * narrow, sums[...])
        grads.put(0, dot_tn(tokens_own, key_low))
        grads.put(1, dot_tn(tokens_own, value_low))
        grad = in_part[...] + dot_nt(key_low, key_w[...]) + dot_nt(value_low, value_w[...])
        in_own[...] = grad[:block, :]
        in_send[:block, :] = grad[block:, :].astype(BF16)
        in_send[block:, :] = memory_send[...]

    outs = [((block, width), F32), ((block + memory_block, width), BF16)]
    if packed:
        outs += [((16, 3 * narrow + 8, width), BF16)] * 2
    else:
        outs += [((width, width), F32)] * 2 + [((8, width), F32)]
    scratch = [((8, width), F32)]
    if packed:
        scratch += [((width, width), BF16)] * 2 + [((width, width), F32)]
    return kernel, outs, scratch


def combine(arrays, splits, micros=0.1):
    count = arrays[0].shape[0] // splits
    shape = (count,) + arrays[0].shape[1:]

    def kernel(*refs):
        given, outs = refs[: len(arrays)], refs[len(arrays) :]
        for i, out in enumerate(outs):
            here = slice(i * count, (i + 1) * count)
            found = given[0][here].astype(F32)
            for ref in given[1:]:
                found = found + ref[here].astype(F32)
            out[...] = found.astype(out.dtype)

    return pl.pallas_call(
        kernel,
        out_shape=[jax.ShapeDtypeStruct(shape, BF16)] * splits,
        in_specs=[VM] * len(arrays),
        out_specs=[VM] * splits,
        compiler_params=pltpu.CompilerParams(vmem_limit_bytes=snug(arrays)),
        cost_estimate=pl.CostEstimate(flops=int(micros * 1.15e9), bytes_accessed=0, transcendentals=0),
        name="combine",
    )(*arrays)


def combine_joint(groups, splits):
    count, sizes = groups[0][0].shape[0] // splits, [g[0].shape[1] for g in groups]
    shape = (count, sum(sizes)) + groups[0][0].shape[2:]
    flat = [a for group in groups for a in group]

    def kernel(*refs):
        outs, at, row = refs[len(flat) :], 0, 0
        for group, size in zip(groups, sizes):
            given = refs[at : at + len(group)]
            at += len(group)
            for i, out in enumerate(outs):
                here = slice(i * count, (i + 1) * count)
                found = given[0][here].astype(F32)
                for ref in given[1:]:
                    found = found + ref[here].astype(F32)
                out[:, row : row + size, :] = found.astype(BF16)
            row += size

    return pl.pallas_call(
        kernel,
        out_shape=[jax.ShapeDtypeStruct(shape, BF16)] * splits,
        in_specs=[VM] * len(flat),
        out_specs=[VM] * splits,
        compiler_params=pltpu.CompilerParams(vmem_limit_bytes=snug(flat)),
        cost_estimate=pl.CostEstimate(flops=1, bytes_accessed=1, transcendentals=0),
        name="combine_joint",
    )(*flat)


def chosen(me, rows, wide):
    width = rows.shape[1]
    line = lax.broadcasted_iota(jnp.int32, (width, wide), 0)
    here = lax.broadcasted_iota(jnp.int32, (width, wide), 1) + me * wide
    choice = jnp.where(line == here, 1.0, 0.0)
    return lax.dot_general(rows, choice, (((1,), (0,)), ((), ())), precision=lax.Precision.HIGHEST, preferred_element_type=F32)


def reduce_all(array, devices):
    mask = 1
    while mask < devices:
        array = array + swap(array, mask, devices)
        mask *= 2
    return array


def per_device(
    tokens, memory, target_ids, source_ids, cotangent,
    query_weight, key_weight, value_weight, output_weight, query_bias, value_bias, output_bias,
    attention_gain, attention_shift,
    source_query, source_key, source_value, source_output, source_query_bias, source_value_bias,
    source_output_bias, source_gain, source_shift,
    inner_weight, inner_bias, outer_weight, outer_bias, final_gain, final_shift,
    *, devices, sequence,
):
    packed = devices == 32
    rows, block, width = tokens.shape
    memory_block = memory.shape[1]
    parts = sequence // rows
    share, memory_share = rows * block, rows * memory_block
    hidden = inner_weight.shape[1]
    blocks = hidden // width
    me = lax.axis_index(AXES)
    me_array = me.reshape(1).astype(jnp.int32)
    turn = lax.rem(lax.div(me, parts), rows)
    narrow, wide = width // devices, hidden // devices

    def run(made, micros, name, *args, room=10):
        kernel, outs, *scratch = made
        return call(kernel, outs, (me_array,) + args, scratch[0] if scratch else [], micros, name, room)

    short = [query_bias, value_bias, output_bias, attention_gain, attention_shift, source_query_bias,
             source_value_bias, source_output_bias, source_gain, source_shift, outer_bias, final_gain,
             final_shift]

    def whole(array):
        return lax.all_gather(array, AXES, axis=0, tiled=True)

    sent, kept = tokens_packet(
        turn.reshape(1).astype(jnp.int32), tokens, memory, target_ids, source_ids, cotangent
    )
    came = swap(sent, parts, devices)
    row_tokens = [kept, came]
    kept_swaps = [swap(kept, m, devices) for m in range(1, parts)]
    came_swaps = [swap(came, m, devices) for m in range(1, parts)]
    for pair in zip(kept_swaps, came_swaps):
        row_tokens += pair
    own_tokens = row_tokens[:rows]

    if packed:
        first, second, third = run(make_weights_packet(narrow, width, blocks), 1.0, "weights_packet",
                          query_weight, key_weight, value_weight, output_weight, source_query,
                          source_key, source_value, source_output, inner_weight, outer_weight,
                          inner_bias.reshape(1, wide), *[v.reshape(1, narrow) for v in short], room=58)
        first = after(first, sent)
        first = join([first, turned_swap(first, 0)])
        first_b = turned_swap(first, 1)
        second = after(second, first)
        second_b = turned_swap(second, 0)
        first, second = join(after([first, first_b], second_b)), join(after([second, second_b], first_b))
        third = after(third, second)
        first_b, second_b, third_b = turned_swap(first, 2), turned_swap(second, 1), turned_swap(third, 0)
        first_c = join(after([first, first_b], second_b, third_b, came, *kept_swaps))
        second = join(after([second, second_b], first_b, third_b))
        third = join(after([third, third_b], first_b, second_b))
        first_d, second_b, third_b = turned_swap(first_c, 3), turned_swap(second, 2), turned_swap(third, 1)
        second_c = join(after([second, second_b], first_d, third_b))
        third = join(after([third, third_b], first_d, second_b))
        first_d = after(first_d, second_c, third, *came_swaps)
        second_d, third_b = turned_swap(second_c, 3), turned_swap(third, 2)
        set_self = [first_c, first_d, swap(first_c, 1, 32), swap(first_d, 1, 32)]
    else:
        full = [whole(w) for w in (query_weight, key_weight, value_weight, output_weight, source_query, source_key, source_value, source_output)]
        lane = lax.broadcasted_iota(jnp.int32, (1, width), 1)
        place = lax.broadcasted_iota(jnp.int32, (blocks, width), 0) * width + lane
        spread_wide = jnp.where(place // wide == me, jnp.tile(inner_bias.reshape(1, wide), (blocks, width // wide)), 0)

        def natural(rows):
            return jnp.where(lane // narrow == me, jnp.tile(rows, (1, devices)), 0)

        vectors = jnp.concatenate([natural(jnp.stack(short[:2])), jnp.zeros((6, width), BF16), natural(jnp.stack(short[2:])), spread_wide, jnp.zeros((1, width), BF16)])
        vectors = reduce_all(vectors, devices).astype(F32)
        set_self = full[:3] + [vectors]
        set_cross = full[3:]
        set_inner = [
            whole(inner_weight).reshape(width, blocks, width).transpose(1, 0, 2),
            whole(outer_weight).reshape(blocks, width, width),
        ]
    found = run(
        make_project(packed, parts, rows, block, memory_block, width, narrow, blocks, len(set_self)), 5.0,
        "project", *set_self, *row_tokens,
    )
    query, query_t, keys, values, value_t = (found[2 * i : 2 * i + 2] for i in range(5))
    row_memory, ids, memory_ids, vectors = found[10:]
    query_t = list(query_t)
    if packed:
        set_query, set_last = set_self, set_self
    else:
        set_back, set_query, set_last, set_memory = [full[3], full[4], full[7]], full[:1], full[1:3], full[5:7]
    found = run(
        make_self_attention(share, parts * share, width), 12.0, "self_attention",
        *query_t, *keys, *value_t, ids,
    )
    mixtures, logs = found[:2], found[2:]
    if packed:
        third_c = join(after([third, third_b], mixtures[0]))
        third_d = turned_swap(third_c, 3)
        second_d = after(second_d, mixtures[0])
        set_cross = [second_c, second_d, swap(second_c, 1, 32), swap(second_d, 1, 32)]
        set_back, set_memory = set_cross, set_cross
    first_sum, second_sum, cross_query, memory_keys, memory_values, cross_t, cross_logs = run(
        make_cross_forward(packed, rows, block, parts * memory_share, width, narrow, len(set_cross)),
        9.0, "cross_forward", *set_cross, *own_tokens, row_memory, ids, memory_ids, *mixtures, vectors,
    )
    if packed:
        third_d = after(third_d, second_sum)
        set_inner = [third_c, third_d, swap(third_c, 1, 32), swap(third_d, 1, 32)]
    out_own, out_send, back2_in, sums_inner, *grads_inner = run(
        make_inner(packed, rows, block, width, hidden, narrow, len(set_inner)), 18.0, "inner",
        *set_inner, second_sum, kept, came, vectors,
    )
    found = run(
        make_cross_back(packed, parts, share, memory_share, width, narrow, len(set_back)), 14.0,
        "cross_back", *set_back, back2_in, first_sum, second_sum, cross_query, memory_keys,
        memory_values, cross_t, cross_logs, ids, memory_ids, vectors, sums_inner, *mixtures,
    )
    back1, memory_key_own, memory_value_own, sums_cross = found[:4]
    slope, slope_t, deltas = (found[4 + 2 * i : 6 + 2 * i] for i in range(3))
    memory_received = [swap(a, m + 1, devices) for m, a in enumerate(found[10 : 10 + parts - 1])]
    grads_early = found[10 + parts - 1 :]
    query = list(query)
    if packed:
        keep, send = combine(after([grads_inner[0], swap(grads_inner[1], 1, 32)], back1), 2)
        inner_step = [keep, turned_swap(send, 3)]
        memory_key_own = after(memory_key_own, keep)
    memory_own, memory_send, *grads_cross = run(
        make_memory_back(packed, parts, rows, block, memory_block, width, narrow, len(set_memory)),
        2.0, "memory_back", *set_memory, *own_tokens, memory_key_own, memory_value_own, sums_cross,
        *grads_early, *memory_received,
    )
    if packed:
        cross_came = swap(grads_cross[1], 1, 32)
        query[0] = after(query[0], grads_cross[0])
    found = run(
        make_self_back_upper(parts, share, width), 7.0, "self_back_upper", query[0], keys[0],
        values[0], slope[0], slope_t[0], logs[0], deltas[0], ids,
    )
    query_upper, own_upper = found[:2]
    received_upper = [swap(a, m // 2 + 1, devices) for m, a in enumerate(found[2:])]
    if packed:
        keep_cross, send = combine(after([grads_cross[0], cross_came], query_upper), 2)
        cross_step = [keep_cross, turned_swap(send, 3, CROSSED)]
        query[1] = after(query[1], keep_cross)
    in_part, query_sum, query_w_grad, own_lower, *sends = run(
        make_self_back_lower(packed, parts, rows, block, width, narrow, len(set_query)), 11.0,
        "self_back_lower", *set_query, *own_tokens, query[1], keys[1], values[1], slope[1],
        slope_t[1], logs[1], deltas[1], ids, back1, query_upper,
    )
    received_lower = [swap(a, m // 2 + 1, devices) for m, a in enumerate(sends)]
    if packed:
        keep, send = combine(after(inner_step, query_sum), 2)
        inner_step = [keep, turned_swap(send, 2)]
        keep_cross, send = combine(after(cross_step, query_sum), 2)
        cross_step = [keep_cross, turned_swap(send, 2, CROSSED)]
        in_part = after(in_part, keep, keep_cross)
    in_own, in_send, *grads_last = run(
        make_last(packed, parts, rows, block, memory_block, width, narrow, len(set_last)), 6.0,
        "last", *set_last, *own_tokens, in_part, query_sum, query_w_grad, memory_send, own_upper,
        own_lower, *received_upper, *received_lower,
    )

    if packed:
        keep, send = combine([grads_last[0], swap(grads_last[1], 1, 32)], 2)
        last_step = [keep, turned_swap(send, 3)]
        in_send = after(in_send, last_step[1])
        keep_joint, send = combine_joint(after([inner_step, cross_step], in_own), 2)
        joint_step = [keep_joint, turned_swap(send, 1)]
        keep, send = combine(after(last_step, keep_joint), 2)
        last_step = [keep, turned_swap(send, 2)]
        out_send = after(out_send, keep)
        keep_joint, send = combine(joint_step, 2)
        joint_step = [keep_joint, turned_swap(send, 0)]
        keep, send = combine(after(last_step, keep_joint), 2)
        last_step = [keep, turned_swap(send, 1)]
        keep, send = combine(last_step, 2)
        last_step = [keep, turned_swap(send, 0)]

        def plan(me_ref, *refs):
            me = me_ref[0]
            joint, last = (sum(r[0].astype(F32) for r in given) for given in (refs[:2], refs[2:4]))
            outs = refs[4:]
            inner, cross = joint[: 2 * blocks * narrow, :], joint[2 * blocks * narrow :, :]
            for i in range(blocks):
                outs[0][:, i * width : (i + 1) * width] = inner[i * narrow : (i + 1) * narrow, :]
            outs[1][...] = inner[blocks * narrow :, :]
            for i in range(5):
                outs[2 + i][...] = cross[i * narrow : (i + 1) * narrow, :]
            for i in range(3):
                outs[7 + i][...] = last[i * narrow : (i + 1) * narrow, :]
            rows_in = jnp.concatenate([cross[5 * narrow :, :], last[3 * narrow :, :]], axis=0)
            outs[10][...] = chosen(me, rows_in, narrow)
            per = width // wide
            line = lax.broadcasted_iota(jnp.int32, (blocks, width), 0)
            row = jnp.sum(jnp.where(line == lax.div(me, per), rows_in[3 : 3 + blocks, :], 0.0), axis=0, keepdims=True)
            outs[11][...] = chosen(lax.rem(me, per), row, wide)

        part = (narrow, width)
        shapes = [(narrow, hidden), (wide, width)] + [part] * 8 + [(24, narrow), (1, wide)]
        (inner_share, outer_share, source_key_share, source_value_share, source_output_share,
         source_query_share, output_share, key_share, value_share, query_share, sums,
         inner_bias_share) = call(
            plan, [(s, F32) for s in shapes], (me_array, *joint_step, *last_step), [], 2.0,
            "finish",
        )
        inner_bias_share = inner_bias_share.reshape(wide)
    else:
        def scatter(array):
            return lax.psum_scatter(array, AXES, scatter_dimension=0, tiled=True)

        inner_share = scatter(grads_inner[0].transpose(1, 0, 2).reshape(width, hidden))
        outer_share = scatter(grads_inner[1].reshape(hidden, width))
        source_output_share, source_query_share, output_share = (scatter(g.astype(F32)) for g in grads_early)
        source_key_share, source_value_share = (scatter(g) for g in grads_cross[:2])
        key_share, value_share = (scatter(g) for g in grads_last[:2])
        query_share = scatter(query_w_grad)
        sums = reduce_all(jnp.concatenate([grads_cross[2], grads_last[2]], axis=0), devices)
        inner_bias_share = lax.dynamic_slice(sums[3 : 3 + blocks].reshape(hidden), (me * wide,), (wide,))
        sums = lax.dynamic_slice(sums, (0, me * narrow), (sums.shape[0], narrow))
    def regroup(mine, came):
        came = came.astype(F32)
        return jnp.where(turn == 0, jnp.stack([mine, came]), jnp.stack([came, mine]))

    output = regroup(out_own, swap(out_send, parts, devices))
    in_came = swap(in_send, parts, devices)
    input_gradient = regroup(in_own, in_came[:block])
    memory_gradient = regroup(memory_own, in_came[block:])

    return (
        output,
        input_gradient,
        memory_gradient,
        query_share,
        key_share,
        value_share,
        output_share,
        sums[16],
        sums[17],
        sums[13],
        sums[11],
        sums[12],
        source_query_share,
        source_key_share,
        source_value_share,
        source_output_share,
        sums[10],
        sums[14],
        sums[9],
        sums[7],
        sums[8],
        inner_share,
        inner_bias_share,
        outer_share,
        sums[2],
        sums[0],
        sums[1],
    )


def solution(mesh):
    sequence, devices = mesh.shape["seq"], mesh.size
    tokens, ids = P("dp", "seq", None), P("dp", "seq")
    matrix, vector = P(AXES, None), P(AXES)
    attention = (matrix,) * 4 + (vector,) * 5
    inner = (matrix, vector, matrix, vector, vector, vector)
    return jax.shard_map(
        functools.partial(per_device, devices=devices, sequence=sequence),
        mesh=mesh,
        in_specs=(tokens, tokens, ids, ids, tokens) + attention + attention + inner,
        out_specs=(tokens, tokens, tokens) + attention + attention + inner,
        check_vma=False,
    )
```
